32 devices in a mesh: dp: 8 (over y, x, core), seq: 4 (over z).
Axes of the slice: x: 2, y: 2, z: 4, core: 2. Of those that a mesh axis runs over, the one named last changes fastest.
Arguments:
- tokens: bfloat16 [2, 8192, 1536], P(None, ('dp', 'seq')), may hold values from -6 to 6
- segment_ids: int32 [2, 8192], P(None, ('dp', 'seq')), may hold values from 0 to 31, never falling along the last dimension, each value on 1 to 1024 neighbouring positions
- out_grad: bfloat16 [2, 8192, 1536], P(None, ('dp', 'seq')), may hold values from -6 to 6
- w_q: bfloat16 [1536, 1536], P('dp'), may hold values from -0.15625 to 0.15625
- w_k: bfloat16 [1536, 1536], P('dp'), may hold values from -0.15625 to 0.15625
- w_v: bfloat16 [1536, 1536], P('dp'), may hold values from -0.15625 to 0.15625
- w_o: bfloat16 [1536, 1536], P('dp'), may hold values from -0.875 to 0.875
- w_gate: bfloat16 [1536, 4096], P('dp'), may hold values from -0.15625 to 0.15625
- w_up: bfloat16 [1536, 4096], P('dp'), may hold values from -0.15625 to 0.15625
- w_down: bfloat16 [4096, 1536], P('dp'), may hold values from -0.09375 to 0.09375
- gain_attn: bfloat16 [1536], P('dp'), may hold values from 0.5 to 1.5
- gain_ffn: bfloat16 [1536], P('dp'), may hold values from 0.5 to 1.5
Outputs:
- out: bfloat16 [2, 8192, 1536], P(None, ('dp', 'seq'))
- grad_tokens: float32 [2, 8192, 1536], P(None, ('dp', 'seq'))
- grad_w_q: float32 [1536, 1536], P('dp')
- grad_w_k: float32 [1536, 1536], P('dp')
- grad_w_v: float32 [1536, 1536], P('dp')
- grad_w_o: float32 [1536, 1536], P('dp')
- grad_w_gate: float32 [1536, 4096], P('dp')
- grad_w_up: float32 [1536, 4096], P('dp')
- grad_w_down: float32 [4096, 1536], P('dp')
- grad_gain_attn: float32 [1536], P('dp')
- grad_gain_ffn: float32 [1536], P('dp')
The draws below stay inside these ranges and needn't reach their ends.
Inputs may be any that keep to these rules, and one draw needn't show every extreme that they name: `segment_ids`: along each micro-batch's 8192 tokens the ids never fall; a document holds 1 to 1024 tokens and may run on into the next sequence.
All inputs are finite; a program needn't handle non-finite values.
Results may differ from the reference program's by a relative error of at most 0.02.
Values may be sent and summed in bfloat16 or wider, within the bound.
A program may use at most 320 MiB of HBM per device.

```python
import math
import jax
import jax.numpy as jnp
import numpy as np
from jax import lax

D = 1536
HEADS = 24
HD = 64
FF = 4096
MICRO = 2
SEQ_LEN = 1024
TOKENS = 8192
SEGS = 32
N_DP = 8


def levels(rng, extent, shards, smallest, high):
    def one(axis_at, blocks):
        draws = jax.random.uniform(jax.random.fold_in(jax.random.fold_in(rng, 6), axis_at), (blocks,), jnp.float32, smallest / len(shards), high / len(shards))
        return jnp.repeat(jnp.exp(draws), extent[axis_at] // blocks).reshape((-1,) + (1,) * (len(extent) - axis_at - 1))

    loudness = one(*shards[0])
    for cut in shards[1:]:
        loudness = loudness * one(*cut)
    return loudness


def profile(number_of, total, bound, lean):
    portions = [(1 << 20) // math.isqrt(standing ** lean) + 1 for standing in range(2, number_of + 1)]
    surplus, given = total - bound - (number_of - 1), [1] * (number_of - 1)
    while surplus > 0:
        free = [i for i in range(number_of - 1) if given[i] < bound]
        mass, budget = sum([portions[i] for i in free]), surplus
        for i in free:
            extra = min(bound - given[i], max(1, budget * portions[i] // mass), surplus)
            given[i] = given[i] + extra
            surplus = surplus - extra
    return np.array([bound] + given)


def ragged_sizes(key, count, total, limit, lean):
    if count == 2:
        one = jax.random.randint(key, (), max(1, total - limit), min(limit, total - 1) + 1)
        return jnp.stack([one, total - one])
    sizes = jnp.asarray(profile(count, total, limit, lean), jnp.int32)
    couples = (count - 1) // 2
    giver, sink = sizes[1:1 + 2 * couples:2], sizes[2:2 + 2 * couples:2]
    slack = jnp.minimum(giver - 1, limit - sink)
    passed = jax.random.randint(jax.random.fold_in(key, 1), (couples,), 0, 1 << 20) % (slack + 1)
    sizes = sizes.at[1:1 + 2 * couples:2].set(giver - passed).at[2:2 + 2 * couples:2].set(sink + passed)
    return sizes[jax.random.permutation(jax.random.fold_in(key, 2), count)]


def noise(stream_key, dims, width, most, shards=(), kind=jnp.bfloat16):
    entries = jax.random.normal(stream_key, dims, jnp.float32) * width
    if len(shards) > 0:
        entries = levels(stream_key, dims, shards, -0.22, 0.18) * entries
    return jnp.clip(entries, min=-most, max=most).astype(kind)


def setup_inputs(seed: int = 0) -> dict:
    arg_keys = jax.random.split(jax.random.key(seed), 13)
    return {
        "tokens": noise(arg_keys[0], (MICRO, TOKENS, D), 1.0, 6.0, ((1, 32),)),
        "segment_ids": jax.vmap(lambda own: jnp.searchsorted(jnp.cumsum(ragged_sizes(own, SEGS, TOKENS, SEQ_LEN, 2)), jnp.arange(TOKENS), side="right"))(jax.random.split(arg_keys[1], MICRO)).reshape((MICRO, TOKENS)).astype(jnp.int32),
        "out_grad": noise(arg_keys[2], (MICRO, TOKENS, D), 1.0, 6.0, ((1, 32),)),
        "w_q": noise(arg_keys[3], (D, D), D ** -0.5, 0.15625, ((0, 8),)),
        "w_k": noise(arg_keys[4], (D, D), D ** -0.5, 0.15625, ((0, 8),)),
        "w_v": noise(arg_keys[5], (D, D), D ** -0.5, 0.15625, ((0, 8),)),
        "w_o": noise(arg_keys[6], (D, D), (D // 32) ** -0.5, 0.875, ((0, 8),)),
        "w_gate": noise(arg_keys[7], (D, FF), D ** -0.5, 0.15625, ((0, 8),)),
        "w_up": noise(arg_keys[8], (D, FF), D ** -0.5, 0.15625, ((0, 8),)),
        "w_down": noise(arg_keys[9], (FF, D), FF ** -0.5, 0.09375, ((0, 8),)),
        "gain_attn": jnp.clip(1.0 + 0.1 * jax.random.normal(arg_keys[10], (D,), jnp.float32), 0.5, 1.5).astype(jnp.bfloat16),
        "gain_ffn": jnp.clip(1.0 + 0.1 * jax.random.normal(arg_keys[11], (D,), jnp.float32), 0.5, 1.5).astype(jnp.bfloat16),
    }


@jax.custom_vjp
def low(v):
    return lax.optimization_barrier(v.astype(jnp.bfloat16)).astype(jnp.float32)

@jax.custom_vjp
def low_back(v):
    return v

def low_keep(v):
    return (low(v), None)

def low_pass(kept, grad):
    return (grad,)

def back_keep(v):
    return (v, None)

def back_low(kept, grad):
    return (low(grad),)
low.defvjp(low_keep, low_pass)
low_back.defvjp(back_keep, back_low)
EPS = 1e-05
HIGH = lax.Precision.HIGHEST

def positions_of(doc_row):
    count = doc_row.shape[0]
    place = jnp.arange(count, dtype=jnp.int32)
    before = jnp.concatenate([doc_row[:1], doc_row[:-1]])
    starts = (place == 0) | (doc_row != before)
    first_place = lax.cummax(jnp.where(starts, place, jnp.zeros_like(place)), axis=0)
    return (place - first_place).astype(jnp.int32)

def rope_tables(where_at, half):
    inverse = jnp.exp(jnp.arange(half, dtype=jnp.float32) * (-math.log(10000.0) / half))
    angle = where_at.astype(jnp.float32)[:, None] * inverse[None, :]
    return (jnp.cos(angle), jnp.sin(angle))

def rotate(values, cosine, sine):
    half = values.shape[-1] // 2
    first, second = (values[..., :half], values[..., half:])
    cos_heads, sin_heads = (cosine[:, None, :], sine[:, None, :])
    return jnp.concatenate([first * cos_heads - second * sin_heads, second * cos_heads + first * sin_heads], axis=-1)

def rms_norm(values, gain):
    return values * lax.rsqrt(lax.optimization_barrier(jnp.mean(values * values, axis=-1, keepdims=True)) + EPS) * gain

def layer_sequence(rows_in, doc_row, params):
    w_q, w_k, w_v, w_o, w_gate, w_up, w_down, gain_attn, gain_ffn = params
    length = rows_in.shape[0]
    head_shape = (length, HEADS, HD)
    cosine, sine = rope_tables(positions_of(doc_row), HD // 2)
    normed = low(rms_norm(rows_in, gain_attn))
    query = low(rotate(low_back(jnp.dot(normed, w_q, precision=HIGH)).reshape(head_shape), cosine, sine))
    key = low(rotate(low_back(jnp.dot(normed, w_k, precision=HIGH)).reshape(head_shape), cosine, sine))
    value = low(low_back(jnp.dot(normed, w_v, precision=HIGH))).reshape(head_shape)
    block = min(512, length)
    place = jnp.arange(length, dtype=jnp.int32)

    def attend(start):
        query_block = lax.dynamic_slice_in_dim(query, start, block, 0)
        doc_block = lax.dynamic_slice_in_dim(doc_row, start, block, 0)
        rows_block = start + jnp.arange(block, dtype=jnp.int32)
        scores = low_back(jnp.einsum('qhd,khd->hqk', query_block, key, precision=HIGH) * 0.125)
        allowed = (doc_block[:, None] == doc_row[None, :]) & (rows_block[:, None] >= place[None, :])
        scores = jnp.where(allowed[None], scores, -1e+30)
        peak = lax.optimization_barrier(jnp.max(scores, axis=-1, keepdims=True))
        expo = jnp.exp(scores - peak)
        probs = low(expo / lax.optimization_barrier(jnp.sum(expo, axis=-1, keepdims=True)))
        return jnp.einsum('hqk,khd->qhd', probs, value, precision=HIGH)
    starts = jnp.arange(length // block, dtype=jnp.int32) * block
    mixed = lax.map(jax.checkpoint(attend), starts)
    mixed = low_back(low(mixed.reshape(length, D)))
    middle = rows_in + low_back(jnp.dot(mixed, w_o, precision=HIGH))
    normed_ffn = low(rms_norm(middle, gain_ffn))
    gate = low_back(jnp.dot(normed_ffn, w_gate, precision=HIGH))
    up_value = low_back(jnp.dot(normed_ffn, w_up, precision=HIGH))
    hidden = low(jax.nn.silu(gate) * up_value)
    return middle + low_back(jnp.dot(hidden, w_down, precision=HIGH))

def reference(tokens, segment_ids, out_grad, w_q, w_k, w_v, w_o, w_gate, w_up, w_down, gain_attn, gain_ffn):
    params = tuple((weight.astype(jnp.float32) for weight in (w_q, w_k, w_v, w_o, w_gate, w_up, w_down, gain_attn, gain_ffn)))
    rows_all = tokens.astype(jnp.float32).reshape(MICRO * N_DP, SEQ_LEN, D)
    docs_all = segment_ids.reshape(MICRO * N_DP, SEQ_LEN)
    cotangent = out_grad.astype(jnp.float32).reshape(MICRO * N_DP, SEQ_LEN, D)

    def forward(rows_given, weights):

        def one_sequence(rows_in, doc_row):
            return layer_sequence(rows_in, doc_row, weights)
        saved_fn = jax.checkpoint(one_sequence)

        def scan_step(carry, item):
            return (carry, saved_fn(item[0], item[1]))
        carry_zero = jnp.zeros((), jnp.float32)
        final, results = lax.scan(scan_step, carry_zero, (rows_given, docs_all))
        return results
    result, pullback = jax.vjp(forward, rows_all, params)
    grad_rows, grads = pullback(cotangent)
    return (result.reshape(MICRO, TOKENS, D).astype(jnp.bfloat16), grad_rows.reshape(MICRO, TOKENS, D), grads[0], grads[1], grads[2], grads[3], grads[4], grads[5], grads[6], grads[7], grads[8])
```

```python
import math

import jax
import jax.numpy as jnp
from jax import lax
from jax.experimental import pallas as pl
from jax.experimental.pallas import tpu as pltpu
from jax.sharding import PartitionSpec as P

HEADS = 24
HD = 64


EPS = 1e-05


def positions_of(doc_row):
    count = doc_row.shape[0]
    place = jnp.arange(count, dtype=jnp.int32)
    before = jnp.concatenate([doc_row[:1], doc_row[:-1]])
    starts = (place == 0) | (doc_row != before)
    first_place = lax.cummax(jnp.where(starts, place, jnp.zeros_like(place)), axis=0)
    return place - first_place


def rope_tables(where_at, half):
    inverse = jnp.exp(jnp.arange(half, dtype=jnp.float32) * (-math.log(10000.0) / half))
    angle = where_at.astype(jnp.float32)[:, None] * inverse[None, :]
    return (jnp.cos(angle), jnp.sin(angle))


def rotate(values, cosine, sine):
    half = values.shape[-1] // 2
    first, second = (values[..., :half], values[..., half:])
    cos_heads, sin_heads = (cosine[:, None, :], sine[:, None, :])
    return jnp.concatenate(
        [first * cos_heads - second * sin_heads, second * cos_heads + first * sin_heads], axis=-1
    )


def rotate_back(grads, cosine, sine):
    half = grads.shape[-1] // 2
    first, second = (grads[..., :half], grads[..., half:])
    cos_heads, sin_heads = (cosine[:, None, :], sine[:, None, :])
    return jnp.concatenate(
        [first * cos_heads + second * sin_heads, second * cos_heads - first * sin_heads], axis=-1
    )


def rms_norm(values, gain):
    return values * lax.rsqrt(jnp.mean(values * values, axis=-1, keepdims=True) + EPS) * gain


def norm_backward(values, gain, grad_normed):
    scale = lax.rsqrt(jnp.mean(values * values, axis=-1, keepdims=True) + EPS)
    unit = values * scale
    grad_gain = jnp.sum(grad_normed * unit, axis=0)
    inner = grad_normed * gain
    grad_values = scale * (inner - unit * jnp.mean(inner * unit, axis=-1, keepdims=True))
    return (grad_gain, grad_values)


def block_scores(query_heads, key_heads, doc_row, start, block):
    length = doc_row.shape[0]
    place = jnp.arange(length, dtype=jnp.int32)
    query_block = lax.dynamic_slice_in_dim(query_heads, start, block, 0)
    doc_block = lax.dynamic_slice_in_dim(doc_row, start, block, 0)
    rows_block = start + jnp.arange(block, dtype=jnp.int32)
    allowed = (doc_block[:, None] == doc_row[None, :]) & (rows_block[:, None] >= place[None, :])
    scores = (
        jnp.einsum("qhd,khd->hqk", query_block, key_heads, preferred_element_type=jnp.float32)
        * 0.125
    )
    return (query_block, jnp.where(allowed[None], scores, -1e30))


def attention_forward(query, key, value, doc_row):
    length = query.shape[0]
    head_shape = (length, query.shape[1] // HD, HD)
    query_heads, key_heads, value_heads = (
        query.reshape(head_shape),
        key.reshape(head_shape),
        value.reshape(head_shape),
    )
    block = min(512, length)
    starts = jnp.arange(length // block, dtype=jnp.int32) * block

    def one_block(start):
        unused, scores = block_scores(query_heads, key_heads, doc_row, start, block)
        peak = jnp.max(scores, axis=-1, keepdims=True)
        expo = jnp.exp(scores - peak)
        total = jnp.sum(expo, axis=-1, keepdims=True)
        probs_low = (expo / total).astype(jnp.bfloat16)
        mixed = jnp.einsum(
            "hqk,khd->qhd", probs_low, value_heads, preferred_element_type=jnp.float32
        )
        return (mixed.astype(jnp.bfloat16), (peak + jnp.log(total))[..., 0])

    mixed, logsum = lax.map(one_block, starts)
    return (mixed.reshape(length, query.shape[1]), logsum)


def attention_backward(query, key, value, doc_row, logsum, grad_mixed, cosine, sine):
    length = query.shape[0]
    head_shape = (length, query.shape[1] // HD, HD)
    query_heads, key_heads, value_heads = (
        query.reshape(head_shape),
        key.reshape(head_shape),
        value.reshape(head_shape),
    )
    grad_heads = grad_mixed.reshape(head_shape)
    block = min(512, length)
    starts = jnp.arange(length // block, dtype=jnp.int32) * block

    def one_block(carry, item):
        grad_key, grad_value = carry
        start, logsum_block = item
        query_block, scores = block_scores(query_heads, key_heads, doc_row, start, block)
        probs = jnp.exp(scores - logsum_block[..., None])
        probs_low = probs.astype(jnp.bfloat16)
        grad_block = lax.dynamic_slice_in_dim(grad_heads, start, block, 0)
        grad_probs = jnp.einsum(
            "qhd,khd->hqk", grad_block, value_heads, preferred_element_type=jnp.float32
        )
        inner = jnp.sum(probs * grad_probs, axis=-1, keepdims=True)
        grad_scores = (probs * (grad_probs - inner)).astype(jnp.bfloat16)
        grad_query = (
            jnp.einsum("hqk,khd->qhd", grad_scores, key_heads, preferred_element_type=jnp.float32)
            * 0.125
        )
        grad_key = (
            grad_key
            + jnp.einsum(
                "hqk,qhd->khd", grad_scores, query_block, preferred_element_type=jnp.float32
            )
            * 0.125
        )
        grad_value = grad_value + jnp.einsum(
            "hqk,qhd->khd", probs_low, grad_block, preferred_element_type=jnp.float32
        )
        return ((grad_key, grad_value), grad_query)

    zeros_heads = jnp.zeros(head_shape, jnp.float32)
    (grad_key, grad_value), grad_query = lax.scan(
        one_block, (zeros_heads, zeros_heads), (starts, logsum)
    )
    grad_query = rotate_back(grad_query.reshape(head_shape), cosine, sine)
    grad_key = rotate_back(grad_key, cosine, sine)
    width_here = query.shape[1]
    return (
        grad_query.reshape(length, width_here).astype(jnp.bfloat16),
        grad_key.reshape(length, width_here).astype(jnp.bfloat16),
        grad_value.reshape(length, width_here).astype(jnp.bfloat16),
    )


def per_device(
    tokens, segment_ids, out_grad, w_q, w_k, w_v, w_o, w_gate, w_up, w_down, gain_attn, gain_ffn
):
    micro, rows, width = tokens.shape
    offset = lax.axis_index("seq") * rows
    shards = (w_q, w_k, w_v, w_o, w_gate, w_up, w_down, gain_attn, gain_ffn)
    gathered = (
        lax.all_gather(shards[0], "dp", axis=0, tiled=True),
        lax.all_gather(shards[1], "dp", axis=0, tiled=True),
        lax.all_gather(shards[2], "dp", axis=0, tiled=True),
        lax.all_gather(shards[3], "dp", axis=0, tiled=True),
        lax.all_gather(shards[4], "dp", axis=0, tiled=True),
        lax.all_gather(shards[5], "dp", axis=0, tiled=True),
        lax.all_gather(shards[6], "dp", axis=0, tiled=True),
        lax.all_gather(shards[7], "dp", axis=0, tiled=True),
        lax.all_gather(shards[8], "dp", axis=0, tiled=True),
    )
    docs = lax.all_gather(segment_ids, "seq", axis=1, tiled=True)
    full_q, full_k, full_v, full_o, full_gate, full_up, full_down, full_gain_a, full_gain_f = (
        gathered
    )
    gain_a = full_gain_a.astype(jnp.float32)
    gain_f = full_gain_f.astype(jnp.float32)
    row_heads = (rows, HEADS, HD)
    saved = []
    results = []
    for micro_index in range(micro):
        rows_in = tokens[micro_index].astype(jnp.float32)
        doc_row = docs[micro_index]
        cosine, sine = rope_tables(positions_of(doc_row), HD // 2)
        own_cos = lax.dynamic_slice_in_dim(cosine, offset, rows, 0)
        own_sin = lax.dynamic_slice_in_dim(sine, offset, rows, 0)
        normed = rms_norm(rows_in, gain_a).astype(jnp.bfloat16)
        query_rows = jnp.dot(normed, full_q, preferred_element_type=jnp.float32).reshape(row_heads)
        query_rows = rotate(query_rows, own_cos, own_sin).reshape(rows, width).astype(jnp.bfloat16)
        key_rows = jnp.dot(normed, full_k, preferred_element_type=jnp.float32).reshape(row_heads)
        key_rows = rotate(key_rows, own_cos, own_sin).reshape(rows, width).astype(jnp.bfloat16)
        value_rows = jnp.dot(normed, full_v, preferred_element_type=jnp.float32).astype(
            jnp.bfloat16
        )
        query, key, value = (
            lax.all_to_all(query_rows, "seq", split_axis=1, concat_axis=0, tiled=True),
            lax.all_to_all(key_rows, "seq", split_axis=1, concat_axis=0, tiled=True),
            lax.all_to_all(value_rows, "seq", split_axis=1, concat_axis=0, tiled=True),
        )
        mixed, logsum = attention_forward(query, key, value, doc_row)
        mixed_rows = lax.all_to_all(mixed, "seq", split_axis=0, concat_axis=1, tiled=True)
        middle = rows_in + jnp.dot(mixed_rows, full_o, preferred_element_type=jnp.float32)
        normed_ffn = rms_norm(middle, gain_f).astype(jnp.bfloat16)
        gate = jnp.dot(normed_ffn, full_gate, preferred_element_type=jnp.float32)
        up_value = jnp.dot(normed_ffn, full_up, preferred_element_type=jnp.float32)
        hidden = (jax.nn.silu(gate) * up_value).astype(jnp.bfloat16)
        result = middle + jnp.dot(hidden, full_down, preferred_element_type=jnp.float32)
        results.append(result.astype(jnp.bfloat16))
        saved.append(
            (
                rows_in,
                doc_row,
                cosine,
                sine,
                normed,
                query,
                key,
                value,
                logsum,
                mixed_rows,
                middle,
                normed_ffn,
                gate,
                up_value,
                hidden,
            )
        )
    back_weights = (
        lax.all_gather(shards[0], "dp", axis=0, tiled=True),
        lax.all_gather(shards[1], "dp", axis=0, tiled=True),
        lax.all_gather(shards[2], "dp", axis=0, tiled=True),
        lax.all_gather(shards[3], "dp", axis=0, tiled=True),
        lax.all_gather(shards[4], "dp", axis=0, tiled=True),
        lax.all_gather(shards[5], "dp", axis=0, tiled=True),
        lax.all_gather(shards[6], "dp", axis=0, tiled=True),
        lax.all_gather(shards[7], "dp", axis=0, tiled=True),
        lax.all_gather(shards[8], "dp", axis=0, tiled=True),
    )
    back_q, back_k, back_v, back_o, back_gate, back_up, back_down, back_gain_a, back_gain_f = (
        back_weights
    )
    gain_back_a = back_gain_a.astype(jnp.float32)
    gain_back_f = back_gain_f.astype(jnp.float32)
    totals = [jnp.zeros(weight.shape, jnp.float32) for weight in back_weights]
    grad_inputs = []
    for micro_index in range(micro):
        (
            rows_in,
            doc_row,
            cosine,
            sine,
            normed,
            query,
            key,
            value,
            logsum,
            mixed_rows,
            middle,
            normed_ffn,
            gate,
            up_value,
            hidden,
        ) = saved[micro_index]
        grad_out = out_grad[micro_index].astype(jnp.float32)
        grad_branch = grad_out.astype(jnp.bfloat16)
        totals[6] = totals[6] + jnp.einsum(
            "tf,td->fd", hidden, grad_branch, preferred_element_type=jnp.float32
        )
        grad_hidden = jnp.einsum(
            "td,fd->tf", grad_branch, back_down, preferred_element_type=jnp.float32
        )
        sigma = jax.nn.sigmoid(gate)
        grad_gate = (grad_hidden * up_value * sigma * (1.0 + gate * (1.0 - sigma))).astype(
            jnp.bfloat16
        )
        grad_up = (grad_hidden * jax.nn.silu(gate)).astype(jnp.bfloat16)
        totals[4] = totals[4] + jnp.einsum(
            "td,tf->df", normed_ffn, grad_gate, preferred_element_type=jnp.float32
        )
        totals[5] = totals[5] + jnp.einsum(
            "td,tf->df", normed_ffn, grad_up, preferred_element_type=jnp.float32
        )
        grad_normed_ffn = jnp.einsum(
            "tf,df->td", grad_gate, back_gate, preferred_element_type=jnp.float32
        )
        grad_normed_ffn = grad_normed_ffn + jnp.einsum(
            "tf,df->td", grad_up, back_up, preferred_element_type=jnp.float32
        )
        grad_gain_f, grad_middle = norm_backward(middle, gain_back_f, grad_normed_ffn)
        totals[8] = totals[8] + grad_gain_f
        grad_middle = grad_middle + grad_out
        grad_attn = grad_middle.astype(jnp.bfloat16)
        totals[3] = totals[3] + jnp.einsum(
            "ti,td->id", mixed_rows, grad_attn, preferred_element_type=jnp.float32
        )
        grad_mixed_rows = jnp.einsum(
            "td,id->ti", grad_attn, back_o, preferred_element_type=jnp.float32
        ).astype(jnp.bfloat16)
        grad_mixed = lax.all_to_all(grad_mixed_rows, "seq", split_axis=1, concat_axis=0, tiled=True)
        grad_query, grad_key, grad_value = attention_backward(
            query, key, value, doc_row, logsum, grad_mixed, cosine, sine
        )
        query_back, key_back, value_back = (
            lax.all_to_all(grad_query, "seq", split_axis=0, concat_axis=1, tiled=True),
            lax.all_to_all(grad_key, "seq", split_axis=0, concat_axis=1, tiled=True),
            lax.all_to_all(grad_value, "seq", split_axis=0, concat_axis=1, tiled=True),
        )
        totals[0] = totals[0] + jnp.einsum(
            "td,te->de", normed, query_back, preferred_element_type=jnp.float32
        )
        totals[1] = totals[1] + jnp.einsum(
            "td,te->de", normed, key_back, preferred_element_type=jnp.float32
        )
        totals[2] = totals[2] + jnp.einsum(
            "td,te->de", normed, value_back, preferred_element_type=jnp.float32
        )
        grad_normed = jnp.einsum(
            "te,de->td", query_back, back_q, preferred_element_type=jnp.float32
        )
        grad_normed = grad_normed + jnp.einsum(
            "te,de->td", key_back, back_k, preferred_element_type=jnp.float32
        )
        grad_normed = grad_normed + jnp.einsum(
            "te,de->td", value_back, back_v, preferred_element_type=jnp.float32
        )
        grad_gain_a, grad_rows = norm_backward(rows_in, gain_back_a, grad_normed)
        totals[7] = totals[7] + grad_gain_a
        grad_inputs.append(grad_rows + grad_middle)
    summed_all = (
        totals[0],
        totals[1],
        totals[2],
        totals[3],
        totals[4],
        totals[5],
        totals[6],
        totals[7],
        totals[8],
    )
    pieces = (
        lax.psum_scatter(
            summed_all[0].astype(jnp.bfloat16), "dp", scatter_dimension=0, tiled=True
        ).astype(jnp.float32),
        lax.psum_scatter(
            summed_all[1].astype(jnp.bfloat16), "dp", scatter_dimension=0, tiled=True
        ).astype(jnp.float32),
        lax.psum_scatter(
            summed_all[2].astype(jnp.bfloat16), "dp", scatter_dimension=0, tiled=True
        ).astype(jnp.float32),
        lax.psum_scatter(
            summed_all[3].astype(jnp.bfloat16), "dp", scatter_dimension=0, tiled=True
        ).astype(jnp.float32),
        lax.psum_scatter(
            summed_all[4].astype(jnp.bfloat16), "dp", scatter_dimension=0, tiled=True
        ).astype(jnp.float32),
        lax.psum_scatter(
            summed_all[5].astype(jnp.bfloat16), "dp", scatter_dimension=0, tiled=True
        ).astype(jnp.float32),
        lax.psum_scatter(
            summed_all[6].astype(jnp.bfloat16), "dp", scatter_dimension=0, tiled=True
        ).astype(jnp.float32),
        lax.psum_scatter(
            summed_all[7].astype(jnp.bfloat16), "dp", scatter_dimension=0, tiled=True
        ).astype(jnp.float32),
        lax.psum_scatter(
            summed_all[8].astype(jnp.bfloat16), "dp", scatter_dimension=0, tiled=True
        ).astype(jnp.float32),
    )
    pieces = (
        lax.psum(pieces[0].astype(jnp.bfloat16), "seq").astype(jnp.float32),
        lax.psum(pieces[1].astype(jnp.bfloat16), "seq").astype(jnp.float32),
        lax.psum(pieces[2].astype(jnp.bfloat16), "seq").astype(jnp.float32),
        lax.psum(pieces[3].astype(jnp.bfloat16), "seq").astype(jnp.float32),
        lax.psum(pieces[4].astype(jnp.bfloat16), "seq").astype(jnp.float32),
        lax.psum(pieces[5].astype(jnp.bfloat16), "seq").astype(jnp.float32),
        lax.psum(pieces[6].astype(jnp.bfloat16), "seq").astype(jnp.float32),
        lax.psum(pieces[7].astype(jnp.bfloat16), "seq").astype(jnp.float32),
        lax.psum(pieces[8].astype(jnp.bfloat16), "seq").astype(jnp.float32),
    )
    return (
        jnp.stack(results),
        jnp.stack(grad_inputs),
        pieces[0],
        pieces[1],
        pieces[2],
        pieces[3],
        pieces[4],
        pieces[5],
        pieces[6],
        pieces[7],
        pieces[8],
    )


BLK = 256
LOG2E = 1.4426950408889634


def swap_halves(v):
    lane = lax.broadcasted_iota(jnp.int32, v.shape, 1)
    width = v.shape[1]
    up = pltpu.roll(v, width - 32, axis=1)
    down = pltpu.roll(v, 32, axis=1)
    return jnp.where(lane % 64 < 32, up, down)


def nt(a, b):
    return lax.dot_general(a, b, (((1,), (1,)), ((), ())), preferred_element_type=jnp.float32)


def tn(a, b):
    return lax.dot_general(a, b, (((0,), (0,)), ((), ())), preferred_element_type=jnp.float32)


def attn_fwd_kernel(count_ref, q_ref, k_ref, v_ref, cos_ref, sin_ref, start_ref,
                    qr_ref, kr_ref, vr_ref, mixed_ref, lse_ref):
    pair = pl.program_id(0)
    cosine, sine = cos_ref[...], sin_ref[...]
    q = q_ref[...]
    qr_ref[...] = (q * cosine + swap_halves(q) * sine).astype(jnp.bfloat16)
    k = k_ref[...]
    kr_ref[...] = (k * cosine + swap_halves(k) * sine).astype(jnp.bfloat16)
    vr_ref[...] = v_ref[...].astype(jnp.bfloat16)
    length = q_ref.shape[0]
    lane = lax.broadcasted_iota(jnp.int32, (BLK, 128), 1)

    def one_block(i, carry):
        row0 = pl.multiple_of(i * BLK, BLK)
        rows = pl.ds(row0, BLK)
        for n in range(1, length // BLK + 1):
            @pl.when(count_ref[i] == n)
            def _():
                width = n * BLK
                key0 = pl.multiple_of((i - (n - 1)) * BLK, BLK)
                keys = pl.ds(key0, width)
                place = key0 + lax.broadcasted_iota(jnp.int32, (BLK, width), 1)
                own = row0 + lax.broadcasted_iota(jnp.int32, (BLK, width), 0)
                allowed = (place >= start_ref[rows, :]) & (place <= own)
                for half in range(2):
                    cols = slice(64 * half, 64 * half + 64)
                    s = nt(qr_ref[rows, cols] * jnp.bfloat16(0.125), kr_ref[keys, cols])
                    s = jnp.where(allowed, s, -1e30)
                    peak = jnp.max(s, axis=-1, keepdims=True)
                    expo = jnp.exp(s - peak)
                    total = jnp.sum(expo, axis=-1, keepdims=True)
                    out = jnp.dot(expo.astype(jnp.bfloat16), vr_ref[keys, cols],
                                  preferred_element_type=jnp.float32)
                    mixed_ref[rows, cols] = (out / total).astype(jnp.bfloat16)
                    lse = peak + jnp.log(total)
                    old = lse_ref[rows, :]
                    lse_ref[rows, :] = jnp.where(lane == 2 * pair + half, lse, old)
        return carry

    lax.fori_loop(0, length // BLK, one_block, 0)


def attn_fwd(qkv, cosine, sine, start, counts):
    length, width = qkv.shape[0], qkv.shape[1] // 3
    pairs = width // 128
    col = pl.BlockSpec((length, 128), lambda p, c: (0, p))
    key_col = pl.BlockSpec((length, 128), lambda p, c: (0, pairs + p))
    value_col = pl.BlockSpec((length, 128), lambda p, c: (0, 2 * pairs + p))
    fixed = pl.BlockSpec((length, 128), lambda p, c: (0, 0))
    scol = pl.BlockSpec((length, 1), lambda p, c: (0, 0))
    low = jax.ShapeDtypeStruct((length, width), jnp.bfloat16)
    return pl.pallas_call(
        attn_fwd_kernel,
        grid_spec=pltpu.PrefetchScalarGridSpec(
            num_scalar_prefetch=1, grid=(pairs,),
            in_specs=[col, key_col, value_col, fixed, fixed, scol],
            out_specs=[col, col, col, col, fixed],
        ),
        out_shape=[low, low, low, low, jax.ShapeDtypeStruct((length, 128), jnp.float32)],
        compiler_params=pltpu.CompilerParams(vmem_limit_bytes=40 * 1024 * 1024),
        cost_estimate=pl.CostEstimate(flops=8 * length * length * width // 2, bytes_accessed=20 * length * width,
                                      transcendentals=length * length * pairs),
        name="attn_fwd",
    )(counts, qkv, qkv, qkv, cosine, sine, start)


def attn_bwd_kernel(count_ref, q_ref, k_ref, v_ref, do_ref, cos_ref, sin_ref, start_ref, lse_ref,
                    dq_ref, dk_ref, dv_ref, dk_acc, dv_acc, dq_acc):
    length = q_ref.shape[0]
    dk_acc[...] = jnp.zeros_like(dk_acc)
    dv_acc[...] = jnp.zeros_like(dv_acc)

    def one_block(i, carry):
        row0 = pl.multiple_of(i * BLK, BLK)
        rows = pl.ds(row0, BLK)
        for n in range(1, length // BLK + 1):
            @pl.when(count_ref[i] == n)
            def _():
                width = n * BLK
                key0 = pl.multiple_of((i - (n - 1)) * BLK, BLK)
                keys = pl.ds(key0, width)
                place = key0 + lax.broadcasted_iota(jnp.int32, (width, BLK), 0)
                own = row0 + lax.broadcasted_iota(jnp.int32, (width, BLK), 1)
                allowed = (place >= start_ref[:, rows]) & (place <= own)
                for half in range(2):
                    cols = slice(64 * half, 64 * half + 64)
                    q = q_ref[rows, cols] * jnp.bfloat16(0.125)
                    k = k_ref[keys, cols]
                    do = do_ref[rows, cols]
                    s = nt(k, q)
                    probs = jnp.where(allowed, jnp.exp(s - lse_ref[0, half:half + 1, rows]), 0.0)
                    gp = nt(v_ref[keys, cols], do)
                    inner = jnp.sum(probs * gp, axis=0, keepdims=True)
                    gs = (probs * (gp - inner)).astype(jnp.bfloat16)
                    dv_acc[keys, cols] += jnp.dot(probs.astype(jnp.bfloat16), do,
                                                  preferred_element_type=jnp.float32)
                    dk_acc[keys, cols] += jnp.dot(gs, q, preferred_element_type=jnp.float32)
                    dq_acc[rows, cols] = tn(gs, k) * 0.125
        return carry

    lax.fori_loop(0, length // BLK, one_block, 0)
    cosine, sine = cos_ref[...], sin_ref[...]
    g = dq_acc[...]
    dq_ref[...] = (g * cosine - swap_halves(g) * sine).astype(jnp.bfloat16)
    g = dk_acc[...]
    dk_ref[...] = (g * cosine - swap_halves(g) * sine).astype(jnp.bfloat16)
    dv_ref[...] = dv_acc[...].astype(jnp.bfloat16)


def attn_bwd(q, k, v, grad, cosine, sine, start_row, counts, lse):
    length, width = q.shape
    pairs = width // 128
    col = pl.BlockSpec((length, 128), lambda p, c: (0, p))
    fixed = pl.BlockSpec((length, 128), lambda p, c: (0, 0))
    srow = pl.BlockSpec((1, length), lambda p, c: (0, 0))
    lrow = pl.BlockSpec((1, 2, length), lambda p, c: (p, 0, 0))
    low = jax.ShapeDtypeStruct((length, width), jnp.bfloat16)
    return pl.pallas_call(
        attn_bwd_kernel,
        grid_spec=pltpu.PrefetchScalarGridSpec(
            num_scalar_prefetch=1, grid=(pairs,),
            in_specs=[col, col, col, col, fixed, fixed, srow, lrow],
            out_specs=[col, col, col],
            scratch_shapes=[pltpu.VMEM((length, 128), jnp.float32)] * 3,
        ),
        out_shape=[low, low, low],
        compiler_params=pltpu.CompilerParams(vmem_limit_bytes=40 * 1024 * 1024),
        cost_estimate=pl.CostEstimate(flops=20 * length * length * width // 2, bytes_accessed=14 * length * width,
                                      transcendentals=length * length * pairs),
        name="attn_bwd",
    )(counts, q, k, v, grad, cosine, sine, start_row, lse)


FAST_MESH = {"dp": 8, "seq": 4}
CORE, ALONG_X, ALONG_Y = 1, 2, 4


def swap(value, bit):
    return lax.ppermute(value, "dp", [(i, i ^ bit) for i in range(8)])


def after(value, *others):
    return lax.optimization_barrier((value,) + others)[0]


def ordered(own, other, core):
    first = core == 0
    return jnp.where(first, own, other), jnp.where(first, other, own)


def reshard_pairs(turn, back):
    pairs = []
    for d in range(8):
        for z in range(4):
            target = ((d & 6) | (z >> 1)) * 4 + 2 * ((turn + z) % 2) + (d & 1)
            pairs.append((target, d * 4 + z) if back else (d * 4 + z, target))
    return pairs


def to_sequence(blocks, seq_at):
    got = []
    for turn in range(2):
        block = lax.dynamic_index_in_dim(blocks, (turn + seq_at) & 1, 0, keepdims=False)
        got.append(lax.ppermute(block, ("dp", "seq"), reshard_pairs(turn, False)))
    early = seq_at < 2
    return jnp.concatenate(
        [jnp.where(early, got[0], got[1]), jnp.where(early, got[1], got[0])], axis=0
    )


def from_sequence(half, seq_at):
    rows = half.shape[0] // 2
    early = seq_at < 2
    got = []
    for turn in range(2):
        block = jnp.where(
            early, half[rows * turn : rows * (turn + 1)], half[rows * (1 - turn) : rows * (2 - turn)]
        )
        got.append(lax.ppermute(block, ("dp", "seq"), reshard_pairs(turn, True)))
    even = (seq_at & 1) == 0
    return jnp.stack([jnp.where(even, got[0], got[1]), jnp.where(even, got[1], got[0])])


def whole(half, core):
    return jnp.concatenate(ordered(half, swap(half, CORE), core), axis=0)


def relative_blocks(values, chip, axis):
    size = values.shape[axis] // 4
    return [lax.dynamic_slice_in_dim(values, size * (chip ^ k), size, axis) for k in range(4)]


def relative(values, chip):
    return jnp.concatenate(relative_blocks(values, chip, values.ndim - 1), axis=-1)


def gather_start(piece_x, piece_y):
    pieces = (piece_x, piece_y)
    return (
        pieces,
        [swap(piece, ALONG_X) for piece in pieces],
        [swap(piece, ALONG_Y) for piece in pieces],
    )


def gather_relay(started):
    pieces, over_x, over_y = started
    corner = [swap(over_x[0], ALONG_Y), swap(over_y[1], ALONG_X)]
    return [[pieces[k], over_x[k], over_y[k], corner[k]] for k in range(2)]


def dot(a, b):
    return jnp.dot(a, b, preferred_element_type=jnp.float32)


def low(value):
    return value.astype(jnp.bfloat16)


def wide(value):
    return value.astype(jnp.float32)


def scatter_first(send, bit):
    return swap(low(send), bit)


def scatter_second(keep, got, bit):
    both = low(wide(keep) + wide(got))
    rows = both.shape[0] // 2
    return both[:rows], swap(both[rows:], bit)


def sum_over_seq(value, seq_at):
    one = low(wide(value) + wide(lax.ppermute(value, "seq", [(0, 1), (3, 2)])))
    two = low(wide(one) + wide(lax.ppermute(one, "seq", [(1, 2), (2, 1)])))
    ends = lax.ppermute(two, "seq", [(1, 0), (2, 3)])
    return jnp.where((seq_at == 1) | (seq_at == 2), two, ends)


def both_cores(reduced, core, blocks):
    rows = reduced.shape[0] // 2
    own = lax.dynamic_slice_in_dim(reduced, rows * core, rows, 0)
    other = swap(lax.dynamic_slice_in_dim(reduced, rows * (1 - core), rows, 0), CORE)
    width = reduced.shape[1]
    shape = (rows, blocks, 1, width // blocks)
    even, odd = ordered(own, other, core)
    return wide(
        jnp.concatenate([even.reshape(shape), odd.reshape(shape)], axis=2).reshape(rows, 2 * width)
    )


def column_device(
    tokens, segment_ids, out_grad, w_q, w_k, w_v, w_o, w_gate, w_up, w_down, gain_attn, gain_ffn
):
    dp_at, seq_at = lax.axis_index("dp"), lax.axis_index("seq")
    core, chip = dp_at & 1, dp_at >> 1
    rows, width = tokens.shape[1], tokens.shape[2]
    own_width = width // 2

    def own_columns(weight, which):
        parts = weight.reshape(weight.shape[0], 4, 2, weight.shape[1] // 8)
        return lax.dynamic_index_in_dim(parts, which, 2, keepdims=False).reshape(
            weight.shape[0], weight.shape[1] // 2
        )

    def chip_rows(weights):
        own = jnp.concatenate([own_columns(weight, core) for weight in weights], axis=1)
        other = jnp.concatenate([own_columns(weight, 1 - core) for weight in weights], axis=1)
        return jnp.concatenate(ordered(own, swap(other, CORE), core), axis=0)

    qkv = chip_rows((w_q, w_k, w_v))
    third = own_width
    qkv_x = jnp.concatenate([qkv[:, :third], qkv[:, 2 * third : 2 * third + third // 2]], axis=1)
    qkv_y = jnp.concatenate(
        [qkv[:, third : 2 * third], qkv[:, 2 * third + third // 2 :]], axis=1
    )
    gate_up = chip_rows((w_gate, w_up))
    half_ff = gate_up.shape[1] // 2

    gains = jnp.stack([gain_attn, gain_ffn])[None]
    gains = jnp.concatenate(ordered(gains, swap(gains, CORE), core), axis=0)
    gains = jnp.concatenate(ordered(gains, swap(gains, ALONG_X), chip & 1), axis=0)
    gains = jnp.concatenate(ordered(gains, swap(gains, ALONG_Y), chip >> 1), axis=0)
    gains = wide(gains.transpose(1, 0, 2).reshape(2, width))
    gain_a, gain_f = gains[0], gains[1]

    x_half = to_sequence(tokens, seq_at)
    qkv_started = gather_start(qkv_x, qkv_y)
    docs = to_sequence(segment_ids.reshape(2, 2, rows // 2), seq_at)
    docs = whole(docs, core).reshape(4 * rows)
    x_low = whole(x_half, core)
    length = 4 * rows

    qkv_pieces = gather_relay(qkv_started)
    o_started = gather_start(
        after(w_o[: w_o.shape[0] // 2], qkv_started[1][0], qkv_started[1][1]),
        after(w_o[w_o.shape[0] // 2 :], qkv_started[2][0], qkv_started[2][1]),
    )
    o_pieces = gather_relay(o_started)
    ff_started = gather_start(
        after(gate_up[:, :half_ff], o_started[1][0], o_started[1][1], qkv_pieces[1][3]),
        after(gate_up[:, half_ff:], o_started[2][0], o_started[2][1], qkv_pieces[0][3]),
    )
    ff_pieces = gather_relay(ff_started)
    down_started = gather_start(
        after(w_down[: w_down.shape[0] // 2], ff_started[1][0], ff_started[1][1]),
        after(w_down[w_down.shape[0] // 2 :], ff_started[2][0], ff_started[2][1]),
    )
    down_pieces = gather_relay(down_started)
    g_half = to_sequence(after(out_grad, x_half), seq_at)
    grad_branch = whole(g_half, core)

    full_qkv = jnp.concatenate(
        [
            jnp.concatenate(
                [a[:, :third], b[:, :third], a[:, third:], b[:, third:]], axis=1
            )
            for a, b in zip(*qkv_pieces)
        ],
        axis=0,
    )
    full_gate = jnp.concatenate(ff_pieces[0], axis=0)
    full_up = jnp.concatenate(ff_pieces[1], axis=0)

    def in_chip_order(pieces):
        rows_each = pieces[0][0].shape[0]
        full = jnp.zeros((8 * rows_each, pieces[0][0].shape[1]), jnp.bfloat16)
        for k in range(4):
            for part in range(2):
                full = lax.dynamic_update_slice_in_dim(
                    full, pieces[part][k], rows_each * (2 * (chip ^ k) + part), 0
                )
        return full

    full_o = in_chip_order(o_pieces)
    full_down = in_chip_order(down_pieces)

    place = jnp.arange(length, dtype=jnp.int32)
    before = jnp.concatenate([docs[:1], docs[:-1]])
    begins = (place == 0) | (docs != before)
    start = lax.cummax(jnp.where(begins, place, jnp.zeros_like(place)), axis=0)
    counts = place[: length // BLK] - start[::BLK] // BLK + 1
    cosine, sine = rope_tables(place - start, HD // 2)
    cosine = jnp.concatenate([cosine] * 4, axis=1)
    sine = jnp.concatenate([-sine, sine, -sine, sine], axis=1)

    x = wide(x_low)
    normed = low(relative(rms_norm(x, gain_a), chip))
    qkv_rows = dot(normed, full_qkv)
    query, key, value, mixed, logsum = attn_fwd(qkv_rows, cosine, sine, start[:, None], counts)
    logsum = logsum[:, : own_width // HD].T.reshape(own_width // 128, 2, length)
    part = dot(mixed, full_o)
    middle = x + part + wide(swap(low(part), CORE))
    normed_ffn = low(relative(rms_norm(middle, gain_f), chip))
    gate = dot(normed_ffn, full_gate)
    up_value = dot(normed_ffn, full_up)
    hidden = low(jax.nn.silu(gate) * up_value)
    half_rows = length // 2

    def of_core(values, which):
        return lax.dynamic_slice_in_dim(values, half_rows * which, half_rows, 0)

    out_other = swap(low(dot(of_core(hidden, 1 - core), full_down)), CORE)
    result = of_core(middle, core) + dot(of_core(hidden, core), full_down) + wide(out_other)
    result = from_sequence(low(result), seq_at)

    def split_rows(blocks):
        return (
            jnp.concatenate([blocks[1], blocks[3]], axis=-1),
            jnp.concatenate([blocks[0], blocks[2]], axis=-1),
            jnp.concatenate([blocks[2], blocks[3]], axis=-1),
            jnp.concatenate([blocks[0], blocks[1]], axis=-1),
        )

    def weight_grads(blocks, grad_x, grad_y):
        send_x, keep_x, send_y, keep_y = split_rows(blocks)
        got_x = scatter_first(tn(send_x, grad_x), ALONG_X)
        got_y = scatter_first(tn(send_y, grad_y), ALONG_Y)
        kept_x, last_x = scatter_second(tn(keep_x, grad_x), got_x, ALONG_Y)
        kept_y, last_y = scatter_second(tn(keep_y, grad_y), got_y, ALONG_X)
        return (
            sum_over_seq(low(wide(kept_x) + wide(last_x)), seq_at),
            sum_over_seq(low(wide(kept_y) + wide(last_y)), seq_at),
        )

    def static_blocks(values):
        return jnp.split(values, 4, axis=1)

    hidden_blocks = relative_blocks(hidden, chip, 1)
    down_x, down_y = weight_grads(
        hidden_blocks, grad_branch[:, :own_width], grad_branch[:, own_width:]
    )
    grad_hidden = nt(grad_branch, full_down)
    sigma = jax.nn.sigmoid(gate)
    grad_gate = low(grad_hidden * up_value * sigma * (1.0 + gate * (1.0 - sigma)))
    grad_up = low(grad_hidden * (gate * sigma))
    grad_nf = nt(grad_gate, full_gate) + nt(grad_up, full_up)
    grad_nf_other = swap(low(grad_nf), CORE)
    sum_gate, sum_up = weight_grads(static_blocks(normed_ffn), grad_gate, grad_up)
    grad_nf = relative(grad_nf + wide(grad_nf_other), chip)
    grad_gain_f, grad_middle = norm_backward(middle, gain_f, grad_nf)
    grad_middle = grad_middle + wide(grad_branch)
    grad_attn = low(grad_middle)

    grad_mixed = low(nt(grad_attn, full_o))
    grad_o = low(tn(mixed, grad_attn))
    o_blocks = relative_blocks(grad_o, chip, 0)

    def o_half(order, columns):
        return jnp.concatenate([o_blocks[k][:, columns] for k in order], axis=0)

    left, right = slice(0, own_width), slice(own_width, width)
    kept_x, last_x = scatter_second(
        o_half((0, 2), left), scatter_first(o_half((1, 3), left), ALONG_X), ALONG_Y
    )
    kept_y, last_y = scatter_second(
        o_half((0, 1), right), scatter_first(o_half((2, 3), right), ALONG_Y), ALONG_X
    )
    sum_o = sum_over_seq(
        jnp.concatenate(
            [low(wide(kept_x) + wide(last_x)), low(wide(kept_y) + wide(last_y))], axis=1
        ),
        seq_at,
    )
    grad_query, grad_key, grad_value = attn_bwd(
        query, key, value, grad_mixed, cosine, sine, start[None, :], counts, logsum
    )
    quarter = own_width // 2
    qkv_sum_x, qkv_sum_y = weight_grads(
        static_blocks(normed),
        jnp.concatenate([grad_query, grad_value[:, :quarter]], axis=1),
        jnp.concatenate([grad_key, grad_value[:, quarter:]], axis=1),
    )
    grad_qkv = jnp.concatenate([grad_query, grad_key, grad_value], axis=1)
    normed_other = swap(low(nt(of_core(grad_qkv, 1 - core), full_qkv)), CORE)
    grad_normed = nt(of_core(grad_qkv, core), full_qkv) + wide(normed_other)
    grad_normed = relative(grad_normed, chip)
    grad_gain_a, grad_rows = norm_backward(wide(x_half), gain_a, grad_normed)
    grad_rows = grad_rows + of_core(grad_middle, core)
    grad_tokens = wide(from_sequence(low(grad_rows), seq_at))

    grad_gain_a = grad_gain_a + swap(grad_gain_a, CORE)
    grad_gains = jnp.stack([grad_gain_a, grad_gain_f])
    for bit in (ALONG_X, ALONG_Y):
        grad_gains = grad_gains + swap(grad_gains, bit)
    for bit in (1, 2):
        grad_gains = grad_gains + lax.ppermute(
            grad_gains, "seq", [(i, i ^ bit) for i in range(4)]
        )
    grad_gains = lax.dynamic_slice_in_dim(grad_gains, dp_at * (width // 8), width // 8, 1)

    sum_qkv = jnp.concatenate(
        [
            qkv_sum_x[:, :own_width],
            qkv_sum_y[:, :own_width],
            qkv_sum_x[:, own_width:],
            qkv_sum_y[:, own_width:],
        ],
        axis=1,
    )
    grads_qkv = both_cores(sum_qkv, core, 12)
    grads_ff = both_cores(jnp.concatenate([sum_gate, sum_up], axis=1), core, 8)
    return (
        result,
        grad_tokens,
        grads_qkv[:, :width],
        grads_qkv[:, width : 2 * width],
        grads_qkv[:, 2 * width :],
        wide(sum_o),
        grads_ff[:, : w_gate.shape[1]],
        grads_ff[:, w_gate.shape[1] :],
        wide(jnp.concatenate([down_x, down_y], axis=1)),
        grad_gains[0],
        grad_gains[1],
    )


def solution(mesh):
    placed = (
        P(None, ("dp", "seq"), None),
        P(None, ("dp", "seq")),
        P(None, ("dp", "seq"), None),
        P("dp", None),
        P("dp", None),
        P("dp", None),
        P("dp", None),
        P("dp", None),
        P("dp", None),
        P("dp", None),
        P("dp"),
        P("dp"),
    )
    return jax.shard_map(
        column_device if dict(mesh.shape) == FAST_MESH else per_device,
        mesh=mesh,
        in_specs=placed,
        out_specs=(
            P(None, ("dp", "seq"), None),
            P(None, ("dp", "seq"), None),
            P("dp", None),
            P("dp", None),
            P("dp", None),
            P("dp", None),
            P("dp", None),
            P("dp", None),
            P("dp", None),
            P("dp"),
            P("dp"),
        ),
        check_vma=False,
    )
```

```python
import math

import jax
import jax.numpy as jnp
from jax import lax
from jax.experimental import pallas as pl
from jax.experimental.pallas import tpu as pltpu
from jax.sharding import PartitionSpec as P

HEADS = 24
HD = 64


EPS = 1e-05


def positions_of(doc_row):
    count = doc_row.shape[0]
    place = jnp.arange(count, dtype=jnp.int32)
    before = jnp.concatenate([doc_row[:1], doc_row[:-1]])
    starts = (place == 0) | (doc_row != before)
    first_place = lax.cummax(jnp.where(starts, place, jnp.zeros_like(place)), axis=0)
    return place - first_place


def rope_tables(where_at, half):
    inverse = jnp.exp(jnp.arange(half, dtype=jnp.float32) * (-math.log(10000.0) / half))
    angle = where_at.astype(jnp.float32)[:, None] * inverse[None, :]
    return (jnp.cos(angle), jnp.sin(angle))


def rotate(values, cosine, sine):
    half = values.shape[-1] // 2
    first, second = (values[..., :half], values[..., half:])
    cos_heads, sin_heads = (cosine[:, None, :], sine[:, None, :])
    return jnp.concatenate(
        [first * cos_heads - second * sin_heads, second * cos_heads + first * sin_heads], axis=-1
    )


def rotate_back(grads, cosine, sine):
    half = grads.shape[-1] // 2
    first, second = (grads[..., :half], grads[..., half:])
    cos_heads, sin_heads = (cosine[:, None, :], sine[:, None, :])
    return jnp.concatenate(
        [first * cos_heads + second * sin_heads, second * cos_heads - first * sin_heads], axis=-1
    )


def rms_norm(values, gain):
    return values * lax.rsqrt(jnp.mean(values * values, axis=-1, keepdims=True) + EPS) * gain


def norm_backward(values, gain, grad_normed):
    scale = lax.rsqrt(jnp.mean(values * values, axis=-1, keepdims=True) + EPS)
    unit = values * scale
    grad_gain = jnp.sum(grad_normed * unit, axis=0)
    inner = grad_normed * gain
    grad_values = scale * (inner - unit * jnp.mean(inner * unit, axis=-1, keepdims=True))
    return (grad_gain, grad_values)


def block_scores(query_heads, key_heads, doc_row, start, block):
    length = doc_row.shape[0]
    place = jnp.arange(length, dtype=jnp.int32)
    query_block = lax.dynamic_slice_in_dim(query_heads, start, block, 0)
    doc_block = lax.dynamic_slice_in_dim(doc_row, start, block, 0)
    rows_block = start + jnp.arange(block, dtype=jnp.int32)
    allowed = (doc_block[:, None] == doc_row[None, :]) & (rows_block[:, None] >= place[None, :])
    scores = (
        jnp.einsum("qhd,khd->hqk", query_block, key_heads, preferred_element_type=jnp.float32)
        * 0.125
    )
    return (query_block, jnp.where(allowed[None], scores, -1e30))


def attention_forward(query, key, value, doc_row):
    length = query.shape[0]
    head_shape = (length, query.shape[1] // HD, HD)
    query_heads, key_heads, value_heads = (
        query.reshape(head_shape),
        key.reshape(head_shape),
        value.reshape(head_shape),
    )
    block = min(512, length)
    starts = jnp.arange(length // block, dtype=jnp.int32) * block

    def one_block(start):
        unused, scores = block_scores(query_heads, key_heads, doc_row, start, block)
        peak = jnp.max(scores, axis=-1, keepdims=True)
        expo = jnp.exp(scores - peak)
        total = jnp.sum(expo, axis=-1, keepdims=True)
        probs_low = (expo / total).astype(jnp.bfloat16)
        mixed = jnp.einsum(
            "hqk,khd->qhd", probs_low, value_heads, preferred_element_type=jnp.float32
        )
        return (mixed.astype(jnp.bfloat16), (peak + jnp.log(total))[..., 0])

    mixed, logsum = lax.map(one_block, starts)
    return (mixed.reshape(length, query.shape[1]), logsum)


def attention_backward(query, key, value, doc_row, logsum, grad_mixed, cosine, sine):
    length = query.shape[0]
    head_shape = (length, query.shape[1] // HD, HD)
    query_heads, key_heads, value_heads = (
        query.reshape(head_shape),
        key.reshape(head_shape),
        value.reshape(head_shape),
    )
    grad_heads = grad_mixed.reshape(head_shape)
    block = min(512, length)
    starts = jnp.arange(length // block, dtype=jnp.int32) * block

    def one_block(carry, item):
        grad_key, grad_value = carry
        start, logsum_block = item
        query_block, scores = block_scores(query_heads, key_heads, doc_row, start, block)
        probs = jnp.exp(scores - logsum_block[..., None])
        probs_low = probs.astype(jnp.bfloat16)
        grad_block = lax.dynamic_slice_in_dim(grad_heads, start, block, 0)
        grad_probs = jnp.einsum(
            "qhd,khd->hqk", grad_block, value_heads, preferred_element_type=jnp.float32
        )
        inner = jnp.sum(probs * grad_probs, axis=-1, keepdims=True)
        grad_scores = (probs * (grad_probs - inner)).astype(jnp.bfloat16)
        grad_query = (
            jnp.einsum("hqk,khd->qhd", grad_scores, key_heads, preferred_element_type=jnp.float32)
            * 0.125
        )
        grad_key = (
            grad_key
            + jnp.einsum(
                "hqk,qhd->khd", grad_scores, query_block, preferred_element_type=jnp.float32
            )
            * 0.125
        )
        grad_value = grad_value + jnp.einsum(
            "hqk,qhd->khd", probs_low, grad_block, preferred_element_type=jnp.float32
        )
        return ((grad_key, grad_value), grad_query)

    zeros_heads = jnp.zeros(head_shape, jnp.float32)
    (grad_key, grad_value), grad_query = lax.scan(
        one_block, (zeros_heads, zeros_heads), (starts, logsum)
    )
    grad_query = rotate_back(grad_query.reshape(head_shape), cosine, sine)
    grad_key = rotate_back(grad_key, cosine, sine)
    width_here = query.shape[1]
    return (
        grad_query.reshape(length, width_here).astype(jnp.bfloat16),
        grad_key.reshape(length, width_here).astype(jnp.bfloat16),
        grad_value.reshape(length, width_here).astype(jnp.bfloat16),
    )


def per_device(
    tokens, segment_ids, out_grad, w_q, w_k, w_v, w_o, w_gate, w_up, w_down, gain_attn, gain_ffn
):
    micro, rows, width = tokens.shape
    offset = lax.axis_index("seq") * rows
    shards = (w_q, w_k, w_v, w_o, w_gate, w_up, w_down, gain_attn, gain_ffn)
    gathered = (
        lax.all_gather(shards[0], "dp", axis=0, tiled=True),
        lax.all_gather(shards[1], "dp", axis=0, tiled=True),
        lax.all_gather(shards[2], "dp", axis=0, tiled=True),
        lax.all_gather(shards[3], "dp", axis=0, tiled=True),
        lax.all_gather(shards[4], "dp", axis=0, tiled=True),
        lax.all_gather(shards[5], "dp", axis=0, tiled=True),
        lax.all_gather(shards[6], "dp", axis=0, tiled=True),
        lax.all_gather(shards[7], "dp", axis=0, tiled=True),
        lax.all_gather(shards[8], "dp", axis=0, tiled=True),
    )
    docs = lax.all_gather(segment_ids, "seq", axis=1, tiled=True)
    full_q, full_k, full_v, full_o, full_gate, full_up, full_down, full_gain_a, full_gain_f = (
        gathered
    )
    gain_a = full_gain_a.astype(jnp.float32)
    gain_f = full_gain_f.astype(jnp.float32)
    row_heads = (rows, HEADS, HD)
    saved = []
    results = []
    for micro_index in range(micro):
        rows_in = tokens[micro_index].astype(jnp.float32)
        doc_row = docs[micro_index]
        cosine, sine = rope_tables(positions_of(doc_row), HD // 2)
        own_cos = lax.dynamic_slice_in_dim(cosine, offset, rows, 0)
        own_sin = lax.dynamic_slice_in_dim(sine, offset, rows, 0)
        normed = rms_norm(rows_in, gain_a).astype(jnp.bfloat16)
        query_rows = jnp.dot(normed, full_q, preferred_element_type=jnp.float32).reshape(row_heads)
        query_rows = rotate(query_rows, own_cos, own_sin).reshape(rows, width).astype(jnp.bfloat16)
        key_rows = jnp.dot(normed, full_k, preferred_element_type=jnp.float32).reshape(row_heads)
        key_rows = rotate(key_rows, own_cos, own_sin).reshape(rows, width).astype(jnp.bfloat16)
        value_rows = jnp.dot(normed, full_v, preferred_element_type=jnp.float32).astype(
            jnp.bfloat16
        )
        query, key, value = (
            lax.all_to_all(query_rows, "seq", split_axis=1, concat_axis=0, tiled=True),
            lax.all_to_all(key_rows, "seq", split_axis=1, concat_axis=0, tiled=True),
            lax.all_to_all(value_rows, "seq", split_axis=1, concat_axis=0, tiled=True),
        )
        mixed, logsum = attention_forward(query, key, value, doc_row)
        mixed_rows = lax.all_to_all(mixed, "seq", split_axis=0, concat_axis=1, tiled=True)
        middle = rows_in + jnp.dot(mixed_rows, full_o, preferred_element_type=jnp.float32)
        normed_ffn = rms_norm(middle, gain_f).astype(jnp.bfloat16)
        gate = jnp.dot(normed_ffn, full_gate, preferred_element_type=jnp.float32)
        up_value = jnp.dot(normed_ffn, full_up, preferred_element_type=jnp.float32)
        hidden = (jax.nn.silu(gate) * up_value).astype(jnp.bfloat16)
        result = middle + jnp.dot(hidden, full_down, preferred_element_type=jnp.float32)
        results.append(result.astype(jnp.bfloat16))
        saved.append(
            (
                rows_in,
                doc_row,
                cosine,
                sine,
                normed,
                query,
                key,
                value,
                logsum,
                mixed_rows,
                middle,
                normed_ffn,
                gate,
                up_value,
                hidden,
            )
        )
    back_weights = (
        lax.all_gather(shards[0], "dp", axis=0, tiled=True),
        lax.all_gather(shards[1], "dp", axis=0, tiled=True),
        lax.all_gather(shards[2], "dp", axis=0, tiled=True),
        lax.all_gather(shards[3], "dp", axis=0, tiled=True),
        lax.all_gather(shards[4], "dp", axis=0, tiled=True),
        lax.all_gather(shards[5], "dp", axis=0, tiled=True),
        lax.all_gather(shards[6], "dp", axis=0, tiled=True),
        lax.all_gather(shards[7], "dp", axis=0, tiled=True),
        lax.all_gather(shards[8], "dp", axis=0, tiled=True),
    )
    back_q, back_k, back_v, back_o, back_gate, back_up, back_down, back_gain_a, back_gain_f = (
        back_weights
    )
    gain_back_a = back_gain_a.astype(jnp.float32)
    gain_back_f = back_gain_f.astype(jnp.float32)
    totals = [jnp.zeros(weight.shape, jnp.float32) for weight in back_weights]
    grad_inputs = []
    for micro_index in range(micro):
        (
            rows_in,
            doc_row,
            cosine,
            sine,
            normed,
            query,
            key,
            value,
            logsum,
            mixed_rows,
            middle,
            normed_ffn,
            gate,
            up_value,
            hidden,
        ) = saved[micro_index]
        grad_out = out_grad[micro_index].astype(jnp.float32)
        grad_branch = grad_out.astype(jnp.bfloat16)
        totals[6] = totals[6] + jnp.einsum(
            "tf,td->fd", hidden, grad_branch, preferred_element_type=jnp.float32
        )
        grad_hidden = jnp.einsum(
            "td,fd->tf", grad_branch, back_down, preferred_element_type=jnp.float32
        )
        sigma = jax.nn.sigmoid(gate)
        grad_gate = (grad_hidden * up_value * sigma * (1.0 + gate * (1.0 - sigma))).astype(
            jnp.bfloat16
        )
        grad_up = (grad_hidden * jax.nn.silu(gate)).astype(jnp.bfloat16)
        totals[4] = totals[4] + jnp.einsum(
            "td,tf->df", normed_ffn, grad_gate, preferred_element_type=jnp.float32
        )
        totals[5] = totals[5] + jnp.einsum(
            "td,tf->df", normed_ffn, grad_up, preferred_element_type=jnp.float32
        )
        grad_normed_ffn = jnp.einsum(
            "tf,df->td", grad_gate, back_gate, preferred_element_type=jnp.float32
        )
        grad_normed_ffn = grad_normed_ffn + jnp.einsum(
            "tf,df->td", grad_up, back_up, preferred_element_type=jnp.float32
        )
        grad_gain_f, grad_middle = norm_backward(middle, gain_back_f, grad_normed_ffn)
        totals[8] = totals[8] + grad_gain_f
        grad_middle = grad_middle + grad_out
        grad_attn = grad_middle.astype(jnp.bfloat16)
        totals[3] = totals[3] + jnp.einsum(
            "ti,td->id", mixed_rows, grad_attn, preferred_element_type=jnp.float32
        )
        grad_mixed_rows = jnp.einsum(
            "td,id->ti", grad_attn, back_o, preferred_element_type=jnp.float32
        ).astype(jnp.bfloat16)
        grad_mixed = lax.all_to_all(grad_mixed_rows, "seq", split_axis=1, concat_axis=0, tiled=True)
        grad_query, grad_key, grad_value = attention_backward(
            query, key, value, doc_row, logsum, grad_mixed, cosine, sine
        )
        query_back, key_back, value_back = (
            lax.all_to_all(grad_query, "seq", split_axis=0, concat_axis=1, tiled=True),
            lax.all_to_all(grad_key, "seq", split_axis=0, concat_axis=1, tiled=True),
            lax.all_to_all(grad_value, "seq", split_axis=0, concat_axis=1, tiled=True),
        )
        totals[0] = totals[0] + jnp.einsum(
            "td,te->de", normed, query_back, preferred_element_type=jnp.float32
        )
        totals[1] = totals[1] + jnp.einsum(
            "td,te->de", normed, key_back, preferred_element_type=jnp.float32
        )
        totals[2] = totals[2] + jnp.einsum(
            "td,te->de", normed, value_back, preferred_element_type=jnp.float32
        )
        grad_normed = jnp.einsum(
            "te,de->td", query_back, back_q, preferred_element_type=jnp.float32
        )
        grad_normed = grad_normed + jnp.einsum(
            "te,de->td", key_back, back_k, preferred_element_type=jnp.float32
        )
        grad_normed = grad_normed + jnp.einsum(
            "te,de->td", value_back, back_v, preferred_element_type=jnp.float32
        )
        grad_gain_a, grad_rows = norm_backward(rows_in, gain_back_a, grad_normed)
        totals[7] = totals[7] + grad_gain_a
        grad_inputs.append(grad_rows + grad_middle)
    summed_all = (
        totals[0],
        totals[1],
        totals[2],
        totals[3],
        totals[4],
        totals[5],
        totals[6],
        totals[7],
        totals[8],
    )
    pieces = (
        lax.psum_scatter(
            summed_all[0].astype(jnp.bfloat16), "dp", scatter_dimension=0, tiled=True
        ).astype(jnp.float32),
        lax.psum_scatter(
            summed_all[1].astype(jnp.bfloat16), "dp", scatter_dimension=0, tiled=True
        ).astype(jnp.float32),
        lax.psum_scatter(
            summed_all[2].astype(jnp.bfloat16), "dp", scatter_dimension=0, tiled=True
        ).astype(jnp.float32),
        lax.psum_scatter(
            summed_all[3].astype(jnp.bfloat16), "dp", scatter_dimension=0, tiled=True
        ).astype(jnp.float32),
        lax.psum_scatter(
            summed_all[4].astype(jnp.bfloat16), "dp", scatter_dimension=0, tiled=True
        ).astype(jnp.float32),
        lax.psum_scatter(
            summed_all[5].astype(jnp.bfloat16), "dp", scatter_dimension=0, tiled=True
        ).astype(jnp.float32),
        lax.psum_scatter(
            summed_all[6].astype(jnp.bfloat16), "dp", scatter_dimension=0, tiled=True
        ).astype(jnp.float32),
        lax.psum_scatter(
            summed_all[7].astype(jnp.bfloat16), "dp", scatter_dimension=0, tiled=True
        ).astype(jnp.float32),
        lax.psum_scatter(
            summed_all[8].astype(jnp.bfloat16), "dp", scatter_dimension=0, tiled=True
        ).astype(jnp.float32),
    )
    pieces = (
        lax.psum(pieces[0].astype(jnp.bfloat16), "seq").astype(jnp.float32),
        lax.psum(pieces[1].astype(jnp.bfloat16), "seq").astype(jnp.float32),
        lax.psum(pieces[2].astype(jnp.bfloat16), "seq").astype(jnp.float32),
        lax.psum(pieces[3].astype(jnp.bfloat16), "seq").astype(jnp.float32),
        lax.psum(pieces[4].astype(jnp.bfloat16), "seq").astype(jnp.float32),
        lax.psum(pieces[5].astype(jnp.bfloat16), "seq").astype(jnp.float32),
        lax.psum(pieces[6].astype(jnp.bfloat16), "seq").astype(jnp.float32),
        lax.psum(pieces[7].astype(jnp.bfloat16), "seq").astype(jnp.float32),
        lax.psum(pieces[8].astype(jnp.bfloat16), "seq").astype(jnp.float32),
    )
    return (
        jnp.stack(results),
        jnp.stack(grad_inputs),
        pieces[0],
        pieces[1],
        pieces[2],
        pieces[3],
        pieces[4],
        pieces[5],
        pieces[6],
        pieces[7],
        pieces[8],
    )


BLK = 256
LOG2E = 1.4426950408889634


def swap_halves(v):
    lane = lax.broadcasted_iota(jnp.int32, v.shape, 1)
    width = v.shape[1]
    up = pltpu.roll(v, width - 32, axis=1)
    down = pltpu.roll(v, 32, axis=1)
    return jnp.where(lane % 64 < 32, up, down)


def nt(a, b):
    return lax.dot_general(a, b, (((1,), (1,)), ((), ())), preferred_element_type=jnp.float32)


def tn(a, b):
    return lax.dot_general(a, b, (((0,), (0,)), ((), ())), preferred_element_type=jnp.float32)


def attn_fwd_kernel(count_ref, q_ref, k_ref, v_ref, cos_ref, sin_ref, start_ref,
                    qr_ref, kr_ref, vr_ref, mixed_ref, lse_ref):
    pair = pl.program_id(0)
    cosine, sine = cos_ref[...], sin_ref[...]
    q = q_ref[...]
    qr_ref[...] = (q * cosine + swap_halves(q) * sine).astype(jnp.bfloat16)
    k = k_ref[...]
    kr_ref[...] = (k * cosine + swap_halves(k) * sine).astype(jnp.bfloat16)
    vr_ref[...] = v_ref[...].astype(jnp.bfloat16)
    length = q_ref.shape[0]
    lane = lax.broadcasted_iota(jnp.int32, (BLK, 128), 1)

    def one_block(i, carry):
        row0 = pl.multiple_of(i * BLK, BLK)
        rows = pl.ds(row0, BLK)
        for n in range(1, length // BLK + 1):
            @pl.when(count_ref[i] == n)
            def _():
                width = n * BLK
                key0 = pl.multiple_of((i - (n - 1)) * BLK, BLK)
                keys = pl.ds(key0, width)
                place = key0 + lax.broadcasted_iota(jnp.int32, (BLK, width), 1)
                own = row0 + lax.broadcasted_iota(jnp.int32, (BLK, width), 0)
                allowed = (place >= start_ref[rows, :]) & (place <= own)
                for half in range(2):
                    cols = slice(64 * half, 64 * half + 64)
                    s = nt(qr_ref[rows, cols] * jnp.bfloat16(0.125), kr_ref[keys, cols])
                    s = jnp.where(allowed, s, -1e30)
                    peak = jnp.max(s, axis=-1, keepdims=True)
                    expo = jnp.exp(s - peak)
                    total = jnp.sum(expo, axis=-1, keepdims=True)
                    out = jnp.dot(expo.astype(jnp.bfloat16), vr_ref[keys, cols],
                                  preferred_element_type=jnp.float32)
                    mixed_ref[rows, cols] = (out / total).astype(jnp.bfloat16)
                    lse = peak + jnp.log(total)
                    old = lse_ref[rows, :]
                    lse_ref[rows, :] = jnp.where(lane == 2 * pair + half, lse, old)
        return carry

    lax.fori_loop(0, length // BLK, one_block, 0)


def attn_fwd(qkv, cosine, sine, start, counts):
    length, width = qkv.shape[0], qkv.shape[1] // 3
    pairs = width // 128
    col = pl.BlockSpec((length, 128), lambda p, c: (0, p))
    key_col = pl.BlockSpec((length, 128), lambda p, c: (0, pairs + p))
    value_col = pl.BlockSpec((length, 128), lambda p, c: (0, 2 * pairs + p))
    fixed = pl.BlockSpec((length, 128), lambda p, c: (0, 0))
    scol = pl.BlockSpec((length, 1), lambda p, c: (0, 0))
    low = jax.ShapeDtypeStruct((length, width), jnp.bfloat16)
    return pl.pallas_call(
        attn_fwd_kernel,
        grid_spec=pltpu.PrefetchScalarGridSpec(
            num_scalar_prefetch=1, grid=(pairs,),
            in_specs=[col, key_col, value_col, fixed, fixed, scol],
            out_specs=[col, col, col, col, fixed],
        ),
        out_shape=[low, low, low, low, jax.ShapeDtypeStruct((length, 128), jnp.float32)],
        compiler_params=pltpu.CompilerParams(vmem_limit_bytes=40 * 1024 * 1024),
        cost_estimate=pl.CostEstimate(flops=8 * length * length * width // 2, bytes_accessed=20 * length * width,
                                      transcendentals=length * length * pairs),
        name="attn_fwd",
    )(counts, qkv, qkv, qkv, cosine, sine, start)


def attn_bwd_kernel(count_ref, q_ref, k_ref, v_ref, do_ref, cos_ref, sin_ref, start_ref, lse_ref,
                    dq_ref, dk_ref, dv_ref, dk_acc, dv_acc, dq_acc):
    length = q_ref.shape[0]
    dk_acc[...] = jnp.zeros_like(dk_acc)
    dv_acc[...] = jnp.zeros_like(dv_acc)

    def one_block(i, carry):
        row0 = pl.multiple_of(i * BLK, BLK)
        rows = pl.ds(row0, BLK)
        for n in range(1, length // BLK + 1):
            @pl.when(count_ref[i] == n)
            def _():
                width = n * BLK
                key0 = pl.multiple_of((i - (n - 1)) * BLK, BLK)
                keys = pl.ds(key0, width)
                place = key0 + lax.broadcasted_iota(jnp.int32, (width, BLK), 0)
                own = row0 + lax.broadcasted_iota(jnp.int32, (width, BLK), 1)
                allowed = (place >= start_ref[:, rows]) & (place <= own)
                for half in range(2):
                    cols = slice(64 * half, 64 * half + 64)
                    q = q_ref[rows, cols] * jnp.bfloat16(0.125)
                    k = k_ref[keys, cols]
                    do = do_ref[rows, cols]
                    s = nt(k, q)
                    probs = jnp.where(allowed, jnp.exp(s - lse_ref[0, half:half + 1, rows]), 0.0)
                    gp = nt(v_ref[keys, cols], do)
                    inner = jnp.sum(probs * gp, axis=0, keepdims=True)
                    gs = (probs * (gp - inner)).astype(jnp.bfloat16)
                    dv_acc[keys, cols] += jnp.dot(probs.astype(jnp.bfloat16), do,
                                                  preferred_element_type=jnp.float32)
                    dk_acc[keys, cols] += jnp.dot(gs, q, preferred_element_type=jnp.float32)
                    dq_acc[rows, cols] = tn(gs, k) * 0.125
        return carry

    lax.fori_loop(0, length // BLK, one_block, 0)
    cosine, sine = cos_ref[...], sin_ref[...]
    g = dq_acc[...]
    dq_ref[...] = (g * cosine - swap_halves(g) * sine).astype(jnp.bfloat16)
    g = dk_acc[...]
    dk_ref[...] = (g * cosine - swap_halves(g) * sine).astype(jnp.bfloat16)
    dv_ref[...] = dv_acc[...].astype(jnp.bfloat16)


def attn_bwd(q, k, v, grad, cosine, sine, start_row, counts, lse):
    length, width = q.shape
    pairs = width // 128
    col = pl.BlockSpec((length, 128), lambda p, c: (0, p))
    fixed = pl.BlockSpec((length, 128), lambda p, c: (0, 0))
    srow = pl.BlockSpec((1, length), lambda p, c: (0, 0))
    lrow = pl.BlockSpec((1, 2, length), lambda p, c: (p, 0, 0))
    low = jax.ShapeDtypeStruct((length, width), jnp.bfloat16)
    return pl.pallas_call(
        attn_bwd_kernel,
        grid_spec=pltpu.PrefetchScalarGridSpec(
            num_scalar_prefetch=1, grid=(pairs,),
            in_specs=[col, col, col, col, fixed, fixed, srow, lrow],
            out_specs=[col, col, col],
            scratch_shapes=[pltpu.VMEM((length, 128), jnp.float32)] * 3,
        ),
        out_shape=[low, low, low],
        compiler_params=pltpu.CompilerParams(vmem_limit_bytes=40 * 1024 * 1024),
        cost_estimate=pl.CostEstimate(flops=20 * length * length * width // 2, bytes_accessed=14 * length * width,
                                      transcendentals=length * length * pairs),
        name="attn_bwd",
    )(counts, q, k, v, grad, cosine, sine, start_row, lse)


FAST_MESH = {"dp": 8, "seq": 4}
ANY = pl.BlockSpec(memory_space=pl.ANY)


class Place:
    def __init__(self):
        self.dp, self.z = lax.axis_index("dp"), lax.axis_index("seq")
        self.core = self.dp % 2
        self.x = (self.dp // 2) % 2
        self.y = self.dp // 4
        self.over_core = self.dp + 1 - 2 * self.core
        self.over_x = self.dp + 2 - 4 * self.x
        self.over_y = self.dp + 4 - 8 * self.y
        self.middle = (self.z == 1) | (self.z == 2)


def enter(devices):
    barrier = pltpu.get_barrier_semaphore()
    for dp, seq in devices:
        pl.semaphore_signal(
            barrier, inc=1, device_id={"dp": dp, "seq": seq}, device_id_type=pl.DeviceIdType.MESH
        )
    pl.semaphore_wait(barrier, len(devices))


def remote(src, dst, send_sem, recv_sem, dp, seq):
    return pltpu.make_async_remote_copy(
        src_ref=src,
        dst_ref=dst,
        send_sem=send_sem,
        recv_sem=recv_sem,
        device_id={"dp": dp, "seq": seq},
        device_id_type=pl.DeviceIdType.MESH,
    )


def gather_kernel(
    tokens, segments, out_grad, gains, w_q, w_k, w_v, w_o, w_gate, w_up, w_down,
    x_out, seg_out, g_out, gains_out, qkv_out, o_out, ff_out, down_out,
    send, recv, local, row_send, row_recv, row_local, gain_send, gain_recv,
):
    me = Place()
    rows = tokens.shape[1]
    plane = [(lax.rem(me.dp + k, 8), me.z) for k in range(1, 8)]
    column = [
        (me.dp - me.core + core, lax.rem(me.z + k, 4)) for k in range(1, 4) for core in range(2)
    ]
    enter(plane + column)
    started = []

    def begin(copy):
        copy.start()
        started.append(copy)

    streams = ((tokens, x_out), (segments, seg_out), (out_grad, g_out))

    def place_of(ref, seq):
        return ref.at[pl.ds(rows * seq, rows)] if ref.shape[0] == 4 * rows else ref.at[seq]

    def row_copies(index):
        source, target = streams[index]
        for m in range(2):
            core, seq = me.z // 2, 2 * m + me.core
            here = (core == me.core) & (seq == me.z)

            @pl.when(here)
            def _():
                pltpu.make_async_copy(
                    source.at[m], place_of(target, me.z), row_local.at[index]
                ).start()

            @pl.when(jnp.logical_not(here))
            def _():
                remote(
                    source.at[m], place_of(target, me.z), row_send.at[index, m],
                    row_recv.at[index, me.z % 2], me.dp - me.core + core, seq,
                ).start()

    def row_wait_send(index):
        source, target = streams[index]
        for m in range(2):
            core, seq = me.z // 2, 2 * m + me.core
            here = (core == me.core) & (seq == me.z)

            @pl.when(jnp.logical_not(here))
            def _():
                remote(
                    source.at[m], place_of(target, me.z), row_send.at[index, m],
                    row_recv.at[index, me.z % 2], me.dp - me.core + core, seq,
                ).wait_send()

    def row_relay(index):
        source, target = streams[index]
        for slot in range(2):
            seq = 2 * me.core + slot
            block = place_of(target, seq)
            here = (seq == me.z) & (me.z % 2 == me.core)

            @pl.when(here)
            def _():
                pltpu.make_async_copy(block, block, row_local.at[index]).wait()

            @pl.when(jnp.logical_not(here))
            def _():
                remote(
                    block, block, row_send.at[index, slot], row_recv.at[index, slot], me.over_core, me.z
                ).wait_recv()

            begin(
                remote(
                    block, block, row_send.at[index, 2 + slot], row_recv.at[index, 2 + slot],
                    me.over_core, me.z,
                )
            )

    def row_finish(index):
        source, target = streams[index]
        for slot in range(2):
            block = place_of(target, 2 * (1 - me.core) + slot)
            remote(
                block, block, row_send.at[index, 2 + slot], row_recv.at[index, 2 + slot], me.over_core, me.z
            ).wait_recv()

    by_columns = []
    base = 0
    for source in (w_q, w_k, w_v):
        by_columns.append((source, qkv_out, base))
        base += source.shape[1] // 2
    by_columns.append((w_gate, ff_out, 0))
    by_columns.append((w_up, ff_out, w_gate.shape[1] // 2))
    by_rows = [(w_o, o_out), (w_down, down_out)]

    def column_piece(index, owner):
        source, target, first = by_columns[index]
        depth, width = source.shape[0], source.shape[1] // 2
        return target.at[pl.ds(depth * owner, depth), pl.ds(first, width)]

    def columns_start(index):
        source, target, first = by_columns[index]
        width = source.shape[1] // 2
        mine = column_piece(index, me.dp)
        for core in range(2):
            half = source.at[:, pl.ds(width * core, width)]
            begin(remote(half, mine, send.at[index, core], recv.at[index, me.core],
                         me.over_x - me.core + core, me.z))
            begin(remote(half, mine, send.at[index, 2 + core], recv.at[index, 2 + me.core],
                         me.over_y - me.core + core, me.z))

            @pl.when(core == me.core)
            def _():
                pltpu.make_async_copy(half, mine, local.at[index]).start()

            @pl.when(core != me.core)
            def _():
                remote(half, mine, send.at[index, 4], recv.at[index, 4], me.over_core, me.z).start()

    def columns_relay(index):
        piece = column_piece(index, me.over_x - me.core)
        remote(piece, piece, send.at[index, 5], recv.at[index, 0], me.over_y, me.z).wait_recv()
        begin(remote(piece, piece, send.at[index, 5], recv.at[index, 5], me.over_y, me.z))
        piece = column_piece(index, me.over_y - me.core + 1)
        remote(piece, piece, send.at[index, 6], recv.at[index, 3], me.over_x, me.z).wait_recv()
        begin(remote(piece, piece, send.at[index, 6], recv.at[index, 6], me.over_x, me.z))

    def columns_finish(index):
        source, target, first = by_columns[index]
        width = source.shape[1] // 2
        corner = me.over_x + me.over_y - me.dp - me.core
        for slot, owner in (
            (1, me.over_x - me.core + 1), (2, me.over_y - me.core), (4, me.over_core),
            (5, corner), (6, corner + 1),
        ):
            piece = column_piece(index, owner)
            remote(piece, piece, send.at[index, 5], recv.at[index, slot], me.over_core, me.z).wait_recv()
        mine = column_piece(index, me.dp)
        pltpu.make_async_copy(mine, mine, local.at[index]).wait()
        half = source.at[:, pl.ds(0, width)]
        remote(half, mine, send.at[index, 4], recv.at[index, 4], me.over_core, me.z).wait_send()

    def row_piece(which, owner):
        source, target = by_rows[which]
        depth = source.shape[0]
        return target.at[pl.ds(depth * lax.rem(owner, 4), depth), :]

    def rows_start(which):
        source, target = by_rows[which]
        index = 5 + which
        mine = row_piece(which, me.dp)
        begin(remote(source, mine, send.at[index, 0], recv.at[index, me.core],
                     me.over_x - me.core + me.y, me.z))
        begin(remote(source, mine, send.at[index, 1], recv.at[index, 2 + me.core],
                     me.over_y - me.core + me.y, me.z))

        @pl.when(me.core == me.y)
        def _():
            pltpu.make_async_copy(source, mine, local.at[index]).start()

        @pl.when(me.core != me.y)
        def _():
            remote(source, mine, send.at[index, 4], recv.at[index, 4], me.over_core, me.z).start()

    def rows_relay(which):
        index = 5 + which

        @pl.when(me.core == me.y)
        def _():
            piece = row_piece(which, me.over_x - me.core)
            remote(piece, piece, send.at[index, 5], recv.at[index, 0], me.over_y, me.z).wait_recv()
            remote(piece, piece, send.at[index, 5], recv.at[index, 5], me.over_y, me.z).start()

        @pl.when(me.core != me.y)
        def _():
            piece = row_piece(which, me.over_y - me.core + 1)
            remote(piece, piece, send.at[index, 6], recv.at[index, 3], me.over_x, me.z).wait_recv()
            remote(piece, piece, send.at[index, 6], recv.at[index, 6], me.over_x, me.z).start()

    def rows_finish(which):
        source, target = by_rows[which]
        index = 5 + which
        corner = me.over_x + me.over_y - me.dp - me.core

        def arrived(slot, owner):
            piece = row_piece(which, owner)
            remote(piece, piece, send.at[index, 5], recv.at[index, slot], me.over_core, me.z).wait_recv()

        def left(slot):
            piece = row_piece(which, me.dp)
            remote(source, piece, send.at[index, slot], recv.at[index, slot], me.over_core, me.z).wait_send()

        @pl.when(me.core == me.y)
        def _():
            arrived(1, me.over_x - me.core + 1)
            arrived(4, me.over_core)
            mine = row_piece(which, me.dp)
            pltpu.make_async_copy(source, mine, local.at[index]).wait()
            left(5)

        @pl.when(me.core != me.y)
        def _():
            arrived(2, me.over_y - me.core)
            arrived(5, corner)
            arrived(6, corner + 1)
            left(4)
            left(6)

    row_copies(0)
    row_copies(1)
    for index in range(3):
        columns_start(index)
    for k in range(1, 8):
        begin(remote(gains, gains_out.at[me.dp], gain_send.at[k - 1], gain_recv.at[k - 1],
                     lax.rem(me.dp + k, 8), me.z))
    pltpu.make_async_copy(gains, gains_out.at[me.dp], gain_recv.at[7]).start()
    rows_start(0)
    row_copies(2)
    for index in range(3):
        columns_relay(index)
    columns_start(3)
    rows_relay(0)
    columns_start(4)
    row_relay(0)
    row_relay(1)
    columns_relay(3)
    rows_start(1)
    columns_relay(4)
    row_relay(2)
    rows_relay(1)
    for index in range(5):
        columns_finish(index)
    for which in range(2):
        rows_finish(which)
    for index in range(3):
        row_finish(index)
        row_wait_send(index)
    for k in range(1, 8):
        piece = gains_out.at[lax.rem(me.dp + 8 - k, 8)]
        remote(piece, piece, gain_send.at[k - 1], gain_recv.at[k - 1], me.over_core, me.z).wait_recv()
    pltpu.make_async_copy(gains, gains_out.at[me.dp], gain_recv.at[7]).wait()
    for copy in started:
        copy.wait_send()


def gather_all(tokens, segments, out_grad, gains, weights):
    rows, width = tokens.shape[1], tokens.shape[2]
    ff = weights[4].shape[1]
    low = jnp.bfloat16
    shapes = [
        jax.ShapeDtypeStruct((4 * rows, width), low),
        jax.ShapeDtypeStruct((4,) + segments.shape[1:], jnp.int32),
        jax.ShapeDtypeStruct((4 * rows, width), low),
        jax.ShapeDtypeStruct((8,) + gains.shape, low),
        jax.ShapeDtypeStruct((width, 3 * width // 2), low),
        jax.ShapeDtypeStruct((width // 2, width), low),
        jax.ShapeDtypeStruct((width, ff), low),
        jax.ShapeDtypeStruct((ff // 2, width), low),
    ]
    dma = pltpu.SemaphoreType.DMA
    return pl.pallas_call(
        gather_kernel,
        in_specs=[ANY] * 11,
        out_specs=[ANY] * 8,
        out_shape=shapes,
        scratch_shapes=[
            dma((7, 7)), dma((7, 7)), dma((7,)), dma((3, 4)), dma((3, 4)), dma((3,)), dma((7,)), dma((8,)),
        ],
        compiler_params=pltpu.CompilerParams(collective_id=0, has_side_effects=True),
        cost_estimate=pl.CostEstimate(flops=0, bytes_accessed=500_000_000, transcendentals=0),
        name="gather_all",
    )(tokens, segments, out_grad, gains, *weights)


class ColumnJob:
    def __init__(self, me, refs, source, target, first, width, half, x_first):
        self.me, self.refs, self.x_first = me, refs, x_first
        self.source, self.target = source, target
        self.cols = pl.ds(first, width)
        which, inside = first // half, first % half
        self.out_first, self.half, self.width = 2 * half * which + inside, half, width
        self.rows = source.shape[0] // 4

    def chip_rows(self, x, y):
        return self.source.at[pl.ds(self.rows * (2 * y + x), self.rows), self.cols]

    def first_copies(self, sends_only=False):
        me, (got, keep) = self.me, (self.refs[0], self.refs[1])
        copies, loads = [], []
        for k in range(2):
            part = pl.ds(self.rows * k, self.rows)
            if self.x_first:
                sent, kept, to = self.chip_rows(1 - me.x, k), self.chip_rows(me.x, k), me.over_x
            else:
                sent, kept, to = self.chip_rows(k, 1 - me.y), self.chip_rows(k, me.y), me.over_y
            copies.append(remote(sent, got.at[part], self.sem(0, k), self.sem(1, k), to, me.z))
            if not sends_only:
                loads.append(pltpu.make_async_copy(kept, keep.at[part], self.sem(2, k)))
        return copies, loads

    def sem(self, kind, k):
        return self.refs[4].at[kind, k]

    def second_copy(self):
        me, (got, keep, second) = self.me, self.refs[:3]
        at, to = (me.y, me.over_y) if self.x_first else (me.x, me.over_x)
        part = keep.at[pl.ds(self.rows * (1 - at), self.rows)]
        return remote(part, second, self.sem(0, 2), self.sem(1, 2), to, me.z)

    def start(self):
        for copy in sum(self.first_copies(), []):
            copy.start()

    def pass_second(self):
        copies, loads = self.first_copies()
        for k in range(2):
            loads[k].wait()
            copies[k].wait_recv()
        got, keep = self.refs[:2]
        add_rows(keep, 0, got, 2 * self.rows)
        self.second_copy().start()

    def reduce_plane(self):
        me, (got, keep, second) = self.me, self.refs[:3]
        at = me.y if self.x_first else me.x
        self.second_copy().wait_recv()
        add_rows(second, self.rows * at, keep, self.rows)

    active = None

    def out_piece(self, row_first, rows, core):
        first = pl.multiple_of(self.out_first + self.half * core, 128)
        return self.target.at[pl.ds(row_first, rows), pl.ds(first, self.width)]

    def last_copy(self, final):
        me, rows = self.me, self.rows // 2
        part = final.at[pl.ds(rows * (1 - me.core), rows)]
        return remote(
            part, self.out_piece(0, rows, me.core), self.sem(0, 3), self.sem(1, 3), me.over_core, me.z
        )

    def own_copy(self, final):
        me, rows = self.me, self.rows // 2
        part = final.at[pl.ds(rows * me.core, rows)]
        return pltpu.make_async_copy(part, self.out_piece(0, rows, me.core), self.sem(2, 0))

    def finish(self, final):
        self.last_copy(final).start()
        self.own_copy(final).start()

    def drain(self, final):
        me, rows = self.me, self.rows // 2
        for copy in self.first_copies(True)[0]:
            copy.wait_send()
        self.second_copy().wait_send()
        self.last_copy(final).wait_send()
        self.own_copy(final).wait()
        part = final.at[pl.ds(rows * me.core, rows)]
        remote(
            part, self.out_piece(0, rows, 1 - me.core), self.sem(0, 3), self.sem(1, 3), me.over_core, me.z
        ).wait_recv()


class RowJob:
    def __init__(self, me, refs, source, target, first, width):
        self.me, self.refs = me, refs
        self.source, self.target = source, target
        self.cols = pl.ds(first, width)
        self.rows = source.shape[0] // 2
        self.active = me.core == me.y

    sem = ColumnJob.sem

    def first_copy(self):
        me, got = self.me, self.refs[0]
        sent = self.source.at[pl.ds(self.rows * (1 - me.x), self.rows), self.cols]
        return remote(sent, got, self.sem(0, 0), self.sem(1, 0), me.over_x, me.z)

    def load(self):
        kept = self.source.at[pl.ds(self.rows * self.me.x, self.rows), self.cols]
        return pltpu.make_async_copy(kept, self.refs[1], self.sem(2, 0))

    def second_copy(self):
        me, (got, keep, second) = self.me, self.refs[:3]
        return remote(keep, second, self.sem(0, 2), self.sem(1, 2), me.over_y, me.z)

    def start(self):
        self.first_copy().start()
        self.load().start()

    def pass_second(self):
        self.load().wait()
        self.first_copy().wait_recv()
        got, keep = self.refs[:2]
        add_rows(keep, 0, got, self.rows)

        @pl.when(jnp.logical_not(self.active))
        def _():
            self.second_copy().start()

    def reduce_plane(self):
        got, keep, second = self.refs[:3]

        @pl.when(self.active)
        def _():
            self.second_copy().wait_recv()
            add_rows(second, 0, keep, self.rows)

    def last_copy(self, final):
        me, rows = self.me, self.rows // 2
        part = final.at[pl.ds(rows * (1 - me.core), rows)]
        target = self.target.at[:, self.cols]
        return remote(part, target, self.sem(0, 3), self.sem(1, 3), me.over_core, me.z)

    def own_copy(self, final):
        me, rows = self.me, self.rows // 2
        part = final.at[pl.ds(rows * me.core, rows)]
        return pltpu.make_async_copy(part, self.target.at[:, self.cols], self.sem(2, 1))

    def finish(self, final):
        @pl.when(self.active)
        def _():
            self.last_copy(final).start()
            self.own_copy(final).start()

    def drain(self, final):
        self.first_copy().wait_send()

        @pl.when(self.active)
        def _():
            self.last_copy(final).wait_send()
            self.own_copy(final).wait()

        @pl.when(jnp.logical_not(self.active))
        def _():
            self.second_copy().wait_send()
            self.last_copy(final).wait_recv()


def add_rows(target, first, other, rows, step=64):
    def chunk(k, carry):
        at = pl.multiple_of(k * step, step)
        source = pl.multiple_of(first + k * step, step)
        target[pl.ds(at, step), :] += other[pl.ds(source, step), :]
        return carry

    lax.fori_loop(0, rows // step, chunk, 0)


def both(active, condition):
    return condition if active is None else active & condition


def final_of(job):
    return job.refs[0].at[pl.ds(0, job.rows)]


def seq_copy(job, step):
    me, total, over, sem = job.me, job.refs[2], job.refs[3], job.refs[5]
    inner = me.z + 1 - 2 * (me.z // 2)
    opposite = 3 - me.z
    outer = 3 * (me.z // 2)
    if step == 0:
        return remote(total, over.at[0], sem.at[0, 0], sem.at[1, 0], me.dp, inner)
    if step == 1:
        return remote(total, over.at[1], sem.at[0, 1], sem.at[1, 1], me.dp, opposite)
    return remote(final_of(job), final_of(job), sem.at[0, 2], sem.at[1, 2], me.dp, outer)


def plane_and_seq_first(job):
    job.reduce_plane()

    @pl.when(both(job.active, jnp.logical_not(job.me.middle)))
    def _():
        seq_copy(job, 0).start()


def seq_second(job):
    @pl.when(both(job.active, job.me.middle))
    def _():
        seq_copy(job, 0).wait_recv()
        add_rows(job.refs[2], 0, job.refs[3].at[0], job.rows)
        seq_copy(job, 1).start()


def seq_third(job):
    @pl.when(both(job.active, job.me.middle))
    def _():
        seq_copy(job, 1).wait_recv()
        final, total, over, step = final_of(job), job.refs[2], job.refs[3].at[1], 64

        def chunk(k, carry):
            part = pl.ds(pl.multiple_of(k * step, step), step)
            final[part, :] = total[part, :] + over[part, :]
            return carry

        lax.fori_loop(0, job.rows // step, chunk, 0)
        seq_copy(job, 2).start()


def finish(job):
    @pl.when(both(job.active, jnp.logical_not(job.me.middle)))
    def _():
        seq_copy(job, 2).wait_recv()

    job.finish(final_of(job))


def drain(job):
    job.drain(final_of(job))

    @pl.when(both(job.active, jnp.logical_not(job.me.middle)))
    def _():
        seq_copy(job, 0).wait_send()

    @pl.when(both(job.active, job.me.middle))
    def _():
        seq_copy(job, 1).wait_send()
        seq_copy(job, 2).wait_send()


STAGES = (
    (0, lambda job: job.start()),
    (2, lambda job: job.pass_second()),
    (3, plane_and_seq_first),
    (4, seq_second),
    (5, seq_third),
    (6, finish),
)


def run_jobs(jobs):
    for tick in range(len(jobs) + STAGES[-1][0]):
        for late, stage in reversed(STAGES):
            if 0 <= tick - late < len(jobs):
                stage(jobs[tick - late])
    for job in jobs:
        drain(job)


def job_plan(d_model, ff):
    half = d_model // 2
    down = [("down", 384 * k, 384, True) for k in range(d_model // 384)]
    wide_ff = [("ff", 512 * k, 512, False) for k in range(ff // 512)]
    rest = [("o", half * k, half, True) for k in range(2)]
    qkv = [("qkv", 384 * k, 384, k % 2 == 1) for k in range(3 * half // 384)]
    return [job for pair in zip(down, wide_ff) for job in pair] + wide_ff[len(down) :] + rest + qkv


def reduce_all(g_qkv, g_o, g_ff, g_down):
    d_model, ff = g_o.shape[1], g_ff.shape[1]
    plan = job_plan(d_model, ff)
    sources = {"qkv": g_qkv, "o": g_o, "ff": g_ff, "down": g_down}
    names = ("qkv", "o", "ff", "down")
    halves = {"qkv": d_model // 2, "ff": ff // 2}
    outs = [
        jax.ShapeDtypeStruct((d_model // 8, 3 * d_model), jnp.bfloat16),
        jax.ShapeDtypeStruct((d_model // 8, d_model), jnp.bfloat16),
        jax.ShapeDtypeStruct((d_model // 8, 2 * ff), jnp.bfloat16),
        jax.ShapeDtypeStruct((ff // 8, d_model), jnp.bfloat16),
    ]
    scratch = []
    dma = pltpu.SemaphoreType.DMA
    for name, first, width, x_first in plan:
        by_columns = name in halves
        rows = sources[name].shape[0] // (4 if by_columns else 2)
        many = 2 * rows if by_columns else rows

        def vmem(*shape):
            return pltpu.VMEM(shape, jnp.bfloat16)

        scratch += [
            vmem(many, width), vmem(many, width), vmem(rows, width), vmem(2, rows, width), dma((3, 4)), dma((2, 3)),
        ]

    def kernel(*refs):
        source = dict(zip(names, refs[:4]))
        target = dict(zip(names, refs[4:8]))
        buffers = refs[8:]
        me = Place()
        enter(
            [(me.over_core, me.z)]
            + [(me.over_x, me.z), (me.over_y, me.z)]
            + [(me.dp, lax.rem(me.z + k, 4)) for k in range(1, 4)]
        )
        jobs = []
        for k, (name, first, width, x_first) in enumerate(plan):
            own = buffers[6 * k : 6 * k + 6]
            if name in halves:
                jobs.append(
                    ColumnJob(me, own, source[name], target[name], first, width, halves[name], x_first)
                )
            else:
                jobs.append(RowJob(me, own, source[name], target[name], first, width))
        run_jobs(jobs)

    return pl.pallas_call(
        kernel,
        in_specs=[ANY] * 4,
        out_specs=[ANY] * 4,
        out_shape=outs,
        scratch_shapes=scratch,
        compiler_params=pltpu.CompilerParams(
            collective_id=1, has_side_effects=True, vmem_limit_bytes=61 * 1024 * 1024
        ),
        cost_estimate=pl.CostEstimate(flops=0, bytes_accessed=800_000_000, transcendentals=0),
        name="reduce_all",
    )(g_qkv, g_o, g_ff, g_down)


def swap_core(value):
    return lax.ppermute(value, "dp", [(i, i ^ 1) for i in range(8)])


def reshard_pairs(turn):
    pairs = []
    for d in range(8):
        for z in range(4):
            target = ((d & 6) | (z >> 1)) * 4 + 2 * ((turn + z) % 2) + (d & 1)
            pairs.append((target, d * 4 + z))
    return pairs


def from_sequence(half, seq_at):
    rows = half.shape[0] // 2
    early = seq_at < 2
    got = []
    for turn in range(2):
        block = jnp.where(
            early, half[rows * turn : rows * (turn + 1)], half[rows * (1 - turn) : rows * (2 - turn)]
        )
        got.append(lax.ppermute(block, ("dp", "seq"), reshard_pairs(turn)))
    even = (seq_at & 1) == 0
    return jnp.stack([jnp.where(even, got[0], got[1]), jnp.where(even, got[1], got[0])])


def dot(a, b):
    return jnp.dot(a, b, preferred_element_type=jnp.float32)


def low(value):
    return value.astype(jnp.bfloat16)


def wide(value):
    return value.astype(jnp.float32)


def column_device(
    tokens, segment_ids, out_grad, w_q, w_k, w_v, w_o, w_gate, w_up, w_down, gain_attn, gain_ffn
):
    dp_at, seq_at = lax.axis_index("dp"), lax.axis_index("seq")
    core = dp_at & 1
    rows, width = tokens.shape[1], tokens.shape[2]
    own_width = width // 2
    length = 4 * rows
    pad = -gain_attn.shape[0] % 128
    gains = jnp.pad(jnp.stack([gain_attn, gain_ffn]), ((0, 0), (0, pad)))
    x_low, docs, grad_branch, gains, full_qkv, full_o, full_ff, full_down = gather_all(
        tokens, segment_ids.reshape(2, 1, rows), out_grad, gains,
        (w_q, w_k, w_v, w_o, w_gate, w_up, w_down),
    )
    docs = docs.reshape(length)
    gains = wide(gains[:, :, : width // 8].transpose(1, 0, 2).reshape(2, width))
    gain_a, gain_f = gains[0], gains[1]
    half_ff = full_ff.shape[1] // 2

    place = jnp.arange(length, dtype=jnp.int32)
    before = jnp.concatenate([docs[:1], docs[:-1]])
    begins = (place == 0) | (docs != before)
    start = lax.cummax(jnp.where(begins, place, jnp.zeros_like(place)), axis=0)
    counts = place[: length // BLK] - start[::BLK] // BLK + 1
    cosine, sine = rope_tables(place - start, HD // 2)
    cosine = jnp.concatenate([cosine] * 4, axis=1)
    sine = jnp.concatenate([-sine, sine, -sine, sine], axis=1)

    def of_core(values, which):
        return lax.dynamic_slice_in_dim(values, length // 2 * which, length // 2, 0)

    x = wide(x_low)
    normed = low(rms_norm(x, gain_a))
    qkv_rows = dot(normed, full_qkv)
    query, key, value, mixed, logsum = attn_fwd(qkv_rows, cosine, sine, start[:, None], counts)
    logsum = logsum[:, : own_width // HD].T.reshape(own_width // 128, 2, length)
    part = dot(mixed, full_o)
    middle = x + part + wide(swap_core(low(part)))
    normed_ffn = low(rms_norm(middle, gain_f))
    gate = dot(normed_ffn, full_ff[:, :half_ff])
    up_value = dot(normed_ffn, full_ff[:, half_ff:])
    hidden = low(jax.nn.silu(gate) * up_value)
    out_other = swap_core(low(dot(of_core(hidden, 1 - core), full_down)))
    result = of_core(middle, core) + dot(of_core(hidden, core), full_down) + wide(out_other)
    result = from_sequence(low(result), seq_at)

    g_down = low(tn(hidden, grad_branch))
    grad_hidden = nt(grad_branch, full_down)
    sigma = jax.nn.sigmoid(gate)
    grad_gate = low(grad_hidden * up_value * sigma * (1.0 + gate * (1.0 - sigma)))
    grad_up = low(grad_hidden * (gate * sigma))
    grad_ff = jnp.concatenate([grad_gate, grad_up], axis=1)
    g_ff = low(tn(normed_ffn, grad_ff))
    grad_nf = nt(grad_ff, full_ff)
    grad_nf = grad_nf + wide(swap_core(low(grad_nf)))
    grad_gain_f, grad_middle = norm_backward(middle, gain_f, grad_nf)
    grad_middle = grad_middle + wide(grad_branch)
    grad_attn = low(grad_middle)

    grad_mixed = low(nt(grad_attn, full_o))
    g_o = low(tn(mixed, grad_attn))
    grad_qkv = jnp.concatenate(
        attn_bwd(query, key, value, grad_mixed, cosine, sine, start[None, :], counts, logsum), axis=1
    )
    g_qkv = low(tn(normed, grad_qkv))
    normed_other = swap_core(low(nt(of_core(grad_qkv, 1 - core), full_qkv)))
    grad_normed = nt(of_core(grad_qkv, core), full_qkv) + wide(normed_other)
    grad_gain_a, grad_rows = norm_backward(of_core(x, core), gain_a, grad_normed)
    grad_rows = grad_rows + of_core(grad_middle, core)
    grad_tokens = wide(from_sequence(low(grad_rows), seq_at))

    grad_gain_a = grad_gain_a + swap_core(grad_gain_a)
    grad_gains = jnp.stack([grad_gain_a, grad_gain_f])
    for bit in (2, 4):
        grad_gains = grad_gains + lax.ppermute(grad_gains, "dp", [(i, i ^ bit) for i in range(8)])
    for bit in (1, 2):
        grad_gains = grad_gains + lax.ppermute(grad_gains, "seq", [(i, i ^ bit) for i in range(4)])
    grad_gains = lax.dynamic_slice_in_dim(grad_gains, dp_at * (width // 8), width // 8, 1)

    r_qkv, r_o, r_ff, r_down = reduce_all(g_qkv, g_o, g_ff, g_down)
    return (
        result,
        grad_tokens,
        wide(r_qkv[:, :width]),
        wide(r_qkv[:, width : 2 * width]),
        wide(r_qkv[:, 2 * width :]),
        wide(r_o),
        wide(r_ff[:, : w_gate.shape[1]]),
        wide(r_ff[:, w_gate.shape[1] :]),
        wide(r_down),
        grad_gains[0],
        grad_gains[1],
    )


def solution(mesh):
    placed = (
        P(None, ("dp", "seq"), None),
        P(None, ("dp", "seq")),
        P(None, ("dp", "seq"), None),
        P("dp", None),
        P("dp", None),
        P("dp", None),
        P("dp", None),
        P("dp", None),
        P("dp", None),
        P("dp", None),
        P("dp"),
        P("dp"),
    )
    return jax.shard_map(
        column_device if dict(mesh.shape) == FAST_MESH else per_device,
        mesh=mesh,
        in_specs=placed,
        out_specs=(
            P(None, ("dp", "seq"), None),
            P(None, ("dp", "seq"), None),
            P("dp", None),
            P("dp", None),
            P("dp", None),
            P("dp", None),
            P("dp", None),
            P("dp", None),
            P("dp", None),
            P("dp"),
            P("dp"),
        ),
        check_vma=False,
    )
```

```python
import math

import jax
import jax.numpy as jnp
from jax import lax
from jax.experimental import pallas as pl
from jax.experimental.pallas import tpu as pltpu
from jax.sharding import PartitionSpec as P

HEADS = 24
HD = 64


EPS = 1e-05


def positions_of(doc_row):
    count = doc_row.shape[0]
    place = jnp.arange(count, dtype=jnp.int32)
    before = jnp.concatenate([doc_row[:1], doc_row[:-1]])
    starts = (place == 0) | (doc_row != before)
    first_place = lax.cummax(jnp.where(starts, place, jnp.zeros_like(place)), axis=0)
    return place - first_place


def rope_tables(where_at, half):
    inverse = jnp.exp(jnp.arange(half, dtype=jnp.float32) * (-math.log(10000.0) / half))
    angle = where_at.astype(jnp.float32)[:, None] * inverse[None, :]
    return (jnp.cos(angle), jnp.sin(angle))


def rotate(values, cosine, sine):
    half = values.shape[-1] // 2
    first, second = (values[..., :half], values[..., half:])
    cos_heads, sin_heads = (cosine[:, None, :], sine[:, None, :])
    return jnp.concatenate(
        [first * cos_heads - second * sin_heads, second * cos_heads + first * sin_heads], axis=-1
    )


def rotate_back(grads, cosine, sine):
    half = grads.shape[-1] // 2
    first, second = (grads[..., :half], grads[..., half:])
    cos_heads, sin_heads = (cosine[:, None, :], sine[:, None, :])
    return jnp.concatenate(
        [first * cos_heads + second * sin_heads, second * cos_heads - first * sin_heads], axis=-1
    )


def rms_norm(values, gain):
    return values * lax.rsqrt(jnp.mean(values * values, axis=-1, keepdims=True) + EPS) * gain


def norm_backward(values, gain, grad_normed):
    scale = lax.rsqrt(jnp.mean(values * values, axis=-1, keepdims=True) + EPS)
    unit = values * scale
    grad_gain = jnp.sum(grad_normed * unit, axis=0)
    inner = grad_normed * gain
    grad_values = scale * (inner - unit * jnp.mean(inner * unit, axis=-1, keepdims=True))
    return (grad_gain, grad_values)


def block_scores(query_heads, key_heads, doc_row, start, block):
    length = doc_row.shape[0]
    place = jnp.arange(length, dtype=jnp.int32)
    query_block = lax.dynamic_slice_in_dim(query_heads, start, block, 0)
    doc_block = lax.dynamic_slice_in_dim(doc_row, start, block, 0)
    rows_block = start + jnp.arange(block, dtype=jnp.int32)
    allowed = (doc_block[:, None] == doc_row[None, :]) & (rows_block[:, None] >= place[None, :])
    scores = (
        jnp.einsum("qhd,khd->hqk", query_block, key_heads, preferred_element_type=jnp.float32)
        * 0.125
    )
    return (query_block, jnp.where(allowed[None], scores, -1e30))


def attention_forward(query, key, value, doc_row):
    length = query.shape[0]
    head_shape = (length, query.shape[1] // HD, HD)
    query_heads, key_heads, value_heads = (
        query.reshape(head_shape),
        key.reshape(head_shape),
        value.reshape(head_shape),
    )
    block = min(512, length)
    starts = jnp.arange(length // block, dtype=jnp.int32) * block

    def one_block(start):
        unused, scores = block_scores(query_heads, key_heads, doc_row, start, block)
        peak = jnp.max(scores, axis=-1, keepdims=True)
        expo = jnp.exp(scores - peak)
        total = jnp.sum(expo, axis=-1, keepdims=True)
        probs_low = (expo / total).astype(jnp.bfloat16)
        mixed = jnp.einsum(
            "hqk,khd->qhd", probs_low, value_heads, preferred_element_type=jnp.float32
        )
        return (mixed.astype(jnp.bfloat16), (peak + jnp.log(total))[..., 0])

    mixed, logsum = lax.map(one_block, starts)
    return (mixed.reshape(length, query.shape[1]), logsum)


def attention_backward(query, key, value, doc_row, logsum, grad_mixed, cosine, sine):
    length = query.shape[0]
    head_shape = (length, query.shape[1] // HD, HD)
    query_heads, key_heads, value_heads = (
        query.reshape(head_shape),
        key.reshape(head_shape),
        value.reshape(head_shape),
    )
    grad_heads = grad_mixed.reshape(head_shape)
    block = min(512, length)
    starts = jnp.arange(length // block, dtype=jnp.int32) * block

    def one_block(carry, item):
        grad_key, grad_value = carry
        start, logsum_block = item
        query_block, scores = block_scores(query_heads, key_heads, doc_row, start, block)
        probs = jnp.exp(scores - logsum_block[..., None])
        probs_low = probs.astype(jnp.bfloat16)
        grad_block = lax.dynamic_slice_in_dim(grad_heads, start, block, 0)
        grad_probs = jnp.einsum(
            "qhd,khd->hqk", grad_block, value_heads, preferred_element_type=jnp.float32
        )
        inner = jnp.sum(probs * grad_probs, axis=-1, keepdims=True)
        grad_scores = (probs * (grad_probs - inner)).astype(jnp.bfloat16)
        grad_query = (
            jnp.einsum("hqk,khd->qhd", grad_scores, key_heads, preferred_element_type=jnp.float32)
            * 0.125
        )
        grad_key = (
            grad_key
            + jnp.einsum(
                "hqk,qhd->khd", grad_scores, query_block, preferred_element_type=jnp.float32
            )
            * 0.125
        )
        grad_value = grad_value + jnp.einsum(
            "hqk,qhd->khd", probs_low, grad_block, preferred_element_type=jnp.float32
        )
        return ((grad_key, grad_value), grad_query)

    zeros_heads = jnp.zeros(head_shape, jnp.float32)
    (grad_key, grad_value), grad_query = lax.scan(
        one_block, (zeros_heads, zeros_heads), (starts, logsum)
    )
    grad_query = rotate_back(grad_query.reshape(head_shape), cosine, sine)
    grad_key = rotate_back(grad_key, cosine, sine)
    width_here = query.shape[1]
    return (
        grad_query.reshape(length, width_here).astype(jnp.bfloat16),
        grad_key.reshape(length, width_here).astype(jnp.bfloat16),
        grad_value.reshape(length, width_here).astype(jnp.bfloat16),
    )


def per_device(
    tokens, segment_ids, out_grad, w_q, w_k, w_v, w_o, w_gate, w_up, w_down, gain_attn, gain_ffn
):
    micro, rows, width = tokens.shape
    offset = lax.axis_index("seq") * rows
    shards = (w_q, w_k, w_v, w_o, w_gate, w_up, w_down, gain_attn, gain_ffn)
    gathered = (
        lax.all_gather(shards[0], "dp", axis=0, tiled=True),
        lax.all_gather(shards[1], "dp", axis=0, tiled=True),
        lax.all_gather(shards[2], "dp", axis=0, tiled=True),
        lax.all_gather(shards[3], "dp", axis=0, tiled=True),
        lax.all_gather(shards[4], "dp", axis=0, tiled=True),
        lax.all_gather(shards[5], "dp", axis=0, tiled=True),
        lax.all_gather(shards[6], "dp", axis=0, tiled=True),
        lax.all_gather(shards[7], "dp", axis=0, tiled=True),
        lax.all_gather(shards[8], "dp", axis=0, tiled=True),
    )
    docs = lax.all_gather(segment_ids, "seq", axis=1, tiled=True)
    full_q, full_k, full_v, full_o, full_gate, full_up, full_down, full_gain_a, full_gain_f = (
        gathered
    )
    gain_a = full_gain_a.astype(jnp.float32)
    gain_f = full_gain_f.astype(jnp.float32)
    row_heads = (rows, HEADS, HD)
    saved = []
    results = []
    for micro_index in range(micro):
        rows_in = tokens[micro_index].astype(jnp.float32)
        doc_row = docs[micro_index]
        cosine, sine = rope_tables(positions_of(doc_row), HD // 2)
        own_cos = lax.dynamic_slice_in_dim(cosine, offset, rows, 0)
        own_sin = lax.dynamic_slice_in_dim(sine, offset, rows, 0)
        normed = rms_norm(rows_in, gain_a).astype(jnp.bfloat16)
        query_rows = jnp.dot(normed, full_q, preferred_element_type=jnp.float32).reshape(row_heads)
        query_rows = rotate(query_rows, own_cos, own_sin).reshape(rows, width).astype(jnp.bfloat16)
        key_rows = jnp.dot(normed, full_k, preferred_element_type=jnp.float32).reshape(row_heads)
        key_rows = rotate(key_rows, own_cos, own_sin).reshape(rows, width).astype(jnp.bfloat16)
        value_rows = jnp.dot(normed, full_v, preferred_element_type=jnp.float32).astype(
            jnp.bfloat16
        )
        query, key, value = (
            lax.all_to_all(query_rows, "seq", split_axis=1, concat_axis=0, tiled=True),
            lax.all_to_all(key_rows, "seq", split_axis=1, concat_axis=0, tiled=True),
            lax.all_to_all(value_rows, "seq", split_axis=1, concat_axis=0, tiled=True),
        )
        mixed, logsum = attention_forward(query, key, value, doc_row)
        mixed_rows = lax.all_to_all(mixed, "seq", split_axis=0, concat_axis=1, tiled=True)
        middle = rows_in + jnp.dot(mixed_rows, full_o, preferred_element_type=jnp.float32)
        normed_ffn = rms_norm(middle, gain_f).astype(jnp.bfloat16)
        gate = jnp.dot(normed_ffn, full_gate, preferred_element_type=jnp.float32)
        up_value = jnp.dot(normed_ffn, full_up, preferred_element_type=jnp.float32)
        hidden = (jax.nn.silu(gate) * up_value).astype(jnp.bfloat16)
        result = middle + jnp.dot(hidden, full_down, preferred_element_type=jnp.float32)
        results.append(result.astype(jnp.bfloat16))
        saved.append(
            (
                rows_in,
                doc_row,
                cosine,
                sine,
                normed,
                query,
                key,
                value,
                logsum,
                mixed_rows,
                middle,
                normed_ffn,
                gate,
                up_value,
                hidden,
            )
        )
    back_weights = (
        lax.all_gather(shards[0], "dp", axis=0, tiled=True),
        lax.all_gather(shards[1], "dp", axis=0, tiled=True),
        lax.all_gather(shards[2], "dp", axis=0, tiled=True),
        lax.all_gather(shards[3], "dp", axis=0, tiled=True),
        lax.all_gather(shards[4], "dp", axis=0, tiled=True),
        lax.all_gather(shards[5], "dp", axis=0, tiled=True),
        lax.all_gather(shards[6], "dp", axis=0, tiled=True),
        lax.all_gather(shards[7], "dp", axis=0, tiled=True),
        lax.all_gather(shards[8], "dp", axis=0, tiled=True),
    )
    back_q, back_k, back_v, back_o, back_gate, back_up, back_down, back_gain_a, back_gain_f = (
        back_weights
    )
    gain_back_a = back_gain_a.astype(jnp.float32)
    gain_back_f = back_gain_f.astype(jnp.float32)
    totals = [jnp.zeros(weight.shape, jnp.float32) for weight in back_weights]
    grad_inputs = []
    for micro_index in range(micro):
        (
            rows_in,
            doc_row,
            cosine,
            sine,
            normed,
            query,
            key,
            value,
            logsum,
            mixed_rows,
            middle,
            normed_ffn,
            gate,
            up_value,
            hidden,
        ) = saved[micro_index]
        grad_out = out_grad[micro_index].astype(jnp.float32)
        grad_branch = grad_out.astype(jnp.bfloat16)
        totals[6] = totals[6] + jnp.einsum(
            "tf,td->fd", hidden, grad_branch, preferred_element_type=jnp.float32
        )
        grad_hidden = jnp.einsum(
            "td,fd->tf", grad_branch, back_down, preferred_element_type=jnp.float32
        )
        sigma = jax.nn.sigmoid(gate)
        grad_gate = (grad_hidden * up_value * sigma * (1.0 + gate * (1.0 - sigma))).astype(
            jnp.bfloat16
        )
        grad_up = (grad_hidden * jax.nn.silu(gate)).astype(jnp.bfloat16)
        totals[4] = totals[4] + jnp.einsum(
            "td,tf->df", normed_ffn, grad_gate, preferred_element_type=jnp.float32
        )
        totals[5] = totals[5] + jnp.einsum(
            "td,tf->df", normed_ffn, grad_up, preferred_element_type=jnp.float32
        )
        grad_normed_ffn = jnp.einsum(
            "tf,df->td", grad_gate, back_gate, preferred_element_type=jnp.float32
        )
        grad_normed_ffn = grad_normed_ffn + jnp.einsum(
            "tf,df->td", grad_up, back_up, preferred_element_type=jnp.float32
        )
        grad_gain_f, grad_middle = norm_backward(middle, gain_back_f, grad_normed_ffn)
        totals[8] = totals[8] + grad_gain_f
        grad_middle = grad_middle + grad_out
        grad_attn = grad_middle.astype(jnp.bfloat16)
        totals[3] = totals[3] + jnp.einsum(
            "ti,td->id", mixed_rows, grad_attn, preferred_element_type=jnp.float32
        )
        grad_mixed_rows = jnp.einsum(
            "td,id->ti", grad_attn, back_o, preferred_element_type=jnp.float32
        ).astype(jnp.bfloat16)
        grad_mixed = lax.all_to_all(grad_mixed_rows, "seq", split_axis=1, concat_axis=0, tiled=True)
        grad_query, grad_key, grad_value = attention_backward(
            query, key, value, doc_row, logsum, grad_mixed, cosine, sine
        )
        query_back, key_back, value_back = (
            lax.all_to_all(grad_query, "seq", split_axis=0, concat_axis=1, tiled=True),
            lax.all_to_all(grad_key, "seq", split_axis=0, concat_axis=1, tiled=True),
            lax.all_to_all(grad_value, "seq", split_axis=0, concat_axis=1, tiled=True),
        )
        totals[0] = totals[0] + jnp.einsum(
            "td,te->de", normed, query_back, preferred_element_type=jnp.float32
        )
        totals[1] = totals[1] + jnp.einsum(
            "td,te->de", normed, key_back, preferred_element_type=jnp.float32
        )
        totals[2] = totals[2] + jnp.einsum(
            "td,te->de", normed, value_back, preferred_element_type=jnp.float32
        )
        grad_normed = jnp.einsum(
            "te,de->td", query_back, back_q, preferred_element_type=jnp.float32
        )
        grad_normed = grad_normed + jnp.einsum(
            "te,de->td", key_back, back_k, preferred_element_type=jnp.float32
        )
        grad_normed = grad_normed + jnp.einsum(
            "te,de->td", value_back, back_v, preferred_element_type=jnp.float32
        )
        grad_gain_a, grad_rows = norm_backward(rows_in, gain_back_a, grad_normed)
        totals[7] = totals[7] + grad_gain_a
        grad_inputs.append(grad_rows + grad_middle)
    summed_all = (
        totals[0],
        totals[1],
        totals[2],
        totals[3],
        totals[4],
        totals[5],
        totals[6],
        totals[7],
        totals[8],
    )
    pieces = (
        lax.psum_scatter(
            summed_all[0].astype(jnp.bfloat16), "dp", scatter_dimension=0, tiled=True
        ).astype(jnp.float32),
        lax.psum_scatter(
            summed_all[1].astype(jnp.bfloat16), "dp", scatter_dimension=0, tiled=True
        ).astype(jnp.float32),
        lax.psum_scatter(
            summed_all[2].astype(jnp.bfloat16), "dp", scatter_dimension=0, tiled=True
        ).astype(jnp.float32),
        lax.psum_scatter(
            summed_all[3].astype(jnp.bfloat16), "dp", scatter_dimension=0, tiled=True
        ).astype(jnp.float32),
        lax.psum_scatter(
            summed_all[4].astype(jnp.bfloat16), "dp", scatter_dimension=0, tiled=True
        ).astype(jnp.float32),
        lax.psum_scatter(
            summed_all[5].astype(jnp.bfloat16), "dp", scatter_dimension=0, tiled=True
        ).astype(jnp.float32),
        lax.psum_scatter(
            summed_all[6].astype(jnp.bfloat16), "dp", scatter_dimension=0, tiled=True
        ).astype(jnp.float32),
        lax.psum_scatter(
            summed_all[7].astype(jnp.bfloat16), "dp", scatter_dimension=0, tiled=True
        ).astype(jnp.float32),
        lax.psum_scatter(
            summed_all[8].astype(jnp.bfloat16), "dp", scatter_dimension=0, tiled=True
        ).astype(jnp.float32),
    )
    pieces = (
        lax.psum(pieces[0].astype(jnp.bfloat16), "seq").astype(jnp.float32),
        lax.psum(pieces[1].astype(jnp.bfloat16), "seq").astype(jnp.float32),
        lax.psum(pieces[2].astype(jnp.bfloat16), "seq").astype(jnp.float32),
        lax.psum(pieces[3].astype(jnp.bfloat16), "seq").astype(jnp.float32),
        lax.psum(pieces[4].astype(jnp.bfloat16), "seq").astype(jnp.float32),
        lax.psum(pieces[5].astype(jnp.bfloat16), "seq").astype(jnp.float32),
        lax.psum(pieces[6].astype(jnp.bfloat16), "seq").astype(jnp.float32),
        lax.psum(pieces[7].astype(jnp.bfloat16), "seq").astype(jnp.float32),
        lax.psum(pieces[8].astype(jnp.bfloat16), "seq").astype(jnp.float32),
    )
    return (
        jnp.stack(results),
        jnp.stack(grad_inputs),
        pieces[0],
        pieces[1],
        pieces[2],
        pieces[3],
        pieces[4],
        pieces[5],
        pieces[6],
        pieces[7],
        pieces[8],
    )


BLK = 256
LOG2E = 1.4426950408889634


def swap_halves(v):
    lane = lax.broadcasted_iota(jnp.int32, v.shape, 1)
    width = v.shape[1]
    up = pltpu.roll(v, width - 32, axis=1)
    down = pltpu.roll(v, 32, axis=1)
    return jnp.where(lane % 64 < 32, up, down)


def nt(a, b):
    return lax.dot_general(a, b, (((1,), (1,)), ((), ())), preferred_element_type=jnp.float32)


def tn(a, b):
    return lax.dot_general(a, b, (((0,), (0,)), ((), ())), preferred_element_type=jnp.float32)


def attn_fwd_kernel(count_ref, q_ref, k_ref, v_ref, cos_ref, sin_ref, start_ref,
                    qr_ref, kr_ref, vr_ref, mixed_ref, lse_ref):
    pair = pl.program_id(0)
    cosine, sine = cos_ref[...], sin_ref[...]
    q = q_ref[...]
    qr_ref[...] = (q * cosine + swap_halves(q) * sine).astype(jnp.bfloat16)
    k = k_ref[...]
    kr_ref[...] = (k * cosine + swap_halves(k) * sine).astype(jnp.bfloat16)
    vr_ref[...] = v_ref[...].astype(jnp.bfloat16)
    length = q_ref.shape[0]
    lane = lax.broadcasted_iota(jnp.int32, (BLK, 128), 1)

    def one_block(i, carry):
        row0 = pl.multiple_of(i * BLK, BLK)
        rows = pl.ds(row0, BLK)
        for n in range(1, length // BLK + 1):
            @pl.when(count_ref[i] == n)
            def _():
                width = n * BLK
                key0 = pl.multiple_of((i - (n - 1)) * BLK, BLK)
                keys = pl.ds(key0, width)
                place = key0 + lax.broadcasted_iota(jnp.int32, (BLK, width), 1)
                own = row0 + lax.broadcasted_iota(jnp.int32, (BLK, width), 0)
                allowed = (place >= start_ref[rows, :]) & (place <= own)
                for half in range(2):
                    cols = slice(64 * half, 64 * half + 64)
                    s = nt(qr_ref[rows, cols] * jnp.bfloat16(0.125), kr_ref[keys, cols])
                    s = jnp.where(allowed, s, -1e30)
                    peak = jnp.max(s, axis=-1, keepdims=True)
                    expo = jnp.exp(s - peak)
                    total = jnp.sum(expo, axis=-1, keepdims=True)
                    out = jnp.dot(expo.astype(jnp.bfloat16), vr_ref[keys, cols],
                                  preferred_element_type=jnp.float32)
                    mixed_ref[rows, cols] = (out / total).astype(jnp.bfloat16)
                    lse = peak + jnp.log(total)
                    old = lse_ref[rows, :]
                    lse_ref[rows, :] = jnp.where(lane == 2 * pair + half, lse, old)
        return carry

    lax.fori_loop(0, length // BLK, one_block, 0)


def attn_fwd(qkv, cosine, sine, start, counts):
    length, width = qkv.shape[0], qkv.shape[1] // 3
    pairs = width // 128
    col = pl.BlockSpec((length, 128), lambda p, c: (0, p))
    key_col = pl.BlockSpec((length, 128), lambda p, c: (0, pairs + p))
    value_col = pl.BlockSpec((length, 128), lambda p, c: (0, 2 * pairs + p))
    fixed = pl.BlockSpec((length, 128), lambda p, c: (0, 0))
    scol = pl.BlockSpec((length, 1), lambda p, c: (0, 0))
    low = jax.ShapeDtypeStruct((length, width), jnp.bfloat16)
    return pl.pallas_call(
        attn_fwd_kernel,
        grid_spec=pltpu.PrefetchScalarGridSpec(
            num_scalar_prefetch=1, grid=(pairs,),
            in_specs=[col, key_col, value_col, fixed, fixed, scol],
            out_specs=[col, col, col, col, fixed],
        ),
        out_shape=[low, low, low, low, jax.ShapeDtypeStruct((length, 128), jnp.float32)],
        compiler_params=pltpu.CompilerParams(vmem_limit_bytes=40 * 1024 * 1024),
        cost_estimate=pl.CostEstimate(flops=8 * length * length * width // 2, bytes_accessed=20 * length * width,
                                      transcendentals=length * length * pairs),
        name="attn_fwd",
    )(counts, qkv, qkv, qkv, cosine, sine, start)


def attn_bwd_kernel(count_ref, q_ref, k_ref, v_ref, do_ref, cos_ref, sin_ref, start_ref, lse_ref,
                    dq_ref, dk_ref, dv_ref, dk_acc, dv_acc, dq_acc):
    length = q_ref.shape[0]
    dk_acc[...] = jnp.zeros_like(dk_acc)
    dv_acc[...] = jnp.zeros_like(dv_acc)

    def one_block(i, carry):
        row0 = pl.multiple_of(i * BLK, BLK)
        rows = pl.ds(row0, BLK)
        for n in range(1, length // BLK + 1):
            @pl.when(count_ref[i] == n)
            def _():
                width = n * BLK
                key0 = pl.multiple_of((i - (n - 1)) * BLK, BLK)
                keys = pl.ds(key0, width)
                place = key0 + lax.broadcasted_iota(jnp.int32, (width, BLK), 0)
                own = row0 + lax.broadcasted_iota(jnp.int32, (width, BLK), 1)
                allowed = (place >= start_ref[:, rows]) & (place <= own)
                for half in range(2):
                    cols = slice(64 * half, 64 * half + 64)
                    q = q_ref[rows, cols] * jnp.bfloat16(0.125)
                    k = k_ref[keys, cols]
                    do = do_ref[rows, cols]
                    s = nt(k, q)
                    probs = jnp.where(allowed, jnp.exp(s - lse_ref[0, half:half + 1, rows]), 0.0)
                    gp = nt(v_ref[keys, cols], do)
                    inner = jnp.sum(probs * gp, axis=0, keepdims=True)
                    gs = (probs * (gp - inner)).astype(jnp.bfloat16)
                    dv_acc[keys, cols] += jnp.dot(probs.astype(jnp.bfloat16), do,
                                                  preferred_element_type=jnp.float32)
                    dk_acc[keys, cols] += jnp.dot(gs, q, preferred_element_type=jnp.float32)
                    dq_acc[rows, cols] = tn(gs, k) * 0.125
        return carry

    lax.fori_loop(0, length // BLK, one_block, 0)
    cosine, sine = cos_ref[...], sin_ref[...]
    g = dq_acc[...]
    dq_ref[...] = (g * cosine - swap_halves(g) * sine).astype(jnp.bfloat16)
    g = dk_acc[...]
    dk_ref[...] = (g * cosine - swap_halves(g) * sine).astype(jnp.bfloat16)
    dv_ref[...] = dv_acc[...].astype(jnp.bfloat16)


def attn_bwd(q, k, v, grad, cosine, sine, start_row, counts, lse):
    length, width = q.shape
    pairs = width // 128
    col = pl.BlockSpec((length, 128), lambda p, c: (0, p))
    fixed = pl.BlockSpec((length, 128), lambda p, c: (0, 0))
    srow = pl.BlockSpec((1, length), lambda p, c: (0, 0))
    lrow = pl.BlockSpec((1, 2, length), lambda p, c: (p, 0, 0))
    low = jax.ShapeDtypeStruct((length, width), jnp.bfloat16)
    return pl.pallas_call(
        attn_bwd_kernel,
        grid_spec=pltpu.PrefetchScalarGridSpec(
            num_scalar_prefetch=1, grid=(pairs,),
            in_specs=[col, col, col, col, fixed, fixed, srow, lrow],
            out_specs=[col, col, col],
            scratch_shapes=[pltpu.VMEM((length, 128), jnp.float32)] * 3,
        ),
        out_shape=[low, low, low],
        compiler_params=pltpu.CompilerParams(vmem_limit_bytes=40 * 1024 * 1024),
        cost_estimate=pl.CostEstimate(flops=20 * length * length * width // 2, bytes_accessed=14 * length * width,
                                      transcendentals=length * length * pairs),
        name="attn_bwd",
    )(counts, q, k, v, grad, cosine, sine, start_row, lse)


FAST_MESH = {"dp": 8, "seq": 4}
ANY = pl.BlockSpec(memory_space=pl.ANY)


class Place:
    def __init__(self):
        self.dp, self.z = lax.axis_index("dp"), lax.axis_index("seq")
        self.core = self.dp % 2
        self.x = (self.dp // 2) % 2
        self.y = self.dp // 4
        self.over_core = self.dp + 1 - 2 * self.core
        self.over_x = self.dp + 2 - 4 * self.x
        self.over_y = self.dp + 4 - 8 * self.y
        self.middle = (self.z == 1) | (self.z == 2)


def enter(devices):
    barrier = pltpu.get_barrier_semaphore()
    for dp, seq in devices:
        pl.semaphore_signal(
            barrier, inc=1, device_id={"dp": dp, "seq": seq}, device_id_type=pl.DeviceIdType.MESH
        )
    pl.semaphore_wait(barrier, len(devices))


def remote(src, dst, send_sem, recv_sem, dp, seq):
    return pltpu.make_async_remote_copy(
        src_ref=src,
        dst_ref=dst,
        send_sem=send_sem,
        recv_sem=recv_sem,
        device_id={"dp": dp, "seq": seq},
        device_id_type=pl.DeviceIdType.MESH,
    )


def gather_kernel(
    tokens, segments, out_grad, gains, w_q, w_k, w_v, w_o, w_gate, w_up, w_down,
    x_out, seg_out, g_out, gains_out, qkv_out, o_out, ff_out, down_out,
    send, recv, local, row_send, row_recv, row_local, gain_send, gain_recv,
):
    me = Place()
    rows = tokens.shape[1]
    plane = [(lax.rem(me.dp + k, 8), me.z) for k in range(1, 8)]
    column = [
        (me.dp - me.core + core, lax.rem(me.z + k, 4)) for k in range(1, 4) for core in range(2)
    ]
    enter(plane + column)
    started = []

    def begin(copy):
        copy.start()
        started.append(copy)

    streams = ((tokens, x_out), (segments, seg_out), (out_grad, g_out))

    def place_of(ref, seq):
        return ref.at[pl.ds(rows * seq, rows)] if ref.shape[0] == 4 * rows else ref.at[seq]

    def row_copies(index):
        source, target = streams[index]
        for m in range(2):
            core, seq = me.z // 2, 2 * m + me.core
            here = (core == me.core) & (seq == me.z)

            @pl.when(here)
            def _():
                pltpu.make_async_copy(
                    source.at[m], place_of(target, me.z), row_local.at[index]
                ).start()

            @pl.when(jnp.logical_not(here))
            def _():
                remote(
                    source.at[m], place_of(target, me.z), row_send.at[index, m],
                    row_recv.at[index, me.z % 2], me.dp - me.core + core, seq,
                ).start()

    def row_wait_send(index):
        source, target = streams[index]
        for m in range(2):
            core, seq = me.z // 2, 2 * m + me.core
            here = (core == me.core) & (seq == me.z)

            @pl.when(jnp.logical_not(here))
            def _():
                remote(
                    source.at[m], place_of(target, me.z), row_send.at[index, m],
                    row_recv.at[index, me.z % 2], me.dp - me.core + core, seq,
                ).wait_send()

    def row_relay(index):
        source, target = streams[index]
        for slot in range(2):
            seq = 2 * me.core + slot
            block = place_of(target, seq)
            here = (seq == me.z) & (me.z % 2 == me.core)

            @pl.when(here)
            def _():
                pltpu.make_async_copy(block, block, row_local.at[index]).wait()

            @pl.when(jnp.logical_not(here))
            def _():
                remote(
                    block, block, row_send.at[index, slot], row_recv.at[index, slot], me.over_core, me.z
                ).wait_recv()

            begin(
                remote(
                    block, block, row_send.at[index, 2 + slot], row_recv.at[index, 2 + slot],
                    me.over_core, me.z,
                )
            )

    def row_finish(index):
        source, target = streams[index]
        for slot in range(2):
            block = place_of(target, 2 * (1 - me.core) + slot)
            remote(
                block, block, row_send.at[index, 2 + slot], row_recv.at[index, 2 + slot], me.over_core, me.z
            ).wait_recv()

    by_columns = []
    base = 0
    for source in (w_q, w_k, w_v):
        by_columns.append((source, qkv_out, base))
        base += source.shape[1] // 2
    by_columns.append((w_gate, ff_out, 0))
    by_columns.append((w_up, ff_out, w_gate.shape[1] // 2))
    by_rows = [(w_o, o_out), (w_down, down_out)]

    def column_piece(index, owner):
        source, target, first = by_columns[index]
        depth, width = source.shape[0], source.shape[1] // 2
        return target.at[pl.ds(depth * owner, depth), pl.ds(first, width)]

    def columns_start(index):
        source, target, first = by_columns[index]
        width = source.shape[1] // 2
        mine = column_piece(index, me.dp)
        for core in range(2):
            half = source.at[:, pl.ds(width * core, width)]
            begin(remote(half, mine, send.at[index, core], recv.at[index, me.core],
                         me.over_x - me.core + core, me.z))
            begin(remote(half, mine, send.at[index, 2 + core], recv.at[index, 2 + me.core],
                         me.over_y - me.core + core, me.z))

            @pl.when(core == me.core)
            def _():
                pltpu.make_async_copy(half, mine, local.at[index]).start()

            @pl.when(core != me.core)
            def _():
                remote(half, mine, send.at[index, 4], recv.at[index, 4], me.over_core, me.z).start()

    def columns_relay(index):
        piece = column_piece(index, me.over_x - me.core)
        remote(piece, piece, send.at[index, 5], recv.at[index, 0], me.over_y, me.z).wait_recv()
        begin(remote(piece, piece, send.at[index, 5], recv.at[index, 5], me.over_y, me.z))
        piece = column_piece(index, me.over_y - me.core + 1)
        remote(piece, piece, send.at[index, 6], recv.at[index, 3], me.over_x, me.z).wait_recv()
        begin(remote(piece, piece, send.at[index, 6], recv.at[index, 6], me.over_x, me.z))

    def columns_finish(index):
        source, target, first = by_columns[index]
        width = source.shape[1] // 2
        corner = me.over_x + me.over_y - me.dp - me.core
        for slot, owner in (
            (1, me.over_x - me.core + 1), (2, me.over_y - me.core), (4, me.over_core),
            (5, corner), (6, corner + 1),
        ):
            piece = column_piece(index, owner)
            remote(piece, piece, send.at[index, 5], recv.at[index, slot], me.over_core, me.z).wait_recv()
        mine = column_piece(index, me.dp)
        pltpu.make_async_copy(mine, mine, local.at[index]).wait()
        half = source.at[:, pl.ds(0, width)]
        remote(half, mine, send.at[index, 4], recv.at[index, 4], me.over_core, me.z).wait_send()

    def row_piece(which, owner):
        source, target = by_rows[which]
        depth = source.shape[0]
        return target.at[pl.ds(depth * lax.rem(owner, 4), depth), :]

    def rows_start(which):
        source, target = by_rows[which]
        index = 5 + which
        mine = row_piece(which, me.dp)
        begin(remote(source, mine, send.at[index, 0], recv.at[index, me.core],
                     me.over_x - me.core + me.y, me.z))
        begin(remote(source, mine, send.at[index, 1], recv.at[index, 2 + me.core],
                     me.over_y - me.core + me.y, me.z))

        @pl.when(me.core == me.y)
        def _():
            pltpu.make_async_copy(source, mine, local.at[index]).start()

        @pl.when(me.core != me.y)
        def _():
            remote(source, mine, send.at[index, 4], recv.at[index, 4], me.over_core, me.z).start()

    def rows_relay(which):
        index = 5 + which

        @pl.when(me.core == me.y)
        def _():
            piece = row_piece(which, me.over_x - me.core)
            remote(piece, piece, send.at[index, 5], recv.at[index, 0], me.over_y, me.z).wait_recv()
            remote(piece, piece, send.at[index, 5], recv.at[index, 5], me.over_y, me.z).start()

        @pl.when(me.core != me.y)
        def _():
            piece = row_piece(which, me.over_y - me.core + 1)
            remote(piece, piece, send.at[index, 6], recv.at[index, 3], me.over_x, me.z).wait_recv()
            remote(piece, piece, send.at[index, 6], recv.at[index, 6], me.over_x, me.z).start()

    def rows_finish(which):
        source, target = by_rows[which]
        index = 5 + which
        corner = me.over_x + me.over_y - me.dp - me.core

        def arrived(slot, owner):
            piece = row_piece(which, owner)
            remote(piece, piece, send.at[index, 5], recv.at[index, slot], me.over_core, me.z).wait_recv()

        def left(slot):
            piece = row_piece(which, me.dp)
            remote(source, piece, send.at[index, slot], recv.at[index, slot], me.over_core, me.z).wait_send()

        @pl.when(me.core == me.y)
        def _():
            arrived(1, me.over_x - me.core + 1)
            arrived(4, me.over_core)
            mine = row_piece(which, me.dp)
            pltpu.make_async_copy(source, mine, local.at[index]).wait()
            left(5)

        @pl.when(me.core != me.y)
        def _():
            arrived(2, me.over_y - me.core)
            arrived(5, corner)
            arrived(6, corner + 1)
            left(4)
            left(6)

    row_copies(0)
    row_copies(1)
    for index in range(3):
        columns_start(index)
    for k in range(1, 8):
        begin(remote(gains, gains_out.at[me.dp], gain_send.at[k - 1], gain_recv.at[k - 1],
                     lax.rem(me.dp + k, 8), me.z))
    pltpu.make_async_copy(gains, gains_out.at[me.dp], gain_recv.at[7]).start()
    rows_start(0)
    row_copies(2)
    for index in range(3):
        columns_relay(index)
    columns_start(3)
    rows_relay(0)
    columns_start(4)
    row_relay(0)
    row_relay(1)
    columns_relay(3)
    rows_start(1)
    columns_relay(4)
    row_relay(2)
    rows_relay(1)
    for index in range(5):
        columns_finish(index)
    for which in range(2):
        rows_finish(which)
    for index in range(3):
        row_finish(index)
        row_wait_send(index)
    for k in range(1, 8):
        piece = gains_out.at[lax.rem(me.dp + 8 - k, 8)]
        remote(piece, piece, gain_send.at[k - 1], gain_recv.at[k - 1], me.over_core, me.z).wait_recv()
    pltpu.make_async_copy(gains, gains_out.at[me.dp], gain_recv.at[7]).wait()
    for copy in started:
        copy.wait_send()


def gather_all(tokens, segments, out_grad, gains, weights):
    rows, width = tokens.shape[1], tokens.shape[2]
    ff = weights[4].shape[1]
    low = jnp.bfloat16
    shapes = [
        jax.ShapeDtypeStruct((4 * rows, width), low),
        jax.ShapeDtypeStruct((4,) + segments.shape[1:], jnp.int32),
        jax.ShapeDtypeStruct((4 * rows, width), low),
        jax.ShapeDtypeStruct((8,) + gains.shape, low),
        jax.ShapeDtypeStruct((width, 3 * width // 2), low),
        jax.ShapeDtypeStruct((width // 2, width), low),
        jax.ShapeDtypeStruct((width, ff), low),
        jax.ShapeDtypeStruct((ff // 2, width), low),
    ]
    dma = pltpu.SemaphoreType.DMA
    return pl.pallas_call(
        gather_kernel,
        in_specs=[ANY] * 11,
        out_specs=[ANY] * 8,
        out_shape=shapes,
        scratch_shapes=[
            dma((7, 7)), dma((7, 7)), dma((7,)), dma((3, 4)), dma((3, 4)), dma((3,)), dma((7,)), dma((8,)),
        ],
        compiler_params=pltpu.CompilerParams(collective_id=0, has_side_effects=True),
        cost_estimate=pl.CostEstimate(flops=0, bytes_accessed=500_000_000, transcendentals=0),
        name="gather_all",
    )(tokens, segments, out_grad, gains, *weights)


class ColumnJob:
    def __init__(self, me, refs, source, target, first, width, half, x_first):
        self.me, self.refs, self.x_first = me, refs, x_first
        self.source, self.target = source, target
        self.cols = pl.ds(first, width)
        which, inside = first // half, first % half
        self.out_first, self.half, self.width = 2 * half * which + inside, half, width
        self.rows = source.shape[0] // 4

    def chip_rows(self, x, y):
        return self.source.at[pl.ds(self.rows * (2 * y + x), self.rows), self.cols]

    def first_copies(self, sends_only=False):
        me, (got, keep) = self.me, (self.refs[0], self.refs[1])
        copies, loads = [], []
        for k in range(2):
            part = pl.ds(self.rows * k, self.rows)
            if self.x_first:
                sent, kept, to = self.chip_rows(1 - me.x, k), self.chip_rows(me.x, k), me.over_x
            else:
                sent, kept, to = self.chip_rows(k, 1 - me.y), self.chip_rows(k, me.y), me.over_y
            copies.append(remote(sent, got.at[part], self.sem(0, k), self.sem(1, k), to, me.z))
            if not sends_only:
                loads.append(pltpu.make_async_copy(kept, keep.at[part], self.sem(2, k)))
        return copies, loads

    def sem(self, kind, k):
        return self.refs[4].at[kind, k]

    def second_copy(self):
        me, (got, keep, second) = self.me, self.refs[:3]
        at, to = (me.y, me.over_y) if self.x_first else (me.x, me.over_x)
        part = keep.at[pl.ds(self.rows * (1 - at), self.rows)]
        return remote(part, second, self.sem(0, 2), self.sem(1, 2), to, me.z)

    def start(self):
        for copy in sum(self.first_copies(), []):
            copy.start()

    def pass_second(self):
        copies, loads = self.first_copies()
        for k in range(2):
            loads[k].wait()
            copies[k].wait_recv()
        got, keep = self.refs[:2]
        add_rows(keep, 0, got, 2 * self.rows)
        self.second_copy().start()

    def reduce_plane(self):
        me, (got, keep, second) = self.me, self.refs[:3]
        at = me.y if self.x_first else me.x
        self.second_copy().wait_recv()
        add_rows(second, self.rows * at, keep, self.rows)

    active = None

    def out_piece(self, row_first, rows, core):
        first = pl.multiple_of(self.out_first + self.half * core, 128)
        return self.target.at[pl.ds(row_first, rows), pl.ds(first, self.width)]

    def last_copy(self, final):
        me, rows = self.me, self.rows // 2
        part = final.at[pl.ds(rows * (1 - me.core), rows)]
        return remote(
            part, self.out_piece(0, rows, me.core), self.sem(0, 3), self.sem(1, 3), me.over_core, me.z
        )

    def own_copy(self, final):
        me, rows = self.me, self.rows // 2
        part = final.at[pl.ds(rows * me.core, rows)]
        return pltpu.make_async_copy(part, self.out_piece(0, rows, me.core), self.sem(2, 0))

    def finish(self, final):
        self.last_copy(final).start()
        self.own_copy(final).start()

    def drain(self, final):
        me, rows = self.me, self.rows // 2
        for copy in self.first_copies(True)[0]:
            copy.wait_send()
        self.second_copy().wait_send()
        self.last_copy(final).wait_send()
        self.own_copy(final).wait()
        part = final.at[pl.ds(rows * me.core, rows)]
        remote(
            part, self.out_piece(0, rows, 1 - me.core), self.sem(0, 3), self.sem(1, 3), me.over_core, me.z
        ).wait_recv()


class RowJob:
    def __init__(self, me, refs, source, target, first, width):
        self.me, self.refs = me, refs
        self.source, self.target = source, target
        self.cols = pl.ds(first, width)
        self.rows = source.shape[0] // 2
        self.active = me.core == me.y

    sem = ColumnJob.sem

    def first_copy(self):
        me, got = self.me, self.refs[0]
        sent = self.source.at[pl.ds(self.rows * (1 - me.x), self.rows), self.cols]
        return remote(sent, got, self.sem(0, 0), self.sem(1, 0), me.over_x, me.z)

    def load(self):
        kept = self.source.at[pl.ds(self.rows * self.me.x, self.rows), self.cols]
        return pltpu.make_async_copy(kept, self.refs[1], self.sem(2, 0))

    def second_copy(self):
        me, (got, keep, second) = self.me, self.refs[:3]
        return remote(keep, second, self.sem(0, 2), self.sem(1, 2), me.over_y, me.z)

    def start(self):
        self.first_copy().start()
        self.load().start()

    def pass_second(self):
        self.load().wait()
        self.first_copy().wait_recv()
        got, keep = self.refs[:2]
        add_rows(keep, 0, got, self.rows)

        @pl.when(jnp.logical_not(self.active))
        def _():
            self.second_copy().start()

    def reduce_plane(self):
        got, keep, second = self.refs[:3]

        @pl.when(self.active)
        def _():
            self.second_copy().wait_recv()
            add_rows(second, 0, keep, self.rows)

    def last_copy(self, final):
        me, rows = self.me, self.rows // 2
        part = final.at[pl.ds(rows * (1 - me.core), rows)]
        target = self.target.at[:, self.cols]
        return remote(part, target, self.sem(0, 3), self.sem(1, 3), me.over_core, me.z)

    def own_copy(self, final):
        me, rows = self.me, self.rows // 2
        part = final.at[pl.ds(rows * me.core, rows)]
        return pltpu.make_async_copy(part, self.target.at[:, self.cols], self.sem(2, 1))

    def finish(self, final):
        @pl.when(self.active)
        def _():
            self.last_copy(final).start()
            self.own_copy(final).start()

    def drain(self, final):
        self.first_copy().wait_send()

        @pl.when(self.active)
        def _():
            self.last_copy(final).wait_send()
            self.own_copy(final).wait()

        @pl.when(jnp.logical_not(self.active))
        def _():
            self.second_copy().wait_send()
            self.last_copy(final).wait_recv()


def add_rows(target, first, other, rows, step=64):
    def chunk(k, carry):
        at = pl.multiple_of(k * step, step)
        source = pl.multiple_of(first + k * step, step)
        target[pl.ds(at, step), :] += other[pl.ds(source, step), :]
        return carry

    lax.fori_loop(0, rows // step, chunk, 0)


def both(active, condition):
    return condition if active is None else active & condition


def final_of(job):
    return job.refs[0].at[pl.ds(0, job.rows)]


def seq_copy(job, step):
    me, total, over, sem = job.me, job.refs[2], job.refs[3], job.refs[5]
    inner = me.z + 1 - 2 * (me.z // 2)
    opposite = 3 - me.z
    outer = 3 * (me.z // 2)
    if step == 0:
        return remote(total, over.at[0], sem.at[0, 0], sem.at[1, 0], me.dp, inner)
    if step == 1:
        return remote(total, over.at[1], sem.at[0, 1], sem.at[1, 1], me.dp, opposite)
    return remote(final_of(job), final_of(job), sem.at[0, 2], sem.at[1, 2], me.dp, outer)


def plane_and_seq_first(job):
    job.reduce_plane()

    @pl.when(both(job.active, jnp.logical_not(job.me.middle)))
    def _():
        seq_copy(job, 0).start()


def seq_second(job):
    @pl.when(both(job.active, job.me.middle))
    def _():
        seq_copy(job, 0).wait_recv()
        add_rows(job.refs[2], 0, job.refs[3].at[0], job.rows)
        seq_copy(job, 1).start()


def seq_third(job):
    @pl.when(both(job.active, job.me.middle))
    def _():
        seq_copy(job, 1).wait_recv()
        final, total, over, step = final_of(job), job.refs[2], job.refs[3].at[1], 64

        def chunk(k, carry):
            part = pl.ds(pl.multiple_of(k * step, step), step)
            final[part, :] = total[part, :] + over[part, :]
            return carry

        lax.fori_loop(0, job.rows // step, chunk, 0)
        seq_copy(job, 2).start()


def finish(job):
    @pl.when(both(job.active, jnp.logical_not(job.me.middle)))
    def _():
        seq_copy(job, 2).wait_recv()

    job.finish(final_of(job))


def drain(job):
    job.drain(final_of(job))

    @pl.when(both(job.active, jnp.logical_not(job.me.middle)))
    def _():
        seq_copy(job, 0).wait_send()

    @pl.when(both(job.active, job.me.middle))
    def _():
        seq_copy(job, 1).wait_send()
        seq_copy(job, 2).wait_send()


STAGES = (
    (0, lambda job: job.start()),
    (2, lambda job: job.pass_second()),
    (3, plane_and_seq_first),
    (4, seq_second),
    (5, seq_third),
    (6, finish),
)


GAIN_HOPS = 5


class GainSums:
    def __init__(self, me, source, target, buffer, sem):
        self.me, self.source, self.target, self.buffer, self.sem = me, source, target, buffer, sem

    def hop(self, k):
        me = self.me
        across = me.z + 2 - 4 * (me.z // 2)
        beside = me.z + 1 - 2 * (me.z % 2)
        dp = (me.over_core, me.over_x, me.over_y, me.dp, me.dp)[k]
        seq = (me.z, me.z, me.z, beside, across)[k]
        return remote(
            self.buffer.at[k, 0], self.buffer.at[k, 1], self.sem.at[0, k], self.sem.at[1, k], dp, seq
        )

    def start(self):
        self.buffer[0, 0] = self.source[...]
        self.hop(0).start()

    def step(self, k):
        self.hop(k).wait_recv()
        total = self.buffer[k, 0] + self.buffer[k, 1]
        if k + 1 < GAIN_HOPS:
            self.buffer[k + 1, 0] = total
            self.hop(k + 1).start()
        else:
            self.target[...] = total

    def drain(self):
        for k in range(GAIN_HOPS):
            self.hop(k).wait_send()


class RowsBack:
    def __init__(self, me, source, target, sem):
        self.me, self.source, self.target, self.sem = me, source, target, sem

    def each(self, local, elsewhere):
        me = self.me
        rows = self.source.shape[0] // 2
        for slot in range(2):
            core, seq = me.z % 2, 2 * me.core + slot
            here = (core == me.core) & (seq == me.z)
            block, target = self.source.at[pl.ds(rows * slot, rows)], self.target.at[me.z // 2]

            @pl.when(here)
            def _():
                local(pltpu.make_async_copy(block, target, self.sem.at[2, 0]))

            @pl.when(jnp.logical_not(here))
            def _():
                elsewhere(
                    remote(
                        block, target, self.sem.at[0, slot], self.sem.at[1, me.z // 2],
                        me.dp - me.core + core, seq,
                    )
                )

    def start(self):
        self.each(lambda copy: copy.start(), lambda copy: copy.start())

    def drain(self):
        me = self.me
        self.each(lambda copy: copy.wait(), lambda copy: copy.wait_send())
        rows = self.source.shape[0] // 2
        for m in range(2):
            here = (me.z == 2 * m + me.core) & (me.core == me.z // 2)

            @pl.when(jnp.logical_not(here))
            def _():
                remote(
                    self.source.at[pl.ds(0, rows)], self.target.at[m], self.sem.at[0, 0],
                    self.sem.at[1, m], me.over_core, me.z,
                ).wait_recv()


def run_jobs(jobs, gains):
    for tick in range(len(jobs) + STAGES[-1][0]):
        for late, stage in reversed(STAGES):
            if 0 <= tick - late < len(jobs):
                stage(jobs[tick - late])
        if tick % 2 == 1 and tick // 2 < GAIN_HOPS:
            gains.step(tick // 2)
    for job in jobs:
        drain(job)
    gains.drain()


def job_plan(d_model, ff):
    half = d_model // 2
    down = [("down", 384 * k, 384, True) for k in range(d_model // 384)]
    by_y = [("ff", 512 * k, 512, False) for k in range(len(down))]
    by_turns = [("ff", 512 * k, 512, k % 2 == 0) for k in range(len(down), ff // 512)]
    rest = [("o", half, half, True), ("qkv", 0, 384, False), ("o", 0, half, True), ("qkv", 384, 384, False)]
    qkv = [("qkv", 384 * k, 384, k % 2 == 0) for k in range(2, 3 * half // 384)]
    return [job for pair in zip(down, by_y) for job in pair] + by_turns + rest + qkv


def reduce_all(g_qkv, g_o, g_ff, g_down, half_rows, gain_sums):
    d_model, ff = g_o.shape[1], g_ff.shape[1]
    plan = job_plan(d_model, ff)
    sources = {"qkv": g_qkv, "o": g_o, "ff": g_ff, "down": g_down}
    names = ("qkv", "o", "ff", "down")
    halves = {"qkv": d_model // 2, "ff": ff // 2}
    outs = [
        jax.ShapeDtypeStruct((d_model // 8, 3 * d_model), jnp.bfloat16),
        jax.ShapeDtypeStruct((d_model // 8, d_model), jnp.bfloat16),
        jax.ShapeDtypeStruct((d_model // 8, 2 * ff), jnp.bfloat16),
        jax.ShapeDtypeStruct((ff // 8, d_model), jnp.bfloat16),
        jax.ShapeDtypeStruct((2, half_rows.shape[0] // 2, d_model), jnp.bfloat16),
        jax.ShapeDtypeStruct(gain_sums.shape, jnp.float32),
    ]
    dma = pltpu.SemaphoreType.DMA
    scratch = [
        dma((3, 2)),
        pltpu.VMEM((GAIN_HOPS, 2) + gain_sums.shape, jnp.float32),
        dma((2, GAIN_HOPS)),
    ]
    for name, first, width, x_first in plan:
        by_columns = name in halves
        rows = sources[name].shape[0] // (4 if by_columns else 2)
        many = 2 * rows if by_columns else rows

        def vmem(*shape):
            return pltpu.VMEM(shape, jnp.bfloat16)

        scratch += [
            vmem(many, width), vmem(many, width), vmem(rows, width), vmem(2, rows, width), dma((3, 4)), dma((2, 3)),
        ]

    def kernel(*refs):
        source = dict(zip(names, refs[:4]))
        target = dict(zip(names, refs[6:10]))
        row_sem, gain_buffer, gain_sem = refs[12:15]
        buffers = refs[15:]
        me = Place()
        enter(
            [(me.over_core, me.z)]
            + [(me.over_x, me.z), (me.over_y, me.z)]
            + [
                (me.dp - me.core + core, lax.rem(me.z + k, 4))
                for k in range(1, 4)
                for core in range(2)
            ]
        )
        rows_back = RowsBack(me, refs[4], refs[10], row_sem)
        gains = GainSums(me, refs[5], refs[11], gain_buffer, gain_sem)
        rows_back.start()
        gains.start()
        jobs = []
        for k, (name, first, width, x_first) in enumerate(plan):
            own = buffers[6 * k : 6 * k + 6]
            if name in halves:
                jobs.append(
                    ColumnJob(me, own, source[name], target[name], first, width, halves[name], x_first)
                )
            else:
                jobs.append(RowJob(me, own, source[name], target[name], first, width))
        run_jobs(jobs, gains)
        rows_back.drain()

    return pl.pallas_call(
        kernel,
        in_specs=[ANY] * 5 + [pl.BlockSpec(memory_space=pltpu.VMEM)],
        out_specs=[ANY] * 5 + [pl.BlockSpec(memory_space=pltpu.VMEM)],
        out_shape=outs,
        scratch_shapes=scratch,
        compiler_params=pltpu.CompilerParams(
            collective_id=1, has_side_effects=True, vmem_limit_bytes=61 * 1024 * 1024
        ),
        cost_estimate=pl.CostEstimate(flops=0, bytes_accessed=800_000_000, transcendentals=0),
        name="reduce_all",
    )(g_qkv, g_o, g_ff, g_down, half_rows, gain_sums)


def swap_core(value):
    return lax.ppermute(value, "dp", [(i, i ^ 1) for i in range(8)])


def reshard_pairs(turn):
    pairs = []
    for d in range(8):
        for z in range(4):
            target = ((d & 6) | (z >> 1)) * 4 + 2 * ((turn + z) % 2) + (d & 1)
            pairs.append((target, d * 4 + z))
    return pairs


def from_sequence(half, seq_at):
    rows = half.shape[0] // 2
    early = seq_at < 2
    got = []
    for turn in range(2):
        block = jnp.where(
            early, half[rows * turn : rows * (turn + 1)], half[rows * (1 - turn) : rows * (2 - turn)]
        )
        got.append(lax.ppermute(block, ("dp", "seq"), reshard_pairs(turn)))
    even = (seq_at & 1) == 0
    return jnp.stack([jnp.where(even, got[0], got[1]), jnp.where(even, got[1], got[0])])


def dot(a, b):
    return jnp.dot(a, b, preferred_element_type=jnp.float32)


def low(value):
    return value.astype(jnp.bfloat16)


def wide(value):
    return value.astype(jnp.float32)


def column_device(
    tokens, segment_ids, out_grad, w_q, w_k, w_v, w_o, w_gate, w_up, w_down, gain_attn, gain_ffn
):
    dp_at, seq_at = lax.axis_index("dp"), lax.axis_index("seq")
    core = dp_at & 1
    rows, width = tokens.shape[1], tokens.shape[2]
    own_width = width // 2
    length = 4 * rows
    pad = -gain_attn.shape[0] % 128
    gains = jnp.pad(jnp.stack([gain_attn, gain_ffn]), ((0, 0), (0, pad)))
    x_low, docs, grad_branch, gains, full_qkv, full_o, full_ff, full_down = gather_all(
        tokens, segment_ids.reshape(2, 1, rows), out_grad, gains,
        (w_q, w_k, w_v, w_o, w_gate, w_up, w_down),
    )
    docs = docs.reshape(length)
    gains = wide(gains[:, :, : width // 8].transpose(1, 0, 2).reshape(2, width))
    gain_a, gain_f = gains[0], gains[1]
    half_ff = full_ff.shape[1] // 2

    place = jnp.arange(length, dtype=jnp.int32)
    before = jnp.concatenate([docs[:1], docs[:-1]])
    begins = (place == 0) | (docs != before)
    start = lax.cummax(jnp.where(begins, place, jnp.zeros_like(place)), axis=0)
    counts = place[: length // BLK] - start[::BLK] // BLK + 1
    cosine, sine = rope_tables(place - start, HD // 2)
    cosine = jnp.concatenate([cosine] * 4, axis=1)
    sine = jnp.concatenate([-sine, sine, -sine, sine], axis=1)

    def of_core(values, which):
        return lax.dynamic_slice_in_dim(values, length // 2 * which, length // 2, 0)

    x = wide(x_low)
    normed = low(rms_norm(x, gain_a))
    qkv_rows = dot(normed, full_qkv)
    query, key, value, mixed, logsum = attn_fwd(qkv_rows, cosine, sine, start[:, None], counts)
    logsum = logsum[:, : own_width // HD].T.reshape(own_width // 128, 2, length)
    part = dot(mixed, full_o)
    middle = x + part + wide(swap_core(low(part)))
    normed_ffn = low(rms_norm(middle, gain_f))
    gate = dot(normed_ffn, full_ff[:, :half_ff])
    up_value = dot(normed_ffn, full_ff[:, half_ff:])
    hidden = low(jax.nn.silu(gate) * up_value)
    out_other = swap_core(low(dot(of_core(hidden, 1 - core), full_down)))
    result = of_core(middle, core) + dot(of_core(hidden, core), full_down) + wide(out_other)
    result = from_sequence(low(result), seq_at)

    g_down = low(tn(hidden, grad_branch))
    grad_hidden = nt(grad_branch, full_down)
    sigma = jax.nn.sigmoid(gate)
    grad_gate = low(grad_hidden * up_value * sigma * (1.0 + gate * (1.0 - sigma)))
    grad_up = low(grad_hidden * (gate * sigma))
    grad_ff = jnp.concatenate([grad_gate, grad_up], axis=1)
    g_ff = low(tn(normed_ffn, grad_ff))
    grad_nf = nt(grad_ff, full_ff)
    grad_nf = grad_nf + wide(swap_core(low(grad_nf)))
    grad_gain_f, grad_middle = norm_backward(middle, gain_f, grad_nf)
    grad_middle = grad_middle + wide(grad_branch)
    grad_attn = low(grad_middle)

    grad_mixed = low(nt(grad_attn, full_o))
    g_o = low(tn(mixed, grad_attn))
    grad_qkv = jnp.concatenate(
        attn_bwd(query, key, value, grad_mixed, cosine, sine, start[None, :], counts, logsum), axis=1
    )
    g_qkv = low(tn(normed, grad_qkv))
    normed_other = swap_core(low(nt(of_core(grad_qkv, 1 - core), full_qkv)))
    grad_normed = nt(of_core(grad_qkv, core), full_qkv) + wide(normed_other)
    grad_gain_a, grad_rows = norm_backward(of_core(x, core), gain_a, grad_normed)
    grad_rows = grad_rows + of_core(grad_middle, core)
    gain_sums = jnp.stack([grad_gain_a, 0.5 * grad_gain_f])
    r_qkv, r_o, r_ff, r_down, grad_tokens, grad_gains = reduce_all(
        g_qkv, g_o, g_ff, g_down, low(grad_rows), gain_sums
    )
    grad_gains = lax.dynamic_slice_in_dim(grad_gains, dp_at * (width // 8), width // 8, 1)
    return (
        result,
        wide(grad_tokens),
        wide(r_qkv[:, :width]),
        wide(r_qkv[:, width : 2 * width]),
        wide(r_qkv[:, 2 * width :]),
        wide(r_o),
        wide(r_ff[:, : w_gate.shape[1]]),
        wide(r_ff[:, w_gate.shape[1] :]),
        wide(r_down),
        grad_gains[0],
        grad_gains[1],
    )


def solution(mesh):
    placed = (
        P(None, ("dp", "seq"), None),
        P(None, ("dp", "seq")),
        P(None, ("dp", "seq"), None),
        P("dp", None),
        P("dp", None),
        P("dp", None),
        P("dp", None),
        P("dp", None),
        P("dp", None),
        P("dp", None),
        P("dp"),
        P("dp"),
    )
    return jax.shard_map(
        column_device if dict(mesh.shape) == FAST_MESH else per_device,
        mesh=mesh,
        in_specs=placed,
        out_specs=(
            P(None, ("dp", "seq"), None),
            P(None, ("dp", "seq"), None),
            P("dp", None),
            P("dp", None),
            P("dp", None),
            P("dp", None),
            P("dp", None),
            P("dp", None),
            P("dp", None),
            P("dp"),
            P("dp"),
        ),
        check_vma=False,
    )
```

```python
import math

import jax
import jax.numpy as jnp
from jax import lax
from jax.experimental import pallas as pl
from jax.experimental.pallas import tpu as pltpu
from jax.sharding import PartitionSpec as P

HEADS = 24
HD = 64


EPS = 1e-05


def positions_of(doc_row):
    count = doc_row.shape[0]
    place = jnp.arange(count, dtype=jnp.int32)
    before = jnp.concatenate([doc_row[:1], doc_row[:-1]])
    starts = (place == 0) | (doc_row != before)
    first_place = lax.cummax(jnp.where(starts, place, jnp.zeros_like(place)), axis=0)
    return place - first_place


def rope_tables(where_at, half):
    inverse = jnp.exp(jnp.arange(half, dtype=jnp.float32) * (-math.log(10000.0) / half))
    angle = where_at.astype(jnp.float32)[:, None] * inverse[None, :]
    return (jnp.cos(angle), jnp.sin(angle))


def rotate(values, cosine, sine):
    half = values.shape[-1] // 2
    first, second = (values[..., :half], values[..., half:])
    cos_heads, sin_heads = (cosine[:, None, :], sine[:, None, :])
    return jnp.concatenate(
        [first * cos_heads - second * sin_heads, second * cos_heads + first * sin_heads], axis=-1
    )


def rotate_back(grads, cosine, sine):
    half = grads.shape[-1] // 2
    first, second = (grads[..., :half], grads[..., half:])
    cos_heads, sin_heads = (cosine[:, None, :], sine[:, None, :])
    return jnp.concatenate(
        [first * cos_heads + second * sin_heads, second * cos_heads - first * sin_heads], axis=-1
    )


def rms_norm(values, gain):
    return values * lax.rsqrt(jnp.mean(values * values, axis=-1, keepdims=True) + EPS) * gain


def norm_backward(values, gain, grad_normed):
    scale = lax.rsqrt(jnp.mean(values * values, axis=-1, keepdims=True) + EPS)
    unit = values * scale
    grad_gain = jnp.sum(grad_normed * unit, axis=0)
    inner = grad_normed * gain
    grad_values = scale * (inner - unit * jnp.mean(inner * unit, axis=-1, keepdims=True))
    return (grad_gain, grad_values)


def block_scores(query_heads, key_heads, doc_row, start, block):
    length = doc_row.shape[0]
    place = jnp.arange(length, dtype=jnp.int32)
    query_block = lax.dynamic_slice_in_dim(query_heads, start, block, 0)
    doc_block = lax.dynamic_slice_in_dim(doc_row, start, block, 0)
    rows_block = start + jnp.arange(block, dtype=jnp.int32)
    allowed = (doc_block[:, None] == doc_row[None, :]) & (rows_block[:, None] >= place[None, :])
    scores = (
        jnp.einsum("qhd,khd->hqk", query_block, key_heads, preferred_element_type=jnp.float32)
        * 0.125
    )
    return (query_block, jnp.where(allowed[None], scores, -1e30))


def attention_forward(query, key, value, doc_row):
    length = query.shape[0]
    head_shape = (length, query.shape[1] // HD, HD)
    query_heads, key_heads, value_heads = (
        query.reshape(head_shape),
        key.reshape(head_shape),
        value.reshape(head_shape),
    )
    block = min(512, length)
    starts = jnp.arange(length // block, dtype=jnp.int32) * block

    def one_block(start):
        unused, scores = block_scores(query_heads, key_heads, doc_row, start, block)
        peak = jnp.max(scores, axis=-1, keepdims=True)
        expo = jnp.exp(scores - peak)
        total = jnp.sum(expo, axis=-1, keepdims=True)
        probs_low = (expo / total).astype(jnp.bfloat16)
        mixed = jnp.einsum(
            "hqk,khd->qhd", probs_low, value_heads, preferred_element_type=jnp.float32
        )
        return (mixed.astype(jnp.bfloat16), (peak + jnp.log(total))[..., 0])

    mixed, logsum = lax.map(one_block, starts)
    return (mixed.reshape(length, query.shape[1]), logsum)


def attention_backward(query, key, value, doc_row, logsum, grad_mixed, cosine, sine):
    length = query.shape[0]
    head_shape = (length, query.shape[1] // HD, HD)
    query_heads, key_heads, value_heads = (
        query.reshape(head_shape),
        key.reshape(head_shape),
        value.reshape(head_shape),
    )
    grad_heads = grad_mixed.reshape(head_shape)
    block = min(512, length)
    starts = jnp.arange(length // block, dtype=jnp.int32) * block

    def one_block(carry, item):
        grad_key, grad_value = carry
        start, logsum_block = item
        query_block, scores = block_scores(query_heads, key_heads, doc_row, start, block)
        probs = jnp.exp(scores - logsum_block[..., None])
        probs_low = probs.astype(jnp.bfloat16)
        grad_block = lax.dynamic_slice_in_dim(grad_heads, start, block, 0)
        grad_probs = jnp.einsum(
            "qhd,khd->hqk", grad_block, value_heads, preferred_element_type=jnp.float32
        )
        inner = jnp.sum(probs * grad_probs, axis=-1, keepdims=True)
        grad_scores = (probs * (grad_probs - inner)).astype(jnp.bfloat16)
        grad_query = (
            jnp.einsum("hqk,khd->qhd", grad_scores, key_heads, preferred_element_type=jnp.float32)
            * 0.125
        )
        grad_key = (
            grad_key
            + jnp.einsum(
                "hqk,qhd->khd", grad_scores, query_block, preferred_element_type=jnp.float32
            )
            * 0.125
        )
        grad_value = grad_value + jnp.einsum(
            "hqk,qhd->khd", probs_low, grad_block, preferred_element_type=jnp.float32
        )
        return ((grad_key, grad_value), grad_query)

    zeros_heads = jnp.zeros(head_shape, jnp.float32)
    (grad_key, grad_value), grad_query = lax.scan(
        one_block, (zeros_heads, zeros_heads), (starts, logsum)
    )
    grad_query = rotate_back(grad_query.reshape(head_shape), cosine, sine)
    grad_key = rotate_back(grad_key, cosine, sine)
    width_here = query.shape[1]
    return (
        grad_query.reshape(length, width_here).astype(jnp.bfloat16),
        grad_key.reshape(length, width_here).astype(jnp.bfloat16),
        grad_value.reshape(length, width_here).astype(jnp.bfloat16),
    )


def per_device(
    tokens, segment_ids, out_grad, w_q, w_k, w_v, w_o, w_gate, w_up, w_down, gain_attn, gain_ffn
):
    micro, rows, width = tokens.shape
    offset = lax.axis_index("seq") * rows
    shards = (w_q, w_k, w_v, w_o, w_gate, w_up, w_down, gain_attn, gain_ffn)
    gathered = (
        lax.all_gather(shards[0], "dp", axis=0, tiled=True),
        lax.all_gather(shards[1], "dp", axis=0, tiled=True),
        lax.all_gather(shards[2], "dp", axis=0, tiled=True),
        lax.all_gather(shards[3], "dp", axis=0, tiled=True),
        lax.all_gather(shards[4], "dp", axis=0, tiled=True),
        lax.all_gather(shards[5], "dp", axis=0, tiled=True),
        lax.all_gather(shards[6], "dp", axis=0, tiled=True),
        lax.all_gather(shards[7], "dp", axis=0, tiled=True),
        lax.all_gather(shards[8], "dp", axis=0, tiled=True),
    )
    docs = lax.all_gather(segment_ids, "seq", axis=1, tiled=True)
    full_q, full_k, full_v, full_o, full_gate, full_up, full_down, full_gain_a, full_gain_f = (
        gathered
    )
    gain_a = full_gain_a.astype(jnp.float32)
    gain_f = full_gain_f.astype(jnp.float32)
    row_heads = (rows, HEADS, HD)
    saved = []
    results = []
    for micro_index in range(micro):
        rows_in = tokens[micro_index].astype(jnp.float32)
        doc_row = docs[micro_index]
        cosine, sine = rope_tables(positions_of(doc_row), HD // 2)
        own_cos = lax.dynamic_slice_in_dim(cosine, offset, rows, 0)
        own_sin = lax.dynamic_slice_in_dim(sine, offset, rows, 0)
        normed = rms_norm(rows_in, gain_a).astype(jnp.bfloat16)
        query_rows = jnp.dot(normed, full_q, preferred_element_type=jnp.float32).reshape(row_heads)
        query_rows = rotate(query_rows, own_cos, own_sin).reshape(rows, width).astype(jnp.bfloat16)
        key_rows = jnp.dot(normed, full_k, preferred_element_type=jnp.float32).reshape(row_heads)
        key_rows = rotate(key_rows, own_cos, own_sin).reshape(rows, width).astype(jnp.bfloat16)
        value_rows = jnp.dot(normed, full_v, preferred_element_type=jnp.float32).astype(
            jnp.bfloat16
        )
        query, key, value = (
            lax.all_to_all(query_rows, "seq", split_axis=1, concat_axis=0, tiled=True),
            lax.all_to_all(key_rows, "seq", split_axis=1, concat_axis=0, tiled=True),
            lax.all_to_all(value_rows, "seq", split_axis=1, concat_axis=0, tiled=True),
        )
        mixed, logsum = attention_forward(query, key, value, doc_row)
        mixed_rows = lax.all_to_all(mixed, "seq", split_axis=0, concat_axis=1, tiled=True)
        middle = rows_in + jnp.dot(mixed_rows, full_o, preferred_element_type=jnp.float32)
        normed_ffn = rms_norm(middle, gain_f).astype(jnp.bfloat16)
        gate = jnp.dot(normed_ffn, full_gate, preferred_element_type=jnp.float32)
        up_value = jnp.dot(normed_ffn, full_up, preferred_element_type=jnp.float32)
        hidden = (jax.nn.silu(gate) * up_value).astype(jnp.bfloat16)
        result = middle + jnp.dot(hidden, full_down, preferred_element_type=jnp.float32)
        results.append(result.astype(jnp.bfloat16))
        saved.append(
            (
                rows_in,
                doc_row,
                cosine,
                sine,
                normed,
                query,
                key,
                value,
                logsum,
                mixed_rows,
                middle,
                normed_ffn,
                gate,
                up_value,
                hidden,
            )
        )
    back_weights = (
        lax.all_gather(shards[0], "dp", axis=0, tiled=True),
        lax.all_gather(shards[1], "dp", axis=0, tiled=True),
        lax.all_gather(shards[2], "dp", axis=0, tiled=True),
        lax.all_gather(shards[3], "dp", axis=0, tiled=True),
        lax.all_gather(shards[4], "dp", axis=0, tiled=True),
        lax.all_gather(shards[5], "dp", axis=0, tiled=True),
        lax.all_gather(shards[6], "dp", axis=0, tiled=True),
        lax.all_gather(shards[7], "dp", axis=0, tiled=True),
        lax.all_gather(shards[8], "dp", axis=0, tiled=True),
    )
    back_q, back_k, back_v, back_o, back_gate, back_up, back_down, back_gain_a, back_gain_f = (
        back_weights
    )
    gain_back_a = back_gain_a.astype(jnp.float32)
    gain_back_f = back_gain_f.astype(jnp.float32)
    totals = [jnp.zeros(weight.shape, jnp.float32) for weight in back_weights]
    grad_inputs = []
    for micro_index in range(micro):
        (
            rows_in,
            doc_row,
            cosine,
            sine,
            normed,
            query,
            key,
            value,
            logsum,
            mixed_rows,
            middle,
            normed_ffn,
            gate,
            up_value,
            hidden,
        ) = saved[micro_index]
        grad_out = out_grad[micro_index].astype(jnp.float32)
        grad_branch = grad_out.astype(jnp.bfloat16)
        totals[6] = totals[6] + jnp.einsum(
            "tf,td->fd", hidden, grad_branch, preferred_element_type=jnp.float32
        )
        grad_hidden = jnp.einsum(
            "td,fd->tf", grad_branch, back_down, preferred_element_type=jnp.float32
        )
        sigma = jax.nn.sigmoid(gate)
        grad_gate = (grad_hidden * up_value * sigma * (1.0 + gate * (1.0 - sigma))).astype(
            jnp.bfloat16
        )
        grad_up = (grad_hidden * jax.nn.silu(gate)).astype(jnp.bfloat16)
        totals[4] = totals[4] + jnp.einsum(
            "td,tf->df", normed_ffn, grad_gate, preferred_element_type=jnp.float32
        )
        totals[5] = totals[5] + jnp.einsum(
            "td,tf->df", normed_ffn, grad_up, preferred_element_type=jnp.float32
        )
        grad_normed_ffn = jnp.einsum(
            "tf,df->td", grad_gate, back_gate, preferred_element_type=jnp.float32
        )
        grad_normed_ffn = grad_normed_ffn + jnp.einsum(
            "tf,df->td", grad_up, back_up, preferred_element_type=jnp.float32
        )
        grad_gain_f, grad_middle = norm_backward(middle, gain_back_f, grad_normed_ffn)
        totals[8] = totals[8] + grad_gain_f
        grad_middle = grad_middle + grad_out
        grad_attn = grad_middle.astype(jnp.bfloat16)
        totals[3] = totals[3] + jnp.einsum(
            "ti,td->id", mixed_rows, grad_attn, preferred_element_type=jnp.float32
        )
        grad_mixed_rows = jnp.einsum(
            "td,id->ti", grad_attn, back_o, preferred_element_type=jnp.float32
        ).astype(jnp.bfloat16)
        grad_mixed = lax.all_to_all(grad_mixed_rows, "seq", split_axis=1, concat_axis=0, tiled=True)
        grad_query, grad_key, grad_value = attention_backward(
            query, key, value, doc_row, logsum, grad_mixed, cosine, sine
        )
        query_back, key_back, value_back = (
            lax.all_to_all(grad_query, "seq", split_axis=0, concat_axis=1, tiled=True),
            lax.all_to_all(grad_key, "seq", split_axis=0, concat_axis=1, tiled=True),
            lax.all_to_all(grad_value, "seq", split_axis=0, concat_axis=1, tiled=True),
        )
        totals[0] = totals[0] + jnp.einsum(
            "td,te->de", normed, query_back, preferred_element_type=jnp.float32
        )
        totals[1] = totals[1] + jnp.einsum(
            "td,te->de", normed, key_back, preferred_element_type=jnp.float32
        )
        totals[2] = totals[2] + jnp.einsum(
            "td,te->de", normed, value_back, preferred_element_type=jnp.float32
        )
        grad_normed = jnp.einsum(
            "te,de->td", query_back, back_q, preferred_element_type=jnp.float32
        )
        grad_normed = grad_normed + jnp.einsum(
            "te,de->td", key_back, back_k, preferred_element_type=jnp.float32
        )
        grad_normed = grad_normed + jnp.einsum(
            "te,de->td", value_back, back_v, preferred_element_type=jnp.float32
        )
        grad_gain_a, grad_rows = norm_backward(rows_in, gain_back_a, grad_normed)
        totals[7] = totals[7] + grad_gain_a
        grad_inputs.append(grad_rows + grad_middle)
    summed_all = (
        totals[0],
        totals[1],
        totals[2],
        totals[3],
        totals[4],
        totals[5],
        totals[6],
        totals[7],
        totals[8],
    )
    pieces = (
        lax.psum_scatter(
            summed_all[0].astype(jnp.bfloat16), "dp", scatter_dimension=0, tiled=True
        ).astype(jnp.float32),
        lax.psum_scatter(
            summed_all[1].astype(jnp.bfloat16), "dp", scatter_dimension=0, tiled=True
        ).astype(jnp.float32),
        lax.psum_scatter(
            summed_all[2].astype(jnp.bfloat16), "dp", scatter_dimension=0, tiled=True
        ).astype(jnp.float32),
        lax.psum_scatter(
            summed_all[3].astype(jnp.bfloat16), "dp", scatter_dimension=0, tiled=True
        ).astype(jnp.float32),
        lax.psum_scatter(
            summed_all[4].astype(jnp.bfloat16), "dp", scatter_dimension=0, tiled=True
        ).astype(jnp.float32),
        lax.psum_scatter(
            summed_all[5].astype(jnp.bfloat16), "dp", scatter_dimension=0, tiled=True
        ).astype(jnp.float32),
        lax.psum_scatter(
            summed_all[6].astype(jnp.bfloat16), "dp", scatter_dimension=0, tiled=True
        ).astype(jnp.float32),
        lax.psum_scatter(
            summed_all[7].astype(jnp.bfloat16), "dp", scatter_dimension=0, tiled=True
        ).astype(jnp.float32),
        lax.psum_scatter(
            summed_all[8].astype(jnp.bfloat16), "dp", scatter_dimension=0, tiled=True
        ).astype(jnp.float32),
    )
    pieces = (
        lax.psum(pieces[0].astype(jnp.bfloat16), "seq").astype(jnp.float32),
        lax.psum(pieces[1].astype(jnp.bfloat16), "seq").astype(jnp.float32),
        lax.psum(pieces[2].astype(jnp.bfloat16), "seq").astype(jnp.float32),
        lax.psum(pieces[3].astype(jnp.bfloat16), "seq").astype(jnp.float32),
        lax.psum(pieces[4].astype(jnp.bfloat16), "seq").astype(jnp.float32),
        lax.psum(pieces[5].astype(jnp.bfloat16), "seq").astype(jnp.float32),
        lax.psum(pieces[6].astype(jnp.bfloat16), "seq").astype(jnp.float32),
        lax.psum(pieces[7].astype(jnp.bfloat16), "seq").astype(jnp.float32),
        lax.psum(pieces[8].astype(jnp.bfloat16), "seq").astype(jnp.float32),
    )
    return (
        jnp.stack(results),
        jnp.stack(grad_inputs),
        pieces[0],
        pieces[1],
        pieces[2],
        pieces[3],
        pieces[4],
        pieces[5],
        pieces[6],
        pieces[7],
        pieces[8],
    )


BLK = 256
LOG2E = 1.4426950408889634


def swap_halves(v):
    lane = lax.broadcasted_iota(jnp.int32, v.shape, 1)
    width = v.shape[1]
    up = pltpu.roll(v, width - 32, axis=1)
    down = pltpu.roll(v, 32, axis=1)
    return jnp.where(lane % 64 < 32, up, down)


def nt(a, b):
    return lax.dot_general(a, b, (((1,), (1,)), ((), ())), preferred_element_type=jnp.float32)


def tn(a, b):
    return lax.dot_general(a, b, (((0,), (0,)), ((), ())), preferred_element_type=jnp.float32)


def attn_fwd_kernel(count_ref, q_ref, k_ref, v_ref, cos_ref, sin_ref, start_ref,
                    qr_ref, kr_ref, vr_ref, mixed_ref, lse_ref):
    pair = pl.program_id(0)
    cosine, sine = cos_ref[...], sin_ref[...]
    q = q_ref[...]
    qr_ref[...] = (q * cosine + swap_halves(q) * sine).astype(jnp.bfloat16)
    k = k_ref[...]
    kr_ref[...] = (k * cosine + swap_halves(k) * sine).astype(jnp.bfloat16)
    vr_ref[...] = v_ref[...].astype(jnp.bfloat16)
    length = q_ref.shape[0]
    lane = lax.broadcasted_iota(jnp.int32, (BLK, 128), 1)

    def one_block(i, carry):
        row0 = pl.multiple_of(i * BLK, BLK)
        rows = pl.ds(row0, BLK)
        for n in range(1, length // BLK + 1):
            @pl.when(count_ref[i] == n)
            def _():
                width = n * BLK
                key0 = pl.multiple_of((i - (n - 1)) * BLK, BLK)
                keys = pl.ds(key0, width)
                place = key0 + lax.broadcasted_iota(jnp.int32, (BLK, width), 1)
                own = row0 + lax.broadcasted_iota(jnp.int32, (BLK, width), 0)
                allowed = (place >= start_ref[rows, :]) & (place <= own)
                for half in range(2):
                    cols = slice(64 * half, 64 * half + 64)
                    s = nt(qr_ref[rows, cols] * jnp.bfloat16(0.125), kr_ref[keys, cols])
                    s = jnp.where(allowed, s, -1e30)
                    peak = jnp.max(s, axis=-1, keepdims=True)
                    expo = jnp.exp(s - peak)
                    total = jnp.sum(expo, axis=-1, keepdims=True)
                    out = jnp.dot(expo.astype(jnp.bfloat16), vr_ref[keys, cols],
                                  preferred_element_type=jnp.float32)
                    mixed_ref[rows, cols] = (out / total).astype(jnp.bfloat16)
                    lse = peak + jnp.log(total)
                    old = lse_ref[rows, :]
                    lse_ref[rows, :] = jnp.where(lane == 2 * pair + half, lse, old)
        return carry

    lax.fori_loop(0, length // BLK, one_block, 0)


def attn_fwd(qkv, cosine, sine, start, counts):
    length, width = qkv.shape[0], qkv.shape[1] // 3
    pairs = width // 128
    col = pl.BlockSpec((length, 128), lambda p, c: (0, p))
    key_col = pl.BlockSpec((length, 128), lambda p, c: (0, pairs + p))
    value_col = pl.BlockSpec((length, 128), lambda p, c: (0, 2 * pairs + p))
    fixed = pl.BlockSpec((length, 128), lambda p, c: (0, 0))
    scol = pl.BlockSpec((length, 1), lambda p, c: (0, 0))
    low = jax.ShapeDtypeStruct((length, width), jnp.bfloat16)
    return pl.pallas_call(
        attn_fwd_kernel,
        grid_spec=pltpu.PrefetchScalarGridSpec(
            num_scalar_prefetch=1, grid=(pairs,),
            in_specs=[col, key_col, value_col, fixed, fixed, scol],
            out_specs=[col, col, col, col, fixed],
        ),
        out_shape=[low, low, low, low, jax.ShapeDtypeStruct((length, 128), jnp.float32)],
        compiler_params=pltpu.CompilerParams(vmem_limit_bytes=40 * 1024 * 1024),
        cost_estimate=pl.CostEstimate(flops=8 * length * length * width // 2, bytes_accessed=20 * length * width,
                                      transcendentals=length * length * pairs),
        name="attn_fwd",
    )(counts, qkv, qkv, qkv, cosine, sine, start)


def attn_bwd_kernel(count_ref, q_ref, k_ref, v_ref, do_ref, cos_ref, sin_ref, start_ref, lse_ref,
                    dq_ref, dk_ref, dv_ref, dk_acc, dv_acc, dq_acc):
    length = q_ref.shape[0]
    dk_acc[...] = jnp.zeros_like(dk_acc)
    dv_acc[...] = jnp.zeros_like(dv_acc)

    def one_block(i, carry):
        row0 = pl.multiple_of(i * BLK, BLK)
        rows = pl.ds(row0, BLK)
        for n in range(1, length // BLK + 1):
            @pl.when(count_ref[i] == n)
            def _():
                width = n * BLK
                key0 = pl.multiple_of((i - (n - 1)) * BLK, BLK)
                keys = pl.ds(key0, width)
                place = key0 + lax.broadcasted_iota(jnp.int32, (width, BLK), 0)
                own = row0 + lax.broadcasted_iota(jnp.int32, (width, BLK), 1)
                allowed = (place >= start_ref[:, rows]) & (place <= own)
                for half in range(2):
                    cols = slice(64 * half, 64 * half + 64)
                    q = q_ref[rows, cols] * jnp.bfloat16(0.125)
                    k = k_ref[keys, cols]
                    do = do_ref[rows, cols]
                    s = nt(k, q)
                    probs = jnp.where(allowed, jnp.exp(s - lse_ref[0, half:half + 1, rows]), 0.0)
                    gp = nt(v_ref[keys, cols], do)
                    inner = jnp.sum(probs * gp, axis=0, keepdims=True)
                    gs = (probs * (gp - inner)).astype(jnp.bfloat16)
                    dv_acc[keys, cols] += jnp.dot(probs.astype(jnp.bfloat16), do,
                                                  preferred_element_type=jnp.float32)
                    dk_acc[keys, cols] += jnp.dot(gs, q, preferred_element_type=jnp.float32)
                    dq_acc[rows, cols] = tn(gs, k) * 0.125
        return carry

    lax.fori_loop(0, length // BLK, one_block, 0)
    cosine, sine = cos_ref[...], sin_ref[...]
    g = dq_acc[...]
    dq_ref[...] = (g * cosine - swap_halves(g) * sine).astype(jnp.bfloat16)
    g = dk_acc[...]
    dk_ref[...] = (g * cosine - swap_halves(g) * sine).astype(jnp.bfloat16)
    dv_ref[...] = dv_acc[...].astype(jnp.bfloat16)


def attn_bwd(q, k, v, grad, cosine, sine, start_row, counts, lse):
    length, width = q.shape
    pairs = width // 128
    col = pl.BlockSpec((length, 128), lambda p, c: (0, p))
    fixed = pl.BlockSpec((length, 128), lambda p, c: (0, 0))
    srow = pl.BlockSpec((1, length), lambda p, c: (0, 0))
    lrow = pl.BlockSpec((1, 2, length), lambda p, c: (p, 0, 0))
    low = jax.ShapeDtypeStruct((length, width), jnp.bfloat16)
    return pl.pallas_call(
        attn_bwd_kernel,
        grid_spec=pltpu.PrefetchScalarGridSpec(
            num_scalar_prefetch=1, grid=(pairs,),
            in_specs=[col, col, col, col, fixed, fixed, srow, lrow],
            out_specs=[col, col, col],
            scratch_shapes=[pltpu.VMEM((length, 128), jnp.float32)] * 3,
        ),
        out_shape=[low, low, low],
        compiler_params=pltpu.CompilerParams(vmem_limit_bytes=40 * 1024 * 1024),
        cost_estimate=pl.CostEstimate(flops=20 * length * length * width // 2, bytes_accessed=14 * length * width,
                                      transcendentals=length * length * pairs),
        name="attn_bwd",
    )(counts, q, k, v, grad, cosine, sine, start_row, lse)


FAST_MESH = {"dp": 8, "seq": 4}
ANY = pl.BlockSpec(memory_space=pl.ANY)


class Place:
    def __init__(self):
        self.dp, self.z = lax.axis_index("dp"), lax.axis_index("seq")
        self.core = self.dp % 2
        self.x = (self.dp // 2) % 2
        self.y = self.dp // 4
        self.over_core = self.dp + 1 - 2 * self.core
        self.over_x = self.dp + 2 - 4 * self.x
        self.over_y = self.dp + 4 - 8 * self.y
        self.middle = (self.z == 1) | (self.z == 2)


def enter(devices):
    barrier = pltpu.get_barrier_semaphore()
    for dp, seq in devices:
        pl.semaphore_signal(
            barrier, inc=1, device_id={"dp": dp, "seq": seq}, device_id_type=pl.DeviceIdType.MESH
        )
    pl.semaphore_wait(barrier, len(devices))


def remote(src, dst, send_sem, recv_sem, dp, seq):
    return pltpu.make_async_remote_copy(
        src_ref=src,
        dst_ref=dst,
        send_sem=send_sem,
        recv_sem=recv_sem,
        device_id={"dp": dp, "seq": seq},
        device_id_type=pl.DeviceIdType.MESH,
    )


def gather_kernel(
    tokens, segments, out_grad, gains, cosine, sine, w_q, w_k, w_v, w_o, w_gate, w_up, w_down,
    x_out, seg_out, g_out, gains_out, qkv_out, o_out, ff_out, down_out,
    normed_out, heads_out, mixed_out, lse_out, middle_out, nf_out, slope_gate_out, slope_up_out,
    hidden_out, g_down_out, start_out,
    send, recv, local, row_send, row_recv, row_local, gain_send, gain_recv,
    x_v, seg_v, gains_v, normed_v, w_qkv_v, heads_v, mixed_v, w_o_v, middle_v, part_send, part_recv,
    nf_v, w_ff_v, branch_v, tile_v, g_tile_v, lse_v, start_v,
    part_sem, load_sem, w_sem, tile_sem, store_sem,
):
    me = Place()
    rows = tokens.shape[1]
    plane = [(lax.rem(me.dp + k, 8), me.z) for k in range(1, 8)]
    column = [
        (me.dp - me.core + core, lax.rem(me.z + k, 4)) for k in range(1, 4) for core in range(2)
    ]
    enter(plane + column)
    started = []

    def begin(copy):
        copy.start()
        started.append(copy)

    streams = ((tokens, x_out), (segments, seg_out), (out_grad, g_out))

    def place_of(ref, seq):
        return ref.at[pl.ds(rows * seq, rows)] if ref.shape[0] == 4 * rows else ref.at[seq]

    def row_copies(index):
        source, target = streams[index]
        for m in range(2):
            core, seq = me.z // 2, 2 * m + me.core
            here = (core == me.core) & (seq == me.z)

            @pl.when(here)
            def _():
                pltpu.make_async_copy(
                    source.at[m], place_of(target, me.z), row_local.at[index]
                ).start()

            @pl.when(jnp.logical_not(here))
            def _():
                remote(
                    source.at[m], place_of(target, me.z), row_send.at[index, m],
                    row_recv.at[index, me.z % 2], me.dp - me.core + core, seq,
                ).start()

    def row_wait_send(index):
        source, target = streams[index]
        for m in range(2):
            core, seq = me.z // 2, 2 * m + me.core
            here = (core == me.core) & (seq == me.z)

            @pl.when(jnp.logical_not(here))
            def _():
                remote(
                    source.at[m], place_of(target, me.z), row_send.at[index, m],
                    row_recv.at[index, me.z % 2], me.dp - me.core + core, seq,
                ).wait_send()

    def row_relay(index):
        source, target = streams[index]
        for slot in range(2):
            seq = 2 * me.core + slot
            block = place_of(target, seq)
            here = (seq == me.z) & (me.z % 2 == me.core)

            @pl.when(here)
            def _():
                pltpu.make_async_copy(block, block, row_local.at[index]).wait()

            @pl.when(jnp.logical_not(here))
            def _():
                remote(
                    block, block, row_send.at[index, slot], row_recv.at[index, slot], me.over_core, me.z
                ).wait_recv()

            begin(
                remote(
                    block, block, row_send.at[index, 2 + slot], row_recv.at[index, 2 + slot],
                    me.over_core, me.z,
                )
            )

    def row_finish(index):
        source, target = streams[index]
        for slot in range(2):
            block = place_of(target, 2 * (1 - me.core) + slot)
            remote(
                block, block, row_send.at[index, 2 + slot], row_recv.at[index, 2 + slot], me.over_core, me.z
            ).wait_recv()

    by_columns = []
    base = 0
    for source in (w_q, w_k, w_v):
        by_columns.append((source, qkv_out, base))
        base += source.shape[1] // 2
    by_columns.append((w_gate, ff_out, 0))
    by_columns.append((w_up, ff_out, w_gate.shape[1] // 2))
    by_rows = [(w_o, o_out), (w_down, down_out)]

    def column_piece(index, owner):
        source, target, first = by_columns[index]
        depth, width = source.shape[0], source.shape[1] // 2
        return target.at[pl.ds(depth * owner, depth), pl.ds(first, width)]

    def columns_start(index):
        source, target, first = by_columns[index]
        width = source.shape[1] // 2
        mine = column_piece(index, me.dp)
        for core in range(2):
            half = source.at[:, pl.ds(width * core, width)]
            begin(remote(half, mine, send.at[index, core], recv.at[index, me.core],
                         me.over_x - me.core + core, me.z))
            begin(remote(half, mine, send.at[index, 2 + core], recv.at[index, 2 + me.core],
                         me.over_y - me.core + core, me.z))

            @pl.when(core == me.core)
            def _():
                pltpu.make_async_copy(half, mine, local.at[index]).start()

            @pl.when(core != me.core)
            def _():
                remote(half, mine, send.at[index, 4], recv.at[index, 4], me.over_core, me.z).start()

    def columns_relay(index):
        piece = column_piece(index, me.over_x - me.core)
        remote(piece, piece, send.at[index, 5], recv.at[index, 0], me.over_y, me.z).wait_recv()
        begin(remote(piece, piece, send.at[index, 5], recv.at[index, 5], me.over_y, me.z))
        piece = column_piece(index, me.over_y - me.core + 1)
        remote(piece, piece, send.at[index, 6], recv.at[index, 3], me.over_x, me.z).wait_recv()
        begin(remote(piece, piece, send.at[index, 6], recv.at[index, 6], me.over_x, me.z))

    def columns_finish(index):
        source, target, first = by_columns[index]
        width = source.shape[1] // 2
        corner = me.over_x + me.over_y - me.dp - me.core
        for slot, owner in (
            (1, me.over_x - me.core + 1), (2, me.over_y - me.core), (4, me.over_core),
            (5, corner), (6, corner + 1),
        ):
            piece = column_piece(index, owner)
            remote(piece, piece, send.at[index, 5], recv.at[index, slot], me.over_core, me.z).wait_recv()
        mine = column_piece(index, me.dp)
        pltpu.make_async_copy(mine, mine, local.at[index]).wait()
        half = source.at[:, pl.ds(0, width)]
        remote(half, mine, send.at[index, 4], recv.at[index, 4], me.over_core, me.z).wait_send()

    def row_piece(which, owner):
        source, target = by_rows[which]
        depth = source.shape[0]
        return target.at[pl.ds(depth * lax.rem(owner, 4), depth), :]

    def rows_start(which):
        source, target = by_rows[which]
        index = 5 + which
        mine = row_piece(which, me.dp)
        begin(remote(source, mine, send.at[index, 0], recv.at[index, me.core],
                     me.over_x - me.core + me.y, me.z))
        begin(remote(source, mine, send.at[index, 1], recv.at[index, 2 + me.core],
                     me.over_y - me.core + me.y, me.z))

        @pl.when(me.core == me.y)
        def _():
            pltpu.make_async_copy(source, mine, local.at[index]).start()

        @pl.when(me.core != me.y)
        def _():
            remote(source, mine, send.at[index, 4], recv.at[index, 4], me.over_core, me.z).start()

    def rows_relay(which):
        index = 5 + which

        @pl.when(me.core == me.y)
        def _():
            piece = row_piece(which, me.over_x - me.core)
            remote(piece, piece, send.at[index, 5], recv.at[index, 0], me.over_y, me.z).wait_recv()
            remote(piece, piece, send.at[index, 5], recv.at[index, 5], me.over_y, me.z).start()

        @pl.when(me.core != me.y)
        def _():
            piece = row_piece(which, me.over_y - me.core + 1)
            remote(piece, piece, send.at[index, 6], recv.at[index, 3], me.over_x, me.z).wait_recv()
            remote(piece, piece, send.at[index, 6], recv.at[index, 6], me.over_x, me.z).start()

    def rows_finish(which):
        source, target = by_rows[which]
        index = 5 + which
        corner = me.over_x + me.over_y - me.dp - me.core

        def arrived(slot, owner):
            piece = row_piece(which, owner)
            remote(piece, piece, send.at[index, 5], recv.at[index, slot], me.over_core, me.z).wait_recv()

        def left(slot):
            piece = row_piece(which, me.dp)
            remote(source, piece, send.at[index, slot], recv.at[index, slot], me.over_core, me.z).wait_send()

        @pl.when(me.core == me.y)
        def _():
            arrived(1, me.over_x - me.core + 1)
            arrived(4, me.over_core)
            mine = row_piece(which, me.dp)
            pltpu.make_async_copy(source, mine, local.at[index]).wait()
            left(5)

        @pl.when(me.core != me.y)
        def _():
            arrived(2, me.over_y - me.core)
            arrived(5, corner)
            arrived(6, corner + 1)
            left(4)
            left(6)

    def load(source, target, k):
        return pltpu.make_async_copy(source, target, load_sem.at[k])

    stores = []

    def store(source, target):
        copy = pltpu.make_async_copy(source, target, store_sem.at[len(stores)])
        stores.append(copy)
        copy.start()

    length, width = x_v.shape
    own_width = width // 2
    half_ff = ff_out.shape[1] // 2

    row_copies(0)
    row_copies(1)
    for index in range(3):
        columns_start(index)
    for k in range(1, 8):
        begin(remote(gains, gains_out.at[me.dp], gain_send.at[k - 1], gain_recv.at[k - 1],
                     lax.rem(me.dp + k, 8), me.z))
    pltpu.make_async_copy(gains, gains_out.at[me.dp], gain_recv.at[7]).start()
    row_copies(2)
    for index in range(3):
        columns_relay(index)
    rows_start(0)
    row_relay(0)
    row_relay(1)
    for k in range(1, 8):
        piece = gains_out.at[lax.rem(me.dp + 8 - k, 8)]
        remote(piece, piece, gain_send.at[k - 1], gain_recv.at[k - 1], me.over_core, me.z).wait_recv()
    pltpu.make_async_copy(gains, gains_out.at[me.dp], gain_recv.at[7]).wait()
    load(gains_out, gains_v, 0).start()
    row_finish(1)
    load(seg_out, seg_v, 1).start()
    row_finish(0)
    load(x_out, x_v, 2).start()
    load(gains_out, gains_v, 0).wait()
    load(seg_out, seg_v, 1).wait()
    load(x_out, x_v, 2).wait()
    both_gains = gains_v[0].astype(jnp.float32)
    for k in range(1, 8):
        both_gains = both_gains + gains_v[k].astype(jnp.float32)
    gain_a, gain_f = both_gains[0:1], both_gains[1:2]

    norm_rows(lambda part: x_v[part, :].astype(jnp.float32), gain_a, normed_v, length)
    store(normed_v, normed_out)

    docs = jnp.concatenate([seg_v[k] for k in range(4)], axis=1)
    for k in range(4):
        square = lax.broadcasted_iota(jnp.int32, (rows, rows), 0) == lax.broadcasted_iota(
            jnp.int32, (rows, rows), 1
        )
        ids = jnp.sum(jnp.where(square, seg_v[k], 0), axis=1, keepdims=True)
        start_v[pl.ds(rows * k, rows), :] = jnp.sum(
            jnp.where(docs < ids, 1, 0), axis=1, keepdims=True
        )
    store(start_v, start_out)

    for index in range(3):
        columns_finish(index)
    columns_start(3)
    columns_start(4)
    rows_relay(0)
    tile = 256
    tiles = own_width // tile
    for t in range(tiles):
        for kind in range(3):
            part = pl.ds(own_width * kind + tile * t, tile)
            pltpu.make_async_copy(qkv_out.at[:, part], w_qkv_v.at[:, part], w_sem.at[kind, t]).start()
    for t in range(tiles):
        for kind in range(3):
            part = pl.ds(own_width * kind + tile * t, tile)
            pltpu.make_async_copy(qkv_out.at[:, part], w_qkv_v.at[:, part], w_sem.at[kind, t]).wait()
            product = jnp.dot(normed_v[...], w_qkv_v[:, part], preferred_element_type=jnp.float32)
            for k in range(tile // 128):
                piece = product[:, 128 * k : 128 * k + 128]
                if kind < 2:
                    piece = piece * cosine[...] + swap_halves(piece) * sine[...]
                heads_v[:, pl.ds(own_width * kind + tile * t + 128 * k, 128)] = piece.astype(jnp.bfloat16)

        def pair_step(pair, carry):
            attend(pair, own_width, heads_v, start_v, mixed_v, lse_v)
            return carry

        lax.fori_loop(tile // 128 * t, tile // 128 * (t + 1), pair_step, 0)
        if t == 0:
            row_relay(2)
        if t == 1:
            rows_start(1)
    store(heads_v, heads_out)
    store(mixed_v, mixed_out)
    store(lse_v, lse_out)

    rows_finish(0)
    load(o_out, w_o_v, 0).start()
    row_finish(2)
    load(g_out, branch_v, 1).start()
    load(o_out, w_o_v, 0).wait()
    chunk = width // 3

    def part_copy(k):
        part = pl.ds(chunk * k, chunk)
        return remote(
            part_send.at[:, part], part_recv.at[:, part], part_sem.at[0, k], part_sem.at[1, k], me.over_core, me.z
        )

    for k in range(3):
        for at in range(chunk * k, chunk * (k + 1), tile):
            part = pl.ds(at, tile)
            product = jnp.dot(mixed_v[...], w_o_v[:, part], preferred_element_type=jnp.float32)
            part_send[:, part] = product.astype(jnp.bfloat16)
            middle_v[:, part] = x_v[:, part].astype(jnp.float32) + product
        part_copy(k).start()
    columns_relay(3)
    columns_relay(4)
    for k in range(3):
        part_copy(k).wait_recv()

    def middle_rows(part):
        value = middle_v[part, :] + part_recv[part, :].astype(jnp.float32)
        middle_v[part, :] = value
        return value

    norm_rows(middle_rows, gain_f, nf_v, length)
    store(middle_v, middle_out)
    store(nf_v, nf_out)
    load(g_out, branch_v, 1).wait()
    rows_relay(1)
    columns_finish(3)
    columns_finish(4)

    def ff_load(n, slot, kind):
        first = pl.multiple_of(half_ff * kind + tile * n, 128)
        return pltpu.make_async_copy(
            ff_out.at[:, pl.ds(first, tile)], w_ff_v.at[slot, kind], tile_sem.at[0, slot, kind]
        )

    def tile_store(n, slot, kind):
        part = pl.ds(pl.multiple_of(tile * n, 128), tile)
        target = (slope_gate_out, slope_up_out, hidden_out)[kind]
        return pltpu.make_async_copy(tile_v.at[slot, kind], target.at[:, part], tile_sem.at[1, slot, kind])

    def grad_store(n, slot):
        part = pl.ds(pl.multiple_of(tile * n, tile), tile)
        return pltpu.make_async_copy(g_tile_v.at[slot], g_down_out.at[part, :], tile_sem.at[2, slot, 0])

    count = half_ff // tile
    for kind in range(2):
        ff_load(0, 0, kind).start()

    def ff_step(n, carry):
        slot = lax.rem(n, 2)
        for kind in range(2):
            ff_load(n, slot, kind).wait()

        @pl.when(n + 1 < count)
        def _():
            for kind in range(2):
                ff_load(n + 1, 1 - slot, kind).start()

        @pl.when(n >= 2)
        def _():
            for kind in range(3):
                tile_store(n - 2, slot, kind).wait()
            grad_store(n - 2, slot).wait()

        gate = jnp.dot(nf_v[...], w_ff_v[slot, 0], preferred_element_type=jnp.float32)
        up_value = jnp.dot(nf_v[...], w_ff_v[slot, 1], preferred_element_type=jnp.float32)
        sigma = jax.nn.sigmoid(gate)
        silu = gate * sigma
        tile_v[slot, 0] = (up_value * sigma * (1.0 + gate * (1.0 - sigma))).astype(jnp.bfloat16)
        tile_v[slot, 1] = silu.astype(jnp.bfloat16)
        hidden = (silu * up_value).astype(jnp.bfloat16)
        tile_v[slot, 2] = hidden
        g_tile_v[slot] = jnp.dot(
            hidden.T, branch_v[...], preferred_element_type=jnp.float32
        ).astype(jnp.bfloat16)
        for kind in range(3):
            tile_store(n, slot, kind).start()
        grad_store(n, slot).start()
        return carry

    lax.fori_loop(0, count, ff_step, 0)
    for n in range(count - 2, count):
        for kind in range(3):
            tile_store(n, n % 2, kind).wait()
        grad_store(n, n % 2).wait()
    rows_finish(1)
    for copy in stores:
        copy.wait()
    for k in range(3):
        part_copy(k).wait_send()
    for index in range(3):
        row_wait_send(index)
    for copy in started:
        copy.wait_send()


def norm_rows(read, gain, target, length, step=64):
    def chunk(k, carry):
        part = pl.ds(pl.multiple_of(k * step, step), step)
        values = read(part)
        scale = lax.rsqrt(jnp.mean(values * values, axis=-1, keepdims=True) + EPS)
        target[part, :] = (values * scale * gain).astype(target.dtype)
        return carry

    lax.fori_loop(0, length // step, chunk, 0)


def attend(pair, width, heads, start, mixed, lse):
    length = heads.shape[0]
    lane = lax.broadcasted_iota(jnp.int32, (BLK, 128), 1)
    cols = [pl.ds(pl.multiple_of(width * kind + 128 * pair, 128), 128) for kind in range(3)]
    for i in range(length // BLK):
        own_rows, keys = slice(BLK * i, BLK * (i + 1)), BLK * (i + 1)
        place = lax.broadcasted_iota(jnp.int32, (BLK, keys), 1)
        own = BLK * i + lax.broadcasted_iota(jnp.int32, (BLK, keys), 0)
        allowed = (place >= start[own_rows, :]) & (place <= own)
        query = heads[own_rows, cols[0]] * jnp.bfloat16(0.125)
        key, value = heads[0:keys, cols[1]], heads[0:keys, cols[2]]
        kept = lse[own_rows, :]
        outs = []
        for half in range(2):
            part = slice(64 * half, 64 * half + 64)
            scores = jnp.where(allowed, nt(query[:, part], key[:, part]), -1e30)
            peak = jnp.max(scores, axis=-1, keepdims=True)
            expo = jnp.exp(scores - peak)
            total = jnp.sum(expo, axis=-1, keepdims=True)
            out = jnp.dot(expo.astype(jnp.bfloat16), value[:, part], preferred_element_type=jnp.float32)
            outs.append((out / total).astype(jnp.bfloat16))
            kept = jnp.where(lane == 2 * pair + half, peak + jnp.log(total), kept)
        mixed[own_rows, cols[0]] = jnp.concatenate(outs, axis=1)
        lse[own_rows, :] = kept


def gather_all(tokens, segments, out_grad, gains, cosine, sine, weights):
    rows, width = tokens.shape[1], tokens.shape[2]
    length, half, ff = 4 * rows, width // 2, weights[4].shape[1]
    half_ff = ff // 2
    low = jnp.bfloat16

    def shape(*dims, dtype=low):
        return jax.ShapeDtypeStruct(dims, dtype)

    shapes = [
        shape(length, width),
        shape(4, *segments.shape[1:], dtype=jnp.int32),
        shape(length, width),
        shape(8, *gains.shape),
        shape(width, 3 * half),
        shape(half, width),
        shape(width, ff),
        shape(half_ff, width),
        shape(length, width),
        shape(length, 3 * half),
        shape(length, half),
        shape(length, 128, dtype=jnp.float32),
        shape(length, width, dtype=jnp.float32),
        shape(length, width),
        shape(length, half_ff),
        shape(length, half_ff),
        shape(length, half_ff),
        shape(half_ff, width),
        shape(length, 1, dtype=jnp.int32),
    ]
    dma, vmem = pltpu.SemaphoreType.DMA, pltpu.VMEM
    whole = pl.BlockSpec(memory_space=pltpu.VMEM)
    return pl.pallas_call(
        gather_kernel,
        in_specs=[ANY] * 4 + [whole] * 2 + [ANY] * 7,
        out_specs=[ANY] * len(shapes),
        out_shape=shapes,
        scratch_shapes=[
            dma((7, 7)), dma((7, 7)), dma((7,)), dma((3, 4)), dma((3, 4)), dma((3,)), dma((7,)), dma((8,)),
            vmem((length, width), low),
            vmem((4,) + segments.shape[1:], jnp.int32),
            vmem((8,) + gains.shape, low),
            vmem((length, width), low),
            vmem((width, 3 * half), low),
            vmem((length, 3 * half), low),
            vmem((length, half), low),
            vmem((half, width), low),
            vmem((length, width), jnp.float32),
            vmem((length, width), low),
            vmem((length, width), low),
            vmem((length, width), low),
            vmem((2, 2, width, 256), low),
            vmem((length, width), low),
            vmem((2, 3, length, 256), low),
            vmem((2, 256, width), low),
            vmem((length, 128), jnp.float32),
            vmem((length, 1), jnp.int32),
            dma((2, 3)), dma((3,)), dma((3, 3)), dma((3, 2, 3)), dma((7,)),
        ],
        compiler_params=pltpu.CompilerParams(
            collective_id=0, has_side_effects=True, vmem_limit_bytes=61 * 1024 * 1024
        ),
        cost_estimate=pl.CostEstimate(flops=0, bytes_accessed=500_000_000, transcendentals=0),
        name="gather_all",
    )(tokens, segments, out_grad, gains, cosine, sine, *weights)


class ColumnJob:
    def __init__(self, me, refs, source, target, first, width, half, x_first):
        self.me, self.refs, self.x_first = me, refs, x_first
        self.source, self.target = source, target
        self.cols = pl.ds(first, width)
        which, inside = first // half, first % half
        self.out_first, self.half, self.width = 2 * half * which + inside, half, width
        self.rows = source.shape[0] // 4

    def chip_rows(self, x, y):
        return self.source.at[pl.ds(self.rows * (2 * y + x), self.rows), self.cols]

    def first_copies(self, sends_only=False):
        me, (got, keep) = self.me, (self.refs[0], self.refs[1])
        copies, loads = [], []
        for k in range(2):
            part = pl.ds(self.rows * k, self.rows)
            if self.x_first:
                sent, kept, to = self.chip_rows(1 - me.x, k), self.chip_rows(me.x, k), me.over_x
            else:
                sent, kept, to = self.chip_rows(k, 1 - me.y), self.chip_rows(k, me.y), me.over_y
            copies.append(remote(sent, got.at[part], self.sem(0, k), self.sem(1, k), to, me.z))
            if not sends_only:
                loads.append(pltpu.make_async_copy(kept, keep.at[part], self.sem(2, k)))
        return copies, loads

    def sem(self, kind, k):
        return self.refs[4].at[kind, k]

    def second_copy(self):
        me, (got, keep, second) = self.me, self.refs[:3]
        at, to = (me.y, me.over_y) if self.x_first else (me.x, me.over_x)
        part = keep.at[pl.ds(self.rows * (1 - at), self.rows)]
        return remote(part, second, self.sem(0, 2), self.sem(1, 2), to, me.z)

    def start(self):
        for copy in sum(self.first_copies(), []):
            copy.start()

    def pass_second(self):
        copies, loads = self.first_copies()
        for k in range(2):
            loads[k].wait()
            copies[k].wait_recv()
        got, keep = self.refs[:2]
        add_rows(keep, 0, got, 2 * self.rows)
        self.second_copy().start()

    def reduce_plane(self):
        me, (got, keep, second) = self.me, self.refs[:3]
        at = me.y if self.x_first else me.x
        self.second_copy().wait_recv()
        add_rows(second, self.rows * at, keep, self.rows)

    active = None

    def out_piece(self, row_first, rows, core):
        first = pl.multiple_of(self.out_first + self.half * core, 128)
        return self.target.at[pl.ds(row_first, rows), pl.ds(first, self.width)]

    def last_copy(self, final):
        me, rows = self.me, self.rows // 2
        part = final.at[pl.ds(rows * (1 - me.core), rows)]
        return remote(
            part, self.out_piece(0, rows, me.core), self.sem(0, 3), self.sem(1, 3), me.over_core, me.z
        )

    def own_copy(self, final):
        me, rows = self.me, self.rows // 2
        part = final.at[pl.ds(rows * me.core, rows)]
        return pltpu.make_async_copy(part, self.out_piece(0, rows, me.core), self.sem(2, 0))

    def finish(self, final):
        self.last_copy(final).start()
        self.own_copy(final).start()

    def drain(self, final):
        me, rows = self.me, self.rows // 2
        for copy in self.first_copies(True)[0]:
            copy.wait_send()
        self.second_copy().wait_send()
        self.last_copy(final).wait_send()
        self.own_copy(final).wait()
        part = final.at[pl.ds(rows * me.core, rows)]
        remote(
            part, self.out_piece(0, rows, 1 - me.core), self.sem(0, 3), self.sem(1, 3), me.over_core, me.z
        ).wait_recv()


class RowJob:
    def __init__(self, me, refs, source, target, first, width):
        self.me, self.refs = me, refs
        self.source, self.target = source, target
        self.cols = pl.ds(first, width)
        self.rows = source.shape[0] // 2
        self.active = me.core == me.y

    sem = ColumnJob.sem

    def first_copy(self):
        me, got = self.me, self.refs[0]
        sent = self.source.at[pl.ds(self.rows * (1 - me.x), self.rows), self.cols]
        return remote(sent, got, self.sem(0, 0), self.sem(1, 0), me.over_x, me.z)

    def load(self):
        kept = self.source.at[pl.ds(self.rows * self.me.x, self.rows), self.cols]
        return pltpu.make_async_copy(kept, self.refs[1], self.sem(2, 0))

    def second_copy(self):
        me, (got, keep, second) = self.me, self.refs[:3]
        return remote(keep, second, self.sem(0, 2), self.sem(1, 2), me.over_y, me.z)

    def start(self):
        self.first_copy().start()
        self.load().start()

    def pass_second(self):
        self.load().wait()
        self.first_copy().wait_recv()
        got, keep = self.refs[:2]
        add_rows(keep, 0, got, self.rows)

        @pl.when(jnp.logical_not(self.active))
        def _():
            self.second_copy().start()

    def reduce_plane(self):
        got, keep, second = self.refs[:3]

        @pl.when(self.active)
        def _():
            self.second_copy().wait_recv()
            add_rows(second, 0, keep, self.rows)

    def last_copy(self, final):
        me, rows = self.me, self.rows // 2
        part = final.at[pl.ds(rows * (1 - me.core), rows)]
        target = self.target.at[:, self.cols]
        return remote(part, target, self.sem(0, 3), self.sem(1, 3), me.over_core, me.z)

    def own_copy(self, final):
        me, rows = self.me, self.rows // 2
        part = final.at[pl.ds(rows * me.core, rows)]
        return pltpu.make_async_copy(part, self.target.at[:, self.cols], self.sem(2, 1))

    def finish(self, final):
        @pl.when(self.active)
        def _():
            self.last_copy(final).start()
            self.own_copy(final).start()

    def drain(self, final):
        self.first_copy().wait_send()

        @pl.when(self.active)
        def _():
            self.last_copy(final).wait_send()
            self.own_copy(final).wait()

        @pl.when(jnp.logical_not(self.active))
        def _():
            self.second_copy().wait_send()
            self.last_copy(final).wait_recv()


def add_rows(target, first, other, rows, step=64):
    def chunk(k, carry):
        at = pl.multiple_of(k * step, step)
        source = pl.multiple_of(first + k * step, step)
        target[pl.ds(at, step), :] += other[pl.ds(source, step), :]
        return carry

    lax.fori_loop(0, rows // step, chunk, 0)


def both(active, condition):
    return condition if active is None else active & condition


def final_of(job):
    return job.refs[0].at[pl.ds(0, job.rows)]


def seq_copy(job, step):
    me, total, over, sem = job.me, job.refs[2], job.refs[3], job.refs[5]
    inner = me.z + 1 - 2 * (me.z // 2)
    opposite = 3 - me.z
    outer = 3 * (me.z // 2)
    if step == 0:
        return remote(total, over.at[0], sem.at[0, 0], sem.at[1, 0], me.dp, inner)
    if step == 1:
        return remote(total, over.at[1], sem.at[0, 1], sem.at[1, 1], me.dp, opposite)
    return remote(final_of(job), final_of(job), sem.at[0, 2], sem.at[1, 2], me.dp, outer)


def plane_and_seq_first(job):
    job.reduce_plane()

    @pl.when(both(job.active, jnp.logical_not(job.me.middle)))
    def _():
        seq_copy(job, 0).start()


def seq_second(job):
    @pl.when(both(job.active, job.me.middle))
    def _():
        seq_copy(job, 0).wait_recv()
        add_rows(job.refs[2], 0, job.refs[3].at[0], job.rows)
        seq_copy(job, 1).start()


def seq_third(job):
    @pl.when(both(job.active, job.me.middle))
    def _():
        seq_copy(job, 1).wait_recv()
        final, total, over, step = final_of(job), job.refs[2], job.refs[3].at[1], 64

        def chunk(k, carry):
            part = pl.ds(pl.multiple_of(k * step, step), step)
            final[part, :] = total[part, :] + over[part, :]
            return carry

        lax.fori_loop(0, job.rows // step, chunk, 0)
        seq_copy(job, 2).start()


def finish(job):
    @pl.when(both(job.active, jnp.logical_not(job.me.middle)))
    def _():
        seq_copy(job, 2).wait_recv()

    job.finish(final_of(job))


def drain(job):
    job.drain(final_of(job))

    @pl.when(both(job.active, jnp.logical_not(job.me.middle)))
    def _():
        seq_copy(job, 0).wait_send()

    @pl.when(both(job.active, job.me.middle))
    def _():
        seq_copy(job, 1).wait_send()
        seq_copy(job, 2).wait_send()


STAGES = (
    (0, lambda job: job.start()),
    (2, lambda job: job.pass_second()),
    (3, plane_and_seq_first),
    (4, seq_second),
    (5, seq_third),
    (6, finish),
)


GAIN_HOPS = 5


class GainSums:
    def __init__(self, me, source, target, buffer, sem):
        self.me, self.source, self.target, self.buffer, self.sem = me, source, target, buffer, sem

    def hop(self, k):
        me = self.me
        across = me.z + 2 - 4 * (me.z // 2)
        beside = me.z + 1 - 2 * (me.z % 2)
        dp = (me.over_core, me.over_x, me.over_y, me.dp, me.dp)[k]
        seq = (me.z, me.z, me.z, beside, across)[k]
        return remote(
            self.buffer.at[k, 0], self.buffer.at[k, 1], self.sem.at[0, k], self.sem.at[1, k], dp, seq
        )

    def start(self):
        self.buffer[0, 0] = self.source[...]
        self.hop(0).start()

    def step(self, k):
        self.hop(k).wait_recv()
        total = self.buffer[k, 0] + self.buffer[k, 1]
        if k + 1 < GAIN_HOPS:
            self.buffer[k + 1, 0] = total
            self.hop(k + 1).start()
        else:
            self.target[...] = total

    def drain(self):
        for k in range(GAIN_HOPS):
            self.hop(k).wait_send()


class RowsBack:
    def __init__(self, me, source, target, sem):
        self.me, self.source, self.target, self.sem = me, source, target, sem

    def each(self, local, elsewhere):
        me = self.me
        rows = self.source.shape[0] // 2
        for slot in range(2):
            core, seq = me.z % 2, 2 * me.core + slot
            here = (core == me.core) & (seq == me.z)
            block, target = self.source.at[pl.ds(rows * slot, rows)], self.target.at[me.z // 2]

            @pl.when(here)
            def _():
                local(pltpu.make_async_copy(block, target, self.sem.at[2, 0]))

            @pl.when(jnp.logical_not(here))
            def _():
                elsewhere(
                    remote(
                        block, target, self.sem.at[0, slot], self.sem.at[1, me.z // 2],
                        me.dp - me.core + core, seq,
                    )
                )

    def start(self):
        self.each(lambda copy: copy.start(), lambda copy: copy.start())

    def drain(self):
        me = self.me
        self.each(lambda copy: copy.wait(), lambda copy: copy.wait_send())
        rows = self.source.shape[0] // 2
        for m in range(2):
            here = (me.z == 2 * m + me.core) & (me.core == me.z // 2)

            @pl.when(jnp.logical_not(here))
            def _():
                remote(
                    self.source.at[pl.ds(0, rows)], self.target.at[m], self.sem.at[0, 0],
                    self.sem.at[1, m], me.over_core, me.z,
                ).wait_recv()


def run_jobs(jobs, gains):
    for tick in range(len(jobs) + STAGES[-1][0]):
        for late, stage in reversed(STAGES):
            if 0 <= tick - late < len(jobs):
                stage(jobs[tick - late])
        if tick % 2 == 1 and tick // 2 < GAIN_HOPS:
            gains.step(tick // 2)
    for job in jobs:
        drain(job)
    gains.drain()


def job_plan(d_model, ff):
    half = d_model // 2
    down = [("down", 384 * k, 384, True) for k in range(d_model // 384)]
    by_y = [("ff", 512 * k, 512, False) for k in range(len(down))]
    by_turns = [("ff", 512 * k, 512, k % 2 == 0) for k in range(len(down), ff // 512)]
    rest = [("o", half, half, True), ("qkv", 0, 384, False), ("o", 0, half, True), ("qkv", 384, 384, False)]
    qkv = [("qkv", 384 * k, 384, k % 2 == 0) for k in range(2, 3 * half // 384)]
    return [job for pair in zip(down, by_y) for job in pair] + by_turns + rest + qkv


def reduce_all(g_qkv, g_o, g_ff, g_down, half_rows, gain_sums):
    d_model, ff = g_o.shape[1], g_ff.shape[1]
    plan = job_plan(d_model, ff)
    sources = {"qkv": g_qkv, "o": g_o, "ff": g_ff, "down": g_down}
    names = ("qkv", "o", "ff", "down")
    halves = {"qkv": d_model // 2, "ff": ff // 2}
    outs = [
        jax.ShapeDtypeStruct((d_model // 8, 3 * d_model), jnp.bfloat16),
        jax.ShapeDtypeStruct((d_model // 8, d_model), jnp.bfloat16),
        jax.ShapeDtypeStruct((d_model // 8, 2 * ff), jnp.bfloat16),
        jax.ShapeDtypeStruct((ff // 8, d_model), jnp.bfloat16),
        jax.ShapeDtypeStruct((2, half_rows.shape[0] // 2, d_model), jnp.bfloat16),
        jax.ShapeDtypeStruct(gain_sums.shape, jnp.float32),
    ]
    dma = pltpu.SemaphoreType.DMA
    scratch = [
        dma((3, 2)),
        pltpu.VMEM((GAIN_HOPS, 2) + gain_sums.shape, jnp.float32),
        dma((2, GAIN_HOPS)),
    ]
    for name, first, width, x_first in plan:
        by_columns = name in halves
        rows = sources[name].shape[0] // (4 if by_columns else 2)
        many = 2 * rows if by_columns else rows

        def vmem(*shape):
            return pltpu.VMEM(shape, jnp.bfloat16)

        scratch += [
            vmem(many, width), vmem(many, width), vmem(rows, width), vmem(2, rows, width), dma((3, 4)), dma((2, 3)),
        ]

    def kernel(*refs):
        source = dict(zip(names, refs[:4]))
        target = dict(zip(names, refs[6:10]))
        row_sem, gain_buffer, gain_sem = refs[12:15]
        buffers = refs[15:]
        me = Place()
        enter(
            [(me.over_core, me.z)]
            + [(me.over_x, me.z), (me.over_y, me.z)]
            + [
                (me.dp - me.core + core, lax.rem(me.z + k, 4))
                for k in range(1, 4)
                for core in range(2)
            ]
        )
        rows_back = RowsBack(me, refs[4], refs[10], row_sem)
        gains = GainSums(me, refs[5], refs[11], gain_buffer, gain_sem)
        rows_back.start()
        gains.start()
        jobs = []
        for k, (name, first, width, x_first) in enumerate(plan):
            own = buffers[6 * k : 6 * k + 6]
            if name in halves:
                jobs.append(
                    ColumnJob(me, own, source[name], target[name], first, width, halves[name], x_first)
                )
            else:
                jobs.append(RowJob(me, own, source[name], target[name], first, width))
        run_jobs(jobs, gains)
        rows_back.drain()

    return pl.pallas_call(
        kernel,
        in_specs=[ANY] * 5 + [pl.BlockSpec(memory_space=pltpu.VMEM)],
        out_specs=[ANY] * 5 + [pl.BlockSpec(memory_space=pltpu.VMEM)],
        out_shape=outs,
        scratch_shapes=scratch,
        compiler_params=pltpu.CompilerParams(
            collective_id=1, has_side_effects=True, vmem_limit_bytes=61 * 1024 * 1024
        ),
        cost_estimate=pl.CostEstimate(flops=0, bytes_accessed=800_000_000, transcendentals=0),
        name="reduce_all",
    )(g_qkv, g_o, g_ff, g_down, half_rows, gain_sums)


def swap_core(value):
    return lax.ppermute(value, "dp", [(i, i ^ 1) for i in range(8)])


def reshard_pairs(turn):
    pairs = []
    for d in range(8):
        for z in range(4):
            target = ((d & 6) | (z >> 1)) * 4 + 2 * ((turn + z) % 2) + (d & 1)
            pairs.append((target, d * 4 + z))
    return pairs


def from_sequence(half, seq_at):
    rows = half.shape[0] // 2
    early = seq_at < 2
    got = []
    for turn in range(2):
        block = jnp.where(
            early, half[rows * turn : rows * (turn + 1)], half[rows * (1 - turn) : rows * (2 - turn)]
        )
        got.append(lax.ppermute(block, ("dp", "seq"), reshard_pairs(turn)))
    even = (seq_at & 1) == 0
    return jnp.stack([jnp.where(even, got[0], got[1]), jnp.where(even, got[1], got[0])])


def dot(a, b):
    return jnp.dot(a, b, preferred_element_type=jnp.float32)


def low(value):
    return value.astype(jnp.bfloat16)


def wide(value):
    return value.astype(jnp.float32)


def column_device(
    tokens, segment_ids, out_grad, w_q, w_k, w_v, w_o, w_gate, w_up, w_down, gain_attn, gain_ffn
):
    dp_at, seq_at = lax.axis_index("dp"), lax.axis_index("seq")
    core = dp_at & 1
    rows, width = tokens.shape[1], tokens.shape[2]
    own_width = width // 2
    length = 4 * rows
    gains = lax.dynamic_update_slice_in_dim(
        jnp.zeros((2, width), jnp.bfloat16),
        jnp.stack([gain_attn, gain_ffn]),
        dp_at * gain_attn.shape[0],
        1,
    )
    place = jnp.arange(length, dtype=jnp.int32)
    cosine, sine = rope_tables(place, HD // 2)
    cosine = jnp.concatenate([cosine] * 4, axis=1)
    sine = jnp.concatenate([-sine, sine, -sine, sine], axis=1)
    (
        x_low, docs, grad_branch, gains, full_qkv, full_o, full_ff, full_down, normed, heads, mixed,
        logsum, middle, normed_ffn, slope_gate, slope_up, hidden, g_down, start,
    ) = gather_all(
        tokens, segment_ids.reshape(2, 1, rows), out_grad, gains, cosine, sine,
        (w_q, w_k, w_v, w_o, w_gate, w_up, w_down),
    )
    gains = jnp.sum(wide(gains), axis=0)
    gain_a, gain_f = gains[0], gains[1]
    start = start.reshape(length)
    counts = place[: length // BLK] - start[::BLK] // BLK + 1
    logsum = logsum[:, : own_width // HD].T.reshape(own_width // 128, 2, length)
    query, key, value = jnp.split(heads, 3, axis=1)
    x = wide(x_low)

    def of_core(values, which):
        return lax.dynamic_slice_in_dim(values, length // 2 * which, length // 2, 0)

    out_other = swap_core(low(dot(of_core(hidden, 1 - core), full_down)))
    result = of_core(middle, core) + dot(of_core(hidden, core), full_down) + wide(out_other)
    result = from_sequence(low(result), seq_at)

    grad_hidden = nt(grad_branch, full_down)
    grad_ff = jnp.concatenate(
        [low(grad_hidden * wide(slope_gate)), low(grad_hidden * wide(slope_up))], axis=1
    )
    g_ff = low(tn(normed_ffn, grad_ff))
    grad_nf = nt(grad_ff, full_ff)
    grad_nf = grad_nf + wide(swap_core(low(grad_nf)))
    grad_gain_f, grad_middle = norm_backward(middle, gain_f, grad_nf)
    grad_middle = grad_middle + wide(grad_branch)
    grad_attn = low(grad_middle)

    grad_mixed = low(nt(grad_attn, full_o))
    g_o = low(tn(mixed, grad_attn))
    grad_qkv = jnp.concatenate(
        attn_bwd(query, key, value, grad_mixed, cosine, sine, start[None, :], counts, logsum), axis=1
    )
    g_qkv = low(tn(normed, grad_qkv))
    normed_other = swap_core(low(nt(of_core(grad_qkv, 1 - core), full_qkv)))
    grad_normed = nt(of_core(grad_qkv, core), full_qkv) + wide(normed_other)
    grad_gain_a, grad_rows = norm_backward(of_core(x, core), gain_a, grad_normed)
    grad_rows = grad_rows + of_core(grad_middle, core)
    gain_sums = jnp.stack([grad_gain_a, 0.5 * grad_gain_f])
    r_qkv, r_o, r_ff, r_down, grad_tokens, grad_gains = reduce_all(
        g_qkv, g_o, g_ff, g_down, low(grad_rows), gain_sums
    )
    grad_gains = lax.dynamic_slice_in_dim(grad_gains, dp_at * (width // 8), width // 8, 1)
    return (
        result,
        wide(grad_tokens),
        wide(r_qkv[:, :width]),
        wide(r_qkv[:, width : 2 * width]),
        wide(r_qkv[:, 2 * width :]),
        wide(r_o),
        wide(r_ff[:, : w_gate.shape[1]]),
        wide(r_ff[:, w_gate.shape[1] :]),
        wide(r_down),
        grad_gains[0],
        grad_gains[1],
    )


def solution(mesh):
    placed = (
        P(None, ("dp", "seq"), None),
        P(None, ("dp", "seq")),
        P(None, ("dp", "seq"), None),
        P("dp", None),
        P("dp", None),
        P("dp", None),
        P("dp", None),
        P("dp", None),
        P("dp", None),
        P("dp", None),
        P("dp"),
        P("dp"),
    )
    return jax.shard_map(
        column_device if dict(mesh.shape) == FAST_MESH else per_device,
        mesh=mesh,
        in_specs=placed,
        out_specs=(
            P(None, ("dp", "seq"), None),
            P(None, ("dp", "seq"), None),
            P("dp", None),
            P("dp", None),
            P("dp", None),
            P("dp", None),
            P("dp", None),
            P("dp", None),
            P("dp", None),
            P("dp"),
            P("dp"),
        ),
        check_vma=False,
    )
```

```python
import functools
import math

import jax
import jax.numpy as jnp
import numpy as np
from jax import lax
from jax.experimental import pallas as pl
from jax.experimental.pallas import tpu as pltpu
from jax.sharding import PartitionSpec as P

HEADS = 24
HD = 64


EPS = 1e-05


def positions_of(doc_row):
    count = doc_row.shape[0]
    place = jnp.arange(count, dtype=jnp.int32)
    before = jnp.concatenate([doc_row[:1], doc_row[:-1]])
    starts = (place == 0) | (doc_row != before)
    first_place = lax.cummax(jnp.where(starts, place, jnp.zeros_like(place)), axis=0)
    return place - first_place


def rope_tables(where_at, half):
    inverse = jnp.exp(jnp.arange(half, dtype=jnp.float32) * (-math.log(10000.0) / half))
    angle = where_at.astype(jnp.float32)[:, None] * inverse[None, :]
    return (jnp.cos(angle), jnp.sin(angle))


def rotate(values, cosine, sine):
    half = values.shape[-1] // 2
    first, second = (values[..., :half], values[..., half:])
    cos_heads, sin_heads = (cosine[:, None, :], sine[:, None, :])
    return jnp.concatenate(
        [first * cos_heads - second * sin_heads, second * cos_heads + first * sin_heads], axis=-1
    )


def rotate_back(grads, cosine, sine):
    half = grads.shape[-1] // 2
    first, second = (grads[..., :half], grads[..., half:])
    cos_heads, sin_heads = (cosine[:, None, :], sine[:, None, :])
    return jnp.concatenate(
        [first * cos_heads + second * sin_heads, second * cos_heads - first * sin_heads], axis=-1
    )


def rms_norm(values, gain):
    return values * lax.rsqrt(jnp.mean(values * values, axis=-1, keepdims=True) + EPS) * gain


def norm_backward(values, gain, grad_normed):
    scale = lax.rsqrt(jnp.mean(values * values, axis=-1, keepdims=True) + EPS)
    unit = values * scale
    grad_gain = jnp.sum(grad_normed * unit, axis=0)
    inner = grad_normed * gain
    grad_values = scale * (inner - unit * jnp.mean(inner * unit, axis=-1, keepdims=True))
    return (grad_gain, grad_values)


def block_scores(query_heads, key_heads, doc_row, start, block):
    length = doc_row.shape[0]
    place = jnp.arange(length, dtype=jnp.int32)
    query_block = lax.dynamic_slice_in_dim(query_heads, start, block, 0)
    doc_block = lax.dynamic_slice_in_dim(doc_row, start, block, 0)
    rows_block = start + jnp.arange(block, dtype=jnp.int32)
    allowed = (doc_block[:, None] == doc_row[None, :]) & (rows_block[:, None] >= place[None, :])
    scores = (
        jnp.einsum("qhd,khd->hqk", query_block, key_heads, preferred_element_type=jnp.float32)
        * 0.125
    )
    return (query_block, jnp.where(allowed[None], scores, -1e30))


def attention_forward(query, key, value, doc_row):
    length = query.shape[0]
    head_shape = (length, query.shape[1] // HD, HD)
    query_heads, key_heads, value_heads = (
        query.reshape(head_shape),
        key.reshape(head_shape),
        value.reshape(head_shape),
    )
    block = min(512, length)
    starts = jnp.arange(length // block, dtype=jnp.int32) * block

    def one_block(start):
        unused, scores = block_scores(query_heads, key_heads, doc_row, start, block)
        peak = jnp.max(scores, axis=-1, keepdims=True)
        expo = jnp.exp(scores - peak)
        total = jnp.sum(expo, axis=-1, keepdims=True)
        probs_low = (expo / total).astype(jnp.bfloat16)
        mixed = jnp.einsum(
            "hqk,khd->qhd", probs_low, value_heads, preferred_element_type=jnp.float32
        )
        return (mixed.astype(jnp.bfloat16), (peak + jnp.log(total))[..., 0])

    mixed, logsum = lax.map(one_block, starts)
    return (mixed.reshape(length, query.shape[1]), logsum)


def attention_backward(query, key, value, doc_row, logsum, grad_mixed, cosine, sine):
    length = query.shape[0]
    head_shape = (length, query.shape[1] // HD, HD)
    query_heads, key_heads, value_heads = (
        query.reshape(head_shape),
        key.reshape(head_shape),
        value.reshape(head_shape),
    )
    grad_heads = grad_mixed.reshape(head_shape)
    block = min(512, length)
    starts = jnp.arange(length // block, dtype=jnp.int32) * block

    def one_block(carry, item):
        grad_key, grad_value = carry
        start, logsum_block = item
        query_block, scores = block_scores(query_heads, key_heads, doc_row, start, block)
        probs = jnp.exp(scores - logsum_block[..., None])
        probs_low = probs.astype(jnp.bfloat16)
        grad_block = lax.dynamic_slice_in_dim(grad_heads, start, block, 0)
        grad_probs = jnp.einsum(
            "qhd,khd->hqk", grad_block, value_heads, preferred_element_type=jnp.float32
        )
        inner = jnp.sum(probs * grad_probs, axis=-1, keepdims=True)
        grad_scores = (probs * (grad_probs - inner)).astype(jnp.bfloat16)
        grad_query = (
            jnp.einsum("hqk,khd->qhd", grad_scores, key_heads, preferred_element_type=jnp.float32)
            * 0.125
        )
        grad_key = (
            grad_key
            + jnp.einsum(
                "hqk,qhd->khd", grad_scores, query_block, preferred_element_type=jnp.float32
            )
            * 0.125
        )
        grad_value = grad_value + jnp.einsum(
            "hqk,qhd->khd", probs_low, grad_block, preferred_element_type=jnp.float32
        )
        return ((grad_key, grad_value), grad_query)

    zeros_heads = jnp.zeros(head_shape, jnp.float32)
    (grad_key, grad_value), grad_query = lax.scan(
        one_block, (zeros_heads, zeros_heads), (starts, logsum)
    )
    grad_query = rotate_back(grad_query.reshape(head_shape), cosine, sine)
    grad_key = rotate_back(grad_key, cosine, sine)
    width_here = query.shape[1]
    return (
        grad_query.reshape(length, width_here).astype(jnp.bfloat16),
        grad_key.reshape(length, width_here).astype(jnp.bfloat16),
        grad_value.reshape(length, width_here).astype(jnp.bfloat16),
    )


def per_device(
    tokens, segment_ids, out_grad, w_q, w_k, w_v, w_o, w_gate, w_up, w_down, gain_attn, gain_ffn
):
    micro, rows, width = tokens.shape
    offset = lax.axis_index("seq") * rows
    shards = (w_q, w_k, w_v, w_o, w_gate, w_up, w_down, gain_attn, gain_ffn)
    gathered = (
        lax.all_gather(shards[0], "dp", axis=0, tiled=True),
        lax.all_gather(shards[1], "dp", axis=0, tiled=True),
        lax.all_gather(shards[2], "dp", axis=0, tiled=True),
        lax.all_gather(shards[3], "dp", axis=0, tiled=True),
        lax.all_gather(shards[4], "dp", axis=0, tiled=True),
        lax.all_gather(shards[5], "dp", axis=0, tiled=True),
        lax.all_gather(shards[6], "dp", axis=0, tiled=True),
        lax.all_gather(shards[7], "dp", axis=0, tiled=True),
        lax.all_gather(shards[8], "dp", axis=0, tiled=True),
    )
    docs = lax.all_gather(segment_ids, "seq", axis=1, tiled=True)
    full_q, full_k, full_v, full_o, full_gate, full_up, full_down, full_gain_a, full_gain_f = (
        gathered
    )
    gain_a = full_gain_a.astype(jnp.float32)
    gain_f = full_gain_f.astype(jnp.float32)
    row_heads = (rows, HEADS, HD)
    saved = []
    results = []
    for micro_index in range(micro):
        rows_in = tokens[micro_index].astype(jnp.float32)
        doc_row = docs[micro_index]
        cosine, sine = rope_tables(positions_of(doc_row), HD // 2)
        own_cos = lax.dynamic_slice_in_dim(cosine, offset, rows, 0)
        own_sin = lax.dynamic_slice_in_dim(sine, offset, rows, 0)
        normed = rms_norm(rows_in, gain_a).astype(jnp.bfloat16)
        query_rows = jnp.dot(normed, full_q, preferred_element_type=jnp.float32).reshape(row_heads)
        query_rows = rotate(query_rows, own_cos, own_sin).reshape(rows, width).astype(jnp.bfloat16)
        key_rows = jnp.dot(normed, full_k, preferred_element_type=jnp.float32).reshape(row_heads)
        key_rows = rotate(key_rows, own_cos, own_sin).reshape(rows, width).astype(jnp.bfloat16)
        value_rows = jnp.dot(normed, full_v, preferred_element_type=jnp.float32).astype(
            jnp.bfloat16
        )
        query, key, value = (
            lax.all_to_all(query_rows, "seq", split_axis=1, concat_axis=0, tiled=True),
            lax.all_to_all(key_rows, "seq", split_axis=1, concat_axis=0, tiled=True),
            lax.all_to_all(value_rows, "seq", split_axis=1, concat_axis=0, tiled=True),
        )
        mixed, logsum = attention_forward(query, key, value, doc_row)
        mixed_rows = lax.all_to_all(mixed, "seq", split_axis=0, concat_axis=1, tiled=True)
        middle = rows_in + jnp.dot(mixed_rows, full_o, preferred_element_type=jnp.float32)
        normed_ffn = rms_norm(middle, gain_f).astype(jnp.bfloat16)
        gate = jnp.dot(normed_ffn, full_gate, preferred_element_type=jnp.float32)
        up_value = jnp.dot(normed_ffn, full_up, preferred_element_type=jnp.float32)
        hidden = (jax.nn.silu(gate) * up_value).astype(jnp.bfloat16)
        result = middle + jnp.dot(hidden, full_down, preferred_element_type=jnp.float32)
        results.append(result.astype(jnp.bfloat16))
        saved.append(
            (
                rows_in,
                doc_row,
                cosine,
                sine,
                normed,
                query,
                key,
                value,
                logsum,
                mixed_rows,
                middle,
                normed_ffn,
                gate,
                up_value,
                hidden,
            )
        )
    back_weights = (
        lax.all_gather(shards[0], "dp", axis=0, tiled=True),
        lax.all_gather(shards[1], "dp", axis=0, tiled=True),
        lax.all_gather(shards[2], "dp", axis=0, tiled=True),
        lax.all_gather(shards[3], "dp", axis=0, tiled=True),
        lax.all_gather(shards[4], "dp", axis=0, tiled=True),
        lax.all_gather(shards[5], "dp", axis=0, tiled=True),
        lax.all_gather(shards[6], "dp", axis=0, tiled=True),
        lax.all_gather(shards[7], "dp", axis=0, tiled=True),
        lax.all_gather(shards[8], "dp", axis=0, tiled=True),
    )
    back_q, back_k, back_v, back_o, back_gate, back_up, back_down, back_gain_a, back_gain_f = (
        back_weights
    )
    gain_back_a = back_gain_a.astype(jnp.float32)
    gain_back_f = back_gain_f.astype(jnp.float32)
    totals = [jnp.zeros(weight.shape, jnp.float32) for weight in back_weights]
    grad_inputs = []
    for micro_index in range(micro):
        (
            rows_in,
            doc_row,
            cosine,
            sine,
            normed,
            query,
            key,
            value,
            logsum,
            mixed_rows,
            middle,
            normed_ffn,
            gate,
            up_value,
            hidden,
        ) = saved[micro_index]
        grad_out = out_grad[micro_index].astype(jnp.float32)
        grad_branch = grad_out.astype(jnp.bfloat16)
        totals[6] = totals[6] + jnp.einsum(
            "tf,td->fd", hidden, grad_branch, preferred_element_type=jnp.float32
        )
        grad_hidden = jnp.einsum(
            "td,fd->tf", grad_branch, back_down, preferred_element_type=jnp.float32
        )
        sigma = jax.nn.sigmoid(gate)
        grad_gate = (grad_hidden * up_value * sigma * (1.0 + gate * (1.0 - sigma))).astype(
            jnp.bfloat16
        )
        grad_up = (grad_hidden * jax.nn.silu(gate)).astype(jnp.bfloat16)
        totals[4] = totals[4] + jnp.einsum(
            "td,tf->df", normed_ffn, grad_gate, preferred_element_type=jnp.float32
        )
        totals[5] = totals[5] + jnp.einsum(
            "td,tf->df", normed_ffn, grad_up, preferred_element_type=jnp.float32
        )
        grad_normed_ffn = jnp.einsum(
            "tf,df->td", grad_gate, back_gate, preferred_element_type=jnp.float32
        )
        grad_normed_ffn = grad_normed_ffn + jnp.einsum(
            "tf,df->td", grad_up, back_up, preferred_element_type=jnp.float32
        )
        grad_gain_f, grad_middle = norm_backward(middle, gain_back_f, grad_normed_ffn)
        totals[8] = totals[8] + grad_gain_f
        grad_middle = grad_middle + grad_out
        grad_attn = grad_middle.astype(jnp.bfloat16)
        totals[3] = totals[3] + jnp.einsum(
            "ti,td->id", mixed_rows, grad_attn, preferred_element_type=jnp.float32
        )
        grad_mixed_rows = jnp.einsum(
            "td,id->ti", grad_attn, back_o, preferred_element_type=jnp.float32
        ).astype(jnp.bfloat16)
        grad_mixed = lax.all_to_all(grad_mixed_rows, "seq", split_axis=1, concat_axis=0, tiled=True)
        grad_query, grad_key, grad_value = attention_backward(
            query, key, value, doc_row, logsum, grad_mixed, cosine, sine
        )
        query_back, key_back, value_back = (
            lax.all_to_all(grad_query, "seq", split_axis=0, concat_axis=1, tiled=True),
            lax.all_to_all(grad_key, "seq", split_axis=0, concat_axis=1, tiled=True),
            lax.all_to_all(grad_value, "seq", split_axis=0, concat_axis=1, tiled=True),
        )
        totals[0] = totals[0] + jnp.einsum(
            "td,te->de", normed, query_back, preferred_element_type=jnp.float32
        )
        totals[1] = totals[1] + jnp.einsum(
            "td,te->de", normed, key_back, preferred_element_type=jnp.float32
        )
        totals[2] = totals[2] + jnp.einsum(
            "td,te->de", normed, value_back, preferred_element_type=jnp.float32
        )
        grad_normed = jnp.einsum(
            "te,de->td", query_back, back_q, preferred_element_type=jnp.float32
        )
        grad_normed = grad_normed + jnp.einsum(
            "te,de->td", key_back, back_k, preferred_element_type=jnp.float32
        )
        grad_normed = grad_normed + jnp.einsum(
            "te,de->td", value_back, back_v, preferred_element_type=jnp.float32
        )
        grad_gain_a, grad_rows = norm_backward(rows_in, gain_back_a, grad_normed)
        totals[7] = totals[7] + grad_gain_a
        grad_inputs.append(grad_rows + grad_middle)
    summed_all = (
        totals[0],
        totals[1],
        totals[2],
        totals[3],
        totals[4],
        totals[5],
        totals[6],
        totals[7],
        totals[8],
    )
    pieces = (
        lax.psum_scatter(
            summed_all[0].astype(jnp.bfloat16), "dp", scatter_dimension=0, tiled=True
        ).astype(jnp.float32),
        lax.psum_scatter(
            summed_all[1].astype(jnp.bfloat16), "dp", scatter_dimension=0, tiled=True
        ).astype(jnp.float32),
        lax.psum_scatter(
            summed_all[2].astype(jnp.bfloat16), "dp", scatter_dimension=0, tiled=True
        ).astype(jnp.float32),
        lax.psum_scatter(
            summed_all[3].astype(jnp.bfloat16), "dp", scatter_dimension=0, tiled=True
        ).astype(jnp.float32),
        lax.psum_scatter(
            summed_all[4].astype(jnp.bfloat16), "dp", scatter_dimension=0, tiled=True
        ).astype(jnp.float32),
        lax.psum_scatter(
            summed_all[5].astype(jnp.bfloat16), "dp", scatter_dimension=0, tiled=True
        ).astype(jnp.float32),
        lax.psum_scatter(
            summed_all[6].astype(jnp.bfloat16), "dp", scatter_dimension=0, tiled=True
        ).astype(jnp.float32),
        lax.psum_scatter(
            summed_all[7].astype(jnp.bfloat16), "dp", scatter_dimension=0, tiled=True
        ).astype(jnp.float32),
        lax.psum_scatter(
            summed_all[8].astype(jnp.bfloat16), "dp", scatter_dimension=0, tiled=True
        ).astype(jnp.float32),
    )
    pieces = (
        lax.psum(pieces[0].astype(jnp.bfloat16), "seq").astype(jnp.float32),
        lax.psum(pieces[1].astype(jnp.bfloat16), "seq").astype(jnp.float32),
        lax.psum(pieces[2].astype(jnp.bfloat16), "seq").astype(jnp.float32),
        lax.psum(pieces[3].astype(jnp.bfloat16), "seq").astype(jnp.float32),
        lax.psum(pieces[4].astype(jnp.bfloat16), "seq").astype(jnp.float32),
        lax.psum(pieces[5].astype(jnp.bfloat16), "seq").astype(jnp.float32),
        lax.psum(pieces[6].astype(jnp.bfloat16), "seq").astype(jnp.float32),
        lax.psum(pieces[7].astype(jnp.bfloat16), "seq").astype(jnp.float32),
        lax.psum(pieces[8].astype(jnp.bfloat16), "seq").astype(jnp.float32),
    )
    return (
        jnp.stack(results),
        jnp.stack(grad_inputs),
        pieces[0],
        pieces[1],
        pieces[2],
        pieces[3],
        pieces[4],
        pieces[5],
        pieces[6],
        pieces[7],
        pieces[8],
    )


BLK = 256
LOG2E = 1.4426950408889634


def swap_halves(v):
    lane = lax.broadcasted_iota(jnp.int32, v.shape, 1)
    width = v.shape[1]
    up = pltpu.roll(v, width - 32, axis=1)
    down = pltpu.roll(v, 32, axis=1)
    return jnp.where(lane % 64 < 32, up, down)


def nt(a, b):
    return lax.dot_general(a, b, (((1,), (1,)), ((), ())), preferred_element_type=jnp.float32)


def tn(a, b):
    return lax.dot_general(a, b, (((0,), (0,)), ((), ())), preferred_element_type=jnp.float32)


FAST_MESH = {"dp": 8, "seq": 4}
ANY = pl.BlockSpec(memory_space=pl.ANY)


class Place:
    def __init__(self):
        self.dp, self.z = lax.axis_index("dp"), lax.axis_index("seq")
        self.core = self.dp % 2
        self.x = (self.dp // 2) % 2
        self.y = self.dp // 4
        self.over_core = self.dp + 1 - 2 * self.core
        self.over_x = self.dp + 2 - 4 * self.x
        self.over_y = self.dp + 4 - 8 * self.y
        self.middle = (self.z == 1) | (self.z == 2)


def enter(devices):
    barrier = pltpu.get_barrier_semaphore()
    for dp, seq in devices:
        pl.semaphore_signal(
            barrier, inc=1, device_id={"dp": dp, "seq": seq}, device_id_type=pl.DeviceIdType.MESH
        )
    pl.semaphore_wait(barrier, len(devices))


def remote(src, dst, send_sem, recv_sem, dp, seq):
    return pltpu.make_async_remote_copy(
        src_ref=src,
        dst_ref=dst,
        send_sem=send_sem,
        recv_sem=recv_sem,
        device_id={"dp": dp, "seq": seq},
        device_id_type=pl.DeviceIdType.MESH,
    )


def gather_kernel(
    tokens, segments, out_grad, gains, cosine, sine, w_q, w_k, w_v, w_o, w_gate, w_up, w_down,
    x_out, seg_out, g_out, gains_out, qkv_out, o_out, ff_out, down_out,
    heads_out, lse_out, middle_out, slope_gate_out, slope_up_out, hidden_out, g_down_out, start_out,
    gain_out, normed_t_out, nf_t_out, mixed_t_out,
    send, recv, local, row_send, row_recv, row_local, gain_send, gain_recv,
    x_v, seg_v, gains_v, normed_v, w_qkv_v, heads_v, mixed_v, w_o_v, middle_v, part_send, part_recv,
    nf_v, w_ff_v, branch_v, tile_v, g_tile_v, lse_v, start_v, lse_t_v, start_row_v, gain_v, turned_v, mixed_t_v,
    part_sem, load_sem, w_sem, tile_sem, store_sem,
):
    me = Place()
    rows = tokens.shape[1]
    plane = [(lax.rem(me.dp + k, 8), me.z) for k in range(1, 8)]
    column = [
        (me.dp - me.core + core, lax.rem(me.z + k, 4)) for k in range(1, 4) for core in range(2)
    ]
    enter(plane + column)
    started = []

    def begin(copy):
        copy.start()
        started.append(copy)

    streams = ((tokens, x_out), (segments, seg_out), (out_grad, g_out))

    def place_of(ref, seq):
        return ref.at[pl.ds(rows * seq, rows)] if ref.shape[0] == 4 * rows else ref.at[seq]

    def row_copies(index):
        source, target = streams[index]
        for m in range(2):
            core, seq = me.z // 2, 2 * m + me.core
            here = (core == me.core) & (seq == me.z)

            @pl.when(here)
            def _():
                pltpu.make_async_copy(
                    source.at[m], place_of(target, me.z), row_local.at[index]
                ).start()

            @pl.when(jnp.logical_not(here))
            def _():
                remote(
                    source.at[m], place_of(target, me.z), row_send.at[index, m],
                    row_recv.at[index, me.z % 2], me.dp - me.core + core, seq,
                ).start()

    def row_wait_send(index):
        source, target = streams[index]
        for m in range(2):
            core, seq = me.z // 2, 2 * m + me.core
            here = (core == me.core) & (seq == me.z)

            @pl.when(jnp.logical_not(here))
            def _():
                remote(
                    source.at[m], place_of(target, me.z), row_send.at[index, m],
                    row_recv.at[index, me.z % 2], me.dp - me.core + core, seq,
                ).wait_send()

    def row_relay(index):
        source, target = streams[index]
        for slot in range(2):
            seq = 2 * me.core + slot
            block = place_of(target, seq)
            here = (seq == me.z) & (me.z % 2 == me.core)

            @pl.when(here)
            def _():
                pltpu.make_async_copy(block, block, row_local.at[index]).wait()

            @pl.when(jnp.logical_not(here))
            def _():
                remote(
                    block, block, row_send.at[index, slot], row_recv.at[index, slot], me.over_core, me.z
                ).wait_recv()

            begin(
                remote(
                    block, block, row_send.at[index, 2 + slot], row_recv.at[index, 2 + slot],
                    me.over_core, me.z,
                )
            )

    def row_finish(index):
        source, target = streams[index]
        for slot in range(2):
            block = place_of(target, 2 * (1 - me.core) + slot)
            remote(
                block, block, row_send.at[index, 2 + slot], row_recv.at[index, 2 + slot], me.over_core, me.z
            ).wait_recv()

    by_columns = []
    base = 0
    for source in (w_q, w_k, w_v):
        by_columns.append((source, qkv_out, base))
        base += source.shape[1] // 2
    by_columns.append((w_gate, ff_out, 0))
    by_columns.append((w_up, ff_out, w_gate.shape[1] // 2))
    by_rows = [(w_o, o_out), (w_down, down_out)]

    def column_piece(index, owner):
        source, target, first = by_columns[index]
        depth, width = source.shape[0], source.shape[1] // 2
        return target.at[pl.ds(depth * owner, depth), pl.ds(first, width)]

    def columns_start(index):
        source, target, first = by_columns[index]
        width = source.shape[1] // 2
        mine = column_piece(index, me.dp)
        for core in range(2):
            half = source.at[:, pl.ds(width * core, width)]
            begin(remote(half, mine, send.at[index, core], recv.at[index, me.core],
                         me.over_x - me.core + core, me.z))
            begin(remote(half, mine, send.at[index, 2 + core], recv.at[index, 2 + me.core],
                         me.over_y - me.core + core, me.z))

            @pl.when(core == me.core)
            def _():
                pltpu.make_async_copy(half, mine, local.at[index]).start()

            @pl.when(core != me.core)
            def _():
                remote(half, mine, send.at[index, 4], recv.at[index, 4], me.over_core, me.z).start()

    def columns_relay(index):
        piece = column_piece(index, me.over_x - me.core)
        remote(piece, piece, send.at[index, 5], recv.at[index, 0], me.over_y, me.z).wait_recv()
        begin(remote(piece, piece, send.at[index, 5], recv.at[index, 5], me.over_y, me.z))
        piece = column_piece(index, me.over_y - me.core + 1)
        remote(piece, piece, send.at[index, 6], recv.at[index, 3], me.over_x, me.z).wait_recv()
        begin(remote(piece, piece, send.at[index, 6], recv.at[index, 6], me.over_x, me.z))

    def columns_finish(index):
        source, target, first = by_columns[index]
        width = source.shape[1] // 2
        corner = me.over_x + me.over_y - me.dp - me.core
        for slot, owner in (
            (1, me.over_x - me.core + 1), (2, me.over_y - me.core), (4, me.over_core),
            (5, corner), (6, corner + 1),
        ):
            piece = column_piece(index, owner)
            remote(piece, piece, send.at[index, 5], recv.at[index, slot], me.over_core, me.z).wait_recv()
        mine = column_piece(index, me.dp)
        pltpu.make_async_copy(mine, mine, local.at[index]).wait()
        half = source.at[:, pl.ds(0, width)]
        remote(half, mine, send.at[index, 4], recv.at[index, 4], me.over_core, me.z).wait_send()

    def row_piece(which, owner):
        source, target = by_rows[which]
        depth = source.shape[0]
        return target.at[pl.ds(depth * lax.rem(owner, 4), depth), :]

    def rows_start(which):
        source, target = by_rows[which]
        index = 5 + which
        mine = row_piece(which, me.dp)
        begin(remote(source, mine, send.at[index, 0], recv.at[index, me.core],
                     me.over_x - me.core + me.y, me.z))
        begin(remote(source, mine, send.at[index, 1], recv.at[index, 2 + me.core],
                     me.over_y - me.core + me.y, me.z))

        @pl.when(me.core == me.y)
        def _():
            pltpu.make_async_copy(source, mine, local.at[index]).start()

        @pl.when(me.core != me.y)
        def _():
            remote(source, mine, send.at[index, 4], recv.at[index, 4], me.over_core, me.z).start()

    def rows_relay(which):
        index = 5 + which

        @pl.when(me.core == me.y)
        def _():
            piece = row_piece(which, me.over_x - me.core)
            remote(piece, piece, send.at[index, 5], recv.at[index, 0], me.over_y, me.z).wait_recv()
            remote(piece, piece, send.at[index, 5], recv.at[index, 5], me.over_y, me.z).start()

        @pl.when(me.core != me.y)
        def _():
            piece = row_piece(which, me.over_y - me.core + 1)
            remote(piece, piece, send.at[index, 6], recv.at[index, 3], me.over_x, me.z).wait_recv()
            remote(piece, piece, send.at[index, 6], recv.at[index, 6], me.over_x, me.z).start()

    def rows_finish(which):
        source, target = by_rows[which]
        index = 5 + which
        corner = me.over_x + me.over_y - me.dp - me.core

        def arrived(slot, owner):
            piece = row_piece(which, owner)
            remote(piece, piece, send.at[index, 5], recv.at[index, slot], me.over_core, me.z).wait_recv()

        def left(slot):
            piece = row_piece(which, me.dp)
            remote(source, piece, send.at[index, slot], recv.at[index, slot], me.over_core, me.z).wait_send()

        @pl.when(me.core == me.y)
        def _():
            arrived(1, me.over_x - me.core + 1)
            arrived(4, me.over_core)
            mine = row_piece(which, me.dp)
            pltpu.make_async_copy(source, mine, local.at[index]).wait()
            left(5)

        @pl.when(me.core != me.y)
        def _():
            arrived(2, me.over_y - me.core)
            arrived(5, corner)
            arrived(6, corner + 1)
            left(4)
            left(6)

    def load(source, target, k):
        return pltpu.make_async_copy(source, target, load_sem.at[k])

    stores = []

    def store(source, target):
        copy = pltpu.make_async_copy(source, target, store_sem.at[len(stores)])
        stores.append(copy)
        copy.start()
        return copy

    length, width = x_v.shape
    own_width = width // 2
    half_ff = ff_out.shape[1] // 2

    row_copies(0)
    row_copies(1)
    for index in range(3):
        columns_start(index)
    for k in range(1, 8):
        begin(remote(gains, gains_out.at[me.dp], gain_send.at[k - 1], gain_recv.at[k - 1],
                     lax.rem(me.dp + k, 8), me.z))
    pltpu.make_async_copy(gains, gains_out.at[me.dp], gain_recv.at[7]).start()
    row_copies(2)
    for index in range(3):
        columns_relay(index)
    rows_start(0)
    row_relay(0)
    row_relay(1)
    for k in range(1, 8):
        piece = gains_out.at[lax.rem(me.dp + 8 - k, 8)]
        remote(piece, piece, gain_send.at[k - 1], gain_recv.at[k - 1], me.over_core, me.z).wait_recv()
    pltpu.make_async_copy(gains, gains_out.at[me.dp], gain_recv.at[7]).wait()
    load(gains_out, gains_v, 0).start()
    row_finish(1)
    load(seg_out, seg_v, 1).start()
    row_finish(0)
    load(x_out, x_v, 2).start()
    load(gains_out, gains_v, 0).wait()
    load(seg_out, seg_v, 1).wait()
    load(x_out, x_v, 2).wait()
    both_gains = gains_v[0].astype(jnp.float32)
    for k in range(1, 8):
        both_gains = both_gains + gains_v[k].astype(jnp.float32)
    gain_a, gain_f = both_gains[0:1], both_gains[1:2]
    gain_v[...] = both_gains
    store(gain_v, gain_out)

    norm_rows(lambda part: x_v[part, :].astype(jnp.float32), gain_a, normed_v, length)

    docs = jnp.concatenate([seg_v[k] for k in range(4)], axis=1)
    start_row = jnp.zeros((1, length), jnp.int32)
    for k in range(4):
        square = lax.broadcasted_iota(jnp.int32, (rows, rows), 0) == lax.broadcasted_iota(
            jnp.int32, (rows, rows), 1
        )
        ids = jnp.sum(jnp.where(square, seg_v[k], 0), axis=1, keepdims=True)
        start_v[pl.ds(rows * k, rows), :] = jnp.sum(
            jnp.where(docs < ids, 1, 0), axis=1, keepdims=True
        )
        start_row = start_row + jnp.sum(jnp.where(ids < docs, 1, 0), axis=0, keepdims=True)
    start_row_v[...] = start_row
    store(start_row_v, start_out)
    turn(normed_v, turned_v)
    normed_store = store(turned_v, normed_t_out)

    for index in range(3):
        columns_finish(index)
    columns_start(3)
    columns_start(4)
    rows_relay(0)
    tile = 256
    tiles = own_width // tile
    for t in range(tiles):
        for kind in range(3):
            part = pl.ds(own_width * kind + tile * t, tile)
            pltpu.make_async_copy(qkv_out.at[:, part], w_qkv_v.at[:, part], w_sem.at[kind, t]).start()
    for t in range(tiles):
        for kind in range(3):
            part = pl.ds(own_width * kind + tile * t, tile)
            pltpu.make_async_copy(qkv_out.at[:, part], w_qkv_v.at[:, part], w_sem.at[kind, t]).wait()
            product = jnp.dot(normed_v[...], w_qkv_v[:, part], preferred_element_type=jnp.float32)
            for k in range(tile // 128):
                piece = product[:, 128 * k : 128 * k + 128]
                if kind < 2:
                    piece = piece * cosine[...] + swap_halves(piece) * sine[...]
                heads_v[:, pl.ds(own_width * kind + tile * t + 128 * k, 128)] = piece.astype(jnp.bfloat16)

        def pair_step(pair, carry):
            attend(pair, own_width, heads_v, start_v, mixed_v, lse_v)
            return carry

        lax.fori_loop(tile // 128 * t, tile // 128 * (t + 1), pair_step, 0)
        if t == 0:
            row_relay(2)
        if t == 1:
            rows_start(1)
    store(heads_v, heads_out)
    lse_t_v[...] = lse_v[...].T
    store(lse_t_v, lse_out)
    turn(mixed_v, mixed_t_v)
    store(mixed_t_v, mixed_t_out)

    rows_finish(0)
    load(o_out, w_o_v, 0).start()
    row_finish(2)
    load(g_out, branch_v, 1).start()
    load(o_out, w_o_v, 0).wait()
    chunk = width // 3

    def part_copy(k):
        part = pl.ds(chunk * k, chunk)
        return remote(
            part_send.at[:, part], part_recv.at[:, part], part_sem.at[0, k], part_sem.at[1, k], me.over_core, me.z
        )

    for k in range(3):
        for at in range(chunk * k, chunk * (k + 1), tile):
            part = pl.ds(at, tile)
            product = jnp.dot(mixed_v[...], w_o_v[:, part], preferred_element_type=jnp.float32)
            part_send[:, part] = product.astype(jnp.bfloat16)
            middle_v[:, part] = x_v[:, part].astype(jnp.float32) + product
        part_copy(k).start()
    columns_relay(3)
    columns_relay(4)
    for k in range(3):
        part_copy(k).wait_recv()

    def middle_rows(part):
        value = middle_v[part, :] + part_recv[part, :].astype(jnp.float32)
        middle_v[part, :] = value
        return value

    norm_rows(middle_rows, gain_f, nf_v, length)
    store(middle_v, middle_out)
    normed_store.wait()
    turn(nf_v, turned_v)
    store(turned_v, nf_t_out)
    load(g_out, branch_v, 1).wait()
    rows_relay(1)
    columns_finish(3)
    columns_finish(4)

    def ff_load(n, slot, kind):
        first = pl.multiple_of(half_ff * kind + tile * n, 128)
        return pltpu.make_async_copy(
            ff_out.at[:, pl.ds(first, tile)], w_ff_v.at[slot, kind], tile_sem.at[0, slot, kind]
        )

    def tile_store(n, slot, kind):
        part = pl.ds(pl.multiple_of(tile * n, 128), tile)
        target = (slope_gate_out, slope_up_out, hidden_out)[kind]
        return pltpu.make_async_copy(tile_v.at[slot, kind], target.at[:, part], tile_sem.at[1, slot, kind])

    def grad_store(n, slot):
        part = pl.ds(pl.multiple_of(tile * n, tile), tile)
        return pltpu.make_async_copy(g_tile_v.at[slot], g_down_out.at[part, :], tile_sem.at[2, slot, 0])

    count = half_ff // tile
    for kind in range(2):
        ff_load(0, 0, kind).start()

    def ff_step(n, carry):
        slot = lax.rem(n, 2)
        for kind in range(2):
            ff_load(n, slot, kind).wait()

        @pl.when(n + 1 < count)
        def _():
            for kind in range(2):
                ff_load(n + 1, 1 - slot, kind).start()

        @pl.when(n >= 2)
        def _():
            for kind in range(3):
                tile_store(n - 2, slot, kind).wait()
            grad_store(n - 2, slot).wait()

        gate = jnp.dot(nf_v[...], w_ff_v[slot, 0], preferred_element_type=jnp.float32)
        up_value = jnp.dot(nf_v[...], w_ff_v[slot, 1], preferred_element_type=jnp.float32)
        sigma = jax.nn.sigmoid(gate)
        silu = gate * sigma
        tile_v[slot, 0] = (up_value * sigma * (1.0 + gate * (1.0 - sigma))).astype(jnp.bfloat16)
        tile_v[slot, 1] = silu.astype(jnp.bfloat16)
        hidden = (silu * up_value).astype(jnp.bfloat16)
        tile_v[slot, 2] = hidden
        g_tile_v[slot] = jnp.dot(
            hidden.T, branch_v[...], preferred_element_type=jnp.float32
        ).astype(jnp.bfloat16)
        for kind in range(3):
            tile_store(n, slot, kind).start()
        grad_store(n, slot).start()
        return carry

    lax.fori_loop(0, count, ff_step, 0)
    for n in range(count - 2, count):
        for kind in range(3):
            tile_store(n, n % 2, kind).wait()
        grad_store(n, n % 2).wait()
    rows_finish(1)
    for copy in stores:
        if copy is not normed_store:
            copy.wait()
    for k in range(3):
        part_copy(k).wait_send()
    for index in range(3):
        row_wait_send(index)
    for copy in started:
        copy.wait_send()


def turn(source, target):
    for k in range(source.shape[1] // 256):
        target[256 * k : 256 * (k + 1), :] = source[:, 256 * k : 256 * (k + 1)].T


def norm_rows(read, gain, target, length, step=64):
    def chunk(k, carry):
        part = pl.ds(pl.multiple_of(k * step, step), step)
        values = read(part)
        scale = lax.rsqrt(jnp.mean(values * values, axis=-1, keepdims=True) + EPS)
        target[part, :] = (values * scale * gain).astype(target.dtype)
        return carry

    lax.fori_loop(0, length // step, chunk, 0)


def attend(pair, width, heads, start, mixed, lse):
    length = heads.shape[0]
    lane = lax.broadcasted_iota(jnp.int32, (BLK, 128), 1)
    cols = [pl.ds(pl.multiple_of(width * kind + 128 * pair, 128), 128) for kind in range(3)]
    for i in range(length // BLK):
        own_rows, keys = slice(BLK * i, BLK * (i + 1)), BLK * (i + 1)
        place = lax.broadcasted_iota(jnp.int32, (BLK, keys), 1)
        own = BLK * i + lax.broadcasted_iota(jnp.int32, (BLK, keys), 0)
        allowed = (place >= start[own_rows, :]) & (place <= own)
        query = heads[own_rows, cols[0]] * jnp.bfloat16(0.125)
        key, value = heads[0:keys, cols[1]], heads[0:keys, cols[2]]
        kept = lse[own_rows, :]
        outs = []
        for half in range(2):
            part = slice(64 * half, 64 * half + 64)
            scores = jnp.where(allowed, nt(query[:, part], key[:, part]), -1e30)
            peak = jnp.max(scores, axis=-1, keepdims=True)
            expo = jnp.exp(scores - peak)
            total = jnp.sum(expo, axis=-1, keepdims=True)
            out = jnp.dot(expo.astype(jnp.bfloat16), value[:, part], preferred_element_type=jnp.float32)
            outs.append((out / total).astype(jnp.bfloat16))
            kept = jnp.where(lane == 2 * pair + half, peak + jnp.log(total), kept)
        mixed[own_rows, cols[0]] = jnp.concatenate(outs, axis=1)
        lse[own_rows, :] = kept


def gather_all(tokens, segments, out_grad, gains, cosine, sine, weights):
    rows, width = tokens.shape[1], tokens.shape[2]
    length, half, ff = 4 * rows, width // 2, weights[4].shape[1]
    half_ff = ff // 2
    low = jnp.bfloat16

    def shape(*dims, dtype=low):
        return jax.ShapeDtypeStruct(dims, dtype)

    shapes = [
        shape(length, width),
        shape(4, *segments.shape[1:], dtype=jnp.int32),
        shape(length, width),
        shape(8, *gains.shape),
        shape(width, 3 * half),
        shape(half, width),
        shape(width, ff),
        shape(half_ff, width),
        shape(length, 3 * half),
        shape(128, length, dtype=jnp.float32),
        shape(length, width, dtype=jnp.float32),
        shape(length, half_ff),
        shape(length, half_ff),
        shape(length, half_ff),
        shape(half_ff, width),
        shape(1, length, dtype=jnp.int32),
        shape(2, width, dtype=jnp.float32),
        shape(width, length),
        shape(width, length),
        shape(half, length),
    ]
    dma, vmem = pltpu.SemaphoreType.DMA, pltpu.VMEM
    whole = pl.BlockSpec(memory_space=pltpu.VMEM)
    return pl.pallas_call(
        gather_kernel,
        in_specs=[ANY] * 4 + [whole] * 2 + [ANY] * 7,
        out_specs=[ANY] * len(shapes),
        out_shape=shapes,
        scratch_shapes=[
            dma((7, 7)), dma((7, 7)), dma((7,)), dma((3, 4)), dma((3, 4)), dma((3,)), dma((7,)), dma((8,)),
            vmem((length, width), low),
            vmem((4,) + segments.shape[1:], jnp.int32),
            vmem((8,) + gains.shape, low),
            vmem((length, width), low),
            vmem((width, 3 * half), low),
            vmem((length, 3 * half), low),
            vmem((length, half), low),
            vmem((half, width), low),
            vmem((length, width), jnp.float32),
            vmem((length, width), low),
            vmem((length, width), low),
            vmem((length, width), low),
            vmem((2, 2, width, 256), low),
            vmem((length, width), low),
            vmem((2, 3, length, 256), low),
            vmem((2, 256, width), low),
            vmem((length, 128), jnp.float32),
            vmem((length, 1), jnp.int32),
            vmem((128, length), jnp.float32),
            vmem((1, length), jnp.int32),
            vmem((2, width), jnp.float32),
            vmem((width, length), low),
            vmem((half, length), low),
            dma((2, 3)), dma((3,)), dma((3, 3)), dma((3, 2, 3)), dma((9,)),
        ],
        compiler_params=pltpu.CompilerParams(
            collective_id=0, has_side_effects=True, vmem_limit_bytes=61 * 1024 * 1024
        ),
        cost_estimate=pl.CostEstimate(flops=0, bytes_accessed=500_000_000, transcendentals=0),
        name="gather_all",
    )(tokens, segments, out_grad, gains, cosine, sine, *weights)


def guard(condition, action):
    if isinstance(condition, (bool, np.bool_)):
        if condition:
            action()
    else:
        pl.when(condition)(action)


def everything(*conditions):
    known = [c for c in conditions if isinstance(c, (bool, np.bool_))]
    if not all(known):
        return False
    rest = [c for c in conditions if not isinstance(c, (bool, np.bool_))]
    if not rest:
        return True
    total = rest[0]
    for c in rest[1:]:
        total = total & c
    return total


def add_rows(target, first, other, rows, step=64):
    def chunk(k, carry):
        at = pl.multiple_of(k * step, step)
        source = pl.multiple_of(first + k * step, step)
        target[pl.ds(at, step), :] += other[pl.ds(source, step), :]
        return carry

    lax.fori_loop(0, rows // step, chunk, 0)


JOB = 256


class Stream:
    active = True

    def tick(self, t):
        for late, stage in reversed(self.stages):
            k = t - late
            guard(everything(k >= 0, k < self.count), functools.partial(stage, k))

    @property
    def ticks(self):
        return self.count + self.stages[-1][0]

    def slot(self, k):
        return k % self.slots if isinstance(k, int) else lax.rem(k, self.slots)

    def column(self, k, base=0):
        return pl.ds(pl.multiple_of(base + JOB * k, 128), JOB)

    def total(self, k):
        return self.second.at[self.slot(k)]

    def final(self, k):
        return self.got.at[self.slot(k), pl.ds(0, self.rows)]

    def seq_copy(self, k, step):
        me, slot, sem = self.me, self.slot(k), self.seq_sem
        inner = me.z + 1 - 2 * (me.z // 2)
        opposite = 3 - me.z
        outer = 3 * (me.z // 2)
        if step == 0:
            return remote(self.total(k), self.over.at[slot, 0], sem.at[slot, 0, 0], sem.at[slot, 1, 0], me.dp, inner)
        if step == 1:
            return remote(
                self.total(k), self.over.at[slot, 1], sem.at[slot, 0, 1], sem.at[slot, 1, 1], me.dp, opposite
            )
        return remote(self.final(k), self.final(k), sem.at[slot, 0, 2], sem.at[slot, 1, 2], me.dp, outer)

    def plane_and_ends(self, k):
        self.reduce_plane(k)
        guard(
            everything(self.active, jnp.logical_not(self.me.middle)),
            lambda: self.seq_copy(k, 0).start(),
        )

    def across(self, k):
        def action():
            self.seq_copy(k, 0).wait_recv()
            add_rows(self.total(k), 0, self.over.at[self.slot(k), 0], self.rows)
            self.seq_copy(k, 1).start()

        guard(everything(self.active, self.me.middle), action)

    def back(self, k):
        def action():
            self.seq_copy(k, 1).wait_recv()
            final, total, over, step = self.final(k), self.total(k), self.over.at[self.slot(k), 1], 64

            def chunk(at, carry):
                part = pl.ds(pl.multiple_of(at * step, step), step)
                final[part, :] = total[part, :] + over[part, :]
                return carry

            lax.fori_loop(0, self.rows // step, chunk, 0)
            self.seq_copy(k, 2).start()

        guard(everything(self.active, self.me.middle), action)

    def finish(self, k):
        guard(
            everything(self.active, jnp.logical_not(self.me.middle)),
            lambda: self.seq_copy(k, 2).wait_recv(),
        )
        self.output(k)

    def drain(self, k):
        self.drain_plane(k)

        def ends():
            self.seq_copy(k, 0).wait_send()

        def middles():
            self.seq_copy(k, 1).wait_send()
            self.seq_copy(k, 2).wait_send()

        guard(everything(self.active, jnp.logical_not(self.me.middle)), ends)
        guard(everything(self.active, self.me.middle), middles)


class ColumnStream(Stream):
    def __init__(self, me, source, target, ff_jobs, d_model, ff, refs):
        self.me, self.source, self.target = me, source, target
        self.got, self.keep, self.second, self.over, self.sem, self.seq_sem, self.credit = refs
        self.slots, self.rows = self.got.shape[0], source.shape[0] // 4
        self.count, self.ff_jobs = source.shape[1] // JOB, ff_jobs
        self.ff, self.d_model = ff, d_model
        self.stages = (
            (0, self.start), (3, self.pass_second), (4, self.plane_and_ends), (5, self.across),
            (6, self.back), (7, self.finish), (8, self.drain),
        )

    def x_first(self, k):
        late = k // self.ff_jobs
        return (1 - late) * ((k // (self.ff_jobs // 2)) % 2) * ((k + 1) % 2) + late * (k % 2)

    def first_copy(self, k, part):
        me, slot, x_first = self.me, self.slot(k), self.x_first(k)
        block = x_first * (2 * part + 1 - me.x) + (1 - x_first) * (2 * (1 - me.y) + part)
        sent = self.source.at[pl.ds(pl.multiple_of(self.rows * block, self.rows), self.rows), self.column(k)]
        to = x_first * me.over_x + (1 - x_first) * me.over_y
        return remote(
            sent, self.got.at[slot, pl.ds(self.rows * part, self.rows)],
            self.sem.at[slot, 0, part], self.sem.at[slot, 1, part], to, me.z,
        )

    def keep_copy(self, k, part):
        me, slot, x_first = self.me, self.slot(k), self.x_first(k)
        block = x_first * (2 * part + me.x) + (1 - x_first) * (2 * me.y + part)
        kept = self.source.at[pl.ds(pl.multiple_of(self.rows * block, self.rows), self.rows), self.column(k)]
        return pltpu.make_async_copy(
            kept, self.keep.at[slot, pl.ds(self.rows * part, self.rows)], self.sem.at[slot, 2, part]
        )

    def at(self, k):
        x_first = self.x_first(k)
        return x_first * self.me.y + (1 - x_first) * self.me.x

    def second_copy(self, k):
        me, slot, x_first = self.me, self.slot(k), self.x_first(k)
        row = pl.multiple_of(self.rows * (1 - self.at(k)), self.rows)
        to = x_first * me.over_y + (1 - x_first) * me.over_x
        return remote(
            self.keep.at[slot, pl.ds(row, self.rows)], self.second.at[slot],
            self.sem.at[slot, 0, 2], self.sem.at[slot, 1, 2], to, me.z,
        )

    def start(self, k):
        def credits():
            slot = self.slot(k)

            @pl.when(self.me.middle)
            def _():
                pl.semaphore_wait(self.credit.at[slot], 5)

            @pl.when(jnp.logical_not(self.me.middle))
            def _():
                pl.semaphore_wait(self.credit.at[slot], 4)

        guard(k >= self.slots, credits)
        for part in range(2):
            self.first_copy(k, part).start()
            self.keep_copy(k, part).start()

    def pass_second(self, k):
        for part in range(2):
            self.keep_copy(k, part).wait()
            self.first_copy(k, part).wait_recv()
        slot = self.slot(k)
        add_rows(self.keep.at[slot], 0, self.got.at[slot], 2 * self.rows)
        self.second_copy(k).start()

    def reduce_plane(self, k):
        self.second_copy(k).wait_recv()
        add_rows(self.total(k), self.rows * self.at(k), self.keep.at[self.slot(k)], self.rows)

    def out_column(self, k, core, late):
        if late:
            m, half = k - self.ff_jobs, self.d_model // 2
            tiles = half // JOB
            first = 2 * self.ff + self.d_model * (m // tiles) + JOB * (m % tiles) + half * core
        else:
            first = self.ff * (k % 2) + JOB * (k // 2) + self.ff // 2 * core
        return self.target.at[:, pl.ds(pl.multiple_of(first, 128), JOB)]

    def last_copy(self, k, late=False):
        me, slot, rows = self.me, self.slot(k), self.rows // 2
        part = self.got.at[slot, pl.ds(pl.multiple_of(rows * (1 - me.core), rows), rows)]
        return remote(
            part, self.out_column(k, me.core, late), self.sem.at[slot, 0, 3], self.sem.at[slot, 1, 3],
            me.over_core, me.z,
        )

    def own_copy(self, k, late=False):
        me, slot, rows = self.me, self.slot(k), self.rows // 2
        part = self.got.at[slot, pl.ds(pl.multiple_of(rows * me.core, rows), rows)]
        return pltpu.make_async_copy(part, self.out_column(k, me.core, late), self.sem.at[slot, 2, 0])

    def output(self, k):
        def begin(late):
            self.last_copy(k, late).start()
            self.own_copy(k, late).start()

        guard(k < self.ff_jobs, lambda: begin(False))
        guard(k >= self.ff_jobs, lambda: begin(True))

    def drain_plane(self, k):
        for part in range(2):
            self.first_copy(k, part).wait_send()
        self.second_copy(k).wait_send()

        def end(late):
            self.last_copy(k, late).wait()
            self.own_copy(k, late).wait()

        guard(k < self.ff_jobs, lambda: end(False))
        guard(k >= self.ff_jobs, lambda: end(True))

    def drain(self, k):
        super().drain(k)

        def signal(dp, seq):
            pl.semaphore_signal(
                self.credit.at[self.slot(k)], inc=1, device_id={"dp": dp, "seq": seq},
                device_id_type=pl.DeviceIdType.MESH,
            )

        def free():
            me = self.me
            for dp in (me.over_core, me.over_x, me.over_y):
                signal(dp, me.z)

            @pl.when(me.middle)
            def _():
                signal(me.dp, 3 - me.z)
                signal(me.dp, 3 * (me.z // 2))

            @pl.when(jnp.logical_not(me.middle))
            def _():
                signal(me.dp, me.z + 1 - 2 * (me.z // 2))

        guard(k + self.slots < self.count, free)


class RowStream(Stream):
    def __init__(self, me, source, target, refs):
        self.me, self.source, self.target = me, source, target
        self.got, self.second, self.over, self.stage, self.sem, self.seq_sem = refs
        self.slots, self.rows = self.got.shape[0], source.shape[0] // 2
        self.count = source.shape[1] // JOB
        self.active = me.core == me.y
        self.stages = (
            (0, self.start), (1, self.load), (2, self.pass_second), (3, self.plane_and_ends), (4, self.across),
            (5, self.back), (6, self.finish), (7, self.drain),
        )

    def first_copy(self, k):
        me, slot = self.me, self.slot(k)
        sent = self.source.at[pl.ds(pl.multiple_of(self.rows * (1 - me.x), self.rows), self.rows), self.column(k)]
        return remote(sent, self.got.at[slot], self.sem.at[slot, 0, 0], self.sem.at[slot, 1, 0], me.over_x, me.z)

    def load_copy(self, k):
        kept = self.source.at[
            pl.ds(pl.multiple_of(self.rows * self.me.x, self.rows), self.rows), self.column(k)
        ]
        return pltpu.make_async_copy(kept, self.stage, self.sem.at[self.slot(k), 2, 0])

    def second_copy(self, k):
        me, slot = self.me, self.slot(k)
        return remote(
            self.got.at[slot], self.second.at[slot], self.sem.at[slot, 0, 2], self.sem.at[slot, 1, 2],
            me.over_y, me.z,
        )

    def start(self, k):
        self.first_copy(k).start()

    def load(self, k):
        self.load_copy(k).start()

    def pass_second(self, k):
        self.load_copy(k).wait()
        self.first_copy(k).wait_recv()
        add_rows(self.got.at[self.slot(k)], 0, self.stage, self.rows)
        guard(jnp.logical_not(self.active), lambda: self.second_copy(k).start())

    def reduce_plane(self, k):
        def action():
            self.second_copy(k).wait_recv()
            add_rows(self.total(k), 0, self.got.at[self.slot(k)], self.rows)

        guard(self.active, action)

    def last_copy(self, k):
        me, slot, rows = self.me, self.slot(k), self.rows // 2
        part = self.got.at[slot, pl.ds(pl.multiple_of(rows * (1 - me.core), rows), rows)]
        return remote(
            part, self.target.at[:, self.column(k)], self.sem.at[slot, 0, 3], self.sem.at[slot, 1, 3],
            me.over_core, me.z,
        )

    def own_copy(self, k):
        me, slot, rows = self.me, self.slot(k), self.rows // 2
        part = self.got.at[slot, pl.ds(pl.multiple_of(rows * me.core, rows), rows)]
        return pltpu.make_async_copy(part, self.target.at[:, self.column(k)], self.sem.at[slot, 2, 1])

    def output(self, k):
        def action():
            self.last_copy(k).start()
            self.own_copy(k).start()

        guard(self.active, action)

    def drain_plane(self, k):
        self.first_copy(k).wait_send()

        def active():
            self.last_copy(k).wait_send()
            self.own_copy(k).wait()

        def passive():
            self.second_copy(k).wait_send()
            self.last_copy(k).wait_recv()

        guard(self.active, active)
        guard(jnp.logical_not(self.active), passive)


GAIN_HOPS = 5


class GainSums:
    def __init__(self, me, target, buffer, sem):
        self.me, self.target, self.buffer, self.sem = me, target, buffer, sem

    def hop(self, k):
        me = self.me
        across = me.z + 2 - 4 * (me.z // 2)
        beside = me.z + 1 - 2 * (me.z % 2)
        dp = (me.over_core, me.over_x, me.over_y, me.dp, me.dp)[k]
        seq = (me.z, me.z, me.z, beside, across)[k]
        return remote(
            self.buffer.at[k, 0], self.buffer.at[k, 1], self.sem.at[0, k], self.sem.at[1, k], dp, seq
        )

    def start(self):
        self.hop(0).start()

    def step(self, k):
        self.hop(k).wait_recv()
        total = self.buffer[k, 0] + self.buffer[k, 1]
        if k + 1 < GAIN_HOPS:
            self.buffer[k + 1, 0] = total
            self.hop(k + 1).start()
        else:
            self.target[...] = total

    def drain(self):
        for k in range(GAIN_HOPS):
            self.hop(k).wait_send()


class RowsBack:
    def __init__(self, me, source, target, sem):
        self.me, self.source, self.target, self.sem = me, source, target, sem

    def each(self, local, elsewhere):
        me = self.me
        rows = self.source.shape[0] // 2
        for slot in range(2):
            core, seq = me.z % 2, 2 * me.core + slot
            here = (core == me.core) & (seq == me.z)
            block, target = self.source.at[pl.ds(rows * slot, rows)], self.target.at[me.z // 2]

            @pl.when(here)
            def _():
                local(pltpu.make_async_copy(block, target, self.sem.at[2, 0]))

            @pl.when(jnp.logical_not(here))
            def _():
                elsewhere(
                    remote(
                        block, target, self.sem.at[0, slot], self.sem.at[1, me.z // 2],
                        me.dp - me.core + core, seq,
                    )
                )

    def start(self):
        self.each(lambda copy: copy.start(), lambda copy: copy.start())

    def drain(self):
        me = self.me
        self.each(lambda copy: copy.wait(), lambda copy: copy.wait_send())
        rows = self.source.shape[0] // 2
        for m in range(2):
            here = (me.z == 2 * m + me.core) & (me.core == me.z // 2)

            @pl.when(jnp.logical_not(here))
            def _():
                remote(
                    self.source.at[pl.ds(0, rows)], self.target.at[m], self.sem.at[0, 0],
                    self.sem.at[1, m], me.over_core, me.z,
                ).wait_recv()


def attend_back(pair, width, heads, grad_mixed, start, lse, grads, key_sum, value_sum, query_sum, cosine, sine):
    length = heads.shape[0]
    cols = [pl.ds(pl.multiple_of(width * kind + 128 * pair, 128), 128) for kind in range(3)]
    key_sum[...] = jnp.zeros_like(key_sum)
    value_sum[...] = jnp.zeros_like(value_sum)
    for i in range(length // BLK):
        own_rows, keys = slice(BLK * i, BLK * (i + 1)), BLK * (i + 1)
        place = lax.broadcasted_iota(jnp.int32, (keys, BLK), 0)
        own = BLK * i + lax.broadcasted_iota(jnp.int32, (keys, BLK), 1)
        allowed = (place >= start[:, own_rows]) & (place <= own)
        query = heads[own_rows, cols[0]] * jnp.bfloat16(0.125)
        key, value = heads[0:keys, cols[1]], heads[0:keys, cols[2]]
        grad = grad_mixed[own_rows, cols[0]]
        for half in range(2):
            part = slice(64 * half, 64 * half + 64)
            scores = nt(key[:, part], query[:, part])
            logsum = lse[pl.ds(2 * pair + half, 1), own_rows]
            probs = jnp.where(allowed, jnp.exp(scores - logsum), 0.0)
            grad_probs = nt(value[:, part], grad[:, part])
            inner = jnp.sum(probs * grad_probs, axis=0, keepdims=True)
            grad_scores = (probs * (grad_probs - inner)).astype(jnp.bfloat16)
            value_sum[0:keys, part] += dot(probs.astype(jnp.bfloat16), grad[:, part])
            key_sum[0:keys, part] += dot(grad_scores, query[:, part])
            query_sum[own_rows, part] = tn(grad_scores, key[:, part]) * 0.125
    for kind, total in enumerate((query_sum, key_sum)):
        value = total[...]
        grads[:, cols[kind]] = (value * cosine[...] - swap_halves(value) * sine[...]).astype(jnp.bfloat16)
    grads[:, cols[2]] = value_sum[...].astype(jnp.bfloat16)


def backward_kernel(
    branch_h, slope_gate_h, slope_up_h, hidden_h, nf_t_h, normed_t_h, mixed_t_h, heads_h, lse_h, middle_h, x_h,
    g_down_h, w_qkv_h, w_o_h, w_ff_h, w_down_h, start_ref, gain_ref, cosine, sine,
    out_o, tokens_o, cols_o, o_o, down_o, gains_o, g_cols_h, g_o_h, kept_h, rows_h, grad_nf_h,
    col_got, col_keep, col_second, col_over, col_sem, col_seq, col_credit,
    down_got, down_second, down_over, down_stage, down_sem, down_seq,
    o_got, o_second, o_over, o_stage, o_sem, o_seq,
    wide_recv, half_recv, half_free, wide_sem, half_sem,
    gain_buffer, gain_sem, row_sem, load_sem, tile_sem, store_sem,
):
    me = Place()
    enter(
        [(me.over_core, me.z), (me.over_x, me.z), (me.over_y, me.z)]
        + [(me.dp - me.core + core, lax.rem(me.z + k, 4)) for k in range(1, 4) for core in range(2)]
    )
    length, width = branch_h.shape
    half_rows, own_width, half_ff = length // 2, width // 2, slope_gate_h.shape[1]
    bf16, f32 = jnp.bfloat16, jnp.float32
    vmem = pltpu.VMEM
    ff_jobs = 2 * half_ff // JOB
    cols = ColumnStream(
        me, g_cols_h, cols_o, ff_jobs, width, 2 * half_ff,
        (col_got, col_keep, col_second, col_over, col_sem, col_seq, col_credit),
    )
    downs = RowStream(
        me, g_down_h, down_o, (down_got, down_second, down_over, down_stage, down_sem, down_seq)
    )
    outs = RowStream(me, g_o_h, o_o, (o_got, o_second, o_over, o_stage, o_sem, o_seq))
    back_out = RowsBack(me, rows_h.at[0], out_o, row_sem.at[0])
    back_tokens = RowsBack(me, rows_h.at[1], tokens_o, row_sem.at[1])
    gains = GainSums(me, gains_o, gain_buffer, gain_sem)

    def load(source, target, k=0):
        return pltpu.make_async_copy(source, target, load_sem.at[k])

    def fetch(*pairs):
        for k, (source, target) in enumerate(pairs):
            load(source, target, k).start()
        for k, (source, target) in enumerate(pairs):
            load(source, target, k).wait()

    def lanes(n, size=JOB, base=0):
        return pl.ds(pl.multiple_of(base + size * n, 128), size)

    def sublanes(n, size):
        return pl.ds(pl.multiple_of(n * size, size), size)

    def grad_store(buffer, slot, target, n, k):
        return pltpu.make_async_copy(buffer.at[slot], target.at[:, lanes(n)], store_sem.at[slot, k])

    downs.tick(0)

    def feed_forward(grad_ff):
        steps = half_ff // JOB

        def hidden_grads(branch, w_tile, slopes, nf_t, g_tile):
            def tile_loads(n, slot):
                return (
                    pltpu.make_async_copy(w_down_h.at[sublanes(n, JOB), :], w_tile.at[slot], tile_sem.at[slot, 0]),
                    pltpu.make_async_copy(slope_gate_h.at[:, lanes(n)], slopes.at[slot, 0], tile_sem.at[slot, 1]),
                    pltpu.make_async_copy(slope_up_h.at[:, lanes(n)], slopes.at[slot, 1], tile_sem.at[slot, 2]),
                )

            for copy in tile_loads(0, 0):
                copy.start()
            fetch((branch_h, branch), (nf_t_h, nf_t))
            downs.tick(1)

            def step(n, carry):
                slot = lax.rem(n, 2)
                for copy in tile_loads(n, slot):
                    copy.wait()

                @pl.when(n + 1 < steps)
                def _():
                    for copy in tile_loads(n + 1, 1 - slot):
                        copy.start()

                grad_hidden = nt(branch[...], w_tile[slot])

                @pl.when(n > 0)
                def _():
                    for kind in range(2):
                        grad_store(g_tile, kind, g_cols_h, 2 * n - 2 + kind, 0).wait()

                for kind in range(2):
                    grad = (grad_hidden * slopes[slot, kind].astype(f32)).astype(bf16)
                    grad_ff[:, lanes(n, JOB, half_ff * kind)] = grad
                    g_tile[kind] = dot(nf_t[...], grad).astype(bf16)
                    grad_store(g_tile, kind, g_cols_h, 2 * n + kind, 0).start()

                @pl.when(lax.rem(n, 2) == 1)
                def _():
                    cols.tick(n // 2)

                @pl.when((lax.rem(n, 2) == 0) & (n > 0))
                def _():
                    downs.tick(1 + n // 2)

                return carry

            lax.fori_loop(0, steps, step, 0)
            for kind in range(2):
                grad_store(g_tile, kind, g_cols_h, 2 * steps - 2 + kind, 0).wait()

        pl.run_scoped(
            hidden_grads, vmem((length, width), bf16), vmem((2, JOB, width), bf16),
            vmem((2, 2, length, JOB), bf16), vmem((width, length), bf16), vmem((2, width, JOB), bf16),
        )

        def layer_out(hidden, w_down, send, total):
            other, own = 1 - me.core, me.core
            fetch((w_down_h, w_down), (hidden_h.at[sublanes(other, half_rows), :], hidden))
            load(middle_h.at[sublanes(own, half_rows), :], total, 2).start()

            def other_tile(n, carry):
                send[:, lanes(n)] = dot(hidden[...], w_down[:, lanes(n)]).astype(bf16)
                return carry

            lax.fori_loop(0, width // JOB, other_tile, 0)
            exchange = remote(send, half_recv, half_sem.at[0, 0], half_sem.at[1, 0], me.over_core, me.z)
            exchange.start()
            fetch((hidden_h.at[sublanes(own, half_rows), :], hidden))
            load(middle_h.at[sublanes(own, half_rows), :], total, 2).wait()

            def own_tile(n, carry):
                total[:, lanes(n)] += dot(hidden[...], w_down[:, lanes(n)])
                return carry

            lax.fori_loop(0, width // JOB, own_tile, 0)
            exchange.wait()

            def combine(k, carry):
                part = sublanes(k, 64)
                send[part, :] = (total[part, :] + half_recv[part, :].astype(f32)).astype(bf16)
                return carry

            lax.fori_loop(0, half_rows // 64, combine, 0)
            pl.semaphore_signal(
                half_free, inc=1, device_id={"dp": me.over_core, "seq": me.z},
                device_id_type=pl.DeviceIdType.MESH,
            )
            fetch((send, rows_h.at[0]))

        pl.run_scoped(
            layer_out, vmem((half_rows, half_ff), bf16), vmem((half_ff, width), bf16),
            vmem((half_rows, width), bf16), vmem((half_rows, width), f32),
        )
        back_out.start()
        cols.tick(steps // 2)
        downs.tick(1 + steps // 2)

    chunk = 2 * JOB
    chunks = width // chunk

    def wide_copy(send, k):
        part = pl.ds(chunk * k, chunk)
        return remote(
            send.at[:, part], wide_recv.at[:, part], wide_sem.at[0, k], wide_sem.at[1, k], me.over_core, me.z
        )

    def with_grad_ff(grad_ff):
        feed_forward(grad_ff)

        def input_grads(w_tile, send, parts):
            def tile_load(n, kind):
                return pltpu.make_async_copy(
                    w_ff_h.at[sublanes(n, JOB), pl.ds(half_ff * kind, half_ff)], w_tile.at[kind],
                    tile_sem.at[kind, 0],
                )

            def part_store(n, slot):
                return pltpu.make_async_copy(parts.at[slot], grad_nf_h.at[:, lanes(n)], store_sem.at[slot, 0])

            for kind in range(2):
                tile_load(0, kind).start()
            count = width // JOB

            def step(n, carry):
                slot = lax.rem(n, 2)
                tile_load(n, 0).wait()
                part = nt(grad_ff[:, 0:half_ff], w_tile[0])

                @pl.when(n + 1 < count)
                def _():
                    tile_load(n + 1, 0).start()

                tile_load(n, 1).wait()
                part = part + nt(grad_ff[:, half_ff : 2 * half_ff], w_tile[1])

                @pl.when(n + 1 < count)
                def _():
                    tile_load(n + 1, 1).start()

                @pl.when(n >= 2)
                def _():
                    part_store(n - 2, slot).wait()

                parts[slot] = part
                part_store(n, slot).start()
                send[:, lanes(n)] = part.astype(bf16)
                for k in range(chunks):
                    @pl.when(n == 2 * k + 1)
                    def _():
                        wide_copy(send, k).start()

                @pl.when(lax.rem(n, 2) == 1)
                def _():
                    cols.tick(5 + n // 2)

                @pl.when(lax.rem(n, 2) == 0)
                def _():
                    downs.tick(6 + n // 2)

                return carry

            lax.fori_loop(0, count, step, 0)
            for n in range(count - 2, count):
                part_store(n, n % 2).wait()
            for k in range(chunks):
                wide_copy(send, k).wait()

        pl.run_scoped(
            input_grads, vmem((2, JOB, half_ff), bf16), vmem((length, width), bf16), vmem((2, length, JOB), f32)
        )

    pl.run_scoped(with_grad_ff, vmem((length, 2 * half_ff), bf16))

    def to_attention(grad_attn):
        def norm_back(grad_nf, middle, branch):
            fetch((middle_h, middle), (branch_h, branch), (grad_nf_h, grad_nf))
            gain = gain_ref[1:2, :]

            def rows(k, total):
                part = sublanes(k, 64)
                grad = grad_nf[part, :] + wide_recv[part, :].astype(f32)
                gained, values = norm_rows_back(middle[part, :], gain, grad)
                values = values + branch[part, :].astype(f32)
                grad_nf[part, :] = values
                grad_attn[part, :] = values.astype(bf16)
                return total + gained

            total = lax.fori_loop(0, length // 64, rows, jnp.zeros((1, width), f32))
            gain_buffer[0, 0, 1:2, :] = 0.5 * total
            kept = load(grad_nf.at[sublanes(me.core, half_rows), :], kept_h, 0)
            kept.start()
            cols.tick(8)
            kept.wait()

        pl.run_scoped(
            norm_back, vmem((length, width), f32), vmem((length, width), f32), vmem((length, width), bf16)
        )

        def out_projection(w_o, mixed_t, g_tile, grad_mixed):
            fetch((w_o_h, w_o), (mixed_t_h, mixed_t))
            for n in range(own_width // JOB):
                grad_mixed[:, JOB * n : JOB * (n + 1)] = nt(
                    grad_attn[...], w_o[JOB * n : JOB * (n + 1), :]
                ).astype(bf16)
            placed = load(grad_mixed, wide_recv.at[:, pl.ds(0, own_width)], 3)
            placed.start()
            count = width // JOB

            def step(n, carry):
                slot = lax.rem(n, 2)

                @pl.when(n >= 2)
                def _():
                    grad_store(g_tile, slot, g_o_h, n - 2, 1).wait()

                g_tile[slot] = dot(mixed_t[...], grad_attn[:, lanes(n)]).astype(bf16)
                grad_store(g_tile, slot, g_o_h, n, 1).start()

                @pl.when(lax.rem(n, 3) == 2)
                def _():
                    cols.tick(9 + n // 3)

                return carry

            lax.fori_loop(0, count, step, 0)
            for n in range(count - 2, count):
                grad_store(g_tile, n % 2, g_o_h, n, 1).wait()
            placed.wait()

        pl.run_scoped(
            out_projection, vmem((own_width, width), bf16), vmem((own_width, length), bf16),
            vmem((2, own_width, JOB), bf16), vmem((length, own_width), bf16),
        )

    pl.run_scoped(to_attention, vmem((length, width), bf16))

    def attention(grads):
        def heads_back(heads, lse, key_sum, value_sum, query_sum):
            fetch((heads_h, heads), (lse_h, lse))

            def step(pair, carry):
                attend_back(
                    pair, own_width, heads, wide_recv, start_ref, lse, grads, key_sum, value_sum, query_sum, cosine, sine
                )
                outs.tick(pair)

                @pl.when(pair > 0)
                def _():
                    cols.tick(10 + pair)

                @pl.when(pair < 4)
                def _():
                    downs.tick(9 + pair)

                return carry

            lax.fori_loop(0, own_width // 128, step, 0)

        pl.run_scoped(
            heads_back, vmem((length, 3 * own_width), bf16), vmem((128, length), f32),
            *[vmem((length, 128), f32)] * 3,
        )

        def projection_grads(normed_t, g_tile):
            fetch((normed_t_h, normed_t))
            count = 3 * own_width // JOB

            def step(n, carry):
                slot = lax.rem(n, 2)
                g_tile[slot] = dot(normed_t[...], grads[:, lanes(n)]).astype(bf16)

                @pl.when(n >= 1)
                def _():
                    grad_store(g_tile, 1 - slot, g_cols_h, ff_jobs + n - 1, 1).wait()

                grad_store(g_tile, slot, g_cols_h, ff_jobs + n, 1).start()

                @pl.when(n >= 1)
                def _():
                    cols.tick(15 + n)

                @pl.when(n < 7)
                def _():
                    outs.tick(6 + n)

                return carry

            lax.fori_loop(0, count, step, 0)
            grad_store(g_tile, (count - 1) % 2, g_cols_h, ff_jobs + count - 1, 1).wait()

        pl.run_scoped(projection_grads, vmem((width, length), bf16), vmem((2, width, JOB), bf16))

        def tokens_back(w_tile, send, total, x_rows, kept):
            def tile_load(n, slot):
                return pltpu.make_async_copy(w_qkv_h.at[sublanes(n, JOB), :], w_tile.at[slot], tile_sem.at[slot, 0])

            tile_load(0, 0).start()
            load(x_h.at[sublanes(me.core, half_rows), :], x_rows, 0).start()
            load(kept_h, kept, 1).start()
            count = width // JOB

            def step(n, carry):
                slot = lax.rem(n, 2)
                tile_load(n, slot).wait()

                @pl.when(n + 1 < count)
                def _():
                    tile_load(n + 1, 1 - slot).start()

                send[:, lanes(n)] = nt(grads[sublanes(1 - me.core, half_rows), :], w_tile[slot]).astype(bf16)
                total[:, lanes(n)] = nt(grads[sublanes(me.core, half_rows), :], w_tile[slot])
                return carry

            lax.fori_loop(0, count, step, 0)
            pl.semaphore_wait(half_free, 1)
            exchange = remote(send, half_recv, half_sem.at[0, 0], half_sem.at[1, 0], me.over_core, me.z)
            exchange.start()
            cols.tick(15 + 3 * own_width // JOB)
            load(x_h.at[sublanes(me.core, half_rows), :], x_rows, 0).wait()
            load(kept_h, kept, 1).wait()
            exchange.wait()
            gain = gain_ref[0:1, :]

            def rows(k, sums):
                part = sublanes(k, 64)
                grad = total[part, :] + half_recv[part, :].astype(f32)
                gained, values = norm_rows_back(x_rows[part, :].astype(f32), gain, grad)
                send[part, :] = (values + kept[part, :]).astype(bf16)
                return sums + gained

            gain_buffer[0, 0, 0:1, :] = lax.fori_loop(0, half_rows // 64, rows, jnp.zeros((1, width), f32))
            gains.start()
            fetch((send, rows_h.at[1]))

        pl.run_scoped(
            tokens_back, vmem((2, JOB, 3 * own_width), bf16), vmem((half_rows, width), bf16),
            vmem((half_rows, width), f32), vmem((half_rows, width), bf16), vmem((half_rows, width), f32),
        )
        back_tokens.start()

    pl.run_scoped(attention, vmem((length, 3 * own_width), bf16))

    first = 16 + 3 * own_width // JOB

    def rest(t, carry):
        cols.tick(t)
        for k in range(GAIN_HOPS):
            @pl.when(t == first + 1 + k)
            def _():
                gains.step(k)

        return carry

    lax.fori_loop(first, cols.ticks, rest, 0)
    gains.drain()
    back_out.drain()
    back_tokens.drain()


def norm_rows_back(values, gain, grad):
    scale = lax.rsqrt(jnp.mean(values * values, axis=-1, keepdims=True) + EPS)
    unit = values * scale
    inner = grad * gain
    return (
        jnp.sum(grad * unit, axis=0, keepdims=True),
        scale * (inner - unit * jnp.mean(inner * unit, axis=-1, keepdims=True)),
    )


COLUMN_SLOTS = 10


def backward(branch, slopes, hidden, turned, heads, lse, middle, x, g_down, weights, start, gain, cosine, sine):
    length, width = branch.shape
    half, half_ff = width // 2, hidden.shape[1]
    rows = length // 4
    bf16, f32 = jnp.bfloat16, jnp.float32

    def shape(*dims, dtype=bf16):
        return jax.ShapeDtypeStruct(dims, dtype)

    columns = 2 * half_ff + 3 * half
    shapes = [
        shape(2, rows, width),
        shape(2, rows, width),
        shape(width // 8, 2 * columns),
        shape(width // 8, width),
        shape(half_ff // 4, width),
        shape(2, width, dtype=f32),
        shape(width, columns),
        shape(half, width),
        shape(length // 2, width, dtype=f32),
        shape(2, length // 2, width),
        shape(length, width, dtype=f32),
    ]
    dma, vmem = pltpu.SemaphoreType.DMA, pltpu.VMEM
    whole = pl.BlockSpec(memory_space=pltpu.VMEM)
    ring, row = COLUMN_SLOTS, width // 4
    jobs = width // JOB
    row_buffers = []
    for depth in (half_ff // 2, half // 2):
        row_buffers += [
            vmem((jobs, depth, JOB), bf16), vmem((jobs, depth, JOB), bf16), vmem((jobs, 2, depth, JOB), bf16),
            vmem((depth, JOB), bf16), dma((jobs, 3, 4)), dma((jobs, 2, 3)),
        ]
    return pl.pallas_call(
        backward_kernel,
        in_specs=[ANY] * 16 + [whole] * 4,
        out_specs=[ANY] * 5 + [whole] + [ANY] * 5,
        out_shape=shapes,
        scratch_shapes=[
            vmem((ring, 2 * row, JOB), bf16), vmem((ring, 2 * row, JOB), bf16), vmem((ring, row, JOB), bf16),
            vmem((ring, 2, row, JOB), bf16), dma((ring, 3, 4)), dma((ring, 2, 3)),
            pltpu.SemaphoreType.REGULAR((ring,)),
        ]
        + row_buffers
        + [
            vmem((length, width), bf16), vmem((length // 2, width), bf16), pltpu.SemaphoreType.REGULAR,
            dma((2, 3)), dma((2, 1)),
            vmem((GAIN_HOPS, 2, 2, width), f32), dma((2, GAIN_HOPS)), dma((2, 3, 2)), dma((4,)), dma((2, 3)),
            dma((2, 2)),
        ],
        compiler_params=pltpu.CompilerParams(
            collective_id=1, has_side_effects=True, vmem_limit_bytes=63 * 1024 * 1024
        ),
        cost_estimate=pl.CostEstimate(flops=0, bytes_accessed=800_000_000, transcendentals=0),
        name="backward",
    )(
        branch, *slopes, hidden, *turned, heads, lse, middle, x, g_down, *weights, start, gain, cosine, sine
    )


def wide(value):
    return value.astype(jnp.float32)


def dot(a, b):
    return jnp.dot(a, b, preferred_element_type=jnp.float32)


def column_device(
    tokens, segment_ids, out_grad, w_q, w_k, w_v, w_o, w_gate, w_up, w_down, gain_attn, gain_ffn
):
    dp_at = lax.axis_index("dp")
    rows, width = tokens.shape[1], tokens.shape[2]
    length, ff = 4 * rows, w_gate.shape[1]
    gains = lax.dynamic_update_slice_in_dim(
        jnp.zeros((2, width), jnp.bfloat16),
        jnp.stack([gain_attn, gain_ffn]),
        dp_at * gain_attn.shape[0],
        1,
    )
    cosine, sine = rope_tables(jnp.arange(length, dtype=jnp.int32), HD // 2)
    cosine = jnp.concatenate([cosine] * 4, axis=1)
    sine = jnp.concatenate([-sine, sine, -sine, sine], axis=1)
    (
        x_low, docs, grad_branch, gains, full_qkv, full_o, full_ff, full_down, heads, lse, middle,
        slope_gate, slope_up, hidden, g_down, start, gain, normed_t, nf_t, mixed_t,
    ) = gather_all(
        tokens, segment_ids.reshape(2, 1, rows), out_grad, gains, cosine, sine,
        (w_q, w_k, w_v, w_o, w_gate, w_up, w_down),
    )
    result, grad_tokens, g_cols, g_o, g_down, grad_gains = backward(
        grad_branch, (slope_gate, slope_up), hidden, (nf_t, normed_t, mixed_t), heads, lse, middle, x_low, g_down,
        (full_qkv, full_o, full_ff, full_down), start, gain, cosine, sine,
    )[:6]
    grad_gains = lax.dynamic_slice_in_dim(grad_gains, dp_at * (width // 8), width // 8, 1)
    first = 2 * ff
    return (
        result,
        wide(grad_tokens),
        wide(g_cols[:, first : first + width]),
        wide(g_cols[:, first + width : first + 2 * width]),
        wide(g_cols[:, first + 2 * width :]),
        wide(g_o),
        wide(g_cols[:, :ff]),
        wide(g_cols[:, ff:first]),
        wide(g_down),
        grad_gains[0],
        grad_gains[1],
    )


def solution(mesh):
    placed = (
        P(None, ("dp", "seq"), None),
        P(None, ("dp", "seq")),
        P(None, ("dp", "seq"), None),
        P("dp", None),
        P("dp", None),
        P("dp", None),
        P("dp", None),
        P("dp", None),
        P("dp", None),
        P("dp", None),
        P("dp"),
        P("dp"),
    )
    return jax.shard_map(
        column_device if dict(mesh.shape) == FAST_MESH else per_device,
        mesh=mesh,
        in_specs=placed,
        out_specs=(
            P(None, ("dp", "seq"), None),
            P(None, ("dp", "seq"), None),
            P("dp", None),
            P("dp", None),
            P("dp", None),
            P("dp", None),
            P("dp", None),
            P("dp", None),
            P("dp", None),
            P("dp"),
            P("dp"),
        ),
        check_vma=False,
    )
```

```python
import functools
import math

import jax
import jax.numpy as jnp
import numpy as np
from jax import lax
from jax.experimental import pallas as pl
from jax.experimental.pallas import tpu as pltpu
from jax.sharding import PartitionSpec as P

HEADS = 24
HD = 64


EPS = 1e-05


def positions_of(doc_row):
    count = doc_row.shape[0]
    place = jnp.arange(count, dtype=jnp.int32)
    before = jnp.concatenate([doc_row[:1], doc_row[:-1]])
    starts = (place == 0) | (doc_row != before)
    first_place = lax.cummax(jnp.where(starts, place, jnp.zeros_like(place)), axis=0)
    return place - first_place


def rope_tables(where_at, half):
    inverse = jnp.exp(jnp.arange(half, dtype=jnp.float32) * (-math.log(10000.0) / half))
    angle = where_at.astype(jnp.float32)[:, None] * inverse[None, :]
    return (jnp.cos(angle), jnp.sin(angle))


def rotate(values, cosine, sine):
    half = values.shape[-1] // 2
    first, second = (values[..., :half], values[..., half:])
    cos_heads, sin_heads = (cosine[:, None, :], sine[:, None, :])
    return jnp.concatenate(
        [first * cos_heads - second * sin_heads, second * cos_heads + first * sin_heads], axis=-1
    )


def rotate_back(grads, cosine, sine):
    half = grads.shape[-1] // 2
    first, second = (grads[..., :half], grads[..., half:])
    cos_heads, sin_heads = (cosine[:, None, :], sine[:, None, :])
    return jnp.concatenate(
        [first * cos_heads + second * sin_heads, second * cos_heads - first * sin_heads], axis=-1
    )


def rms_norm(values, gain):
    return values * lax.rsqrt(jnp.mean(values * values, axis=-1, keepdims=True) + EPS) * gain


def norm_backward(values, gain, grad_normed):
    scale = lax.rsqrt(jnp.mean(values * values, axis=-1, keepdims=True) + EPS)
    unit = values * scale
    grad_gain = jnp.sum(grad_normed * unit, axis=0)
    inner = grad_normed * gain
    grad_values = scale * (inner - unit * jnp.mean(inner * unit, axis=-1, keepdims=True))
    return (grad_gain, grad_values)


def block_scores(query_heads, key_heads, doc_row, start, block):
    length = doc_row.shape[0]
    place = jnp.arange(length, dtype=jnp.int32)
    query_block = lax.dynamic_slice_in_dim(query_heads, start, block, 0)
    doc_block = lax.dynamic_slice_in_dim(doc_row, start, block, 0)
    rows_block = start + jnp.arange(block, dtype=jnp.int32)
    allowed = (doc_block[:, None] == doc_row[None, :]) & (rows_block[:, None] >= place[None, :])
    scores = (
        jnp.einsum("qhd,khd->hqk", query_block, key_heads, preferred_element_type=jnp.float32)
        * 0.125
    )
    return (query_block, jnp.where(allowed[None], scores, -1e30))


def attention_forward(query, key, value, doc_row):
    length = query.shape[0]
    head_shape = (length, query.shape[1] // HD, HD)
    query_heads, key_heads, value_heads = (
        query.reshape(head_shape),
        key.reshape(head_shape),
        value.reshape(head_shape),
    )
    block = min(512, length)
    starts = jnp.arange(length // block, dtype=jnp.int32) * block

    def one_block(start):
        unused, scores = block_scores(query_heads, key_heads, doc_row, start, block)
        peak = jnp.max(scores, axis=-1, keepdims=True)
        expo = jnp.exp(scores - peak)
        total = jnp.sum(expo, axis=-1, keepdims=True)
        probs_low = (expo / total).astype(jnp.bfloat16)
        mixed = jnp.einsum(
            "hqk,khd->qhd", probs_low, value_heads, preferred_element_type=jnp.float32
        )
        return (mixed.astype(jnp.bfloat16), (peak + jnp.log(total))[..., 0])

    mixed, logsum = lax.map(one_block, starts)
    return (mixed.reshape(length, query.shape[1]), logsum)


def attention_backward(query, key, value, doc_row, logsum, grad_mixed, cosine, sine):
    length = query.shape[0]
    head_shape = (length, query.shape[1] // HD, HD)
    query_heads, key_heads, value_heads = (
        query.reshape(head_shape),
        key.reshape(head_shape),
        value.reshape(head_shape),
    )
    grad_heads = grad_mixed.reshape(head_shape)
    block = min(512, length)
    starts = jnp.arange(length // block, dtype=jnp.int32) * block

    def one_block(carry, item):
        grad_key, grad_value = carry
        start, logsum_block = item
        query_block, scores = block_scores(query_heads, key_heads, doc_row, start, block)
        probs = jnp.exp(scores - logsum_block[..., None])
        probs_low = probs.astype(jnp.bfloat16)
        grad_block = lax.dynamic_slice_in_dim(grad_heads, start, block, 0)
        grad_probs = jnp.einsum(
            "qhd,khd->hqk", grad_block, value_heads, preferred_element_type=jnp.float32
        )
        inner = jnp.sum(probs * grad_probs, axis=-1, keepdims=True)
        grad_scores = (probs * (grad_probs - inner)).astype(jnp.bfloat16)
        grad_query = (
            jnp.einsum("hqk,khd->qhd", grad_scores, key_heads, preferred_element_type=jnp.float32)
            * 0.125
        )
        grad_key = (
            grad_key
            + jnp.einsum(
                "hqk,qhd->khd", grad_scores, query_block, preferred_element_type=jnp.float32
            )
            * 0.125
        )
        grad_value = grad_value + jnp.einsum(
            "hqk,qhd->khd", probs_low, grad_block, preferred_element_type=jnp.float32
        )
        return ((grad_key, grad_value), grad_query)

    zeros_heads = jnp.zeros(head_shape, jnp.float32)
    (grad_key, grad_value), grad_query = lax.scan(
        one_block, (zeros_heads, zeros_heads), (starts, logsum)
    )
    grad_query = rotate_back(grad_query.reshape(head_shape), cosine, sine)
    grad_key = rotate_back(grad_key, cosine, sine)
    width_here = query.shape[1]
    return (
        grad_query.reshape(length, width_here).astype(jnp.bfloat16),
        grad_key.reshape(length, width_here).astype(jnp.bfloat16),
        grad_value.reshape(length, width_here).astype(jnp.bfloat16),
    )


def per_device(
    tokens, segment_ids, out_grad, w_q, w_k, w_v, w_o, w_gate, w_up, w_down, gain_attn, gain_ffn
):
    micro, rows, width = tokens.shape
    offset = lax.axis_index("seq") * rows
    shards = (w_q, w_k, w_v, w_o, w_gate, w_up, w_down, gain_attn, gain_ffn)
    gathered = (
        lax.all_gather(shards[0], "dp", axis=0, tiled=True),
        lax.all_gather(shards[1], "dp", axis=0, tiled=True),
        lax.all_gather(shards[2], "dp", axis=0, tiled=True),
        lax.all_gather(shards[3], "dp", axis=0, tiled=True),
        lax.all_gather(shards[4], "dp", axis=0, tiled=True),
        lax.all_gather(shards[5], "dp", axis=0, tiled=True),
        lax.all_gather(shards[6], "dp", axis=0, tiled=True),
        lax.all_gather(shards[7], "dp", axis=0, tiled=True),
        lax.all_gather(shards[8], "dp", axis=0, tiled=True),
    )
    docs = lax.all_gather(segment_ids, "seq", axis=1, tiled=True)
    full_q, full_k, full_v, full_o, full_gate, full_up, full_down, full_gain_a, full_gain_f = (
        gathered
    )
    gain_a = full_gain_a.astype(jnp.float32)
    gain_f = full_gain_f.astype(jnp.float32)
    row_heads = (rows, HEADS, HD)
    saved = []
    results = []
    for micro_index in range(micro):
        rows_in = tokens[micro_index].astype(jnp.float32)
        doc_row = docs[micro_index]
        cosine, sine = rope_tables(positions_of(doc_row), HD // 2)
        own_cos = lax.dynamic_slice_in_dim(cosine, offset, rows, 0)
        own_sin = lax.dynamic_slice_in_dim(sine, offset, rows, 0)
        normed = rms_norm(rows_in, gain_a).astype(jnp.bfloat16)
        query_rows = jnp.dot(normed, full_q, preferred_element_type=jnp.float32).reshape(row_heads)
        query_rows = rotate(query_rows, own_cos, own_sin).reshape(rows, width).astype(jnp.bfloat16)
        key_rows = jnp.dot(normed, full_k, preferred_element_type=jnp.float32).reshape(row_heads)
        key_rows = rotate(key_rows, own_cos, own_sin).reshape(rows, width).astype(jnp.bfloat16)
        value_rows = jnp.dot(normed, full_v, preferred_element_type=jnp.float32).astype(
            jnp.bfloat16
        )
        query, key, value = (
            lax.all_to_all(query_rows, "seq", split_axis=1, concat_axis=0, tiled=True),
            lax.all_to_all(key_rows, "seq", split_axis=1, concat_axis=0, tiled=True),
            lax.all_to_all(value_rows, "seq", split_axis=1, concat_axis=0, tiled=True),
        )
        mixed, logsum = attention_forward(query, key, value, doc_row)
        mixed_rows = lax.all_to_all(mixed, "seq", split_axis=0, concat_axis=1, tiled=True)
        middle = rows_in + jnp.dot(mixed_rows, full_o, preferred_element_type=jnp.float32)
        normed_ffn = rms_norm(middle, gain_f).astype(jnp.bfloat16)
        gate = jnp.dot(normed_ffn, full_gate, preferred_element_type=jnp.float32)
        up_value = jnp.dot(normed_ffn, full_up, preferred_element_type=jnp.float32)
        hidden = (jax.nn.silu(gate) * up_value).astype(jnp.bfloat16)
        result = middle + jnp.dot(hidden, full_down, preferred_element_type=jnp.float32)
        results.append(result.astype(jnp.bfloat16))
        saved.append(
            (
                rows_in,
                doc_row,
                cosine,
                sine,
                normed,
                query,
                key,
                value,
                logsum,
                mixed_rows,
                middle,
                normed_ffn,
                gate,
                up_value,
                hidden,
            )
        )
    back_weights = (
        lax.all_gather(shards[0], "dp", axis=0, tiled=True),
        lax.all_gather(shards[1], "dp", axis=0, tiled=True),
        lax.all_gather(shards[2], "dp", axis=0, tiled=True),
        lax.all_gather(shards[3], "dp", axis=0, tiled=True),
        lax.all_gather(shards[4], "dp", axis=0, tiled=True),
        lax.all_gather(shards[5], "dp", axis=0, tiled=True),
        lax.all_gather(shards[6], "dp", axis=0, tiled=True),
        lax.all_gather(shards[7], "dp", axis=0, tiled=True),
        lax.all_gather(shards[8], "dp", axis=0, tiled=True),
    )
    back_q, back_k, back_v, back_o, back_gate, back_up, back_down, back_gain_a, back_gain_f = (
        back_weights
    )
    gain_back_a = back_gain_a.astype(jnp.float32)
    gain_back_f = back_gain_f.astype(jnp.float32)
    totals = [jnp.zeros(weight.shape, jnp.float32) for weight in back_weights]
    grad_inputs = []
    for micro_index in range(micro):
        (
            rows_in,
            doc_row,
            cosine,
            sine,
            normed,
            query,
            key,
            value,
            logsum,
            mixed_rows,
            middle,
            normed_ffn,
            gate,
            up_value,
            hidden,
        ) = saved[micro_index]
        grad_out = out_grad[micro_index].astype(jnp.float32)
        grad_branch = grad_out.astype(jnp.bfloat16)
        totals[6] = totals[6] + jnp.einsum(
            "tf,td->fd", hidden, grad_branch, preferred_element_type=jnp.float32
        )
        grad_hidden = jnp.einsum(
            "td,fd->tf", grad_branch, back_down, preferred_element_type=jnp.float32
        )
        sigma = jax.nn.sigmoid(gate)
        grad_gate = (grad_hidden * up_value * sigma * (1.0 + gate * (1.0 - sigma))).astype(
            jnp.bfloat16
        )
        grad_up = (grad_hidden * jax.nn.silu(gate)).astype(jnp.bfloat16)
        totals[4] = totals[4] + jnp.einsum(
            "td,tf->df", normed_ffn, grad_gate, preferred_element_type=jnp.float32
        )
        totals[5] = totals[5] + jnp.einsum(
            "td,tf->df", normed_ffn, grad_up, preferred_element_type=jnp.float32
        )
        grad_normed_ffn = jnp.einsum(
            "tf,df->td", grad_gate, back_gate, preferred_element_type=jnp.float32
        )
        grad_normed_ffn = grad_normed_ffn + jnp.einsum(
            "tf,df->td", grad_up, back_up, preferred_element_type=jnp.float32
        )
        grad_gain_f, grad_middle = norm_backward(middle, gain_back_f, grad_normed_ffn)
        totals[8] = totals[8] + grad_gain_f
        grad_middle = grad_middle + grad_out
        grad_attn = grad_middle.astype(jnp.bfloat16)
        totals[3] = totals[3] + jnp.einsum(
            "ti,td->id", mixed_rows, grad_attn, preferred_element_type=jnp.float32
        )
        grad_mixed_rows = jnp.einsum(
            "td,id->ti", grad_attn, back_o, preferred_element_type=jnp.float32
        ).astype(jnp.bfloat16)
        grad_mixed = lax.all_to_all(grad_mixed_rows, "seq", split_axis=1, concat_axis=0, tiled=True)
        grad_query, grad_key, grad_value = attention_backward(
            query, key, value, doc_row, logsum, grad_mixed, cosine, sine
        )
        query_back, key_back, value_back = (
            lax.all_to_all(grad_query, "seq", split_axis=0, concat_axis=1, tiled=True),
            lax.all_to_all(grad_key, "seq", split_axis=0, concat_axis=1, tiled=True),
            lax.all_to_all(grad_value, "seq", split_axis=0, concat_axis=1, tiled=True),
        )
        totals[0] = totals[0] + jnp.einsum(
            "td,te->de", normed, query_back, preferred_element_type=jnp.float32
        )
        totals[1] = totals[1] + jnp.einsum(
            "td,te->de", normed, key_back, preferred_element_type=jnp.float32
        )
        totals[2] = totals[2] + jnp.einsum(
            "td,te->de", normed, value_back, preferred_element_type=jnp.float32
        )
        grad_normed = jnp.einsum(
            "te,de->td", query_back, back_q, preferred_element_type=jnp.float32
        )
        grad_normed = grad_normed + jnp.einsum(
            "te,de->td", key_back, back_k, preferred_element_type=jnp.float32
        )
        grad_normed = grad_normed + jnp.einsum(
            "te,de->td", value_back, back_v, preferred_element_type=jnp.float32
        )
        grad_gain_a, grad_rows = norm_backward(rows_in, gain_back_a, grad_normed)
        totals[7] = totals[7] + grad_gain_a
        grad_inputs.append(grad_rows + grad_middle)
    summed_all = (
        totals[0],
        totals[1],
        totals[2],
        totals[3],
        totals[4],
        totals[5],
        totals[6],
        totals[7],
        totals[8],
    )
    pieces = (
        lax.psum_scatter(
            summed_all[0].astype(jnp.bfloat16), "dp", scatter_dimension=0, tiled=True
        ).astype(jnp.float32),
        lax.psum_scatter(
            summed_all[1].astype(jnp.bfloat16), "dp", scatter_dimension=0, tiled=True
        ).astype(jnp.float32),
        lax.psum_scatter(
            summed_all[2].astype(jnp.bfloat16), "dp", scatter_dimension=0, tiled=True
        ).astype(jnp.float32),
        lax.psum_scatter(
            summed_all[3].astype(jnp.bfloat16), "dp", scatter_dimension=0, tiled=True
        ).astype(jnp.float32),
        lax.psum_scatter(
            summed_all[4].astype(jnp.bfloat16), "dp", scatter_dimension=0, tiled=True
        ).astype(jnp.float32),
        lax.psum_scatter(
            summed_all[5].astype(jnp.bfloat16), "dp", scatter_dimension=0, tiled=True
        ).astype(jnp.float32),
        lax.psum_scatter(
            summed_all[6].astype(jnp.bfloat16), "dp", scatter_dimension=0, tiled=True
        ).astype(jnp.float32),
        lax.psum_scatter(
            summed_all[7].astype(jnp.bfloat16), "dp", scatter_dimension=0, tiled=True
        ).astype(jnp.float32),
        lax.psum_scatter(
            summed_all[8].astype(jnp.bfloat16), "dp", scatter_dimension=0, tiled=True
        ).astype(jnp.float32),
    )
    pieces = (
        lax.psum(pieces[0].astype(jnp.bfloat16), "seq").astype(jnp.float32),
        lax.psum(pieces[1].astype(jnp.bfloat16), "seq").astype(jnp.float32),
        lax.psum(pieces[2].astype(jnp.bfloat16), "seq").astype(jnp.float32),
        lax.psum(pieces[3].astype(jnp.bfloat16), "seq").astype(jnp.float32),
        lax.psum(pieces[4].astype(jnp.bfloat16), "seq").astype(jnp.float32),
        lax.psum(pieces[5].astype(jnp.bfloat16), "seq").astype(jnp.float32),
        lax.psum(pieces[6].astype(jnp.bfloat16), "seq").astype(jnp.float32),
        lax.psum(pieces[7].astype(jnp.bfloat16), "seq").astype(jnp.float32),
        lax.psum(pieces[8].astype(jnp.bfloat16), "seq").astype(jnp.float32),
    )
    return (
        jnp.stack(results),
        jnp.stack(grad_inputs),
        pieces[0],
        pieces[1],
        pieces[2],
        pieces[3],
        pieces[4],
        pieces[5],
        pieces[6],
        pieces[7],
        pieces[8],
    )


BLK = 256
LOG2E = 1.4426950408889634


def swap_halves(v):
    lane = lax.broadcasted_iota(jnp.int32, v.shape, 1)
    width = v.shape[1]
    up = pltpu.roll(v, width - 32, axis=1)
    down = pltpu.roll(v, 32, axis=1)
    return jnp.where(lane % 64 < 32, up, down)


def nt(a, b):
    return lax.dot_general(a, b, (((1,), (1,)), ((), ())), preferred_element_type=jnp.float32)


def tn(a, b):
    return lax.dot_general(a, b, (((0,), (0,)), ((), ())), preferred_element_type=jnp.float32)


FAST_MESH = {"dp": 8, "seq": 4}
ANY = pl.BlockSpec(memory_space=pl.ANY)


class Place:
    def __init__(self):
        self.dp, self.z = lax.axis_index("dp"), lax.axis_index("seq")
        self.core = self.dp % 2
        self.x = (self.dp // 2) % 2
        self.y = self.dp // 4
        self.over_core = self.dp + 1 - 2 * self.core
        self.over_x = self.dp + 2 - 4 * self.x
        self.over_y = self.dp + 4 - 8 * self.y
        self.middle = (self.z == 1) | (self.z == 2)


def enter(devices):
    barrier = pltpu.get_barrier_semaphore()
    for dp, seq in devices:
        pl.semaphore_signal(
            barrier, inc=1, device_id={"dp": dp, "seq": seq}, device_id_type=pl.DeviceIdType.MESH
        )
    pl.semaphore_wait(barrier, len(devices))


def remote(src, dst, send_sem, recv_sem, dp, seq):
    return pltpu.make_async_remote_copy(
        src_ref=src,
        dst_ref=dst,
        send_sem=send_sem,
        recv_sem=recv_sem,
        device_id={"dp": dp, "seq": seq},
        device_id_type=pl.DeviceIdType.MESH,
    )


def gather_kernel(
    tokens, segments, out_grad, gains, cosine, sine, w_q, w_k, w_v, w_o, w_gate, w_up, w_down,
    x_out, seg_out, g_out, gains_out, qkv_out, o_out, ff_out, down_out,
    heads_out, lse_out, middle_out, slope_gate_out, slope_up_out, hidden_out, g_down_out, start_out,
    gain_out, normed_t_out, nf_t_out, mixed_t_out,
    send, recv, local, row_send, row_recv, row_local, gain_send, gain_recv,
    x_v, seg_v, gains_v, normed_v, w_qkv_v, heads_v, mixed_v, w_o_v, middle_v, part_send, part_recv,
    nf_v, w_ff_v, branch_v, tile_v, g_tile_v, lse_v, start_v, lse_t_v, start_row_v, gain_v, turned_v, mixed_t_v,
    part_sem, load_sem, w_sem, tile_sem, store_sem,
):
    me = Place()
    rows = tokens.shape[1]
    plane = [(lax.rem(me.dp + k, 8), me.z) for k in range(1, 8)]
    column = [
        (me.dp - me.core + core, lax.rem(me.z + k, 4)) for k in range(1, 4) for core in range(2)
    ]
    enter(plane + column)
    started = []

    def begin(copy):
        copy.start()
        started.append(copy)

    streams = ((tokens, x_out), (segments, seg_out), (out_grad, g_out))

    def place_of(ref, seq):
        return ref.at[pl.ds(rows * seq, rows)] if ref.shape[0] == 4 * rows else ref.at[seq]

    def row_copies(index):
        source, target = streams[index]
        for m in range(2):
            core, seq = me.z // 2, 2 * m + me.core
            here = (core == me.core) & (seq == me.z)

            @pl.when(here)
            def _():
                pltpu.make_async_copy(
                    source.at[m], place_of(target, me.z), row_local.at[index]
                ).start()

            @pl.when(jnp.logical_not(here))
            def _():
                remote(
                    source.at[m], place_of(target, me.z), row_send.at[index, m],
                    row_recv.at[index, me.z % 2], me.dp - me.core + core, seq,
                ).start()

    def row_wait_send(index):
        source, target = streams[index]
        for m in range(2):
            core, seq = me.z // 2, 2 * m + me.core
            here = (core == me.core) & (seq == me.z)

            @pl.when(jnp.logical_not(here))
            def _():
                remote(
                    source.at[m], place_of(target, me.z), row_send.at[index, m],
                    row_recv.at[index, me.z % 2], me.dp - me.core + core, seq,
                ).wait_send()

    def row_relay(index):
        source, target = streams[index]
        for slot in range(2):
            seq = 2 * me.core + slot
            block = place_of(target, seq)
            here = (seq == me.z) & (me.z % 2 == me.core)

            @pl.when(here)
            def _():
                pltpu.make_async_copy(block, block, row_local.at[index]).wait()

            @pl.when(jnp.logical_not(here))
            def _():
                remote(
                    block, block, row_send.at[index, slot], row_recv.at[index, slot], me.over_core, me.z
                ).wait_recv()

            begin(
                remote(
                    block, block, row_send.at[index, 2 + slot], row_recv.at[index, 2 + slot],
                    me.over_core, me.z,
                )
            )

    def row_finish(index):
        source, target = streams[index]
        for slot in range(2):
            block = place_of(target, 2 * (1 - me.core) + slot)
            remote(
                block, block, row_send.at[index, 2 + slot], row_recv.at[index, 2 + slot], me.over_core, me.z
            ).wait_recv()

    by_columns = []
    base = 0
    for source in (w_q, w_k, w_v):
        by_columns.append((source, qkv_out, base))
        base += source.shape[1] // 2
    by_columns.append((w_gate, ff_out, 0))
    by_columns.append((w_up, ff_out, w_gate.shape[1] // 2))
    by_rows = [(w_o, o_out), (w_down, down_out)]

    def column_piece(index, owner):
        source, target, first = by_columns[index]
        depth, width = source.shape[0], source.shape[1] // 2
        return target.at[pl.ds(depth * owner, depth), pl.ds(first, width)]

    def columns_start(index):
        source, target, first = by_columns[index]
        width = source.shape[1] // 2
        mine = column_piece(index, me.dp)
        for core in range(2):
            half = source.at[:, pl.ds(width * core, width)]
            begin(remote(half, mine, send.at[index, core], recv.at[index, me.core],
                         me.over_x - me.core + core, me.z))
            begin(remote(half, mine, send.at[index, 2 + core], recv.at[index, 2 + me.core],
                         me.over_y - me.core + core, me.z))

            @pl.when(core == me.core)
            def _():
                pltpu.make_async_copy(half, mine, local.at[index]).start()

            @pl.when(core != me.core)
            def _():
                remote(half, mine, send.at[index, 4], recv.at[index, 4], me.over_core, me.z).start()

    def columns_relay(index):
        piece = column_piece(index, me.over_x - me.core)
        remote(piece, piece, send.at[index, 5], recv.at[index, 0], me.over_y, me.z).wait_recv()
        begin(remote(piece, piece, send.at[index, 5], recv.at[index, 5], me.over_y, me.z))
        piece = column_piece(index, me.over_y - me.core + 1)
        remote(piece, piece, send.at[index, 6], recv.at[index, 3], me.over_x, me.z).wait_recv()
        begin(remote(piece, piece, send.at[index, 6], recv.at[index, 6], me.over_x, me.z))

    def columns_finish(index):
        source, target, first = by_columns[index]
        width = source.shape[1] // 2
        corner = me.over_x + me.over_y - me.dp - me.core
        for slot, owner in (
            (1, me.over_x - me.core + 1), (2, me.over_y - me.core), (4, me.over_core),
            (5, corner), (6, corner + 1),
        ):
            piece = column_piece(index, owner)
            remote(piece, piece, send.at[index, 5], recv.at[index, slot], me.over_core, me.z).wait_recv()
        mine = column_piece(index, me.dp)
        pltpu.make_async_copy(mine, mine, local.at[index]).wait()
        half = source.at[:, pl.ds(0, width)]
        remote(half, mine, send.at[index, 4], recv.at[index, 4], me.over_core, me.z).wait_send()

    def row_piece(which, owner):
        source, target = by_rows[which]
        depth = source.shape[0]
        return target.at[pl.ds(depth * lax.rem(owner, 4), depth), :]

    def rows_start(which):
        source, target = by_rows[which]
        index = 5 + which
        mine = row_piece(which, me.dp)
        begin(remote(source, mine, send.at[index, 0], recv.at[index, me.core],
                     me.over_x - me.core + me.y, me.z))
        begin(remote(source, mine, send.at[index, 1], recv.at[index, 2 + me.core],
                     me.over_y - me.core + me.y, me.z))

        @pl.when(me.core == me.y)
        def _():
            pltpu.make_async_copy(source, mine, local.at[index]).start()

        @pl.when(me.core != me.y)
        def _():
            remote(source, mine, send.at[index, 4], recv.at[index, 4], me.over_core, me.z).start()

    def rows_relay(which):
        index = 5 + which

        @pl.when(me.core == me.y)
        def _():
            piece = row_piece(which, me.over_x - me.core)
            remote(piece, piece, send.at[index, 5], recv.at[index, 0], me.over_y, me.z).wait_recv()
            remote(piece, piece, send.at[index, 5], recv.at[index, 5], me.over_y, me.z).start()

        @pl.when(me.core != me.y)
        def _():
            piece = row_piece(which, me.over_y - me.core + 1)
            remote(piece, piece, send.at[index, 6], recv.at[index, 3], me.over_x, me.z).wait_recv()
            remote(piece, piece, send.at[index, 6], recv.at[index, 6], me.over_x, me.z).start()

    def rows_finish(which):
        source, target = by_rows[which]
        index = 5 + which
        corner = me.over_x + me.over_y - me.dp - me.core

        def arrived(slot, owner):
            piece = row_piece(which, owner)
            remote(piece, piece, send.at[index, 5], recv.at[index, slot], me.over_core, me.z).wait_recv()

        def left(slot):
            piece = row_piece(which, me.dp)
            remote(source, piece, send.at[index, slot], recv.at[index, slot], me.over_core, me.z).wait_send()

        @pl.when(me.core == me.y)
        def _():
            arrived(1, me.over_x - me.core + 1)
            arrived(4, me.over_core)
            mine = row_piece(which, me.dp)
            pltpu.make_async_copy(source, mine, local.at[index]).wait()
            left(5)

        @pl.when(me.core != me.y)
        def _():
            arrived(2, me.over_y - me.core)
            arrived(5, corner)
            arrived(6, corner + 1)
            left(4)
            left(6)

    def load(source, target, k):
        return pltpu.make_async_copy(source, target, load_sem.at[k])

    stores = []

    def store(source, target):
        copy = pltpu.make_async_copy(source, target, store_sem.at[len(stores)])
        stores.append(copy)
        copy.start()
        return copy

    length, width = x_v.shape
    own_width = width // 2
    half_ff = ff_out.shape[1] // 2

    row_copies(0)
    row_copies(1)
    for index in range(3):
        columns_start(index)
    for k in range(1, 8):
        begin(remote(gains, gains_out.at[me.dp], gain_send.at[k - 1], gain_recv.at[k - 1],
                     lax.rem(me.dp + k, 8), me.z))
    pltpu.make_async_copy(gains, gains_out.at[me.dp], gain_recv.at[7]).start()
    row_copies(2)
    for index in range(3):
        columns_relay(index)
    rows_start(0)
    row_relay(0)
    row_relay(1)
    for k in range(1, 8):
        piece = gains_out.at[lax.rem(me.dp + 8 - k, 8)]
        remote(piece, piece, gain_send.at[k - 1], gain_recv.at[k - 1], me.over_core, me.z).wait_recv()
    pltpu.make_async_copy(gains, gains_out.at[me.dp], gain_recv.at[7]).wait()
    load(gains_out, gains_v, 0).start()
    row_finish(1)
    load(seg_out, seg_v, 1).start()
    row_finish(0)
    load(x_out, x_v, 2).start()
    load(gains_out, gains_v, 0).wait()
    load(seg_out, seg_v, 1).wait()
    load(x_out, x_v, 2).wait()
    both_gains = gains_v[0].astype(jnp.float32)
    for k in range(1, 8):
        both_gains = both_gains + gains_v[k].astype(jnp.float32)
    gain_a, gain_f = both_gains[0:1], both_gains[1:2]
    gain_v[...] = both_gains
    store(gain_v, gain_out)

    norm_rows(lambda part: x_v[part, :].astype(jnp.float32), gain_a, normed_v, length)

    docs = jnp.concatenate([seg_v[k] for k in range(4)], axis=1)
    start_row = jnp.zeros((1, length), jnp.int32)
    for k in range(4):
        square = lax.broadcasted_iota(jnp.int32, (rows, rows), 0) == lax.broadcasted_iota(
            jnp.int32, (rows, rows), 1
        )
        ids = jnp.sum(jnp.where(square, seg_v[k], 0), axis=1, keepdims=True)
        start_v[pl.ds(rows * k, rows), :] = jnp.sum(
            jnp.where(docs < ids, 1, 0), axis=1, keepdims=True
        )
        start_row = start_row + jnp.sum(jnp.where(ids < docs, 1, 0), axis=0, keepdims=True)
    start_row_v[...] = start_row
    store(start_row_v, start_out)
    turn(normed_v, turned_v)
    normed_store = store(turned_v, normed_t_out)

    for index in range(3):
        columns_finish(index)
    columns_start(3)
    columns_start(4)
    rows_relay(0)
    tile = 256
    tiles = own_width // tile
    for t in range(tiles):
        for kind in range(3):
            part = pl.ds(own_width * kind + tile * t, tile)
            pltpu.make_async_copy(qkv_out.at[:, part], w_qkv_v.at[:, part], w_sem.at[kind, t]).start()
    for t in range(tiles):
        for kind in range(3):
            part = pl.ds(own_width * kind + tile * t, tile)
            pltpu.make_async_copy(qkv_out.at[:, part], w_qkv_v.at[:, part], w_sem.at[kind, t]).wait()
            product = jnp.dot(normed_v[...], w_qkv_v[:, part], preferred_element_type=jnp.float32)
            for k in range(tile // 128):
                piece = product[:, 128 * k : 128 * k + 128]
                if kind < 2:
                    piece = piece * cosine[...] + swap_halves(piece) * sine[...]
                heads_v[:, pl.ds(own_width * kind + tile * t + 128 * k, 128)] = piece.astype(jnp.bfloat16)

        def pair_step(pair, carry):
            attend(pair, own_width, heads_v, start_v, mixed_v, lse_v)
            return carry

        lax.fori_loop(tile // 128 * t, tile // 128 * (t + 1), pair_step, 0)
        if t == 0:
            row_relay(2)
        if t == 1:
            rows_start(1)
    store(heads_v, heads_out)
    lse_t_v[...] = lse_v[...].T
    store(lse_t_v, lse_out)
    turn(mixed_v, mixed_t_v)
    store(mixed_t_v, mixed_t_out)

    rows_finish(0)
    load(o_out, w_o_v, 0).start()
    row_finish(2)
    load(g_out, branch_v, 1).start()
    load(o_out, w_o_v, 0).wait()
    chunk = width // 3

    def part_copy(k):
        part = pl.ds(chunk * k, chunk)
        return remote(
            part_send.at[:, part], part_recv.at[:, part], part_sem.at[0, k], part_sem.at[1, k], me.over_core, me.z
        )

    for k in range(3):
        for at in range(chunk * k, chunk * (k + 1), tile):
            part = pl.ds(at, tile)
            product = jnp.dot(mixed_v[...], w_o_v[:, part], preferred_element_type=jnp.float32)
            part_send[:, part] = product.astype(jnp.bfloat16)
            middle_v[:, part] = x_v[:, part].astype(jnp.float32) + product
        part_copy(k).start()
    columns_relay(3)
    columns_relay(4)
    for k in range(3):
        part_copy(k).wait_recv()

    def middle_rows(part):
        value = middle_v[part, :] + part_recv[part, :].astype(jnp.float32)
        middle_v[part, :] = value
        return value

    norm_rows(middle_rows, gain_f, nf_v, length)
    store(middle_v, middle_out)
    normed_store.wait()
    turn(nf_v, turned_v)
    store(turned_v, nf_t_out)
    load(g_out, branch_v, 1).wait()
    rows_relay(1)
    columns_finish(3)
    columns_finish(4)

    def ff_load(n, slot, kind):
        first = pl.multiple_of(half_ff * kind + tile * n, 128)
        return pltpu.make_async_copy(
            ff_out.at[:, pl.ds(first, tile)], w_ff_v.at[slot, kind], tile_sem.at[0, slot, kind]
        )

    def tile_store(n, slot, kind):
        part = pl.ds(pl.multiple_of(tile * n, 128), tile)
        target = (slope_gate_out, slope_up_out, hidden_out)[kind]
        return pltpu.make_async_copy(tile_v.at[slot, kind], target.at[:, part], tile_sem.at[1, slot, kind])

    def grad_store(n, slot):
        part = pl.ds(pl.multiple_of(tile * n, tile), tile)
        return pltpu.make_async_copy(g_tile_v.at[slot], g_down_out.at[part, :], tile_sem.at[2, slot, 0])

    count = half_ff // tile
    for kind in range(2):
        ff_load(0, 0, kind).start()

    def ff_step(n, carry):
        slot = lax.rem(n, 2)
        for kind in range(2):
            ff_load(n, slot, kind).wait()

        @pl.when(n + 1 < count)
        def _():
            for kind in range(2):
                ff_load(n + 1, 1 - slot, kind).start()

        @pl.when(n >= 2)
        def _():
            for kind in range(3):
                tile_store(n - 2, slot, kind).wait()
            grad_store(n - 2, slot).wait()

        gate = jnp.dot(nf_v[...], w_ff_v[slot, 0], preferred_element_type=jnp.float32)
        up_value = jnp.dot(nf_v[...], w_ff_v[slot, 1], preferred_element_type=jnp.float32)
        sigma = jax.nn.sigmoid(gate)
        silu = gate * sigma
        tile_v[slot, 0] = (up_value * sigma * (1.0 + gate * (1.0 - sigma))).astype(jnp.bfloat16)
        tile_v[slot, 1] = silu.astype(jnp.bfloat16)
        hidden = (silu * up_value).astype(jnp.bfloat16)
        tile_v[slot, 2] = hidden
        g_tile_v[slot] = jnp.dot(
            hidden.T, branch_v[...], preferred_element_type=jnp.float32
        ).astype(jnp.bfloat16)
        for kind in range(3):
            tile_store(n, slot, kind).start()
        grad_store(n, slot).start()
        return carry

    lax.fori_loop(0, count, ff_step, 0)
    for n in range(count - 2, count):
        for kind in range(3):
            tile_store(n, n % 2, kind).wait()
        grad_store(n, n % 2).wait()
    rows_finish(1)
    for copy in stores:
        if copy is not normed_store:
            copy.wait()
    for k in range(3):
        part_copy(k).wait_send()
    for index in range(3):
        row_wait_send(index)
    for copy in started:
        copy.wait_send()


def turn(source, target):
    for k in range(source.shape[1] // 256):
        target[256 * k : 256 * (k + 1), :] = source[:, 256 * k : 256 * (k + 1)].T


def norm_rows(read, gain, target, length, step=64):
    def chunk(k, carry):
        part = pl.ds(pl.multiple_of(k * step, step), step)
        values = read(part)
        scale = lax.rsqrt(jnp.mean(values * values, axis=-1, keepdims=True) + EPS)
        target[part, :] = (values * scale * gain).astype(target.dtype)
        return carry

    lax.fori_loop(0, length // step, chunk, 0)


def attend(pair, width, heads, start, mixed, lse):
    length = heads.shape[0]
    lane = lax.broadcasted_iota(jnp.int32, (BLK, 128), 1)
    cols = [pl.ds(pl.multiple_of(width * kind + 128 * pair, 128), 128) for kind in range(3)]
    for i in range(length // BLK):
        own_rows, keys = slice(BLK * i, BLK * (i + 1)), BLK * (i + 1)
        place = lax.broadcasted_iota(jnp.int32, (BLK, keys), 1)
        own = BLK * i + lax.broadcasted_iota(jnp.int32, (BLK, keys), 0)
        allowed = (place >= start[own_rows, :]) & (place <= own)
        query = heads[own_rows, cols[0]] * jnp.bfloat16(0.125)
        key, value = heads[0:keys, cols[1]], heads[0:keys, cols[2]]
        kept = lse[own_rows, :]
        outs = []
        for half in range(2):
            part = slice(64 * half, 64 * half + 64)
            scores = jnp.where(allowed, nt(query[:, part], key[:, part]), -1e30)
            peak = jnp.max(scores, axis=-1, keepdims=True)
            expo = jnp.exp(scores - peak)
            total = jnp.sum(expo, axis=-1, keepdims=True)
            out = jnp.dot(expo.astype(jnp.bfloat16), value[:, part], preferred_element_type=jnp.float32)
            outs.append((out / total).astype(jnp.bfloat16))
            kept = jnp.where(lane == 2 * pair + half, peak + jnp.log(total), kept)
        mixed[own_rows, cols[0]] = jnp.concatenate(outs, axis=1)
        lse[own_rows, :] = kept


def gather_all(tokens, segments, out_grad, gains, cosine, sine, weights):
    rows, width = tokens.shape[1], tokens.shape[2]
    length, half, ff = 4 * rows, width // 2, weights[4].shape[1]
    half_ff = ff // 2
    low = jnp.bfloat16

    def shape(*dims, dtype=low):
        return jax.ShapeDtypeStruct(dims, dtype)

    shapes = [
        shape(length, width),
        shape(4, *segments.shape[1:], dtype=jnp.int32),
        shape(length, width),
        shape(8, *gains.shape),
        shape(width, 3 * half),
        shape(half, width),
        shape(width, ff),
        shape(half_ff, width),
        shape(length, 3 * half),
        shape(128, length, dtype=jnp.float32),
        shape(length, width, dtype=jnp.float32),
        shape(length, half_ff),
        shape(length, half_ff),
        shape(length, half_ff),
        shape(half_ff, width),
        shape(1, length, dtype=jnp.int32),
        shape(2, width, dtype=jnp.float32),
        shape(width, length),
        shape(width, length),
        shape(half, length),
    ]
    dma, vmem = pltpu.SemaphoreType.DMA, pltpu.VMEM
    whole = pl.BlockSpec(memory_space=pltpu.VMEM)
    return pl.pallas_call(
        gather_kernel,
        in_specs=[ANY] * 4 + [whole] * 2 + [ANY] * 7,
        out_specs=[ANY] * len(shapes),
        out_shape=shapes,
        scratch_shapes=[
            dma((7, 7)), dma((7, 7)), dma((7,)), dma((3, 4)), dma((3, 4)), dma((3,)), dma((7,)), dma((8,)),
            vmem((length, width), low),
            vmem((4,) + segments.shape[1:], jnp.int32),
            vmem((8,) + gains.shape, low),
            vmem((length, width), low),
            vmem((width, 3 * half), low),
            vmem((length, 3 * half), low),
            vmem((length, half), low),
            vmem((half, width), low),
            vmem((length, width), jnp.float32),
            vmem((length, width), low),
            vmem((length, width), low),
            vmem((length, width), low),
            vmem((2, 2, width, 256), low),
            vmem((length, width), low),
            vmem((2, 3, length, 256), low),
            vmem((2, 256, width), low),
            vmem((length, 128), jnp.float32),
            vmem((length, 1), jnp.int32),
            vmem((128, length), jnp.float32),
            vmem((1, length), jnp.int32),
            vmem((2, width), jnp.float32),
            vmem((width, length), low),
            vmem((half, length), low),
            dma((2, 3)), dma((3,)), dma((3, 3)), dma((3, 2, 3)), dma((9,)),
        ],
        compiler_params=pltpu.CompilerParams(
            collective_id=0, has_side_effects=True, vmem_limit_bytes=61 * 1024 * 1024
        ),
        cost_estimate=pl.CostEstimate(flops=0, bytes_accessed=500_000_000, transcendentals=0),
        name="gather_all",
    )(tokens, segments, out_grad, gains, cosine, sine, *weights)


def guard(condition, action):
    if isinstance(condition, (bool, np.bool_)):
        if condition:
            action()
    else:
        pl.when(condition)(action)


def everything(*conditions):
    known = [c for c in conditions if isinstance(c, (bool, np.bool_))]
    if not all(known):
        return False
    rest = [c for c in conditions if not isinstance(c, (bool, np.bool_))]
    if not rest:
        return True
    total = rest[0]
    for c in rest[1:]:
        total = total & c
    return total


def chunk_of(rows):
    return 384 if rows % 384 == 0 else 512


def add_rows(target, first, other, rows):
    step = chunk_of(rows)

    def chunk(k, carry):
        at = pl.multiple_of(k * step, step)
        source = pl.multiple_of(first + k * step, step)
        target[pl.ds(at, step), :] += other[pl.ds(source, step), :]
        return carry

    lax.fori_loop(0, rows // step, chunk, 0)


JOB = 256


class Stream:
    active = True

    def tick(self, t):
        for late, stage in reversed(self.stages):
            k = t - late
            guard(everything(k >= 0, k < self.count), functools.partial(stage, k))

    @property
    def ticks(self):
        return self.count + self.stages[-1][0]

    def slot(self, k):
        return k % self.slots if isinstance(k, int) else lax.rem(k, self.slots)

    def column(self, k, base=0):
        return pl.ds(pl.multiple_of(base + JOB * k, 128), JOB)

    def total(self, k):
        return self.second.at[self.slot(k)]

    def final(self, k):
        return self.got.at[self.slot(k), pl.ds(0, self.rows)]

    def seq_copy(self, k, step):
        me, slot, sem = self.me, self.slot(k), self.seq_sem
        inner = me.z + 1 - 2 * (me.z // 2)
        opposite = 3 - me.z
        outer = 3 * (me.z // 2)
        if step == 0:
            return remote(self.total(k), self.over.at[slot, 0], sem.at[slot, 0, 0], sem.at[slot, 1, 0], me.dp, inner)
        if step == 1:
            return remote(
                self.total(k), self.over.at[slot, 1], sem.at[slot, 0, 1], sem.at[slot, 1, 1], me.dp, opposite
            )
        return remote(self.final(k), self.final(k), sem.at[slot, 0, 2], sem.at[slot, 1, 2], me.dp, outer)

    def plane_and_ends(self, k):
        self.reduce_plane(k)
        guard(
            everything(self.active, jnp.logical_not(self.me.middle)),
            lambda: self.seq_copy(k, 0).start(),
        )

    def across(self, k):
        def action():
            self.seq_copy(k, 0).wait_recv()
            add_rows(self.total(k), 0, self.over.at[self.slot(k), 0], self.rows)
            self.seq_copy(k, 1).start()

        guard(everything(self.active, self.me.middle), action)

    def back(self, k):
        def action():
            self.seq_copy(k, 1).wait_recv()
            final, total, over = self.final(k), self.total(k), self.over.at[self.slot(k), 1]
            step = chunk_of(self.rows)

            def chunk(at, carry):
                part = pl.ds(pl.multiple_of(at * step, step), step)
                final[part, :] = total[part, :] + over[part, :]
                return carry

            lax.fori_loop(0, self.rows // step, chunk, 0)
            self.seq_copy(k, 2).start()

        guard(everything(self.active, self.me.middle), action)

    def finish(self, k):
        guard(
            everything(self.active, jnp.logical_not(self.me.middle)),
            lambda: self.seq_copy(k, 2).wait_recv(),
        )
        self.output(k)

    def drain(self, k):
        self.drain_plane(k)

        def ends():
            self.seq_copy(k, 0).wait_send()

        def middles():
            self.seq_copy(k, 1).wait_send()
            self.seq_copy(k, 2).wait_send()

        guard(everything(self.active, jnp.logical_not(self.me.middle)), ends)
        guard(everything(self.active, self.me.middle), middles)


class ColumnStream(Stream):
    def __init__(self, me, source, target, ff_jobs, d_model, ff, refs):
        self.me, self.source, self.target = me, source, target
        self.got, self.keep, self.second, self.over, self.sem, self.seq_sem, self.credit = refs
        self.slots, self.rows = self.got.shape[0], source.shape[0] // 4
        self.count, self.ff_jobs = source.shape[1] // JOB, ff_jobs
        self.ff, self.d_model = ff, d_model
        self.stages = (
            (0, self.start), (2, self.pass_second), (4, self.plane_and_ends), (6, self.across),
            (8, self.back), (9, self.finish), (10, self.drain),
        )

    def x_first(self, k):
        late = k // self.ff_jobs
        return (1 - late) * ((k // (self.ff_jobs // 2)) % 2) * ((k + 1) % 2) + late * (k % 2)

    def first_copy(self, k, part):
        me, slot, x_first = self.me, self.slot(k), self.x_first(k)
        block = x_first * (2 * part + 1 - me.x) + (1 - x_first) * (2 * (1 - me.y) + part)
        sent = self.source.at[pl.ds(pl.multiple_of(self.rows * block, self.rows), self.rows), self.column(k)]
        to = x_first * me.over_x + (1 - x_first) * me.over_y
        return remote(
            sent, self.got.at[slot, pl.ds(self.rows * part, self.rows)],
            self.sem.at[slot, 0, part], self.sem.at[slot, 1, part], to, me.z,
        )

    def keep_copy(self, k, part):
        me, slot, x_first = self.me, self.slot(k), self.x_first(k)
        block = x_first * (2 * part + me.x) + (1 - x_first) * (2 * me.y + part)
        kept = self.source.at[pl.ds(pl.multiple_of(self.rows * block, self.rows), self.rows), self.column(k)]
        return pltpu.make_async_copy(
            kept, self.keep.at[slot, pl.ds(self.rows * part, self.rows)], self.sem.at[slot, 2, part]
        )

    def at(self, k):
        x_first = self.x_first(k)
        return x_first * self.me.y + (1 - x_first) * self.me.x

    def second_copy(self, k):
        me, slot, x_first = self.me, self.slot(k), self.x_first(k)
        row = pl.multiple_of(self.rows * (1 - self.at(k)), self.rows)
        to = x_first * me.over_y + (1 - x_first) * me.over_x
        return remote(
            self.keep.at[slot, pl.ds(row, self.rows)], self.second.at[slot],
            self.sem.at[slot, 0, 2], self.sem.at[slot, 1, 2], to, me.z,
        )

    def start(self, k):
        def credits():
            slot = self.slot(k)

            @pl.when(self.me.middle)
            def _():
                pl.semaphore_wait(self.credit.at[slot], 5)

            @pl.when(jnp.logical_not(self.me.middle))
            def _():
                pl.semaphore_wait(self.credit.at[slot], 4)

        guard(k >= self.slots, credits)
        for part in range(2):
            self.first_copy(k, part).start()
            self.keep_copy(k, part).start()

    def pass_second(self, k):
        for part in range(2):
            self.keep_copy(k, part).wait()
            self.first_copy(k, part).wait_recv()
        slot = self.slot(k)
        add_rows(self.keep.at[slot], 0, self.got.at[slot], 2 * self.rows)
        self.second_copy(k).start()

    def reduce_plane(self, k):
        self.second_copy(k).wait_recv()
        add_rows(self.total(k), self.rows * self.at(k), self.keep.at[self.slot(k)], self.rows)

    def out_column(self, k, core, late):
        if late:
            m, half = k - self.ff_jobs, self.d_model // 2
            tiles = half // JOB
            first = 2 * self.ff + self.d_model * (m // tiles) + JOB * (m % tiles) + half * core
        else:
            first = self.ff * (k % 2) + JOB * (k // 2) + self.ff // 2 * core
        return self.target.at[:, pl.ds(pl.multiple_of(first, 128), JOB)]

    def last_copy(self, k, late=False):
        me, slot, rows = self.me, self.slot(k), self.rows // 2
        part = self.got.at[slot, pl.ds(pl.multiple_of(rows * (1 - me.core), rows), rows)]
        return remote(
            part, self.out_column(k, me.core, late), self.sem.at[slot, 0, 3], self.sem.at[slot, 1, 3],
            me.over_core, me.z,
        )

    def own_copy(self, k, late=False):
        me, slot, rows = self.me, self.slot(k), self.rows // 2
        part = self.got.at[slot, pl.ds(pl.multiple_of(rows * me.core, rows), rows)]
        return pltpu.make_async_copy(part, self.out_column(k, me.core, late), self.sem.at[slot, 2, 0])

    def output(self, k):
        def begin(late):
            self.last_copy(k, late).start()
            self.own_copy(k, late).start()

        guard(k < self.ff_jobs, lambda: begin(False))
        guard(k >= self.ff_jobs, lambda: begin(True))

    def drain_plane(self, k):
        for part in range(2):
            self.first_copy(k, part).wait_send()
        self.second_copy(k).wait_send()

        def end(late):
            self.last_copy(k, late).wait()
            self.own_copy(k, late).wait()

        guard(k < self.ff_jobs, lambda: end(False))
        guard(k >= self.ff_jobs, lambda: end(True))

    def drain(self, k):
        super().drain(k)

        def signal(dp, seq):
            pl.semaphore_signal(
                self.credit.at[self.slot(k)], inc=1, device_id={"dp": dp, "seq": seq},
                device_id_type=pl.DeviceIdType.MESH,
            )

        def free():
            me = self.me
            for dp in (me.over_core, me.over_x, me.over_y):
                signal(dp, me.z)

            @pl.when(me.middle)
            def _():
                signal(me.dp, 3 - me.z)
                signal(me.dp, 3 * (me.z // 2))

            @pl.when(jnp.logical_not(me.middle))
            def _():
                signal(me.dp, me.z + 1 - 2 * (me.z // 2))

        guard(k + self.slots < self.count, free)


class RowStream(Stream):
    def __init__(self, me, source, target, lates, refs):
        self.me, self.source, self.target = me, source, target
        self.got, self.second, self.over, self.stage, self.sem, self.seq_sem = refs
        self.slots, self.rows = self.got.shape[0], source.shape[0] // 2
        self.count = source.shape[1] // JOB
        self.active = me.core == me.y
        steps = (
            self.start, self.load, self.pass_second, self.plane_and_ends, self.across, self.back, self.finish,
            self.drain,
        )
        self.stages = tuple(zip(lates, steps))

    def first_copy(self, k):
        me, slot = self.me, self.slot(k)
        sent = self.source.at[pl.ds(pl.multiple_of(self.rows * (1 - me.x), self.rows), self.rows), self.column(k)]
        return remote(sent, self.got.at[slot], self.sem.at[slot, 0, 0], self.sem.at[slot, 1, 0], me.over_x, me.z)

    def load_copy(self, k):
        kept = self.source.at[
            pl.ds(pl.multiple_of(self.rows * self.me.x, self.rows), self.rows), self.column(k)
        ]
        return pltpu.make_async_copy(kept, self.stage, self.sem.at[self.slot(k), 2, 0])

    def second_copy(self, k):
        me, slot = self.me, self.slot(k)
        return remote(
            self.got.at[slot], self.second.at[slot], self.sem.at[slot, 0, 2], self.sem.at[slot, 1, 2],
            me.over_y, me.z,
        )

    def start(self, k):
        self.first_copy(k).start()

    def load(self, k):
        self.load_copy(k).start()

    def pass_second(self, k):
        self.load_copy(k).wait()
        self.first_copy(k).wait_recv()
        add_rows(self.got.at[self.slot(k)], 0, self.stage, self.rows)
        guard(jnp.logical_not(self.active), lambda: self.second_copy(k).start())

    def reduce_plane(self, k):
        def action():
            self.second_copy(k).wait_recv()
            add_rows(self.total(k), 0, self.got.at[self.slot(k)], self.rows)

        guard(self.active, action)

    def last_copy(self, k):
        me, slot, rows = self.me, self.slot(k), self.rows // 2
        part = self.got.at[slot, pl.ds(pl.multiple_of(rows * (1 - me.core), rows), rows)]
        return remote(
            part, self.target.at[:, self.column(k)], self.sem.at[slot, 0, 3], self.sem.at[slot, 1, 3],
            me.over_core, me.z,
        )

    def own_copy(self, k):
        me, slot, rows = self.me, self.slot(k), self.rows // 2
        part = self.got.at[slot, pl.ds(pl.multiple_of(rows * me.core, rows), rows)]
        return pltpu.make_async_copy(part, self.target.at[:, self.column(k)], self.sem.at[slot, 2, 1])

    def output(self, k):
        def action():
            self.last_copy(k).start()
            self.own_copy(k).start()

        guard(self.active, action)

    def drain_plane(self, k):
        self.first_copy(k).wait_send()

        def active():
            self.last_copy(k).wait_send()
            self.own_copy(k).wait()

        def passive():
            self.second_copy(k).wait_send()
            self.last_copy(k).wait_recv()

        guard(self.active, active)
        guard(jnp.logical_not(self.active), passive)


GAIN_HOPS = 5


class GainSums:
    def __init__(self, me, target, buffer, sem):
        self.me, self.target, self.buffer, self.sem = me, target, buffer, sem

    def hop(self, k):
        me = self.me
        across = me.z + 2 - 4 * (me.z // 2)
        beside = me.z + 1 - 2 * (me.z % 2)
        dp = (me.over_core, me.over_x, me.over_y, me.dp, me.dp)[k]
        seq = (me.z, me.z, me.z, beside, across)[k]
        return remote(
            self.buffer.at[k, 0], self.buffer.at[k, 1], self.sem.at[0, k], self.sem.at[1, k], dp, seq
        )

    def start(self):
        self.hop(0).start()

    def step(self, k):
        self.hop(k).wait_recv()
        total = self.buffer[k, 0] + self.buffer[k, 1]
        if k + 1 < GAIN_HOPS:
            self.buffer[k + 1, 0] = total
            self.hop(k + 1).start()
        else:
            self.target[...] = total

    def drain(self):
        for k in range(GAIN_HOPS):
            self.hop(k).wait_send()


class RowsBack:
    def __init__(self, me, source, target, sem):
        self.me, self.source, self.target, self.sem = me, source, target, sem

    def each(self, local, elsewhere):
        me = self.me
        rows = self.source.shape[0] // 2
        for slot in range(2):
            core, seq = me.z % 2, 2 * me.core + slot
            here = (core == me.core) & (seq == me.z)
            block, target = self.source.at[pl.ds(rows * slot, rows)], self.target.at[me.z // 2]

            @pl.when(here)
            def _():
                local(pltpu.make_async_copy(block, target, self.sem.at[2, 0]))

            @pl.when(jnp.logical_not(here))
            def _():
                elsewhere(
                    remote(
                        block, target, self.sem.at[0, slot], self.sem.at[1, me.z // 2],
                        me.dp - me.core + core, seq,
                    )
                )

    def start(self):
        self.each(lambda copy: copy.start(), lambda copy: copy.start())

    def drain(self):
        me = self.me
        self.each(lambda copy: copy.wait(), lambda copy: copy.wait_send())
        rows = self.source.shape[0] // 2
        for m in range(2):
            here = (me.z == 2 * m + me.core) & (me.core == me.z // 2)

            @pl.when(jnp.logical_not(here))
            def _():
                remote(
                    self.source.at[pl.ds(0, rows)], self.target.at[m], self.sem.at[0, 0],
                    self.sem.at[1, m], me.over_core, me.z,
                ).wait_recv()


def attend_back(pair, width, heads, grad_mixed, start, lse, grads, key_sum, value_sum, query_sum, cosine, sine):
    length = heads.shape[0]
    cols = [pl.ds(pl.multiple_of(width * kind + 128 * pair, 128), 128) for kind in range(3)]
    key_sum[...] = jnp.zeros_like(key_sum)
    value_sum[...] = jnp.zeros_like(value_sum)
    for i in range(length // BLK):
        own_rows, keys = slice(BLK * i, BLK * (i + 1)), BLK * (i + 1)
        place = lax.broadcasted_iota(jnp.int32, (keys, BLK), 0)
        own = BLK * i + lax.broadcasted_iota(jnp.int32, (keys, BLK), 1)
        allowed = (place >= start[:, own_rows]) & (place <= own)
        query = heads[own_rows, cols[0]] * jnp.bfloat16(0.125)
        key, value = heads[0:keys, cols[1]], heads[0:keys, cols[2]]
        grad = grad_mixed[own_rows, cols[0]]
        for half in range(2):
            part = slice(64 * half, 64 * half + 64)
            scores = nt(key[:, part], query[:, part])
            logsum = lse[pl.ds(2 * pair + half, 1), own_rows]
            probs = jnp.where(allowed, jnp.exp(scores - logsum), 0.0)
            grad_probs = nt(value[:, part], grad[:, part])
            inner = jnp.sum(probs * grad_probs, axis=0, keepdims=True)
            grad_scores = (probs * (grad_probs - inner)).astype(jnp.bfloat16)
            value_sum[0:keys, part] += dot(probs.astype(jnp.bfloat16), grad[:, part])
            key_sum[0:keys, part] += dot(grad_scores, query[:, part])
            query_sum[own_rows, part] = tn(grad_scores, key[:, part]) * 0.125
    for kind, total in enumerate((query_sum, key_sum)):
        value = total[...]
        grads[:, cols[kind]] = (value * cosine[...] - swap_halves(value) * sine[...]).astype(jnp.bfloat16)
    grads[:, cols[2]] = value_sum[...].astype(jnp.bfloat16)


def backward_kernel(
    branch_h, slope_gate_h, slope_up_h, hidden_h, nf_t_h, normed_t_h, mixed_t_h, heads_h, lse_h, middle_h, x_h,
    g_down_h, w_qkv_h, w_o_h, w_ff_h, w_down_h, start_ref, gain_ref, cosine, sine,
    out_o, tokens_o, cols_o, o_o, down_o, gains_o, g_cols_h, g_o_h, kept_h, rows_h, grad_nf_h,
    col_got, col_keep, col_second, col_over, col_sem, col_seq, col_credit,
    down_got, down_second, down_over, down_stage, down_sem, down_seq,
    o_got, o_second, o_over, o_stage, o_sem, o_seq,
    wide_recv, half_recv, half_free, wide_sem, half_sem,
    gain_buffer, gain_sem, row_sem, load_sem, tile_sem, store_sem,
):
    me = Place()
    enter(
        [(me.over_core, me.z), (me.over_x, me.z), (me.over_y, me.z)]
        + [(me.dp - me.core + core, lax.rem(me.z + k, 4)) for k in range(1, 4) for core in range(2)]
    )
    length, width = branch_h.shape
    half_rows, own_width, half_ff = length // 2, width // 2, slope_gate_h.shape[1]
    bf16, f32 = jnp.bfloat16, jnp.float32
    vmem = pltpu.VMEM
    ff_jobs = 2 * half_ff // JOB
    cols = ColumnStream(
        me, g_cols_h, cols_o, ff_jobs, width, 2 * half_ff,
        (col_got, col_keep, col_second, col_over, col_sem, col_seq, col_credit),
    )
    downs = RowStream(
        me, g_down_h, down_o, (0, 2, 3, 5, 7, 8, 9, 10), (down_got, down_second, down_over, down_stage, down_sem, down_seq)
    )
    outs = RowStream(me, g_o_h, o_o, (0, 1, 2, 4, 6, 7, 8, 9), (o_got, o_second, o_over, o_stage, o_sem, o_seq))
    back_out = RowsBack(me, rows_h.at[0], out_o, row_sem.at[0])
    back_tokens = RowsBack(me, rows_h.at[1], tokens_o, row_sem.at[1])
    gains = GainSums(me, gains_o, gain_buffer, gain_sem)

    def load(source, target, k=0):
        return pltpu.make_async_copy(source, target, load_sem.at[k])

    def fetch(*pairs):
        for k, (source, target) in enumerate(pairs):
            load(source, target, k).start()
        for k, (source, target) in enumerate(pairs):
            load(source, target, k).wait()

    def lanes(n, size=JOB, base=0):
        return pl.ds(pl.multiple_of(base + size * n, 128), size)

    def sublanes(n, size):
        return pl.ds(pl.multiple_of(n * size, size), size)

    def grad_store(buffer, slot, target, n, k):
        return pltpu.make_async_copy(buffer.at[slot], target.at[:, lanes(n)], store_sem.at[slot, k])

    downs.tick(0)

    def feed_forward(grad_ff):
        steps = half_ff // JOB

        def hidden_grads(branch, w_tile, slopes, nf_t, g_tile):
            def tile_loads(n, slot):
                return (
                    pltpu.make_async_copy(w_down_h.at[sublanes(n, JOB), :], w_tile.at[slot], tile_sem.at[slot, 0]),
                    pltpu.make_async_copy(slope_gate_h.at[:, lanes(n)], slopes.at[slot, 0], tile_sem.at[slot, 1]),
                    pltpu.make_async_copy(slope_up_h.at[:, lanes(n)], slopes.at[slot, 1], tile_sem.at[slot, 2]),
                )

            for copy in tile_loads(0, 0):
                copy.start()
            fetch((branch_h, branch), (nf_t_h, nf_t))
            downs.tick(1)

            def step(n, carry):
                slot = lax.rem(n, 2)
                for copy in tile_loads(n, slot):
                    copy.wait()

                @pl.when(n + 1 < steps)
                def _():
                    for copy in tile_loads(n + 1, 1 - slot):
                        copy.start()

                grad_hidden = nt(branch[...], w_tile[slot])

                @pl.when(n > 0)
                def _():
                    for kind in range(2):
                        grad_store(g_tile, kind, g_cols_h, 2 * n - 2 + kind, 0).wait()

                for kind in range(2):
                    grad = (grad_hidden * slopes[slot, kind].astype(f32)).astype(bf16)
                    grad_ff[:, lanes(n, JOB, half_ff * kind)] = grad
                    g_tile[kind] = dot(nf_t[...], grad).astype(bf16)
                    grad_store(g_tile, kind, g_cols_h, 2 * n + kind, 0).start()

                @pl.when((n >= 2) & (n != 5))
                def _():
                    cols.tick(n - 2 - n // 6)

                @pl.when((n == 2) | (n == 6))
                def _():
                    downs.tick(2 + n // 6)

                return carry

            lax.fori_loop(0, steps, step, 0)
            for kind in range(2):
                grad_store(g_tile, kind, g_cols_h, 2 * steps - 2 + kind, 0).wait()

        pl.run_scoped(
            hidden_grads, vmem((length, width), bf16), vmem((2, JOB, width), bf16),
            vmem((2, 2, length, JOB), bf16), vmem((width, length), bf16), vmem((2, width, JOB), bf16),
        )

        def layer_out(hidden, w_down, send, total):
            other, own = 1 - me.core, me.core
            fetch((w_down_h, w_down), (hidden_h.at[sublanes(other, half_rows), :], hidden))
            load(middle_h.at[sublanes(own, half_rows), :], total, 2).start()

            def other_tile(n, carry):
                send[:, lanes(n)] = dot(hidden[...], w_down[:, lanes(n)]).astype(bf16)
                return carry

            lax.fori_loop(0, width // JOB, other_tile, 0)
            exchange = remote(send, half_recv, half_sem.at[0, 0], half_sem.at[1, 0], me.over_core, me.z)
            exchange.start()
            fetch((hidden_h.at[sublanes(own, half_rows), :], hidden))
            load(middle_h.at[sublanes(own, half_rows), :], total, 2).wait()

            def own_tile(n, carry):
                total[:, lanes(n)] += dot(hidden[...], w_down[:, lanes(n)])
                return carry

            lax.fori_loop(0, width // JOB, own_tile, 0)
            exchange.wait()

            def combine(k, carry):
                part = sublanes(k, 64)
                send[part, :] = (total[part, :] + half_recv[part, :].astype(f32)).astype(bf16)
                return carry

            lax.fori_loop(0, half_rows // 64, combine, 0)
            pl.semaphore_signal(
                half_free, inc=1, device_id={"dp": me.over_core, "seq": me.z},
                device_id_type=pl.DeviceIdType.MESH,
            )
            fetch((send, rows_h.at[0]))

        pl.run_scoped(
            layer_out, vmem((half_rows, half_ff), bf16), vmem((half_ff, width), bf16),
            vmem((half_rows, width), bf16), vmem((half_rows, width), f32),
        )
        back_out.start()

    chunk = 2 * JOB
    chunks = width // chunk

    def wide_copy(send, k):
        part = pl.ds(chunk * k, chunk)
        return remote(
            send.at[:, part], wide_recv.at[:, part], wide_sem.at[0, k], wide_sem.at[1, k], me.over_core, me.z
        )

    def with_grad_ff(grad_ff):
        feed_forward(grad_ff)

        def input_grads(w_tile, send, parts):
            def tile_load(n, kind):
                return pltpu.make_async_copy(
                    w_ff_h.at[sublanes(n, JOB), pl.ds(half_ff * kind, half_ff)], w_tile.at[kind],
                    tile_sem.at[kind, 0],
                )

            def part_store(n, slot):
                return pltpu.make_async_copy(parts.at[slot], grad_nf_h.at[:, lanes(n)], store_sem.at[slot, 0])

            for kind in range(2):
                tile_load(0, kind).start()
            count = width // JOB

            def step(n, carry):
                slot = lax.rem(n, 2)
                tile_load(n, 0).wait()
                part = nt(grad_ff[:, 0:half_ff], w_tile[0])

                @pl.when(n + 1 < count)
                def _():
                    tile_load(n + 1, 0).start()

                tile_load(n, 1).wait()
                part = part + nt(grad_ff[:, half_ff : 2 * half_ff], w_tile[1])

                @pl.when(n + 1 < count)
                def _():
                    tile_load(n + 1, 1).start()

                @pl.when(n >= 2)
                def _():
                    part_store(n - 2, slot).wait()

                parts[slot] = part
                part_store(n, slot).start()
                send[:, lanes(n)] = part.astype(bf16)
                for k in range(chunks):
                    @pl.when(n == 2 * k + 1)
                    def _():
                        wide_copy(send, k).start()

                @pl.when(lax.rem(n, 3) == 0)
                def _():
                    downs.tick(4 + n // 3)

                @pl.when(lax.rem(n, 3) == 2)
                def _():
                    cols.tick(5 + n // 3)

                return carry

            lax.fori_loop(0, count, step, 0)
            for n in range(count - 2, count):
                part_store(n, n % 2).wait()
            cols.tick(7)
            downs.tick(6)
            for k in range(chunks):
                wide_copy(send, k).wait()

        pl.run_scoped(
            input_grads, vmem((2, JOB, half_ff), bf16), vmem((length, width), bf16), vmem((2, length, JOB), f32)
        )

    pl.run_scoped(with_grad_ff, vmem((length, 2 * half_ff), bf16))

    def to_attention(grad_attn):
        def norm_back(grad_nf, middle, branch):
            fetch((middle_h, middle), (branch_h, branch), (grad_nf_h, grad_nf))
            gain = gain_ref[1:2, :]

            def rows(k, total):
                part = sublanes(k, 64)
                grad = grad_nf[part, :] + wide_recv[part, :].astype(f32)
                gained, values = norm_rows_back(middle[part, :], gain, grad)
                values = values + branch[part, :].astype(f32)
                grad_nf[part, :] = values
                grad_attn[part, :] = values.astype(bf16)
                return total + gained

            total = lax.fori_loop(0, length // 64, rows, jnp.zeros((1, width), f32))
            gain_buffer[0, 0, 1:2, :] = 0.5 * total
            kept = load(grad_nf.at[sublanes(me.core, half_rows), :], kept_h, 0)
            kept.start()
            cols.tick(8)
            downs.tick(7)
            kept.wait()

        pl.run_scoped(
            norm_back, vmem((length, width), f32), vmem((length, width), f32), vmem((length, width), bf16)
        )

        def out_projection(w_o, mixed_t, g_tile, grad_mixed):
            fetch((w_o_h, w_o), (mixed_t_h, mixed_t))
            for n in range(own_width // JOB):
                grad_mixed[:, JOB * n : JOB * (n + 1)] = nt(
                    grad_attn[...], w_o[JOB * n : JOB * (n + 1), :]
                ).astype(bf16)
            placed = load(grad_mixed, wide_recv.at[:, pl.ds(0, own_width)], 3)
            placed.start()
            count = width // JOB

            def step(n, carry):
                slot = lax.rem(n, 2)

                @pl.when(n >= 2)
                def _():
                    grad_store(g_tile, slot, g_o_h, n - 2, 1).wait()

                g_tile[slot] = dot(mixed_t[...], grad_attn[:, lanes(n)]).astype(bf16)
                grad_store(g_tile, slot, g_o_h, n, 1).start()

                @pl.when(lax.rem(n, 3) == 1)
                def _():
                    cols.tick(9 + n // 3)

                return carry

            lax.fori_loop(0, count, step, 0)
            for n in range(count - 2, count):
                grad_store(g_tile, n % 2, g_o_h, n, 1).wait()
            placed.wait()

        pl.run_scoped(
            out_projection, vmem((own_width, width), bf16), vmem((own_width, length), bf16),
            vmem((2, own_width, JOB), bf16), vmem((length, own_width), bf16),
        )

    pl.run_scoped(to_attention, vmem((length, width), bf16))

    def attention(grads):
        def heads_back(heads, lse, key_sum, value_sum, query_sum):
            fetch((heads_h, heads), (lse_h, lse))

            def step(pair, carry):
                attend_back(
                    pair, own_width, heads, wide_recv, start_ref, lse, grads, key_sum, value_sum, query_sum, cosine, sine
                )
                outs.tick(pair)

                @pl.when(lax.rem(pair, 3) != 2)
                def _():
                    cols.tick(11 + pair - pair // 3)

                @pl.when(lax.rem(pair, 3) != 1)
                def _():
                    downs.tick(8 + pair - lax.rem(pair, 3) // 2 - pair // 3)

                return carry

            lax.fori_loop(0, own_width // 128, step, 0)

        pl.run_scoped(
            heads_back, vmem((length, 3 * own_width), bf16), vmem((128, length), f32),
            *[vmem((length, 128), f32)] * 3,
        )

        def projection_grads(normed_t, g_tile):
            fetch((normed_t_h, normed_t))
            cols.tick(15)
            count = 3 * own_width // JOB

            def step(n, carry):
                slot = lax.rem(n, 2)
                g_tile[slot] = dot(normed_t[...], grads[:, lanes(n)]).astype(bf16)

                @pl.when(n >= 1)
                def _():
                    grad_store(g_tile, 1 - slot, g_cols_h, ff_jobs + n - 1, 1).wait()

                grad_store(g_tile, slot, g_cols_h, ff_jobs + n, 1).start()

                @pl.when(n >= 1)
                def _():
                    cols.tick(15 + n)

                @pl.when(n >= 1)
                def _():
                    outs.tick(5 + n)

                return carry

            lax.fori_loop(0, count, step, 0)
            grad_store(g_tile, (count - 1) % 2, g_cols_h, ff_jobs + count - 1, 1).wait()

        pl.run_scoped(projection_grads, vmem((width, length), bf16), vmem((2, width, JOB), bf16))

        cols.tick(24)

        def tokens_back(w_tile, send, total, x_rows, kept):
            def tile_load(n, slot):
                return pltpu.make_async_copy(w_qkv_h.at[sublanes(n, JOB), :], w_tile.at[slot], tile_sem.at[slot, 0])

            tile_load(0, 0).start()
            load(x_h.at[sublanes(me.core, half_rows), :], x_rows, 0).start()
            load(kept_h, kept, 1).start()
            count = width // JOB

            def step(n, carry):
                slot = lax.rem(n, 2)
                tile_load(n, slot).wait()

                @pl.when(n + 1 < count)
                def _():
                    tile_load(n + 1, 1 - slot).start()

                send[:, lanes(n)] = nt(grads[sublanes(1 - me.core, half_rows), :], w_tile[slot]).astype(bf16)
                total[:, lanes(n)] = nt(grads[sublanes(me.core, half_rows), :], w_tile[slot])

                @pl.when((n == 1) | (n == 3))
                def _():
                    cols.tick(25 + n - 1)
                    cols.tick(26 + n - 1)
                    downs.tick(12 + n // 2)

                return carry

            lax.fori_loop(0, count, step, 0)
            pl.semaphore_wait(half_free, 1)
            exchange = remote(send, half_recv, half_sem.at[0, 0], half_sem.at[1, 0], me.over_core, me.z)
            exchange.start()
            cols.tick(29)
            cols.tick(30)
            load(x_h.at[sublanes(me.core, half_rows), :], x_rows, 0).wait()
            load(kept_h, kept, 1).wait()
            exchange.wait()
            gain = gain_ref[0:1, :]

            def rows(k, sums):
                part = sublanes(k, 64)
                grad = total[part, :] + half_recv[part, :].astype(f32)
                gained, values = norm_rows_back(x_rows[part, :].astype(f32), gain, grad)
                send[part, :] = (values + kept[part, :]).astype(bf16)
                return sums + gained

            gain_buffer[0, 0, 0:1, :] = lax.fori_loop(0, half_rows // 64, rows, jnp.zeros((1, width), f32))
            gains.start()
            fetch((send, rows_h.at[1]))

        pl.run_scoped(
            tokens_back, vmem((2, JOB, 3 * own_width), bf16), vmem((half_rows, width), bf16),
            vmem((half_rows, width), f32), vmem((half_rows, width), bf16), vmem((half_rows, width), f32),
        )
        back_tokens.start()

    pl.run_scoped(attention, vmem((length, 3 * own_width), bf16))

    downs.tick(14)
    outs.tick(14)
    downs.tick(15)
    first = 31

    def rest(t, carry):
        cols.tick(t)
        for k in range(GAIN_HOPS - 1):
            @pl.when(t == first + k)
            def _():
                gains.step(k)

        return carry

    lax.fori_loop(first, cols.ticks, rest, 0)
    gains.step(GAIN_HOPS - 1)
    gains.drain()
    back_out.drain()
    back_tokens.drain()


def norm_rows_back(values, gain, grad):
    scale = lax.rsqrt(jnp.mean(values * values, axis=-1, keepdims=True) + EPS)
    unit = values * scale
    inner = grad * gain
    return (
        jnp.sum(grad * unit, axis=0, keepdims=True),
        scale * (inner - unit * jnp.mean(inner * unit, axis=-1, keepdims=True)),
    )


COLUMN_SLOTS = 12


def backward(branch, slopes, hidden, turned, heads, lse, middle, x, g_down, weights, start, gain, cosine, sine):
    length, width = branch.shape
    half, half_ff = width // 2, hidden.shape[1]
    rows = length // 4
    bf16, f32 = jnp.bfloat16, jnp.float32

    def shape(*dims, dtype=bf16):
        return jax.ShapeDtypeStruct(dims, dtype)

    columns = 2 * half_ff + 3 * half
    shapes = [
        shape(2, rows, width),
        shape(2, rows, width),
        shape(width // 8, 2 * columns),
        shape(width // 8, width),
        shape(half_ff // 4, width),
        shape(2, width, dtype=f32),
        shape(width, columns),
        shape(half, width),
        shape(length // 2, width, dtype=f32),
        shape(2, length // 2, width),
        shape(length, width, dtype=f32),
    ]
    dma, vmem = pltpu.SemaphoreType.DMA, pltpu.VMEM
    whole = pl.BlockSpec(memory_space=pltpu.VMEM)
    ring, row = COLUMN_SLOTS, width // 4
    jobs = width // JOB
    row_buffers = []
    for depth in (half_ff // 2, half // 2):
        row_buffers += [
            vmem((jobs, depth, JOB), bf16), vmem((jobs, depth, JOB), bf16), vmem((jobs, 2, depth, JOB), bf16),
            vmem((depth, JOB), bf16), dma((jobs, 3, 4)), dma((jobs, 2, 3)),
        ]
    return pl.pallas_call(
        backward_kernel,
        in_specs=[ANY] * 16 + [whole] * 4,
        out_specs=[ANY] * 5 + [whole] + [ANY] * 5,
        out_shape=shapes,
        scratch_shapes=[
            vmem((ring, 2 * row, JOB), bf16), vmem((ring, 2 * row, JOB), bf16), vmem((ring, row, JOB), bf16),
            vmem((ring, 2, row, JOB), bf16), dma((ring, 3, 4)), dma((ring, 2, 3)),
            pltpu.SemaphoreType.REGULAR((ring,)),
        ]
        + row_buffers
        + [
            vmem((length, width), bf16), vmem((length // 2, width), bf16), pltpu.SemaphoreType.REGULAR,
            dma((2, 3)), dma((2, 1)),
            vmem((GAIN_HOPS, 2, 2, width), f32), dma((2, GAIN_HOPS)), dma((2, 3, 2)), dma((4,)), dma((2, 3)),
            dma((2, 2)),
        ],
        compiler_params=pltpu.CompilerParams(
            collective_id=1, has_side_effects=True, vmem_limit_bytes=63 * 1024 * 1024
        ),
        cost_estimate=pl.CostEstimate(flops=0, bytes_accessed=800_000_000, transcendentals=0),
        name="backward",
    )(
        branch, *slopes, hidden, *turned, heads, lse, middle, x, g_down, *weights, start, gain, cosine, sine
    )


def wide(value):
    return value.astype(jnp.float32)


def dot(a, b):
    return jnp.dot(a, b, preferred_element_type=jnp.float32)


def column_device(
    tokens, segment_ids, out_grad, w_q, w_k, w_v, w_o, w_gate, w_up, w_down, gain_attn, gain_ffn
):
    dp_at = lax.axis_index("dp")
    rows, width = tokens.shape[1], tokens.shape[2]
    length, ff = 4 * rows, w_gate.shape[1]
    gains = lax.dynamic_update_slice_in_dim(
        jnp.zeros((2, width), jnp.bfloat16),
        jnp.stack([gain_attn, gain_ffn]),
        dp_at * gain_attn.shape[0],
        1,
    )
    cosine, sine = rope_tables(jnp.arange(length, dtype=jnp.int32), HD // 2)
    cosine = jnp.concatenate([cosine] * 4, axis=1)
    sine = jnp.concatenate([-sine, sine, -sine, sine], axis=1)
    (
        x_low, docs, grad_branch, gains, full_qkv, full_o, full_ff, full_down, heads, lse, middle,
        slope_gate, slope_up, hidden, g_down, start, gain, normed_t, nf_t, mixed_t,
    ) = gather_all(
        tokens, segment_ids.reshape(2, 1, rows), out_grad, gains, cosine, sine,
        (w_q, w_k, w_v, w_o, w_gate, w_up, w_down),
    )
    result, grad_tokens, g_cols, g_o, g_down, grad_gains = backward(
        grad_branch, (slope_gate, slope_up), hidden, (nf_t, normed_t, mixed_t), heads, lse, middle, x_low, g_down,
        (full_qkv, full_o, full_ff, full_down), start, gain, cosine, sine,
    )[:6]
    grad_gains = lax.dynamic_slice_in_dim(grad_gains, dp_at * (width // 8), width // 8, 1)
    first = 2 * ff
    return (
        result,
        wide(grad_tokens),
        wide(g_cols[:, first : first + width]),
        wide(g_cols[:, first + width : first + 2 * width]),
        wide(g_cols[:, first + 2 * width :]),
        wide(g_o),
        wide(g_cols[:, :ff]),
        wide(g_cols[:, ff:first]),
        wide(g_down),
        grad_gains[0],
        grad_gains[1],
    )


def solution(mesh):
    placed = (
        P(None, ("dp", "seq"), None),
        P(None, ("dp", "seq")),
        P(None, ("dp", "seq"), None),
        P("dp", None),
        P("dp", None),
        P("dp", None),
        P("dp", None),
        P("dp", None),
        P("dp", None),
        P("dp", None),
        P("dp"),
        P("dp"),
    )
    return jax.shard_map(
        column_device if dict(mesh.shape) == FAST_MESH else per_device,
        mesh=mesh,
        in_specs=placed,
        out_specs=(
            P(None, ("dp", "seq"), None),
            P(None, ("dp", "seq"), None),
            P("dp", None),
            P("dp", None),
            P("dp", None),
            P("dp", None),
            P("dp", None),
            P("dp", None),
            P("dp", None),
            P("dp"),
            P("dp"),
        ),
        check_vma=False,
    )
```

```python
import functools
import math

import jax
import jax.numpy as jnp
import numpy as np
from jax import lax
from jax.experimental import pallas as pl
from jax.experimental.pallas import tpu as pltpu
from jax.sharding import PartitionSpec as P

HEADS = 24
HD = 64


EPS = 1e-05


def positions_of(doc_row):
    count = doc_row.shape[0]
    place = jnp.arange(count, dtype=jnp.int32)
    before = jnp.concatenate([doc_row[:1], doc_row[:-1]])
    starts = (place == 0) | (doc_row != before)
    first_place = lax.cummax(jnp.where(starts, place, jnp.zeros_like(place)), axis=0)
    return place - first_place


def rope_tables(where_at, half):
    inverse = jnp.exp(jnp.arange(half, dtype=jnp.float32) * (-math.log(10000.0) / half))
    angle = where_at.astype(jnp.float32)[:, None] * inverse[None, :]
    return (jnp.cos(angle), jnp.sin(angle))


def rotate(values, cosine, sine):
    half = values.shape[-1] // 2
    first, second = (values[..., :half], values[..., half:])
    cos_heads, sin_heads = (cosine[:, None, :], sine[:, None, :])
    return jnp.concatenate(
        [first * cos_heads - second * sin_heads, second * cos_heads + first * sin_heads], axis=-1
    )


def rotate_back(grads, cosine, sine):
    half = grads.shape[-1] // 2
    first, second = (grads[..., :half], grads[..., half:])
    cos_heads, sin_heads = (cosine[:, None, :], sine[:, None, :])
    return jnp.concatenate(
        [first * cos_heads + second * sin_heads, second * cos_heads - first * sin_heads], axis=-1
    )


def rms_norm(values, gain):
    return values * lax.rsqrt(jnp.mean(values * values, axis=-1, keepdims=True) + EPS) * gain


def norm_backward(values, gain, grad_normed):
    scale = lax.rsqrt(jnp.mean(values * values, axis=-1, keepdims=True) + EPS)
    unit = values * scale
    grad_gain = jnp.sum(grad_normed * unit, axis=0)
    inner = grad_normed * gain
    grad_values = scale * (inner - unit * jnp.mean(inner * unit, axis=-1, keepdims=True))
    return (grad_gain, grad_values)


def block_scores(query_heads, key_heads, doc_row, start, block):
    length = doc_row.shape[0]
    place = jnp.arange(length, dtype=jnp.int32)
    query_block = lax.dynamic_slice_in_dim(query_heads, start, block, 0)
    doc_block = lax.dynamic_slice_in_dim(doc_row, start, block, 0)
    rows_block = start + jnp.arange(block, dtype=jnp.int32)
    allowed = (doc_block[:, None] == doc_row[None, :]) & (rows_block[:, None] >= place[None, :])
    scores = (
        jnp.einsum("qhd,khd->hqk", query_block, key_heads, preferred_element_type=jnp.float32)
        * 0.125
    )
    return (query_block, jnp.where(allowed[None], scores, -1e30))


def attention_forward(query, key, value, doc_row):
    length = query.shape[0]
    head_shape = (length, query.shape[1] // HD, HD)
    query_heads, key_heads, value_heads = (
        query.reshape(head_shape),
        key.reshape(head_shape),
        value.reshape(head_shape),
    )
    block = min(512, length)
    starts = jnp.arange(length // block, dtype=jnp.int32) * block

    def one_block(start):
        unused, scores = block_scores(query_heads, key_heads, doc_row, start, block)
        peak = jnp.max(scores, axis=-1, keepdims=True)
        expo = jnp.exp(scores - peak)
        total = jnp.sum(expo, axis=-1, keepdims=True)
        probs_low = (expo / total).astype(jnp.bfloat16)
        mixed = jnp.einsum(
            "hqk,khd->qhd", probs_low, value_heads, preferred_element_type=jnp.float32
        )
        return (mixed.astype(jnp.bfloat16), (peak + jnp.log(total))[..., 0])

    mixed, logsum = lax.map(one_block, starts)
    return (mixed.reshape(length, query.shape[1]), logsum)


def attention_backward(query, key, value, doc_row, logsum, grad_mixed, cosine, sine):
    length = query.shape[0]
    head_shape = (length, query.shape[1] // HD, HD)
    query_heads, key_heads, value_heads = (
        query.reshape(head_shape),
        key.reshape(head_shape),
        value.reshape(head_shape),
    )
    grad_heads = grad_mixed.reshape(head_shape)
    block = min(512, length)
    starts = jnp.arange(length // block, dtype=jnp.int32) * block

    def one_block(carry, item):
        grad_key, grad_value = carry
        start, logsum_block = item
        query_block, scores = block_scores(query_heads, key_heads, doc_row, start, block)
        probs = jnp.exp(scores - logsum_block[..., None])
        probs_low = probs.astype(jnp.bfloat16)
        grad_block = lax.dynamic_slice_in_dim(grad_heads, start, block, 0)
        grad_probs = jnp.einsum(
            "qhd,khd->hqk", grad_block, value_heads, preferred_element_type=jnp.float32
        )
        inner = jnp.sum(probs * grad_probs, axis=-1, keepdims=True)
        grad_scores = (probs * (grad_probs - inner)).astype(jnp.bfloat16)
        grad_query = (
            jnp.einsum("hqk,khd->qhd", grad_scores, key_heads, preferred_element_type=jnp.float32)
            * 0.125
        )
        grad_key = (
            grad_key
            + jnp.einsum(
                "hqk,qhd->khd", grad_scores, query_block, preferred_element_type=jnp.float32
            )
            * 0.125
        )
        grad_value = grad_value + jnp.einsum(
            "hqk,qhd->khd", probs_low, grad_block, preferred_element_type=jnp.float32
        )
        return ((grad_key, grad_value), grad_query)

    zeros_heads = jnp.zeros(head_shape, jnp.float32)
    (grad_key, grad_value), grad_query = lax.scan(
        one_block, (zeros_heads, zeros_heads), (starts, logsum)
    )
    grad_query = rotate_back(grad_query.reshape(head_shape), cosine, sine)
    grad_key = rotate_back(grad_key, cosine, sine)
    width_here = query.shape[1]
    return (
        grad_query.reshape(length, width_here).astype(jnp.bfloat16),
        grad_key.reshape(length, width_here).astype(jnp.bfloat16),
        grad_value.reshape(length, width_here).astype(jnp.bfloat16),
    )


def per_device(
    tokens, segment_ids, out_grad, w_q, w_k, w_v, w_o, w_gate, w_up, w_down, gain_attn, gain_ffn
):
    micro, rows, width = tokens.shape
    offset = lax.axis_index("seq") * rows
    shards = (w_q, w_k, w_v, w_o, w_gate, w_up, w_down, gain_attn, gain_ffn)
    gathered = (
        lax.all_gather(shards[0], "dp", axis=0, tiled=True),
        lax.all_gather(shards[1], "dp", axis=0, tiled=True),
        lax.all_gather(shards[2], "dp", axis=0, tiled=True),
        lax.all_gather(shards[3], "dp", axis=0, tiled=True),
        lax.all_gather(shards[4], "dp", axis=0, tiled=True),
        lax.all_gather(shards[5], "dp", axis=0, tiled=True),
        lax.all_gather(shards[6], "dp", axis=0, tiled=True),
        lax.all_gather(shards[7], "dp", axis=0, tiled=True),
        lax.all_gather(shards[8], "dp", axis=0, tiled=True),
    )
    docs = lax.all_gather(segment_ids, "seq", axis=1, tiled=True)
    full_q, full_k, full_v, full_o, full_gate, full_up, full_down, full_gain_a, full_gain_f = (
        gathered
    )
    gain_a = full_gain_a.astype(jnp.float32)
    gain_f = full_gain_f.astype(jnp.float32)
    row_heads = (rows, HEADS, HD)
    saved = []
    results = []
    for micro_index in range(micro):
        rows_in = tokens[micro_index].astype(jnp.float32)
        doc_row = docs[micro_index]
        cosine, sine = rope_tables(positions_of(doc_row), HD // 2)
        own_cos = lax.dynamic_slice_in_dim(cosine, offset, rows, 0)
        own_sin = lax.dynamic_slice_in_dim(sine, offset, rows, 0)
        normed = rms_norm(rows_in, gain_a).astype(jnp.bfloat16)
        query_rows = jnp.dot(normed, full_q, preferred_element_type=jnp.float32).reshape(row_heads)
        query_rows = rotate(query_rows, own_cos, own_sin).reshape(rows, width).astype(jnp.bfloat16)
        key_rows = jnp.dot(normed, full_k, preferred_element_type=jnp.float32).reshape(row_heads)
        key_rows = rotate(key_rows, own_cos, own_sin).reshape(rows, width).astype(jnp.bfloat16)
        value_rows = jnp.dot(normed, full_v, preferred_element_type=jnp.float32).astype(
            jnp.bfloat16
        )
        query, key, value = (
            lax.all_to_all(query_rows, "seq", split_axis=1, concat_axis=0, tiled=True),
            lax.all_to_all(key_rows, "seq", split_axis=1, concat_axis=0, tiled=True),
            lax.all_to_all(value_rows, "seq", split_axis=1, concat_axis=0, tiled=True),
        )
        mixed, logsum = attention_forward(query, key, value, doc_row)
        mixed_rows = lax.all_to_all(mixed, "seq", split_axis=0, concat_axis=1, tiled=True)
        middle = rows_in + jnp.dot(mixed_rows, full_o, preferred_element_type=jnp.float32)
        normed_ffn = rms_norm(middle, gain_f).astype(jnp.bfloat16)
        gate = jnp.dot(normed_ffn, full_gate, preferred_element_type=jnp.float32)
        up_value = jnp.dot(normed_ffn, full_up, preferred_element_type=jnp.float32)
        hidden = (jax.nn.silu(gate) * up_value).astype(jnp.bfloat16)
        result = middle + jnp.dot(hidden, full_down, preferred_element_type=jnp.float32)
        results.append(result.astype(jnp.bfloat16))
        saved.append(
            (
                rows_in,
                doc_row,
                cosine,
                sine,
                normed,
                query,
                key,
                value,
                logsum,
                mixed_rows,
                middle,
                normed_ffn,
                gate,
                up_value,
                hidden,
            )
        )
    back_weights = (
        lax.all_gather(shards[0], "dp", axis=0, tiled=True),
        lax.all_gather(shards[1], "dp", axis=0, tiled=True),
        lax.all_gather(shards[2], "dp", axis=0, tiled=True),
        lax.all_gather(shards[3], "dp", axis=0, tiled=True),
        lax.all_gather(shards[4], "dp", axis=0, tiled=True),
        lax.all_gather(shards[5], "dp", axis=0, tiled=True),
        lax.all_gather(shards[6], "dp", axis=0, tiled=True),
        lax.all_gather(shards[7], "dp", axis=0, tiled=True),
        lax.all_gather(shards[8], "dp", axis=0, tiled=True),
    )
    back_q, back_k, back_v, back_o, back_gate, back_up, back_down, back_gain_a, back_gain_f = (
        back_weights
    )
    gain_back_a = back_gain_a.astype(jnp.float32)
    gain_back_f = back_gain_f.astype(jnp.float32)
    totals = [jnp.zeros(weight.shape, jnp.float32) for weight in back_weights]
    grad_inputs = []
    for micro_index in range(micro):
        (
            rows_in,
            doc_row,
            cosine,
            sine,
            normed,
            query,
            key,
            value,
            logsum,
            mixed_rows,
            middle,
            normed_ffn,
            gate,
            up_value,
            hidden,
        ) = saved[micro_index]
        grad_out = out_grad[micro_index].astype(jnp.float32)
        grad_branch = grad_out.astype(jnp.bfloat16)
        totals[6] = totals[6] + jnp.einsum(
            "tf,td->fd", hidden, grad_branch, preferred_element_type=jnp.float32
        )
        grad_hidden = jnp.einsum(
            "td,fd->tf", grad_branch, back_down, preferred_element_type=jnp.float32
        )
        sigma = jax.nn.sigmoid(gate)
        grad_gate = (grad_hidden * up_value * sigma * (1.0 + gate * (1.0 - sigma))).astype(
            jnp.bfloat16
        )
        grad_up = (grad_hidden * jax.nn.silu(gate)).astype(jnp.bfloat16)
        totals[4] = totals[4] + jnp.einsum(
            "td,tf->df", normed_ffn, grad_gate, preferred_element_type=jnp.float32
        )
        totals[5] = totals[5] + jnp.einsum(
            "td,tf->df", normed_ffn, grad_up, preferred_element_type=jnp.float32
        )
        grad_normed_ffn = jnp.einsum(
            "tf,df->td", grad_gate, back_gate, preferred_element_type=jnp.float32
        )
        grad_normed_ffn = grad_normed_ffn + jnp.einsum(
            "tf,df->td", grad_up, back_up, preferred_element_type=jnp.float32
        )
        grad_gain_f, grad_middle = norm_backward(middle, gain_back_f, grad_normed_ffn)
        totals[8] = totals[8] + grad_gain_f
        grad_middle = grad_middle + grad_out
        grad_attn = grad_middle.astype(jnp.bfloat16)
        totals[3] = totals[3] + jnp.einsum(
            "ti,td->id", mixed_rows, grad_attn, preferred_element_type=jnp.float32
        )
        grad_mixed_rows = jnp.einsum(
            "td,id->ti", grad_attn, back_o, preferred_element_type=jnp.float32
        ).astype(jnp.bfloat16)
        grad_mixed = lax.all_to_all(grad_mixed_rows, "seq", split_axis=1, concat_axis=0, tiled=True)
        grad_query, grad_key, grad_value = attention_backward(
            query, key, value, doc_row, logsum, grad_mixed, cosine, sine
        )
        query_back, key_back, value_back = (
            lax.all_to_all(grad_query, "seq", split_axis=0, concat_axis=1, tiled=True),
            lax.all_to_all(grad_key, "seq", split_axis=0, concat_axis=1, tiled=True),
            lax.all_to_all(grad_value, "seq", split_axis=0, concat_axis=1, tiled=True),
        )
        totals[0] = totals[0] + jnp.einsum(
            "td,te->de", normed, query_back, preferred_element_type=jnp.float32
        )
        totals[1] = totals[1] + jnp.einsum(
            "td,te->de", normed, key_back, preferred_element_type=jnp.float32
        )
        totals[2] = totals[2] + jnp.einsum(
            "td,te->de", normed, value_back, preferred_element_type=jnp.float32
        )
        grad_normed = jnp.einsum(
            "te,de->td", query_back, back_q, preferred_element_type=jnp.float32
        )
        grad_normed = grad_normed + jnp.einsum(
            "te,de->td", key_back, back_k, preferred_element_type=jnp.float32
        )
        grad_normed = grad_normed + jnp.einsum(
            "te,de->td", value_back, back_v, preferred_element_type=jnp.float32
        )
        grad_gain_a, grad_rows = norm_backward(rows_in, gain_back_a, grad_normed)
        totals[7] = totals[7] + grad_gain_a
        grad_inputs.append(grad_rows + grad_middle)
    summed_all = (
        totals[0],
        totals[1],
        totals[2],
        totals[3],
        totals[4],
        totals[5],
        totals[6],
        totals[7],
        totals[8],
    )
    pieces = (
        lax.psum_scatter(
            summed_all[0].astype(jnp.bfloat16), "dp", scatter_dimension=0, tiled=True
        ).astype(jnp.float32),
        lax.psum_scatter(
            summed_all[1].astype(jnp.bfloat16), "dp", scatter_dimension=0, tiled=True
        ).astype(jnp.float32),
        lax.psum_scatter(
            summed_all[2].astype(jnp.bfloat16), "dp", scatter_dimension=0, tiled=True
        ).astype(jnp.float32),
        lax.psum_scatter(
            summed_all[3].astype(jnp.bfloat16), "dp", scatter_dimension=0, tiled=True
        ).astype(jnp.float32),
        lax.psum_scatter(
            summed_all[4].astype(jnp.bfloat16), "dp", scatter_dimension=0, tiled=True
        ).astype(jnp.float32),
        lax.psum_scatter(
            summed_all[5].astype(jnp.bfloat16), "dp", scatter_dimension=0, tiled=True
        ).astype(jnp.float32),
        lax.psum_scatter(
            summed_all[6].astype(jnp.bfloat16), "dp", scatter_dimension=0, tiled=True
        ).astype(jnp.float32),
        lax.psum_scatter(
            summed_all[7].astype(jnp.bfloat16), "dp", scatter_dimension=0, tiled=True
        ).astype(jnp.float32),
        lax.psum_scatter(
            summed_all[8].astype(jnp.bfloat16), "dp", scatter_dimension=0, tiled=True
        ).astype(jnp.float32),
    )
    pieces = (
        lax.psum(pieces[0].astype(jnp.bfloat16), "seq").astype(jnp.float32),
        lax.psum(pieces[1].astype(jnp.bfloat16), "seq").astype(jnp.float32),
        lax.psum(pieces[2].astype(jnp.bfloat16), "seq").astype(jnp.float32),
        lax.psum(pieces[3].astype(jnp.bfloat16), "seq").astype(jnp.float32),
        lax.psum(pieces[4].astype(jnp.bfloat16), "seq").astype(jnp.float32),
        lax.psum(pieces[5].astype(jnp.bfloat16), "seq").astype(jnp.float32),
        lax.psum(pieces[6].astype(jnp.bfloat16), "seq").astype(jnp.float32),
        lax.psum(pieces[7].astype(jnp.bfloat16), "seq").astype(jnp.float32),
        lax.psum(pieces[8].astype(jnp.bfloat16), "seq").astype(jnp.float32),
    )
    return (
        jnp.stack(results),
        jnp.stack(grad_inputs),
        pieces[0],
        pieces[1],
        pieces[2],
        pieces[3],
        pieces[4],
        pieces[5],
        pieces[6],
        pieces[7],
        pieces[8],
    )


BLK = 256
LOG2E = 1.4426950408889634


def swap_halves(v):
    lane = lax.broadcasted_iota(jnp.int32, v.shape, 1)
    width = v.shape[1]
    up = pltpu.roll(v, width - 32, axis=1)
    down = pltpu.roll(v, 32, axis=1)
    return jnp.where(lane % 64 < 32, up, down)


def nt(a, b):
    return lax.dot_general(a, b, (((1,), (1,)), ((), ())), preferred_element_type=jnp.float32)


def tn(a, b):
    return lax.dot_general(a, b, (((0,), (0,)), ((), ())), preferred_element_type=jnp.float32)


FAST_MESH = {"dp": 8, "seq": 4}
ANY = pl.BlockSpec(memory_space=pl.ANY)


class Place:
    def __init__(self):
        self.dp, self.z = lax.axis_index("dp"), lax.axis_index("seq")
        self.core = self.dp % 2
        self.x = (self.dp // 2) % 2
        self.y = self.dp // 4
        self.over_core = self.dp + 1 - 2 * self.core
        self.over_x = self.dp + 2 - 4 * self.x
        self.over_y = self.dp + 4 - 8 * self.y
        self.middle = (self.z == 1) | (self.z == 2)


def enter(devices):
    barrier = pltpu.get_barrier_semaphore()
    for dp, seq in devices:
        pl.semaphore_signal(
            barrier, inc=1, device_id={"dp": dp, "seq": seq}, device_id_type=pl.DeviceIdType.MESH
        )
    pl.semaphore_wait(barrier, len(devices))


def remote(src, dst, send_sem, recv_sem, dp, seq):
    return pltpu.make_async_remote_copy(
        src_ref=src,
        dst_ref=dst,
        send_sem=send_sem,
        recv_sem=recv_sem,
        device_id={"dp": dp, "seq": seq},
        device_id_type=pl.DeviceIdType.MESH,
    )


def gather_kernel(
    tokens, segments, out_grad, gains, cosine, sine, w_q, w_k, w_v, w_o, w_gate, w_up, w_down,
    x_out, seg_out, g_out, gains_out, qkv_out, o_out, ff_out, down_out,
    heads_out, lse_out, middle_out, slope_gate_out, slope_up_out, hidden_out, g_down_out, start_out,
    gain_out, normed_t_out, nf_t_out, mixed_t_out,
    send, recv, local, row_send, row_recv, row_local, gain_send, gain_recv,
    x_v, seg_v, gains_v, normed_v, w_qkv_v, heads_v, mixed_v, w_o_v, middle_v, part_send, part_recv,
    nf_v, w_ff_v, branch_v, tile_v, g_tile_v, lse_v, start_v, lse_t_v, start_row_v, gain_v, turned_v, mixed_t_v,
    part_sem, load_sem, w_sem, tile_sem, store_sem,
):
    me = Place()
    rows = tokens.shape[1]
    plane = [(lax.rem(me.dp + k, 8), me.z) for k in range(1, 8)]
    column = [
        (me.dp - me.core + core, lax.rem(me.z + k, 4)) for k in range(1, 4) for core in range(2)
    ]
    enter(plane + column)
    started = []

    def begin(copy):
        copy.start()
        started.append(copy)

    streams = ((tokens, x_out), (segments, seg_out), (out_grad, g_out))

    def place_of(ref, seq):
        return ref.at[pl.ds(rows * seq, rows)] if ref.shape[0] == 4 * rows else ref.at[seq]

    def row_copies(index):
        source, target = streams[index]
        for m in range(2):
            core, seq = me.z // 2, 2 * m + me.core
            here = (core == me.core) & (seq == me.z)

            @pl.when(here)
            def _():
                pltpu.make_async_copy(
                    source.at[m], place_of(target, me.z), row_local.at[index]
                ).start()

            @pl.when(jnp.logical_not(here))
            def _():
                remote(
                    source.at[m], place_of(target, me.z), row_send.at[index, m],
                    row_recv.at[index, me.z % 2], me.dp - me.core + core, seq,
                ).start()

    def row_wait_send(index):
        source, target = streams[index]
        for m in range(2):
            core, seq = me.z // 2, 2 * m + me.core
            here = (core == me.core) & (seq == me.z)

            @pl.when(jnp.logical_not(here))
            def _():
                remote(
                    source.at[m], place_of(target, me.z), row_send.at[index, m],
                    row_recv.at[index, me.z % 2], me.dp - me.core + core, seq,
                ).wait_send()

    def row_relay(index):
        source, target = streams[index]
        for slot in range(2):
            seq = 2 * me.core + slot
            block = place_of(target, seq)
            here = (seq == me.z) & (me.z % 2 == me.core)

            @pl.when(here)
            def _():
                pltpu.make_async_copy(block, block, row_local.at[index]).wait()

            @pl.when(jnp.logical_not(here))
            def _():
                remote(
                    block, block, row_send.at[index, slot], row_recv.at[index, slot], me.over_core, me.z
                ).wait_recv()

            begin(
                remote(
                    block, block, row_send.at[index, 2 + slot], row_recv.at[index, 2 + slot],
                    me.over_core, me.z,
                )
            )

    def row_finish(index):
        source, target = streams[index]
        for slot in range(2):
            block = place_of(target, 2 * (1 - me.core) + slot)
            remote(
                block, block, row_send.at[index, 2 + slot], row_recv.at[index, 2 + slot], me.over_core, me.z
            ).wait_recv()

    by_columns = []
    base = 0
    for source in (w_q, w_k, w_v):
        by_columns.append((source, qkv_out, base))
        base += source.shape[1] // 2
    by_columns.append((w_gate, ff_out, 0))
    by_columns.append((w_up, ff_out, w_gate.shape[1] // 2))
    by_rows = [(w_o, o_out), (w_down, down_out)]

    def column_piece(index, owner):
        source, target, first = by_columns[index]
        depth, width = source.shape[0], source.shape[1] // 2
        return target.at[pl.ds(depth * owner, depth), pl.ds(first, width)]

    def columns_start(index):
        source, target, first = by_columns[index]
        width = source.shape[1] // 2
        mine = column_piece(index, me.dp)
        for core in range(2):
            half = source.at[:, pl.ds(width * core, width)]
            begin(remote(half, mine, send.at[index, core], recv.at[index, me.core],
                         me.over_x - me.core + core, me.z))
            begin(remote(half, mine, send.at[index, 2 + core], recv.at[index, 2 + me.core],
                         me.over_y - me.core + core, me.z))

            @pl.when(core == me.core)
            def _():
                pltpu.make_async_copy(half, mine, local.at[index]).start()

            @pl.when(core != me.core)
            def _():
                remote(half, mine, send.at[index, 4], recv.at[index, 4], me.over_core, me.z).start()

    beside = me.z + 1 - 2 * lax.rem(me.z, 2)
    corner = me.over_x + me.over_y - me.dp - me.core

    def turn_of(index):
        return lax.rem(index + me.z, 2)

    last = 6

    def hand_on(index, piece, came, slot, send_slot, dp, seq):
        remote(piece, piece, send.at[index, send_slot], recv.at[index, came], dp, seq).wait_recv()
        remote(piece, piece, send.at[index, send_slot], recv.at[index, slot], dp, seq).start()

    def arrived(index, piece, slot):
        remote(piece, piece, send.at[index, 5], recv.at[index, slot], me.over_core, me.z).wait_recv()

    def left(index, piece, slot):
        remote(piece, piece, send.at[index, slot], recv.at[index, 5], me.over_core, me.z).wait_send()

    def columns_relay(index):
        @pl.when(turn_of(index) == 0)
        def _():
            hand_on(index, column_piece(index, me.over_x - me.core), 0, 5, 5, me.over_y, me.z)

        @pl.when(turn_of(index) == 1)
        def _():
            hand_on(index, column_piece(index, me.over_y - me.core + 1), 3, 6, 6, me.over_x, me.z)

    def columns_forward(index):
        @pl.when(turn_of(index) == 0)
        def _():
            hand_on(index, column_piece(index, corner), 5, 5, 6, me.dp, beside)

        @pl.when(turn_of(index) == 1)
        def _():
            hand_on(index, column_piece(index, corner + 1), 6, 6, 5, me.dp, beside)

    def columns_finish(index):
        source, target, first = by_columns[index]
        width = source.shape[1] // 2
        arrived(index, column_piece(index, me.over_x - me.core + 1), 1)
        arrived(index, column_piece(index, me.over_y - me.core), 2)
        arrived(index, column_piece(index, me.over_core), 4)

        @pl.when(turn_of(index) == 0)
        def _():
            arrived(index, column_piece(index, me.over_y - me.core + 1), 3)
            arrived(index, column_piece(index, corner + 1), 6)

        @pl.when(turn_of(index) == 1)
        def _():
            arrived(index, column_piece(index, me.over_x - me.core), 0)
            arrived(index, column_piece(index, corner), 5)

        mine = column_piece(index, me.dp)
        pltpu.make_async_copy(mine, mine, local.at[index]).wait()
        for slot in (4, 5, 6):
            left(index, mine, slot)

    def row_piece(which, owner):
        source, target = by_rows[which]
        depth = source.shape[0]
        return target.at[pl.ds(depth * lax.rem(owner, 4), depth), :]

    def rows_start(which):
        source, target = by_rows[which]
        index = 5 + which
        mine = row_piece(which, me.dp)
        begin(remote(source, mine, send.at[index, 0], recv.at[index, me.core],
                     me.over_x - me.core + me.y, me.z))
        begin(remote(source, mine, send.at[index, 1], recv.at[index, 2 + me.core],
                     me.over_y - me.core + me.y, me.z))

        @pl.when(me.core == me.y)
        def _():
            pltpu.make_async_copy(source, mine, local.at[index]).start()

        @pl.when(me.core != me.y)
        def _():
            remote(source, mine, send.at[index, 4], recv.at[index, 4], me.over_core, me.z).start()

    def rows_relay(which):
        index = 5 + which

        @pl.when((me.core == me.y) & ((index == last) | (turn_of(index) == 0)))
        def _():
            hand_on(index, row_piece(which, me.over_x - me.core), 0, 5, 5, me.over_y, me.z)

        @pl.when((me.core != me.y) & ((index == last) | (turn_of(index) == 1)))
        def _():
            hand_on(index, row_piece(which, me.over_y - me.core + 1), 3, 6, 6, me.over_x, me.z)

    def rows_forward(which):
        index = 5 + which

        @pl.when((me.core != me.y) & (turn_of(index) == 0))
        def _():
            hand_on(index, row_piece(which, corner), 5, 5, 6, me.dp, beside)

        @pl.when((me.core != me.y) & (turn_of(index) == 1))
        def _():
            hand_on(index, row_piece(which, corner + 1), 6, 6, 5, me.dp, beside)

    def rows_finish(which):
        source, target = by_rows[which]
        index = 5 + which
        mine = row_piece(which, me.dp)

        @pl.when(me.core == me.y)
        def _():
            arrived(index, row_piece(which, me.over_x - me.core + 1), 1)
            arrived(index, row_piece(which, me.over_core), 4)
            pltpu.make_async_copy(source, mine, local.at[index]).wait()

            @pl.when((index == last) | (turn_of(index) == 0))
            def _():
                left(index, mine, 5)

            @pl.when((index != last) & (turn_of(index) == 1))
            def _():
                arrived(index, row_piece(which, me.over_x - me.core), 0)

        @pl.when(me.core != me.y)
        def _():
            arrived(index, row_piece(which, me.over_y - me.core), 2)
            left(index, mine, 4)
            left(index, mine, 6)

            @pl.when((index != last) & (turn_of(index) == 0))
            def _():
                arrived(index, row_piece(which, me.over_y - me.core + 1), 3)
                arrived(index, row_piece(which, corner + 1), 6)

            @pl.when((index == last) | (turn_of(index) == 1))
            def _():
                arrived(index, row_piece(which, corner), 5)

            @pl.when(index == last)
            def _():
                arrived(index, row_piece(which, corner + 1), 6)

            @pl.when((index != last) & (turn_of(index) == 1))
            def _():
                left(index, mine, 5)

    def load(source, target, k):
        return pltpu.make_async_copy(source, target, load_sem.at[k])

    stores = []

    def store(source, target):
        copy = pltpu.make_async_copy(source, target, store_sem.at[len(stores)])
        stores.append(copy)
        copy.start()
        return copy

    length, width = x_v.shape
    own_width = width // 2
    half_ff = ff_out.shape[1] // 2

    row_copies(0)
    row_copies(1)
    for index in range(3):
        columns_start(index)
    for k in range(1, 8):
        begin(remote(gains, gains_out.at[me.dp], gain_send.at[k - 1], gain_recv.at[k - 1],
                     lax.rem(me.dp + k, 8), me.z))
    pltpu.make_async_copy(gains, gains_out.at[me.dp], gain_recv.at[7]).start()
    for index in range(3):
        columns_relay(index)
    rows_start(0)
    columns_start(3)
    row_relay(0)
    row_relay(1)
    for k in range(1, 8):
        piece = gains_out.at[lax.rem(me.dp + 8 - k, 8)]
        remote(piece, piece, gain_send.at[k - 1], gain_recv.at[k - 1], me.over_core, me.z).wait_recv()
    pltpu.make_async_copy(gains, gains_out.at[me.dp], gain_recv.at[7]).wait()
    load(gains_out, gains_v, 0).start()
    row_finish(1)
    load(seg_out, seg_v, 1).start()
    row_finish(0)
    load(x_out, x_v, 2).start()
    load(gains_out, gains_v, 0).wait()
    load(seg_out, seg_v, 1).wait()
    load(x_out, x_v, 2).wait()
    both_gains = gains_v[0].astype(jnp.float32)
    for k in range(1, 8):
        both_gains = both_gains + gains_v[k].astype(jnp.float32)
    gain_a, gain_f = both_gains[0:1], both_gains[1:2]
    gain_v[...] = both_gains
    store(gain_v, gain_out)

    norm_rows(lambda part: x_v[part, :].astype(jnp.float32), gain_a, normed_v, length)

    docs = jnp.concatenate([seg_v[k] for k in range(4)], axis=1)
    start_row = jnp.zeros((1, length), jnp.int32)
    for k in range(4):
        square = lax.broadcasted_iota(jnp.int32, (rows, rows), 0) == lax.broadcasted_iota(
            jnp.int32, (rows, rows), 1
        )
        ids = jnp.sum(jnp.where(square, seg_v[k], 0), axis=1, keepdims=True)
        start_v[pl.ds(rows * k, rows), :] = jnp.sum(
            jnp.where(docs < ids, 1, 0), axis=1, keepdims=True
        )
        start_row = start_row + jnp.sum(jnp.where(ids < docs, 1, 0), axis=0, keepdims=True)
    start_row_v[...] = start_row
    store(start_row_v, start_out)
    turn(normed_v, turned_v)
    normed_store = store(turned_v, normed_t_out)

    for index in range(3):
        columns_forward(index)
    rows_relay(0)
    columns_start(4)
    for index in range(3):
        columns_finish(index)
    tile = 256
    tiles = own_width // tile
    for t in range(tiles):
        for kind in range(3):
            part = pl.ds(own_width * kind + tile * t, tile)
            pltpu.make_async_copy(qkv_out.at[:, part], w_qkv_v.at[:, part], w_sem.at[kind, t]).start()
    for t in range(tiles):
        for kind in range(3):
            part = pl.ds(own_width * kind + tile * t, tile)
            pltpu.make_async_copy(qkv_out.at[:, part], w_qkv_v.at[:, part], w_sem.at[kind, t]).wait()
            product = jnp.dot(normed_v[...], w_qkv_v[:, part], preferred_element_type=jnp.float32)
            for k in range(tile // 128):
                piece = product[:, 128 * k : 128 * k + 128]
                if kind < 2:
                    piece = piece * cosine[...] + swap_halves(piece) * sine[...]
                heads_v[:, pl.ds(own_width * kind + tile * t + 128 * k, 128)] = piece.astype(jnp.bfloat16)

        def pair_step(pair, carry):
            attend(pair, own_width, heads_v, start_v, mixed_v, lse_v)
            return carry

        lax.fori_loop(tile // 128 * t, tile // 128 * (t + 1), pair_step, 0)
        if t == 0:
            row_copies(2)
        if t == 1:
            rows_forward(0)
            columns_relay(3)
    store(heads_v, heads_out)
    lse_t_v[...] = lse_v[...].T
    store(lse_t_v, lse_out)
    turn(mixed_v, mixed_t_v)
    store(mixed_t_v, mixed_t_out)

    rows_finish(0)
    load(o_out, w_o_v, 0).start()
    load(o_out, w_o_v, 0).wait()
    chunk = width // 3

    def part_copy(k):
        part = pl.ds(chunk * k, chunk)
        return remote(
            part_send.at[:, part], part_recv.at[:, part], part_sem.at[0, k], part_sem.at[1, k], me.over_core, me.z
        )

    for k in range(3):
        for at in range(chunk * k, chunk * (k + 1), tile):
            part = pl.ds(at, tile)
            product = jnp.dot(mixed_v[...], w_o_v[:, part], preferred_element_type=jnp.float32)
            part_send[:, part] = product.astype(jnp.bfloat16)
            middle_v[:, part] = x_v[:, part].astype(jnp.float32) + product
        part_copy(k).start()
    row_relay(2)
    columns_relay(4)
    rows_start(1)
    row_finish(2)
    load(g_out, branch_v, 1).start()
    for k in range(3):
        part_copy(k).wait_recv()

    def middle_rows(part):
        value = middle_v[part, :] + part_recv[part, :].astype(jnp.float32)
        middle_v[part, :] = value
        return value

    norm_rows(middle_rows, gain_f, nf_v, length)
    store(middle_v, middle_out)
    normed_store.wait()
    turn(nf_v, turned_v)
    store(turned_v, nf_t_out)
    load(g_out, branch_v, 1).wait()
    columns_forward(3)
    columns_forward(4)
    columns_finish(3)
    columns_finish(4)

    def ff_load(n, slot, kind):
        first = pl.multiple_of(half_ff * kind + tile * n, 128)
        return pltpu.make_async_copy(
            ff_out.at[:, pl.ds(first, tile)], w_ff_v.at[slot, kind], tile_sem.at[0, slot, kind]
        )

    def tile_store(n, slot, kind):
        part = pl.ds(pl.multiple_of(tile * n, 128), tile)
        target = (slope_gate_out, slope_up_out, hidden_out)[kind]
        return pltpu.make_async_copy(tile_v.at[slot, kind], target.at[:, part], tile_sem.at[1, slot, kind])

    def grad_store(n, slot):
        part = pl.ds(pl.multiple_of(tile * n, tile), tile)
        return pltpu.make_async_copy(g_tile_v.at[slot], g_down_out.at[part, :], tile_sem.at[2, slot, 0])

    count = half_ff // tile
    for kind in range(2):
        ff_load(0, 0, kind).start()

    def ff_step(n, carry):
        slot = lax.rem(n, 2)
        for kind in range(2):
            ff_load(n, slot, kind).wait()

        @pl.when(n + 1 < count)
        def _():
            for kind in range(2):
                ff_load(n + 1, 1 - slot, kind).start()

        @pl.when(n >= 2)
        def _():
            for kind in range(3):
                tile_store(n - 2, slot, kind).wait()
            grad_store(n - 2, slot).wait()

        gate = jnp.dot(nf_v[...], w_ff_v[slot, 0], preferred_element_type=jnp.float32)
        up_value = jnp.dot(nf_v[...], w_ff_v[slot, 1], preferred_element_type=jnp.float32)
        sigma = jax.nn.sigmoid(gate)
        silu = gate * sigma
        tile_v[slot, 0] = (up_value * sigma * (1.0 + gate * (1.0 - sigma))).astype(jnp.bfloat16)
        tile_v[slot, 1] = silu.astype(jnp.bfloat16)
        hidden = (silu * up_value).astype(jnp.bfloat16)
        tile_v[slot, 2] = hidden
        g_tile_v[slot] = jnp.dot(
            hidden.T, branch_v[...], preferred_element_type=jnp.float32
        ).astype(jnp.bfloat16)
        for kind in range(3):
            tile_store(n, slot, kind).start()
        grad_store(n, slot).start()

        @pl.when(n == count // 4)
        def _():
            rows_relay(1)

        return carry

    lax.fori_loop(0, count, ff_step, 0)
    for n in range(count - 2, count):
        for kind in range(3):
            tile_store(n, n % 2, kind).wait()
        grad_store(n, n % 2).wait()
    rows_finish(1)
    for copy in stores:
        if copy is not normed_store:
            copy.wait()
    for k in range(3):
        part_copy(k).wait_send()
    for index in range(3):
        row_wait_send(index)
    for copy in started:
        copy.wait_send()


def turn(source, target):
    for k in range(source.shape[1] // 256):
        target[256 * k : 256 * (k + 1), :] = source[:, 256 * k : 256 * (k + 1)].T


def norm_rows(read, gain, target, length, step=64):
    def chunk(k, carry):
        part = pl.ds(pl.multiple_of(k * step, step), step)
        values = read(part)
        scale = lax.rsqrt(jnp.mean(values * values, axis=-1, keepdims=True) + EPS)
        target[part, :] = (values * scale * gain).astype(target.dtype)
        return carry

    lax.fori_loop(0, length // step, chunk, 0)


def attend(pair, width, heads, start, mixed, lse):
    length = heads.shape[0]
    lane = lax.broadcasted_iota(jnp.int32, (BLK, 128), 1)
    cols = [pl.ds(pl.multiple_of(width * kind + 128 * pair, 128), 128) for kind in range(3)]
    for i in range(length // BLK):
        own_rows, keys = slice(BLK * i, BLK * (i + 1)), BLK * (i + 1)
        place = lax.broadcasted_iota(jnp.int32, (BLK, keys), 1)
        own = BLK * i + lax.broadcasted_iota(jnp.int32, (BLK, keys), 0)
        allowed = (place >= start[own_rows, :]) & (place <= own)
        query = heads[own_rows, cols[0]] * jnp.bfloat16(0.125)
        key, value = heads[0:keys, cols[1]], heads[0:keys, cols[2]]
        kept = lse[own_rows, :]
        outs = []
        for half in range(2):
            part = slice(64 * half, 64 * half + 64)
            scores = jnp.where(allowed, nt(query[:, part], key[:, part]), -1e30)
            peak = jnp.max(scores, axis=-1, keepdims=True)
            expo = jnp.exp(scores - peak)
            total = jnp.sum(expo, axis=-1, keepdims=True)
            out = jnp.dot(expo.astype(jnp.bfloat16), value[:, part], preferred_element_type=jnp.float32)
            outs.append((out / total).astype(jnp.bfloat16))
            kept = jnp.where(lane == 2 * pair + half, peak + jnp.log(total), kept)
        mixed[own_rows, cols[0]] = jnp.concatenate(outs, axis=1)
        lse[own_rows, :] = kept


def gather_all(tokens, segments, out_grad, gains, cosine, sine, weights):
    rows, width = tokens.shape[1], tokens.shape[2]
    length, half, ff = 4 * rows, width // 2, weights[4].shape[1]
    half_ff = ff // 2
    low = jnp.bfloat16

    def shape(*dims, dtype=low):
        return jax.ShapeDtypeStruct(dims, dtype)

    shapes = [
        shape(length, width),
        shape(4, *segments.shape[1:], dtype=jnp.int32),
        shape(length, width),
        shape(8, *gains.shape),
        shape(width, 3 * half),
        shape(half, width),
        shape(width, ff),
        shape(half_ff, width),
        shape(length, 3 * half),
        shape(128, length, dtype=jnp.float32),
        shape(length, width, dtype=jnp.float32),
        shape(length, half_ff),
        shape(length, half_ff),
        shape(length, half_ff),
        shape(half_ff, width),
        shape(1, length, dtype=jnp.int32),
        shape(2, width, dtype=jnp.float32),
        shape(width, length),
        shape(width, length),
        shape(half, length),
    ]
    dma, vmem = pltpu.SemaphoreType.DMA, pltpu.VMEM
    whole = pl.BlockSpec(memory_space=pltpu.VMEM)
    return pl.pallas_call(
        gather_kernel,
        in_specs=[ANY] * 4 + [whole] * 2 + [ANY] * 7,
        out_specs=[ANY] * len(shapes),
        out_shape=shapes,
        scratch_shapes=[
            dma((7, 7)), dma((7, 7)), dma((7,)), dma((3, 4)), dma((3, 4)), dma((3,)), dma((7,)), dma((8,)),
            vmem((length, width), low),
            vmem((4,) + segments.shape[1:], jnp.int32),
            vmem((8,) + gains.shape, low),
            vmem((length, width), low),
            vmem((width, 3 * half), low),
            vmem((length, 3 * half), low),
            vmem((length, half), low),
            vmem((half, width), low),
            vmem((length, width), jnp.float32),
            vmem((length, width), low),
            vmem((length, width), low),
            vmem((length, width), low),
            vmem((2, 2, width, 256), low),
            vmem((length, width), low),
            vmem((2, 3, length, 256), low),
            vmem((2, 256, width), low),
            vmem((length, 128), jnp.float32),
            vmem((length, 1), jnp.int32),
            vmem((128, length), jnp.float32),
            vmem((1, length), jnp.int32),
            vmem((2, width), jnp.float32),
            vmem((width, length), low),
            vmem((half, length), low),
            dma((2, 3)), dma((3,)), dma((3, 3)), dma((3, 2, 3)), dma((9,)),
        ],
        compiler_params=pltpu.CompilerParams(
            collective_id=0, has_side_effects=True, vmem_limit_bytes=61 * 1024 * 1024
        ),
        cost_estimate=pl.CostEstimate(flops=0, bytes_accessed=500_000_000, transcendentals=0),
        name="gather_all",
    )(tokens, segments, out_grad, gains, cosine, sine, *weights)


def guard(condition, action):
    if isinstance(condition, (bool, np.bool_)):
        if condition:
            action()
    else:
        pl.when(condition)(action)


def everything(*conditions):
    known = [c for c in conditions if isinstance(c, (bool, np.bool_))]
    if not all(known):
        return False
    rest = [c for c in conditions if not isinstance(c, (bool, np.bool_))]
    if not rest:
        return True
    total = rest[0]
    for c in rest[1:]:
        total = total & c
    return total


def chunk_of(rows):
    return 384 if rows % 384 == 0 else 512


def add_rows(target, first, other, rows):
    step = chunk_of(rows)

    def chunk(k, carry):
        at = pl.multiple_of(k * step, step)
        source = pl.multiple_of(first + k * step, step)
        target[pl.ds(at, step), :] += other[pl.ds(source, step), :]
        return carry

    lax.fori_loop(0, rows // step, chunk, 0)


JOB = 256


class Stream:
    active = True

    def tick(self, t):
        for late, stage in reversed(self.stages):
            k = t - late
            guard(everything(k >= 0, k < self.count), functools.partial(stage, k))

    @property
    def ticks(self):
        return self.count + self.stages[-1][0]

    def slot(self, k):
        return k % self.slots if isinstance(k, int) else lax.rem(k, self.slots)

    def column(self, k, base=0):
        return pl.ds(pl.multiple_of(base + JOB * k, 128), JOB)

    def total(self, k):
        return self.second.at[self.slot(k)]

    def final(self, k):
        return self.got.at[self.slot(k), pl.ds(0, self.rows)]

    def seq_copy(self, k, step):
        me, slot, sem = self.me, self.slot(k), self.seq_sem
        inner = me.z + 1 - 2 * (me.z // 2)
        opposite = 3 - me.z
        outer = 3 * (me.z // 2)
        if step == 0:
            return remote(self.total(k), self.over.at[slot, 0], sem.at[slot, 0, 0], sem.at[slot, 1, 0], me.dp, inner)
        if step == 1:
            return remote(
                self.total(k), self.over.at[slot, 1], sem.at[slot, 0, 1], sem.at[slot, 1, 1], me.dp, opposite
            )
        return remote(self.final(k), self.final(k), sem.at[slot, 0, 2], sem.at[slot, 1, 2], me.dp, outer)

    def plane_and_ends(self, k):
        self.reduce_plane(k)
        guard(
            everything(self.active, jnp.logical_not(self.me.middle)),
            lambda: self.seq_copy(k, 0).start(),
        )

    def across(self, k):
        def action():
            self.seq_copy(k, 0).wait_recv()
            add_rows(self.total(k), 0, self.over.at[self.slot(k), 0], self.rows)
            self.seq_copy(k, 1).start()

        guard(everything(self.active, self.me.middle), action)

    def back(self, k):
        def action():
            self.seq_copy(k, 1).wait_recv()
            final, total, over = self.final(k), self.total(k), self.over.at[self.slot(k), 1]
            step = chunk_of(self.rows)

            def chunk(at, carry):
                part = pl.ds(pl.multiple_of(at * step, step), step)
                final[part, :] = total[part, :] + over[part, :]
                return carry

            lax.fori_loop(0, self.rows // step, chunk, 0)
            self.seq_copy(k, 2).start()

        guard(everything(self.active, self.me.middle), action)

    def finish(self, k):
        guard(
            everything(self.active, jnp.logical_not(self.me.middle)),
            lambda: self.seq_copy(k, 2).wait_recv(),
        )
        self.output(k)

    def drain(self, k):
        self.drain_plane(k)

        def ends():
            self.seq_copy(k, 0).wait_send()

        def middles():
            self.seq_copy(k, 1).wait_send()
            self.seq_copy(k, 2).wait_send()

        guard(everything(self.active, jnp.logical_not(self.me.middle)), ends)
        guard(everything(self.active, self.me.middle), middles)


class ColumnStream(Stream):
    def __init__(self, me, source, target, ff_jobs, d_model, ff, refs):
        self.me, self.source, self.target = me, source, target
        self.got, self.keep, self.second, self.over, self.sem, self.seq_sem, self.credit = refs
        self.slots, self.rows = self.got.shape[0], source.shape[0] // 4
        self.count, self.ff_jobs = source.shape[1] // JOB, ff_jobs
        self.ff, self.d_model = ff, d_model
        self.stages = (
            (0, self.start), (2, self.pass_second), (4, self.plane_and_ends), (6, self.across),
            (8, self.back), (9, self.finish), (10, self.drain),
        )

    def x_first(self, k):
        late = k // self.ff_jobs
        return (1 - late) * ((k // (self.ff_jobs // 2)) % 2) * ((k + 1) % 2) + late * (k % 2)

    def first_copy(self, k, part):
        me, slot, x_first = self.me, self.slot(k), self.x_first(k)
        block = x_first * (2 * part + 1 - me.x) + (1 - x_first) * (2 * (1 - me.y) + part)
        sent = self.source.at[pl.ds(pl.multiple_of(self.rows * block, self.rows), self.rows), self.column(k)]
        to = x_first * me.over_x + (1 - x_first) * me.over_y
        return remote(
            sent, self.got.at[slot, pl.ds(self.rows * part, self.rows)],
            self.sem.at[slot, 0, part], self.sem.at[slot, 1, part], to, me.z,
        )

    def keep_copy(self, k, part):
        me, slot, x_first = self.me, self.slot(k), self.x_first(k)
        block = x_first * (2 * part + me.x) + (1 - x_first) * (2 * me.y + part)
        kept = self.source.at[pl.ds(pl.multiple_of(self.rows * block, self.rows), self.rows), self.column(k)]
        return pltpu.make_async_copy(
            kept, self.keep.at[slot, pl.ds(self.rows * part, self.rows)], self.sem.at[slot, 2, part]
        )

    def at(self, k):
        x_first = self.x_first(k)
        return x_first * self.me.y + (1 - x_first) * self.me.x

    def second_copy(self, k):
        me, slot, x_first = self.me, self.slot(k), self.x_first(k)
        row = pl.multiple_of(self.rows * (1 - self.at(k)), self.rows)
        to = x_first * me.over_y + (1 - x_first) * me.over_x
        return remote(
            self.keep.at[slot, pl.ds(row, self.rows)], self.second.at[slot],
            self.sem.at[slot, 0, 2], self.sem.at[slot, 1, 2], to, me.z,
        )

    def start(self, k):
        def credits():
            slot = self.slot(k)

            @pl.when(self.me.middle)
            def _():
                pl.semaphore_wait(self.credit.at[slot], 5)

            @pl.when(jnp.logical_not(self.me.middle))
            def _():
                pl.semaphore_wait(self.credit.at[slot], 4)

        guard(k >= self.slots, credits)
        for part in range(2):
            self.first_copy(k, part).start()
            self.keep_copy(k, part).start()

    def pass_second(self, k):
        for part in range(2):
            self.keep_copy(k, part).wait()
            self.first_copy(k, part).wait_recv()
        slot = self.slot(k)
        add_rows(self.keep.at[slot], 0, self.got.at[slot], 2 * self.rows)
        self.second_copy(k).start()

    def reduce_plane(self, k):
        self.second_copy(k).wait_recv()
        add_rows(self.total(k), self.rows * self.at(k), self.keep.at[self.slot(k)], self.rows)

    def out_column(self, k, core, late):
        if late:
            m, half = k - self.ff_jobs, self.d_model // 2
            tiles = half // JOB
            first = 2 * self.ff + self.d_model * (m // tiles) + JOB * (m % tiles) + half * core
        else:
            first = self.ff * (k % 2) + JOB * (k // 2) + self.ff // 2 * core
        return self.target.at[:, pl.ds(pl.multiple_of(first, 128), JOB)]

    def last_copy(self, k, late=False):
        me, slot, rows = self.me, self.slot(k), self.rows // 2
        part = self.got.at[slot, pl.ds(pl.multiple_of(rows * (1 - me.core), rows), rows)]
        return remote(
            part, self.out_column(k, me.core, late), self.sem.at[slot, 0, 3], self.sem.at[slot, 1, 3],
            me.over_core, me.z,
        )

    def own_copy(self, k, late=False):
        me, slot, rows = self.me, self.slot(k), self.rows // 2
        part = self.got.at[slot, pl.ds(pl.multiple_of(rows * me.core, rows), rows)]
        return pltpu.make_async_copy(part, self.out_column(k, me.core, late), self.sem.at[slot, 2, 0])

    def output(self, k):
        def begin(late):
            self.last_copy(k, late).start()
            self.own_copy(k, late).start()

        guard(k < self.ff_jobs, lambda: begin(False))
        guard(k >= self.ff_jobs, lambda: begin(True))

    def drain_plane(self, k):
        for part in range(2):
            self.first_copy(k, part).wait_send()
        self.second_copy(k).wait_send()

        def end(late):
            self.last_copy(k, late).wait()
            self.own_copy(k, late).wait()

        guard(k < self.ff_jobs, lambda: end(False))
        guard(k >= self.ff_jobs, lambda: end(True))

    def drain(self, k):
        super().drain(k)

        def signal(dp, seq):
            pl.semaphore_signal(
                self.credit.at[self.slot(k)], inc=1, device_id={"dp": dp, "seq": seq},
                device_id_type=pl.DeviceIdType.MESH,
            )

        def free():
            me = self.me
            for dp in (me.over_core, me.over_x, me.over_y):
                signal(dp, me.z)

            @pl.when(me.middle)
            def _():
                signal(me.dp, 3 - me.z)
                signal(me.dp, 3 * (me.z // 2))

            @pl.when(jnp.logical_not(me.middle))
            def _():
                signal(me.dp, me.z + 1 - 2 * (me.z // 2))

        guard(k + self.slots < self.count, free)


class RowStream(Stream):
    def __init__(self, me, source, target, lates, refs):
        self.me, self.source, self.target = me, source, target
        self.got, self.second, self.over, self.stage, self.sem, self.seq_sem = refs
        self.slots, self.rows = self.got.shape[0], source.shape[0] // 2
        self.count = source.shape[1] // JOB
        self.active = me.core == me.y
        steps = (
            self.start, self.load, self.pass_second, self.plane_and_ends, self.across, self.back, self.finish,
            self.drain,
        )
        self.stages = tuple(zip(lates, steps))

    def first_copy(self, k):
        me, slot = self.me, self.slot(k)
        sent = self.source.at[pl.ds(pl.multiple_of(self.rows * (1 - me.x), self.rows), self.rows), self.column(k)]
        return remote(sent, self.got.at[slot], self.sem.at[slot, 0, 0], self.sem.at[slot, 1, 0], me.over_x, me.z)

    def load_copy(self, k):
        kept = self.source.at[
            pl.ds(pl.multiple_of(self.rows * self.me.x, self.rows), self.rows), self.column(k)
        ]
        return pltpu.make_async_copy(kept, self.stage, self.sem.at[self.slot(k), 2, 0])

    def second_copy(self, k):
        me, slot = self.me, self.slot(k)
        return remote(
            self.got.at[slot], self.second.at[slot], self.sem.at[slot, 0, 2], self.sem.at[slot, 1, 2],
            me.over_y, me.z,
        )

    def start(self, k):
        self.first_copy(k).start()

    def load(self, k):
        self.load_copy(k).start()

    def pass_second(self, k):
        self.load_copy(k).wait()
        self.first_copy(k).wait_recv()
        add_rows(self.got.at[self.slot(k)], 0, self.stage, self.rows)
        guard(jnp.logical_not(self.active), lambda: self.second_copy(k).start())

    def reduce_plane(self, k):
        def action():
            self.second_copy(k).wait_recv()
            add_rows(self.total(k), 0, self.got.at[self.slot(k)], self.rows)

        guard(self.active, action)

    def last_copy(self, k):
        me, slot, rows = self.me, self.slot(k), self.rows // 2
        part = self.got.at[slot, pl.ds(pl.multiple_of(rows * (1 - me.core), rows), rows)]
        return remote(
            part, self.target.at[:, self.column(k)], self.sem.at[slot, 0, 3], self.sem.at[slot, 1, 3],
            me.over_core, me.z,
        )

    def own_copy(self, k):
        me, slot, rows = self.me, self.slot(k), self.rows // 2
        part = self.got.at[slot, pl.ds(pl.multiple_of(rows * me.core, rows), rows)]
        return pltpu.make_async_copy(part, self.target.at[:, self.column(k)], self.sem.at[slot, 2, 1])

    def output(self, k):
        def action():
            self.last_copy(k).start()
            self.own_copy(k).start()

        guard(self.active, action)

    def drain_plane(self, k):
        self.first_copy(k).wait_send()

        def active():
            self.last_copy(k).wait_send()
            self.own_copy(k).wait()

        def passive():
            self.second_copy(k).wait_send()
            self.last_copy(k).wait_recv()

        guard(self.active, active)
        guard(jnp.logical_not(self.active), passive)


GAIN_HOPS = 5


class GainSums:
    def __init__(self, me, target, buffer, sem):
        self.me, self.target, self.buffer, self.sem = me, target, buffer, sem

    def hop(self, k):
        me = self.me
        across = me.z + 2 - 4 * (me.z // 2)
        beside = me.z + 1 - 2 * (me.z % 2)
        dp = (me.over_core, me.over_x, me.over_y, me.dp, me.dp)[k]
        seq = (me.z, me.z, me.z, beside, across)[k]
        return remote(
            self.buffer.at[k, 0], self.buffer.at[k, 1], self.sem.at[0, k], self.sem.at[1, k], dp, seq
        )

    def start(self):
        self.hop(0).start()

    def step(self, k):
        self.hop(k).wait_recv()
        total = self.buffer[k, 0] + self.buffer[k, 1]
        if k + 1 < GAIN_HOPS:
            self.buffer[k + 1, 0] = total
            self.hop(k + 1).start()
        else:
            self.target[...] = total

    def drain(self):
        for k in range(GAIN_HOPS):
            self.hop(k).wait_send()


class RowsBack:
    def __init__(self, me, source, target, sem):
        self.me, self.source, self.target, self.sem = me, source, target, sem

    def each(self, local, elsewhere):
        me = self.me
        rows = self.source.shape[0] // 2
        for slot in range(2):
            core, seq = me.z % 2, 2 * me.core + slot
            here = (core == me.core) & (seq == me.z)
            block, target = self.source.at[pl.ds(rows * slot, rows)], self.target.at[me.z // 2]

            @pl.when(here)
            def _():
                local(pltpu.make_async_copy(block, target, self.sem.at[2, 0]))

            @pl.when(jnp.logical_not(here))
            def _():
                elsewhere(
                    remote(
                        block, target, self.sem.at[0, slot], self.sem.at[1, me.z // 2],
                        me.dp - me.core + core, seq,
                    )
                )

    def start(self):
        self.each(lambda copy: copy.start(), lambda copy: copy.start())

    def drain(self):
        me = self.me
        self.each(lambda copy: copy.wait(), lambda copy: copy.wait_send())
        rows = self.source.shape[0] // 2
        for m in range(2):
            here = (me.z == 2 * m + me.core) & (me.core == me.z // 2)

            @pl.when(jnp.logical_not(here))
            def _():
                remote(
                    self.source.at[pl.ds(0, rows)], self.target.at[m], self.sem.at[0, 0],
                    self.sem.at[1, m], me.over_core, me.z,
                ).wait_recv()


def attend_back(pair, width, heads, grad_mixed, start, lse, grads, key_sum, value_sum, query_sum, cosine, sine):
    length = heads.shape[0]
    cols = [pl.ds(pl.multiple_of(width * kind + 128 * pair, 128), 128) for kind in range(3)]
    key_sum[...] = jnp.zeros_like(key_sum)
    value_sum[...] = jnp.zeros_like(value_sum)
    for i in range(length // BLK):
        own_rows, keys = slice(BLK * i, BLK * (i + 1)), BLK * (i + 1)
        place = lax.broadcasted_iota(jnp.int32, (keys, BLK), 0)
        own = BLK * i + lax.broadcasted_iota(jnp.int32, (keys, BLK), 1)
        allowed = (place >= start[:, own_rows]) & (place <= own)
        query = heads[own_rows, cols[0]] * jnp.bfloat16(0.125)
        key, value = heads[0:keys, cols[1]], heads[0:keys, cols[2]]
        grad = grad_mixed[own_rows, cols[0]]
        for half in range(2):
            part = slice(64 * half, 64 * half + 64)
            scores = nt(key[:, part], query[:, part])
            logsum = lse[pl.ds(2 * pair + half, 1), own_rows]
            probs = jnp.where(allowed, jnp.exp(scores - logsum), 0.0)
            grad_probs = nt(value[:, part], grad[:, part])
            inner = jnp.sum(probs * grad_probs, axis=0, keepdims=True)
            grad_scores = (probs * (grad_probs - inner)).astype(jnp.bfloat16)
            value_sum[0:keys, part] += dot(probs.astype(jnp.bfloat16), grad[:, part])
            key_sum[0:keys, part] += dot(grad_scores, query[:, part])
            query_sum[own_rows, part] = tn(grad_scores, key[:, part]) * 0.125
    for kind, total in enumerate((query_sum, key_sum)):
        value = total[...]
        grads[:, cols[kind]] = (value * cosine[...] - swap_halves(value) * sine[...]).astype(jnp.bfloat16)
    grads[:, cols[2]] = value_sum[...].astype(jnp.bfloat16)


def backward_kernel(
    branch_h, slope_gate_h, slope_up_h, hidden_h, nf_t_h, normed_t_h, mixed_t_h, heads_h, lse_h, middle_h, x_h,
    g_down_h, w_qkv_h, w_o_h, w_ff_h, w_down_h, start_ref, gain_ref, cosine, sine,
    out_o, tokens_o, cols_o, o_o, down_o, gains_o, g_cols_h, g_o_h, kept_h, rows_h, grad_nf_h,
    col_got, col_keep, col_second, col_over, col_sem, col_seq, col_credit,
    down_got, down_second, down_over, down_stage, down_sem, down_seq,
    o_got, o_second, o_over, o_stage, o_sem, o_seq,
    wide_recv, half_recv, half_free, wide_sem, half_sem,
    gain_buffer, gain_sem, row_sem, load_sem, tile_sem, store_sem,
):
    me = Place()
    enter(
        [(me.over_core, me.z), (me.over_x, me.z), (me.over_y, me.z)]
        + [(me.dp - me.core + core, lax.rem(me.z + k, 4)) for k in range(1, 4) for core in range(2)]
    )
    length, width = branch_h.shape
    half_rows, own_width, half_ff = length // 2, width // 2, slope_gate_h.shape[1]
    bf16, f32 = jnp.bfloat16, jnp.float32
    vmem = pltpu.VMEM
    ff_jobs = 2 * half_ff // JOB
    cols = ColumnStream(
        me, g_cols_h, cols_o, ff_jobs, width, 2 * half_ff,
        (col_got, col_keep, col_second, col_over, col_sem, col_seq, col_credit),
    )
    downs = RowStream(
        me, g_down_h, down_o, (0, 2, 3, 5, 7, 8, 9, 10), (down_got, down_second, down_over, down_stage, down_sem, down_seq)
    )
    outs = RowStream(me, g_o_h, o_o, (0, 1, 2, 4, 6, 7, 8, 9), (o_got, o_second, o_over, o_stage, o_sem, o_seq))
    back_out = RowsBack(me, rows_h.at[0], out_o, row_sem.at[0])
    back_tokens = RowsBack(me, rows_h.at[1], tokens_o, row_sem.at[1])
    gains = GainSums(me, gains_o, gain_buffer, gain_sem)

    def load(source, target, k=0):
        return pltpu.make_async_copy(source, target, load_sem.at[k])

    def fetch(*pairs):
        for k, (source, target) in enumerate(pairs):
            load(source, target, k).start()
        for k, (source, target) in enumerate(pairs):
            load(source, target, k).wait()

    def lanes(n, size=JOB, base=0):
        return pl.ds(pl.multiple_of(base + size * n, 128), size)

    def sublanes(n, size):
        return pl.ds(pl.multiple_of(n * size, size), size)

    def grad_store(buffer, slot, target, n, k):
        return pltpu.make_async_copy(buffer.at[slot], target.at[:, lanes(n)], store_sem.at[slot, k])

    downs.tick(0)

    def feed_forward(grad_ff):
        steps = half_ff // JOB

        def hidden_grads(branch, w_tile, slopes, nf_t, g_tile):
            def tile_loads(n, slot):
                return (
                    pltpu.make_async_copy(w_down_h.at[sublanes(n, JOB), :], w_tile.at[slot], tile_sem.at[slot, 0]),
                    pltpu.make_async_copy(slope_gate_h.at[:, lanes(n)], slopes.at[slot, 0], tile_sem.at[slot, 1]),
                    pltpu.make_async_copy(slope_up_h.at[:, lanes(n)], slopes.at[slot, 1], tile_sem.at[slot, 2]),
                )

            for copy in tile_loads(0, 0):
                copy.start()
            fetch((branch_h, branch), (nf_t_h, nf_t))
            downs.tick(1)

            def step(n, carry):
                slot = lax.rem(n, 2)
                for copy in tile_loads(n, slot):
                    copy.wait()

                @pl.when(n + 1 < steps)
                def _():
                    for copy in tile_loads(n + 1, 1 - slot):
                        copy.start()

                grad_hidden = nt(branch[...], w_tile[slot])

                @pl.when(n > 0)
                def _():
                    for kind in range(2):
                        grad_store(g_tile, kind, g_cols_h, 2 * n - 2 + kind, 0).wait()

                for kind in range(2):
                    grad = (grad_hidden * slopes[slot, kind].astype(f32)).astype(bf16)
                    grad_ff[:, lanes(n, JOB, half_ff * kind)] = grad
                    g_tile[kind] = dot(nf_t[...], grad).astype(bf16)
                    grad_store(g_tile, kind, g_cols_h, 2 * n + kind, 0).start()

                @pl.when((n >= 2) & (n != 5))
                def _():
                    cols.tick(n - 2 - n // 6)

                @pl.when((n == 2) | (n == 6))
                def _():
                    downs.tick(2 + n // 6)

                return carry

            lax.fori_loop(0, steps, step, 0)
            for kind in range(2):
                grad_store(g_tile, kind, g_cols_h, 2 * steps - 2 + kind, 0).wait()

        pl.run_scoped(
            hidden_grads, vmem((length, width), bf16), vmem((2, JOB, width), bf16),
            vmem((2, 2, length, JOB), bf16), vmem((width, length), bf16), vmem((2, width, JOB), bf16),
        )

        def layer_out(hidden, w_down, send, total):
            other, own = 1 - me.core, me.core
            fetch((w_down_h, w_down), (hidden_h.at[sublanes(other, half_rows), :], hidden))
            load(middle_h.at[sublanes(own, half_rows), :], total, 2).start()

            def other_tile(n, carry):
                send[:, lanes(n)] = dot(hidden[...], w_down[:, lanes(n)]).astype(bf16)
                return carry

            lax.fori_loop(0, width // JOB, other_tile, 0)
            exchange = remote(send, half_recv, half_sem.at[0, 0], half_sem.at[1, 0], me.over_core, me.z)
            exchange.start()
            fetch((hidden_h.at[sublanes(own, half_rows), :], hidden))
            load(middle_h.at[sublanes(own, half_rows), :], total, 2).wait()

            def own_tile(n, carry):
                total[:, lanes(n)] += dot(hidden[...], w_down[:, lanes(n)])
                return carry

            lax.fori_loop(0, width // JOB, own_tile, 0)
            exchange.wait()

            def combine(k, carry):
                part = sublanes(k, 64)
                send[part, :] = (total[part, :] + half_recv[part, :].astype(f32)).astype(bf16)
                return carry

            lax.fori_loop(0, half_rows // 64, combine, 0)
            pl.semaphore_signal(
                half_free, inc=1, device_id={"dp": me.over_core, "seq": me.z},
                device_id_type=pl.DeviceIdType.MESH,
            )
            fetch((send, rows_h.at[0]))

        pl.run_scoped(
            layer_out, vmem((half_rows, half_ff), bf16), vmem((half_ff, width), bf16),
            vmem((half_rows, width), bf16), vmem((half_rows, width), f32),
        )
        back_out.start()

    chunk = 2 * JOB
    chunks = width // chunk

    def wide_copy(send, k):
        part = pl.ds(chunk * k, chunk)
        return remote(
            send.at[:, part], wide_recv.at[:, part], wide_sem.at[0, k], wide_sem.at[1, k], me.over_core, me.z
        )

    def with_grad_ff(grad_ff):
        feed_forward(grad_ff)

        def input_grads(w_tile, send, parts):
            def tile_load(n, kind):
                return pltpu.make_async_copy(
                    w_ff_h.at[sublanes(n, JOB), pl.ds(half_ff * kind, half_ff)], w_tile.at[kind],
                    tile_sem.at[kind, 0],
                )

            def part_store(n, slot):
                return pltpu.make_async_copy(parts.at[slot], grad_nf_h.at[:, lanes(n)], store_sem.at[slot, 0])

            for kind in range(2):
                tile_load(0, kind).start()
            count = width // JOB

            def step(n, carry):
                slot = lax.rem(n, 2)
                tile_load(n, 0).wait()
                part = nt(grad_ff[:, 0:half_ff], w_tile[0])

                @pl.when(n + 1 < count)
                def _():
                    tile_load(n + 1, 0).start()

                tile_load(n, 1).wait()
                part = part + nt(grad_ff[:, half_ff : 2 * half_ff], w_tile[1])

                @pl.when(n + 1 < count)
                def _():
                    tile_load(n + 1, 1).start()

                @pl.when(n >= 2)
                def _():
                    part_store(n - 2, slot).wait()

                parts[slot] = part
                part_store(n, slot).start()
                send[:, lanes(n)] = part.astype(bf16)
                for k in range(chunks):
                    @pl.when(n == 2 * k + 1)
                    def _():
                        wide_copy(send, k).start()

                @pl.when(lax.rem(n, 3) == 0)
                def _():
                    downs.tick(4 + n // 3)

                @pl.when(lax.rem(n, 3) == 2)
                def _():
                    cols.tick(5 + n // 3)

                return carry

            lax.fori_loop(0, count, step, 0)
            for n in range(count - 2, count):
                part_store(n, n % 2).wait()
            cols.tick(7)
            downs.tick(6)
            for k in range(chunks):
                wide_copy(send, k).wait()

        pl.run_scoped(
            input_grads, vmem((2, JOB, half_ff), bf16), vmem((length, width), bf16), vmem((2, length, JOB), f32)
        )

    pl.run_scoped(with_grad_ff, vmem((length, 2 * half_ff), bf16))

    def to_attention(grad_attn):
        def norm_back(grad_nf, middle, branch):
            fetch((middle_h, middle), (branch_h, branch), (grad_nf_h, grad_nf))
            gain = gain_ref[1:2, :]

            def rows(k, total):
                part = sublanes(k, 64)
                grad = grad_nf[part, :] + wide_recv[part, :].astype(f32)
                gained, values = norm_rows_back(middle[part, :], gain, grad)
                values = values + branch[part, :].astype(f32)
                grad_nf[part, :] = values
                grad_attn[part, :] = values.astype(bf16)
                return total + gained

            total = lax.fori_loop(0, length // 64, rows, jnp.zeros((1, width), f32))
            gain_buffer[0, 0, 1:2, :] = 0.5 * total
            kept = load(grad_nf.at[sublanes(me.core, half_rows), :], kept_h, 0)
            kept.start()
            cols.tick(8)
            downs.tick(7)
            kept.wait()

        pl.run_scoped(
            norm_back, vmem((length, width), f32), vmem((length, width), f32), vmem((length, width), bf16)
        )

        def out_projection(w_o, mixed_t, g_tile, grad_mixed):
            fetch((w_o_h, w_o), (mixed_t_h, mixed_t))
            for n in range(own_width // JOB):
                grad_mixed[:, JOB * n : JOB * (n + 1)] = nt(
                    grad_attn[...], w_o[JOB * n : JOB * (n + 1), :]
                ).astype(bf16)
            placed = load(grad_mixed, wide_recv.at[:, pl.ds(0, own_width)], 3)
            placed.start()
            count = width // JOB

            def step(n, carry):
                slot = lax.rem(n, 2)

                @pl.when(n >= 2)
                def _():
                    grad_store(g_tile, slot, g_o_h, n - 2, 1).wait()

                g_tile[slot] = dot(mixed_t[...], grad_attn[:, lanes(n)]).astype(bf16)
                grad_store(g_tile, slot, g_o_h, n, 1).start()

                @pl.when(lax.rem(n, 3) == 1)
                def _():
                    cols.tick(9 + n // 3)

                return carry

            lax.fori_loop(0, count, step, 0)
            for n in range(count - 2, count):
                grad_store(g_tile, n % 2, g_o_h, n, 1).wait()
            placed.wait()

        pl.run_scoped(
            out_projection, vmem((own_width, width), bf16), vmem((own_width, length), bf16),
            vmem((2, own_width, JOB), bf16), vmem((length, own_width), bf16),
        )

    pl.run_scoped(to_attention, vmem((length, width), bf16))

    def attention(grads):
        def heads_back(heads, lse, key_sum, value_sum, query_sum):
            fetch((heads_h, heads), (lse_h, lse))

            def step(pair, carry):
                attend_back(
                    pair, own_width, heads, wide_recv, start_ref, lse, grads, key_sum, value_sum, query_sum, cosine, sine
                )
                outs.tick(pair)

                @pl.when(lax.rem(pair, 3) != 2)
                def _():
                    cols.tick(11 + pair - pair // 3)

                @pl.when(lax.rem(pair, 3) != 1)
                def _():
                    downs.tick(8 + pair - lax.rem(pair, 3) // 2 - pair // 3)

                return carry

            lax.fori_loop(0, own_width // 128, step, 0)

        pl.run_scoped(
            heads_back, vmem((length, 3 * own_width), bf16), vmem((128, length), f32),
            *[vmem((length, 128), f32)] * 3,
        )

        def projection_grads(normed_t, g_tile):
            fetch((normed_t_h, normed_t))
            cols.tick(15)
            count = 3 * own_width // JOB

            def step(n, carry):
                slot = lax.rem(n, 2)
                g_tile[slot] = dot(normed_t[...], grads[:, lanes(n)]).astype(bf16)

                @pl.when(n >= 1)
                def _():
                    grad_store(g_tile, 1 - slot, g_cols_h, ff_jobs + n - 1, 1).wait()

                grad_store(g_tile, slot, g_cols_h, ff_jobs + n, 1).start()

                @pl.when(n >= 1)
                def _():
                    cols.tick(15 + n)

                @pl.when(n >= 1)
                def _():
                    outs.tick(5 + n)

                return carry

            lax.fori_loop(0, count, step, 0)
            grad_store(g_tile, (count - 1) % 2, g_cols_h, ff_jobs + count - 1, 1).wait()

        pl.run_scoped(projection_grads, vmem((width, length), bf16), vmem((2, width, JOB), bf16))

        cols.tick(24)

        def tokens_back(w_tile, send, total, x_rows, kept):
            def tile_load(n, slot):
                return pltpu.make_async_copy(w_qkv_h.at[sublanes(n, JOB), :], w_tile.at[slot], tile_sem.at[slot, 0])

            tile_load(0, 0).start()
            load(x_h.at[sublanes(me.core, half_rows), :], x_rows, 0).start()
            load(kept_h, kept, 1).start()
            count = width // JOB

            def step(n, carry):
                slot = lax.rem(n, 2)
                tile_load(n, slot).wait()

                @pl.when(n + 1 < count)
                def _():
                    tile_load(n + 1, 1 - slot).start()

                send[:, lanes(n)] = nt(grads[sublanes(1 - me.core, half_rows), :], w_tile[slot]).astype(bf16)
                total[:, lanes(n)] = nt(grads[sublanes(me.core, half_rows), :], w_tile[slot])

                @pl.when((n == 1) | (n == 3))
                def _():
                    cols.tick(25 + n - 1)
                    cols.tick(26 + n - 1)
                    downs.tick(12 + n // 2)

                return carry

            lax.fori_loop(0, count, step, 0)
            pl.semaphore_wait(half_free, 1)
            exchange = remote(send, half_recv, half_sem.at[0, 0], half_sem.at[1, 0], me.over_core, me.z)
            exchange.start()
            cols.tick(29)
            cols.tick(30)
            load(x_h.at[sublanes(me.core, half_rows), :], x_rows, 0).wait()
            load(kept_h, kept, 1).wait()
            exchange.wait()
            gain = gain_ref[0:1, :]

            def rows(k, sums):
                part = sublanes(k, 64)
                grad = total[part, :] + half_recv[part, :].astype(f32)
                gained, values = norm_rows_back(x_rows[part, :].astype(f32), gain, grad)
                send[part, :] = (values + kept[part, :]).astype(bf16)
                return sums + gained

            gain_buffer[0, 0, 0:1, :] = lax.fori_loop(0, half_rows // 64, rows, jnp.zeros((1, width), f32))
            gains.start()
            fetch((send, rows_h.at[1]))

        pl.run_scoped(
            tokens_back, vmem((2, JOB, 3 * own_width), bf16), vmem((half_rows, width), bf16),
            vmem((half_rows, width), f32), vmem((half_rows, width), bf16), vmem((half_rows, width), f32),
        )
        back_tokens.start()

    pl.run_scoped(attention, vmem((length, 3 * own_width), bf16))

    downs.tick(14)
    outs.tick(14)
    downs.tick(15)
    first = 31

    def rest(t, carry):
        cols.tick(t)
        for k in range(GAIN_HOPS - 1):
            @pl.when(t == first + k)
            def _():
                gains.step(k)

        return carry

    lax.fori_loop(first, cols.ticks, rest, 0)
    gains.step(GAIN_HOPS - 1)
    gains.drain()
    back_out.drain()
    back_tokens.drain()


def norm_rows_back(values, gain, grad):
    scale = lax.rsqrt(jnp.mean(values * values, axis=-1, keepdims=True) + EPS)
    unit = values * scale
    inner = grad * gain
    return (
        jnp.sum(grad * unit, axis=0, keepdims=True),
        scale * (inner - unit * jnp.mean(inner * unit, axis=-1, keepdims=True)),
    )


COLUMN_SLOTS = 12


def backward(branch, slopes, hidden, turned, heads, lse, middle, x, g_down, weights, start, gain, cosine, sine):
    length, width = branch.shape
    half, half_ff = width // 2, hidden.shape[1]
    rows = length // 4
    bf16, f32 = jnp.bfloat16, jnp.float32

    def shape(*dims, dtype=bf16):
        return jax.ShapeDtypeStruct(dims, dtype)

    columns = 2 * half_ff + 3 * half
    shapes = [
        shape(2, rows, width),
        shape(2, rows, width),
        shape(width // 8, 2 * columns),
        shape(width // 8, width),
        shape(half_ff // 4, width),
        shape(2, width, dtype=f32),
        shape(width, columns),
        shape(half, width),
        shape(length // 2, width, dtype=f32),
        shape(2, length // 2, width),
        shape(length, width, dtype=f32),
    ]
    dma, vmem = pltpu.SemaphoreType.DMA, pltpu.VMEM
    whole = pl.BlockSpec(memory_space=pltpu.VMEM)
    ring, row = COLUMN_SLOTS, width // 4
    jobs = width // JOB
    row_buffers = []
    for depth in (half_ff // 2, half // 2):
        row_buffers += [
            vmem((jobs, depth, JOB), bf16), vmem((jobs, depth, JOB), bf16), vmem((jobs, 2, depth, JOB), bf16),
            vmem((depth, JOB), bf16), dma((jobs, 3, 4)), dma((jobs, 2, 3)),
        ]
    return pl.pallas_call(
        backward_kernel,
        in_specs=[ANY] * 16 + [whole] * 4,
        out_specs=[ANY] * 5 + [whole] + [ANY] * 5,
        out_shape=shapes,
        scratch_shapes=[
            vmem((ring, 2 * row, JOB), bf16), vmem((ring, 2 * row, JOB), bf16), vmem((ring, row, JOB), bf16),
            vmem((ring, 2, row, JOB), bf16), dma((ring, 3, 4)), dma((ring, 2, 3)),
            pltpu.SemaphoreType.REGULAR((ring,)),
        ]
        + row_buffers
        + [
            vmem((length, width), bf16), vmem((length // 2, width), bf16), pltpu.SemaphoreType.REGULAR,
            dma((2, 3)), dma((2, 1)),
            vmem((GAIN_HOPS, 2, 2, width), f32), dma((2, GAIN_HOPS)), dma((2, 3, 2)), dma((4,)), dma((2, 3)),
            dma((2, 2)),
        ],
        compiler_params=pltpu.CompilerParams(
            collective_id=1, has_side_effects=True, vmem_limit_bytes=63 * 1024 * 1024
        ),
        cost_estimate=pl.CostEstimate(flops=0, bytes_accessed=800_000_000, transcendentals=0),
        name="backward",
    )(
        branch, *slopes, hidden, *turned, heads, lse, middle, x, g_down, *weights, start, gain, cosine, sine
    )


def wide(value):
    return value.astype(jnp.float32)


def dot(a, b):
    return jnp.dot(a, b, preferred_element_type=jnp.float32)


def column_device(
    tokens, segment_ids, out_grad, w_q, w_k, w_v, w_o, w_gate, w_up, w_down, gain_attn, gain_ffn
):
    dp_at = lax.axis_index("dp")
    rows, width = tokens.shape[1], tokens.shape[2]
    length, ff = 4 * rows, w_gate.shape[1]
    gains = lax.dynamic_update_slice_in_dim(
        jnp.zeros((2, width), jnp.bfloat16),
        jnp.stack([gain_attn, gain_ffn]),
        dp_at * gain_attn.shape[0],
        1,
    )
    cosine, sine = rope_tables(jnp.arange(length, dtype=jnp.int32), HD // 2)
    cosine = jnp.concatenate([cosine] * 4, axis=1)
    sine = jnp.concatenate([-sine, sine, -sine, sine], axis=1)
    (
        x_low, docs, grad_branch, gains, full_qkv, full_o, full_ff, full_down, heads, lse, middle,
        slope_gate, slope_up, hidden, g_down, start, gain, normed_t, nf_t, mixed_t,
    ) = gather_all(
        tokens, segment_ids.reshape(2, 1, rows), out_grad, gains, cosine, sine,
        (w_q, w_k, w_v, w_o, w_gate, w_up, w_down),
    )
    result, grad_tokens, g_cols, g_o, g_down, grad_gains = backward(
        grad_branch, (slope_gate, slope_up), hidden, (nf_t, normed_t, mixed_t), heads, lse, middle, x_low, g_down,
        (full_qkv, full_o, full_ff, full_down), start, gain, cosine, sine,
    )[:6]
    grad_gains = lax.dynamic_slice_in_dim(grad_gains, dp_at * (width // 8), width // 8, 1)
    first = 2 * ff
    return (
        result,
        wide(grad_tokens),
        wide(g_cols[:, first : first + width]),
        wide(g_cols[:, first + width : first + 2 * width]),
        wide(g_cols[:, first + 2 * width :]),
        wide(g_o),
        wide(g_cols[:, :ff]),
        wide(g_cols[:, ff:first]),
        wide(g_down),
        grad_gains[0],
        grad_gains[1],
    )


def solution(mesh):
    placed = (
        P(None, ("dp", "seq"), None),
        P(None, ("dp", "seq")),
        P(None, ("dp", "seq"), None),
        P("dp", None),
        P("dp", None),
        P("dp", None),
        P("dp", None),
        P("dp", None),
        P("dp", None),
        P("dp", None),
        P("dp"),
        P("dp"),
    )
    return jax.shard_map(
        column_device if dict(mesh.shape) == FAST_MESH else per_device,
        mesh=mesh,
        in_specs=placed,
        out_specs=(
            P(None, ("dp", "seq"), None),
            P(None, ("dp", "seq"), None),
            P("dp", None),
            P("dp", None),
            P("dp", None),
            P("dp", None),
            P("dp", None),
            P("dp", None),
            P("dp", None),
            P("dp"),
            P("dp"),
        ),
        check_vma=False,
    )
```

```python
import functools
import math

import jax
import jax.numpy as jnp
import numpy as np
from jax import lax
from jax.experimental import pallas as pl
from jax.experimental.pallas import tpu as pltpu
from jax.sharding import PartitionSpec as P

HEADS = 24
HD = 64


EPS = 1e-05


def positions_of(doc_row):
    count = doc_row.shape[0]
    place = jnp.arange(count, dtype=jnp.int32)
    before = jnp.concatenate([doc_row[:1], doc_row[:-1]])
    starts = (place == 0) | (doc_row != before)
    first_place = lax.cummax(jnp.where(starts, place, jnp.zeros_like(place)), axis=0)
    return place - first_place


def rope_tables(where_at, half):
    inverse = jnp.exp(jnp.arange(half, dtype=jnp.float32) * (-math.log(10000.0) / half))
    angle = where_at.astype(jnp.float32)[:, None] * inverse[None, :]
    return (jnp.cos(angle), jnp.sin(angle))


def rotate(values, cosine, sine):
    half = values.shape[-1] // 2
    first, second = (values[..., :half], values[..., half:])
    cos_heads, sin_heads = (cosine[:, None, :], sine[:, None, :])
    return jnp.concatenate(
        [first * cos_heads - second * sin_heads, second * cos_heads + first * sin_heads], axis=-1
    )


def rotate_back(grads, cosine, sine):
    half = grads.shape[-1] // 2
    first, second = (grads[..., :half], grads[..., half:])
    cos_heads, sin_heads = (cosine[:, None, :], sine[:, None, :])
    return jnp.concatenate(
        [first * cos_heads + second * sin_heads, second * cos_heads - first * sin_heads], axis=-1
    )


def rms_norm(values, gain):
    return values * lax.rsqrt(jnp.mean(values * values, axis=-1, keepdims=True) + EPS) * gain


def norm_backward(values, gain, grad_normed):
    scale = lax.rsqrt(jnp.mean(values * values, axis=-1, keepdims=True) + EPS)
    unit = values * scale
    grad_gain = jnp.sum(grad_normed * unit, axis=0)
    inner = grad_normed * gain
    grad_values = scale * (inner - unit * jnp.mean(inner * unit, axis=-1, keepdims=True))
    return (grad_gain, grad_values)


def block_scores(query_heads, key_heads, doc_row, start, block):
    length = doc_row.shape[0]
    place = jnp.arange(length, dtype=jnp.int32)
    query_block = lax.dynamic_slice_in_dim(query_heads, start, block, 0)
    doc_block = lax.dynamic_slice_in_dim(doc_row, start, block, 0)
    rows_block = start + jnp.arange(block, dtype=jnp.int32)
    allowed = (doc_block[:, None] == doc_row[None, :]) & (rows_block[:, None] >= place[None, :])
    scores = (
        jnp.einsum("qhd,khd->hqk", query_block, key_heads, preferred_element_type=jnp.float32)
        * 0.125
    )
    return (query_block, jnp.where(allowed[None], scores, -1e30))


def attention_forward(query, key, value, doc_row):
    length = query.shape[0]
    head_shape = (length, query.shape[1] // HD, HD)
    query_heads, key_heads, value_heads = (
        query.reshape(head_shape),
        key.reshape(head_shape),
        value.reshape(head_shape),
    )
    block = min(512, length)
    starts = jnp.arange(length // block, dtype=jnp.int32) * block

    def one_block(start):
        unused, scores = block_scores(query_heads, key_heads, doc_row, start, block)
        peak = jnp.max(scores, axis=-1, keepdims=True)
        expo = jnp.exp(scores - peak)
        total = jnp.sum(expo, axis=-1, keepdims=True)
        probs_low = (expo / total).astype(jnp.bfloat16)
        mixed = jnp.einsum(
            "hqk,khd->qhd", probs_low, value_heads, preferred_element_type=jnp.float32
        )
        return (mixed.astype(jnp.bfloat16), (peak + jnp.log(total))[..., 0])

    mixed, logsum = lax.map(one_block, starts)
    return (mixed.reshape(length, query.shape[1]), logsum)


def attention_backward(query, key, value, doc_row, logsum, grad_mixed, cosine, sine):
    length = query.shape[0]
    head_shape = (length, query.shape[1] // HD, HD)
    query_heads, key_heads, value_heads = (
        query.reshape(head_shape),
        key.reshape(head_shape),
        value.reshape(head_shape),
    )
    grad_heads = grad_mixed.reshape(head_shape)
    block = min(512, length)
    starts = jnp.arange(length // block, dtype=jnp.int32) * block

    def one_block(carry, item):
        grad_key, grad_value = carry
        start, logsum_block = item
        query_block, scores = block_scores(query_heads, key_heads, doc_row, start, block)
        probs = jnp.exp(scores - logsum_block[..., None])
        probs_low = probs.astype(jnp.bfloat16)
        grad_block = lax.dynamic_slice_in_dim(grad_heads, start, block, 0)
        grad_probs = jnp.einsum(
            "qhd,khd->hqk", grad_block, value_heads, preferred_element_type=jnp.float32
        )
        inner = jnp.sum(probs * grad_probs, axis=-1, keepdims=True)
        grad_scores = (probs * (grad_probs - inner)).astype(jnp.bfloat16)
        grad_query = (
            jnp.einsum("hqk,khd->qhd", grad_scores, key_heads, preferred_element_type=jnp.float32)
            * 0.125
        )
        grad_key = (
            grad_key
            + jnp.einsum(
                "hqk,qhd->khd", grad_scores, query_block, preferred_element_type=jnp.float32
            )
            * 0.125
        )
        grad_value = grad_value + jnp.einsum(
            "hqk,qhd->khd", probs_low, grad_block, preferred_element_type=jnp.float32
        )
        return ((grad_key, grad_value), grad_query)

    zeros_heads = jnp.zeros(head_shape, jnp.float32)
    (grad_key, grad_value), grad_query = lax.scan(
        one_block, (zeros_heads, zeros_heads), (starts, logsum)
    )
    grad_query = rotate_back(grad_query.reshape(head_shape), cosine, sine)
    grad_key = rotate_back(grad_key, cosine, sine)
    width_here = query.shape[1]
    return (
        grad_query.reshape(length, width_here).astype(jnp.bfloat16),
        grad_key.reshape(length, width_here).astype(jnp.bfloat16),
        grad_value.reshape(length, width_here).astype(jnp.bfloat16),
    )


def per_device(
    tokens, segment_ids, out_grad, w_q, w_k, w_v, w_o, w_gate, w_up, w_down, gain_attn, gain_ffn
):
    micro, rows, width = tokens.shape
    offset = lax.axis_index("seq") * rows
    shards = (w_q, w_k, w_v, w_o, w_gate, w_up, w_down, gain_attn, gain_ffn)
    gathered = (
        lax.all_gather(shards[0], "dp", axis=0, tiled=True),
        lax.all_gather(shards[1], "dp", axis=0, tiled=True),
        lax.all_gather(shards[2], "dp", axis=0, tiled=True),
        lax.all_gather(shards[3], "dp", axis=0, tiled=True),
        lax.all_gather(shards[4], "dp", axis=0, tiled=True),
        lax.all_gather(shards[5], "dp", axis=0, tiled=True),
        lax.all_gather(shards[6], "dp", axis=0, tiled=True),
        lax.all_gather(shards[7], "dp", axis=0, tiled=True),
        lax.all_gather(shards[8], "dp", axis=0, tiled=True),
    )
    docs = lax.all_gather(segment_ids, "seq", axis=1, tiled=True)
    full_q, full_k, full_v, full_o, full_gate, full_up, full_down, full_gain_a, full_gain_f = (
        gathered
    )
    gain_a = full_gain_a.astype(jnp.float32)
    gain_f = full_gain_f.astype(jnp.float32)
    row_heads = (rows, HEADS, HD)
    saved = []
    results = []
    for micro_index in range(micro):
        rows_in = tokens[micro_index].astype(jnp.float32)
        doc_row = docs[micro_index]
        cosine, sine = rope_tables(positions_of(doc_row), HD // 2)
        own_cos = lax.dynamic_slice_in_dim(cosine, offset, rows, 0)
        own_sin = lax.dynamic_slice_in_dim(sine, offset, rows, 0)
        normed = rms_norm(rows_in, gain_a).astype(jnp.bfloat16)
        query_rows = jnp.dot(normed, full_q, preferred_element_type=jnp.float32).reshape(row_heads)
        query_rows = rotate(query_rows, own_cos, own_sin).reshape(rows, width).astype(jnp.bfloat16)
        key_rows = jnp.dot(normed, full_k, preferred_element_type=jnp.float32).reshape(row_heads)
        key_rows = rotate(key_rows, own_cos, own_sin).reshape(rows, width).astype(jnp.bfloat16)
        value_rows = jnp.dot(normed, full_v, preferred_element_type=jnp.float32).astype(
            jnp.bfloat16
        )
        query, key, value = (
            lax.all_to_all(query_rows, "seq", split_axis=1, concat_axis=0, tiled=True),
            lax.all_to_all(key_rows, "seq", split_axis=1, concat_axis=0, tiled=True),
            lax.all_to_all(value_rows, "seq", split_axis=1, concat_axis=0, tiled=True),
        )
        mixed, logsum = attention_forward(query, key, value, doc_row)
        mixed_rows = lax.all_to_all(mixed, "seq", split_axis=0, concat_axis=1, tiled=True)
        middle = rows_in + jnp.dot(mixed_rows, full_o, preferred_element_type=jnp.float32)
        normed_ffn = rms_norm(middle, gain_f).astype(jnp.bfloat16)
        gate = jnp.dot(normed_ffn, full_gate, preferred_element_type=jnp.float32)
        up_value = jnp.dot(normed_ffn, full_up, preferred_element_type=jnp.float32)
        hidden = (jax.nn.silu(gate) * up_value).astype(jnp.bfloat16)
        result = middle + jnp.dot(hidden, full_down, preferred_element_type=jnp.float32)
        results.append(result.astype(jnp.bfloat16))
        saved.append(
            (
                rows_in,
                doc_row,
                cosine,
                sine,
                normed,
                query,
                key,
                value,
                logsum,
                mixed_rows,
                middle,
                normed_ffn,
                gate,
                up_value,
                hidden,
            )
        )
    back_weights = (
        lax.all_gather(shards[0], "dp", axis=0, tiled=True),
        lax.all_gather(shards[1], "dp", axis=0, tiled=True),
        lax.all_gather(shards[2], "dp", axis=0, tiled=True),
        lax.all_gather(shards[3], "dp", axis=0, tiled=True),
        lax.all_gather(shards[4], "dp", axis=0, tiled=True),
        lax.all_gather(shards[5], "dp", axis=0, tiled=True),
        lax.all_gather(shards[6], "dp", axis=0, tiled=True),
        lax.all_gather(shards[7], "dp", axis=0, tiled=True),
        lax.all_gather(shards[8], "dp", axis=0, tiled=True),
    )
    back_q, back_k, back_v, back_o, back_gate, back_up, back_down, back_gain_a, back_gain_f = (
        back_weights
    )
    gain_back_a = back_gain_a.astype(jnp.float32)
    gain_back_f = back_gain_f.astype(jnp.float32)
    totals = [jnp.zeros(weight.shape, jnp.float32) for weight in back_weights]
    grad_inputs = []
    for micro_index in range(micro):
        (
            rows_in,
            doc_row,
            cosine,
            sine,
            normed,
            query,
            key,
            value,
            logsum,
            mixed_rows,
            middle,
            normed_ffn,
            gate,
            up_value,
            hidden,
        ) = saved[micro_index]
        grad_out = out_grad[micro_index].astype(jnp.float32)
        grad_branch = grad_out.astype(jnp.bfloat16)
        totals[6] = totals[6] + jnp.einsum(
            "tf,td->fd", hidden, grad_branch, preferred_element_type=jnp.float32
        )
        grad_hidden = jnp.einsum(
            "td,fd->tf", grad_branch, back_down, preferred_element_type=jnp.float32
        )
        sigma = jax.nn.sigmoid(gate)
        grad_gate = (grad_hidden * up_value * sigma * (1.0 + gate * (1.0 - sigma))).astype(
            jnp.bfloat16
        )
        grad_up = (grad_hidden * jax.nn.silu(gate)).astype(jnp.bfloat16)
        totals[4] = totals[4] + jnp.einsum(
            "td,tf->df", normed_ffn, grad_gate, preferred_element_type=jnp.float32
        )
        totals[5] = totals[5] + jnp.einsum(
            "td,tf->df", normed_ffn, grad_up, preferred_element_type=jnp.float32
        )
        grad_normed_ffn = jnp.einsum(
            "tf,df->td", grad_gate, back_gate, preferred_element_type=jnp.float32
        )
        grad_normed_ffn = grad_normed_ffn + jnp.einsum(
            "tf,df->td", grad_up, back_up, preferred_element_type=jnp.float32
        )
        grad_gain_f, grad_middle = norm_backward(middle, gain_back_f, grad_normed_ffn)
        totals[8] = totals[8] + grad_gain_f
        grad_middle = grad_middle + grad_out
        grad_attn = grad_middle.astype(jnp.bfloat16)
        totals[3] = totals[3] + jnp.einsum(
            "ti,td->id", mixed_rows, grad_attn, preferred_element_type=jnp.float32
        )
        grad_mixed_rows = jnp.einsum(
            "td,id->ti", grad_attn, back_o, preferred_element_type=jnp.float32
        ).astype(jnp.bfloat16)
        grad_mixed = lax.all_to_all(grad_mixed_rows, "seq", split_axis=1, concat_axis=0, tiled=True)
        grad_query, grad_key, grad_value = attention_backward(
            query, key, value, doc_row, logsum, grad_mixed, cosine, sine
        )
        query_back, key_back, value_back = (
            lax.all_to_all(grad_query, "seq", split_axis=0, concat_axis=1, tiled=True),
            lax.all_to_all(grad_key, "seq", split_axis=0, concat_axis=1, tiled=True),
            lax.all_to_all(grad_value, "seq", split_axis=0, concat_axis=1, tiled=True),
        )
        totals[0] = totals[0] + jnp.einsum(
            "td,te->de", normed, query_back, preferred_element_type=jnp.float32
        )
        totals[1] = totals[1] + jnp.einsum(
            "td,te->de", normed, key_back, preferred_element_type=jnp.float32
        )
        totals[2] = totals[2] + jnp.einsum(
            "td,te->de", normed, value_back, preferred_element_type=jnp.float32
        )
        grad_normed = jnp.einsum(
            "te,de->td", query_back, back_q, preferred_element_type=jnp.float32
        )
        grad_normed = grad_normed + jnp.einsum(
            "te,de->td", key_back, back_k, preferred_element_type=jnp.float32
        )
        grad_normed = grad_normed + jnp.einsum(
            "te,de->td", value_back, back_v, preferred_element_type=jnp.float32
        )
        grad_gain_a, grad_rows = norm_backward(rows_in, gain_back_a, grad_normed)
        totals[7] = totals[7] + grad_gain_a
        grad_inputs.append(grad_rows + grad_middle)
    summed_all = (
        totals[0],
        totals[1],
        totals[2],
        totals[3],
        totals[4],
        totals[5],
        totals[6],
        totals[7],
        totals[8],
    )
    pieces = (
        lax.psum_scatter(
            summed_all[0].astype(jnp.bfloat16), "dp", scatter_dimension=0, tiled=True
        ).astype(jnp.float32),
        lax.psum_scatter(
            summed_all[1].astype(jnp.bfloat16), "dp", scatter_dimension=0, tiled=True
        ).astype(jnp.float32),
        lax.psum_scatter(
            summed_all[2].astype(jnp.bfloat16), "dp", scatter_dimension=0, tiled=True
        ).astype(jnp.float32),
        lax.psum_scatter(
            summed_all[3].astype(jnp.bfloat16), "dp", scatter_dimension=0, tiled=True
        ).astype(jnp.float32),
        lax.psum_scatter(
            summed_all[4].astype(jnp.bfloat16), "dp", scatter_dimension=0, tiled=True
        ).astype(jnp.float32),
        lax.psum_scatter(
            summed_all[5].astype(jnp.bfloat16), "dp", scatter_dimension=0, tiled=True
        ).astype(jnp.float32),
        lax.psum_scatter(
            summed_all[6].astype(jnp.bfloat16), "dp", scatter_dimension=0, tiled=True
        ).astype(jnp.float32),
        lax.psum_scatter(
            summed_all[7].astype(jnp.bfloat16), "dp", scatter_dimension=0, tiled=True
        ).astype(jnp.float32),
        lax.psum_scatter(
            summed_all[8].astype(jnp.bfloat16), "dp", scatter_dimension=0, tiled=True
        ).astype(jnp.float32),
    )
    pieces = (
        lax.psum(pieces[0].astype(jnp.bfloat16), "seq").astype(jnp.float32),
        lax.psum(pieces[1].astype(jnp.bfloat16), "seq").astype(jnp.float32),
        lax.psum(pieces[2].astype(jnp.bfloat16), "seq").astype(jnp.float32),
        lax.psum(pieces[3].astype(jnp.bfloat16), "seq").astype(jnp.float32),
        lax.psum(pieces[4].astype(jnp.bfloat16), "seq").astype(jnp.float32),
        lax.psum(pieces[5].astype(jnp.bfloat16), "seq").astype(jnp.float32),
        lax.psum(pieces[6].astype(jnp.bfloat16), "seq").astype(jnp.float32),
        lax.psum(pieces[7].astype(jnp.bfloat16), "seq").astype(jnp.float32),
        lax.psum(pieces[8].astype(jnp.bfloat16), "seq").astype(jnp.float32),
    )
    return (
        jnp.stack(results),
        jnp.stack(grad_inputs),
        pieces[0],
        pieces[1],
        pieces[2],
        pieces[3],
        pieces[4],
        pieces[5],
        pieces[6],
        pieces[7],
        pieces[8],
    )


BLK = 256
LOG2E = 1.4426950408889634


def swap_halves(v):
    lane = lax.broadcasted_iota(jnp.int32, v.shape, 1)
    width = v.shape[1]
    up = pltpu.roll(v, width - 32, axis=1)
    down = pltpu.roll(v, 32, axis=1)
    return jnp.where(lane % 64 < 32, up, down)


def nt(a, b):
    return lax.dot_general(a, b, (((1,), (1,)), ((), ())), preferred_element_type=jnp.float32)


def tn(a, b):
    return lax.dot_general(a, b, (((0,), (0,)), ((), ())), preferred_element_type=jnp.float32)


FAST_MESH = {"dp": 8, "seq": 4}
ANY = pl.BlockSpec(memory_space=pl.ANY)


class Place:
    def __init__(self):
        self.dp, self.z = lax.axis_index("dp"), lax.axis_index("seq")
        self.core = self.dp % 2
        self.x = (self.dp // 2) % 2
        self.y = self.dp // 4
        self.over_core = self.dp + 1 - 2 * self.core
        self.over_x = self.dp + 2 - 4 * self.x
        self.over_y = self.dp + 4 - 8 * self.y
        self.middle = (self.z == 1) | (self.z == 2)


def enter(devices):
    barrier = pltpu.get_barrier_semaphore()
    for dp, seq in devices:
        pl.semaphore_signal(
            barrier, inc=1, device_id={"dp": dp, "seq": seq}, device_id_type=pl.DeviceIdType.MESH
        )
    pl.semaphore_wait(barrier, len(devices))


def remote(src, dst, send_sem, recv_sem, dp, seq):
    return pltpu.make_async_remote_copy(
        src_ref=src,
        dst_ref=dst,
        send_sem=send_sem,
        recv_sem=recv_sem,
        device_id={"dp": dp, "seq": seq},
        device_id_type=pl.DeviceIdType.MESH,
    )


def gather_kernel(
    tokens, segments, out_grad, gains, cosine, sine, w_q, w_k, w_v, w_o, w_gate, w_up, w_down,
    x_out, seg_out, g_out, gains_out, qkv_out, o_out, ff_out, down_out,
    heads_out, lse_out, middle_out, slope_gate_out, slope_up_out, hidden_out, g_down_out, start_out,
    gain_out, normed_t_out, nf_t_out, mixed_t_out,
    send, recv, local, row_send, row_recv, row_local, gain_send, gain_recv,
    x_v, seg_v, gains_v, normed_v, w_qkv_v, heads_v, mixed_v, w_o_v, middle_v, part_send, part_recv,
    nf_v, w_ff_v, branch_v, tile_v, g_tile_v, lse_v, start_v, lse_t_v, start_row_v, gain_v, turned_v, mixed_t_v,
    part_sem, load_sem, w_sem, tile_sem, store_sem,
):
    me = Place()
    rows = tokens.shape[1]
    plane = [(lax.rem(me.dp + k, 8), me.z) for k in range(1, 8)]
    column = [
        (me.dp - me.core + core, lax.rem(me.z + k, 4)) for k in range(1, 4) for core in range(2)
    ]
    enter(plane + column)
    started = []

    def begin(copy):
        copy.start()
        started.append(copy)

    streams = ((tokens, x_out), (segments, seg_out), (out_grad, g_out))

    def place_of(ref, seq):
        return ref.at[pl.ds(rows * seq, rows)] if ref.shape[0] == 4 * rows else ref.at[seq]

    def row_copies(index):
        source, target = streams[index]
        for m in range(2):
            core, seq = me.z // 2, 2 * m + me.core
            here = (core == me.core) & (seq == me.z)

            @pl.when(here)
            def _():
                pltpu.make_async_copy(
                    source.at[m], place_of(target, me.z), row_local.at[index]
                ).start()

            @pl.when(jnp.logical_not(here))
            def _():
                remote(
                    source.at[m], place_of(target, me.z), row_send.at[index, m],
                    row_recv.at[index, me.z % 2], me.dp - me.core + core, seq,
                ).start()

    def row_wait_send(index):
        source, target = streams[index]
        for m in range(2):
            core, seq = me.z // 2, 2 * m + me.core
            here = (core == me.core) & (seq == me.z)

            @pl.when(jnp.logical_not(here))
            def _():
                remote(
                    source.at[m], place_of(target, me.z), row_send.at[index, m],
                    row_recv.at[index, me.z % 2], me.dp - me.core + core, seq,
                ).wait_send()

    def row_relay(index):
        source, target = streams[index]
        for slot in range(2):
            seq = 2 * me.core + slot
            block = place_of(target, seq)
            here = (seq == me.z) & (me.z % 2 == me.core)

            @pl.when(here)
            def _():
                pltpu.make_async_copy(block, block, row_local.at[index]).wait()

            @pl.when(jnp.logical_not(here))
            def _():
                remote(
                    block, block, row_send.at[index, slot], row_recv.at[index, slot], me.over_core, me.z
                ).wait_recv()

            begin(
                remote(
                    block, block, row_send.at[index, 2 + slot], row_recv.at[index, 2 + slot],
                    me.over_core, me.z,
                )
            )

    def row_finish(index):
        source, target = streams[index]
        for slot in range(2):
            block = place_of(target, 2 * (1 - me.core) + slot)
            remote(
                block, block, row_send.at[index, 2 + slot], row_recv.at[index, 2 + slot], me.over_core, me.z
            ).wait_recv()

    by_columns = []
    base = 0
    for source in (w_q, w_k, w_v):
        by_columns.append((source, qkv_out, base))
        base += source.shape[1] // 2
    by_columns.append((w_gate, ff_out, 0))
    by_columns.append((w_up, ff_out, w_gate.shape[1] // 2))
    by_rows = [(w_o, o_out), (w_down, down_out)]

    def column_piece(index, owner):
        source, target, first = by_columns[index]
        depth, width = source.shape[0], source.shape[1] // 2
        return target.at[pl.ds(depth * owner, depth), pl.ds(first, width)]

    def columns_start(index):
        source, target, first = by_columns[index]
        width = source.shape[1] // 2
        mine = column_piece(index, me.dp)
        for core in range(2):
            half = source.at[:, pl.ds(width * core, width)]
            begin(remote(half, mine, send.at[index, core], recv.at[index, me.core],
                         me.over_x - me.core + core, me.z))
            begin(remote(half, mine, send.at[index, 2 + core], recv.at[index, 2 + me.core],
                         me.over_y - me.core + core, me.z))

            @pl.when(core == me.core)
            def _():
                pltpu.make_async_copy(half, mine, local.at[index]).start()

            @pl.when(core != me.core)
            def _():
                remote(half, mine, send.at[index, 4], recv.at[index, 4], me.over_core, me.z).start()

    beside = me.z + 1 - 2 * lax.rem(me.z, 2)
    corner = me.over_x + me.over_y - me.dp - me.core

    def turn_of(index):
        return lax.rem(index + me.z, 2)

    last = 6

    def hand_on(index, piece, came, slot, send_slot, dp, seq):
        remote(piece, piece, send.at[index, send_slot], recv.at[index, came], dp, seq).wait_recv()
        remote(piece, piece, send.at[index, send_slot], recv.at[index, slot], dp, seq).start()

    def arrived(index, piece, slot):
        remote(piece, piece, send.at[index, 5], recv.at[index, slot], me.over_core, me.z).wait_recv()

    def left(index, piece, slot):
        remote(piece, piece, send.at[index, slot], recv.at[index, 5], me.over_core, me.z).wait_send()

    def columns_relay(index):
        @pl.when(turn_of(index) == 0)
        def _():
            hand_on(index, column_piece(index, me.over_x - me.core), 0, 5, 5, me.over_y, me.z)

        @pl.when(turn_of(index) == 1)
        def _():
            hand_on(index, column_piece(index, me.over_y - me.core + 1), 3, 6, 6, me.over_x, me.z)

    def columns_forward(index):
        @pl.when(turn_of(index) == 0)
        def _():
            hand_on(index, column_piece(index, corner), 5, 5, 6, me.dp, beside)

        @pl.when(turn_of(index) == 1)
        def _():
            hand_on(index, column_piece(index, corner + 1), 6, 6, 5, me.dp, beside)

    def columns_finish(index):
        source, target, first = by_columns[index]
        width = source.shape[1] // 2
        arrived(index, column_piece(index, me.over_x - me.core + 1), 1)
        arrived(index, column_piece(index, me.over_y - me.core), 2)
        arrived(index, column_piece(index, me.over_core), 4)

        @pl.when(turn_of(index) == 0)
        def _():
            arrived(index, column_piece(index, me.over_y - me.core + 1), 3)
            arrived(index, column_piece(index, corner + 1), 6)

        @pl.when(turn_of(index) == 1)
        def _():
            arrived(index, column_piece(index, me.over_x - me.core), 0)
            arrived(index, column_piece(index, corner), 5)

        mine = column_piece(index, me.dp)
        pltpu.make_async_copy(mine, mine, local.at[index]).wait()
        for slot in (4, 5, 6):
            left(index, mine, slot)

    def row_piece(which, owner):
        source, target = by_rows[which]
        depth = source.shape[0]
        return target.at[pl.ds(depth * lax.rem(owner, 4), depth), :]

    def rows_start(which):
        source, target = by_rows[which]
        index = 5 + which
        mine = row_piece(which, me.dp)
        begin(remote(source, mine, send.at[index, 0], recv.at[index, me.core],
                     me.over_x - me.core + me.y, me.z))
        begin(remote(source, mine, send.at[index, 1], recv.at[index, 2 + me.core],
                     me.over_y - me.core + me.y, me.z))

        @pl.when(me.core == me.y)
        def _():
            pltpu.make_async_copy(source, mine, local.at[index]).start()

        @pl.when(me.core != me.y)
        def _():
            remote(source, mine, send.at[index, 4], recv.at[index, 4], me.over_core, me.z).start()

    def rows_relay(which):
        index = 5 + which

        @pl.when((me.core == me.y) & ((index == last) | (turn_of(index) == 0)))
        def _():
            hand_on(index, row_piece(which, me.over_x - me.core), 0, 5, 5, me.over_y, me.z)

        @pl.when((me.core != me.y) & ((index == last) | (turn_of(index) == 1)))
        def _():
            hand_on(index, row_piece(which, me.over_y - me.core + 1), 3, 6, 6, me.over_x, me.z)

    def rows_forward(which):
        index = 5 + which

        @pl.when((me.core != me.y) & (turn_of(index) == 0))
        def _():
            hand_on(index, row_piece(which, corner), 5, 5, 6, me.dp, beside)

        @pl.when((me.core != me.y) & (turn_of(index) == 1))
        def _():
            hand_on(index, row_piece(which, corner + 1), 6, 6, 5, me.dp, beside)

    def rows_finish(which):
        source, target = by_rows[which]
        index = 5 + which
        mine = row_piece(which, me.dp)

        @pl.when(me.core == me.y)
        def _():
            arrived(index, row_piece(which, me.over_x - me.core + 1), 1)
            arrived(index, row_piece(which, me.over_core), 4)
            pltpu.make_async_copy(source, mine, local.at[index]).wait()

            @pl.when((index == last) | (turn_of(index) == 0))
            def _():
                left(index, mine, 5)

            @pl.when((index != last) & (turn_of(index) == 1))
            def _():
                arrived(index, row_piece(which, me.over_x - me.core), 0)

        @pl.when(me.core != me.y)
        def _():
            arrived(index, row_piece(which, me.over_y - me.core), 2)
            left(index, mine, 4)
            left(index, mine, 6)

            @pl.when((index != last) & (turn_of(index) == 0))
            def _():
                arrived(index, row_piece(which, me.over_y - me.core + 1), 3)
                arrived(index, row_piece(which, corner + 1), 6)

            @pl.when((index == last) | (turn_of(index) == 1))
            def _():
                arrived(index, row_piece(which, corner), 5)

            @pl.when(index == last)
            def _():
                arrived(index, row_piece(which, corner + 1), 6)

            @pl.when((index != last) & (turn_of(index) == 1))
            def _():
                left(index, mine, 5)

    def load(source, target, k):
        return pltpu.make_async_copy(source, target, load_sem.at[k])

    stores = []

    def store(source, target):
        copy = pltpu.make_async_copy(source, target, store_sem.at[len(stores)])
        stores.append(copy)
        copy.start()
        return copy

    length, width = x_v.shape
    own_width = width // 2
    half_ff = ff_out.shape[1] // 2

    row_copies(0)
    row_copies(1)
    for index in range(3):
        columns_start(index)
    for k in range(1, 8):
        begin(remote(gains, gains_out.at[me.dp], gain_send.at[k - 1], gain_recv.at[k - 1],
                     lax.rem(me.dp + k, 8), me.z))
    pltpu.make_async_copy(gains, gains_out.at[me.dp], gain_recv.at[7]).start()
    for index in range(3):
        columns_relay(index)
    rows_start(0)
    columns_start(3)
    row_relay(0)
    row_relay(1)
    for k in range(1, 8):
        piece = gains_out.at[lax.rem(me.dp + 8 - k, 8)]
        remote(piece, piece, gain_send.at[k - 1], gain_recv.at[k - 1], me.over_core, me.z).wait_recv()
    pltpu.make_async_copy(gains, gains_out.at[me.dp], gain_recv.at[7]).wait()
    load(gains_out, gains_v, 0).start()
    row_finish(1)
    load(seg_out, seg_v, 1).start()
    row_finish(0)
    load(x_out, x_v, 2).start()
    load(gains_out, gains_v, 0).wait()
    load(seg_out, seg_v, 1).wait()
    load(x_out, x_v, 2).wait()
    both_gains = gains_v[0].astype(jnp.float32)
    for k in range(1, 8):
        both_gains = both_gains + gains_v[k].astype(jnp.float32)
    gain_a, gain_f = both_gains[0:1], both_gains[1:2]
    gain_v[...] = both_gains
    store(gain_v, gain_out)

    norm_rows(lambda part: x_v[part, :].astype(jnp.float32), gain_a, normed_v, length)

    docs = jnp.concatenate([seg_v[k] for k in range(4)], axis=1)
    start_row = jnp.zeros((1, length), jnp.int32)
    for k in range(4):
        square = lax.broadcasted_iota(jnp.int32, (rows, rows), 0) == lax.broadcasted_iota(
            jnp.int32, (rows, rows), 1
        )
        ids = jnp.sum(jnp.where(square, seg_v[k], 0), axis=1, keepdims=True)
        start_v[pl.ds(rows * k, rows), :] = jnp.sum(
            jnp.where(docs < ids, 1, 0), axis=1, keepdims=True
        )
        start_row = start_row + jnp.sum(jnp.where(ids < docs, 1, 0), axis=0, keepdims=True)
    start_row_v[...] = start_row
    store(start_row_v, start_out)
    turn(normed_v, turned_v)
    normed_store = store(turned_v, normed_t_out)

    for index in range(3):
        columns_forward(index)
    rows_relay(0)
    columns_start(4)
    for index in range(3):
        columns_finish(index)
    tile = 256
    tiles = own_width // tile
    for t in range(tiles):
        for kind in range(3):
            part = pl.ds(own_width * kind + tile * t, tile)
            pltpu.make_async_copy(qkv_out.at[:, part], w_qkv_v.at[:, part], w_sem.at[kind, t]).start()
    for t in range(tiles):
        for kind in range(3):
            part = pl.ds(own_width * kind + tile * t, tile)
            pltpu.make_async_copy(qkv_out.at[:, part], w_qkv_v.at[:, part], w_sem.at[kind, t]).wait()
            product = jnp.dot(normed_v[...], w_qkv_v[:, part], preferred_element_type=jnp.float32)
            for k in range(tile // 128):
                piece = product[:, 128 * k : 128 * k + 128]
                if kind < 2:
                    piece = piece * cosine[...] + swap_halves(piece) * sine[...]
                heads_v[:, pl.ds(own_width * kind + tile * t + 128 * k, 128)] = piece.astype(jnp.bfloat16)

        def pair_step(pair, carry):
            attend(pair, own_width, heads_v, start_v, mixed_v, lse_v)
            return carry

        lax.fori_loop(tile // 128 * t, tile // 128 * (t + 1), pair_step, 0)
        if t == 0:
            row_copies(2)
        if t == 1:
            rows_forward(0)
            columns_relay(3)
    store(heads_v, heads_out)
    lse_t_v[...] = lse_v[...].T
    store(lse_t_v, lse_out)
    turn(mixed_v, mixed_t_v)
    store(mixed_t_v, mixed_t_out)

    rows_finish(0)
    load(o_out, w_o_v, 0).start()
    load(o_out, w_o_v, 0).wait()
    chunk = width // 3

    def part_copy(k):
        part = pl.ds(chunk * k, chunk)
        return remote(
            part_send.at[:, part], part_recv.at[:, part], part_sem.at[0, k], part_sem.at[1, k], me.over_core, me.z
        )

    for k in range(3):
        for at in range(chunk * k, chunk * (k + 1), tile):
            part = pl.ds(at, tile)
            product = jnp.dot(mixed_v[...], w_o_v[:, part], preferred_element_type=jnp.float32)
            part_send[:, part] = product.astype(jnp.bfloat16)
            middle_v[:, part] = x_v[:, part].astype(jnp.float32) + product
        part_copy(k).start()
    row_relay(2)
    columns_relay(4)
    rows_start(1)
    row_finish(2)
    load(g_out, branch_v, 1).start()
    for k in range(3):
        part_copy(k).wait_recv()

    def middle_rows(part):
        value = middle_v[part, :] + part_recv[part, :].astype(jnp.float32)
        middle_v[part, :] = value
        return value

    norm_rows(middle_rows, gain_f, nf_v, length)
    store(middle_v, middle_out)
    normed_store.wait()
    turn(nf_v, turned_v)
    store(turned_v, nf_t_out)
    load(g_out, branch_v, 1).wait()
    columns_forward(3)
    columns_forward(4)
    columns_finish(3)
    columns_finish(4)

    def ff_load(n, slot, kind):
        first = pl.multiple_of(half_ff * kind + tile * n, 128)
        return pltpu.make_async_copy(
            ff_out.at[:, pl.ds(first, tile)], w_ff_v.at[slot, kind], tile_sem.at[0, slot, kind]
        )

    def tile_store(n, slot, kind):
        part = pl.ds(pl.multiple_of(tile * n, 128), tile)
        target = (slope_gate_out, slope_up_out, hidden_out)[kind]
        return pltpu.make_async_copy(tile_v.at[slot, kind], target.at[:, part], tile_sem.at[1, slot, kind])

    def grad_store(n, slot):
        part = pl.ds(pl.multiple_of(tile * n, tile), tile)
        return pltpu.make_async_copy(g_tile_v.at[slot], g_down_out.at[part, :], tile_sem.at[2, slot, 0])

    count = half_ff // tile
    for kind in range(2):
        ff_load(0, 0, kind).start()

    def ff_step(n, carry):
        slot = lax.rem(n, 2)
        for kind in range(2):
            ff_load(n, slot, kind).wait()

        @pl.when(n + 1 < count)
        def _():
            for kind in range(2):
                ff_load(n + 1, 1 - slot, kind).start()

        @pl.when(n >= 2)
        def _():
            for kind in range(3):
                tile_store(n - 2, slot, kind).wait()
            grad_store(n - 2, slot).wait()

        gate = jnp.dot(nf_v[...], w_ff_v[slot, 0], preferred_element_type=jnp.float32)
        up_value = jnp.dot(nf_v[...], w_ff_v[slot, 1], preferred_element_type=jnp.float32)
        sigma = jax.nn.sigmoid(gate)
        silu = gate * sigma
        tile_v[slot, 0] = (up_value * sigma * (1.0 + gate * (1.0 - sigma))).astype(jnp.bfloat16)
        tile_v[slot, 1] = silu.astype(jnp.bfloat16)
        hidden = (silu * up_value).astype(jnp.bfloat16)
        tile_v[slot, 2] = hidden
        g_tile_v[slot] = jnp.dot(
            hidden.T, branch_v[...], preferred_element_type=jnp.float32
        ).astype(jnp.bfloat16)
        for kind in range(3):
            tile_store(n, slot, kind).start()
        grad_store(n, slot).start()

        @pl.when(n == 1)
        def _():
            rows_relay(1)

        return carry

    lax.fori_loop(0, count, ff_step, 0)
    for n in range(count - 2, count):
        for kind in range(3):
            tile_store(n, n % 2, kind).wait()
        grad_store(n, n % 2).wait()
    rows_finish(1)
    for copy in stores:
        if copy is not normed_store:
            copy.wait()
    for k in range(3):
        part_copy(k).wait_send()
    for index in range(3):
        row_wait_send(index)
    for copy in started:
        copy.wait_send()


def turn(source, target):
    for k in range(source.shape[1] // 256):
        target[256 * k : 256 * (k + 1), :] = source[:, 256 * k : 256 * (k + 1)].T


def norm_rows(read, gain, target, length, step=64):
    def chunk(k, carry):
        part = pl.ds(pl.multiple_of(k * step, step), step)
        values = read(part)
        scale = lax.rsqrt(jnp.mean(values * values, axis=-1, keepdims=True) + EPS)
        target[part, :] = (values * scale * gain).astype(target.dtype)
        return carry

    lax.fori_loop(0, length // step, chunk, 0)


def attend(pair, width, heads, start, mixed, lse):
    length = heads.shape[0]
    lane = lax.broadcasted_iota(jnp.int32, (BLK, 128), 1)
    cols = [pl.ds(pl.multiple_of(width * kind + 128 * pair, 128), 128) for kind in range(3)]
    for i in range(length // BLK):
        own_rows, keys = slice(BLK * i, BLK * (i + 1)), BLK * (i + 1)
        place = lax.broadcasted_iota(jnp.int32, (BLK, keys), 1)
        own = BLK * i + lax.broadcasted_iota(jnp.int32, (BLK, keys), 0)
        allowed = (place >= start[own_rows, :]) & (place <= own)
        query = heads[own_rows, cols[0]] * jnp.bfloat16(0.125)
        key, value = heads[0:keys, cols[1]], heads[0:keys, cols[2]]
        kept = lse[own_rows, :]
        outs = []
        for half in range(2):
            part = slice(64 * half, 64 * half + 64)
            scores = jnp.where(allowed, nt(query[:, part], key[:, part]), -1e30)
            peak = jnp.max(scores, axis=-1, keepdims=True)
            expo = jnp.exp(scores - peak)
            total = jnp.sum(expo, axis=-1, keepdims=True)
            out = jnp.dot(expo.astype(jnp.bfloat16), value[:, part], preferred_element_type=jnp.float32)
            outs.append((out / total).astype(jnp.bfloat16))
            kept = jnp.where(lane == 2 * pair + half, peak + jnp.log(total), kept)
        mixed[own_rows, cols[0]] = jnp.concatenate(outs, axis=1)
        lse[own_rows, :] = kept


def gather_all(tokens, segments, out_grad, gains, cosine, sine, weights):
    rows, width = tokens.shape[1], tokens.shape[2]
    length, half, ff = 4 * rows, width // 2, weights[4].shape[1]
    half_ff = ff // 2
    low = jnp.bfloat16

    def shape(*dims, dtype=low):
        return jax.ShapeDtypeStruct(dims, dtype)

    shapes = [
        shape(length, width),
        shape(4, *segments.shape[1:], dtype=jnp.int32),
        shape(length, width),
        shape(8, *gains.shape),
        shape(width, 3 * half),
        shape(half, width),
        shape(width, ff),
        shape(half_ff, width),
        shape(length, 3 * half),
        shape(128, length, dtype=jnp.float32),
        shape(length, width, dtype=jnp.float32),
        shape(length, half_ff),
        shape(length, half_ff),
        shape(length, half_ff),
        shape(half_ff, width),
        shape(1, length, dtype=jnp.int32),
        shape(2, width, dtype=jnp.float32),
        shape(width, length),
        shape(width, length),
        shape(half, length),
    ]
    dma, vmem = pltpu.SemaphoreType.DMA, pltpu.VMEM
    whole = pl.BlockSpec(memory_space=pltpu.VMEM)
    return pl.pallas_call(
        gather_kernel,
        in_specs=[ANY] * 4 + [whole] * 2 + [ANY] * 7,
        out_specs=[ANY] * len(shapes),
        out_shape=shapes,
        scratch_shapes=[
            dma((7, 7)), dma((7, 7)), dma((7,)), dma((3, 4)), dma((3, 4)), dma((3,)), dma((7,)), dma((8,)),
            vmem((length, width), low),
            vmem((4,) + segments.shape[1:], jnp.int32),
            vmem((8,) + gains.shape, low),
            vmem((length, width), low),
            vmem((width, 3 * half), low),
            vmem((length, 3 * half), low),
            vmem((length, half), low),
            vmem((half, width), low),
            vmem((length, width), jnp.float32),
            vmem((length, width), low),
            vmem((length, width), low),
            vmem((length, width), low),
            vmem((2, 2, width, 256), low),
            vmem((length, width), low),
            vmem((2, 3, length, 256), low),
            vmem((2, 256, width), low),
            vmem((length, 128), jnp.float32),
            vmem((length, 1), jnp.int32),
            vmem((128, length), jnp.float32),
            vmem((1, length), jnp.int32),
            vmem((2, width), jnp.float32),
            vmem((width, length), low),
            vmem((half, length), low),
            dma((2, 3)), dma((3,)), dma((3, 3)), dma((3, 2, 3)), dma((9,)),
        ],
        compiler_params=pltpu.CompilerParams(
            collective_id=0, has_side_effects=True, vmem_limit_bytes=61 * 1024 * 1024
        ),
        cost_estimate=pl.CostEstimate(flops=0, bytes_accessed=500_000_000, transcendentals=0),
        name="gather_all",
    )(tokens, segments, out_grad, gains, cosine, sine, *weights)


def guard(condition, action):
    if isinstance(condition, (bool, np.bool_)):
        if condition:
            action()
    else:
        pl.when(condition)(action)


def everything(*conditions):
    known = [c for c in conditions if isinstance(c, (bool, np.bool_))]
    if not all(known):
        return False
    rest = [c for c in conditions if not isinstance(c, (bool, np.bool_))]
    if not rest:
        return True
    total = rest[0]
    for c in rest[1:]:
        total = total & c
    return total


def chunk_of(rows):
    return 384 if rows % 384 == 0 else 512


def add_rows(target, first, other, rows):
    step = chunk_of(rows)

    def chunk(k, carry):
        at = pl.multiple_of(k * step, step)
        source = pl.multiple_of(first + k * step, step)
        target[pl.ds(at, step), :] += other[pl.ds(source, step), :]
        return carry

    lax.fori_loop(0, rows // step, chunk, 0)


JOB = 256


class Stream:
    active = True

    def tick(self, t):
        for late, stage in reversed(self.stages):
            k = t - late
            guard(everything(k >= 0, k < self.count), functools.partial(stage, k))

    @property
    def ticks(self):
        return self.count + self.stages[-1][0]

    def slot(self, k):
        return k % self.slots if isinstance(k, int) else lax.rem(k, self.slots)

    def column(self, k, base=0):
        return pl.ds(pl.multiple_of(base + JOB * k, 128), JOB)

    def total(self, k):
        return self.second.at[self.slot(k)]

    def final(self, k):
        return self.got.at[self.slot(k), pl.ds(0, self.rows)]

    def seq_copy(self, k, step):
        me, slot, sem = self.me, self.slot(k), self.seq_sem
        inner = me.z + 1 - 2 * (me.z // 2)
        opposite = 3 - me.z
        outer = 3 * (me.z // 2)
        if step == 0:
            return remote(self.total(k), self.over.at[slot, 0], sem.at[slot, 0, 0], sem.at[slot, 1, 0], me.dp, inner)
        if step == 1:
            return remote(
                self.total(k), self.over.at[slot, 1], sem.at[slot, 0, 1], sem.at[slot, 1, 1], me.dp, opposite
            )
        return remote(self.final(k), self.final(k), sem.at[slot, 0, 2], sem.at[slot, 1, 2], me.dp, outer)

    def plane_and_ends(self, k):
        self.reduce_plane(k)
        guard(
            everything(self.active, jnp.logical_not(self.me.middle)),
            lambda: self.seq_copy(k, 0).start(),
        )

    def across(self, k):
        def action():
            self.seq_copy(k, 0).wait_recv()
            add_rows(self.total(k), 0, self.over.at[self.slot(k), 0], self.rows)
            self.seq_copy(k, 1).start()

        guard(everything(self.active, self.me.middle), action)

    def back(self, k):
        def action():
            self.seq_copy(k, 1).wait_recv()
            final, total, over = self.final(k), self.total(k), self.over.at[self.slot(k), 1]
            step = chunk_of(self.rows)

            def chunk(at, carry):
                part = pl.ds(pl.multiple_of(at * step, step), step)
                final[part, :] = total[part, :] + over[part, :]
                return carry

            lax.fori_loop(0, self.rows // step, chunk, 0)
            self.seq_copy(k, 2).start()

        guard(everything(self.active, self.me.middle), action)

    def finish(self, k):
        guard(
            everything(self.active, jnp.logical_not(self.me.middle)),
            lambda: self.seq_copy(k, 2).wait_recv(),
        )
        self.output(k)

    def drain(self, k):
        self.drain_plane(k)

        def ends():
            self.seq_copy(k, 0).wait_send()

        def middles():
            self.seq_copy(k, 1).wait_send()
            self.seq_copy(k, 2).wait_send()

        guard(everything(self.active, jnp.logical_not(self.me.middle)), ends)
        guard(everything(self.active, self.me.middle), middles)


class ColumnStream(Stream):
    def __init__(self, me, source, target, ff_jobs, d_model, ff, refs):
        self.me, self.source, self.target = me, source, target
        self.got, self.keep, self.second, self.over, self.sem, self.seq_sem, self.credit = refs
        self.slots, self.rows = self.got.shape[0], source.shape[0] // 4
        self.count, self.ff_jobs = source.shape[1] // JOB, ff_jobs
        self.ff, self.d_model = ff, d_model
        self.stages = (
            *zip(LATE["C"], (self.pass_second, self.plane_and_ends, self.across, self.back, self.finish, self.drain)),
        )

    def x_first(self, k):
        late = k // self.ff_jobs
        return (1 - late) * ((k + self.ff_jobs // 2 - 2) // self.ff_jobs) * ((k + 1) % 2) + late * (k % 2)

    def first_copy(self, k, part):
        me, slot, x_first = self.me, self.slot(k), self.x_first(k)
        block = x_first * (2 * part + 1 - me.x) + (1 - x_first) * (2 * (1 - me.y) + part)
        sent = self.source.at[pl.ds(pl.multiple_of(self.rows * block, self.rows), self.rows), self.column(k)]
        to = x_first * me.over_x + (1 - x_first) * me.over_y
        return remote(
            sent, self.got.at[slot, pl.ds(self.rows * part, self.rows)],
            self.sem.at[slot, 0, part], self.sem.at[slot, 1, part], to, me.z,
        )

    def keep_copy(self, k, part):
        me, slot, x_first = self.me, self.slot(k), self.x_first(k)
        block = x_first * (2 * part + me.x) + (1 - x_first) * (2 * me.y + part)
        kept = self.source.at[pl.ds(pl.multiple_of(self.rows * block, self.rows), self.rows), self.column(k)]
        return pltpu.make_async_copy(
            kept, self.keep.at[slot, pl.ds(self.rows * part, self.rows)], self.sem.at[slot, 2, part]
        )

    def at(self, k):
        x_first = self.x_first(k)
        return x_first * self.me.y + (1 - x_first) * self.me.x

    def second_copy(self, k):
        me, slot, x_first = self.me, self.slot(k), self.x_first(k)
        row = pl.multiple_of(self.rows * (1 - self.at(k)), self.rows)
        to = x_first * me.over_y + (1 - x_first) * me.over_x
        return remote(
            self.keep.at[slot, pl.ds(row, self.rows)], self.second.at[slot],
            self.sem.at[slot, 0, 2], self.sem.at[slot, 1, 2], to, me.z,
        )

    def start(self, k):
        def credits():
            slot = self.slot(k)

            @pl.when(self.me.middle)
            def _():
                pl.semaphore_wait(self.credit.at[slot], 5)

            @pl.when(jnp.logical_not(self.me.middle))
            def _():
                pl.semaphore_wait(self.credit.at[slot], 4)

        guard(k >= self.slots, credits)
        for part in range(2):
            self.first_copy(k, part).start()
            self.keep_copy(k, part).start()

    def pass_second(self, k):
        for part in range(2):
            self.keep_copy(k, part).wait()
            self.first_copy(k, part).wait_recv()
        slot = self.slot(k)
        add_rows(self.keep.at[slot], 0, self.got.at[slot], 2 * self.rows)
        self.second_copy(k).start()

    def reduce_plane(self, k):
        self.second_copy(k).wait_recv()
        add_rows(self.total(k), self.rows * self.at(k), self.keep.at[self.slot(k)], self.rows)

    def out_column(self, k, core, late):
        if late:
            m, half = k - self.ff_jobs, self.d_model // 2
            tiles = half // JOB
            first = 2 * self.ff + self.d_model * (m // tiles) + JOB * (m % tiles) + half * core
        else:
            first = self.ff * (k % 2) + JOB * (k // 2) + self.ff // 2 * core
        return self.target.at[:, pl.ds(pl.multiple_of(first, 128), JOB)]

    def last_copy(self, k, late=False):
        me, slot, rows = self.me, self.slot(k), self.rows // 2
        part = self.got.at[slot, pl.ds(pl.multiple_of(rows * (1 - me.core), rows), rows)]
        return remote(
            part, self.out_column(k, me.core, late), self.sem.at[slot, 0, 3], self.sem.at[slot, 1, 3],
            me.over_core, me.z,
        )

    def own_copy(self, k, late=False):
        me, slot, rows = self.me, self.slot(k), self.rows // 2
        part = self.got.at[slot, pl.ds(pl.multiple_of(rows * me.core, rows), rows)]
        return pltpu.make_async_copy(part, self.out_column(k, me.core, late), self.sem.at[slot, 2, 0])

    def output(self, k):
        def begin(late):
            self.last_copy(k, late).start()
            self.own_copy(k, late).start()

        guard(k < self.ff_jobs, lambda: begin(False))
        guard(k >= self.ff_jobs, lambda: begin(True))

    def drain_plane(self, k):
        for part in range(2):
            self.first_copy(k, part).wait_send()
        self.second_copy(k).wait_send()

        def end(late):
            self.last_copy(k, late).wait()
            self.own_copy(k, late).wait()

        guard(k < self.ff_jobs, lambda: end(False))
        guard(k >= self.ff_jobs, lambda: end(True))

    def drain(self, k):
        super().drain(k)

        def signal(dp, seq):
            pl.semaphore_signal(
                self.credit.at[self.slot(k)], inc=1, device_id={"dp": dp, "seq": seq},
                device_id_type=pl.DeviceIdType.MESH,
            )

        def free():
            me = self.me
            for dp in (me.over_core, me.over_x, me.over_y):
                signal(dp, me.z)

            @pl.when(me.middle)
            def _():
                signal(me.dp, 3 - me.z)
                signal(me.dp, 3 * (me.z // 2))

            @pl.when(jnp.logical_not(me.middle))
            def _():
                signal(me.dp, me.z + 1 - 2 * (me.z // 2))

        guard(k + self.slots < self.count, free)


class RowStream(Stream):
    def __init__(self, me, source, target, lates, refs):
        self.me, self.source, self.target = me, source, target
        self.got, self.second, self.over, self.stage, self.sem, self.seq_sem = refs
        self.slots, self.rows = self.got.shape[0], source.shape[0] // 2
        self.count = source.shape[1] // JOB
        self.active = me.core == me.y
        steps = (self.pass_second, self.plane_and_ends, self.across, self.back, self.finish, self.drain)
        self.stages = tuple(zip(lates, steps))

    def first_copy(self, k):
        me, slot = self.me, self.slot(k)
        sent = self.source.at[pl.ds(pl.multiple_of(self.rows * (1 - me.x), self.rows), self.rows), self.column(k)]
        return remote(sent, self.got.at[slot], self.sem.at[slot, 0, 0], self.sem.at[slot, 1, 0], me.over_x, me.z)

    def load_copy(self, k):
        kept = self.source.at[
            pl.ds(pl.multiple_of(self.rows * self.me.x, self.rows), self.rows), self.column(k)
        ]
        return pltpu.make_async_copy(kept, self.stage, self.sem.at[self.slot(k), 2, 0])

    def second_copy(self, k):
        me, slot = self.me, self.slot(k)
        return remote(
            self.got.at[slot], self.second.at[slot], self.sem.at[slot, 0, 2], self.sem.at[slot, 1, 2],
            me.over_y, me.z,
        )

    def start(self, k):
        self.first_copy(k).start()
        guard(k == 0, lambda: self.load_copy(k).start())

    def pass_second(self, k):
        self.load_copy(k).wait()
        self.first_copy(k).wait_recv()
        add_rows(self.got.at[self.slot(k)], 0, self.stage, self.rows)
        guard(k + 1 < self.count, lambda: self.load_copy(k + 1).start())
        guard(jnp.logical_not(self.active), lambda: self.second_copy(k).start())

    def reduce_plane(self, k):
        def action():
            self.second_copy(k).wait_recv()
            add_rows(self.total(k), 0, self.got.at[self.slot(k)], self.rows)

        guard(self.active, action)

    def last_copy(self, k):
        me, slot, rows = self.me, self.slot(k), self.rows // 2
        part = self.got.at[slot, pl.ds(pl.multiple_of(rows * (1 - me.core), rows), rows)]
        return remote(
            part, self.target.at[:, self.column(k)], self.sem.at[slot, 0, 3], self.sem.at[slot, 1, 3],
            me.over_core, me.z,
        )

    def own_copy(self, k):
        me, slot, rows = self.me, self.slot(k), self.rows // 2
        part = self.got.at[slot, pl.ds(pl.multiple_of(rows * me.core, rows), rows)]
        return pltpu.make_async_copy(part, self.target.at[:, self.column(k)], self.sem.at[slot, 2, 1])

    def output(self, k):
        def action():
            self.last_copy(k).start()
            self.own_copy(k).start()

        guard(self.active, action)

    def drain_plane(self, k):
        self.first_copy(k).wait_send()

        def active():
            self.last_copy(k).wait_send()
            self.own_copy(k).wait()

        def passive():
            self.second_copy(k).wait_send()
            self.last_copy(k).wait_recv()

        guard(self.active, active)
        guard(jnp.logical_not(self.active), passive)


PLAN = {
    "s0": {"E": (0, 3)},
    "a": {"E": (3, 4, 4, 4, 4, 4, 4, 4, 4), "S": (0, 1, 1, 2, 2, 4, 4, 5, 5), "C": (0, 0, 0, 0, 0, 1, 1, 1, 2), "D": (0, 0, 0, 1, 1, 1, 1, 2, 3)},
    "l0": {"C": (2, 3)},
    "l1": {"S": (5, 6), "C": (3, 4)},
    "l2": {},
    "i": {"E": (4, 4, 4, 6, 6, 6, 6), "S": (6, 6, 6, 6, 7, 7, 8), "C": (4, 4, 4, 4, 5, 5, 5)},
    "n0": {"S": (8, 9), "C": (5, 6), "D": (3, 4)},
    "n1": {"S": (9, 10), "C": (6, 7)},
    "n2": {"F": (0, 1)},
    "o": {"S": (10, 11, 11, 11, 11, 11, 12), "C": (7, 8, 8, 8, 8, 8, 9), "D": (4, 4, 5, 5, 6, 6, 6)},
    "h": {"S": (12, 13, 14, 15, 15, 16, 16), "C": (9, 10, 11, 11, 12, 13, 14), "D": (6, 6, 6, 7, 8, 8, 9), "O": (0, 0, 0, 0, 0, 1, 1)},
    "p": {"S": (16, 16, 17, 18, 19, 19, 19, 20, 20, 20), "C": (14, 14, 15, 15, 15, 15, 16, 16, 16, 16)},
    "p9": {},
    "t": {"S": (20, 20, 20, 20, 21, 21, 22), "C": (16, 17, 17, 18, 18, 18, 20), "D": (9, 10, 10, 11, 11, 11, 11)},
    "t6": {"F": (1, 2)},
}
LATE = {"C": (0, 2, 4, 6, 7, 8), "D": (0, 2, 4, 6, 7, 8), "O": (0, 1, 2, 4, 5, 6)}


class Pace:
    def __init__(self, cols, downs, outs):
        self.actions = {
            "E": downs.start, "S": cols.start, "F": outs.start, "C": cols.tick, "D": downs.tick, "O": outs.tick,
        }

    def at(self, place, n=0):
        for kind, bounds in PLAN[place].items():
            action = self.actions[kind]

            def one(t, carry, action=action):
                action(t)
                return carry

            if isinstance(n, int):
                low, high = bounds[n], bounds[n + 1]
                if high - low == 1:
                    action(low)
                elif high > low:
                    lax.fori_loop(low, high, one, 0)
                continue
            low, high = bounds[0], bounds[1]
            for k in range(1, len(bounds) - 1):
                reached = (n + 32 - k) // 32
                low = low + (bounds[k] - bounds[k - 1]) * reached
                high = high + (bounds[k + 1] - bounds[k]) * reached
            lax.fori_loop(low, high, one, 0)


GAIN_HOPS = 5


class GainSums:
    def __init__(self, me, target, buffer, sem):
        self.me, self.target, self.buffer, self.sem = me, target, buffer, sem

    def hop(self, k):
        me = self.me
        across = me.z + 2 - 4 * (me.z // 2)
        beside = me.z + 1 - 2 * (me.z % 2)
        dp = (me.over_core, me.over_x, me.over_y, me.dp, me.dp)[k]
        seq = (me.z, me.z, me.z, beside, across)[k]
        return remote(
            self.buffer.at[k, 0], self.buffer.at[k, 1], self.sem.at[0, k], self.sem.at[1, k], dp, seq
        )

    def start(self):
        self.hop(0).start()

    def step(self, k):
        self.hop(k).wait_recv()
        total = self.buffer[k, 0] + self.buffer[k, 1]
        if k + 1 < GAIN_HOPS:
            self.buffer[k + 1, 0] = total
            self.hop(k + 1).start()
        else:
            self.target[...] = total

    def drain(self):
        for k in range(GAIN_HOPS):
            self.hop(k).wait_send()


class RowsBack:
    def __init__(self, me, source, target, sem):
        self.me, self.source, self.target, self.sem = me, source, target, sem

    def each(self, local, elsewhere):
        me = self.me
        rows = self.source.shape[0] // 2
        for slot in range(2):
            core, seq = me.z % 2, 2 * me.core + slot
            here = (core == me.core) & (seq == me.z)
            block, target = self.source.at[pl.ds(rows * slot, rows)], self.target.at[me.z // 2]

            @pl.when(here)
            def _():
                local(pltpu.make_async_copy(block, target, self.sem.at[2, 0]))

            @pl.when(jnp.logical_not(here))
            def _():
                elsewhere(
                    remote(
                        block, target, self.sem.at[0, slot], self.sem.at[1, me.z // 2],
                        me.dp - me.core + core, seq,
                    )
                )

    def start(self):
        self.each(lambda copy: copy.start(), lambda copy: copy.start())

    def drain(self):
        me = self.me
        self.each(lambda copy: copy.wait(), lambda copy: copy.wait_send())
        rows = self.source.shape[0] // 2
        for m in range(2):
            here = (me.z == 2 * m + me.core) & (me.core == me.z // 2)

            @pl.when(jnp.logical_not(here))
            def _():
                remote(
                    self.source.at[pl.ds(0, rows)], self.target.at[m], self.sem.at[0, 0],
                    self.sem.at[1, m], me.over_core, me.z,
                ).wait_recv()


def attend_back(pair, width, heads, grad_mixed, start, lse, grads, key_sum, value_sum, query_sum, cosine, sine):
    length = heads.shape[0]
    cols = [pl.ds(pl.multiple_of(width * kind + 128 * pair, 128), 128) for kind in range(3)]
    key_sum[...] = jnp.zeros_like(key_sum)
    value_sum[...] = jnp.zeros_like(value_sum)
    for i in range(length // BLK):
        own_rows, keys = slice(BLK * i, BLK * (i + 1)), BLK * (i + 1)
        place = lax.broadcasted_iota(jnp.int32, (keys, BLK), 0)
        own = BLK * i + lax.broadcasted_iota(jnp.int32, (keys, BLK), 1)
        allowed = (place >= start[:, own_rows]) & (place <= own)
        query = heads[own_rows, cols[0]] * jnp.bfloat16(0.125)
        key, value = heads[0:keys, cols[1]], heads[0:keys, cols[2]]
        grad = grad_mixed[own_rows, cols[0]]
        for half in range(2):
            part = slice(64 * half, 64 * half + 64)
            scores = nt(key[:, part], query[:, part])
            logsum = lse[pl.ds(2 * pair + half, 1), own_rows]
            probs = jnp.where(allowed, jnp.exp(scores - logsum), 0.0)
            grad_probs = nt(value[:, part], grad[:, part])
            inner = jnp.sum(probs * grad_probs, axis=0, keepdims=True)
            grad_scores = (probs * (grad_probs - inner)).astype(jnp.bfloat16)
            value_sum[0:keys, part] += dot(probs.astype(jnp.bfloat16), grad[:, part])
            key_sum[0:keys, part] += dot(grad_scores, query[:, part])
            query_sum[own_rows, part] = tn(grad_scores, key[:, part]) * 0.125
    for kind, total in enumerate((query_sum, key_sum)):
        value = total[...]
        grads[:, cols[kind]] = (value * cosine[...] - swap_halves(value) * sine[...]).astype(jnp.bfloat16)
    grads[:, cols[2]] = value_sum[...].astype(jnp.bfloat16)


def backward_kernel(
    branch_h, slope_gate_h, slope_up_h, hidden_h, nf_t_h, normed_t_h, mixed_t_h, heads_h, lse_h, middle_h, x_h,
    g_down_h, w_qkv_h, w_o_h, w_ff_h, w_down_h, start_ref, gain_ref, cosine, sine,
    out_o, tokens_o, cols_o, o_o, down_o, gains_o, g_cols_h, g_o_h, kept_h, rows_h, grad_nf_h,
    col_got, col_keep, col_second, col_over, col_sem, col_seq, col_credit,
    down_got, down_second, down_over, down_stage, down_sem, down_seq,
    o_got, o_second, o_over, o_stage, o_sem, o_seq,
    wide_recv, half_recv, half_free, wide_sem, half_sem,
    gain_buffer, gain_sem, row_sem, load_sem, tile_sem, store_sem,
):
    me = Place()
    enter(
        [(me.over_core, me.z), (me.over_x, me.z), (me.over_y, me.z)]
        + [(me.dp - me.core + core, lax.rem(me.z + k, 4)) for k in range(1, 4) for core in range(2)]
    )
    length, width = branch_h.shape
    half_rows, own_width, half_ff = length // 2, width // 2, slope_gate_h.shape[1]
    bf16, f32 = jnp.bfloat16, jnp.float32
    vmem = pltpu.VMEM
    ff_jobs = 2 * half_ff // JOB
    cols = ColumnStream(
        me, g_cols_h, cols_o, ff_jobs, width, 2 * half_ff,
        (col_got, col_keep, col_second, col_over, col_sem, col_seq, col_credit),
    )
    downs = RowStream(
        me, g_down_h, down_o, LATE["D"], (down_got, down_second, down_over, down_stage, down_sem, down_seq)
    )
    outs = RowStream(me, g_o_h, o_o, LATE["O"], (o_got, o_second, o_over, o_stage, o_sem, o_seq))
    back_out = RowsBack(me, rows_h.at[0], out_o, row_sem.at[0])
    back_tokens = RowsBack(me, rows_h.at[1], tokens_o, row_sem.at[1])
    gains = GainSums(me, gains_o, gain_buffer, gain_sem)

    def load(source, target, k=0):
        return pltpu.make_async_copy(source, target, load_sem.at[k])

    def fetch(*pairs):
        for k, (source, target) in enumerate(pairs):
            load(source, target, k).start()
        for k, (source, target) in enumerate(pairs):
            load(source, target, k).wait()

    def lanes(n, size=JOB, base=0):
        return pl.ds(pl.multiple_of(base + size * n, 128), size)

    def sublanes(n, size):
        return pl.ds(pl.multiple_of(n * size, size), size)

    def grad_store(buffer, slot, target, n, k):
        return pltpu.make_async_copy(buffer.at[slot], target.at[:, lanes(n)], store_sem.at[slot, k])

    pace = Pace(cols, downs, outs)
    pace.at("s0")

    def feed_forward(grad_ff):
        steps = half_ff // JOB

        def hidden_grads(branch, w_tile, slopes, nf_t, g_tile):
            def tile_loads(n, slot):
                return (
                    pltpu.make_async_copy(w_down_h.at[sublanes(n, JOB), :], w_tile.at[slot], tile_sem.at[slot, 0]),
                    pltpu.make_async_copy(slope_gate_h.at[:, lanes(n)], slopes.at[slot, 0], tile_sem.at[slot, 1]),
                    pltpu.make_async_copy(slope_up_h.at[:, lanes(n)], slopes.at[slot, 1], tile_sem.at[slot, 2]),
                )

            for copy in tile_loads(0, 0):
                copy.start()
            fetch((branch_h, branch), (nf_t_h, nf_t))

            def step(n, carry):
                slot = lax.rem(n, 2)
                for copy in tile_loads(n, slot):
                    copy.wait()

                @pl.when(n + 1 < steps)
                def _():
                    for copy in tile_loads(n + 1, 1 - slot):
                        copy.start()

                grad_hidden = nt(branch[...], w_tile[slot])

                @pl.when(n > 1)
                def _():
                    for kind in range(2):
                        grad_store(g_tile, kind, g_cols_h, 2 * n - 2 + kind, 0).wait()

                for kind in range(2):
                    grad = (grad_hidden * slopes[slot, kind].astype(f32)).astype(bf16)
                    grad_ff[:, lanes(n, JOB, half_ff * kind)] = grad
                    g_tile[kind] = dot(nf_t[...], grad).astype(bf16)
                    grad_store(g_tile, kind, g_cols_h, 2 * n + kind, 0).start()

                @pl.when(n == 0)
                def _():
                    for kind in range(2):
                        grad_store(g_tile, kind, g_cols_h, kind, 0).wait()

                pace.at("a", n)

                return carry

            lax.fori_loop(0, steps, step, 0)
            for kind in range(2):
                grad_store(g_tile, kind, g_cols_h, 2 * steps - 2 + kind, 0).wait()

        pl.run_scoped(
            hidden_grads, vmem((length, width), bf16), vmem((2, JOB, width), bf16),
            vmem((2, 2, length, JOB), bf16), vmem((width, length), bf16), vmem((2, width, JOB), bf16),
        )

        def layer_out(hidden, w_down, send, total):
            other, own = 1 - me.core, me.core
            fetch((w_down_h, w_down), (hidden_h.at[sublanes(other, half_rows), :], hidden))
            load(middle_h.at[sublanes(own, half_rows), :], total, 2).start()

            def other_tile(n, carry):
                send[:, lanes(n)] = dot(hidden[...], w_down[:, lanes(n)]).astype(bf16)
                return carry

            lax.fori_loop(0, width // JOB, other_tile, 0)
            exchange = remote(send, half_recv, half_sem.at[0, 0], half_sem.at[1, 0], me.over_core, me.z)
            exchange.start()
            pace.at("l0")
            fetch((hidden_h.at[sublanes(own, half_rows), :], hidden))
            load(middle_h.at[sublanes(own, half_rows), :], total, 2).wait()

            def own_tile(n, carry):
                total[:, lanes(n)] += dot(hidden[...], w_down[:, lanes(n)])
                return carry

            lax.fori_loop(0, width // JOB, own_tile, 0)
            pace.at("l1")
            exchange.wait()

            def combine(k, carry):
                part = sublanes(k, 64)
                send[part, :] = (total[part, :] + half_recv[part, :].astype(f32)).astype(bf16)
                return carry

            lax.fori_loop(0, half_rows // 64, combine, 0)
            pl.semaphore_signal(
                half_free, inc=1, device_id={"dp": me.over_core, "seq": me.z},
                device_id_type=pl.DeviceIdType.MESH,
            )
            fetch((send, rows_h.at[0]))

        pl.run_scoped(
            layer_out, vmem((half_rows, half_ff), bf16), vmem((half_ff, width), bf16),
            vmem((half_rows, width), bf16), vmem((half_rows, width), f32),
        )
        back_out.start()
        pace.at("l2")

    chunk = 2 * JOB
    chunks = width // chunk

    def wide_copy(send, k):
        part = pl.ds(chunk * k, chunk)
        return remote(
            send.at[:, part], wide_recv.at[:, part], wide_sem.at[0, k], wide_sem.at[1, k], me.over_core, me.z
        )

    def with_grad_ff(grad_ff):
        feed_forward(grad_ff)

        def input_grads(w_tile, send, parts):
            def tile_load(n, kind):
                return pltpu.make_async_copy(
                    w_ff_h.at[sublanes(n, JOB), pl.ds(half_ff * kind, half_ff)], w_tile.at[kind],
                    tile_sem.at[kind, 0],
                )

            def part_store(n, slot):
                return pltpu.make_async_copy(parts.at[slot], grad_nf_h.at[:, lanes(n)], store_sem.at[slot, 0])

            for kind in range(2):
                tile_load(0, kind).start()
            count = width // JOB

            def step(n, carry):
                slot = lax.rem(n, 2)
                tile_load(n, 0).wait()
                part = nt(grad_ff[:, 0:half_ff], w_tile[0])

                @pl.when(n + 1 < count)
                def _():
                    tile_load(n + 1, 0).start()

                tile_load(n, 1).wait()
                part = part + nt(grad_ff[:, half_ff : 2 * half_ff], w_tile[1])

                @pl.when(n + 1 < count)
                def _():
                    tile_load(n + 1, 1).start()

                @pl.when(n >= 2)
                def _():
                    part_store(n - 2, slot).wait()

                parts[slot] = part
                part_store(n, slot).start()
                send[:, lanes(n)] = part.astype(bf16)
                for k in range(chunks):
                    @pl.when(n == 2 * k + 1)
                    def _():
                        wide_copy(send, k).start()

                pace.at("i", n)

                return carry

            lax.fori_loop(0, count, step, 0)
            for n in range(count - 2, count):
                part_store(n, n % 2).wait()
            pace.at("n0")
            for k in range(chunks):
                wide_copy(send, k).wait()

        pl.run_scoped(
            input_grads, vmem((2, JOB, half_ff), bf16), vmem((length, width), bf16), vmem((2, length, JOB), f32)
        )

    pl.run_scoped(with_grad_ff, vmem((length, 2 * half_ff), bf16))

    def to_attention(grad_attn):
        def norm_back(grad_nf, middle, branch):
            fetch((middle_h, middle), (branch_h, branch), (grad_nf_h, grad_nf))
            gain = gain_ref[1:2, :]

            def rows(k, total):
                part = sublanes(k, 64)
                grad = grad_nf[part, :] + wide_recv[part, :].astype(f32)
                gained, values = norm_rows_back(middle[part, :], gain, grad)
                values = values + branch[part, :].astype(f32)
                grad_nf[part, :] = values
                grad_attn[part, :] = values.astype(bf16)
                return total + gained

            total = lax.fori_loop(0, length // 64, rows, jnp.zeros((1, width), f32))
            gain_buffer[0, 0, 1:2, :] = 0.5 * total
            kept = load(grad_nf.at[sublanes(me.core, half_rows), :], kept_h, 0)
            kept.start()
            pace.at("n1")
            kept.wait()

        pl.run_scoped(
            norm_back, vmem((length, width), f32), vmem((length, width), f32), vmem((length, width), bf16)
        )

        def out_projection(w_o, mixed_t, g_tile, grad_mixed):
            fetch((w_o_h, w_o), (mixed_t_h, mixed_t))
            for n in range(own_width // JOB):
                grad_mixed[:, JOB * n : JOB * (n + 1)] = nt(
                    grad_attn[...], w_o[JOB * n : JOB * (n + 1), :]
                ).astype(bf16)
            placed = load(grad_mixed, wide_recv.at[:, pl.ds(0, own_width)], 3)
            placed.start()
            count = width // JOB

            def step(n, carry):
                slot = lax.rem(n, 2)

                @pl.when(n >= 2)
                def _():
                    grad_store(g_tile, slot, g_o_h, n - 2, 1).wait()

                g_tile[slot] = dot(mixed_t[...], grad_attn[:, lanes(n)]).astype(bf16)
                grad_store(g_tile, slot, g_o_h, n, 1).start()

                pace.at("o", n)

                return carry

            lax.fori_loop(0, count, step, 0)
            for n in range(count - 2, count):
                grad_store(g_tile, n % 2, g_o_h, n, 1).wait()
            placed.wait()

        pl.run_scoped(
            out_projection, vmem((own_width, width), bf16), vmem((own_width, length), bf16),
            vmem((2, own_width, JOB), bf16), vmem((length, own_width), bf16),
        )

    pl.run_scoped(to_attention, vmem((length, width), bf16))
    pace.at("n2")

    def attention(grads):
        def heads_back(heads, lse, key_sum, value_sum, query_sum):
            fetch((heads_h, heads), (lse_h, lse))

            def step(pair, carry):
                attend_back(
                    pair, own_width, heads, wide_recv, start_ref, lse, grads, key_sum, value_sum, query_sum, cosine, sine
                )
                pace.at("h", pair)
                return carry

            lax.fori_loop(0, own_width // 128, step, 0)

        pl.run_scoped(
            heads_back, vmem((length, 3 * own_width), bf16), vmem((128, length), f32),
            *[vmem((length, 128), f32)] * 3,
        )

        def projection_grads(normed_t, g_tile):
            fetch((normed_t_h, normed_t))
            count = 3 * own_width // JOB

            def step(n, carry):
                slot = lax.rem(n, 2)
                g_tile[slot] = dot(normed_t[...], grads[:, lanes(n)]).astype(bf16)

                @pl.when(n >= 1)
                def _():
                    grad_store(g_tile, 1 - slot, g_cols_h, ff_jobs + n - 1, 1).wait()

                grad_store(g_tile, slot, g_cols_h, ff_jobs + n, 1).start()

                pace.at("p", n)
                return carry

            lax.fori_loop(0, count, step, 0)
            grad_store(g_tile, (count - 1) % 2, g_cols_h, ff_jobs + count - 1, 1).wait()

        pl.run_scoped(projection_grads, vmem((width, length), bf16), vmem((2, width, JOB), bf16))

        pace.at("p9")

        def tokens_back(w_tile, send, total, x_rows, kept):
            def tile_load(n, slot):
                return pltpu.make_async_copy(w_qkv_h.at[sublanes(n, JOB), :], w_tile.at[slot], tile_sem.at[slot, 0])

            tile_load(0, 0).start()
            load(x_h.at[sublanes(me.core, half_rows), :], x_rows, 0).start()
            load(kept_h, kept, 1).start()
            count = width // JOB

            def step(n, carry):
                slot = lax.rem(n, 2)
                tile_load(n, slot).wait()

                @pl.when(n + 1 < count)
                def _():
                    tile_load(n + 1, 1 - slot).start()

                send[:, lanes(n)] = nt(grads[sublanes(1 - me.core, half_rows), :], w_tile[slot]).astype(bf16)
                total[:, lanes(n)] = nt(grads[sublanes(me.core, half_rows), :], w_tile[slot])

                pace.at("t", n)
                return carry

            lax.fori_loop(0, count, step, 0)
            pl.semaphore_wait(half_free, 1)
            exchange = remote(send, half_recv, half_sem.at[0, 0], half_sem.at[1, 0], me.over_core, me.z)
            exchange.start()
            pace.at("t6")
            load(x_h.at[sublanes(me.core, half_rows), :], x_rows, 0).wait()
            load(kept_h, kept, 1).wait()
            exchange.wait()
            gain = gain_ref[0:1, :]

            def rows(k, sums):
                part = sublanes(k, 64)
                grad = total[part, :] + half_recv[part, :].astype(f32)
                gained, values = norm_rows_back(x_rows[part, :].astype(f32), gain, grad)
                send[part, :] = (values + kept[part, :]).astype(bf16)
                return sums + gained

            gain_buffer[0, 0, 0:1, :] = lax.fori_loop(0, half_rows // 64, rows, jnp.zeros((1, width), f32))
            gains.start()
            fetch((send, rows_h.at[1]))

        pl.run_scoped(
            tokens_back, vmem((2, JOB, 3 * own_width), bf16), vmem((half_rows, width), bf16),
            vmem((half_rows, width), f32), vmem((half_rows, width), bf16), vmem((half_rows, width), f32),
        )
        back_tokens.start()

    pl.run_scoped(attention, vmem((length, 3 * own_width), bf16))

    first = {"E": 6, "S": 22, "F": 2, "C": 20, "D": 11, "O": 1}
    steps = max(stream.ticks - first[kind] for kind, stream in (("C", cols), ("D", downs), ("O", outs)))

    def rest(t, carry):
        for kind, stream in (("E", downs), ("S", cols), ("F", outs)):
            if first[kind] < stream.count:
                guard(first[kind] + t < stream.count, functools.partial(stream.start, first[kind] + t))
        for kind, stream in (("C", cols), ("D", downs), ("O", outs)):
            if first[kind] < stream.ticks:
                stream.tick(first[kind] + t)
        for k in range(GAIN_HOPS - 1):
            @pl.when(t == k)
            def _():
                gains.step(k)

        return carry

    lax.fori_loop(0, steps, rest, 0)
    for k in range(min(steps, GAIN_HOPS - 1), GAIN_HOPS):
        gains.step(k)
    gains.drain()
    back_out.drain()
    back_tokens.drain()


def norm_rows_back(values, gain, grad):
    scale = lax.rsqrt(jnp.mean(values * values, axis=-1, keepdims=True) + EPS)
    unit = values * scale
    inner = grad * gain
    return (
        jnp.sum(grad * unit, axis=0, keepdims=True),
        scale * (inner - unit * jnp.mean(inner * unit, axis=-1, keepdims=True)),
    )


COLUMN_SLOTS = 12


def backward(branch, slopes, hidden, turned, heads, lse, middle, x, g_down, weights, start, gain, cosine, sine):
    length, width = branch.shape
    half, half_ff = width // 2, hidden.shape[1]
    rows = length // 4
    bf16, f32 = jnp.bfloat16, jnp.float32

    def shape(*dims, dtype=bf16):
        return jax.ShapeDtypeStruct(dims, dtype)

    columns = 2 * half_ff + 3 * half
    shapes = [
        shape(2, rows, width),
        shape(2, rows, width),
        shape(width // 8, 2 * columns),
        shape(width // 8, width),
        shape(half_ff // 4, width),
        shape(2, width, dtype=f32),
        shape(width, columns),
        shape(half, width),
        shape(length // 2, width, dtype=f32),
        shape(2, length // 2, width),
        shape(length, width, dtype=f32),
    ]
    dma, vmem = pltpu.SemaphoreType.DMA, pltpu.VMEM
    whole = pl.BlockSpec(memory_space=pltpu.VMEM)
    ring, row = COLUMN_SLOTS, width // 4
    jobs = width // JOB
    row_buffers = []
    for depth in (half_ff // 2, half // 2):
        row_buffers += [
            vmem((jobs, depth, JOB), bf16), vmem((jobs, depth, JOB), bf16), vmem((jobs, 2, depth, JOB), bf16),
            vmem((depth, JOB), bf16), dma((jobs, 3, 4)), dma((jobs, 2, 3)),
        ]
    return pl.pallas_call(
        backward_kernel,
        in_specs=[ANY] * 16 + [whole] * 4,
        out_specs=[ANY] * 5 + [whole] + [ANY] * 5,
        out_shape=shapes,
        scratch_shapes=[
            vmem((ring, 2 * row, JOB), bf16), vmem((ring, 2 * row, JOB), bf16), vmem((ring, row, JOB), bf16),
            vmem((ring, 2, row, JOB), bf16), dma((ring, 3, 4)), dma((ring, 2, 3)),
            pltpu.SemaphoreType.REGULAR((ring,)),
        ]
        + row_buffers
        + [
            vmem((length, width), bf16), vmem((length // 2, width), bf16), pltpu.SemaphoreType.REGULAR,
            dma((2, 3)), dma((2, 1)),
            vmem((GAIN_HOPS, 2, 2, width), f32), dma((2, GAIN_HOPS)), dma((2, 3, 2)), dma((4,)), dma((2, 3)),
            dma((2, 2)),
        ],
        compiler_params=pltpu.CompilerParams(
            collective_id=1, has_side_effects=True, vmem_limit_bytes=63 * 1024 * 1024
        ),
        cost_estimate=pl.CostEstimate(flops=0, bytes_accessed=800_000_000, transcendentals=0),
        name="backward",
    )(
        branch, *slopes, hidden, *turned, heads, lse, middle, x, g_down, *weights, start, gain, cosine, sine
    )


def wide(value):
    return value.astype(jnp.float32)


def dot(a, b):
    return jnp.dot(a, b, preferred_element_type=jnp.float32)


WIDEN_STEPS = 4


def widen_kernel(cols, o, down, tokens, result, *outs):
    first = 0
    for out in outs[:5]:
        out[...] = cols[:, first : first + out.shape[1]].astype(jnp.float32)
        first += out.shape[1]
    for source, out in zip((o, down, tokens, result), outs[5:]):
        out[...] = source[...].astype(out.dtype)


def widen(cols, o, down, tokens, result, ff):
    depth, width = o.shape

    def rows(count, columns):
        return pl.BlockSpec((count // WIDEN_STEPS, columns), lambda i: (i, 0))

    shapes = [(depth, ff)] * 2 + [(depth, width)] * 4 + [down.shape, tokens.shape, result.shape]
    return pl.pallas_call(
        widen_kernel,
        grid=(WIDEN_STEPS,),
        in_specs=[rows(*value.shape) for value in (cols, o, down, tokens, result)],
        out_specs=[rows(*shape) for shape in shapes],
        out_shape=[jax.ShapeDtypeStruct(shape, jnp.float32) for shape in shapes[:-1]]
        + [jax.ShapeDtypeStruct(result.shape, result.dtype)],
        compiler_params=pltpu.CompilerParams(vmem_limit_bytes=63 * 1024 * 1024),
        name="widen",
    )(cols, o, down, tokens, result)


def column_device(
    tokens, segment_ids, out_grad, w_q, w_k, w_v, w_o, w_gate, w_up, w_down, gain_attn, gain_ffn
):
    dp_at = lax.axis_index("dp")
    rows, width = tokens.shape[1], tokens.shape[2]
    length, ff = 4 * rows, w_gate.shape[1]
    gains = lax.dynamic_update_slice_in_dim(
        jnp.zeros((2, width), jnp.bfloat16),
        jnp.stack([gain_attn, gain_ffn]),
        dp_at * gain_attn.shape[0],
        1,
    )
    lane = jnp.arange(2 * HD, dtype=jnp.int32)
    pace = jnp.exp((lane % (HD // 2)).astype(jnp.float32) * (-math.log(10000.0) / (HD // 2)))
    angle = jnp.arange(length, dtype=jnp.float32)[:, None] * pace[None, :]
    cosine = jnp.cos(angle)
    sine = jnp.where(lane % HD < HD // 2, -1.0, 1.0)[None, :] * jnp.sin(angle)
    (
        x_low, docs, grad_branch, gains, full_qkv, full_o, full_ff, full_down, heads, lse, middle,
        slope_gate, slope_up, hidden, g_down, start, gain, normed_t, nf_t, mixed_t,
    ) = gather_all(
        tokens, segment_ids.reshape(2, 1, rows), out_grad, gains, cosine, sine,
        (w_q, w_k, w_v, w_o, w_gate, w_up, w_down),
    )
    result, grad_tokens, g_cols, g_o, g_down, grad_gains = backward(
        grad_branch, (slope_gate, slope_up), hidden, (nf_t, normed_t, mixed_t), heads, lse, middle, x_low, g_down,
        (full_qkv, full_o, full_ff, full_down), start, gain, cosine, sine,
    )[:6]
    grad_gains = lax.dynamic_slice_in_dim(grad_gains, dp_at * (width // 8), width // 8, 1)
    flat = (2 * rows, width)
    gate, up, query, key, value, out, down, grad_tokens, result = widen(
        g_cols, g_o, g_down, grad_tokens.reshape(flat), result.reshape(flat), ff
    )
    result = result.reshape(2, rows, width)
    return (
        result, grad_tokens.reshape(2, rows, width), query, key, value, out, gate, up, down, grad_gains[0], grad_gains[1]
    )


def solution(mesh):
    placed = (
        P(None, ("dp", "seq"), None),
        P(None, ("dp", "seq")),
        P(None, ("dp", "seq"), None),
        P("dp", None),
        P("dp", None),
        P("dp", None),
        P("dp", None),
        P("dp", None),
        P("dp", None),
        P("dp", None),
        P("dp"),
        P("dp"),
    )
    return jax.shard_map(
        column_device if dict(mesh.shape) == FAST_MESH else per_device,
        mesh=mesh,
        in_specs=placed,
        out_specs=(
            P(None, ("dp", "seq"), None),
            P(None, ("dp", "seq"), None),
            P("dp", None),
            P("dp", None),
            P("dp", None),
            P("dp", None),
            P("dp", None),
            P("dp", None),
            P("dp", None),
            P("dp"),
            P("dp"),
        ),
        check_vma=False,
    )
```

```python
import functools
import math

import jax
import jax.numpy as jnp
import numpy as np
from jax import lax
from jax.experimental import pallas as pl
from jax.experimental.pallas import tpu as pltpu
from jax.sharding import PartitionSpec as P

HEADS = 24
HD = 64


EPS = 1e-05


def positions_of(doc_row):
    count = doc_row.shape[0]
    place = jnp.arange(count, dtype=jnp.int32)
    before = jnp.concatenate([doc_row[:1], doc_row[:-1]])
    starts = (place == 0) | (doc_row != before)
    first_place = lax.cummax(jnp.where(starts, place, jnp.zeros_like(place)), axis=0)
    return place - first_place


def rope_tables(where_at, half):
    inverse = jnp.exp(jnp.arange(half, dtype=jnp.float32) * (-math.log(10000.0) / half))
    angle = where_at.astype(jnp.float32)[:, None] * inverse[None, :]
    return (jnp.cos(angle), jnp.sin(angle))


def rotate(values, cosine, sine):
    half = values.shape[-1] // 2
    first, second = (values[..., :half], values[..., half:])
    cos_heads, sin_heads = (cosine[:, None, :], sine[:, None, :])
    return jnp.concatenate(
        [first * cos_heads - second * sin_heads, second * cos_heads + first * sin_heads], axis=-1
    )


def rotate_back(grads, cosine, sine):
    half = grads.shape[-1] // 2
    first, second = (grads[..., :half], grads[..., half:])
    cos_heads, sin_heads = (cosine[:, None, :], sine[:, None, :])
    return jnp.concatenate(
        [first * cos_heads + second * sin_heads, second * cos_heads - first * sin_heads], axis=-1
    )


def rms_norm(values, gain):
    return values * lax.rsqrt(jnp.mean(values * values, axis=-1, keepdims=True) + EPS) * gain


def norm_backward(values, gain, grad_normed):
    scale = lax.rsqrt(jnp.mean(values * values, axis=-1, keepdims=True) + EPS)
    unit = values * scale
    grad_gain = jnp.sum(grad_normed * unit, axis=0)
    inner = grad_normed * gain
    grad_values = scale * (inner - unit * jnp.mean(inner * unit, axis=-1, keepdims=True))
    return (grad_gain, grad_values)


def block_scores(query_heads, key_heads, doc_row, start, block):
    length = doc_row.shape[0]
    place = jnp.arange(length, dtype=jnp.int32)
    query_block = lax.dynamic_slice_in_dim(query_heads, start, block, 0)
    doc_block = lax.dynamic_slice_in_dim(doc_row, start, block, 0)
    rows_block = start + jnp.arange(block, dtype=jnp.int32)
    allowed = (doc_block[:, None] == doc_row[None, :]) & (rows_block[:, None] >= place[None, :])
    scores = (
        jnp.einsum("qhd,khd->hqk", query_block, key_heads, preferred_element_type=jnp.float32)
        * 0.125
    )
    return (query_block, jnp.where(allowed[None], scores, -1e30))


def attention_forward(query, key, value, doc_row):
    length = query.shape[0]
    head_shape = (length, query.shape[1] // HD, HD)
    query_heads, key_heads, value_heads = (
        query.reshape(head_shape),
        key.reshape(head_shape),
        value.reshape(head_shape),
    )
    block = min(512, length)
    starts = jnp.arange(length // block, dtype=jnp.int32) * block

    def one_block(start):
        unused, scores = block_scores(query_heads, key_heads, doc_row, start, block)
        peak = jnp.max(scores, axis=-1, keepdims=True)
        expo = jnp.exp(scores - peak)
        total = jnp.sum(expo, axis=-1, keepdims=True)
        probs_low = (expo / total).astype(jnp.bfloat16)
        mixed = jnp.einsum(
            "hqk,khd->qhd", probs_low, value_heads, preferred_element_type=jnp.float32
        )
        return (mixed.astype(jnp.bfloat16), (peak + jnp.log(total))[..., 0])

    mixed, logsum = lax.map(one_block, starts)
    return (mixed.reshape(length, query.shape[1]), logsum)


def attention_backward(query, key, value, doc_row, logsum, grad_mixed, cosine, sine):
    length = query.shape[0]
    head_shape = (length, query.shape[1] // HD, HD)
    query_heads, key_heads, value_heads = (
        query.reshape(head_shape),
        key.reshape(head_shape),
        value.reshape(head_shape),
    )
    grad_heads = grad_mixed.reshape(head_shape)
    block = min(512, length)
    starts = jnp.arange(length // block, dtype=jnp.int32) * block

    def one_block(carry, item):
        grad_key, grad_value = carry
        start, logsum_block = item
        query_block, scores = block_scores(query_heads, key_heads, doc_row, start, block)
        probs = jnp.exp(scores - logsum_block[..., None])
        probs_low = probs.astype(jnp.bfloat16)
        grad_block = lax.dynamic_slice_in_dim(grad_heads, start, block, 0)
        grad_probs = jnp.einsum(
            "qhd,khd->hqk", grad_block, value_heads, preferred_element_type=jnp.float32
        )
        inner = jnp.sum(probs * grad_probs, axis=-1, keepdims=True)
        grad_scores = (probs * (grad_probs - inner)).astype(jnp.bfloat16)
        grad_query = (
            jnp.einsum("hqk,khd->qhd", grad_scores, key_heads, preferred_element_type=jnp.float32)
            * 0.125
        )
        grad_key = (
            grad_key
            + jnp.einsum(
                "hqk,qhd->khd", grad_scores, query_block, preferred_element_type=jnp.float32
            )
            * 0.125
        )
        grad_value = grad_value + jnp.einsum(
            "hqk,qhd->khd", probs_low, grad_block, preferred_element_type=jnp.float32
        )
        return ((grad_key, grad_value), grad_query)

    zeros_heads = jnp.zeros(head_shape, jnp.float32)
    (grad_key, grad_value), grad_query = lax.scan(
        one_block, (zeros_heads, zeros_heads), (starts, logsum)
    )
    grad_query = rotate_back(grad_query.reshape(head_shape), cosine, sine)
    grad_key = rotate_back(grad_key, cosine, sine)
    width_here = query.shape[1]
    return (
        grad_query.reshape(length, width_here).astype(jnp.bfloat16),
        grad_key.reshape(length, width_here).astype(jnp.bfloat16),
        grad_value.reshape(length, width_here).astype(jnp.bfloat16),
    )


def per_device(
    tokens, segment_ids, out_grad, w_q, w_k, w_v, w_o, w_gate, w_up, w_down, gain_attn, gain_ffn
):
    micro, rows, width = tokens.shape
    offset = lax.axis_index("seq") * rows
    shards = (w_q, w_k, w_v, w_o, w_gate, w_up, w_down, gain_attn, gain_ffn)
    gathered = (
        lax.all_gather(shards[0], "dp", axis=0, tiled=True),
        lax.all_gather(shards[1], "dp", axis=0, tiled=True),
        lax.all_gather(shards[2], "dp", axis=0, tiled=True),
        lax.all_gather(shards[3], "dp", axis=0, tiled=True),
        lax.all_gather(shards[4], "dp", axis=0, tiled=True),
        lax.all_gather(shards[5], "dp", axis=0, tiled=True),
        lax.all_gather(shards[6], "dp", axis=0, tiled=True),
        lax.all_gather(shards[7], "dp", axis=0, tiled=True),
        lax.all_gather(shards[8], "dp", axis=0, tiled=True),
    )
    docs = lax.all_gather(segment_ids, "seq", axis=1, tiled=True)
    full_q, full_k, full_v, full_o, full_gate, full_up, full_down, full_gain_a, full_gain_f = (
        gathered
    )
    gain_a = full_gain_a.astype(jnp.float32)
    gain_f = full_gain_f.astype(jnp.float32)
    row_heads = (rows, HEADS, HD)
    saved = []
    results = []
    for micro_index in range(micro):
        rows_in = tokens[micro_index].astype(jnp.float32)
        doc_row = docs[micro_index]
        cosine, sine = rope_tables(positions_of(doc_row), HD // 2)
        own_cos = lax.dynamic_slice_in_dim(cosine, offset, rows, 0)
        own_sin = lax.dynamic_slice_in_dim(sine, offset, rows, 0)
        normed = rms_norm(rows_in, gain_a).astype(jnp.bfloat16)
        query_rows = jnp.dot(normed, full_q, preferred_element_type=jnp.float32).reshape(row_heads)
        query_rows = rotate(query_rows, own_cos, own_sin).reshape(rows, width).astype(jnp.bfloat16)
        key_rows = jnp.dot(normed, full_k, preferred_element_type=jnp.float32).reshape(row_heads)
        key_rows = rotate(key_rows, own_cos, own_sin).reshape(rows, width).astype(jnp.bfloat16)
        value_rows = jnp.dot(normed, full_v, preferred_element_type=jnp.float32).astype(
            jnp.bfloat16
        )
        query, key, value = (
            lax.all_to_all(query_rows, "seq", split_axis=1, concat_axis=0, tiled=True),
            lax.all_to_all(key_rows, "seq", split_axis=1, concat_axis=0, tiled=True),
            lax.all_to_all(value_rows, "seq", split_axis=1, concat_axis=0, tiled=True),
        )
        mixed, logsum = attention_forward(query, key, value, doc_row)
        mixed_rows = lax.all_to_all(mixed, "seq", split_axis=0, concat_axis=1, tiled=True)
        middle = rows_in + jnp.dot(mixed_rows, full_o, preferred_element_type=jnp.float32)
        normed_ffn = rms_norm(middle, gain_f).astype(jnp.bfloat16)
        gate = jnp.dot(normed_ffn, full_gate, preferred_element_type=jnp.float32)
        up_value = jnp.dot(normed_ffn, full_up, preferred_element_type=jnp.float32)
        hidden = (jax.nn.silu(gate) * up_value).astype(jnp.bfloat16)
        result = middle + jnp.dot(hidden, full_down, preferred_element_type=jnp.float32)
        results.append(result.astype(jnp.bfloat16))
        saved.append(
            (
                rows_in,
                doc_row,
                cosine,
                sine,
                normed,
                query,
                key,
                value,
                logsum,
                mixed_rows,
                middle,
                normed_ffn,
                gate,
                up_value,
                hidden,
            )
        )
    back_weights = (
        lax.all_gather(shards[0], "dp", axis=0, tiled=True),
        lax.all_gather(shards[1], "dp", axis=0, tiled=True),
        lax.all_gather(shards[2], "dp", axis=0, tiled=True),
        lax.all_gather(shards[3], "dp", axis=0, tiled=True),
        lax.all_gather(shards[4], "dp", axis=0, tiled=True),
        lax.all_gather(shards[5], "dp", axis=0, tiled=True),
        lax.all_gather(shards[6], "dp", axis=0, tiled=True),
        lax.all_gather(shards[7], "dp", axis=0, tiled=True),
        lax.all_gather(shards[8], "dp", axis=0, tiled=True),
    )
    back_q, back_k, back_v, back_o, back_gate, back_up, back_down, back_gain_a, back_gain_f = (
        back_weights
    )
    gain_back_a = back_gain_a.astype(jnp.float32)
    gain_back_f = back_gain_f.astype(jnp.float32)
    totals = [jnp.zeros(weight.shape, jnp.float32) for weight in back_weights]
    grad_inputs = []
    for micro_index in range(micro):
        (
            rows_in,
            doc_row,
            cosine,
            sine,
            normed,
            query,
            key,
            value,
            logsum,
            mixed_rows,
            middle,
            normed_ffn,
            gate,
            up_value,
            hidden,
        ) = saved[micro_index]
        grad_out = out_grad[micro_index].astype(jnp.float32)
        grad_branch = grad_out.astype(jnp.bfloat16)
        totals[6] = totals[6] + jnp.einsum(
            "tf,td->fd", hidden, grad_branch, preferred_element_type=jnp.float32
        )
        grad_hidden = jnp.einsum(
            "td,fd->tf", grad_branch, back_down, preferred_element_type=jnp.float32
        )
        sigma = jax.nn.sigmoid(gate)
        grad_gate = (grad_hidden * up_value * sigma * (1.0 + gate * (1.0 - sigma))).astype(
            jnp.bfloat16
        )
        grad_up = (grad_hidden * jax.nn.silu(gate)).astype(jnp.bfloat16)
        totals[4] = totals[4] + jnp.einsum(
            "td,tf->df", normed_ffn, grad_gate, preferred_element_type=jnp.float32
        )
        totals[5] = totals[5] + jnp.einsum(
            "td,tf->df", normed_ffn, grad_up, preferred_element_type=jnp.float32
        )
        grad_normed_ffn = jnp.einsum(
            "tf,df->td", grad_gate, back_gate, preferred_element_type=jnp.float32
        )
        grad_normed_ffn = grad_normed_ffn + jnp.einsum(
            "tf,df->td", grad_up, back_up, preferred_element_type=jnp.float32
        )
        grad_gain_f, grad_middle = norm_backward(middle, gain_back_f, grad_normed_ffn)
        totals[8] = totals[8] + grad_gain_f
        grad_middle = grad_middle + grad_out
        grad_attn = grad_middle.astype(jnp.bfloat16)
        totals[3] = totals[3] + jnp.einsum(
            "ti,td->id", mixed_rows, grad_attn, preferred_element_type=jnp.float32
        )
        grad_mixed_rows = jnp.einsum(
            "td,id->ti", grad_attn, back_o, preferred_element_type=jnp.float32
        ).astype(jnp.bfloat16)
        grad_mixed = lax.all_to_all(grad_mixed_rows, "seq", split_axis=1, concat_axis=0, tiled=True)
        grad_query, grad_key, grad_value = attention_backward(
            query, key, value, doc_row, logsum, grad_mixed, cosine, sine
        )
        query_back, key_back, value_back = (
            lax.all_to_all(grad_query, "seq", split_axis=0, concat_axis=1, tiled=True),
            lax.all_to_all(grad_key, "seq", split_axis=0, concat_axis=1, tiled=True),
            lax.all_to_all(grad_value, "seq", split_axis=0, concat_axis=1, tiled=True),
        )
        totals[0] = totals[0] + jnp.einsum(
            "td,te->de", normed, query_back, preferred_element_type=jnp.float32
        )
        totals[1] = totals[1] + jnp.einsum(
            "td,te->de", normed, key_back, preferred_element_type=jnp.float32
        )
        totals[2] = totals[2] + jnp.einsum(
            "td,te->de", normed, value_back, preferred_element_type=jnp.float32
        )
        grad_normed = jnp.einsum(
            "te,de->td", query_back, back_q, preferred_element_type=jnp.float32
        )
        grad_normed = grad_normed + jnp.einsum(
            "te,de->td", key_back, back_k, preferred_element_type=jnp.float32
        )
        grad_normed = grad_normed + jnp.einsum(
            "te,de->td", value_back, back_v, preferred_element_type=jnp.float32
        )
        grad_gain_a, grad_rows = norm_backward(rows_in, gain_back_a, grad_normed)
        totals[7] = totals[7] + grad_gain_a
        grad_inputs.append(grad_rows + grad_middle)
    summed_all = (
        totals[0],
        totals[1],
        totals[2],
        totals[3],
        totals[4],
        totals[5],
        totals[6],
        totals[7],
        totals[8],
    )
    pieces = (
        lax.psum_scatter(
            summed_all[0].astype(jnp.bfloat16), "dp", scatter_dimension=0, tiled=True
        ).astype(jnp.float32),
        lax.psum_scatter(
            summed_all[1].astype(jnp.bfloat16), "dp", scatter_dimension=0, tiled=True
        ).astype(jnp.float32),
        lax.psum_scatter(
            summed_all[2].astype(jnp.bfloat16), "dp", scatter_dimension=0, tiled=True
        ).astype(jnp.float32),
        lax.psum_scatter(
            summed_all[3].astype(jnp.bfloat16), "dp", scatter_dimension=0, tiled=True
        ).astype(jnp.float32),
        lax.psum_scatter(
            summed_all[4].astype(jnp.bfloat16), "dp", scatter_dimension=0, tiled=True
        ).astype(jnp.float32),
        lax.psum_scatter(
            summed_all[5].astype(jnp.bfloat16), "dp", scatter_dimension=0, tiled=True
        ).astype(jnp.float32),
        lax.psum_scatter(
            summed_all[6].astype(jnp.bfloat16), "dp", scatter_dimension=0, tiled=True
        ).astype(jnp.float32),
        lax.psum_scatter(
            summed_all[7].astype(jnp.bfloat16), "dp", scatter_dimension=0, tiled=True
        ).astype(jnp.float32),
        lax.psum_scatter(
            summed_all[8].astype(jnp.bfloat16), "dp", scatter_dimension=0, tiled=True
        ).astype(jnp.float32),
    )
    pieces = (
        lax.psum(pieces[0].astype(jnp.bfloat16), "seq").astype(jnp.float32),
        lax.psum(pieces[1].astype(jnp.bfloat16), "seq").astype(jnp.float32),
        lax.psum(pieces[2].astype(jnp.bfloat16), "seq").astype(jnp.float32),
        lax.psum(pieces[3].astype(jnp.bfloat16), "seq").astype(jnp.float32),
        lax.psum(pieces[4].astype(jnp.bfloat16), "seq").astype(jnp.float32),
        lax.psum(pieces[5].astype(jnp.bfloat16), "seq").astype(jnp.float32),
        lax.psum(pieces[6].astype(jnp.bfloat16), "seq").astype(jnp.float32),
        lax.psum(pieces[7].astype(jnp.bfloat16), "seq").astype(jnp.float32),
        lax.psum(pieces[8].astype(jnp.bfloat16), "seq").astype(jnp.float32),
    )
    return (
        jnp.stack(results),
        jnp.stack(grad_inputs),
        pieces[0],
        pieces[1],
        pieces[2],
        pieces[3],
        pieces[4],
        pieces[5],
        pieces[6],
        pieces[7],
        pieces[8],
    )


BLK = 256
LOG2E = 1.4426950408889634


def swap_halves(v):
    lane = lax.broadcasted_iota(jnp.int32, v.shape, 1)
    width = v.shape[1]
    up = pltpu.roll(v, width - 32, axis=1)
    down = pltpu.roll(v, 32, axis=1)
    return jnp.where(lane % 64 < 32, up, down)


def nt(a, b):
    return lax.dot_general(a, b, (((1,), (1,)), ((), ())), preferred_element_type=jnp.float32)


def tn(a, b):
    return lax.dot_general(a, b, (((0,), (0,)), ((), ())), preferred_element_type=jnp.float32)


FAST_MESH = {"dp": 8, "seq": 4}
ANY = pl.BlockSpec(memory_space=pl.ANY)


class Place:
    def __init__(self):
        self.dp, self.z = lax.axis_index("dp"), lax.axis_index("seq")
        self.core = self.dp % 2
        self.x = (self.dp // 2) % 2
        self.y = self.dp // 4
        self.over_core = self.dp + 1 - 2 * self.core
        self.over_x = self.dp + 2 - 4 * self.x
        self.over_y = self.dp + 4 - 8 * self.y
        self.middle = (self.z == 1) | (self.z == 2)


def enter(devices):
    barrier = pltpu.get_barrier_semaphore()
    for dp, seq in devices:
        pl.semaphore_signal(
            barrier, inc=1, device_id={"dp": dp, "seq": seq}, device_id_type=pl.DeviceIdType.MESH
        )
    pl.semaphore_wait(barrier, len(devices))


def remote(src, dst, send_sem, recv_sem, dp, seq):
    return pltpu.make_async_remote_copy(
        src_ref=src,
        dst_ref=dst,
        send_sem=send_sem,
        recv_sem=recv_sem,
        device_id={"dp": dp, "seq": seq},
        device_id_type=pl.DeviceIdType.MESH,
    )


def gather_kernel(
    tokens, segments, out_grad, gains, cosine, sine, w_q, w_k, w_v, w_o, w_gate, w_up, w_down,
    x_out, seg_out, g_out, gains_out, qkv_out, o_out, ff_out, down_out,
    heads_out, lse_out, middle_out, slope_gate_out, slope_up_out, hidden_out, g_down_out, start_out,
    gain_out, normed_t_out, nf_t_out, mixed_t_out,
    send, recv, local, row_send, row_recv, row_local, gain_send, gain_recv,
    x_v, seg_v, gains_v, normed_v, w_qkv_v, heads_v, mixed_v, w_o_v, middle_v, part_send, part_recv,
    nf_v, w_ff_v, branch_v, tile_v, g_tile_v, lse_v, start_v, lse_t_v, start_row_v, gain_v, turned_v, mixed_t_v,
    part_sem, load_sem, w_sem, tile_sem, store_sem,
):
    me = Place()
    rows = tokens.shape[1]
    plane = [(lax.rem(me.dp + k, 8), me.z) for k in range(1, 8)]
    column = [
        (me.dp - me.core + core, lax.rem(me.z + k, 4)) for k in range(1, 4) for core in range(2)
    ]
    enter(plane + column)
    started = []

    def begin(copy):
        copy.start()
        started.append(copy)

    streams = ((tokens, x_out), (segments, seg_out), (out_grad, g_out))

    def place_of(ref, seq):
        return ref.at[pl.ds(rows * seq, rows)] if ref.shape[0] == 4 * rows else ref.at[seq]

    def row_copies(index):
        source, target = streams[index]
        for m in range(2):
            core, seq = me.z // 2, 2 * m + me.core
            here = (core == me.core) & (seq == me.z)

            @pl.when(here)
            def _():
                pltpu.make_async_copy(
                    source.at[m], place_of(target, me.z), row_local.at[index]
                ).start()

            @pl.when(jnp.logical_not(here))
            def _():
                remote(
                    source.at[m], place_of(target, me.z), row_send.at[index, m],
                    row_recv.at[index, me.z % 2], me.dp - me.core + core, seq,
                ).start()

    def row_wait_send(index):
        source, target = streams[index]
        for m in range(2):
            core, seq = me.z // 2, 2 * m + me.core
            here = (core == me.core) & (seq == me.z)

            @pl.when(jnp.logical_not(here))
            def _():
                remote(
                    source.at[m], place_of(target, me.z), row_send.at[index, m],
                    row_recv.at[index, me.z % 2], me.dp - me.core + core, seq,
                ).wait_send()

    def row_relay(index):
        source, target = streams[index]
        for slot in range(2):
            seq = 2 * me.core + slot
            block = place_of(target, seq)
            here = (seq == me.z) & (me.z % 2 == me.core)

            @pl.when(here)
            def _():
                pltpu.make_async_copy(block, block, row_local.at[index]).wait()

            @pl.when(jnp.logical_not(here))
            def _():
                remote(
                    block, block, row_send.at[index, slot], row_recv.at[index, slot], me.over_core, me.z
                ).wait_recv()

            begin(
                remote(
                    block, block, row_send.at[index, 2 + slot], row_recv.at[index, 2 + slot],
                    me.over_core, me.z,
                )
            )

    def row_finish(index):
        source, target = streams[index]
        for slot in range(2):
            block = place_of(target, 2 * (1 - me.core) + slot)
            remote(
                block, block, row_send.at[index, 2 + slot], row_recv.at[index, 2 + slot], me.over_core, me.z
            ).wait_recv()

    by_columns = []
    base = 0
    for source in (w_q, w_k, w_v):
        by_columns.append((source, qkv_out, base))
        base += source.shape[1] // 2
    by_columns.append((w_gate, ff_out, 0))
    by_columns.append((w_up, ff_out, w_gate.shape[1] // 2))
    by_rows = [(w_o, o_out), (w_down, down_out)]

    def column_piece(index, owner):
        source, target, first = by_columns[index]
        depth, width = source.shape[0], source.shape[1] // 2
        return target.at[pl.ds(depth * owner, depth), pl.ds(first, width)]

    def columns_start(index):
        source, target, first = by_columns[index]
        width = source.shape[1] // 2
        mine = column_piece(index, me.dp)
        for core in range(2):
            half = source.at[:, pl.ds(width * core, width)]
            begin(remote(half, mine, send.at[index, core], recv.at[index, me.core],
                         me.over_x - me.core + core, me.z))
            begin(remote(half, mine, send.at[index, 2 + core], recv.at[index, 2 + me.core],
                         me.over_y - me.core + core, me.z))

            @pl.when(core == me.core)
            def _():
                pltpu.make_async_copy(half, mine, local.at[index]).start()

            @pl.when(core != me.core)
            def _():
                remote(half, mine, send.at[index, 4], recv.at[index, 4], me.over_core, me.z).start()

    beside = me.z + 1 - 2 * lax.rem(me.z, 2)
    corner = me.over_x + me.over_y - me.dp - me.core

    def turn_of(index):
        return lax.rem(index + me.z, 2)

    last = 6

    def hand_on(index, piece, came, slot, send_slot, dp, seq):
        remote(piece, piece, send.at[index, send_slot], recv.at[index, came], dp, seq).wait_recv()
        remote(piece, piece, send.at[index, send_slot], recv.at[index, slot], dp, seq).start()

    def arrived(index, piece, slot):
        remote(piece, piece, send.at[index, 5], recv.at[index, slot], me.over_core, me.z).wait_recv()

    def left(index, piece, slot):
        remote(piece, piece, send.at[index, slot], recv.at[index, 5], me.over_core, me.z).wait_send()

    def columns_relay(index):
        @pl.when(turn_of(index) == 0)
        def _():
            hand_on(index, column_piece(index, me.over_x - me.core), 0, 5, 5, me.over_y, me.z)

        @pl.when(turn_of(index) == 1)
        def _():
            hand_on(index, column_piece(index, me.over_y - me.core + 1), 3, 6, 6, me.over_x, me.z)

    def columns_forward(index):
        @pl.when(turn_of(index) == 0)
        def _():
            hand_on(index, column_piece(index, corner), 5, 5, 6, me.dp, beside)

        @pl.when(turn_of(index) == 1)
        def _():
            hand_on(index, column_piece(index, corner + 1), 6, 6, 5, me.dp, beside)

    def columns_finish(index):
        source, target, first = by_columns[index]
        width = source.shape[1] // 2
        arrived(index, column_piece(index, me.over_x - me.core + 1), 1)
        arrived(index, column_piece(index, me.over_y - me.core), 2)
        arrived(index, column_piece(index, me.over_core), 4)

        @pl.when(turn_of(index) == 0)
        def _():
            arrived(index, column_piece(index, me.over_y - me.core + 1), 3)
            arrived(index, column_piece(index, corner + 1), 6)

        @pl.when(turn_of(index) == 1)
        def _():
            arrived(index, column_piece(index, me.over_x - me.core), 0)
            arrived(index, column_piece(index, corner), 5)

        mine = column_piece(index, me.dp)
        pltpu.make_async_copy(mine, mine, local.at[index]).wait()
        for slot in (4, 5, 6):
            left(index, mine, slot)

    def row_piece(which, owner):
        source, target = by_rows[which]
        depth = source.shape[0]
        return target.at[pl.ds(depth * lax.rem(owner, 4), depth), :]

    def rows_start(which):
        source, target = by_rows[which]
        index = 5 + which
        mine = row_piece(which, me.dp)
        begin(remote(source, mine, send.at[index, 0], recv.at[index, me.core],
                     me.over_x - me.core + me.y, me.z))
        begin(remote(source, mine, send.at[index, 1], recv.at[index, 2 + me.core],
                     me.over_y - me.core + me.y, me.z))

        @pl.when(me.core == me.y)
        def _():
            pltpu.make_async_copy(source, mine, local.at[index]).start()

        @pl.when(me.core != me.y)
        def _():
            remote(source, mine, send.at[index, 4], recv.at[index, 4], me.over_core, me.z).start()

    def rows_relay(which):
        index = 5 + which

        @pl.when((me.core == me.y) & ((index == last) | (turn_of(index) == 0)))
        def _():
            hand_on(index, row_piece(which, me.over_x - me.core), 0, 5, 5, me.over_y, me.z)

        @pl.when((me.core != me.y) & ((index == last) | (turn_of(index) == 1)))
        def _():
            hand_on(index, row_piece(which, me.over_y - me.core + 1), 3, 6, 6, me.over_x, me.z)

    def rows_forward(which):
        index = 5 + which

        @pl.when((me.core != me.y) & (turn_of(index) == 0))
        def _():
            hand_on(index, row_piece(which, corner), 5, 5, 6, me.dp, beside)

        @pl.when((me.core != me.y) & (turn_of(index) == 1))
        def _():
            hand_on(index, row_piece(which, corner + 1), 6, 6, 5, me.dp, beside)

    def rows_finish(which):
        source, target = by_rows[which]
        index = 5 + which
        mine = row_piece(which, me.dp)

        @pl.when(me.core == me.y)
        def _():
            arrived(index, row_piece(which, me.over_x - me.core + 1), 1)
            arrived(index, row_piece(which, me.over_core), 4)
            pltpu.make_async_copy(source, mine, local.at[index]).wait()

            @pl.when((index == last) | (turn_of(index) == 0))
            def _():
                left(index, mine, 5)

            @pl.when((index != last) & (turn_of(index) == 1))
            def _():
                arrived(index, row_piece(which, me.over_x - me.core), 0)

        @pl.when(me.core != me.y)
        def _():
            arrived(index, row_piece(which, me.over_y - me.core), 2)
            left(index, mine, 4)
            left(index, mine, 6)

            @pl.when((index != last) & (turn_of(index) == 0))
            def _():
                arrived(index, row_piece(which, me.over_y - me.core + 1), 3)
                arrived(index, row_piece(which, corner + 1), 6)

            @pl.when((index == last) | (turn_of(index) == 1))
            def _():
                arrived(index, row_piece(which, corner), 5)

            @pl.when(index == last)
            def _():
                arrived(index, row_piece(which, corner + 1), 6)

            @pl.when((index != last) & (turn_of(index) == 1))
            def _():
                left(index, mine, 5)

    def load(source, target, k):
        return pltpu.make_async_copy(source, target, load_sem.at[k])

    stores = []

    def store(source, target):
        copy = pltpu.make_async_copy(source, target, store_sem.at[len(stores)])
        stores.append(copy)
        copy.start()
        return copy

    length, width = x_v.shape
    own_width = width // 2
    half_ff = ff_out.shape[1] // 2

    row_copies(0)
    row_copies(1)
    for index in range(3):
        columns_start(index)
    for k in range(1, 8):
        begin(remote(gains, gains_out.at[me.dp], gain_send.at[k - 1], gain_recv.at[k - 1],
                     lax.rem(me.dp + k, 8), me.z))
    pltpu.make_async_copy(gains, gains_out.at[me.dp], gain_recv.at[7]).start()
    for index in range(3):
        columns_relay(index)
    rows_start(0)
    columns_start(3)
    row_relay(0)
    row_relay(1)
    for k in range(1, 8):
        piece = gains_out.at[lax.rem(me.dp + 8 - k, 8)]
        remote(piece, piece, gain_send.at[k - 1], gain_recv.at[k - 1], me.over_core, me.z).wait_recv()
    pltpu.make_async_copy(gains, gains_out.at[me.dp], gain_recv.at[7]).wait()
    load(gains_out, gains_v, 0).start()
    row_finish(1)
    load(seg_out, seg_v, 1).start()
    row_finish(0)
    load(x_out, x_v, 2).start()
    load(gains_out, gains_v, 0).wait()
    load(seg_out, seg_v, 1).wait()
    load(x_out, x_v, 2).wait()
    both_gains = gains_v[0].astype(jnp.float32)
    for k in range(1, 8):
        both_gains = both_gains + gains_v[k].astype(jnp.float32)
    gain_a, gain_f = both_gains[0:1], both_gains[1:2]
    gain_v[...] = both_gains
    store(gain_v, gain_out)

    norm_rows(lambda part: x_v[part, :].astype(jnp.float32), gain_a, normed_v, length)

    docs = jnp.concatenate([seg_v[k] for k in range(4)], axis=1)
    start_row = jnp.zeros((1, length), jnp.int32)
    for k in range(4):
        square = lax.broadcasted_iota(jnp.int32, (rows, rows), 0) == lax.broadcasted_iota(
            jnp.int32, (rows, rows), 1
        )
        ids = jnp.sum(jnp.where(square, seg_v[k], 0), axis=1, keepdims=True)
        start_v[pl.ds(rows * k, rows), :] = jnp.sum(
            jnp.where(docs < ids, 1, 0), axis=1, keepdims=True
        )
        start_row = start_row + jnp.sum(jnp.where(ids < docs, 1, 0), axis=0, keepdims=True)
    start_row_v[...] = start_row
    store(start_row_v, start_out)
    turn(normed_v, turned_v)
    normed_store = store(turned_v, normed_t_out)

    for index in range(3):
        columns_forward(index)
    rows_relay(0)
    columns_start(4)
    for index in range(3):
        columns_finish(index)
    tile = 256
    tiles = own_width // tile
    for t in range(tiles):
        for kind in range(3):
            part = pl.ds(own_width * kind + tile * t, tile)
            pltpu.make_async_copy(qkv_out.at[:, part], w_qkv_v.at[:, part], w_sem.at[kind, t]).start()
    def tile_step(t, carry):
        def kind_step(kind, carry):
            first = own_width * kind + tile * t
            part = pl.ds(pl.multiple_of(first, 128), tile)
            pltpu.make_async_copy(qkv_out.at[:, part], w_qkv_v.at[:, part], w_sem.at[kind, t]).wait()
            product = jnp.dot(normed_v[...], w_qkv_v[:, part], preferred_element_type=jnp.float32)
            for k in range(tile // 128):
                piece = product[:, 128 * k : 128 * k + 128]
                cols = pl.ds(pl.multiple_of(first + 128 * k, 128), 128)

                @pl.when(kind < 2)
                def _():
                    turned = piece * cosine[...] + swap_halves(piece) * sine[...]
                    heads_v[:, cols] = turned.astype(jnp.bfloat16)

                @pl.when(kind == 2)
                def _():
                    heads_v[:, cols] = piece.astype(jnp.bfloat16)

            return carry

        lax.fori_loop(0, 3, kind_step, 0)

        def pair_step(pair, carry):
            attend(pair, own_width, heads_v, start_v, mixed_v, lse_v)
            return carry

        lax.fori_loop(tile // 128 * t, tile // 128 * (t + 1), pair_step, 0)

        @pl.when(t == 0)
        def _():
            row_copies(2)

        @pl.when(t == 1)
        def _():
            rows_forward(0)
            columns_relay(3)

        return carry

    lax.fori_loop(0, tiles, tile_step, 0)
    store(heads_v, heads_out)
    lse_t_v[...] = lse_v[...].T
    store(lse_t_v, lse_out)
    turn(mixed_v, mixed_t_v)
    store(mixed_t_v, mixed_t_out)

    rows_finish(0)
    load(o_out, w_o_v, 0).start()
    load(o_out, w_o_v, 0).wait()
    chunk = width // 3

    def part_copy(k):
        part = pl.ds(chunk * k, chunk)
        return remote(
            part_send.at[:, part], part_recv.at[:, part], part_sem.at[0, k], part_sem.at[1, k], me.over_core, me.z
        )

    def out_step(n, carry):
        part = pl.ds(pl.multiple_of(tile * n, 128), tile)
        product = jnp.dot(mixed_v[...], w_o_v[:, part], preferred_element_type=jnp.float32)
        part_send[:, part] = product.astype(jnp.bfloat16)
        middle_v[:, part] = x_v[:, part].astype(jnp.float32) + product
        for k in range(3):
            @pl.when(tile * (n + 1) == chunk * (k + 1))
            def _():
                part_copy(k).start()

        return carry

    lax.fori_loop(0, width // tile, out_step, 0)
    row_relay(2)
    columns_relay(4)
    rows_start(1)
    row_finish(2)
    load(g_out, branch_v, 1).start()
    for k in range(3):
        part_copy(k).wait_recv()

    def middle_rows(part):
        value = middle_v[part, :] + part_recv[part, :].astype(jnp.float32)
        middle_v[part, :] = value
        return value

    norm_rows(middle_rows, gain_f, nf_v, length)
    store(middle_v, middle_out)
    normed_store.wait()
    turn(nf_v, turned_v)
    store(turned_v, nf_t_out)
    load(g_out, branch_v, 1).wait()
    columns_forward(3)
    columns_forward(4)
    columns_finish(3)
    columns_finish(4)

    def ff_load(n, slot, kind):
        first = pl.multiple_of(half_ff * kind + tile * n, 128)
        return pltpu.make_async_copy(
            ff_out.at[:, pl.ds(first, tile)], w_ff_v.at[slot, kind], tile_sem.at[0, slot, kind]
        )

    def tile_store(n, slot, kind):
        part = pl.ds(pl.multiple_of(tile * n, 128), tile)
        target = (slope_gate_out, slope_up_out, hidden_out)[kind]
        return pltpu.make_async_copy(tile_v.at[slot, kind], target.at[:, part], tile_sem.at[1, slot, kind])

    def grad_store(n, slot):
        part = pl.ds(pl.multiple_of(tile * n, tile), tile)
        return pltpu.make_async_copy(g_tile_v.at[slot], g_down_out.at[part, :], tile_sem.at[2, slot, 0])

    count = half_ff // tile
    for kind in range(2):
        ff_load(0, 0, kind).start()

    def ff_step(n, carry):
        slot = lax.rem(n, 2)
        for kind in range(2):
            ff_load(n, slot, kind).wait()

        @pl.when(n + 1 < count)
        def _():
            for kind in range(2):
                ff_load(n + 1, 1 - slot, kind).start()

        @pl.when(n >= 2)
        def _():
            for kind in range(3):
                tile_store(n - 2, slot, kind).wait()
            grad_store(n - 2, slot).wait()

        gate = jnp.dot(nf_v[...], w_ff_v[slot, 0], preferred_element_type=jnp.float32)
        up_value = jnp.dot(nf_v[...], w_ff_v[slot, 1], preferred_element_type=jnp.float32)
        sigma = jax.nn.sigmoid(gate)
        silu = gate * sigma
        tile_v[slot, 0] = (up_value * sigma * (1.0 + gate * (1.0 - sigma))).astype(jnp.bfloat16)
        tile_v[slot, 1] = silu.astype(jnp.bfloat16)
        hidden = (silu * up_value).astype(jnp.bfloat16)
        tile_v[slot, 2] = hidden
        g_tile_v[slot] = jnp.dot(
            hidden.T, branch_v[...], preferred_element_type=jnp.float32
        ).astype(jnp.bfloat16)
        for kind in range(3):
            tile_store(n, slot, kind).start()
        grad_store(n, slot).start()

        @pl.when(n == 0)
        def _():
            rows_relay(1)

        return carry

    lax.fori_loop(0, count, ff_step, 0)
    for n in range(count - 2, count):
        for kind in range(3):
            tile_store(n, n % 2, kind).wait()
        grad_store(n, n % 2).wait()
    rows_finish(1)
    for copy in stores:
        if copy is not normed_store:
            copy.wait()
    for k in range(3):
        part_copy(k).wait_send()
    for index in range(3):
        row_wait_send(index)
    for copy in started:
        copy.wait_send()


def turn(source, target):
    def step(k, carry):
        first = pl.multiple_of(256 * k, 256)
        target[pl.ds(first, 256), :] = source[:, pl.ds(first, 256)].T
        return carry

    lax.fori_loop(0, source.shape[1] // 256, step, 0)


def norm_rows(read, gain, target, length, step=64):
    def chunk(k, carry):
        part = pl.ds(pl.multiple_of(k * step, step), step)
        values = read(part)
        scale = lax.rsqrt(jnp.mean(values * values, axis=-1, keepdims=True) + EPS)
        target[part, :] = (values * scale * gain).astype(target.dtype)
        return carry

    lax.fori_loop(0, length // step, chunk, 0)


def attend(pair, width, heads, start, mixed, lse):
    length = heads.shape[0]
    lane = lax.broadcasted_iota(jnp.int32, (BLK, 128), 1)
    cols = [pl.ds(pl.multiple_of(width * kind + 128 * pair, 128), 128) for kind in range(3)]
    for i in range(length // BLK):
        own_rows, keys = slice(BLK * i, BLK * (i + 1)), BLK * (i + 1)
        place = lax.broadcasted_iota(jnp.int32, (BLK, keys), 1)
        own = BLK * i + lax.broadcasted_iota(jnp.int32, (BLK, keys), 0)
        allowed = (place >= start[own_rows, :]) & (place <= own)
        query = heads[own_rows, cols[0]] * jnp.bfloat16(0.125)
        key, value = heads[0:keys, cols[1]], heads[0:keys, cols[2]]
        kept = lse[own_rows, :]
        outs = []
        for half in range(2):
            part = slice(64 * half, 64 * half + 64)
            scores = jnp.where(allowed, nt(query[:, part], key[:, part]), -1e30)
            peak = jnp.max(scores, axis=-1, keepdims=True)
            expo = jnp.exp(scores - peak)
            total = jnp.sum(expo, axis=-1, keepdims=True)
            out = jnp.dot(expo.astype(jnp.bfloat16), value[:, part], preferred_element_type=jnp.float32)
            outs.append((out / total).astype(jnp.bfloat16))
            kept = jnp.where(lane == 2 * pair + half, peak + jnp.log(total), kept)
        mixed[own_rows, cols[0]] = jnp.concatenate(outs, axis=1)
        lse[own_rows, :] = kept


def gather_all(tokens, segments, out_grad, gains, cosine, sine, weights):
    rows, width = tokens.shape[1], tokens.shape[2]
    length, half, ff = 4 * rows, width // 2, weights[4].shape[1]
    half_ff = ff // 2
    low = jnp.bfloat16

    def shape(*dims, dtype=low):
        return jax.ShapeDtypeStruct(dims, dtype)

    shapes = [
        shape(length, width),
        shape(4, *segments.shape[1:], dtype=jnp.int32),
        shape(length, width),
        shape(8, *gains.shape),
        shape(width, 3 * half),
        shape(half, width),
        shape(width, ff),
        shape(half_ff, width),
        shape(length, 3 * half),
        shape(128, length, dtype=jnp.float32),
        shape(length, width, dtype=jnp.float32),
        shape(length, half_ff),
        shape(length, half_ff),
        shape(length, half_ff),
        shape(half_ff, width),
        shape(1, length, dtype=jnp.int32),
        shape(2, width, dtype=jnp.float32),
        shape(width, length),
        shape(width, length),
        shape(half, length),
    ]
    dma, vmem = pltpu.SemaphoreType.DMA, pltpu.VMEM
    whole = pl.BlockSpec(memory_space=pltpu.VMEM)
    return pl.pallas_call(
        gather_kernel,
        in_specs=[ANY] * 4 + [whole] * 2 + [ANY] * 7,
        out_specs=[ANY] * len(shapes),
        out_shape=shapes,
        scratch_shapes=[
            dma((7, 7)), dma((7, 7)), dma((7,)), dma((3, 4)), dma((3, 4)), dma((3,)), dma((7,)), dma((8,)),
            vmem((length, width), low),
            vmem((4,) + segments.shape[1:], jnp.int32),
            vmem((8,) + gains.shape, low),
            vmem((length, width), low),
            vmem((width, 3 * half), low),
            vmem((length, 3 * half), low),
            vmem((length, half), low),
            vmem((half, width), low),
            vmem((length, width), jnp.float32),
            vmem((length, width), low),
            vmem((length, width), low),
            vmem((length, width), low),
            vmem((2, 2, width, 256), low),
            vmem((length, width), low),
            vmem((2, 3, length, 256), low),
            vmem((2, 256, width), low),
            vmem((length, 128), jnp.float32),
            vmem((length, 1), jnp.int32),
            vmem((128, length), jnp.float32),
            vmem((1, length), jnp.int32),
            vmem((2, width), jnp.float32),
            vmem((width, length), low),
            vmem((half, length), low),
            dma((2, 3)), dma((3,)), dma((3, 3)), dma((3, 2, 3)), dma((9,)),
        ],
        compiler_params=pltpu.CompilerParams(
            collective_id=0, has_side_effects=True, vmem_limit_bytes=61 * 1024 * 1024
        ),
        cost_estimate=pl.CostEstimate(flops=0, bytes_accessed=500_000_000, transcendentals=0),
        name="gather_all",
    )(tokens, segments, out_grad, gains, cosine, sine, *weights)


def guard(condition, action):
    if isinstance(condition, (bool, np.bool_)):
        if condition:
            action()
    else:
        pl.when(condition)(action)


def everything(*conditions):
    known = [c for c in conditions if isinstance(c, (bool, np.bool_))]
    if not all(known):
        return False
    rest = [c for c in conditions if not isinstance(c, (bool, np.bool_))]
    if not rest:
        return True
    total = rest[0]
    for c in rest[1:]:
        total = total & c
    return total


def chunk_of(rows):
    return 384 if rows % 384 == 0 else 512


def add_rows(target, first, other, rows):
    step = chunk_of(rows)

    def chunk(k, carry):
        at = pl.multiple_of(k * step, step)
        source = pl.multiple_of(first + k * step, step)
        target[pl.ds(at, step), :] += other[pl.ds(source, step), :]
        return carry

    lax.fori_loop(0, rows // step, chunk, 0)


JOB = 256


class Stream:
    active = True

    def tick(self, t):
        for late, stage in reversed(self.stages):
            k = t - late
            guard(everything(k >= 0, k < self.count), functools.partial(stage, k))

    @property
    def ticks(self):
        return self.count + self.stages[-1][0]

    def slot(self, k):
        return k % self.slots if isinstance(k, int) else lax.rem(k, self.slots)

    def column(self, k, base=0):
        return pl.ds(pl.multiple_of(base + JOB * k, 128), JOB)

    def total(self, k):
        return self.second.at[self.slot(k)]

    def final(self, k):
        return self.got.at[self.slot(k), pl.ds(0, self.rows)]

    def seq_copy(self, k, step):
        me, slot, sem = self.me, self.slot(k), self.seq_sem
        inner = me.z + 1 - 2 * (me.z // 2)
        opposite = 3 - me.z
        outer = 3 * (me.z // 2)
        if step == 0:
            return remote(self.total(k), self.over.at[slot, 0], sem.at[slot, 0, 0], sem.at[slot, 1, 0], me.dp, inner)
        if step == 1:
            return remote(
                self.total(k), self.over.at[slot, 1], sem.at[slot, 0, 1], sem.at[slot, 1, 1], me.dp, opposite
            )
        return remote(self.final(k), self.final(k), sem.at[slot, 0, 2], sem.at[slot, 1, 2], me.dp, outer)

    def plane_and_ends(self, k):
        self.reduce_plane(k)
        guard(
            everything(self.active, jnp.logical_not(self.me.middle)),
            lambda: self.seq_copy(k, 0).start(),
        )

    def across(self, k):
        def action():
            self.seq_copy(k, 0).wait_recv()
            add_rows(self.total(k), 0, self.over.at[self.slot(k), 0], self.rows)
            self.seq_copy(k, 1).start()

        guard(everything(self.active, self.me.middle), action)

    def back(self, k):
        def action():
            self.seq_copy(k, 1).wait_recv()
            final, total, over = self.final(k), self.total(k), self.over.at[self.slot(k), 1]
            step = chunk_of(self.rows)

            def chunk(at, carry):
                part = pl.ds(pl.multiple_of(at * step, step), step)
                final[part, :] = total[part, :] + over[part, :]
                return carry

            lax.fori_loop(0, self.rows // step, chunk, 0)
            self.seq_copy(k, 2).start()

        guard(everything(self.active, self.me.middle), action)

    def finish(self, k):
        guard(
            everything(self.active, jnp.logical_not(self.me.middle)),
            lambda: self.seq_copy(k, 2).wait_recv(),
        )
        self.output(k)

    def drain(self, k):
        self.drain_plane(k)

        def ends():
            self.seq_copy(k, 0).wait_send()

        def middles():
            self.seq_copy(k, 1).wait_send()
            self.seq_copy(k, 2).wait_send()

        guard(everything(self.active, jnp.logical_not(self.me.middle)), ends)
        guard(everything(self.active, self.me.middle), middles)


class ColumnStream(Stream):
    def __init__(self, me, source, target, ff_jobs, d_model, ff, refs):
        self.me, self.source, self.target = me, source, target
        self.got, self.keep, self.second, self.over, self.sem, self.seq_sem, self.credit = refs
        self.slots, self.rows = self.got.shape[0], source.shape[0] // 4
        self.count, self.ff_jobs = source.shape[1] // JOB, ff_jobs
        self.ff, self.d_model = ff, d_model
        self.stages = (
            *zip(LATE["C"], (self.pass_second, self.plane_and_ends, self.across, self.back, self.finish, self.drain)),
        )

    def x_first(self, k):
        late = k // self.ff_jobs
        return (1 - late) * ((k + self.ff_jobs // 2 - 2) // self.ff_jobs) * ((k + 1) % 2) + late * (k % 2)

    def first_copy(self, k, part):
        me, slot, x_first = self.me, self.slot(k), self.x_first(k)
        block = x_first * (2 * part + 1 - me.x) + (1 - x_first) * (2 * (1 - me.y) + part)
        sent = self.source.at[pl.ds(pl.multiple_of(self.rows * block, self.rows), self.rows), self.column(k)]
        to = x_first * me.over_x + (1 - x_first) * me.over_y
        return remote(
            sent, self.got.at[slot, pl.ds(self.rows * part, self.rows)],
            self.sem.at[slot, 0, part], self.sem.at[slot, 1, part], to, me.z,
        )

    def keep_copy(self, k, part):
        me, slot, x_first = self.me, self.slot(k), self.x_first(k)
        block = x_first * (2 * part + me.x) + (1 - x_first) * (2 * me.y + part)
        kept = self.source.at[pl.ds(pl.multiple_of(self.rows * block, self.rows), self.rows), self.column(k)]
        return pltpu.make_async_copy(
            kept, self.keep.at[slot, pl.ds(self.rows * part, self.rows)], self.sem.at[slot, 2, part]
        )

    def at(self, k):
        x_first = self.x_first(k)
        return x_first * self.me.y + (1 - x_first) * self.me.x

    def second_copy(self, k):
        me, slot, x_first = self.me, self.slot(k), self.x_first(k)
        row = pl.multiple_of(self.rows * (1 - self.at(k)), self.rows)
        to = x_first * me.over_y + (1 - x_first) * me.over_x
        return remote(
            self.keep.at[slot, pl.ds(row, self.rows)], self.second.at[slot],
            self.sem.at[slot, 0, 2], self.sem.at[slot, 1, 2], to, me.z,
        )

    def start(self, k):
        def credits():
            slot = self.slot(k)

            @pl.when(self.me.middle)
            def _():
                pl.semaphore_wait(self.credit.at[slot], 5)

            @pl.when(jnp.logical_not(self.me.middle))
            def _():
                pl.semaphore_wait(self.credit.at[slot], 4)

        guard(k >= self.slots, credits)
        for part in range(2):
            self.first_copy(k, part).start()
            self.keep_copy(k, part).start()

    def pass_second(self, k):
        for part in range(2):
            self.keep_copy(k, part).wait()
            self.first_copy(k, part).wait_recv()
        slot = self.slot(k)
        add_rows(self.keep.at[slot], 0, self.got.at[slot], 2 * self.rows)
        self.second_copy(k).start()

    def reduce_plane(self, k):
        self.second_copy(k).wait_recv()
        add_rows(self.total(k), self.rows * self.at(k), self.keep.at[self.slot(k)], self.rows)

    def out_column(self, k, core, late):
        if late:
            m, half = k - self.ff_jobs, self.d_model // 2
            tiles = half // JOB
            first = 2 * self.ff + self.d_model * (m // tiles) + JOB * (m % tiles) + half * core
        else:
            first = self.ff * (k % 2) + JOB * (k // 2) + self.ff // 2 * core
        return self.target.at[:, pl.ds(pl.multiple_of(first, 128), JOB)]

    def last_copy(self, k, late=False):
        me, slot, rows = self.me, self.slot(k), self.rows // 2
        part = self.got.at[slot, pl.ds(pl.multiple_of(rows * (1 - me.core), rows), rows)]
        return remote(
            part, self.out_column(k, me.core, late), self.sem.at[slot, 0, 3], self.sem.at[slot, 1, 3],
            me.over_core, me.z,
        )

    def own_copy(self, k, late=False):
        me, slot, rows = self.me, self.slot(k), self.rows // 2
        part = self.got.at[slot, pl.ds(pl.multiple_of(rows * me.core, rows), rows)]
        return pltpu.make_async_copy(part, self.out_column(k, me.core, late), self.sem.at[slot, 2, 0])

    def output(self, k):
        def begin(late):
            self.last_copy(k, late).start()
            self.own_copy(k, late).start()

        guard(k < self.ff_jobs, lambda: begin(False))
        guard(k >= self.ff_jobs, lambda: begin(True))

    def drain_plane(self, k):
        for part in range(2):
            self.first_copy(k, part).wait_send()
        self.second_copy(k).wait_send()

        def end(late):
            self.last_copy(k, late).wait()
            self.own_copy(k, late).wait()

        guard(k < self.ff_jobs, lambda: end(False))
        guard(k >= self.ff_jobs, lambda: end(True))

    def drain(self, k):
        super().drain(k)

        def signal(dp, seq):
            pl.semaphore_signal(
                self.credit.at[self.slot(k)], inc=1, device_id={"dp": dp, "seq": seq},
                device_id_type=pl.DeviceIdType.MESH,
            )

        def free():
            me = self.me
            for dp in (me.over_core, me.over_x, me.over_y):
                signal(dp, me.z)

            @pl.when(me.middle)
            def _():
                signal(me.dp, 3 - me.z)
                signal(me.dp, 3 * (me.z // 2))

            @pl.when(jnp.logical_not(me.middle))
            def _():
                signal(me.dp, me.z + 1 - 2 * (me.z // 2))

        guard(k + self.slots < self.count, free)


class RowStream(Stream):
    def __init__(self, me, source, target, lates, refs):
        self.me, self.source, self.target = me, source, target
        self.got, self.second, self.over, self.stage, self.sem, self.seq_sem = refs
        self.slots, self.rows = self.got.shape[0], source.shape[0] // 2
        self.count = source.shape[1] // JOB
        self.active = me.core == me.y
        steps = (self.pass_second, self.plane_and_ends, self.across, self.back, self.finish, self.drain)
        self.stages = tuple(zip(lates, steps))

    def first_copy(self, k):
        me, slot = self.me, self.slot(k)
        sent = self.source.at[pl.ds(pl.multiple_of(self.rows * (1 - me.x), self.rows), self.rows), self.column(k)]
        return remote(sent, self.got.at[slot], self.sem.at[slot, 0, 0], self.sem.at[slot, 1, 0], me.over_x, me.z)

    def load_copy(self, k):
        kept = self.source.at[
            pl.ds(pl.multiple_of(self.rows * self.me.x, self.rows), self.rows), self.column(k)
        ]
        return pltpu.make_async_copy(kept, self.stage, self.sem.at[self.slot(k), 2, 0])

    def second_copy(self, k):
        me, slot = self.me, self.slot(k)
        return remote(
            self.got.at[slot], self.second.at[slot], self.sem.at[slot, 0, 2], self.sem.at[slot, 1, 2],
            me.over_y, me.z,
        )

    def start(self, k):
        self.first_copy(k).start()
        guard(k == 0, lambda: self.load_copy(k).start())

    def pass_second(self, k):
        self.load_copy(k).wait()
        self.first_copy(k).wait_recv()
        add_rows(self.got.at[self.slot(k)], 0, self.stage, self.rows)
        guard(k + 1 < self.count, lambda: self.load_copy(k + 1).start())
        guard(jnp.logical_not(self.active), lambda: self.second_copy(k).start())

    def reduce_plane(self, k):
        def action():
            self.second_copy(k).wait_recv()
            add_rows(self.total(k), 0, self.got.at[self.slot(k)], self.rows)

        guard(self.active, action)

    def last_copy(self, k):
        me, slot, rows = self.me, self.slot(k), self.rows // 2
        part = self.got.at[slot, pl.ds(pl.multiple_of(rows * (1 - me.core), rows), rows)]
        return remote(
            part, self.target.at[:, self.column(k)], self.sem.at[slot, 0, 3], self.sem.at[slot, 1, 3],
            me.over_core, me.z,
        )

    def own_copy(self, k):
        me, slot, rows = self.me, self.slot(k), self.rows // 2
        part = self.got.at[slot, pl.ds(pl.multiple_of(rows * me.core, rows), rows)]
        return pltpu.make_async_copy(part, self.target.at[:, self.column(k)], self.sem.at[slot, 2, 1])

    def output(self, k):
        def action():
            self.last_copy(k).start()
            self.own_copy(k).start()

        guard(self.active, action)

    def drain_plane(self, k):
        self.first_copy(k).wait_send()

        def active():
            self.last_copy(k).wait_send()
            self.own_copy(k).wait()

        def passive():
            self.second_copy(k).wait_send()
            self.last_copy(k).wait_recv()

        guard(self.active, active)
        guard(jnp.logical_not(self.active), passive)


PLAN = {
    "s0": {"E": (0, 3)},
    "a": {"E": (3, 4, 4, 5, 5, 5, 6, 6, 6), "S": (0, 1, 2, 3, 3, 5, 5, 5, 5), "C": (0, 0, 0, 0, 0, 1, 1, 2, 2), "D": (0, 0, 0, 0, 1, 1, 1, 1, 1)},
    "l0": {"D": (1, 2)},
    "l1": {"S": (5, 6), "D": (2, 3)},
    "l2": {"S": (6, 8)},
    "i": {"S": (8, 8, 8, 8, 9, 9, 10), "C": (2, 2, 2, 2, 3, 3, 3), "D": (3, 3, 3, 3, 4, 4, 4)},
    "n0": {"S": (10, 12), "C": (3, 5)},
    "n1": {"C": (5, 6)},
    "n2": {"C": (8, 9)},
    "o": {"C": (6, 7, 7, 7, 8, 8, 8), "D": (4, 4, 4, 4, 4, 4, 5)},
    "h": {"S": (12, 13, 13, 14, 14, 15, 15), "C": (9, 10, 11, 12, 13, 13, 13), "D": (5, 6, 7, 7, 7, 8, 9)},
    "t": {"S": (15, 16, 16, 16, 16, 16, 16), "F": (0, 0, 1, 1, 2, 3, 3), "C": (13, 14, 14, 15, 15, 15, 16), "D": (9, 10, 10, 10, 10, 10, 11)},
    "t6": {"F": (3, 4)},
    "p": {"S": (16, 16, 17, 18, 19, 20, 20, 20, 20, 20), "O": (0, 0, 1, 1, 1, 2, 3, 3, 3, 3)},
    "p9": {},
}
LATE = {"C": (0, 2, 4, 6, 7, 8), "D": (0, 2, 4, 6, 7, 8), "O": (0, 2, 4, 6, 7, 8)}


class Pace:
    def __init__(self, cols, downs, outs):
        self.actions = {
            "E": downs.start, "S": cols.start, "F": outs.start, "C": cols.tick, "D": downs.tick, "O": outs.tick,
        }

    def at(self, place, n=0):
        for kind, bounds in PLAN[place].items():
            action = self.actions[kind]

            def one(t, carry, action=action):
                action(t)
                return carry

            if isinstance(n, int):
                low, high = bounds[n], bounds[n + 1]
                if high - low == 1:
                    action(low)
                elif high > low:
                    lax.fori_loop(low, high, one, 0)
                continue
            low, high = bounds[0], bounds[1]
            for k in range(1, len(bounds) - 1):
                reached = (n + 32 - k) // 32
                low = low + (bounds[k] - bounds[k - 1]) * reached
                high = high + (bounds[k + 1] - bounds[k]) * reached
            lax.fori_loop(low, high, one, 0)


GAIN_HOPS = 5


class GainSums:
    def __init__(self, me, target, buffer, sem):
        self.me, self.target, self.buffer, self.sem = me, target, buffer, sem

    def hop(self, k):
        me = self.me
        across = me.z + 2 - 4 * (me.z // 2)
        beside = me.z + 1 - 2 * (me.z % 2)
        dp = (me.over_core, me.over_x, me.over_y, me.dp, me.dp)[k]
        seq = (me.z, me.z, me.z, beside, across)[k]
        return remote(
            self.buffer.at[k, 0], self.buffer.at[k, 1], self.sem.at[0, k], self.sem.at[1, k], dp, seq
        )

    def start(self):
        self.hop(0).start()

    def step(self, k):
        self.hop(k).wait_recv()
        total = self.buffer[k, 0] + self.buffer[k, 1]
        if k + 1 < GAIN_HOPS:
            self.buffer[k + 1, 0] = total
            self.hop(k + 1).start()
        else:
            self.target[...] = total

    def drain(self):
        for k in range(GAIN_HOPS):
            self.hop(k).wait_send()


class RowsBack:
    def __init__(self, me, source, target, sem):
        self.me, self.source, self.target, self.sem = me, source, target, sem

    def each(self, local, elsewhere):
        me = self.me
        rows = self.source.shape[0] // 2
        for slot in range(2):
            core, seq = me.z % 2, 2 * me.core + slot
            here = (core == me.core) & (seq == me.z)
            block, target = self.source.at[pl.ds(rows * slot, rows)], self.target.at[me.z // 2]

            @pl.when(here)
            def _():
                local(pltpu.make_async_copy(block, target, self.sem.at[2, 0]))

            @pl.when(jnp.logical_not(here))
            def _():
                elsewhere(
                    remote(
                        block, target, self.sem.at[0, slot], self.sem.at[1, me.z // 2],
                        me.dp - me.core + core, seq,
                    )
                )

    def start(self):
        self.each(lambda copy: copy.start(), lambda copy: copy.start())

    def drain(self):
        me = self.me
        self.each(lambda copy: copy.wait(), lambda copy: copy.wait_send())
        rows = self.source.shape[0] // 2
        for m in range(2):
            here = (me.z == 2 * m + me.core) & (me.core == me.z // 2)

            @pl.when(jnp.logical_not(here))
            def _():
                remote(
                    self.source.at[pl.ds(0, rows)], self.target.at[m], self.sem.at[0, 0],
                    self.sem.at[1, m], me.over_core, me.z,
                ).wait_recv()


def attend_back(pair, width, heads, grad_mixed, start, lse, grads, key_sum, value_sum, query_sum, cosine, sine):
    length = heads.shape[0]
    cols = [pl.ds(pl.multiple_of(width * kind + 128 * pair, 128), 128) for kind in range(3)]
    key_sum[...] = jnp.zeros_like(key_sum)
    value_sum[...] = jnp.zeros_like(value_sum)
    for i in range(length // BLK):
        own_rows, keys = slice(BLK * i, BLK * (i + 1)), BLK * (i + 1)
        place = lax.broadcasted_iota(jnp.int32, (keys, BLK), 0)
        own = BLK * i + lax.broadcasted_iota(jnp.int32, (keys, BLK), 1)
        allowed = (place >= start[:, own_rows]) & (place <= own)
        query = heads[own_rows, cols[0]] * jnp.bfloat16(0.125)
        key, value = heads[0:keys, cols[1]], heads[0:keys, cols[2]]
        grad = grad_mixed[own_rows, cols[0]]
        for half in range(2):
            part = slice(64 * half, 64 * half + 64)
            scores = nt(key[:, part], query[:, part])
            logsum = lse[pl.ds(2 * pair + half, 1), own_rows]
            probs = jnp.where(allowed, jnp.exp(scores - logsum), 0.0)
            grad_probs = nt(value[:, part], grad[:, part])
            inner = jnp.sum(probs * grad_probs, axis=0, keepdims=True)
            grad_scores = (probs * (grad_probs - inner)).astype(jnp.bfloat16)
            value_sum[0:keys, part] += dot(probs.astype(jnp.bfloat16), grad[:, part])
            key_sum[0:keys, part] += dot(grad_scores, query[:, part])
            query_sum[own_rows, part] = tn(grad_scores, key[:, part]) * 0.125
    for kind, total in enumerate((query_sum, key_sum)):
        value = total[...]
        grads[:, cols[kind]] = (value * cosine[...] - swap_halves(value) * sine[...]).astype(jnp.bfloat16)
    grads[:, cols[2]] = value_sum[...].astype(jnp.bfloat16)


def backward_kernel(
    branch_h, slope_gate_h, slope_up_h, hidden_h, nf_t_h, normed_t_h, mixed_t_h, heads_h, lse_h, middle_h, x_h,
    g_down_h, w_qkv_h, w_o_h, w_ff_h, w_down_h, start_ref, gain_ref, cosine, sine,
    out_o, tokens_o, cols_o, o_o, down_o, gains_o, g_cols_h, g_o_h, kept_h, rows_h, grad_nf_h,
    col_got, col_keep, col_second, col_over, col_sem, col_seq, col_credit,
    down_got, down_second, down_over, down_stage, down_sem, down_seq,
    o_got, o_second, o_over, o_stage, o_sem, o_seq,
    wide_recv, half_recv, half_free, wide_sem, half_sem,
    gain_buffer, gain_sem, row_sem, load_sem, tile_sem, store_sem,
):
    me = Place()
    enter(
        [(me.over_core, me.z), (me.over_x, me.z), (me.over_y, me.z)]
        + [(me.dp - me.core + core, lax.rem(me.z + k, 4)) for k in range(1, 4) for core in range(2)]
    )
    length, width = branch_h.shape
    half_rows, own_width, half_ff = length // 2, width // 2, slope_gate_h.shape[1]
    bf16, f32 = jnp.bfloat16, jnp.float32
    vmem = pltpu.VMEM
    ff_jobs = 2 * half_ff // JOB
    cols = ColumnStream(
        me, g_cols_h, cols_o, ff_jobs, width, 2 * half_ff,
        (col_got, col_keep, col_second, col_over, col_sem, col_seq, col_credit),
    )
    downs = RowStream(
        me, g_down_h, down_o, LATE["D"], (down_got, down_second, down_over, down_stage, down_sem, down_seq)
    )
    outs = RowStream(me, g_o_h, o_o, LATE["O"], (o_got, o_second, o_over, o_stage, o_sem, o_seq))
    back_out = RowsBack(me, rows_h.at[0], out_o, row_sem.at[0])
    back_tokens = RowsBack(me, rows_h.at[1], tokens_o, row_sem.at[1])
    gains = GainSums(me, gains_o, gain_buffer, gain_sem)

    def load(source, target, k=0):
        return pltpu.make_async_copy(source, target, load_sem.at[k])

    def fetch(*pairs):
        for k, (source, target) in enumerate(pairs):
            load(source, target, k).start()
        for k, (source, target) in enumerate(pairs):
            load(source, target, k).wait()

    def lanes(n, size=JOB, base=0):
        return pl.ds(pl.multiple_of(base + size * n, 128), size)

    def sublanes(n, size):
        return pl.ds(pl.multiple_of(n * size, size), size)

    def grad_store(buffer, slot, target, n, k):
        return pltpu.make_async_copy(buffer.at[slot], target.at[:, lanes(n)], store_sem.at[slot, k])

    pace = Pace(cols, downs, outs)
    pace.at("s0")

    def feed_forward(grad_ff):
        steps = half_ff // JOB

        def hidden_grads(branch, w_tile, slopes, nf_t, g_tile):
            def tile_loads(n, slot):
                return (
                    pltpu.make_async_copy(w_down_h.at[sublanes(n, JOB), :], w_tile.at[slot], tile_sem.at[slot, 0]),
                    pltpu.make_async_copy(slope_gate_h.at[:, lanes(n)], slopes.at[slot, 0], tile_sem.at[slot, 1]),
                    pltpu.make_async_copy(slope_up_h.at[:, lanes(n)], slopes.at[slot, 1], tile_sem.at[slot, 2]),
                )

            for copy in tile_loads(0, 0):
                copy.start()
            fetch((branch_h, branch), (nf_t_h, nf_t))

            def step(n, carry):
                slot = lax.rem(n, 2)
                for copy in tile_loads(n, slot):
                    copy.wait()

                @pl.when(n + 1 < steps)
                def _():
                    for copy in tile_loads(n + 1, 1 - slot):
                        copy.start()

                grad_hidden = nt(branch[...], w_tile[slot])

                @pl.when(n > 1)
                def _():
                    for kind in range(2):
                        grad_store(g_tile, kind, g_cols_h, 2 * n - 2 + kind, 0).wait()

                for kind in range(2):
                    grad = (grad_hidden * slopes[slot, kind].astype(f32)).astype(bf16)
                    grad_ff[:, lanes(n, JOB, half_ff * kind)] = grad
                    g_tile[kind] = dot(nf_t[...], grad).astype(bf16)
                    grad_store(g_tile, kind, g_cols_h, 2 * n + kind, 0).start()

                @pl.when(n == 0)
                def _():
                    for kind in range(2):
                        grad_store(g_tile, kind, g_cols_h, kind, 0).wait()

                pace.at("a", n)

                return carry

            lax.fori_loop(0, steps, step, 0)
            for kind in range(2):
                grad_store(g_tile, kind, g_cols_h, 2 * steps - 2 + kind, 0).wait()

        pl.run_scoped(
            hidden_grads, vmem((length, width), bf16), vmem((2, JOB, width), bf16),
            vmem((2, 2, length, JOB), bf16), vmem((width, length), bf16), vmem((2, width, JOB), bf16),
        )

        def layer_out(hidden, w_down, send, total):
            other, own = 1 - me.core, me.core
            fetch((w_down_h, w_down), (hidden_h.at[sublanes(other, half_rows), :], hidden))
            load(middle_h.at[sublanes(own, half_rows), :], total, 2).start()

            def other_tile(n, carry):
                send[:, lanes(n)] = dot(hidden[...], w_down[:, lanes(n)]).astype(bf16)
                return carry

            lax.fori_loop(0, width // JOB, other_tile, 0)
            exchange = remote(send, half_recv, half_sem.at[0, 0], half_sem.at[1, 0], me.over_core, me.z)
            exchange.start()
            pace.at("l0")
            fetch((hidden_h.at[sublanes(own, half_rows), :], hidden))
            load(middle_h.at[sublanes(own, half_rows), :], total, 2).wait()

            def own_tile(n, carry):
                total[:, lanes(n)] += dot(hidden[...], w_down[:, lanes(n)])
                return carry

            lax.fori_loop(0, width // JOB, own_tile, 0)
            pace.at("l1")
            exchange.wait()

            def combine(k, carry):
                part = sublanes(k, 64)
                send[part, :] = (total[part, :] + half_recv[part, :].astype(f32)).astype(bf16)
                return carry

            lax.fori_loop(0, half_rows // 64, combine, 0)
            pl.semaphore_signal(
                half_free, inc=1, device_id={"dp": me.over_core, "seq": me.z},
                device_id_type=pl.DeviceIdType.MESH,
            )
            fetch((send, rows_h.at[0]))

        pl.run_scoped(
            layer_out, vmem((half_rows, half_ff), bf16), vmem((half_ff, width), bf16),
            vmem((half_rows, width), bf16), vmem((half_rows, width), f32),
        )
        back_out.start()
        pace.at("l2")

    chunk = 2 * JOB
    chunks = width // chunk

    def wide_copy(send, k):
        part = pl.ds(chunk * k, chunk)
        return remote(
            send.at[:, part], wide_recv.at[:, part], wide_sem.at[0, k], wide_sem.at[1, k], me.over_core, me.z
        )

    def with_grad_ff(grad_ff):
        feed_forward(grad_ff)

        def input_grads(w_tile, send, parts):
            def tile_load(n, kind):
                return pltpu.make_async_copy(
                    w_ff_h.at[sublanes(n, JOB), pl.ds(half_ff * kind, half_ff)], w_tile.at[kind],
                    tile_sem.at[kind, 0],
                )

            def part_store(n, slot):
                return pltpu.make_async_copy(parts.at[slot], grad_nf_h.at[:, lanes(n)], store_sem.at[slot, 0])

            for kind in range(2):
                tile_load(0, kind).start()
            count = width // JOB

            def step(n, carry):
                slot = lax.rem(n, 2)
                tile_load(n, 0).wait()
                part = nt(grad_ff[:, 0:half_ff], w_tile[0])

                @pl.when(n + 1 < count)
                def _():
                    tile_load(n + 1, 0).start()

                tile_load(n, 1).wait()
                part = part + nt(grad_ff[:, half_ff : 2 * half_ff], w_tile[1])

                @pl.when(n + 1 < count)
                def _():
                    tile_load(n + 1, 1).start()

                @pl.when(n >= 2)
                def _():
                    part_store(n - 2, slot).wait()

                parts[slot] = part
                part_store(n, slot).start()
                send[:, lanes(n)] = part.astype(bf16)
                for k in range(chunks):
                    @pl.when(n == 2 * k + 1)
                    def _():
                        wide_copy(send, k).start()

                pace.at("i", n)

                return carry

            lax.fori_loop(0, count, step, 0)
            for n in range(count - 2, count):
                part_store(n, n % 2).wait()
            pace.at("n0")
            for k in range(chunks):
                wide_copy(send, k).wait()

        pl.run_scoped(
            input_grads, vmem((2, JOB, half_ff), bf16), vmem((length, width), bf16), vmem((2, length, JOB), f32)
        )

    pl.run_scoped(with_grad_ff, vmem((length, 2 * half_ff), bf16))

    def to_attention(grad_attn):
        def norm_back(grad_nf, middle, branch):
            fetch((middle_h, middle), (branch_h, branch), (grad_nf_h, grad_nf))
            gain = gain_ref[1:2, :]

            def rows(k, total):
                part = sublanes(k, 64)
                grad = grad_nf[part, :] + wide_recv[part, :].astype(f32)
                gained, values = norm_rows_back(middle[part, :], gain, grad)
                values = values + branch[part, :].astype(f32)
                grad_nf[part, :] = values
                grad_attn[part, :] = values.astype(bf16)
                return total + gained

            total = lax.fori_loop(0, length // 64, rows, jnp.zeros((1, width), f32))
            gain_buffer[0, 0, 1:2, :] = 0.5 * total
            kept = load(grad_nf.at[sublanes(me.core, half_rows), :], kept_h, 0)
            kept.start()
            pace.at("n1")
            kept.wait()

        pl.run_scoped(
            norm_back, vmem((length, width), f32), vmem((length, width), f32), vmem((length, width), bf16)
        )

        def out_projection(w_o, mixed_t, g_tile, grad_mixed):
            fetch((w_o_h, w_o), (mixed_t_h, mixed_t))

            def mixed_step(n, carry):
                grad_mixed[:, lanes(n)] = nt(grad_attn[...], w_o[sublanes(n, JOB), :]).astype(bf16)
                return carry

            lax.fori_loop(0, own_width // JOB, mixed_step, 0)
            placed = load(grad_mixed, wide_recv.at[:, pl.ds(0, own_width)], 3)
            placed.start()
            count = width // JOB

            def step(n, carry):
                slot = lax.rem(n, 2)

                @pl.when(n >= 2)
                def _():
                    grad_store(g_tile, slot, g_o_h, n - 2, 1).wait()

                g_tile[slot] = dot(mixed_t[...], grad_attn[:, lanes(n)]).astype(bf16)
                grad_store(g_tile, slot, g_o_h, n, 1).start()

                pace.at("o", n)

                return carry

            lax.fori_loop(0, count, step, 0)
            for n in range(count - 2, count):
                grad_store(g_tile, n % 2, g_o_h, n, 1).wait()
            placed.wait()

        pl.run_scoped(
            out_projection, vmem((own_width, width), bf16), vmem((own_width, length), bf16),
            vmem((2, own_width, JOB), bf16), vmem((length, own_width), bf16),
        )

    pl.run_scoped(to_attention, vmem((length, width), bf16))
    pace.at("n2")

    def attention(grads):
        def heads_back(heads, lse, key_sum, value_sum, query_sum):
            fetch((heads_h, heads), (lse_h, lse))

            def step(pair, carry):
                attend_back(
                    pair, own_width, heads, wide_recv, start_ref, lse, grads, key_sum, value_sum, query_sum, cosine, sine
                )
                pace.at("h", pair)
                return carry

            lax.fori_loop(0, own_width // 128, step, 0)

        pl.run_scoped(
            heads_back, vmem((length, 3 * own_width), bf16), vmem((128, length), f32),
            *[vmem((length, 128), f32)] * 3,
        )

        def tokens_back(w_tile, send, total, x_rows, kept):
            def tile_load(n, slot):
                return pltpu.make_async_copy(w_qkv_h.at[sublanes(n, JOB), :], w_tile.at[slot], tile_sem.at[slot, 0])

            tile_load(0, 0).start()
            load(x_h.at[sublanes(me.core, half_rows), :], x_rows, 0).start()
            load(kept_h, kept, 1).start()
            count = width // JOB

            def step(n, carry):
                slot = lax.rem(n, 2)
                tile_load(n, slot).wait()

                @pl.when(n + 1 < count)
                def _():
                    tile_load(n + 1, 1 - slot).start()

                send[:, lanes(n)] = nt(grads[sublanes(1 - me.core, half_rows), :], w_tile[slot]).astype(bf16)
                total[:, lanes(n)] = nt(grads[sublanes(me.core, half_rows), :], w_tile[slot])

                pace.at("t", n)
                return carry

            lax.fori_loop(0, count, step, 0)
            pl.semaphore_wait(half_free, 1)
            exchange = remote(send, half_recv, half_sem.at[0, 0], half_sem.at[1, 0], me.over_core, me.z)
            exchange.start()
            pace.at("t6")
            load(x_h.at[sublanes(me.core, half_rows), :], x_rows, 0).wait()
            load(kept_h, kept, 1).wait()
            exchange.wait()
            gain = gain_ref[0:1, :]

            def rows(k, sums):
                part = sublanes(k, 64)
                grad = total[part, :] + half_recv[part, :].astype(f32)
                gained, values = norm_rows_back(x_rows[part, :].astype(f32), gain, grad)
                send[part, :] = (values + kept[part, :]).astype(bf16)
                return sums + gained

            gain_buffer[0, 0, 0:1, :] = lax.fori_loop(0, half_rows // 64, rows, jnp.zeros((1, width), f32))
            gains.start()
            fetch((send, rows_h.at[1]))

        pl.run_scoped(
            tokens_back, vmem((2, JOB, 3 * own_width), bf16), vmem((half_rows, width), bf16),
            vmem((half_rows, width), f32), vmem((half_rows, width), bf16), vmem((half_rows, width), f32),
        )
        back_tokens.start()

        def projection_grads(normed_t, g_tile):
            fetch((normed_t_h, normed_t))
            count = 3 * own_width // JOB

            def step(n, carry):
                slot = lax.rem(n, 2)
                g_tile[slot] = dot(normed_t[...], grads[:, lanes(n)]).astype(bf16)

                @pl.when(n >= 1)
                def _():
                    grad_store(g_tile, 1 - slot, g_cols_h, ff_jobs + n - 1, 1).wait()

                grad_store(g_tile, slot, g_cols_h, ff_jobs + n, 1).start()

                pace.at("p", n)
                return carry

            lax.fori_loop(0, count, step, 0)
            grad_store(g_tile, (count - 1) % 2, g_cols_h, ff_jobs + count - 1, 1).wait()

        pl.run_scoped(projection_grads, vmem((width, length), bf16), vmem((2, width, JOB), bf16))

        pace.at("p9")

    pl.run_scoped(attention, vmem((length, 3 * own_width), bf16))

    first = {"E": 6, "S": 20, "F": 4, "C": 16, "D": 11, "O": 3}
    later = max(0, first["S"] - first["C"] - cols.slots + LATE["C"][-1] + 1)
    steps = max(stream.ticks - first[kind] for kind, stream in (("C", cols), ("D", downs), ("O", outs)))

    def rest(t, carry):
        for kind, stream in (("E", downs), ("S", cols), ("F", outs)):
            if first[kind] < stream.count:
                k = first[kind] + t - (later if kind == "S" else 0)
                guard((k >= first[kind]) & (k < stream.count), functools.partial(stream.start, k))
        for kind, stream in (("C", cols), ("D", downs), ("O", outs)):
            if first[kind] < stream.ticks:
                stream.tick(first[kind] + t)
        for k in range(GAIN_HOPS - 1):
            @pl.when(t == k)
            def _():
                gains.step(k)

        return carry

    lax.fori_loop(0, steps, rest, 0)
    for k in range(min(steps, GAIN_HOPS - 1), GAIN_HOPS):
        gains.step(k)
    gains.drain()
    back_out.drain()
    back_tokens.drain()


def norm_rows_back(values, gain, grad):
    scale = lax.rsqrt(jnp.mean(values * values, axis=-1, keepdims=True) + EPS)
    unit = values * scale
    inner = grad * gain
    return (
        jnp.sum(grad * unit, axis=0, keepdims=True),
        scale * (inner - unit * jnp.mean(inner * unit, axis=-1, keepdims=True)),
    )


COLUMN_SLOTS = 12


def backward(branch, slopes, hidden, turned, heads, lse, middle, x, g_down, weights, start, gain, cosine, sine):
    length, width = branch.shape
    half, half_ff = width // 2, hidden.shape[1]
    rows = length // 4
    bf16, f32 = jnp.bfloat16, jnp.float32

    def shape(*dims, dtype=bf16):
        return jax.ShapeDtypeStruct(dims, dtype)

    columns = 2 * half_ff + 3 * half
    shapes = [
        shape(2, rows, width),
        shape(2, rows, width),
        shape(width // 8, 2 * columns),
        shape(width // 8, width),
        shape(half_ff // 4, width),
        shape(2, width, dtype=f32),
        shape(width, columns),
        shape(half, width),
        shape(length // 2, width, dtype=f32),
        shape(2, length // 2, width),
        shape(length, width, dtype=f32),
    ]
    dma, vmem = pltpu.SemaphoreType.DMA, pltpu.VMEM
    whole = pl.BlockSpec(memory_space=pltpu.VMEM)
    ring, row = COLUMN_SLOTS, width // 4
    jobs = width // JOB
    row_buffers = []
    for depth in (half_ff // 2, half // 2):
        row_buffers += [
            vmem((jobs, depth, JOB), bf16), vmem((jobs, depth, JOB), bf16), vmem((jobs, 2, depth, JOB), bf16),
            vmem((depth, JOB), bf16), dma((jobs, 3, 4)), dma((jobs, 2, 3)),
        ]
    return pl.pallas_call(
        backward_kernel,
        in_specs=[ANY] * 16 + [whole] * 4,
        out_specs=[ANY] * 5 + [whole] + [ANY] * 5,
        out_shape=shapes,
        scratch_shapes=[
            vmem((ring, 2 * row, JOB), bf16), vmem((ring, 2 * row, JOB), bf16), vmem((ring, row, JOB), bf16),
            vmem((ring, 2, row, JOB), bf16), dma((ring, 3, 4)), dma((ring, 2, 3)),
            pltpu.SemaphoreType.REGULAR((ring,)),
        ]
        + row_buffers
        + [
            vmem((length, width), bf16), vmem((length // 2, width), bf16), pltpu.SemaphoreType.REGULAR,
            dma((2, 3)), dma((2, 1)),
            vmem((GAIN_HOPS, 2, 2, width), f32), dma((2, GAIN_HOPS)), dma((2, 3, 2)), dma((4,)), dma((2, 3)),
            dma((2, 2)),
        ],
        compiler_params=pltpu.CompilerParams(
            collective_id=1, has_side_effects=True, vmem_limit_bytes=63 * 1024 * 1024
        ),
        cost_estimate=pl.CostEstimate(flops=0, bytes_accessed=800_000_000, transcendentals=0),
        name="backward",
    )(
        branch, *slopes, hidden, *turned, heads, lse, middle, x, g_down, *weights, start, gain, cosine, sine
    )


def wide(value):
    return value.astype(jnp.float32)


def dot(a, b):
    return jnp.dot(a, b, preferred_element_type=jnp.float32)


WIDEN_STEPS = 4


def widen_kernel(cols, o, down, tokens, result, *outs):
    first = 0
    for out in outs[:5]:
        out[...] = cols[:, first : first + out.shape[1]].astype(jnp.float32)
        first += out.shape[1]
    for source, out in zip((o, down, tokens, result), outs[5:]):
        out[...] = source[...].astype(out.dtype)


def widen(cols, o, down, tokens, result, ff):
    depth, width = o.shape

    def rows(count, columns):
        return pl.BlockSpec((count // WIDEN_STEPS, columns), lambda i: (i, 0))

    shapes = [(depth, ff)] * 2 + [(depth, width)] * 4 + [down.shape, tokens.shape, result.shape]
    return pl.pallas_call(
        widen_kernel,
        grid=(WIDEN_STEPS,),
        in_specs=[rows(*value.shape) for value in (cols, o, down, tokens, result)],
        out_specs=[rows(*shape) for shape in shapes],
        out_shape=[jax.ShapeDtypeStruct(shape, jnp.float32) for shape in shapes[:-1]]
        + [jax.ShapeDtypeStruct(result.shape, result.dtype)],
        compiler_params=pltpu.CompilerParams(vmem_limit_bytes=63 * 1024 * 1024),
        name="widen",
    )(cols, o, down, tokens, result)


def column_device(
    tokens, segment_ids, out_grad, w_q, w_k, w_v, w_o, w_gate, w_up, w_down, gain_attn, gain_ffn
):
    dp_at = lax.axis_index("dp")
    rows, width = tokens.shape[1], tokens.shape[2]
    length, ff = 4 * rows, w_gate.shape[1]
    gains = lax.dynamic_update_slice_in_dim(
        jnp.zeros((2, width), jnp.bfloat16),
        jnp.stack([gain_attn, gain_ffn]),
        dp_at * gain_attn.shape[0],
        1,
    )
    lane = jnp.arange(2 * HD, dtype=jnp.int32)
    pace = jnp.exp((lane % (HD // 2)).astype(jnp.float32) * (-math.log(10000.0) / (HD // 2)))
    angle = jnp.arange(length, dtype=jnp.float32)[:, None] * pace[None, :]
    cosine = jnp.cos(angle)
    sine = jnp.where(lane % HD < HD // 2, -1.0, 1.0)[None, :] * jnp.sin(angle)
    (
        x_low, docs, grad_branch, gains, full_qkv, full_o, full_ff, full_down, heads, lse, middle,
        slope_gate, slope_up, hidden, g_down, start, gain, normed_t, nf_t, mixed_t,
    ) = gather_all(
        tokens, segment_ids.reshape(2, 1, rows), out_grad, gains, cosine, sine,
        (w_q, w_k, w_v, w_o, w_gate, w_up, w_down),
    )
    result, grad_tokens, g_cols, g_o, g_down, grad_gains = backward(
        grad_branch, (slope_gate, slope_up), hidden, (nf_t, normed_t, mixed_t), heads, lse, middle, x_low, g_down,
        (full_qkv, full_o, full_ff, full_down), start, gain, cosine, sine,
    )[:6]
    grad_gains = lax.dynamic_slice_in_dim(grad_gains, dp_at * (width // 8), width // 8, 1)
    flat = (2 * rows, width)
    gate, up, query, key, value, out, down, grad_tokens, result = widen(
        g_cols, g_o, g_down, grad_tokens.reshape(flat), result.reshape(flat), ff
    )
    result = result.reshape(2, rows, width)
    return (
        result, grad_tokens.reshape(2, rows, width), query, key, value, out, gate, up, down, grad_gains[0], grad_gains[1]
    )


def solution(mesh):
    placed = (
        P(None, ("dp", "seq"), None),
        P(None, ("dp", "seq")),
        P(None, ("dp", "seq"), None),
        P("dp", None),
        P("dp", None),
        P("dp", None),
        P("dp", None),
        P("dp", None),
        P("dp", None),
        P("dp", None),
        P("dp"),
        P("dp"),
    )
    return jax.shard_map(
        column_device if dict(mesh.shape) == FAST_MESH else per_device,
        mesh=mesh,
        in_specs=placed,
        out_specs=(
            P(None, ("dp", "seq"), None),
            P(None, ("dp", "seq"), None),
            P("dp", None),
            P("dp", None),
            P("dp", None),
            P("dp", None),
            P("dp", None),
            P("dp", None),
            P("dp", None),
            P("dp"),
            P("dp"),
        ),
        check_vma=False,
    )
```

```python
import functools
import math

import jax
import jax.numpy as jnp
import numpy as np
from jax import lax
from jax.experimental import pallas as pl
from jax.experimental.pallas import tpu as pltpu
from jax.sharding import PartitionSpec as P

HEADS = 24
HD = 64


EPS = 1e-05


def positions_of(doc_row):
    count = doc_row.shape[0]
    place = jnp.arange(count, dtype=jnp.int32)
    before = jnp.concatenate([doc_row[:1], doc_row[:-1]])
    starts = (place == 0) | (doc_row != before)
    first_place = lax.cummax(jnp.where(starts, place, jnp.zeros_like(place)), axis=0)
    return place - first_place


def rope_tables(where_at, half):
    inverse = jnp.exp(jnp.arange(half, dtype=jnp.float32) * (-math.log(10000.0) / half))
    angle = where_at.astype(jnp.float32)[:, None] * inverse[None, :]
    return (jnp.cos(angle), jnp.sin(angle))


def rotate(values, cosine, sine):
    half = values.shape[-1] // 2
    first, second = (values[..., :half], values[..., half:])
    cos_heads, sin_heads = (cosine[:, None, :], sine[:, None, :])
    return jnp.concatenate(
        [first * cos_heads - second * sin_heads, second * cos_heads + first * sin_heads], axis=-1
    )


def rotate_back(grads, cosine, sine):
    half = grads.shape[-1] // 2
    first, second = (grads[..., :half], grads[..., half:])
    cos_heads, sin_heads = (cosine[:, None, :], sine[:, None, :])
    return jnp.concatenate(
        [first * cos_heads + second * sin_heads, second * cos_heads - first * sin_heads], axis=-1
    )


def rms_norm(values, gain):
    return values * lax.rsqrt(jnp.mean(values * values, axis=-1, keepdims=True) + EPS) * gain


def norm_backward(values, gain, grad_normed):
    scale = lax.rsqrt(jnp.mean(values * values, axis=-1, keepdims=True) + EPS)
    unit = values * scale
    grad_gain = jnp.sum(grad_normed * unit, axis=0)
    inner = grad_normed * gain
    grad_values = scale * (inner - unit * jnp.mean(inner * unit, axis=-1, keepdims=True))
    return (grad_gain, grad_values)


def block_scores(query_heads, key_heads, doc_row, start, block):
    length = doc_row.shape[0]
    place = jnp.arange(length, dtype=jnp.int32)
    query_block = lax.dynamic_slice_in_dim(query_heads, start, block, 0)
    doc_block = lax.dynamic_slice_in_dim(doc_row, start, block, 0)
    rows_block = start + jnp.arange(block, dtype=jnp.int32)
    allowed = (doc_block[:, None] == doc_row[None, :]) & (rows_block[:, None] >= place[None, :])
    scores = (
        jnp.einsum("qhd,khd->hqk", query_block, key_heads, preferred_element_type=jnp.float32)
        * 0.125
    )
    return (query_block, jnp.where(allowed[None], scores, -1e30))


def attention_forward(query, key, value, doc_row):
    length = query.shape[0]
    head_shape = (length, query.shape[1] // HD, HD)
    query_heads, key_heads, value_heads = (
        query.reshape(head_shape),
        key.reshape(head_shape),
        value.reshape(head_shape),
    )
    block = min(512, length)
    starts = jnp.arange(length // block, dtype=jnp.int32) * block

    def one_block(start):
        unused, scores = block_scores(query_heads, key_heads, doc_row, start, block)
        peak = jnp.max(scores, axis=-1, keepdims=True)
        expo = jnp.exp(scores - peak)
        total = jnp.sum(expo, axis=-1, keepdims=True)
        probs_low = (expo / total).astype(jnp.bfloat16)
        mixed = jnp.einsum(
            "hqk,khd->qhd", probs_low, value_heads, preferred_element_type=jnp.float32
        )
        return (mixed.astype(jnp.bfloat16), (peak + jnp.log(total))[..., 0])

    mixed, logsum = lax.map(one_block, starts)
    return (mixed.reshape(length, query.shape[1]), logsum)


def attention_backward(query, key, value, doc_row, logsum, grad_mixed, cosine, sine):
    length = query.shape[0]
    head_shape = (length, query.shape[1] // HD, HD)
    query_heads, key_heads, value_heads = (
        query.reshape(head_shape),
        key.reshape(head_shape),
        value.reshape(head_shape),
    )
    grad_heads = grad_mixed.reshape(head_shape)
    block = min(512, length)
    starts = jnp.arange(length // block, dtype=jnp.int32) * block

    def one_block(carry, item):
        grad_key, grad_value = carry
        start, logsum_block = item
        query_block, scores = block_scores(query_heads, key_heads, doc_row, start, block)
        probs = jnp.exp(scores - logsum_block[..., None])
        probs_low = probs.astype(jnp.bfloat16)
        grad_block = lax.dynamic_slice_in_dim(grad_heads, start, block, 0)
        grad_probs = jnp.einsum(
            "qhd,khd->hqk", grad_block, value_heads, preferred_element_type=jnp.float32
        )
        inner = jnp.sum(probs * grad_probs, axis=-1, keepdims=True)
        grad_scores = (probs * (grad_probs - inner)).astype(jnp.bfloat16)
        grad_query = (
            jnp.einsum("hqk,khd->qhd", grad_scores, key_heads, preferred_element_type=jnp.float32)
            * 0.125
        )
        grad_key = (
            grad_key
            + jnp.einsum(
                "hqk,qhd->khd", grad_scores, query_block, preferred_element_type=jnp.float32
            )
            * 0.125
        )
        grad_value = grad_value + jnp.einsum(
            "hqk,qhd->khd", probs_low, grad_block, preferred_element_type=jnp.float32
        )
        return ((grad_key, grad_value), grad_query)

    zeros_heads = jnp.zeros(head_shape, jnp.float32)
    (grad_key, grad_value), grad_query = lax.scan(
        one_block, (zeros_heads, zeros_heads), (starts, logsum)
    )
    grad_query = rotate_back(grad_query.reshape(head_shape), cosine, sine)
    grad_key = rotate_back(grad_key, cosine, sine)
    width_here = query.shape[1]
    return (
        grad_query.reshape(length, width_here).astype(jnp.bfloat16),
        grad_key.reshape(length, width_here).astype(jnp.bfloat16),
        grad_value.reshape(length, width_here).astype(jnp.bfloat16),
    )


def per_device(
    tokens, segment_ids, out_grad, w_q, w_k, w_v, w_o, w_gate, w_up, w_down, gain_attn, gain_ffn
):
    micro, rows, width = tokens.shape
    offset = lax.axis_index("seq") * rows
    shards = (w_q, w_k, w_v, w_o, w_gate, w_up, w_down, gain_attn, gain_ffn)
    gathered = (
        lax.all_gather(shards[0], "dp", axis=0, tiled=True),
        lax.all_gather(shards[1], "dp", axis=0, tiled=True),
        lax.all_gather(shards[2], "dp", axis=0, tiled=True),
        lax.all_gather(shards[3], "dp", axis=0, tiled=True),
        lax.all_gather(shards[4], "dp", axis=0, tiled=True),
        lax.all_gather(shards[5], "dp", axis=0, tiled=True),
        lax.all_gather(shards[6], "dp", axis=0, tiled=True),
        lax.all_gather(shards[7], "dp", axis=0, tiled=True),
        lax.all_gather(shards[8], "dp", axis=0, tiled=True),
    )
    docs = lax.all_gather(segment_ids, "seq", axis=1, tiled=True)
    full_q, full_k, full_v, full_o, full_gate, full_up, full_down, full_gain_a, full_gain_f = (
        gathered
    )
    gain_a = full_gain_a.astype(jnp.float32)
    gain_f = full_gain_f.astype(jnp.float32)
    row_heads = (rows, HEADS, HD)
    saved = []
    results = []
    for micro_index in range(micro):
        rows_in = tokens[micro_index].astype(jnp.float32)
        doc_row = docs[micro_index]
        cosine, sine = rope_tables(positions_of(doc_row), HD // 2)
        own_cos = lax.dynamic_slice_in_dim(cosine, offset, rows, 0)
        own_sin = lax.dynamic_slice_in_dim(sine, offset, rows, 0)
        normed = rms_norm(rows_in, gain_a).astype(jnp.bfloat16)
        query_rows = jnp.dot(normed, full_q, preferred_element_type=jnp.float32).reshape(row_heads)
        query_rows = rotate(query_rows, own_cos, own_sin).reshape(rows, width).astype(jnp.bfloat16)
        key_rows = jnp.dot(normed, full_k, preferred_element_type=jnp.float32).reshape(row_heads)
        key_rows = rotate(key_rows, own_cos, own_sin).reshape(rows, width).astype(jnp.bfloat16)
        value_rows = jnp.dot(normed, full_v, preferred_element_type=jnp.float32).astype(
            jnp.bfloat16
        )
        query, key, value = (
            lax.all_to_all(query_rows, "seq", split_axis=1, concat_axis=0, tiled=True),
            lax.all_to_all(key_rows, "seq", split_axis=1, concat_axis=0, tiled=True),
            lax.all_to_all(value_rows, "seq", split_axis=1, concat_axis=0, tiled=True),
        )
        mixed, logsum = attention_forward(query, key, value, doc_row)
        mixed_rows = lax.all_to_all(mixed, "seq", split_axis=0, concat_axis=1, tiled=True)
        middle = rows_in + jnp.dot(mixed_rows, full_o, preferred_element_type=jnp.float32)
        normed_ffn = rms_norm(middle, gain_f).astype(jnp.bfloat16)
        gate = jnp.dot(normed_ffn, full_gate, preferred_element_type=jnp.float32)
        up_value = jnp.dot(normed_ffn, full_up, preferred_element_type=jnp.float32)
        hidden = (jax.nn.silu(gate) * up_value).astype(jnp.bfloat16)
        result = middle + jnp.dot(hidden, full_down, preferred_element_type=jnp.float32)
        results.append(result.astype(jnp.bfloat16))
        saved.append(
            (
                rows_in,
                doc_row,
                cosine,
                sine,
                normed,
                query,
                key,
                value,
                logsum,
                mixed_rows,
                middle,
                normed_ffn,
                gate,
                up_value,
                hidden,
            )
        )
    back_weights = (
        lax.all_gather(shards[0], "dp", axis=0, tiled=True),
        lax.all_gather(shards[1], "dp", axis=0, tiled=True),
        lax.all_gather(shards[2], "dp", axis=0, tiled=True),
        lax.all_gather(shards[3], "dp", axis=0, tiled=True),
        lax.all_gather(shards[4], "dp", axis=0, tiled=True),
        lax.all_gather(shards[5], "dp", axis=0, tiled=True),
        lax.all_gather(shards[6], "dp", axis=0, tiled=True),
        lax.all_gather(shards[7], "dp", axis=0, tiled=True),
        lax.all_gather(shards[8], "dp", axis=0, tiled=True),
    )
    back_q, back_k, back_v, back_o, back_gate, back_up, back_down, back_gain_a, back_gain_f = (
        back_weights
    )
    gain_back_a = back_gain_a.astype(jnp.float32)
    gain_back_f = back_gain_f.astype(jnp.float32)
    totals = [jnp.zeros(weight.shape, jnp.float32) for weight in back_weights]
    grad_inputs = []
    for micro_index in range(micro):
        (
            rows_in,
            doc_row,
            cosine,
            sine,
            normed,
            query,
            key,
            value,
            logsum,
            mixed_rows,
            middle,
            normed_ffn,
            gate,
            up_value,
            hidden,
        ) = saved[micro_index]
        grad_out = out_grad[micro_index].astype(jnp.float32)
        grad_branch = grad_out.astype(jnp.bfloat16)
        totals[6] = totals[6] + jnp.einsum(
            "tf,td->fd", hidden, grad_branch, preferred_element_type=jnp.float32
        )
        grad_hidden = jnp.einsum(
            "td,fd->tf", grad_branch, back_down, preferred_element_type=jnp.float32
        )
        sigma = jax.nn.sigmoid(gate)
        grad_gate = (grad_hidden * up_value * sigma * (1.0 + gate * (1.0 - sigma))).astype(
            jnp.bfloat16
        )
        grad_up = (grad_hidden * jax.nn.silu(gate)).astype(jnp.bfloat16)
        totals[4] = totals[4] + jnp.einsum(
            "td,tf->df", normed_ffn, grad_gate, preferred_element_type=jnp.float32
        )
        totals[5] = totals[5] + jnp.einsum(
            "td,tf->df", normed_ffn, grad_up, preferred_element_type=jnp.float32
        )
        grad_normed_ffn = jnp.einsum(
            "tf,df->td", grad_gate, back_gate, preferred_element_type=jnp.float32
        )
        grad_normed_ffn = grad_normed_ffn + jnp.einsum(
            "tf,df->td", grad_up, back_up, preferred_element_type=jnp.float32
        )
        grad_gain_f, grad_middle = norm_backward(middle, gain_back_f, grad_normed_ffn)
        totals[8] = totals[8] + grad_gain_f
        grad_middle = grad_middle + grad_out
        grad_attn = grad_middle.astype(jnp.bfloat16)
        totals[3] = totals[3] + jnp.einsum(
            "ti,td->id", mixed_rows, grad_attn, preferred_element_type=jnp.float32
        )
        grad_mixed_rows = jnp.einsum(
            "td,id->ti", grad_attn, back_o, preferred_element_type=jnp.float32
        ).astype(jnp.bfloat16)
        grad_mixed = lax.all_to_all(grad_mixed_rows, "seq", split_axis=1, concat_axis=0, tiled=True)
        grad_query, grad_key, grad_value = attention_backward(
            query, key, value, doc_row, logsum, grad_mixed, cosine, sine
        )
        query_back, key_back, value_back = (
            lax.all_to_all(grad_query, "seq", split_axis=0, concat_axis=1, tiled=True),
            lax.all_to_all(grad_key, "seq", split_axis=0, concat_axis=1, tiled=True),
            lax.all_to_all(grad_value, "seq", split_axis=0, concat_axis=1, tiled=True),
        )
        totals[0] = totals[0] + jnp.einsum(
            "td,te->de", normed, query_back, preferred_element_type=jnp.float32
        )
        totals[1] = totals[1] + jnp.einsum(
            "td,te->de", normed, key_back, preferred_element_type=jnp.float32
        )
        totals[2] = totals[2] + jnp.einsum(
            "td,te->de", normed, value_back, preferred_element_type=jnp.float32
        )
        grad_normed = jnp.einsum(
            "te,de->td", query_back, back_q, preferred_element_type=jnp.float32
        )
        grad_normed = grad_normed + jnp.einsum(
            "te,de->td", key_back, back_k, preferred_element_type=jnp.float32
        )
        grad_normed = grad_normed + jnp.einsum(
            "te,de->td", value_back, back_v, preferred_element_type=jnp.float32
        )
        grad_gain_a, grad_rows = norm_backward(rows_in, gain_back_a, grad_normed)
        totals[7] = totals[7] + grad_gain_a
        grad_inputs.append(grad_rows + grad_middle)
    summed_all = (
        totals[0],
        totals[1],
        totals[2],
        totals[3],
        totals[4],
        totals[5],
        totals[6],
        totals[7],
        totals[8],
    )
    pieces = (
        lax.psum_scatter(
            summed_all[0].astype(jnp.bfloat16), "dp", scatter_dimension=0, tiled=True
        ).astype(jnp.float32),
        lax.psum_scatter(
            summed_all[1].astype(jnp.bfloat16), "dp", scatter_dimension=0, tiled=True
        ).astype(jnp.float32),
        lax.psum_scatter(
            summed_all[2].astype(jnp.bfloat16), "dp", scatter_dimension=0, tiled=True
        ).astype(jnp.float32),
        lax.psum_scatter(
            summed_all[3].astype(jnp.bfloat16), "dp", scatter_dimension=0, tiled=True
        ).astype(jnp.float32),
        lax.psum_scatter(
            summed_all[4].astype(jnp.bfloat16), "dp", scatter_dimension=0, tiled=True
        ).astype(jnp.float32),
        lax.psum_scatter(
            summed_all[5].astype(jnp.bfloat16), "dp", scatter_dimension=0, tiled=True
        ).astype(jnp.float32),
        lax.psum_scatter(
            summed_all[6].astype(jnp.bfloat16), "dp", scatter_dimension=0, tiled=True
        ).astype(jnp.float32),
        lax.psum_scatter(
            summed_all[7].astype(jnp.bfloat16), "dp", scatter_dimension=0, tiled=True
        ).astype(jnp.float32),
        lax.psum_scatter(
            summed_all[8].astype(jnp.bfloat16), "dp", scatter_dimension=0, tiled=True
        ).astype(jnp.float32),
    )
    pieces = (
        lax.psum(pieces[0].astype(jnp.bfloat16), "seq").astype(jnp.float32),
        lax.psum(pieces[1].astype(jnp.bfloat16), "seq").astype(jnp.float32),
        lax.psum(pieces[2].astype(jnp.bfloat16), "seq").astype(jnp.float32),
        lax.psum(pieces[3].astype(jnp.bfloat16), "seq").astype(jnp.float32),
        lax.psum(pieces[4].astype(jnp.bfloat16), "seq").astype(jnp.float32),
        lax.psum(pieces[5].astype(jnp.bfloat16), "seq").astype(jnp.float32),
        lax.psum(pieces[6].astype(jnp.bfloat16), "seq").astype(jnp.float32),
        lax.psum(pieces[7].astype(jnp.bfloat16), "seq").astype(jnp.float32),
        lax.psum(pieces[8].astype(jnp.bfloat16), "seq").astype(jnp.float32),
    )
    return (
        jnp.stack(results),
        jnp.stack(grad_inputs),
        pieces[0],
        pieces[1],
        pieces[2],
        pieces[3],
        pieces[4],
        pieces[5],
        pieces[6],
        pieces[7],
        pieces[8],
    )


BLK = 256
LOG2E = 1.4426950408889634


def swap_halves(v):
    lane = lax.broadcasted_iota(jnp.int32, v.shape, 1)
    width = v.shape[1]
    up = pltpu.roll(v, width - 32, axis=1)
    down = pltpu.roll(v, 32, axis=1)
    return jnp.where(lane % 64 < 32, up, down)


def nt(a, b):
    return lax.dot_general(a, b, (((1,), (1,)), ((), ())), preferred_element_type=jnp.float32)


def tn(a, b):
    return lax.dot_general(a, b, (((0,), (0,)), ((), ())), preferred_element_type=jnp.float32)


FAST_MESH = {"dp": 8, "seq": 4}
ANY = pl.BlockSpec(memory_space=pl.ANY)


class Place:
    def __init__(self):
        self.dp, self.z = lax.axis_index("dp"), lax.axis_index("seq")
        self.core = self.dp % 2
        self.x = (self.dp // 2) % 2
        self.y = self.dp // 4
        self.over_core = self.dp + 1 - 2 * self.core
        self.over_x = self.dp + 2 - 4 * self.x
        self.over_y = self.dp + 4 - 8 * self.y
        self.middle = (self.z == 1) | (self.z == 2)


def enter(devices):
    barrier = pltpu.get_barrier_semaphore()
    for dp, seq in devices:
        pl.semaphore_signal(
            barrier, inc=1, device_id={"dp": dp, "seq": seq}, device_id_type=pl.DeviceIdType.MESH
        )
    pl.semaphore_wait(barrier, len(devices))


def remote(src, dst, send_sem, recv_sem, dp, seq):
    return pltpu.make_async_remote_copy(
        src_ref=src,
        dst_ref=dst,
        send_sem=send_sem,
        recv_sem=recv_sem,
        device_id={"dp": dp, "seq": seq},
        device_id_type=pl.DeviceIdType.MESH,
    )


def gather_kernel(
    tokens, segments, out_grad, gains, rotary, w_q, w_k, w_v, w_o, w_gate, w_up, w_down,
    x_out, seg_out, g_out, gains_out, qkv_out, o_out, ff_out, down_out,
    heads_out, lse_out, middle_out, slope_gate_out, slope_up_out, hidden_out, g_down_out, start_out,
    gain_out, normed_t_out, nf_t_out, mixed_t_out, cosine_out, sine_out,
    send, recv, local, row_send, row_recv, row_local, gain_send, gain_recv,
    x_v, seg_v, gains_v, normed_v, w_qkv_v, heads_v, mixed_v, w_o_v, middle_v, part_send, part_recv,
    nf_v, w_ff_v, branch_v, tile_v, g_tile_v, lse_v, start_v, lse_t_v, start_row_v, gain_v, turned_v, mixed_t_v, cosine, sine,
    part_sem, load_sem, w_sem, tile_sem, store_sem,
):
    me = Place()
    rows = tokens.shape[1]
    plane = [(lax.rem(me.dp + k, 8), me.z) for k in range(1, 8)]
    column = [
        (me.dp - me.core + core, lax.rem(me.z + k, 4)) for k in range(1, 4) for core in range(2)
    ]
    enter(plane + column)
    started = []

    def begin(copy):
        copy.start()
        started.append(copy)

    streams = ((tokens, x_out), (segments, seg_out), (out_grad, g_out))

    def place_of(ref, seq):
        return ref.at[pl.ds(rows * seq, rows)] if ref.shape[0] == 4 * rows else ref.at[seq]

    def row_copies(index):
        source, target = streams[index]
        for m in range(2):
            core, seq = me.z // 2, 2 * m + me.core
            here = (core == me.core) & (seq == me.z)

            @pl.when(here)
            def _():
                pltpu.make_async_copy(
                    source.at[m], place_of(target, me.z), row_local.at[index]
                ).start()

            @pl.when(jnp.logical_not(here))
            def _():
                remote(
                    source.at[m], place_of(target, me.z), row_send.at[index, m],
                    row_recv.at[index, me.z % 2], me.dp - me.core + core, seq,
                ).start()

    def row_wait_send(index):
        source, target = streams[index]
        for m in range(2):
            core, seq = me.z // 2, 2 * m + me.core
            here = (core == me.core) & (seq == me.z)

            @pl.when(jnp.logical_not(here))
            def _():
                remote(
                    source.at[m], place_of(target, me.z), row_send.at[index, m],
                    row_recv.at[index, me.z % 2], me.dp - me.core + core, seq,
                ).wait_send()

    def row_relay(index):
        source, target = streams[index]
        for slot in range(2):
            seq = 2 * me.core + slot
            block = place_of(target, seq)
            here = (seq == me.z) & (me.z % 2 == me.core)

            @pl.when(here)
            def _():
                pltpu.make_async_copy(block, block, row_local.at[index]).wait()

            @pl.when(jnp.logical_not(here))
            def _():
                remote(
                    block, block, row_send.at[index, slot], row_recv.at[index, slot], me.over_core, me.z
                ).wait_recv()

            begin(
                remote(
                    block, block, row_send.at[index, 2 + slot], row_recv.at[index, 2 + slot],
                    me.over_core, me.z,
                )
            )

    def row_finish(index):
        source, target = streams[index]
        for slot in range(2):
            block = place_of(target, 2 * (1 - me.core) + slot)
            remote(
                block, block, row_send.at[index, 2 + slot], row_recv.at[index, 2 + slot], me.over_core, me.z
            ).wait_recv()

    by_columns = []
    base = 0
    for source in (w_q, w_k, w_v):
        by_columns.append((source, qkv_out, base))
        base += source.shape[1] // 2
    by_columns.append((w_gate, ff_out, 0))
    by_columns.append((w_up, ff_out, w_gate.shape[1] // 2))
    by_rows = [(w_o, o_out), (w_down, down_out)]

    def column_piece(index, owner):
        source, target, first = by_columns[index]
        depth, width = source.shape[0], source.shape[1] // 2
        return target.at[pl.ds(depth * owner, depth), pl.ds(first, width)]

    def columns_start(index):
        source, target, first = by_columns[index]
        width = source.shape[1] // 2
        mine = column_piece(index, me.dp)
        for core in range(2):
            half = source.at[:, pl.ds(width * core, width)]
            begin(remote(half, mine, send.at[index, core], recv.at[index, me.core],
                         me.over_x - me.core + core, me.z))
            begin(remote(half, mine, send.at[index, 2 + core], recv.at[index, 2 + me.core],
                         me.over_y - me.core + core, me.z))

            @pl.when(core == me.core)
            def _():
                pltpu.make_async_copy(half, mine, local.at[index]).start()

            @pl.when(core != me.core)
            def _():
                remote(half, mine, send.at[index, 4], recv.at[index, 4], me.over_core, me.z).start()

    beside = me.z + 1 - 2 * lax.rem(me.z, 2)
    corner = me.over_x + me.over_y - me.dp - me.core

    def turn_of(index):
        return lax.rem(index + me.z, 2)

    last = 6

    def hand_on(index, piece, came, slot, send_slot, dp, seq):
        remote(piece, piece, send.at[index, send_slot], recv.at[index, came], dp, seq).wait_recv()
        remote(piece, piece, send.at[index, send_slot], recv.at[index, slot], dp, seq).start()

    def arrived(index, piece, slot):
        remote(piece, piece, send.at[index, 5], recv.at[index, slot], me.over_core, me.z).wait_recv()

    def left(index, piece, slot):
        remote(piece, piece, send.at[index, slot], recv.at[index, 5], me.over_core, me.z).wait_send()

    def columns_relay(index):
        @pl.when(turn_of(index) == 0)
        def _():
            hand_on(index, column_piece(index, me.over_x - me.core), 0, 5, 5, me.over_y, me.z)

        @pl.when(turn_of(index) == 1)
        def _():
            hand_on(index, column_piece(index, me.over_y - me.core + 1), 3, 6, 6, me.over_x, me.z)

    def columns_forward(index):
        @pl.when(turn_of(index) == 0)
        def _():
            hand_on(index, column_piece(index, corner), 5, 5, 6, me.dp, beside)

        @pl.when(turn_of(index) == 1)
        def _():
            hand_on(index, column_piece(index, corner + 1), 6, 6, 5, me.dp, beside)

    def columns_finish(index):
        source, target, first = by_columns[index]
        width = source.shape[1] // 2
        arrived(index, column_piece(index, me.over_x - me.core + 1), 1)
        arrived(index, column_piece(index, me.over_y - me.core), 2)
        arrived(index, column_piece(index, me.over_core), 4)

        @pl.when(turn_of(index) == 0)
        def _():
            arrived(index, column_piece(index, me.over_y - me.core + 1), 3)
            arrived(index, column_piece(index, corner + 1), 6)

        @pl.when(turn_of(index) == 1)
        def _():
            arrived(index, column_piece(index, me.over_x - me.core), 0)
            arrived(index, column_piece(index, corner), 5)

        mine = column_piece(index, me.dp)
        pltpu.make_async_copy(mine, mine, local.at[index]).wait()
        for slot in (4, 5, 6):
            left(index, mine, slot)

    def row_piece(which, owner):
        source, target = by_rows[which]
        depth = source.shape[0]
        return target.at[pl.ds(depth * lax.rem(owner, 4), depth), :]

    def rows_start(which):
        source, target = by_rows[which]
        index = 5 + which
        mine = row_piece(which, me.dp)
        begin(remote(source, mine, send.at[index, 0], recv.at[index, me.core],
                     me.over_x - me.core + me.y, me.z))
        begin(remote(source, mine, send.at[index, 1], recv.at[index, 2 + me.core],
                     me.over_y - me.core + me.y, me.z))

        @pl.when(me.core == me.y)
        def _():
            pltpu.make_async_copy(source, mine, local.at[index]).start()

        @pl.when(me.core != me.y)
        def _():
            remote(source, mine, send.at[index, 4], recv.at[index, 4], me.over_core, me.z).start()

    def rows_relay(which):
        index = 5 + which

        @pl.when((me.core == me.y) & ((index == last) | (turn_of(index) == 0)))
        def _():
            hand_on(index, row_piece(which, me.over_x - me.core), 0, 5, 5, me.over_y, me.z)

        @pl.when((me.core != me.y) & ((index == last) | (turn_of(index) == 1)))
        def _():
            hand_on(index, row_piece(which, me.over_y - me.core + 1), 3, 6, 6, me.over_x, me.z)

    def rows_forward(which):
        index = 5 + which

        @pl.when((me.core != me.y) & (turn_of(index) == 0))
        def _():
            hand_on(index, row_piece(which, corner), 5, 5, 6, me.dp, beside)

        @pl.when((me.core != me.y) & (turn_of(index) == 1))
        def _():
            hand_on(index, row_piece(which, corner + 1), 6, 6, 5, me.dp, beside)

    def rows_finish(which):
        source, target = by_rows[which]
        index = 5 + which
        mine = row_piece(which, me.dp)

        @pl.when(me.core == me.y)
        def _():
            arrived(index, row_piece(which, me.over_x - me.core + 1), 1)
            arrived(index, row_piece(which, me.over_core), 4)
            pltpu.make_async_copy(source, mine, local.at[index]).wait()

            @pl.when((index == last) | (turn_of(index) == 0))
            def _():
                left(index, mine, 5)

            @pl.when((index != last) & (turn_of(index) == 1))
            def _():
                arrived(index, row_piece(which, me.over_x - me.core), 0)

        @pl.when(me.core != me.y)
        def _():
            arrived(index, row_piece(which, me.over_y - me.core), 2)
            left(index, mine, 4)
            left(index, mine, 6)

            @pl.when((index != last) & (turn_of(index) == 0))
            def _():
                arrived(index, row_piece(which, me.over_y - me.core + 1), 3)
                arrived(index, row_piece(which, corner + 1), 6)

            @pl.when((index == last) | (turn_of(index) == 1))
            def _():
                arrived(index, row_piece(which, corner), 5)

            @pl.when(index == last)
            def _():
                arrived(index, row_piece(which, corner + 1), 6)

            @pl.when((index != last) & (turn_of(index) == 1))
            def _():
                left(index, mine, 5)

    def load(source, target, k):
        return pltpu.make_async_copy(source, target, load_sem.at[k])

    stores = []

    def store(source, target):
        copy = pltpu.make_async_copy(source, target, store_sem.at[len(stores)])
        stores.append(copy)
        copy.start()
        return copy

    length, width = x_v.shape
    own_width = width // 2
    half_ff = ff_out.shape[1] // 2

    row_copies(0)
    row_copies(1)
    for index in range(3):
        columns_start(index)
    for k in range(1, 8):
        begin(remote(gains, gains_out.at[me.dp], gain_send.at[k - 1], gain_recv.at[k - 1],
                     lax.rem(me.dp + k, 8), me.z))
    pltpu.make_async_copy(gains, gains_out.at[me.dp], gain_recv.at[7]).start()
    fill_rotary(rotary, cosine, sine)
    store(cosine, cosine_out)
    store(sine, sine_out)
    for index in range(3):
        columns_relay(index)
    rows_start(0)
    columns_start(3)
    row_relay(0)
    row_relay(1)
    for k in range(1, 8):
        piece = gains_out.at[lax.rem(me.dp + 8 - k, 8)]
        remote(piece, piece, gain_send.at[k - 1], gain_recv.at[k - 1], me.over_core, me.z).wait_recv()
    pltpu.make_async_copy(gains, gains_out.at[me.dp], gain_recv.at[7]).wait()
    load(gains_out, gains_v, 0).start()
    row_finish(1)
    load(seg_out, seg_v, 1).start()
    row_finish(0)
    load(x_out, x_v, 2).start()
    load(gains_out, gains_v, 0).wait()
    load(seg_out, seg_v, 1).wait()
    load(x_out, x_v, 2).wait()
    both_gains = gains_v[0].astype(jnp.float32)
    for k in range(1, 8):
        both_gains = both_gains + gains_v[k].astype(jnp.float32)
    gain_a, gain_f = both_gains[0:1], both_gains[1:2]
    gain_v[...] = both_gains
    store(gain_v, gain_out)

    norm_rows(lambda part: x_v[part, :].astype(jnp.float32), gain_a, normed_v, length)

    docs = jnp.concatenate([seg_v[k] for k in range(4)], axis=1)
    start_row = jnp.zeros((1, length), jnp.int32)
    for k in range(4):
        square = lax.broadcasted_iota(jnp.int32, (rows, rows), 0) == lax.broadcasted_iota(
            jnp.int32, (rows, rows), 1
        )
        ids = jnp.sum(jnp.where(square, seg_v[k], 0), axis=1, keepdims=True)
        start_v[pl.ds(rows * k, rows), :] = jnp.sum(
            jnp.where(docs < ids, 1, 0), axis=1, keepdims=True
        )
        start_row = start_row + jnp.sum(jnp.where(ids < docs, 1, 0), axis=0, keepdims=True)
    start_row_v[...] = start_row
    store(start_row_v, start_out)
    turn(normed_v, turned_v)
    normed_store = store(turned_v, normed_t_out)

    for index in range(3):
        columns_forward(index)
    rows_relay(0)
    columns_start(4)
    for index in range(3):
        columns_finish(index)
    tile = 256
    tiles = own_width // tile
    for t in range(tiles):
        for kind in range(3):
            part = pl.ds(own_width * kind + tile * t, tile)
            pltpu.make_async_copy(qkv_out.at[:, part], w_qkv_v.at[:, part], w_sem.at[kind, t]).start()
    def tile_step(t, carry):
        def kind_step(kind, carry):
            first = own_width * kind + tile * t
            part = pl.ds(pl.multiple_of(first, 128), tile)
            pltpu.make_async_copy(qkv_out.at[:, part], w_qkv_v.at[:, part], w_sem.at[kind, t]).wait()
            product = jnp.dot(normed_v[...], w_qkv_v[:, part], preferred_element_type=jnp.float32)
            for k in range(tile // 128):
                piece = product[:, 128 * k : 128 * k + 128]
                cols = pl.ds(pl.multiple_of(first + 128 * k, 128), 128)

                @pl.when(kind < 2)
                def _():
                    turned = piece * cosine[...] + swap_halves(piece) * sine[...]
                    heads_v[:, cols] = turned.astype(jnp.bfloat16)

                @pl.when(kind == 2)
                def _():
                    heads_v[:, cols] = piece.astype(jnp.bfloat16)

            return carry

        lax.fori_loop(0, 3, kind_step, 0)

        def pair_step(pair, carry):
            attend(pair, own_width, heads_v, start_v, mixed_v, lse_v)
            return carry

        lax.fori_loop(tile // 128 * t, tile // 128 * (t + 1), pair_step, 0)

        @pl.when(t == 0)
        def _():
            row_copies(2)

        @pl.when(t == 1)
        def _():
            rows_forward(0)
            columns_relay(3)

        return carry

    lax.fori_loop(0, tiles, tile_step, 0)
    store(heads_v, heads_out)
    lse_t_v[...] = lse_v[...].T
    store(lse_t_v, lse_out)
    turn(mixed_v, mixed_t_v)
    store(mixed_t_v, mixed_t_out)

    rows_finish(0)
    load(o_out, w_o_v, 0).start()
    load(o_out, w_o_v, 0).wait()
    chunk = width // 3

    def part_copy(k):
        part = pl.ds(chunk * k, chunk)
        return remote(
            part_send.at[:, part], part_recv.at[:, part], part_sem.at[0, k], part_sem.at[1, k], me.over_core, me.z
        )

    def out_step(n, carry):
        part = pl.ds(pl.multiple_of(tile * n, 128), tile)
        product = jnp.dot(mixed_v[...], w_o_v[:, part], preferred_element_type=jnp.float32)
        part_send[:, part] = product.astype(jnp.bfloat16)
        middle_v[:, part] = x_v[:, part].astype(jnp.float32) + product
        for k in range(3):
            @pl.when(tile * (n + 1) == chunk * (k + 1))
            def _():
                part_copy(k).start()

        return carry

    lax.fori_loop(0, width // tile, out_step, 0)
    row_relay(2)
    columns_relay(4)
    rows_start(1)
    row_finish(2)
    load(g_out, branch_v, 1).start()
    for k in range(3):
        part_copy(k).wait_recv()

    def middle_rows(part):
        value = middle_v[part, :] + part_recv[part, :].astype(jnp.float32)
        middle_v[part, :] = value
        return value

    norm_rows(middle_rows, gain_f, nf_v, length)
    store(middle_v, middle_out)
    normed_store.wait()
    turn(nf_v, turned_v)
    store(turned_v, nf_t_out)
    load(g_out, branch_v, 1).wait()
    columns_forward(3)
    columns_forward(4)
    columns_finish(3)
    columns_finish(4)

    def ff_load(n, slot, kind):
        first = pl.multiple_of(half_ff * kind + tile * n, 128)
        return pltpu.make_async_copy(
            ff_out.at[:, pl.ds(first, tile)], w_ff_v.at[slot, kind], tile_sem.at[0, slot, kind]
        )

    def tile_store(n, slot, kind):
        part = pl.ds(pl.multiple_of(tile * n, 128), tile)
        target = (slope_gate_out, slope_up_out, hidden_out)[kind]
        return pltpu.make_async_copy(tile_v.at[slot, kind], target.at[:, part], tile_sem.at[1, slot, kind])

    def grad_store(n, slot):
        part = pl.ds(pl.multiple_of(tile * n, tile), tile)
        return pltpu.make_async_copy(g_tile_v.at[slot], g_down_out.at[part, :], tile_sem.at[2, slot, 0])

    count = half_ff // tile
    for kind in range(2):
        ff_load(0, 0, kind).start()
    rows_relay(1)

    def ff_step(n, carry):
        slot = lax.rem(n, 2)
        for kind in range(2):
            ff_load(n, slot, kind).wait()

        @pl.when(n + 1 < count)
        def _():
            for kind in range(2):
                ff_load(n + 1, 1 - slot, kind).start()

        @pl.when(n >= 2)
        def _():
            for kind in range(3):
                tile_store(n - 2, slot, kind).wait()
            grad_store(n - 2, slot).wait()

        gate = jnp.dot(nf_v[...], w_ff_v[slot, 0], preferred_element_type=jnp.float32)
        up_value = jnp.dot(nf_v[...], w_ff_v[slot, 1], preferred_element_type=jnp.float32)
        sigma = jax.nn.sigmoid(gate)
        silu = gate * sigma
        tile_v[slot, 0] = (up_value * sigma * (1.0 + gate * (1.0 - sigma))).astype(jnp.bfloat16)
        tile_v[slot, 1] = silu.astype(jnp.bfloat16)
        hidden = (silu * up_value).astype(jnp.bfloat16)
        tile_v[slot, 2] = hidden
        g_tile_v[slot] = jnp.dot(
            hidden.T, branch_v[...], preferred_element_type=jnp.float32
        ).astype(jnp.bfloat16)
        for kind in range(3):
            tile_store(n, slot, kind).start()
        grad_store(n, slot).start()

        return carry

    lax.fori_loop(0, count, ff_step, 0)
    for n in range(count - 2, count):
        for kind in range(3):
            tile_store(n, n % 2, kind).wait()
        grad_store(n, n % 2).wait()
    rows_finish(1)
    for copy in stores:
        if copy is not normed_store:
            copy.wait()
    for k in range(3):
        part_copy(k).wait_send()
    for index in range(3):
        row_wait_send(index)
    for copy in started:
        copy.wait_send()


def turn(source, target):
    def step(k, carry):
        first = pl.multiple_of(256 * k, 256)
        target[pl.ds(first, 256), :] = source[:, pl.ds(first, 256)].T
        return carry

    lax.fori_loop(0, source.shape[1] // 256, step, 0)


ROTARY_STEP = 32


def rotary_parts(length):
    lane = np.arange(2 * HD)
    pace = np.exp(-(lane % (HD // 2)) * (math.log(10000.0) / (HD // 2)))
    sign = np.where(lane % HD < HD // 2, -1.0, 1.0)
    far = np.arange(0, length, ROTARY_STEP)[:, None] * pace
    near = np.arange(ROTARY_STEP)[:, None] * pace
    parts = (np.cos(far), np.sin(far), sign * np.cos(far), sign * np.sin(far), np.cos(near), np.sin(near))
    return np.concatenate(parts).astype(np.float32)


def fill_rotary(parts, cosine, sine):
    steps = cosine.shape[0] // ROTARY_STEP
    near_cos = parts[4 * steps : 4 * steps + ROTARY_STEP, :]
    near_sin = parts[4 * steps + ROTARY_STEP : 4 * steps + 2 * ROTARY_STEP, :]

    def step(k, carry):
        far_cos, far_sin, sign_cos, sign_sin = (parts[pl.ds(steps * which + k, 1), :] for which in range(4))
        rows = pl.ds(pl.multiple_of(ROTARY_STEP * k, ROTARY_STEP), ROTARY_STEP)
        cosine[rows, :] = far_cos * near_cos - far_sin * near_sin
        sine[rows, :] = sign_sin * near_cos + sign_cos * near_sin
        return carry

    lax.fori_loop(0, steps, step, 0)


def norm_rows(read, gain, target, length, step=64):
    def chunk(k, carry):
        part = pl.ds(pl.multiple_of(k * step, step), step)
        values = read(part)
        scale = lax.rsqrt(jnp.mean(values * values, axis=-1, keepdims=True) + EPS)
        target[part, :] = (values * scale * gain).astype(target.dtype)
        return carry

    lax.fori_loop(0, length // step, chunk, 0)


def attend(pair, width, heads, start, mixed, lse):
    length = heads.shape[0]
    lane = lax.broadcasted_iota(jnp.int32, (BLK, 128), 1)
    cols = [pl.ds(pl.multiple_of(width * kind + 128 * pair, 128), 128) for kind in range(3)]
    for i in range(length // BLK):
        own_rows, keys = slice(BLK * i, BLK * (i + 1)), BLK * (i + 1)
        place = lax.broadcasted_iota(jnp.int32, (BLK, keys), 1)
        own = BLK * i + lax.broadcasted_iota(jnp.int32, (BLK, keys), 0)
        allowed = (place >= start[own_rows, :]) & (place <= own)
        query = heads[own_rows, cols[0]] * jnp.bfloat16(0.125)
        key, value = heads[0:keys, cols[1]], heads[0:keys, cols[2]]
        kept = lse[own_rows, :]
        outs = []
        for half in range(2):
            part = slice(64 * half, 64 * half + 64)
            scores = jnp.where(allowed, nt(query[:, part], key[:, part]), -1e30)
            peak = jnp.max(scores, axis=-1, keepdims=True)
            expo = jnp.exp(scores - peak)
            total = jnp.sum(expo, axis=-1, keepdims=True)
            out = jnp.dot(expo.astype(jnp.bfloat16), value[:, part], preferred_element_type=jnp.float32)
            outs.append((out / total).astype(jnp.bfloat16))
            kept = jnp.where(lane == 2 * pair + half, peak + jnp.log(total), kept)
        mixed[own_rows, cols[0]] = jnp.concatenate(outs, axis=1)
        lse[own_rows, :] = kept


def gather_all(tokens, segments, out_grad, gains, weights):
    rows, width = tokens.shape[1], tokens.shape[2]
    length, half, ff = 4 * rows, width // 2, weights[4].shape[1]
    half_ff = ff // 2
    low = jnp.bfloat16

    def shape(*dims, dtype=low):
        return jax.ShapeDtypeStruct(dims, dtype)

    shapes = [
        shape(length, width),
        shape(4, *segments.shape[1:], dtype=jnp.int32),
        shape(length, width),
        shape(8, *gains.shape),
        shape(width, 3 * half),
        shape(half, width),
        shape(width, ff),
        shape(half_ff, width),
        shape(length, 3 * half),
        shape(128, length, dtype=jnp.float32),
        shape(length, width, dtype=jnp.float32),
        shape(length, half_ff),
        shape(length, half_ff),
        shape(length, half_ff),
        shape(half_ff, width),
        shape(1, length, dtype=jnp.int32),
        shape(2, width, dtype=jnp.float32),
        shape(width, length),
        shape(width, length),
        shape(half, length),
        shape(length, 128, dtype=jnp.float32),
        shape(length, 128, dtype=jnp.float32),
    ]
    dma, vmem = pltpu.SemaphoreType.DMA, pltpu.VMEM
    whole = pl.BlockSpec(memory_space=pltpu.VMEM)
    return pl.pallas_call(
        gather_kernel,
        in_specs=[ANY] * 4 + [whole] + [ANY] * 7,
        out_specs=[ANY] * len(shapes),
        out_shape=shapes,
        scratch_shapes=[
            dma((7, 7)), dma((7, 7)), dma((7,)), dma((3, 4)), dma((3, 4)), dma((3,)), dma((7,)), dma((8,)),
            vmem((length, width), low),
            vmem((4,) + segments.shape[1:], jnp.int32),
            vmem((8,) + gains.shape, low),
            vmem((length, width), low),
            vmem((width, 3 * half), low),
            vmem((length, 3 * half), low),
            vmem((length, half), low),
            vmem((half, width), low),
            vmem((length, width), jnp.float32),
            vmem((length, width), low),
            vmem((length, width), low),
            vmem((length, width), low),
            vmem((2, 2, width, 256), low),
            vmem((length, width), low),
            vmem((2, 3, length, 256), low),
            vmem((2, 256, width), low),
            vmem((length, 128), jnp.float32),
            vmem((length, 1), jnp.int32),
            vmem((128, length), jnp.float32),
            vmem((1, length), jnp.int32),
            vmem((2, width), jnp.float32),
            vmem((width, length), low),
            vmem((half, length), low),
            vmem((length, 128), jnp.float32),
            vmem((length, 128), jnp.float32),
            dma((2, 3)), dma((3,)), dma((3, 3)), dma((3, 2, 3)), dma((11,)),
        ],
        compiler_params=pltpu.CompilerParams(
            collective_id=0, has_side_effects=True, vmem_limit_bytes=61 * 1024 * 1024
        ),
        cost_estimate=pl.CostEstimate(flops=0, bytes_accessed=500_000_000, transcendentals=0),
        name="gather_all",
    )(tokens, segments, out_grad, gains, jnp.asarray(rotary_parts(length)), *weights)


def guard(condition, action):
    if isinstance(condition, (bool, np.bool_)):
        if condition:
            action()
    else:
        pl.when(condition)(action)


def everything(*conditions):
    known = [c for c in conditions if isinstance(c, (bool, np.bool_))]
    if not all(known):
        return False
    rest = [c for c in conditions if not isinstance(c, (bool, np.bool_))]
    if not rest:
        return True
    total = rest[0]
    for c in rest[1:]:
        total = total & c
    return total


def chunk_of(rows):
    return 384 if rows % 384 == 0 else 512


def add_rows(target, first, other, rows):
    step = chunk_of(rows)

    def chunk(k, carry):
        at = pl.multiple_of(k * step, step)
        source = pl.multiple_of(first + k * step, step)
        target[pl.ds(at, step), :] += other[pl.ds(source, step), :]
        return carry

    lax.fori_loop(0, rows // step, chunk, 0)


JOB = 256


class Stream:
    active = True

    def tick(self, t):
        for late, stage in reversed(self.stages):
            k = t - late
            guard(everything(k >= 0, k < self.count), functools.partial(stage, k))

    @property
    def ticks(self):
        return self.count + self.stages[-1][0]

    def slot(self, k):
        return k % self.slots if isinstance(k, int) else lax.rem(k, self.slots)

    def column(self, k, base=0):
        return pl.ds(pl.multiple_of(base + JOB * k, 128), JOB)

    def total(self, k):
        return self.second.at[self.slot(k)]

    def final(self, k):
        return self.got.at[self.slot(k), pl.ds(0, self.rows)]

    def seq_copy(self, k, step):
        me, slot, sem = self.me, self.slot(k), self.seq_sem
        inner = me.z + 1 - 2 * (me.z // 2)
        opposite = 3 - me.z
        outer = 3 * (me.z // 2)
        if step == 0:
            return remote(self.total(k), self.over.at[slot, 0], sem.at[slot, 0, 0], sem.at[slot, 1, 0], me.dp, inner)
        if step == 1:
            return remote(
                self.total(k), self.over.at[slot, 1], sem.at[slot, 0, 1], sem.at[slot, 1, 1], me.dp, opposite
            )
        return remote(self.final(k), self.final(k), sem.at[slot, 0, 2], sem.at[slot, 1, 2], me.dp, outer)

    def plane_and_ends(self, k):
        self.reduce_plane(k)
        guard(
            everything(self.active, jnp.logical_not(self.me.middle)),
            lambda: self.seq_copy(k, 0).start(),
        )

    def across(self, k):
        def action():
            self.seq_copy(k, 0).wait_recv()
            add_rows(self.total(k), 0, self.over.at[self.slot(k), 0], self.rows)
            self.seq_copy(k, 1).start()

        guard(everything(self.active, self.me.middle), action)

    def back(self, k):
        def action():
            self.seq_copy(k, 1).wait_recv()
            final, total, over = self.final(k), self.total(k), self.over.at[self.slot(k), 1]
            step = chunk_of(self.rows)

            def chunk(at, carry):
                part = pl.ds(pl.multiple_of(at * step, step), step)
                final[part, :] = total[part, :] + over[part, :]
                return carry

            lax.fori_loop(0, self.rows // step, chunk, 0)
            self.seq_copy(k, 2).start()

        guard(everything(self.active, self.me.middle), action)

    def finish(self, k):
        guard(
            everything(self.active, jnp.logical_not(self.me.middle)),
            lambda: self.seq_copy(k, 2).wait_recv(),
        )
        self.output(k)

    def drain(self, k):
        self.drain_plane(k)

        def ends():
            self.seq_copy(k, 0).wait_send()

        def middles():
            self.seq_copy(k, 1).wait_send()
            self.seq_copy(k, 2).wait_send()

        guard(everything(self.active, jnp.logical_not(self.me.middle)), ends)
        guard(everything(self.active, self.me.middle), middles)


class ColumnStream(Stream):
    def __init__(self, me, source, target, ff_jobs, d_model, ff, refs):
        self.me, self.source, self.target = me, source, target
        self.got, self.keep, self.second, self.over, self.sem, self.seq_sem, self.credit = refs
        self.slots, self.rows = self.got.shape[0], source.shape[1] // 4
        self.count, self.ff_jobs = source.shape[0], ff_jobs
        self.ff, self.d_model = ff, d_model
        self.stages = (
            *zip(LATE["C"], (self.pass_second, self.plane_and_ends, self.across, self.back, self.finish, self.drain)),
        )

    def x_first(self, k):
        late = k // self.ff_jobs
        return (1 - late) * ((k + self.ff_jobs // 2 - 2) // self.ff_jobs) * ((k + 1) % 2) + late * (k % 2)

    def first_copy(self, k, part):
        me, slot, x_first = self.me, self.slot(k), self.x_first(k)
        block = x_first * (2 * part + 1 - me.x) + (1 - x_first) * (2 * (1 - me.y) + part)
        sent = self.source.at[k, pl.ds(pl.multiple_of(self.rows * block, self.rows), self.rows)]
        to = x_first * me.over_x + (1 - x_first) * me.over_y
        return remote(
            sent, self.got.at[slot, pl.ds(self.rows * part, self.rows)],
            self.sem.at[slot, 0, part], self.sem.at[slot, 1, part], to, me.z,
        )

    def keep_copy(self, k, part):
        me, slot, x_first = self.me, self.slot(k), self.x_first(k)
        block = x_first * (2 * part + me.x) + (1 - x_first) * (2 * me.y + part)
        kept = self.source.at[k, pl.ds(pl.multiple_of(self.rows * block, self.rows), self.rows)]
        return pltpu.make_async_copy(
            kept, self.keep.at[slot, pl.ds(self.rows * part, self.rows)], self.sem.at[slot, 2, part]
        )

    def at(self, k):
        x_first = self.x_first(k)
        return x_first * self.me.y + (1 - x_first) * self.me.x

    def second_copy(self, k):
        me, slot, x_first = self.me, self.slot(k), self.x_first(k)
        row = pl.multiple_of(self.rows * (1 - self.at(k)), self.rows)
        to = x_first * me.over_y + (1 - x_first) * me.over_x
        return remote(
            self.keep.at[slot, pl.ds(row, self.rows)], self.second.at[slot],
            self.sem.at[slot, 0, 2], self.sem.at[slot, 1, 2], to, me.z,
        )

    def start(self, k):
        def credits():
            slot = self.slot(k)

            @pl.when(self.me.middle)
            def _():
                pl.semaphore_wait(self.credit.at[slot], 5)

            @pl.when(jnp.logical_not(self.me.middle))
            def _():
                pl.semaphore_wait(self.credit.at[slot], 4)

        guard(k >= self.slots, credits)
        for part in range(2):
            self.first_copy(k, part).start()
            self.keep_copy(k, part).start()

    def pass_second(self, k):
        for part in range(2):
            self.keep_copy(k, part).wait()
            self.first_copy(k, part).wait_recv()
        slot = self.slot(k)
        add_rows(self.keep.at[slot], 0, self.got.at[slot], 2 * self.rows)
        self.second_copy(k).start()

    def reduce_plane(self, k):
        self.second_copy(k).wait_recv()
        add_rows(self.total(k), self.rows * self.at(k), self.keep.at[self.slot(k)], self.rows)

    def out_column(self, k, core, late):
        if late:
            m, half = k - self.ff_jobs, self.d_model // 2
            tiles = half // JOB
            first = 2 * self.ff + self.d_model * (m // tiles) + JOB * (m % tiles) + half * core
        else:
            first = self.ff * (k % 2) + JOB * (k // 2) + self.ff // 2 * core
        return self.target.at[:, pl.ds(pl.multiple_of(first, 128), JOB)]

    def last_copy(self, k, late=False):
        me, slot, rows = self.me, self.slot(k), self.rows // 2
        part = self.got.at[slot, pl.ds(pl.multiple_of(rows * (1 - me.core), rows), rows)]
        return remote(
            part, self.out_column(k, me.core, late), self.sem.at[slot, 0, 3], self.sem.at[slot, 1, 3],
            me.over_core, me.z,
        )

    def own_copy(self, k, late=False):
        me, slot, rows = self.me, self.slot(k), self.rows // 2
        part = self.got.at[slot, pl.ds(pl.multiple_of(rows * me.core, rows), rows)]
        return pltpu.make_async_copy(part, self.out_column(k, me.core, late), self.sem.at[slot, 2, 0])

    def output(self, k):
        def begin(late):
            self.last_copy(k, late).start()
            self.own_copy(k, late).start()

        guard(k < self.ff_jobs, lambda: begin(False))
        guard(k >= self.ff_jobs, lambda: begin(True))

    def drain_plane(self, k):
        for part in range(2):
            self.first_copy(k, part).wait_send()
        self.second_copy(k).wait_send()

        def end(late):
            self.last_copy(k, late).wait()
            self.own_copy(k, late).wait()

        guard(k < self.ff_jobs, lambda: end(False))
        guard(k >= self.ff_jobs, lambda: end(True))

    def drain(self, k):
        super().drain(k)

        def signal(dp, seq):
            pl.semaphore_signal(
                self.credit.at[self.slot(k)], inc=1, device_id={"dp": dp, "seq": seq},
                device_id_type=pl.DeviceIdType.MESH,
            )

        def free():
            me = self.me
            for dp in (me.over_core, me.over_x, me.over_y):
                signal(dp, me.z)

            @pl.when(me.middle)
            def _():
                signal(me.dp, 3 - me.z)
                signal(me.dp, 3 * (me.z // 2))

            @pl.when(jnp.logical_not(me.middle))
            def _():
                signal(me.dp, me.z + 1 - 2 * (me.z // 2))

        guard(k + self.slots < self.count, free)


class RowStream(Stream):
    def __init__(self, me, source, target, lates, refs):
        self.me, self.source, self.target = me, source, target
        self.got, self.second, self.over, self.stage, self.sem, self.seq_sem = refs
        self.slots, self.rows = self.got.shape[0], self.got.shape[1]
        self.count = self.slots
        self.active = me.core == me.y
        steps = (self.pass_second, self.plane_and_ends, self.across, self.back, self.finish, self.drain)
        self.stages = tuple(zip(lates, steps))

    def first_copy(self, k):
        me, slot = self.me, self.slot(k)
        return remote(self.part(k, 1 - me.x), self.got.at[slot], self.sem.at[slot, 0, 0], self.sem.at[slot, 1, 0], me.over_x, me.z)

    def part(self, k, x):
        rows = pl.ds(pl.multiple_of(self.rows * x, self.rows), self.rows)
        return self.source.at[k, rows] if len(self.source.shape) == 3 else self.source.at[rows, self.column(k)]

    def load_copy(self, k):
        return pltpu.make_async_copy(self.part(k, self.me.x), self.stage, self.sem.at[self.slot(k), 2, 0])

    def second_copy(self, k):
        me, slot = self.me, self.slot(k)
        return remote(
            self.got.at[slot], self.second.at[slot], self.sem.at[slot, 0, 2], self.sem.at[slot, 1, 2],
            me.over_y, me.z,
        )

    def start(self, k):
        self.first_copy(k).start()
        guard(k == 0, lambda: self.load_copy(k).start())

    def pass_second(self, k):
        self.load_copy(k).wait()
        self.first_copy(k).wait_recv()
        add_rows(self.got.at[self.slot(k)], 0, self.stage, self.rows)
        guard(k + 1 < self.count, lambda: self.load_copy(k + 1).start())
        guard(jnp.logical_not(self.active), lambda: self.second_copy(k).start())

    def reduce_plane(self, k):
        def action():
            self.second_copy(k).wait_recv()
            add_rows(self.total(k), 0, self.got.at[self.slot(k)], self.rows)

        guard(self.active, action)

    def last_copy(self, k):
        me, slot, rows = self.me, self.slot(k), self.rows // 2
        part = self.got.at[slot, pl.ds(pl.multiple_of(rows * (1 - me.core), rows), rows)]
        return remote(
            part, self.target.at[:, self.column(k)], self.sem.at[slot, 0, 3], self.sem.at[slot, 1, 3],
            me.over_core, me.z,
        )

    def own_copy(self, k):
        me, slot, rows = self.me, self.slot(k), self.rows // 2
        part = self.got.at[slot, pl.ds(pl.multiple_of(rows * me.core, rows), rows)]
        return pltpu.make_async_copy(part, self.target.at[:, self.column(k)], self.sem.at[slot, 2, 1])

    def output(self, k):
        def action():
            self.last_copy(k).start()
            self.own_copy(k).start()

        guard(self.active, action)

    def drain_plane(self, k):
        self.first_copy(k).wait_send()

        def active():
            self.last_copy(k).wait_send()
            self.own_copy(k).wait()

        def passive():
            self.second_copy(k).wait_send()
            self.last_copy(k).wait_recv()

        guard(self.active, active)
        guard(jnp.logical_not(self.active), passive)


PLAN = {
    "s0": {"E": (0, 3)},
    "a": {"E": (3, 4, 4, 5, 5, 5, 6, 6, 6), "S": (0, 1, 2, 3, 3, 5, 5, 5, 5), "C": (0, 0, 0, 0, 0, 1, 1, 2, 2), "D": (0, 0, 0, 0, 1, 1, 1, 1, 1)},
    "l0": {"D": (1, 2)},
    "l1": {"S": (5, 6), "D": (2, 3)},
    "l2": {"S": (6, 8)},
    "i": {"S": (8, 8, 8, 8, 9, 9, 10), "C": (2, 2, 2, 2, 3, 3, 3), "D": (3, 3, 3, 3, 4, 4, 4)},
    "n0": {"S": (10, 12), "C": (3, 5)},
    "n1": {"C": (5, 6)},
    "n2": {"C": (8, 9)},
    "o": {"C": (6, 7, 7, 7, 8, 8, 8), "D": (4, 4, 4, 4, 4, 4, 5)},
    "h": {"S": (12, 13, 13, 14, 14, 15, 15), "C": (9, 10, 11, 12, 13, 13, 13), "D": (5, 6, 7, 7, 7, 8, 9)},
    "t": {"S": (15, 16, 16, 16, 16, 16, 16), "F": (0, 0, 1, 1, 2, 3, 3), "C": (13, 14, 14, 15, 15, 15, 16), "D": (9, 10, 10, 10, 10, 10, 11)},
    "t6": {"F": (3, 4)},
    "p": {"S": (16, 16, 17, 18, 19, 20, 20, 20, 20, 20), "O": (0, 0, 1, 1, 1, 2, 3, 3, 3, 3)},
    "p9": {},
}
LATE = {"C": (0, 2, 4, 6, 7, 8), "D": (0, 2, 4, 6, 7, 8), "O": (0, 2, 4, 6, 7, 8)}


class Pace:
    def __init__(self, cols, downs, outs):
        self.actions = {
            "E": downs.start, "S": cols.start, "F": outs.start, "C": cols.tick, "D": downs.tick, "O": outs.tick,
        }

    def at(self, place, n=0):
        for kind, bounds in PLAN[place].items():
            action = self.actions[kind]

            def one(t, carry, action=action):
                action(t)
                return carry

            if isinstance(n, int):
                low, high = bounds[n], bounds[n + 1]
                if high - low == 1:
                    action(low)
                elif high > low:
                    lax.fori_loop(low, high, one, 0)
                continue
            low, high = bounds[0], bounds[1]
            for k in range(1, len(bounds) - 1):
                reached = (n + 32 - k) // 32
                low = low + (bounds[k] - bounds[k - 1]) * reached
                high = high + (bounds[k + 1] - bounds[k]) * reached
            lax.fori_loop(low, high, one, 0)


GAIN_HOPS = 5


class GainSums:
    def __init__(self, me, target, buffer, sem):
        self.me, self.target, self.buffer, self.sem = me, target, buffer, sem

    def hop(self, k):
        me = self.me
        across = me.z + 2 - 4 * (me.z // 2)
        beside = me.z + 1 - 2 * (me.z % 2)
        dp = (me.over_core, me.over_x, me.over_y, me.dp, me.dp)[k]
        seq = (me.z, me.z, me.z, beside, across)[k]
        return remote(
            self.buffer.at[k, 0], self.buffer.at[k, 1], self.sem.at[0, k], self.sem.at[1, k], dp, seq
        )

    def start(self):
        self.hop(0).start()

    def step(self, k):
        self.hop(k).wait_recv()
        total = self.buffer[k, 0] + self.buffer[k, 1]
        if k + 1 < GAIN_HOPS:
            self.buffer[k + 1, 0] = total
            self.hop(k + 1).start()
        else:
            self.target[...] = total

    def drain(self):
        for k in range(GAIN_HOPS):
            self.hop(k).wait_send()


class RowsBack:
    def __init__(self, me, source, target, sem):
        self.me, self.source, self.target, self.sem = me, source, target, sem

    def each(self, local, elsewhere):
        me = self.me
        rows = self.source.shape[0] // 2
        for slot in range(2):
            core, seq = me.z % 2, 2 * me.core + slot
            here = (core == me.core) & (seq == me.z)
            block, target = self.source.at[pl.ds(rows * slot, rows)], self.target.at[me.z // 2]

            @pl.when(here)
            def _():
                local(pltpu.make_async_copy(block, target, self.sem.at[2, 0]))

            @pl.when(jnp.logical_not(here))
            def _():
                elsewhere(
                    remote(
                        block, target, self.sem.at[0, slot], self.sem.at[1, me.z // 2],
                        me.dp - me.core + core, seq,
                    )
                )

    def start(self):
        self.each(lambda copy: copy.start(), lambda copy: copy.start())

    def drain(self):
        me = self.me
        self.each(lambda copy: copy.wait(), lambda copy: copy.wait_send())
        rows = self.source.shape[0] // 2
        for m in range(2):
            here = (me.z == 2 * m + me.core) & (me.core == me.z // 2)

            @pl.when(jnp.logical_not(here))
            def _():
                remote(
                    self.source.at[pl.ds(0, rows)], self.target.at[m], self.sem.at[0, 0],
                    self.sem.at[1, m], me.over_core, me.z,
                ).wait_recv()


def attend_back(pair, width, heads, grad_mixed, start, lse, grads, key_sum, value_sum, query_sum, cosine, sine):
    length = heads.shape[0]
    cols = [pl.ds(pl.multiple_of(width * kind + 128 * pair, 128), 128) for kind in range(3)]
    key_sum[...] = jnp.zeros_like(key_sum)
    value_sum[...] = jnp.zeros_like(value_sum)
    for i in range(length // BLK):
        own_rows, keys = slice(BLK * i, BLK * (i + 1)), BLK * (i + 1)
        place = lax.broadcasted_iota(jnp.int32, (keys, BLK), 0)
        own = BLK * i + lax.broadcasted_iota(jnp.int32, (keys, BLK), 1)
        allowed = (place >= start[:, own_rows]) & (place <= own)
        query = heads[own_rows, cols[0]] * jnp.bfloat16(0.125)
        key, value = heads[0:keys, cols[1]], heads[0:keys, cols[2]]
        grad = grad_mixed[own_rows, cols[0]]
        for half in range(2):
            part = slice(64 * half, 64 * half + 64)
            scores = nt(key[:, part], query[:, part])
            logsum = lse[pl.ds(2 * pair + half, 1), own_rows]
            probs = jnp.where(allowed, jnp.exp(scores - logsum), 0.0)
            grad_probs = nt(value[:, part], grad[:, part])
            inner = jnp.sum(probs * grad_probs, axis=0, keepdims=True)
            grad_scores = (probs * (grad_probs - inner)).astype(jnp.bfloat16)
            value_sum[0:keys, part] += dot(probs.astype(jnp.bfloat16), grad[:, part])
            key_sum[0:keys, part] += dot(grad_scores, query[:, part])
            query_sum[own_rows, part] = tn(grad_scores, key[:, part]) * 0.125
    for kind, total in enumerate((query_sum, key_sum)):
        value = total[...]
        grads[:, cols[kind]] = (value * cosine[...] - swap_halves(value) * sine[...]).astype(jnp.bfloat16)
    grads[:, cols[2]] = value_sum[...].astype(jnp.bfloat16)


def backward_kernel(
    branch_h, slope_gate_h, slope_up_h, hidden_h, nf_t_h, normed_t_h, mixed_t_h, heads_h, lse_h, middle_h, x_h,
    g_down_h, w_qkv_h, w_o_h, w_ff_h, w_down_h, start_ref, gain_ref, cosine, sine,
    out_o, tokens_o, cols_o, o_o, down_o, gains_o, g_cols_h, g_o_h, kept_h, rows_h, grad_nf_h,
    col_got, col_keep, col_second, col_over, col_sem, col_seq, col_credit,
    down_got, down_second, down_over, down_stage, down_sem, down_seq,
    o_got, o_second, o_over, o_stage, o_sem, o_seq,
    wide_recv, half_recv, half_free, wide_sem, half_sem,
    gain_buffer, gain_sem, row_sem, load_sem, tile_sem, store_sem,
):
    me = Place()
    enter(
        [(me.over_core, me.z), (me.over_x, me.z), (me.over_y, me.z)]
        + [(me.dp - me.core + core, lax.rem(me.z + k, 4)) for k in range(1, 4) for core in range(2)]
    )
    length, width = branch_h.shape
    half_rows, own_width, half_ff = length // 2, width // 2, slope_gate_h.shape[1]
    bf16, f32 = jnp.bfloat16, jnp.float32
    vmem = pltpu.VMEM
    ff_jobs = 2 * half_ff // JOB
    cols = ColumnStream(
        me, g_cols_h, cols_o, ff_jobs, width, 2 * half_ff,
        (col_got, col_keep, col_second, col_over, col_sem, col_seq, col_credit),
    )
    downs = RowStream(
        me, g_down_h, down_o, LATE["D"], (down_got, down_second, down_over, down_stage, down_sem, down_seq)
    )
    outs = RowStream(me, g_o_h, o_o, LATE["O"], (o_got, o_second, o_over, o_stage, o_sem, o_seq))
    back_out = RowsBack(me, rows_h.at[0], out_o, row_sem.at[0])
    back_tokens = RowsBack(me, rows_h.at[1], tokens_o, row_sem.at[1])
    gains = GainSums(me, gains_o, gain_buffer, gain_sem)

    def load(source, target, k=0):
        return pltpu.make_async_copy(source, target, load_sem.at[k])

    def fetch(*pairs):
        for k, (source, target) in enumerate(pairs):
            load(source, target, k).start()
        for k, (source, target) in enumerate(pairs):
            load(source, target, k).wait()

    def lanes(n, size=JOB, base=0):
        return pl.ds(pl.multiple_of(base + size * n, 128), size)

    def sublanes(n, size):
        return pl.ds(pl.multiple_of(n * size, size), size)

    def grad_store(buffer, slot, target, n, k):
        return pltpu.make_async_copy(buffer.at[slot], target.at[n], store_sem.at[slot, k])

    pace = Pace(cols, downs, outs)
    pace.at("s0")

    def feed_forward(grad_ff):
        steps = half_ff // JOB

        def hidden_grads(branch, w_tile, slopes, nf_t, g_tile):
            def tile_loads(n, slot):
                return (
                    pltpu.make_async_copy(w_down_h.at[sublanes(n, JOB), :], w_tile.at[slot], tile_sem.at[slot, 0]),
                    pltpu.make_async_copy(slope_gate_h.at[:, lanes(n)], slopes.at[slot, 0], tile_sem.at[slot, 1]),
                    pltpu.make_async_copy(slope_up_h.at[:, lanes(n)], slopes.at[slot, 1], tile_sem.at[slot, 2]),
                )

            for copy in tile_loads(0, 0):
                copy.start()
            load(nf_t_h, nf_t, 1).start()
            fetch((branch_h, branch))

            def step(n, carry):
                slot = lax.rem(n, 2)
                for copy in tile_loads(n, slot):
                    copy.wait()

                @pl.when(n + 1 < steps)
                def _():
                    for copy in tile_loads(n + 1, 1 - slot):
                        copy.start()

                grad_hidden = nt(branch[...], w_tile[slot])

                @pl.when(n == 0)
                def _():
                    load(nf_t_h, nf_t, 1).wait()

                @pl.when(n > 1)
                def _():
                    for kind in range(2):
                        grad_store(g_tile, kind, g_cols_h, 2 * n - 2 + kind, 0).wait()

                for kind in range(2):
                    grad = (grad_hidden * slopes[slot, kind].astype(f32)).astype(bf16)
                    grad_ff[:, lanes(n, JOB, half_ff * kind)] = grad
                    g_tile[kind] = dot(nf_t[...], grad).astype(bf16)
                    grad_store(g_tile, kind, g_cols_h, 2 * n + kind, 0).start()

                @pl.when(n == 0)
                def _():
                    for kind in range(2):
                        grad_store(g_tile, kind, g_cols_h, kind, 0).wait()

                pace.at("a", n)

                return carry

            lax.fori_loop(0, steps, step, 0)
            for kind in range(2):
                grad_store(g_tile, kind, g_cols_h, 2 * steps - 2 + kind, 0).wait()

        pl.run_scoped(
            hidden_grads, vmem((length, width), bf16), vmem((2, JOB, width), bf16),
            vmem((2, 2, length, JOB), bf16), vmem((width, length), bf16), vmem((2, width, JOB), bf16),
        )

        def layer_out(hidden, w_down, send, total):
            other, own = 1 - me.core, me.core
            def w_load(n):
                return load(w_down_h.at[:, lanes(n)], w_down.at[:, lanes(n)], 4 + n)

            load(hidden_h.at[sublanes(other, half_rows), :], hidden, 0).start()
            for n in range(width // JOB):
                w_load(n).start()
            load(hidden_h.at[sublanes(other, half_rows), :], hidden, 0).wait()
            load(middle_h.at[sublanes(own, half_rows), :], total, 2).start()

            def other_tile(n, carry):
                w_load(n).wait()
                send[:, lanes(n)] = dot(hidden[...], w_down[:, lanes(n)]).astype(bf16)
                return carry

            lax.fori_loop(0, width // JOB, other_tile, 0)
            exchange = remote(send, half_recv, half_sem.at[0, 0], half_sem.at[1, 0], me.over_core, me.z)
            exchange.start()
            pace.at("l0")
            fetch((hidden_h.at[sublanes(own, half_rows), :], hidden))
            load(middle_h.at[sublanes(own, half_rows), :], total, 2).wait()

            def own_tile(n, carry):
                total[:, lanes(n)] += dot(hidden[...], w_down[:, lanes(n)])
                return carry

            lax.fori_loop(0, width // JOB, own_tile, 0)
            pace.at("l1")
            exchange.wait()

            def combine(k, carry):
                part = sublanes(k, 64)
                send[part, :] = (total[part, :] + half_recv[part, :].astype(f32)).astype(bf16)
                return carry

            lax.fori_loop(0, half_rows // 64, combine, 0)
            pl.semaphore_signal(
                half_free, inc=1, device_id={"dp": me.over_core, "seq": me.z},
                device_id_type=pl.DeviceIdType.MESH,
            )
            fetch((send, rows_h.at[0]))

        pl.run_scoped(
            layer_out, vmem((half_rows, half_ff), bf16), vmem((half_ff, width), bf16),
            vmem((half_rows, width), bf16), vmem((half_rows, width), f32),
        )
        back_out.start()
        pace.at("l2")

    chunk = 2 * JOB
    chunks = width // chunk

    def wide_copy(send, k):
        part = pl.ds(chunk * k, chunk)
        return remote(
            send.at[:, part], wide_recv.at[:, part], wide_sem.at[0, k], wide_sem.at[1, k], me.over_core, me.z
        )

    def with_grad_ff(grad_ff):
        feed_forward(grad_ff)

        def input_grads(w_tile, send, parts):
            def tile_load(n, kind):
                return pltpu.make_async_copy(
                    w_ff_h.at[sublanes(n, JOB), pl.ds(half_ff * kind, half_ff)], w_tile.at[kind],
                    tile_sem.at[kind, 0],
                )

            def part_store(n, slot):
                return pltpu.make_async_copy(parts.at[slot], grad_nf_h.at[:, lanes(n)], store_sem.at[slot, 0])

            for kind in range(2):
                tile_load(0, kind).start()
            count = width // JOB

            def step(n, carry):
                slot = lax.rem(n, 2)
                tile_load(n, 0).wait()
                part = nt(grad_ff[:, 0:half_ff], w_tile[0])

                @pl.when(n + 1 < count)
                def _():
                    tile_load(n + 1, 0).start()

                tile_load(n, 1).wait()
                part = part + nt(grad_ff[:, half_ff : 2 * half_ff], w_tile[1])

                @pl.when(n + 1 < count)
                def _():
                    tile_load(n + 1, 1).start()

                @pl.when(n >= 2)
                def _():
                    part_store(n - 2, slot).wait()

                parts[slot] = part
                part_store(n, slot).start()
                send[:, lanes(n)] = part.astype(bf16)
                for k in range(chunks):
                    @pl.when(n == 2 * k + 1)
                    def _():
                        wide_copy(send, k).start()

                pace.at("i", n)

                return carry

            lax.fori_loop(0, count, step, 0)
            for n in range(count - 2, count):
                part_store(n, n % 2).wait()
            pace.at("n0")
            for k in range(chunks):
                wide_copy(send, k).wait()

        pl.run_scoped(
            input_grads, vmem((2, JOB, half_ff), bf16), vmem((length, width), bf16), vmem((2, length, JOB), f32)
        )

    pl.run_scoped(with_grad_ff, vmem((length, 2 * half_ff), bf16))

    def to_attention(grad_attn):
        def norm_back(grad_nf, middle, branch):
            def quarter(q):
                part = sublanes(q, length // 4)
                pairs = ((middle_h, middle), (branch_h, branch), (grad_nf_h, grad_nf))
                return [
                    load(source.at[part, :], target.at[part, :], 4 + 3 * q + k)
                    for k, (source, target) in enumerate(pairs)
                ]

            for q in range(4):
                for copy in quarter(q):
                    copy.start()
            gain = gain_ref[1:2, :]

            def rows(k, total):
                part = sublanes(k, 64)
                grad = grad_nf[part, :] + wide_recv[part, :].astype(f32)
                gained, values = norm_rows_back(middle[part, :], gain, grad)
                values = values + branch[part, :].astype(f32)
                grad_nf[part, :] = values
                grad_attn[part, :] = values.astype(bf16)
                return total + gained

            def quarter_rows(q, total):
                for copy in quarter(q):
                    copy.wait()
                return lax.fori_loop(length // 256 * q, length // 256 * (q + 1), rows, total)

            total = lax.fori_loop(0, 4, quarter_rows, jnp.zeros((1, width), f32))
            gain_buffer[0, 0, 1:2, :] = 0.5 * total
            kept = load(grad_nf.at[sublanes(me.core, half_rows), :], kept_h, 0)
            kept.start()
            pace.at("n1")
            kept.wait()

        pl.run_scoped(
            norm_back, vmem((length, width), f32), vmem((length, width), f32), vmem((length, width), bf16)
        )

        def out_projection(w_o, mixed_t, g_tile, grad_mixed):
            fetch((w_o_h, w_o), (mixed_t_h, mixed_t))

            def mixed_step(n, carry):
                grad_mixed[:, lanes(n)] = nt(grad_attn[...], w_o[sublanes(n, JOB), :]).astype(bf16)
                return carry

            lax.fori_loop(0, own_width // JOB, mixed_step, 0)
            placed = load(grad_mixed, wide_recv.at[:, pl.ds(0, own_width)], 3)
            placed.start()
            count = width // JOB

            def step(n, carry):
                slot = lax.rem(n, 2)

                @pl.when(n >= 2)
                def _():
                    grad_store(g_tile, slot, g_o_h, n - 2, 1).wait()

                g_tile[slot] = dot(mixed_t[...], grad_attn[:, lanes(n)]).astype(bf16)
                grad_store(g_tile, slot, g_o_h, n, 1).start()

                pace.at("o", n)

                return carry

            lax.fori_loop(0, count, step, 0)
            for n in range(count - 2, count):
                grad_store(g_tile, n % 2, g_o_h, n, 1).wait()
            placed.wait()

        pl.run_scoped(
            out_projection, vmem((own_width, width), bf16), vmem((own_width, length), bf16),
            vmem((2, own_width, JOB), bf16), vmem((length, own_width), bf16),
        )

    pl.run_scoped(to_attention, vmem((length, width), bf16))
    pace.at("n2")

    def attention(grads):
        def heads_back(heads, lse, key_sum, value_sum, query_sum):
            fetch((heads_h, heads), (lse_h, lse))

            def step(pair, carry):
                attend_back(
                    pair, own_width, heads, wide_recv, start_ref, lse, grads, key_sum, value_sum, query_sum, cosine, sine
                )
                pace.at("h", pair)
                return carry

            lax.fori_loop(0, own_width // 128, step, 0)

        pl.run_scoped(
            heads_back, vmem((length, 3 * own_width), bf16), vmem((128, length), f32),
            *[vmem((length, 128), f32)] * 3,
        )

        def tokens_back(w_tile, send, total, x_rows, kept):
            def tile_load(n, slot):
                return pltpu.make_async_copy(w_qkv_h.at[sublanes(n, JOB), :], w_tile.at[slot], tile_sem.at[slot, 0])

            tile_load(0, 0).start()
            load(x_h.at[sublanes(me.core, half_rows), :], x_rows, 0).start()
            load(kept_h, kept, 1).start()
            count = width // JOB

            def step(n, carry):
                slot = lax.rem(n, 2)
                tile_load(n, slot).wait()

                @pl.when(n + 1 < count)
                def _():
                    tile_load(n + 1, 1 - slot).start()

                send[:, lanes(n)] = nt(grads[sublanes(1 - me.core, half_rows), :], w_tile[slot]).astype(bf16)
                total[:, lanes(n)] = nt(grads[sublanes(me.core, half_rows), :], w_tile[slot])

                pace.at("t", n)
                return carry

            lax.fori_loop(0, count, step, 0)
            pl.semaphore_wait(half_free, 1)
            exchange = remote(send, half_recv, half_sem.at[0, 0], half_sem.at[1, 0], me.over_core, me.z)
            exchange.start()
            pace.at("t6")
            load(x_h.at[sublanes(me.core, half_rows), :], x_rows, 0).wait()
            load(kept_h, kept, 1).wait()
            exchange.wait()
            gain = gain_ref[0:1, :]

            def rows(k, sums):
                part = sublanes(k, 64)
                grad = total[part, :] + half_recv[part, :].astype(f32)
                gained, values = norm_rows_back(x_rows[part, :].astype(f32), gain, grad)
                send[part, :] = (values + kept[part, :]).astype(bf16)
                return sums + gained

            gain_buffer[0, 0, 0:1, :] = lax.fori_loop(0, half_rows // 64, rows, jnp.zeros((1, width), f32))
            gains.start()
            fetch((send, rows_h.at[1]))

        pl.run_scoped(
            tokens_back, vmem((2, JOB, 3 * own_width), bf16), vmem((half_rows, width), bf16),
            vmem((half_rows, width), f32), vmem((half_rows, width), bf16), vmem((half_rows, width), f32),
        )
        back_tokens.start()

        def projection_grads(normed_t, g_tile):
            fetch((normed_t_h, normed_t))
            count = 3 * own_width // JOB

            def step(n, carry):
                slot = lax.rem(n, 2)
                g_tile[slot] = dot(normed_t[...], grads[:, lanes(n)]).astype(bf16)

                @pl.when(n >= 1)
                def _():
                    grad_store(g_tile, 1 - slot, g_cols_h, ff_jobs + n - 1, 1).wait()

                grad_store(g_tile, slot, g_cols_h, ff_jobs + n, 1).start()

                pace.at("p", n)
                return carry

            lax.fori_loop(0, count, step, 0)
            grad_store(g_tile, (count - 1) % 2, g_cols_h, ff_jobs + count - 1, 1).wait()

        pl.run_scoped(projection_grads, vmem((width, length), bf16), vmem((2, width, JOB), bf16))

        pace.at("p9")

    pl.run_scoped(attention, vmem((length, 3 * own_width), bf16))

    first = {"E": 6, "S": 20, "F": 4, "C": 16, "D": 11, "O": 3}
    later = max(0, first["S"] - first["C"] - cols.slots + LATE["C"][-1] + 1)
    steps = max(stream.ticks - first[kind] for kind, stream in (("C", cols), ("D", downs), ("O", outs)))

    def rest(t, carry):
        for kind, stream in (("E", downs), ("S", cols), ("F", outs)):
            if first[kind] < stream.count:
                k = first[kind] + t - (later if kind == "S" else 0)
                guard((k >= first[kind]) & (k < stream.count), functools.partial(stream.start, k))
        for kind, stream in (("C", cols), ("D", downs), ("O", outs)):
            if first[kind] < stream.ticks:
                stream.tick(first[kind] + t)
        for k in range(GAIN_HOPS - 1):
            @pl.when(t == k)
            def _():
                gains.step(k)

        return carry

    lax.fori_loop(0, steps, rest, 0)
    for k in range(min(steps, GAIN_HOPS - 1), GAIN_HOPS):
        gains.step(k)
    gains.drain()
    back_out.drain()
    back_tokens.drain()


def norm_rows_back(values, gain, grad):
    scale = lax.rsqrt(jnp.mean(values * values, axis=-1, keepdims=True) + EPS)
    unit = values * scale
    inner = grad * gain
    return (
        jnp.sum(grad * unit, axis=0, keepdims=True),
        scale * (inner - unit * jnp.mean(inner * unit, axis=-1, keepdims=True)),
    )


COLUMN_SLOTS = 12


def backward(branch, slopes, hidden, turned, heads, lse, middle, x, g_down, weights, start, gain, cosine, sine):
    length, width = branch.shape
    half, half_ff = width // 2, hidden.shape[1]
    rows = length // 4
    bf16, f32 = jnp.bfloat16, jnp.float32

    def shape(*dims, dtype=bf16):
        return jax.ShapeDtypeStruct(dims, dtype)

    columns = 2 * half_ff + 3 * half
    shapes = [
        shape(2, rows, width),
        shape(2, rows, width),
        shape(width // 8, 2 * columns),
        shape(width // 8, width),
        shape(half_ff // 4, width),
        shape(2, width, dtype=f32),
        shape(columns // JOB, width, JOB),
        shape(width // JOB, half, JOB),
        shape(length // 2, width, dtype=f32),
        shape(2, length // 2, width),
        shape(length, width, dtype=f32),
    ]
    dma, vmem = pltpu.SemaphoreType.DMA, pltpu.VMEM
    whole = pl.BlockSpec(memory_space=pltpu.VMEM)
    ring, row = COLUMN_SLOTS, width // 4
    jobs = width // JOB
    row_buffers = []
    for depth in (half_ff // 2, half // 2):
        row_buffers += [
            vmem((jobs, depth, JOB), bf16), vmem((jobs, depth, JOB), bf16), vmem((jobs, 2, depth, JOB), bf16),
            vmem((depth, JOB), bf16), dma((jobs, 3, 4)), dma((jobs, 2, 3)),
        ]
    return pl.pallas_call(
        backward_kernel,
        in_specs=[ANY] * 16 + [whole] * 4,
        out_specs=[ANY] * 5 + [whole] + [ANY] * 5,
        out_shape=shapes,
        scratch_shapes=[
            vmem((ring, 2 * row, JOB), bf16), vmem((ring, 2 * row, JOB), bf16), vmem((ring, row, JOB), bf16),
            vmem((ring, 2, row, JOB), bf16), dma((ring, 3, 4)), dma((ring, 2, 3)),
            pltpu.SemaphoreType.REGULAR((ring,)),
        ]
        + row_buffers
        + [
            vmem((length, width), bf16), vmem((length // 2, width), bf16), pltpu.SemaphoreType.REGULAR,
            dma((2, 3)), dma((2, 1)),
            vmem((GAIN_HOPS, 2, 2, width), f32), dma((2, GAIN_HOPS)), dma((2, 3, 2)), dma((16,)), dma((2, 3)),
            dma((2, 2)),
        ],
        compiler_params=pltpu.CompilerParams(
            collective_id=1, has_side_effects=True, vmem_limit_bytes=63 * 1024 * 1024
        ),
        cost_estimate=pl.CostEstimate(flops=0, bytes_accessed=800_000_000, transcendentals=0),
        name="backward",
    )(
        branch, *slopes, hidden, *turned, heads, lse, middle, x, g_down, *weights, start, gain, cosine, sine
    )


def wide(value):
    return value.astype(jnp.float32)


def dot(a, b):
    return jnp.dot(a, b, preferred_element_type=jnp.float32)


WIDEN_STEPS = 4


def widen_kernel(cols, o, down, tokens, result, *outs):
    first = 0
    for out in outs[:5]:
        out[...] = cols[:, first : first + out.shape[1]].astype(jnp.float32)
        first += out.shape[1]
    for source, out in zip((o, down, tokens, result), outs[5:]):
        out[...] = source[...].astype(out.dtype)


def widen(cols, o, down, tokens, result, ff):
    depth, width = o.shape

    def rows(count, columns):
        return pl.BlockSpec((count // WIDEN_STEPS, columns), lambda i: (i, 0))

    shapes = [(depth, ff)] * 2 + [(depth, width)] * 4 + [down.shape, tokens.shape, result.shape]
    return pl.pallas_call(
        widen_kernel,
        grid=(WIDEN_STEPS,),
        in_specs=[rows(*value.shape) for value in (cols, o, down, tokens, result)],
        out_specs=[rows(*shape) for shape in shapes],
        out_shape=[jax.ShapeDtypeStruct(shape, jnp.float32) for shape in shapes[:-1]]
        + [jax.ShapeDtypeStruct(result.shape, result.dtype)],
        compiler_params=pltpu.CompilerParams(vmem_limit_bytes=63 * 1024 * 1024),
        name="widen",
    )(cols, o, down, tokens, result)


def column_device(
    tokens, segment_ids, out_grad, w_q, w_k, w_v, w_o, w_gate, w_up, w_down, gain_attn, gain_ffn
):
    dp_at = lax.axis_index("dp")
    rows, width = tokens.shape[1], tokens.shape[2]
    length, ff = 4 * rows, w_gate.shape[1]
    gains = lax.dynamic_update_slice_in_dim(
        jnp.zeros((2, width), jnp.bfloat16),
        jnp.stack([gain_attn, gain_ffn]),
        dp_at * gain_attn.shape[0],
        1,
    )
    (
        x_low, docs, grad_branch, gains, full_qkv, full_o, full_ff, full_down, heads, lse, middle,
        slope_gate, slope_up, hidden, g_down, start, gain, normed_t, nf_t, mixed_t,
        cosine, sine,
    ) = gather_all(
        tokens, segment_ids.reshape(2, 1, rows), out_grad, gains,
        (w_q, w_k, w_v, w_o, w_gate, w_up, w_down),
    )
    result, grad_tokens, g_cols, g_o, g_down, grad_gains = backward(
        grad_branch, (slope_gate, slope_up), hidden, (nf_t, normed_t, mixed_t), heads, lse, middle, x_low, g_down,
        (full_qkv, full_o, full_ff, full_down), start, gain, cosine, sine,
    )[:6]
    grad_gains = lax.dynamic_slice_in_dim(grad_gains, dp_at * (width // 8), width // 8, 1)
    flat = (2 * rows, width)
    gate, up, query, key, value, out, down, grad_tokens, result = widen(
        g_cols, g_o, g_down, grad_tokens.reshape(flat), result.reshape(flat), ff
    )
    result = result.reshape(2, rows, width)
    return (
        result, grad_tokens.reshape(2, rows, width), query, key, value, out, gate, up, down, grad_gains[0], grad_gains[1]
    )


def solution(mesh):
    placed = (
        P(None, ("dp", "seq"), None),
        P(None, ("dp", "seq")),
        P(None, ("dp", "seq"), None),
        P("dp", None),
        P("dp", None),
        P("dp", None),
        P("dp", None),
        P("dp", None),
        P("dp", None),
        P("dp", None),
        P("dp"),
        P("dp"),
    )
    return jax.shard_map(
        column_device if dict(mesh.shape) == FAST_MESH else per_device,
        mesh=mesh,
        in_specs=placed,
        out_specs=(
            P(None, ("dp", "seq"), None),
            P(None, ("dp", "seq"), None),
            P("dp", None),
            P("dp", None),
            P("dp", None),
            P("dp", None),
            P("dp", None),
            P("dp", None),
            P("dp", None),
            P("dp"),
            P("dp"),
        ),
        check_vma=False,
    )
```

```python
import functools
import math

import jax
import jax.numpy as jnp
import numpy as np
from jax import lax
from jax.experimental import pallas as pl
from jax.experimental.pallas import tpu as pltpu
from jax.sharding import PartitionSpec as P

HEADS = 24
HD = 64


EPS = 1e-05


def positions_of(doc_row):
    count = doc_row.shape[0]
    place = jnp.arange(count, dtype=jnp.int32)
    before = jnp.concatenate([doc_row[:1], doc_row[:-1]])
    starts = (place == 0) | (doc_row != before)
    first_place = lax.cummax(jnp.where(starts, place, jnp.zeros_like(place)), axis=0)
    return place - first_place


def rope_tables(where_at, half):
    inverse = jnp.exp(jnp.arange(half, dtype=jnp.float32) * (-math.log(10000.0) / half))
    angle = where_at.astype(jnp.float32)[:, None] * inverse[None, :]
    return (jnp.cos(angle), jnp.sin(angle))


def rotate(values, cosine, sine):
    half = values.shape[-1] // 2
    first, second = (values[..., :half], values[..., half:])
    cos_heads, sin_heads = (cosine[:, None, :], sine[:, None, :])
    return jnp.concatenate(
        [first * cos_heads - second * sin_heads, second * cos_heads + first * sin_heads], axis=-1
    )


def rotate_back(grads, cosine, sine):
    half = grads.shape[-1] // 2
    first, second = (grads[..., :half], grads[..., half:])
    cos_heads, sin_heads = (cosine[:, None, :], sine[:, None, :])
    return jnp.concatenate(
        [first * cos_heads + second * sin_heads, second * cos_heads - first * sin_heads], axis=-1
    )


def rms_norm(values, gain):
    return values * lax.rsqrt(jnp.mean(values * values, axis=-1, keepdims=True) + EPS) * gain


def norm_backward(values, gain, grad_normed):
    scale = lax.rsqrt(jnp.mean(values * values, axis=-1, keepdims=True) + EPS)
    unit = values * scale
    grad_gain = jnp.sum(grad_normed * unit, axis=0)
    inner = grad_normed * gain
    grad_values = scale * (inner - unit * jnp.mean(inner * unit, axis=-1, keepdims=True))
    return (grad_gain, grad_values)


def block_scores(query_heads, key_heads, doc_row, start, block):
    length = doc_row.shape[0]
    place = jnp.arange(length, dtype=jnp.int32)
    query_block = lax.dynamic_slice_in_dim(query_heads, start, block, 0)
    doc_block = lax.dynamic_slice_in_dim(doc_row, start, block, 0)
    rows_block = start + jnp.arange(block, dtype=jnp.int32)
    allowed = (doc_block[:, None] == doc_row[None, :]) & (rows_block[:, None] >= place[None, :])
    scores = (
        jnp.einsum("qhd,khd->hqk", query_block, key_heads, preferred_element_type=jnp.float32)
        * 0.125
    )
    return (query_block, jnp.where(allowed[None], scores, -1e30))


def attention_forward(query, key, value, doc_row):
    length = query.shape[0]
    head_shape = (length, query.shape[1] // HD, HD)
    query_heads, key_heads, value_heads = (
        query.reshape(head_shape),
        key.reshape(head_shape),
        value.reshape(head_shape),
    )
    block = min(512, length)
    starts = jnp.arange(length // block, dtype=jnp.int32) * block

    def one_block(start):
        unused, scores = block_scores(query_heads, key_heads, doc_row, start, block)
        peak = jnp.max(scores, axis=-1, keepdims=True)
        expo = jnp.exp(scores - peak)
        total = jnp.sum(expo, axis=-1, keepdims=True)
        probs_low = (expo / total).astype(jnp.bfloat16)
        mixed = jnp.einsum(
            "hqk,khd->qhd", probs_low, value_heads, preferred_element_type=jnp.float32
        )
        return (mixed.astype(jnp.bfloat16), (peak + jnp.log(total))[..., 0])

    mixed, logsum = lax.map(one_block, starts)
    return (mixed.reshape(length, query.shape[1]), logsum)


def attention_backward(query, key, value, doc_row, logsum, grad_mixed, cosine, sine):
    length = query.shape[0]
    head_shape = (length, query.shape[1] // HD, HD)
    query_heads, key_heads, value_heads = (
        query.reshape(head_shape),
        key.reshape(head_shape),
        value.reshape(head_shape),
    )
    grad_heads = grad_mixed.reshape(head_shape)
    block = min(512, length)
    starts = jnp.arange(length // block, dtype=jnp.int32) * block

    def one_block(carry, item):
        grad_key, grad_value = carry
        start, logsum_block = item
        query_block, scores = block_scores(query_heads, key_heads, doc_row, start, block)
        probs = jnp.exp(scores - logsum_block[..., None])
        probs_low = probs.astype(jnp.bfloat16)
        grad_block = lax.dynamic_slice_in_dim(grad_heads, start, block, 0)
        grad_probs = jnp.einsum(
            "qhd,khd->hqk", grad_block, value_heads, preferred_element_type=jnp.float32
        )
        inner = jnp.sum(probs * grad_probs, axis=-1, keepdims=True)
        grad_scores = (probs * (grad_probs - inner)).astype(jnp.bfloat16)
        grad_query = (
            jnp.einsum("hqk,khd->qhd", grad_scores, key_heads, preferred_element_type=jnp.float32)
            * 0.125
        )
        grad_key = (
            grad_key
            + jnp.einsum(
                "hqk,qhd->khd", grad_scores, query_block, preferred_element_type=jnp.float32
            )
            * 0.125
        )
        grad_value = grad_value + jnp.einsum(
            "hqk,qhd->khd", probs_low, grad_block, preferred_element_type=jnp.float32
        )
        return ((grad_key, grad_value), grad_query)

    zeros_heads = jnp.zeros(head_shape, jnp.float32)
    (grad_key, grad_value), grad_query = lax.scan(
        one_block, (zeros_heads, zeros_heads), (starts, logsum)
    )
    grad_query = rotate_back(grad_query.reshape(head_shape), cosine, sine)
    grad_key = rotate_back(grad_key, cosine, sine)
    width_here = query.shape[1]
    return (
        grad_query.reshape(length, width_here).astype(jnp.bfloat16),
        grad_key.reshape(length, width_here).astype(jnp.bfloat16),
        grad_value.reshape(length, width_here).astype(jnp.bfloat16),
    )


def per_device(
    tokens, segment_ids, out_grad, w_q, w_k, w_v, w_o, w_gate, w_up, w_down, gain_attn, gain_ffn
):
    micro, rows, width = tokens.shape
    offset = lax.axis_index("seq") * rows
    shards = (w_q, w_k, w_v, w_o, w_gate, w_up, w_down, gain_attn, gain_ffn)
    gathered = (
        lax.all_gather(shards[0], "dp", axis=0, tiled=True),
        lax.all_gather(shards[1], "dp", axis=0, tiled=True),
        lax.all_gather(shards[2], "dp", axis=0, tiled=True),
        lax.all_gather(shards[3], "dp", axis=0, tiled=True),
        lax.all_gather(shards[4], "dp", axis=0, tiled=True),
        lax.all_gather(shards[5], "dp", axis=0, tiled=True),
        lax.all_gather(shards[6], "dp", axis=0, tiled=True),
        lax.all_gather(shards[7], "dp", axis=0, tiled=True),
        lax.all_gather(shards[8], "dp", axis=0, tiled=True),
    )
    docs = lax.all_gather(segment_ids, "seq", axis=1, tiled=True)
    full_q, full_k, full_v, full_o, full_gate, full_up, full_down, full_gain_a, full_gain_f = (
        gathered
    )
    gain_a = full_gain_a.astype(jnp.float32)
    gain_f = full_gain_f.astype(jnp.float32)
    row_heads = (rows, HEADS, HD)
    saved = []
    results = []
    for micro_index in range(micro):
        rows_in = tokens[micro_index].astype(jnp.float32)
        doc_row = docs[micro_index]
        cosine, sine = rope_tables(positions_of(doc_row), HD // 2)
        own_cos = lax.dynamic_slice_in_dim(cosine, offset, rows, 0)
        own_sin = lax.dynamic_slice_in_dim(sine, offset, rows, 0)
        normed = rms_norm(rows_in, gain_a).astype(jnp.bfloat16)
        query_rows = jnp.dot(normed, full_q, preferred_element_type=jnp.float32).reshape(row_heads)
        query_rows = rotate(query_rows, own_cos, own_sin).reshape(rows, width).astype(jnp.bfloat16)
        key_rows = jnp.dot(normed, full_k, preferred_element_type=jnp.float32).reshape(row_heads)
        key_rows = rotate(key_rows, own_cos, own_sin).reshape(rows, width).astype(jnp.bfloat16)
        value_rows = jnp.dot(normed, full_v, preferred_element_type=jnp.float32).astype(
            jnp.bfloat16
        )
        query, key, value = (
            lax.all_to_all(query_rows, "seq", split_axis=1, concat_axis=0, tiled=True),
            lax.all_to_all(key_rows, "seq", split_axis=1, concat_axis=0, tiled=True),
            lax.all_to_all(value_rows, "seq", split_axis=1, concat_axis=0, tiled=True),
        )
        mixed, logsum = attention_forward(query, key, value, doc_row)
        mixed_rows = lax.all_to_all(mixed, "seq", split_axis=0, concat_axis=1, tiled=True)
        middle = rows_in + jnp.dot(mixed_rows, full_o, preferred_element_type=jnp.float32)
        normed_ffn = rms_norm(middle, gain_f).astype(jnp.bfloat16)
        gate = jnp.dot(normed_ffn, full_gate, preferred_element_type=jnp.float32)
        up_value = jnp.dot(normed_ffn, full_up, preferred_element_type=jnp.float32)
        hidden = (jax.nn.silu(gate) * up_value).astype(jnp.bfloat16)
        result = middle + jnp.dot(hidden, full_down, preferred_element_type=jnp.float32)
        results.append(result.astype(jnp.bfloat16))
        saved.append(
            (
                rows_in,
                doc_row,
                cosine,
                sine,
                normed,
                query,
                key,
                value,
                logsum,
                mixed_rows,
                middle,
                normed_ffn,
                gate,
                up_value,
                hidden,
            )
        )
    back_weights = (
        lax.all_gather(shards[0], "dp", axis=0, tiled=True),
        lax.all_gather(shards[1], "dp", axis=0, tiled=True),
        lax.all_gather(shards[2], "dp", axis=0, tiled=True),
        lax.all_gather(shards[3], "dp", axis=0, tiled=True),
        lax.all_gather(shards[4], "dp", axis=0, tiled=True),
        lax.all_gather(shards[5], "dp", axis=0, tiled=True),
        lax.all_gather(shards[6], "dp", axis=0, tiled=True),
        lax.all_gather(shards[7], "dp", axis=0, tiled=True),
        lax.all_gather(shards[8], "dp", axis=0, tiled=True),
    )
    back_q, back_k, back_v, back_o, back_gate, back_up, back_down, back_gain_a, back_gain_f = (
        back_weights
    )
    gain_back_a = back_gain_a.astype(jnp.float32)
    gain_back_f = back_gain_f.astype(jnp.float32)
    totals = [jnp.zeros(weight.shape, jnp.float32) for weight in back_weights]
    grad_inputs = []
    for micro_index in range(micro):
        (
            rows_in,
            doc_row,
            cosine,
            sine,
            normed,
            query,
            key,
            value,
            logsum,
            mixed_rows,
            middle,
            normed_ffn,
            gate,
            up_value,
            hidden,
        ) = saved[micro_index]
        grad_out = out_grad[micro_index].astype(jnp.float32)
        grad_branch = grad_out.astype(jnp.bfloat16)
        totals[6] = totals[6] + jnp.einsum(
            "tf,td->fd", hidden, grad_branch, preferred_element_type=jnp.float32
        )
        grad_hidden = jnp.einsum(
            "td,fd->tf", grad_branch, back_down, preferred_element_type=jnp.float32
        )
        sigma = jax.nn.sigmoid(gate)
        grad_gate = (grad_hidden * up_value * sigma * (1.0 + gate * (1.0 - sigma))).astype(
            jnp.bfloat16
        )
        grad_up = (grad_hidden * jax.nn.silu(gate)).astype(jnp.bfloat16)
        totals[4] = totals[4] + jnp.einsum(
            "td,tf->df", normed_ffn, grad_gate, preferred_element_type=jnp.float32
        )
        totals[5] = totals[5] + jnp.einsum(
            "td,tf->df", normed_ffn, grad_up, preferred_element_type=jnp.float32
        )
        grad_normed_ffn = jnp.einsum(
            "tf,df->td", grad_gate, back_gate, preferred_element_type=jnp.float32
        )
        grad_normed_ffn = grad_normed_ffn + jnp.einsum(
            "tf,df->td", grad_up, back_up, preferred_element_type=jnp.float32
        )
        grad_gain_f, grad_middle = norm_backward(middle, gain_back_f, grad_normed_ffn)
        totals[8] = totals[8] + grad_gain_f
        grad_middle = grad_middle + grad_out
        grad_attn = grad_middle.astype(jnp.bfloat16)
        totals[3] = totals[3] + jnp.einsum(
            "ti,td->id", mixed_rows, grad_attn, preferred_element_type=jnp.float32
        )
        grad_mixed_rows = jnp.einsum(
            "td,id->ti", grad_attn, back_o, preferred_element_type=jnp.float32
        ).astype(jnp.bfloat16)
        grad_mixed = lax.all_to_all(grad_mixed_rows, "seq", split_axis=1, concat_axis=0, tiled=True)
        grad_query, grad_key, grad_value = attention_backward(
            query, key, value, doc_row, logsum, grad_mixed, cosine, sine
        )
        query_back, key_back, value_back = (
            lax.all_to_all(grad_query, "seq", split_axis=0, concat_axis=1, tiled=True),
            lax.all_to_all(grad_key, "seq", split_axis=0, concat_axis=1, tiled=True),
            lax.all_to_all(grad_value, "seq", split_axis=0, concat_axis=1, tiled=True),
        )
        totals[0] = totals[0] + jnp.einsum(
            "td,te->de", normed, query_back, preferred_element_type=jnp.float32
        )
        totals[1] = totals[1] + jnp.einsum(
            "td,te->de", normed, key_back, preferred_element_type=jnp.float32
        )
        totals[2] = totals[2] + jnp.einsum(
            "td,te->de", normed, value_back, preferred_element_type=jnp.float32
        )
        grad_normed = jnp.einsum(
            "te,de->td", query_back, back_q, preferred_element_type=jnp.float32
        )
        grad_normed = grad_normed + jnp.einsum(
            "te,de->td", key_back, back_k, preferred_element_type=jnp.float32
        )
        grad_normed = grad_normed + jnp.einsum(
            "te,de->td", value_back, back_v, preferred_element_type=jnp.float32
        )
        grad_gain_a, grad_rows = norm_backward(rows_in, gain_back_a, grad_normed)
        totals[7] = totals[7] + grad_gain_a
        grad_inputs.append(grad_rows + grad_middle)
    summed_all = (
        totals[0],
        totals[1],
        totals[2],
        totals[3],
        totals[4],
        totals[5],
        totals[6],
        totals[7],
        totals[8],
    )
    pieces = (
        lax.psum_scatter(
            summed_all[0].astype(jnp.bfloat16), "dp", scatter_dimension=0, tiled=True
        ).astype(jnp.float32),
        lax.psum_scatter(
            summed_all[1].astype(jnp.bfloat16), "dp", scatter_dimension=0, tiled=True
        ).astype(jnp.float32),
        lax.psum_scatter(
            summed_all[2].astype(jnp.bfloat16), "dp", scatter_dimension=0, tiled=True
        ).astype(jnp.float32),
        lax.psum_scatter(
            summed_all[3].astype(jnp.bfloat16), "dp", scatter_dimension=0, tiled=True
        ).astype(jnp.float32),
        lax.psum_scatter(
            summed_all[4].astype(jnp.bfloat16), "dp", scatter_dimension=0, tiled=True
        ).astype(jnp.float32),
        lax.psum_scatter(
            summed_all[5].astype(jnp.bfloat16), "dp", scatter_dimension=0, tiled=True
        ).astype(jnp.float32),
        lax.psum_scatter(
            summed_all[6].astype(jnp.bfloat16), "dp", scatter_dimension=0, tiled=True
        ).astype(jnp.float32),
        lax.psum_scatter(
            summed_all[7].astype(jnp.bfloat16), "dp", scatter_dimension=0, tiled=True
        ).astype(jnp.float32),
        lax.psum_scatter(
            summed_all[8].astype(jnp.bfloat16), "dp", scatter_dimension=0, tiled=True
        ).astype(jnp.float32),
    )
    pieces = (
        lax.psum(pieces[0].astype(jnp.bfloat16), "seq").astype(jnp.float32),
        lax.psum(pieces[1].astype(jnp.bfloat16), "seq").astype(jnp.float32),
        lax.psum(pieces[2].astype(jnp.bfloat16), "seq").astype(jnp.float32),
        lax.psum(pieces[3].astype(jnp.bfloat16), "seq").astype(jnp.float32),
        lax.psum(pieces[4].astype(jnp.bfloat16), "seq").astype(jnp.float32),
        lax.psum(pieces[5].astype(jnp.bfloat16), "seq").astype(jnp.float32),
        lax.psum(pieces[6].astype(jnp.bfloat16), "seq").astype(jnp.float32),
        lax.psum(pieces[7].astype(jnp.bfloat16), "seq").astype(jnp.float32),
        lax.psum(pieces[8].astype(jnp.bfloat16), "seq").astype(jnp.float32),
    )
    return (
        jnp.stack(results),
        jnp.stack(grad_inputs),
        pieces[0],
        pieces[1],
        pieces[2],
        pieces[3],
        pieces[4],
        pieces[5],
        pieces[6],
        pieces[7],
        pieces[8],
    )


BLK = 256
LOG2E = 1.4426950408889634


def swap_halves(v):
    lane = lax.broadcasted_iota(jnp.int32, v.shape, 1)
    width = v.shape[1]
    up = pltpu.roll(v, width - 32, axis=1)
    down = pltpu.roll(v, 32, axis=1)
    return jnp.where(lane % 64 < 32, up, down)


def nt(a, b):
    return lax.dot_general(a, b, (((1,), (1,)), ((), ())), preferred_element_type=jnp.float32)


def tn(a, b):
    return lax.dot_general(a, b, (((0,), (0,)), ((), ())), preferred_element_type=jnp.float32)


FAST_MESH = {"dp": 8, "seq": 4}
ANY = pl.BlockSpec(memory_space=pl.ANY)


class Place:
    def __init__(self):
        self.dp, self.z = lax.axis_index("dp"), lax.axis_index("seq")
        self.core = self.dp % 2
        self.x = (self.dp // 2) % 2
        self.y = self.dp // 4
        self.over_core = self.dp + 1 - 2 * self.core
        self.over_x = self.dp + 2 - 4 * self.x
        self.over_y = self.dp + 4 - 8 * self.y
        self.middle = (self.z == 1) | (self.z == 2)


def enter(devices):
    barrier = pltpu.get_barrier_semaphore()
    for dp, seq in devices:
        pl.semaphore_signal(
            barrier, inc=1, device_id={"dp": dp, "seq": seq}, device_id_type=pl.DeviceIdType.MESH
        )
    pl.semaphore_wait(barrier, len(devices))


def remote(src, dst, send_sem, recv_sem, dp, seq):
    return pltpu.make_async_remote_copy(
        src_ref=src,
        dst_ref=dst,
        send_sem=send_sem,
        recv_sem=recv_sem,
        device_id={"dp": dp, "seq": seq},
        device_id_type=pl.DeviceIdType.MESH,
    )


def gather_kernel(
    tokens, segments, out_grad, gains, rotary, w_q, w_k, w_v, w_o, w_gate, w_up, w_down,
    x_out, seg_out, g_out, gains_out, qkv_out, o_out, ff_out, down_out,
    heads_out, lse_out, middle_out, slope_gate_out, slope_up_out, hidden_out, g_down_out, start_out,
    gain_out, normed_t_out, nf_t_out, mixed_t_out, cosine_out, sine_out,
    send, recv, local, row_send, row_recv, row_local, gain_send, gain_recv,
    x_v, seg_v, gains_v, normed_v, w_qkv_v, heads_v, mixed_v, w_o_v, middle_v, part_send, part_recv,
    nf_v, w_ff_v, branch_v, tile_v, g_tile_v, lse_v, start_v, lse_t_v, start_row_v, gain_v, turned_v, mixed_t_v, cosine, sine,
    part_sem, load_sem, w_sem, tile_sem, store_sem,
):
    me = Place()
    rows = tokens.shape[1]
    plane = [(lax.rem(me.dp + k, 8), me.z) for k in range(1, 8)]
    column = [
        (me.dp - me.core + core, lax.rem(me.z + k, 4)) for k in range(1, 4) for core in range(2)
    ]
    enter(plane + column)
    started = []

    def begin(copy):
        copy.start()
        started.append(copy)

    streams = ((tokens, x_out), (segments, seg_out), (out_grad, g_out))

    def place_of(ref, seq):
        return ref.at[pl.ds(rows * seq, rows)] if ref.shape[0] == 4 * rows else ref.at[seq]

    def row_copies(index):
        source, target = streams[index]
        for m in range(2):
            core, seq = me.z // 2, 2 * m + me.core
            here = (core == me.core) & (seq == me.z)

            @pl.when(here)
            def _():
                pltpu.make_async_copy(
                    source.at[m], place_of(target, me.z), row_local.at[index]
                ).start()

            @pl.when(jnp.logical_not(here))
            def _():
                remote(
                    source.at[m], place_of(target, me.z), row_send.at[index, m],
                    row_recv.at[index, me.z % 2], me.dp - me.core + core, seq,
                ).start()

    def row_wait_send(index):
        source, target = streams[index]
        for m in range(2):
            core, seq = me.z // 2, 2 * m + me.core
            here = (core == me.core) & (seq == me.z)

            @pl.when(jnp.logical_not(here))
            def _():
                remote(
                    source.at[m], place_of(target, me.z), row_send.at[index, m],
                    row_recv.at[index, me.z % 2], me.dp - me.core + core, seq,
                ).wait_send()

    def row_relay(index):
        source, target = streams[index]
        for slot in range(2):
            seq = 2 * me.core + slot
            block = place_of(target, seq)
            here = (seq == me.z) & (me.z % 2 == me.core)

            @pl.when(here)
            def _():
                pltpu.make_async_copy(block, block, row_local.at[index]).wait()

            @pl.when(jnp.logical_not(here))
            def _():
                remote(
                    block, block, row_send.at[index, slot], row_recv.at[index, slot], me.over_core, me.z
                ).wait_recv()

            begin(
                remote(
                    block, block, row_send.at[index, 2 + slot], row_recv.at[index, 2 + slot],
                    me.over_core, me.z,
                )
            )

    def row_finish(index):
        source, target = streams[index]
        for slot in range(2):
            block = place_of(target, 2 * (1 - me.core) + slot)
            remote(
                block, block, row_send.at[index, 2 + slot], row_recv.at[index, 2 + slot], me.over_core, me.z
            ).wait_recv()

    by_columns = []
    base = 0
    for source in (w_q, w_k, w_v):
        by_columns.append((source, qkv_out, base))
        base += source.shape[1] // 2
    by_columns.append((w_gate, ff_out, 0))
    by_columns.append((w_up, ff_out, w_gate.shape[1] // 2))
    by_rows = [(w_o, o_out), (w_down, down_out)]

    def column_piece(index, owner):
        source, target, first = by_columns[index]
        depth, width = source.shape[0], source.shape[1] // 2
        return target.at[pl.ds(depth * owner, depth), pl.ds(first, width)]

    def columns_start(index):
        source, target, first = by_columns[index]
        width = source.shape[1] // 2
        mine = column_piece(index, me.dp)
        for core in range(2):
            half = source.at[:, pl.ds(width * core, width)]
            begin(remote(half, mine, send.at[index, core], recv.at[index, me.core],
                         me.over_x - me.core + core, me.z))
            begin(remote(half, mine, send.at[index, 2 + core], recv.at[index, 2 + me.core],
                         me.over_y - me.core + core, me.z))

            @pl.when(core == me.core)
            def _():
                pltpu.make_async_copy(half, mine, local.at[index]).start()

            @pl.when(core != me.core)
            def _():
                remote(half, mine, send.at[index, 4], recv.at[index, 4], me.over_core, me.z).start()

    beside = me.z + 1 - 2 * lax.rem(me.z, 2)
    corner = me.over_x + me.over_y - me.dp - me.core

    def turn_of(index):
        return lax.rem(index + me.z, 2)

    last = 6

    def hand_on(index, piece, came, slot, send_slot, dp, seq):
        remote(piece, piece, send.at[index, send_slot], recv.at[index, came], dp, seq).wait_recv()
        remote(piece, piece, send.at[index, send_slot], recv.at[index, slot], dp, seq).start()

    def arrived(index, piece, slot):
        remote(piece, piece, send.at[index, 5], recv.at[index, slot], me.over_core, me.z).wait_recv()

    def left(index, piece, slot):
        remote(piece, piece, send.at[index, slot], recv.at[index, 5], me.over_core, me.z).wait_send()

    def columns_relay(index):
        @pl.when(turn_of(index) == 0)
        def _():
            hand_on(index, column_piece(index, me.over_x - me.core), 0, 5, 5, me.over_y, me.z)

        @pl.when(turn_of(index) == 1)
        def _():
            hand_on(index, column_piece(index, me.over_y - me.core + 1), 3, 6, 6, me.over_x, me.z)

    def columns_forward(index):
        @pl.when(turn_of(index) == 0)
        def _():
            hand_on(index, column_piece(index, corner), 5, 5, 6, me.dp, beside)

        @pl.when(turn_of(index) == 1)
        def _():
            hand_on(index, column_piece(index, corner + 1), 6, 6, 5, me.dp, beside)

    def columns_finish(index):
        source, target, first = by_columns[index]
        width = source.shape[1] // 2
        arrived(index, column_piece(index, me.over_x - me.core + 1), 1)
        arrived(index, column_piece(index, me.over_y - me.core), 2)
        arrived(index, column_piece(index, me.over_core), 4)

        @pl.when(turn_of(index) == 0)
        def _():
            arrived(index, column_piece(index, me.over_y - me.core + 1), 3)
            arrived(index, column_piece(index, corner + 1), 6)

        @pl.when(turn_of(index) == 1)
        def _():
            arrived(index, column_piece(index, me.over_x - me.core), 0)
            arrived(index, column_piece(index, corner), 5)

        mine = column_piece(index, me.dp)
        pltpu.make_async_copy(mine, mine, local.at[index]).wait()
        for slot in (4, 5, 6):
            left(index, mine, slot)

    def row_piece(which, owner):
        source, target = by_rows[which]
        depth = source.shape[0]
        return target.at[pl.ds(depth * lax.rem(owner, 4), depth), :]

    def rows_start(which):
        source, target = by_rows[which]
        index = 5 + which
        mine = row_piece(which, me.dp)
        begin(remote(source, mine, send.at[index, 0], recv.at[index, me.core],
                     me.over_x - me.core + me.y, me.z))
        begin(remote(source, mine, send.at[index, 1], recv.at[index, 2 + me.core],
                     me.over_y - me.core + me.y, me.z))

        @pl.when(me.core == me.y)
        def _():
            pltpu.make_async_copy(source, mine, local.at[index]).start()

        @pl.when(me.core != me.y)
        def _():
            remote(source, mine, send.at[index, 4], recv.at[index, 4], me.over_core, me.z).start()

    def rows_relay(which):
        index = 5 + which

        @pl.when((me.core == me.y) & ((index == last) | (turn_of(index) == 0)))
        def _():
            hand_on(index, row_piece(which, me.over_x - me.core), 0, 5, 5, me.over_y, me.z)

        @pl.when((me.core != me.y) & ((index == last) | (turn_of(index) == 1)))
        def _():
            hand_on(index, row_piece(which, me.over_y - me.core + 1), 3, 6, 6, me.over_x, me.z)

    def rows_forward(which):
        index = 5 + which

        @pl.when((me.core != me.y) & (turn_of(index) == 0))
        def _():
            hand_on(index, row_piece(which, corner), 5, 5, 6, me.dp, beside)

        @pl.when((me.core != me.y) & (turn_of(index) == 1))
        def _():
            hand_on(index, row_piece(which, corner + 1), 6, 6, 5, me.dp, beside)

    def rows_finish(which):
        source, target = by_rows[which]
        index = 5 + which
        mine = row_piece(which, me.dp)

        @pl.when(me.core == me.y)
        def _():
            arrived(index, row_piece(which, me.over_x - me.core + 1), 1)
            arrived(index, row_piece(which, me.over_core), 4)
            pltpu.make_async_copy(source, mine, local.at[index]).wait()

            @pl.when((index == last) | (turn_of(index) == 0))
            def _():
                left(index, mine, 5)

            @pl.when((index != last) & (turn_of(index) == 1))
            def _():
                arrived(index, row_piece(which, me.over_x - me.core), 0)

        @pl.when(me.core != me.y)
        def _():
            arrived(index, row_piece(which, me.over_y - me.core), 2)
            left(index, mine, 4)
            left(index, mine, 6)

            @pl.when((index != last) & (turn_of(index) == 0))
            def _():
                arrived(index, row_piece(which, me.over_y - me.core + 1), 3)
                arrived(index, row_piece(which, corner + 1), 6)

            @pl.when((index == last) | (turn_of(index) == 1))
            def _():
                arrived(index, row_piece(which, corner), 5)

            @pl.when(index == last)
            def _():
                arrived(index, row_piece(which, corner + 1), 6)

            @pl.when((index != last) & (turn_of(index) == 1))
            def _():
                left(index, mine, 5)

    def load(source, target, k):
        return pltpu.make_async_copy(source, target, load_sem.at[k])

    stores = []

    def store(source, target):
        copy = pltpu.make_async_copy(source, target, store_sem.at[len(stores)])
        stores.append(copy)
        copy.start()
        return copy

    length, width = x_v.shape
    own_width = width // 2
    half_ff = ff_out.shape[1] // 2

    row_copies(0)
    row_copies(1)
    for index in range(3):
        columns_start(index)
    for k in range(1, 8):
        begin(remote(gains, gains_out.at[me.dp], gain_send.at[k - 1], gain_recv.at[k - 1],
                     lax.rem(me.dp + k, 8), me.z))
    pltpu.make_async_copy(gains, gains_out.at[me.dp], gain_recv.at[7]).start()
    fill_rotary(rotary, cosine, sine)
    store(cosine, cosine_out)
    store(sine, sine_out)
    for index in range(3):
        columns_relay(index)
    rows_start(0)
    columns_start(3)
    row_relay(0)
    row_relay(1)
    for k in range(1, 8):
        piece = gains_out.at[lax.rem(me.dp + 8 - k, 8)]
        remote(piece, piece, gain_send.at[k - 1], gain_recv.at[k - 1], me.over_core, me.z).wait_recv()
    pltpu.make_async_copy(gains, gains_out.at[me.dp], gain_recv.at[7]).wait()
    load(gains_out, gains_v, 0).start()
    row_finish(1)
    load(seg_out, seg_v, 1).start()
    row_finish(0)
    load(x_out, x_v, 2).start()
    load(gains_out, gains_v, 0).wait()
    load(seg_out, seg_v, 1).wait()
    load(x_out, x_v, 2).wait()
    both_gains = gains_v[0].astype(jnp.float32)
    for k in range(1, 8):
        both_gains = both_gains + gains_v[k].astype(jnp.float32)
    gain_a, gain_f = both_gains[0:1], both_gains[1:2]
    gain_v[...] = both_gains
    store(gain_v, gain_out)

    norm_rows(lambda part: x_v[part, :].astype(jnp.float32), gain_a, normed_v, length)

    docs = jnp.concatenate([seg_v[k] for k in range(4)], axis=1)
    start_row = jnp.zeros((1, length), jnp.int32)
    for k in range(4):
        square = lax.broadcasted_iota(jnp.int32, (rows, rows), 0) == lax.broadcasted_iota(
            jnp.int32, (rows, rows), 1
        )
        ids = jnp.sum(jnp.where(square, seg_v[k], 0), axis=1, keepdims=True)
        start_v[pl.ds(rows * k, rows), :] = jnp.sum(
            jnp.where(docs < ids, 1, 0), axis=1, keepdims=True
        )
        start_row = start_row + jnp.sum(jnp.where(ids < docs, 1, 0), axis=0, keepdims=True)
    start_row_v[...] = start_row
    store(start_row_v, start_out)
    turn(normed_v, turned_v)
    normed_store = store(turned_v, normed_t_out)

    for index in range(3):
        columns_forward(index)
    rows_relay(0)
    columns_start(4)
    for index in range(3):
        columns_finish(index)
    tile = 256
    tiles = own_width // tile
    for t in range(tiles):
        for kind in range(3):
            part = pl.ds(own_width * kind + tile * t, tile)
            pltpu.make_async_copy(qkv_out.at[:, part], w_qkv_v.at[:, part], w_sem.at[kind, t]).start()
    def tile_step(t, carry):
        def kind_step(kind, carry):
            first = own_width * kind + tile * t
            part = pl.ds(pl.multiple_of(first, 128), tile)
            pltpu.make_async_copy(qkv_out.at[:, part], w_qkv_v.at[:, part], w_sem.at[kind, t]).wait()
            product = jnp.dot(normed_v[...], w_qkv_v[:, part], preferred_element_type=jnp.float32)
            for k in range(tile // 128):
                piece = product[:, 128 * k : 128 * k + 128]
                cols = pl.ds(pl.multiple_of(first + 128 * k, 128), 128)

                @pl.when(kind < 2)
                def _():
                    turned = piece * cosine[...] + swap_halves(piece) * sine[...]
                    heads_v[:, cols] = turned.astype(jnp.bfloat16)

                @pl.when(kind == 2)
                def _():
                    heads_v[:, cols] = piece.astype(jnp.bfloat16)

            return carry

        lax.fori_loop(0, 3, kind_step, 0)

        def pair_step(pair, carry):
            attend(pair, own_width, heads_v, start_v, mixed_v, lse_v)
            return carry

        lax.fori_loop(tile // 128 * t, tile // 128 * (t + 1), pair_step, 0)

        @pl.when(t == 0)
        def _():
            row_copies(2)

        @pl.when(t == 1)
        def _():
            rows_forward(0)
            columns_relay(3)

        return carry

    lax.fori_loop(0, tiles, tile_step, 0)
    store(heads_v, heads_out)
    lse_t_v[...] = lse_v[...].T
    store(lse_t_v, lse_out)
    turn(mixed_v, mixed_t_v)
    store(mixed_t_v, mixed_t_out)

    rows_finish(0)
    load(o_out, w_o_v, 0).start()
    load(o_out, w_o_v, 0).wait()
    chunk = width // 3

    def part_copy(k):
        part = pl.ds(chunk * k, chunk)
        return remote(
            part_send.at[:, part], part_recv.at[:, part], part_sem.at[0, k], part_sem.at[1, k], me.over_core, me.z
        )

    def out_step(n, carry):
        part = pl.ds(pl.multiple_of(tile * n, 128), tile)
        product = jnp.dot(mixed_v[...], w_o_v[:, part], preferred_element_type=jnp.float32)
        part_send[:, part] = product.astype(jnp.bfloat16)
        middle_v[:, part] = x_v[:, part].astype(jnp.float32) + product
        for k in range(3):
            @pl.when(tile * (n + 1) == chunk * (k + 1))
            def _():
                part_copy(k).start()

        return carry

    lax.fori_loop(0, width // tile, out_step, 0)
    row_relay(2)
    columns_relay(4)
    rows_start(1)
    row_finish(2)
    load(g_out, branch_v, 1).start()
    for k in range(3):
        part_copy(k).wait_recv()

    def middle_rows(part):
        value = middle_v[part, :] + part_recv[part, :].astype(jnp.float32)
        middle_v[part, :] = value
        return value

    norm_rows(middle_rows, gain_f, nf_v, length)
    store(middle_v, middle_out)
    normed_store.wait()
    turn(nf_v, turned_v)
    store(turned_v, nf_t_out)
    load(g_out, branch_v, 1).wait()
    columns_forward(3)
    columns_forward(4)
    columns_finish(3)
    columns_finish(4)

    def ff_load(n, slot, kind):
        first = pl.multiple_of(half_ff * kind + tile * n, 128)
        return pltpu.make_async_copy(
            ff_out.at[:, pl.ds(first, tile)], w_ff_v.at[slot, kind], tile_sem.at[0, slot, kind]
        )

    def tile_store(n, slot, kind):
        part = pl.ds(pl.multiple_of(tile * n, 128), tile)
        target = (slope_gate_out, slope_up_out, hidden_out)[kind]
        return pltpu.make_async_copy(tile_v.at[slot, kind], target.at[:, part], tile_sem.at[1, slot, kind])

    def grad_store(n, slot):
        part = pl.ds(pl.multiple_of(tile * n, tile), tile)
        return pltpu.make_async_copy(g_tile_v.at[slot], g_down_out.at[part, :], tile_sem.at[2, slot, 0])

    count = half_ff // tile
    for kind in range(2):
        ff_load(0, 0, kind).start()
    rows_relay(1)

    def ff_step(n, carry):
        slot = lax.rem(n, 2)
        for kind in range(2):
            ff_load(n, slot, kind).wait()

        @pl.when(n + 1 < count)
        def _():
            for kind in range(2):
                ff_load(n + 1, 1 - slot, kind).start()

        @pl.when(n >= 2)
        def _():
            for kind in range(3):
                tile_store(n - 2, slot, kind).wait()
            grad_store(n - 2, slot).wait()

        gate = jnp.dot(nf_v[...], w_ff_v[slot, 0], preferred_element_type=jnp.float32)
        up_value = jnp.dot(nf_v[...], w_ff_v[slot, 1], preferred_element_type=jnp.float32)
        sigma = jax.nn.sigmoid(gate)
        silu = gate * sigma
        tile_v[slot, 0] = (up_value * sigma * (1.0 + gate * (1.0 - sigma))).astype(jnp.bfloat16)
        tile_v[slot, 1] = silu.astype(jnp.bfloat16)
        hidden = (silu * up_value).astype(jnp.bfloat16)
        tile_v[slot, 2] = hidden
        g_tile_v[slot] = jnp.dot(
            hidden.T, branch_v[...], preferred_element_type=jnp.float32
        ).astype(jnp.bfloat16)
        for kind in range(3):
            tile_store(n, slot, kind).start()
        grad_store(n, slot).start()

        return carry

    lax.fori_loop(0, count, ff_step, 0)
    for n in range(count - 2, count):
        for kind in range(3):
            tile_store(n, n % 2, kind).wait()
        grad_store(n, n % 2).wait()
    rows_finish(1)
    for copy in stores:
        if copy is not normed_store:
            copy.wait()
    for k in range(3):
        part_copy(k).wait_send()
    for index in range(3):
        row_wait_send(index)
    for copy in started:
        copy.wait_send()


def turn(source, target):
    def step(k, carry):
        first = pl.multiple_of(256 * k, 256)
        target[pl.ds(first, 256), :] = source[:, pl.ds(first, 256)].T
        return carry

    lax.fori_loop(0, source.shape[1] // 256, step, 0)


ROTARY_STEP = 32


def rotary_parts(length):
    lane = np.arange(2 * HD)
    pace = np.exp(-(lane % (HD // 2)) * (math.log(10000.0) / (HD // 2)))
    sign = np.where(lane % HD < HD // 2, -1.0, 1.0)
    far = np.arange(0, length, ROTARY_STEP)[:, None] * pace
    near = np.arange(ROTARY_STEP)[:, None] * pace
    parts = (np.cos(far), np.sin(far), sign * np.cos(far), sign * np.sin(far), np.cos(near), np.sin(near))
    return np.concatenate(parts).astype(np.float32)


def fill_rotary(parts, cosine, sine):
    steps = cosine.shape[0] // ROTARY_STEP
    near_cos = parts[4 * steps : 4 * steps + ROTARY_STEP, :]
    near_sin = parts[4 * steps + ROTARY_STEP : 4 * steps + 2 * ROTARY_STEP, :]

    def step(k, carry):
        far_cos, far_sin, sign_cos, sign_sin = (parts[pl.ds(steps * which + k, 1), :] for which in range(4))
        rows = pl.ds(pl.multiple_of(ROTARY_STEP * k, ROTARY_STEP), ROTARY_STEP)
        cosine[rows, :] = far_cos * near_cos - far_sin * near_sin
        sine[rows, :] = sign_sin * near_cos + sign_cos * near_sin
        return carry

    lax.fori_loop(0, steps, step, 0)


def norm_rows(read, gain, target, length, step=64):
    def chunk(k, carry):
        part = pl.ds(pl.multiple_of(k * step, step), step)
        values = read(part)
        scale = lax.rsqrt(jnp.mean(values * values, axis=-1, keepdims=True) + EPS)
        target[part, :] = (values * scale * gain).astype(target.dtype)
        return carry

    lax.fori_loop(0, length // step, chunk, 0)


def attend(pair, width, heads, start, mixed, lse):
    length = heads.shape[0]
    lane = lax.broadcasted_iota(jnp.int32, (BLK, 128), 1)
    cols = [pl.ds(pl.multiple_of(width * kind + 128 * pair, 128), 128) for kind in range(3)]
    for i in range(length // BLK):
        own_rows, keys = slice(BLK * i, BLK * (i + 1)), BLK * (i + 1)
        place = lax.broadcasted_iota(jnp.int32, (BLK, keys), 1)
        own = BLK * i + lax.broadcasted_iota(jnp.int32, (BLK, keys), 0)
        allowed = (place >= start[own_rows, :]) & (place <= own)
        query = heads[own_rows, cols[0]] * jnp.bfloat16(0.125)
        key, value = heads[0:keys, cols[1]], heads[0:keys, cols[2]]
        kept = lse[own_rows, :]
        outs = []
        for half in range(2):
            part = slice(64 * half, 64 * half + 64)
            scores = jnp.where(allowed, nt(query[:, part], key[:, part]), -1e30)
            peak = jnp.max(scores, axis=-1, keepdims=True)
            expo = jnp.exp(scores - peak)
            total = jnp.sum(expo, axis=-1, keepdims=True)
            out = jnp.dot(expo.astype(jnp.bfloat16), value[:, part], preferred_element_type=jnp.float32)
            outs.append((out / total).astype(jnp.bfloat16))
            kept = jnp.where(lane == 2 * pair + half, peak + jnp.log(total), kept)
        mixed[own_rows, cols[0]] = jnp.concatenate(outs, axis=1)
        lse[own_rows, :] = kept


def gather_all(tokens, segments, out_grad, gains, weights):
    rows, width = tokens.shape[1], tokens.shape[2]
    length, half, ff = 4 * rows, width // 2, weights[4].shape[1]
    half_ff = ff // 2
    low = jnp.bfloat16

    def shape(*dims, dtype=low):
        return jax.ShapeDtypeStruct(dims, dtype)

    shapes = [
        shape(length, width),
        shape(4, *segments.shape[1:], dtype=jnp.int32),
        shape(length, width),
        shape(8, *gains.shape),
        shape(width, 3 * half),
        shape(half, width),
        shape(width, ff),
        shape(half_ff, width),
        shape(length, 3 * half),
        shape(128, length, dtype=jnp.float32),
        shape(length, width, dtype=jnp.float32),
        shape(length, half_ff),
        shape(length, half_ff),
        shape(length, half_ff),
        shape(half_ff, width),
        shape(1, length, dtype=jnp.int32),
        shape(2, width, dtype=jnp.float32),
        shape(width, length),
        shape(width, length),
        shape(half, length),
        shape(length, 128, dtype=jnp.float32),
        shape(length, 128, dtype=jnp.float32),
    ]
    dma, vmem = pltpu.SemaphoreType.DMA, pltpu.VMEM
    whole = pl.BlockSpec(memory_space=pltpu.VMEM)
    return pl.pallas_call(
        gather_kernel,
        in_specs=[ANY] * 4 + [whole] + [ANY] * 7,
        out_specs=[ANY] * len(shapes),
        out_shape=shapes,
        scratch_shapes=[
            dma((7, 7)), dma((7, 7)), dma((7,)), dma((3, 4)), dma((3, 4)), dma((3,)), dma((7,)), dma((8,)),
            vmem((length, width), low),
            vmem((4,) + segments.shape[1:], jnp.int32),
            vmem((8,) + gains.shape, low),
            vmem((length, width), low),
            vmem((width, 3 * half), low),
            vmem((length, 3 * half), low),
            vmem((length, half), low),
            vmem((half, width), low),
            vmem((length, width), jnp.float32),
            vmem((length, width), low),
            vmem((length, width), low),
            vmem((length, width), low),
            vmem((2, 2, width, 256), low),
            vmem((length, width), low),
            vmem((2, 3, length, 256), low),
            vmem((2, 256, width), low),
            vmem((length, 128), jnp.float32),
            vmem((length, 1), jnp.int32),
            vmem((128, length), jnp.float32),
            vmem((1, length), jnp.int32),
            vmem((2, width), jnp.float32),
            vmem((width, length), low),
            vmem((half, length), low),
            vmem((length, 128), jnp.float32),
            vmem((length, 128), jnp.float32),
            dma((2, 3)), dma((3,)), dma((3, 3)), dma((3, 2, 3)), dma((11,)),
        ],
        compiler_params=pltpu.CompilerParams(
            collective_id=0, has_side_effects=True, vmem_limit_bytes=61 * 1024 * 1024
        ),
        cost_estimate=pl.CostEstimate(flops=0, bytes_accessed=500_000_000, transcendentals=0),
        name="gather_all",
    )(tokens, segments, out_grad, gains, jnp.asarray(rotary_parts(length)), *weights)


def guard(condition, action):
    if isinstance(condition, (bool, np.bool_)):
        if condition:
            action()
    else:
        pl.when(condition)(action)


def everything(*conditions):
    known = [c for c in conditions if isinstance(c, (bool, np.bool_))]
    if not all(known):
        return False
    rest = [c for c in conditions if not isinstance(c, (bool, np.bool_))]
    if not rest:
        return True
    total = rest[0]
    for c in rest[1:]:
        total = total & c
    return total


def chunk_of(rows):
    return 384 if rows % 384 == 0 else 512


def add_rows(target, first, other, rows):
    step = chunk_of(rows)

    def chunk(k, carry):
        at = pl.multiple_of(k * step, step)
        source = pl.multiple_of(first + k * step, step)
        target[pl.ds(at, step), :] += other[pl.ds(source, step), :]
        return carry

    lax.fori_loop(0, rows // step, chunk, 0)


JOB = 256


class Stream:
    active = True

    def tick(self, t):
        for late, stage in reversed(self.stages):
            k = t - late
            guard(everything(k >= 0, k < self.count), functools.partial(stage, k))

    @property
    def ticks(self):
        return self.count + self.stages[-1][0]

    def slot(self, k):
        return k % self.slots if isinstance(k, int) else lax.rem(k, self.slots)

    def column(self, k, base=0):
        return pl.ds(pl.multiple_of(base + JOB * k, 128), JOB)

    def total(self, k):
        return self.second.at[self.slot(k)]

    def final(self, k):
        return self.got.at[self.slot(k), pl.ds(0, self.rows)]

    def seq_copy(self, k, step):
        me, slot, sem = self.me, self.slot(k), self.seq_sem
        inner = me.z + 1 - 2 * (me.z // 2)
        opposite = 3 - me.z
        outer = 3 * (me.z // 2)
        if step == 0:
            return remote(self.total(k), self.over.at[slot, 0], sem.at[slot, 0, 0], sem.at[slot, 1, 0], me.dp, inner)
        if step == 1:
            return remote(
                self.total(k), self.over.at[slot, 1], sem.at[slot, 0, 1], sem.at[slot, 1, 1], me.dp, opposite
            )
        return remote(self.final(k), self.final(k), sem.at[slot, 0, 2], sem.at[slot, 1, 2], me.dp, outer)

    def plane_and_ends(self, k):
        self.reduce_plane(k)
        guard(
            everything(self.active, jnp.logical_not(self.me.middle)),
            lambda: self.seq_copy(k, 0).start(),
        )

    def across(self, k):
        def action():
            self.seq_copy(k, 0).wait_recv()
            add_rows(self.total(k), 0, self.over.at[self.slot(k), 0], self.rows)
            self.seq_copy(k, 1).start()

        guard(everything(self.active, self.me.middle), action)

    def back(self, k):
        def action():
            self.seq_copy(k, 1).wait_recv()
            final, total, over = self.final(k), self.total(k), self.over.at[self.slot(k), 1]
            step = chunk_of(self.rows)

            def chunk(at, carry):
                part = pl.ds(pl.multiple_of(at * step, step), step)
                final[part, :] = total[part, :] + over[part, :]
                return carry

            lax.fori_loop(0, self.rows // step, chunk, 0)
            self.seq_copy(k, 2).start()

        guard(everything(self.active, self.me.middle), action)

    def finish(self, k):
        guard(
            everything(self.active, jnp.logical_not(self.me.middle)),
            lambda: self.seq_copy(k, 2).wait_recv(),
        )
        self.output(k)

    def drain(self, k):
        self.drain_plane(k)

        def ends():
            self.seq_copy(k, 0).wait_send()

        def middles():
            self.seq_copy(k, 1).wait_send()
            self.seq_copy(k, 2).wait_send()

        guard(everything(self.active, jnp.logical_not(self.me.middle)), ends)
        guard(everything(self.active, self.me.middle), middles)


class ColumnStream(Stream):
    def __init__(self, me, source, target, ff_jobs, d_model, ff, refs):
        self.me, self.source, self.target = me, source, target
        self.got, self.keep, self.second, self.over, self.sem, self.seq_sem, self.credit = refs
        self.slots, self.rows = self.got.shape[0], source.shape[1] // 4
        self.count, self.ff_jobs = source.shape[0], ff_jobs
        self.ff, self.d_model = ff, d_model
        self.stages = (
            *zip(LATE["C"], (self.pass_second, self.plane_and_ends, self.across, self.back, self.finish, self.drain)),
        )

    def x_first(self, k):
        late = k // self.ff_jobs
        return (1 - late) * ((k + self.ff_jobs // 2 - 2) // self.ff_jobs) * ((k + 1) % 2) + late * (k % 2)

    def first_copy(self, k, part):
        me, slot, x_first = self.me, self.slot(k), self.x_first(k)
        block = x_first * (2 * part + 1 - me.x) + (1 - x_first) * (2 * (1 - me.y) + part)
        sent = self.source.at[k, pl.ds(pl.multiple_of(self.rows * block, self.rows), self.rows)]
        to = x_first * me.over_x + (1 - x_first) * me.over_y
        return remote(
            sent, self.got.at[slot, pl.ds(self.rows * part, self.rows)],
            self.sem.at[slot, 0, part], self.sem.at[slot, 1, part], to, me.z,
        )

    def keep_copy(self, k, part):
        me, slot, x_first = self.me, self.slot(k), self.x_first(k)
        block = x_first * (2 * part + me.x) + (1 - x_first) * (2 * me.y + part)
        kept = self.source.at[k, pl.ds(pl.multiple_of(self.rows * block, self.rows), self.rows)]
        return pltpu.make_async_copy(
            kept, self.keep.at[slot, pl.ds(self.rows * part, self.rows)], self.sem.at[slot, 2, part]
        )

    def at(self, k):
        x_first = self.x_first(k)
        return x_first * self.me.y + (1 - x_first) * self.me.x

    def second_copy(self, k):
        me, slot, x_first = self.me, self.slot(k), self.x_first(k)
        row = pl.multiple_of(self.rows * (1 - self.at(k)), self.rows)
        to = x_first * me.over_y + (1 - x_first) * me.over_x
        return remote(
            self.keep.at[slot, pl.ds(row, self.rows)], self.second.at[slot],
            self.sem.at[slot, 0, 2], self.sem.at[slot, 1, 2], to, me.z,
        )

    def start(self, k):
        def credits():
            slot = self.slot(k)

            @pl.when(self.me.middle)
            def _():
                pl.semaphore_wait(self.credit.at[slot], 5)

            @pl.when(jnp.logical_not(self.me.middle))
            def _():
                pl.semaphore_wait(self.credit.at[slot], 4)

        guard(k >= self.slots, credits)
        for part in range(2):
            self.first_copy(k, part).start()
            self.keep_copy(k, part).start()

    def pass_second(self, k):
        for part in range(2):
            self.keep_copy(k, part).wait()
            self.first_copy(k, part).wait_recv()
        slot = self.slot(k)
        add_rows(self.keep.at[slot], 0, self.got.at[slot], 2 * self.rows)
        self.second_copy(k).start()

    def reduce_plane(self, k):
        self.second_copy(k).wait_recv()
        add_rows(self.total(k), self.rows * self.at(k), self.keep.at[self.slot(k)], self.rows)

    def out_column(self, k, core, late):
        if late:
            m, half = k - self.ff_jobs, self.d_model // 2
            tiles = half // JOB
            first = 2 * self.ff + self.d_model * (m // tiles) + JOB * (m % tiles) + half * core
        else:
            first = self.ff * (k % 2) + JOB * (k // 2) + self.ff // 2 * core
        return self.target.at[:, pl.ds(pl.multiple_of(first, 128), JOB)]

    def last_copy(self, k, late=False):
        me, slot, rows = self.me, self.slot(k), self.rows // 2
        part = self.got.at[slot, pl.ds(pl.multiple_of(rows * (1 - me.core), rows), rows)]
        return remote(
            part, self.out_column(k, me.core, late), self.sem.at[slot, 0, 3], self.sem.at[slot, 1, 3],
            me.over_core, me.z,
        )

    def own_copy(self, k, late=False):
        me, slot, rows = self.me, self.slot(k), self.rows // 2
        part = self.got.at[slot, pl.ds(pl.multiple_of(rows * me.core, rows), rows)]
        return pltpu.make_async_copy(part, self.out_column(k, me.core, late), self.sem.at[slot, 2, 0])

    def output(self, k):
        def begin(late):
            self.last_copy(k, late).start()
            self.own_copy(k, late).start()

        guard(k < self.ff_jobs, lambda: begin(False))
        guard(k >= self.ff_jobs, lambda: begin(True))

    def drain_plane(self, k):
        for part in range(2):
            self.first_copy(k, part).wait_send()
        self.second_copy(k).wait_send()

        def end(late):
            self.last_copy(k, late).wait()
            self.own_copy(k, late).wait()

        guard(k < self.ff_jobs, lambda: end(False))
        guard(k >= self.ff_jobs, lambda: end(True))

    def drain(self, k):
        super().drain(k)

        def signal(dp, seq):
            pl.semaphore_signal(
                self.credit.at[self.slot(k)], inc=1, device_id={"dp": dp, "seq": seq},
                device_id_type=pl.DeviceIdType.MESH,
            )

        def free():
            me = self.me
            for dp in (me.over_core, me.over_x, me.over_y):
                signal(dp, me.z)

            @pl.when(me.middle)
            def _():
                signal(me.dp, 3 - me.z)
                signal(me.dp, 3 * (me.z // 2))

            @pl.when(jnp.logical_not(me.middle))
            def _():
                signal(me.dp, me.z + 1 - 2 * (me.z // 2))

        guard(k + self.slots < self.count, free)


class RowStream(Stream):
    def __init__(self, me, source, target, lates, refs):
        self.me, self.source, self.target = me, source, target
        self.got, self.second, self.over, self.stage, self.sem, self.seq_sem = refs
        self.slots, self.rows = self.got.shape[0], self.got.shape[1]
        self.count = self.slots
        self.active = me.core == me.y
        steps = (self.pass_second, self.plane_and_ends, self.across, self.back, self.finish, self.drain)
        self.stages = tuple(zip(lates, steps))

    def first_copy(self, k):
        me, slot = self.me, self.slot(k)
        return remote(self.part(k, 1 - me.x), self.got.at[slot], self.sem.at[slot, 0, 0], self.sem.at[slot, 1, 0], me.over_x, me.z)

    def part(self, k, x):
        rows = pl.ds(pl.multiple_of(self.rows * x, self.rows), self.rows)
        return self.source.at[k, rows] if len(self.source.shape) == 3 else self.source.at[rows, self.column(k)]

    def load_copy(self, k):
        return pltpu.make_async_copy(self.part(k, self.me.x), self.stage, self.sem.at[self.slot(k), 2, 0])

    def second_copy(self, k):
        me, slot = self.me, self.slot(k)
        return remote(
            self.got.at[slot], self.second.at[slot], self.sem.at[slot, 0, 2], self.sem.at[slot, 1, 2],
            me.over_y, me.z,
        )

    def start(self, k):
        self.first_copy(k).start()
        guard(k == 0, lambda: self.load_copy(k).start())

    def pass_second(self, k):
        self.load_copy(k).wait()
        self.first_copy(k).wait_recv()
        add_rows(self.got.at[self.slot(k)], 0, self.stage, self.rows)
        guard(k + 1 < self.count, lambda: self.load_copy(k + 1).start())
        guard(jnp.logical_not(self.active), lambda: self.second_copy(k).start())

    def reduce_plane(self, k):
        def action():
            self.second_copy(k).wait_recv()
            add_rows(self.total(k), 0, self.got.at[self.slot(k)], self.rows)

        guard(self.active, action)

    def last_copy(self, k):
        me, slot, rows = self.me, self.slot(k), self.rows // 2
        part = self.got.at[slot, pl.ds(pl.multiple_of(rows * (1 - me.core), rows), rows)]
        return remote(
            part, self.target.at[:, self.column(k)], self.sem.at[slot, 0, 3], self.sem.at[slot, 1, 3],
            me.over_core, me.z,
        )

    def own_copy(self, k):
        me, slot, rows = self.me, self.slot(k), self.rows // 2
        part = self.got.at[slot, pl.ds(pl.multiple_of(rows * me.core, rows), rows)]
        return pltpu.make_async_copy(part, self.target.at[:, self.column(k)], self.sem.at[slot, 2, 1])

    def output(self, k):
        def action():
            self.last_copy(k).start()
            self.own_copy(k).start()

        guard(self.active, action)

    def drain_plane(self, k):
        self.first_copy(k).wait_send()

        def active():
            self.last_copy(k).wait_send()
            self.own_copy(k).wait()

        def passive():
            self.second_copy(k).wait_send()
            self.last_copy(k).wait_recv()

        guard(self.active, active)
        guard(jnp.logical_not(self.active), passive)


PLAN = {
    "s0": {"E": (0, 3)},
    "a": {"E": (3, 4, 4, 5, 5, 5, 6, 6, 6), "S": (0, 1, 2, 3, 3, 5, 5, 5, 5), "C": (0, 0, 0, 0, 0, 1, 1, 2, 2), "D": (0, 0, 0, 0, 1, 1, 1, 1, 1)},
    "l0": {"D": (1, 2)},
    "l1": {"S": (5, 6), "D": (2, 3)},
    "l2": {"S": (6, 8)},
    "i": {"S": (8, 8, 8, 8, 9, 9, 10), "C": (2, 2, 2, 2, 3, 3, 3), "D": (3, 3, 3, 3, 4, 4, 4)},
    "n0": {"S": (10, 12), "C": (3, 5)},
    "n1": {"C": (5, 6)},
    "n2": {"C": (8, 9)},
    "o": {"C": (6, 7, 7, 7, 8, 8, 8), "D": (4, 4, 4, 4, 4, 4, 5)},
    "h": {"S": (12, 13, 13, 14, 14, 15, 15), "C": (9, 10, 11, 12, 13, 13, 13), "D": (5, 6, 7, 7, 7, 8, 9)},
    "t": {"S": (15, 16, 16, 16, 16, 16, 16), "F": (0, 0, 1, 1, 2, 3, 3), "C": (13, 14, 14, 15, 15, 15, 16), "D": (9, 10, 10, 10, 10, 10, 11)},
    "t6": {"F": (3, 4)},
    "p": {"S": (16, 16, 17, 18, 19, 20, 20, 20, 20, 20), "O": (0, 0, 1, 1, 1, 2, 3, 3, 3, 3)},
    "p9": {},
}
LATE = {"C": (0, 2, 4, 6, 7, 8), "D": (0, 2, 4, 6, 7, 8), "O": (0, 2, 4, 6, 7, 8)}


class Pace:
    def __init__(self, cols, downs, outs):
        self.actions = {
            "E": downs.start, "S": cols.start, "F": outs.start, "C": cols.tick, "D": downs.tick, "O": outs.tick,
        }

    def at(self, place, n=0):
        for kind, bounds in PLAN[place].items():
            action = self.actions[kind]

            def one(t, carry, action=action):
                action(t)
                return carry

            if isinstance(n, int):
                low, high = bounds[n], bounds[n + 1]
                if high - low == 1:
                    action(low)
                elif high > low:
                    lax.fori_loop(low, high, one, 0)
                continue
            low, high = bounds[0], bounds[1]
            for k in range(1, len(bounds) - 1):
                reached = (n + 32 - k) // 32
                low = low + (bounds[k] - bounds[k - 1]) * reached
                high = high + (bounds[k + 1] - bounds[k]) * reached
            lax.fori_loop(low, high, one, 0)


GAIN_HOPS = 5


class GainSums:
    def __init__(self, me, target, buffer, sem):
        self.me, self.target, self.buffer, self.sem = me, target, buffer, sem

    def hop(self, k):
        me = self.me
        across = me.z + 2 - 4 * (me.z // 2)
        beside = me.z + 1 - 2 * (me.z % 2)
        dp = (me.over_core, me.over_x, me.over_y, me.dp, me.dp)[k]
        seq = (me.z, me.z, me.z, beside, across)[k]
        return remote(
            self.buffer.at[k, 0], self.buffer.at[k, 1], self.sem.at[0, k], self.sem.at[1, k], dp, seq
        )

    def start(self):
        self.hop(0).start()

    def step(self, k):
        self.hop(k).wait_recv()
        total = self.buffer[k, 0] + self.buffer[k, 1]
        if k + 1 < GAIN_HOPS:
            self.buffer[k + 1, 0] = total
            self.hop(k + 1).start()
        else:
            self.target[...] = total

    def drain(self):
        for k in range(GAIN_HOPS):
            self.hop(k).wait_send()


class RowsBack:
    def __init__(self, me, source, target, sem):
        self.me, self.source, self.target, self.sem = me, source, target, sem

    def each(self, local, elsewhere):
        me = self.me
        rows = self.source.shape[0] // 2
        for slot in range(2):
            core, seq = me.z % 2, 2 * me.core + slot
            here = (core == me.core) & (seq == me.z)
            block, target = self.source.at[pl.ds(rows * slot, rows)], self.target.at[me.z // 2]

            @pl.when(here)
            def _():
                local(pltpu.make_async_copy(block, target, self.sem.at[2, 0]))

            @pl.when(jnp.logical_not(here))
            def _():
                elsewhere(
                    remote(
                        block, target, self.sem.at[0, slot], self.sem.at[1, me.z // 2],
                        me.dp - me.core + core, seq,
                    )
                )

    def start(self):
        self.each(lambda copy: copy.start(), lambda copy: copy.start())

    def drain(self):
        me = self.me
        self.each(lambda copy: copy.wait(), lambda copy: copy.wait_send())
        rows = self.source.shape[0] // 2
        for m in range(2):
            here = (me.z == 2 * m + me.core) & (me.core == me.z // 2)

            @pl.when(jnp.logical_not(here))
            def _():
                remote(
                    self.source.at[pl.ds(0, rows)], self.target.at[m], self.sem.at[0, 0],
                    self.sem.at[1, m], me.over_core, me.z,
                ).wait_recv()


def attend_back(pair, width, heads, grad_mixed, start, lse, grads, key_sum, value_sum, query_sum, cosine, sine):
    length = heads.shape[0]
    cols = [pl.ds(pl.multiple_of(width * kind + 128 * pair, 128), 128) for kind in range(3)]
    key_sum[...] = jnp.zeros_like(key_sum)
    value_sum[...] = jnp.zeros_like(value_sum)
    for i in range(length // BLK):
        own_rows, keys = slice(BLK * i, BLK * (i + 1)), BLK * (i + 1)
        place = lax.broadcasted_iota(jnp.int32, (keys, BLK), 0)
        own = BLK * i + lax.broadcasted_iota(jnp.int32, (keys, BLK), 1)
        allowed = (place >= start[:, own_rows]) & (place <= own)
        query = heads[own_rows, cols[0]] * jnp.bfloat16(0.125)
        key, value = heads[0:keys, cols[1]], heads[0:keys, cols[2]]
        grad = grad_mixed[own_rows, cols[0]]
        for half in range(2):
            part = slice(64 * half, 64 * half + 64)
            scores = nt(key[:, part], query[:, part])
            logsum = lse[pl.ds(2 * pair + half, 1), own_rows]
            probs = jnp.where(allowed, jnp.exp(scores - logsum), 0.0)
            grad_probs = nt(value[:, part], grad[:, part])
            inner = jnp.sum(probs * grad_probs, axis=0, keepdims=True)
            grad_scores = (probs * (grad_probs - inner)).astype(jnp.bfloat16)
            value_sum[0:keys, part] += dot(probs.astype(jnp.bfloat16), grad[:, part])
            key_sum[0:keys, part] += dot(grad_scores, query[:, part])
            query_sum[own_rows, part] = tn(grad_scores, key[:, part]) * 0.125
    for kind, total in enumerate((query_sum, key_sum)):
        value = total[...]
        grads[:, cols[kind]] = (value * cosine[...] - swap_halves(value) * sine[...]).astype(jnp.bfloat16)
    grads[:, cols[2]] = value_sum[...].astype(jnp.bfloat16)


def backward_kernel(
    branch_h, slope_gate_h, slope_up_h, hidden_h, nf_t_h, normed_t_h, mixed_t_h, heads_h, lse_h, middle_h, x_h,
    g_down_h, w_qkv_h, w_o_h, w_ff_h, w_down_h, start_ref, gain_ref, cosine, sine,
    out_o, tokens_o, cols_o, o_o, down_o, gains_o, g_cols_h, g_o_h, kept_h, rows_h, grad_nf_h,
    col_got, col_keep, col_second, col_over, col_sem, col_seq, col_credit,
    down_got, down_second, down_over, down_stage, down_sem, down_seq,
    o_got, o_second, o_over, o_stage, o_sem, o_seq,
    wide_recv, half_recv, half_free, wide_sem, half_sem,
    gain_buffer, gain_sem, row_sem, load_sem, tile_sem, store_sem,
):
    me = Place()
    enter(
        [(me.over_core, me.z), (me.over_x, me.z), (me.over_y, me.z)]
        + [(me.dp - me.core + core, lax.rem(me.z + k, 4)) for k in range(1, 4) for core in range(2)]
    )
    length, width = branch_h.shape
    half_rows, own_width, half_ff = length // 2, width // 2, slope_gate_h.shape[1]
    bf16, f32 = jnp.bfloat16, jnp.float32
    vmem = pltpu.VMEM
    ff_jobs = 2 * half_ff // JOB
    cols = ColumnStream(
        me, g_cols_h, cols_o, ff_jobs, width, 2 * half_ff,
        (col_got, col_keep, col_second, col_over, col_sem, col_seq, col_credit),
    )
    downs = RowStream(
        me, g_down_h, down_o, LATE["D"], (down_got, down_second, down_over, down_stage, down_sem, down_seq)
    )
    outs = RowStream(me, g_o_h, o_o, LATE["O"], (o_got, o_second, o_over, o_stage, o_sem, o_seq))
    back_out = RowsBack(me, rows_h.at[0], out_o, row_sem.at[0])
    back_tokens = RowsBack(me, rows_h.at[1], tokens_o, row_sem.at[1])
    gains = GainSums(me, gains_o, gain_buffer, gain_sem)

    def load(source, target, k=0):
        return pltpu.make_async_copy(source, target, load_sem.at[k])

    def fetch(*pairs):
        for k, (source, target) in enumerate(pairs):
            load(source, target, k).start()
        for k, (source, target) in enumerate(pairs):
            load(source, target, k).wait()

    def lanes(n, size=JOB, base=0):
        return pl.ds(pl.multiple_of(base + size * n, 128), size)

    def sublanes(n, size):
        return pl.ds(pl.multiple_of(n * size, size), size)

    def grad_store(buffer, slot, target, n, k):
        return pltpu.make_async_copy(buffer.at[slot], target.at[n], store_sem.at[slot, k])

    pace = Pace(cols, downs, outs)
    pace.at("s0")

    def feed_forward(grad_ff):
        steps = half_ff // JOB

        def hidden_grads(branch, w_tile, slopes, nf_t, g_tile):
            def tile_loads(n, slot):
                return (
                    pltpu.make_async_copy(w_down_h.at[sublanes(n, JOB), :], w_tile.at[slot], tile_sem.at[slot, 0]),
                    pltpu.make_async_copy(slope_gate_h.at[:, lanes(n)], slopes.at[slot, 0], tile_sem.at[slot, 1]),
                    pltpu.make_async_copy(slope_up_h.at[:, lanes(n)], slopes.at[slot, 1], tile_sem.at[slot, 2]),
                )

            for copy in tile_loads(0, 0):
                copy.start()
            load(nf_t_h, nf_t, 1).start()
            fetch((branch_h, branch))

            def step(n, carry):
                slot = lax.rem(n, 2)
                for copy in tile_loads(n, slot):
                    copy.wait()

                @pl.when(n + 1 < steps)
                def _():
                    for copy in tile_loads(n + 1, 1 - slot):
                        copy.start()

                grad_hidden = nt(branch[...], w_tile[slot])

                @pl.when(n == 0)
                def _():
                    load(nf_t_h, nf_t, 1).wait()

                @pl.when(n > 1)
                def _():
                    for kind in range(2):
                        grad_store(g_tile, kind, g_cols_h, 2 * n - 2 + kind, 0).wait()

                for kind in range(2):
                    grad = (grad_hidden * slopes[slot, kind].astype(f32)).astype(bf16)
                    grad_ff[:, lanes(n, JOB, half_ff * kind)] = grad
                    g_tile[kind] = dot(nf_t[...], grad).astype(bf16)
                    grad_store(g_tile, kind, g_cols_h, 2 * n + kind, 0).start()

                @pl.when(n == 0)
                def _():
                    for kind in range(2):
                        grad_store(g_tile, kind, g_cols_h, kind, 0).wait()

                pace.at("a", n)

                return carry

            lax.fori_loop(0, steps, step, 0)
            for kind in range(2):
                grad_store(g_tile, kind, g_cols_h, 2 * steps - 2 + kind, 0).wait()

        pl.run_scoped(
            hidden_grads, vmem((length, width), bf16), vmem((2, JOB, width), bf16),
            vmem((2, 2, length, JOB), bf16), vmem((width, length), bf16), vmem((2, width, JOB), bf16),
        )

        def layer_out(hidden, w_down, send, total):
            other, own = 1 - me.core, me.core
            def w_load(n):
                return load(w_down_h.at[:, lanes(n)], w_down.at[:, lanes(n)], 4 + n)

            load(hidden_h.at[sublanes(other, half_rows), :], hidden, 0).start()
            for n in range(width // JOB):
                w_load(n).start()
            load(hidden_h.at[sublanes(other, half_rows), :], hidden, 0).wait()
            load(middle_h.at[sublanes(own, half_rows), :], total, 2).start()

            def other_tile(n, carry):
                w_load(n).wait()
                send[:, lanes(n)] = dot(hidden[...], w_down[:, lanes(n)]).astype(bf16)
                return carry

            lax.fori_loop(0, width // JOB, other_tile, 0)
            exchange = remote(send, half_recv, half_sem.at[0, 0], half_sem.at[1, 0], me.over_core, me.z)
            exchange.start()
            pace.at("l0")
            fetch((hidden_h.at[sublanes(own, half_rows), :], hidden))
            load(middle_h.at[sublanes(own, half_rows), :], total, 2).wait()

            def own_tile(n, carry):
                total[:, lanes(n)] += dot(hidden[...], w_down[:, lanes(n)])
                return carry

            lax.fori_loop(0, width // JOB, own_tile, 0)
            pace.at("l1")
            exchange.wait()

            def combine(k, carry):
                part = sublanes(k, 64)
                send[part, :] = (total[part, :] + half_recv[part, :].astype(f32)).astype(bf16)
                return carry

            lax.fori_loop(0, half_rows // 64, combine, 0)
            pl.semaphore_signal(
                half_free, inc=1, device_id={"dp": me.over_core, "seq": me.z},
                device_id_type=pl.DeviceIdType.MESH,
            )
            fetch((send, rows_h.at[0]))

        pl.run_scoped(
            layer_out, vmem((half_rows, half_ff), bf16), vmem((half_ff, width), bf16),
            vmem((half_rows, width), bf16), vmem((half_rows, width), f32),
        )
        back_out.start()
        pace.at("l2")

    chunk = 2 * JOB
    chunks = width // chunk

    def wide_copy(send, k):
        part = pl.ds(chunk * k, chunk)
        return remote(
            send.at[:, part], wide_recv.at[:, part], wide_sem.at[0, k], wide_sem.at[1, k], me.over_core, me.z
        )

    def with_grad_ff(grad_ff):
        feed_forward(grad_ff)

        def input_grads(w_tile, send, parts):
            def tile_load(n, kind):
                return pltpu.make_async_copy(
                    w_ff_h.at[sublanes(n, JOB), pl.ds(half_ff * kind, half_ff)], w_tile.at[kind],
                    tile_sem.at[kind, 0],
                )

            def part_store(n, slot):
                return pltpu.make_async_copy(parts.at[slot], grad_nf_h.at[:, lanes(n)], store_sem.at[slot, 0])

            for kind in range(2):
                tile_load(0, kind).start()
            count = width // JOB

            def step(n, carry):
                slot = lax.rem(n, 2)
                tile_load(n, 0).wait()
                part = nt(grad_ff[:, 0:half_ff], w_tile[0])

                @pl.when(n + 1 < count)
                def _():
                    tile_load(n + 1, 0).start()

                tile_load(n, 1).wait()
                part = part + nt(grad_ff[:, half_ff : 2 * half_ff], w_tile[1])

                @pl.when(n + 1 < count)
                def _():
                    tile_load(n + 1, 1).start()

                @pl.when(n >= 2)
                def _():
                    part_store(n - 2, slot).wait()

                parts[slot] = part
                part_store(n, slot).start()
                send[:, lanes(n)] = part.astype(bf16)
                for k in range(chunks):
                    @pl.when(n == 2 * k + 1)
                    def _():
                        wide_copy(send, k).start()

                pace.at("i", n)

                return carry

            lax.fori_loop(0, count, step, 0)
            for n in range(count - 2, count):
                part_store(n, n % 2).wait()
            pace.at("n0")
            for k in range(chunks):
                wide_copy(send, k).wait()

        pl.run_scoped(
            input_grads, vmem((2, JOB, half_ff), bf16), vmem((length, width), bf16), vmem((2, length, JOB), f32)
        )

    pl.run_scoped(with_grad_ff, vmem((length, 2 * half_ff), bf16))

    def to_attention(grad_attn):
        def norm_back(grad_nf, middle, branch):
            def quarter(q):
                part = sublanes(q, length // 4)
                pairs = ((middle_h, middle), (branch_h, branch), (grad_nf_h, grad_nf))
                return [
                    load(source.at[part, :], target.at[part, :], 4 + 3 * q + k)
                    for k, (source, target) in enumerate(pairs)
                ]

            for q in range(4):
                for copy in quarter(q):
                    copy.start()
            gain = gain_ref[1:2, :]

            def rows(k, total):
                part = sublanes(k, 64)
                grad = grad_nf[part, :] + wide_recv[part, :].astype(f32)
                gained, values = norm_rows_back(middle[part, :], gain, grad)
                values = values + branch[part, :].astype(f32)
                grad_nf[part, :] = values
                grad_attn[part, :] = values.astype(bf16)
                return total + gained

            def quarter_rows(q, total):
                for copy in quarter(q):
                    copy.wait()
                return lax.fori_loop(length // 256 * q, length // 256 * (q + 1), rows, total)

            total = lax.fori_loop(0, 4, quarter_rows, jnp.zeros((1, width), f32))
            gain_buffer[0, 0, 1:2, :] = 0.5 * total
            kept = load(grad_nf.at[sublanes(me.core, half_rows), :], kept_h, 0)
            kept.start()
            pace.at("n1")
            kept.wait()

        pl.run_scoped(
            norm_back, vmem((length, width), f32), vmem((length, width), f32), vmem((length, width), bf16)
        )

        def out_projection(w_o, mixed_t, g_tile, grad_mixed):
            fetch((w_o_h, w_o), (mixed_t_h, mixed_t))

            def mixed_step(n, carry):
                grad_mixed[:, lanes(n)] = nt(grad_attn[...], w_o[sublanes(n, JOB), :]).astype(bf16)
                return carry

            lax.fori_loop(0, own_width // JOB, mixed_step, 0)
            placed = load(grad_mixed, wide_recv.at[:, pl.ds(0, own_width)], 3)
            placed.start()
            count = width // JOB

            def step(n, carry):
                slot = lax.rem(n, 2)

                @pl.when(n >= 2)
                def _():
                    grad_store(g_tile, slot, g_o_h, n - 2, 1).wait()

                g_tile[slot] = dot(mixed_t[...], grad_attn[:, lanes(n)]).astype(bf16)
                grad_store(g_tile, slot, g_o_h, n, 1).start()

                pace.at("o", n)

                return carry

            lax.fori_loop(0, count, step, 0)
            for n in range(count - 2, count):
                grad_store(g_tile, n % 2, g_o_h, n, 1).wait()
            placed.wait()

        pl.run_scoped(
            out_projection, vmem((own_width, width), bf16), vmem((own_width, length), bf16),
            vmem((2, own_width, JOB), bf16), vmem((length, own_width), bf16),
        )

    pl.run_scoped(to_attention, vmem((length, width), bf16))
    pace.at("n2")

    def attention(grads):
        def heads_back(heads, lse, key_sum, value_sum, query_sum):
            fetch((heads_h, heads), (lse_h, lse))

            def step(pair, carry):
                attend_back(
                    pair, own_width, heads, wide_recv, start_ref, lse, grads, key_sum, value_sum, query_sum, cosine, sine
                )
                pace.at("h", pair)
                return carry

            lax.fori_loop(0, own_width // 128, step, 0)

        pl.run_scoped(
            heads_back, vmem((length, 3 * own_width), bf16), vmem((128, length), f32),
            *[vmem((length, 128), f32)] * 3,
        )

        def tokens_back(w_tile, send, total, x_rows, kept):
            def tile_load(n, slot):
                return pltpu.make_async_copy(w_qkv_h.at[sublanes(n, JOB), :], w_tile.at[slot], tile_sem.at[slot, 0])

            tile_load(0, 0).start()
            load(x_h.at[sublanes(me.core, half_rows), :], x_rows, 0).start()
            load(kept_h, kept, 1).start()
            count = width // JOB

            def step(n, carry):
                slot = lax.rem(n, 2)
                tile_load(n, slot).wait()

                @pl.when(n + 1 < count)
                def _():
                    tile_load(n + 1, 1 - slot).start()

                send[:, lanes(n)] = nt(grads[sublanes(1 - me.core, half_rows), :], w_tile[slot]).astype(bf16)
                total[:, lanes(n)] = nt(grads[sublanes(me.core, half_rows), :], w_tile[slot])

                pace.at("t", n)
                return carry

            lax.fori_loop(0, count, step, 0)
            pl.semaphore_wait(half_free, 1)
            exchange = remote(send, half_recv, half_sem.at[0, 0], half_sem.at[1, 0], me.over_core, me.z)
            exchange.start()
            pace.at("t6")
            load(x_h.at[sublanes(me.core, half_rows), :], x_rows, 0).wait()
            load(kept_h, kept, 1).wait()
            exchange.wait()
            gain = gain_ref[0:1, :]

            def rows(k, sums):
                part = sublanes(k, 64)
                grad = total[part, :] + half_recv[part, :].astype(f32)
                gained, values = norm_rows_back(x_rows[part, :].astype(f32), gain, grad)
                send[part, :] = (values + kept[part, :]).astype(bf16)
                return sums + gained

            gain_buffer[0, 0, 0:1, :] = lax.fori_loop(0, half_rows // 64, rows, jnp.zeros((1, width), f32))
            gains.start()
            fetch((send, rows_h.at[1]))

        pl.run_scoped(
            tokens_back, vmem((2, JOB, 3 * own_width), bf16), vmem((half_rows, width), bf16),
            vmem((half_rows, width), f32), vmem((half_rows, width), bf16), vmem((half_rows, width), f32),
        )
        back_tokens.start()

        def projection_grads(normed_t, g_tile):
            fetch((normed_t_h, normed_t))
            count = 3 * own_width // JOB

            def step(n, carry):
                slot = lax.rem(n, 2)
                g_tile[slot] = dot(normed_t[...], grads[:, lanes(n)]).astype(bf16)

                @pl.when(n >= 1)
                def _():
                    grad_store(g_tile, 1 - slot, g_cols_h, ff_jobs + n - 1, 1).wait()

                grad_store(g_tile, slot, g_cols_h, ff_jobs + n, 1).start()

                pace.at("p", n)
                return carry

            lax.fori_loop(0, count, step, 0)
            grad_store(g_tile, (count - 1) % 2, g_cols_h, ff_jobs + count - 1, 1).wait()

        pl.run_scoped(projection_grads, vmem((width, length), bf16), vmem((2, width, JOB), bf16))

        pace.at("p9")

    pl.run_scoped(attention, vmem((length, 3 * own_width), bf16))

    first = {"E": 6, "S": 20, "F": 4, "C": 16, "D": 11, "O": 3}
    later = max(0, first["S"] - first["C"] - cols.slots + LATE["C"][-1] + 1)
    steps = max(stream.ticks - first[kind] for kind, stream in (("C", cols), ("D", downs), ("O", outs)))

    def rest(t, carry):
        for kind, stream in (("E", downs), ("S", cols), ("F", outs)):
            if first[kind] < stream.count:
                k = first[kind] + t - (later if kind == "S" else 0)
                guard((k >= first[kind]) & (k < stream.count), functools.partial(stream.start, k))
        for kind, stream in (("C", cols), ("D", downs), ("O", outs)):
            if first[kind] < stream.ticks:
                stream.tick(first[kind] + t)
        for k in range(GAIN_HOPS - 1):
            @pl.when(t == k)
            def _():
                gains.step(k)

        return carry

    lax.fori_loop(0, steps, rest, 0)
    for k in range(min(steps, GAIN_HOPS - 1), GAIN_HOPS):
        gains.step(k)
    gains.drain()
    back_out.drain()
    back_tokens.drain()


def norm_rows_back(values, gain, grad):
    scale = lax.rsqrt(jnp.mean(values * values, axis=-1, keepdims=True) + EPS)
    unit = values * scale
    inner = grad * gain
    return (
        jnp.sum(grad * unit, axis=0, keepdims=True),
        scale * (inner - unit * jnp.mean(inner * unit, axis=-1, keepdims=True)),
    )


COLUMN_SLOTS = 12


def backward(branch, slopes, hidden, turned, heads, lse, middle, x, g_down, weights, start, gain, cosine, sine):
    length, width = branch.shape
    half, half_ff = width // 2, hidden.shape[1]
    rows = length // 4
    bf16, f32 = jnp.bfloat16, jnp.float32

    def shape(*dims, dtype=bf16):
        return jax.ShapeDtypeStruct(dims, dtype)

    columns = 2 * half_ff + 3 * half
    shapes = [
        shape(2, rows, width),
        shape(2, rows, width),
        shape(width // 8, 2 * columns),
        shape(width // 8, width),
        shape(half_ff // 4, width),
        shape(2, width, dtype=f32),
        shape(columns // JOB, width, JOB),
        shape(width // JOB, half, JOB),
        shape(length // 2, width, dtype=f32),
        shape(2, length // 2, width),
        shape(length, width, dtype=f32),
    ]
    dma, vmem = pltpu.SemaphoreType.DMA, pltpu.VMEM
    whole = pl.BlockSpec(memory_space=pltpu.VMEM)
    ring, row = COLUMN_SLOTS, width // 4
    jobs = width // JOB
    row_buffers = []
    for depth in (half_ff // 2, half // 2):
        row_buffers += [
            vmem((jobs, depth, JOB), bf16), vmem((jobs, depth, JOB), bf16), vmem((jobs, 2, depth, JOB), bf16),
            vmem((depth, JOB), bf16), dma((jobs, 3, 4)), dma((jobs, 2, 3)),
        ]
    return pl.pallas_call(
        backward_kernel,
        in_specs=[ANY] * 16 + [whole] * 4,
        out_specs=[ANY] * 5 + [whole] + [ANY] * 5,
        out_shape=shapes,
        scratch_shapes=[
            vmem((ring, 2 * row, JOB), bf16), vmem((ring, 2 * row, JOB), bf16), vmem((ring, row, JOB), bf16),
            vmem((ring, 2, row, JOB), bf16), dma((ring, 3, 4)), dma((ring, 2, 3)),
            pltpu.SemaphoreType.REGULAR((ring,)),
        ]
        + row_buffers
        + [
            vmem((length, width), bf16), vmem((length // 2, width), bf16), pltpu.SemaphoreType.REGULAR,
            dma((2, 3)), dma((2, 1)),
            vmem((GAIN_HOPS, 2, 2, width), f32), dma((2, GAIN_HOPS)), dma((2, 3, 2)), dma((16,)), dma((2, 3)),
            dma((2, 2)),
        ],
        compiler_params=pltpu.CompilerParams(
            collective_id=1, has_side_effects=True, vmem_limit_bytes=63 * 1024 * 1024
        ),
        cost_estimate=pl.CostEstimate(flops=0, bytes_accessed=800_000_000, transcendentals=0),
        name="backward",
    )(
        branch, *slopes, hidden, *turned, heads, lse, middle, x, g_down, *weights, start, gain, cosine, sine
    )


def wide(value):
    return value.astype(jnp.float32)


def dot(a, b):
    return jnp.dot(a, b, preferred_element_type=jnp.float32)


WIDEN_STEPS = 2


def widen_kernel(cols, o, down, tokens, result, *outs):
    first = 0
    for out in outs[:5]:
        out[...] = cols[:, first : first + out.shape[1]].astype(jnp.float32)
        first += out.shape[1]
    for source, out in zip((o, down, tokens, result), outs[5:]):
        out[...] = source[...].astype(out.dtype)


def widen(cols, o, down, tokens, result, ff):
    depth, width = o.shape

    def rows(count, columns):
        return pl.BlockSpec((count // WIDEN_STEPS, columns), lambda i: (i, 0))

    shapes = [(depth, ff)] * 2 + [(depth, width)] * 4 + [down.shape, tokens.shape, result.shape]
    return pl.pallas_call(
        widen_kernel,
        grid=(WIDEN_STEPS,),
        in_specs=[rows(*value.shape) for value in (cols, o, down, tokens, result)],
        out_specs=[rows(*shape) for shape in shapes],
        out_shape=[jax.ShapeDtypeStruct(shape, jnp.float32) for shape in shapes[:-1]]
        + [jax.ShapeDtypeStruct(result.shape, result.dtype)],
        compiler_params=pltpu.CompilerParams(vmem_limit_bytes=63 * 1024 * 1024),
        name="widen",
    )(cols, o, down, tokens, result)


def column_device(
    tokens, segment_ids, out_grad, w_q, w_k, w_v, w_o, w_gate, w_up, w_down, gain_attn, gain_ffn
):
    dp_at = lax.axis_index("dp")
    rows, width = tokens.shape[1], tokens.shape[2]
    length, ff = 4 * rows, w_gate.shape[1]
    gains = lax.dynamic_update_slice_in_dim(
        jnp.zeros((2, width), jnp.bfloat16),
        jnp.stack([gain_attn, gain_ffn]),
        dp_at * gain_attn.shape[0],
        1,
    )
    (
        x_low, docs, grad_branch, gains, full_qkv, full_o, full_ff, full_down, heads, lse, middle,
        slope_gate, slope_up, hidden, g_down, start, gain, normed_t, nf_t, mixed_t,
        cosine, sine,
    ) = gather_all(
        tokens, segment_ids.reshape(2, 1, rows), out_grad, gains,
        (w_q, w_k, w_v, w_o, w_gate, w_up, w_down),
    )
    result, grad_tokens, g_cols, g_o, g_down, grad_gains = backward(
        grad_branch, (slope_gate, slope_up), hidden, (nf_t, normed_t, mixed_t), heads, lse, middle, x_low, g_down,
        (full_qkv, full_o, full_ff, full_down), start, gain, cosine, sine,
    )[:6]
    grad_gains = lax.dynamic_slice_in_dim(grad_gains, dp_at * (width // 8), width // 8, 1)
    flat = (2 * rows, width)
    gate, up, query, key, value, out, down, grad_tokens, result = widen(
        g_cols, g_o, g_down, grad_tokens.reshape(flat), result.reshape(flat), ff
    )
    result = result.reshape(2, rows, width)
    return (
        result, grad_tokens.reshape(2, rows, width), query, key, value, out, gate, up, down, grad_gains[0], grad_gains[1]
    )


def solution(mesh):
    placed = (
        P(None, ("dp", "seq"), None),
        P(None, ("dp", "seq")),
        P(None, ("dp", "seq"), None),
        P("dp", None),
        P("dp", None),
        P("dp", None),
        P("dp", None),
        P("dp", None),
        P("dp", None),
        P("dp", None),
        P("dp"),
        P("dp"),
    )
    return jax.shard_map(
        column_device if dict(mesh.shape) == FAST_MESH else per_device,
        mesh=mesh,
        in_specs=placed,
        out_specs=(
            P(None, ("dp", "seq"), None),
            P(None, ("dp", "seq"), None),
            P("dp", None),
            P("dp", None),
            P("dp", None),
            P("dp", None),
            P("dp", None),
            P("dp", None),
            P("dp", None),
            P("dp"),
            P("dp"),
        ),
        check_vma=False,
    )
```
